128 devices in a mesh: dp: 32 (over y, z, x_lo), mp: 4 (over x_hi, core).
Axes of the slice: x: 4 (x_hi: 2, x_lo: 2; x = x_hi * 2 + x_lo), y: 4, z: 4, core: 2. Of those that a mesh axis runs over, the one named last changes fastest.
Arguments:
- hidden_in: bfloat16 [16384, 1024], P('dp'), may hold values from -6 to 6
- lengths: int32 [16], replicated, may hold values from 1 to 4, 32 in all
- block_order: int32 [32], replicated, may hold values from 0 to 31, each once
- routes: int32 [16384, 8], P('dp'), may hold values from 0 to 31, all different within a row; in each aligned block of 512 rows (0 to 511, 512 to 1023, ...) at most 160 rows name the same one
- norm_gain_attn: float32 [1024], replicated, may hold values from 0.25 to 1.75
- w_query: bfloat16 [1024, 1024], P(None, 'mp'), may hold values from -0.75 to 0.75
- w_key: bfloat16 [1024, 512], P(None, 'mp'), may hold values from -0.75 to 0.75
- w_value: bfloat16 [1024, 512], P(None, 'mp'), may hold values from -0.1875 to 0.1875
- w_out: bfloat16 [1024, 1024], P('mp'), may hold values from -3 to 3
- norm_gain_moe: float32 [1024], replicated, may hold values from 0.25 to 1.75
- w_router: bfloat16 [1024, 32], replicated, may hold values from -0.09375 to 0.09375
- w_gate: bfloat16 [32, 1024, 512], P('dp', None, 'mp'), may hold values from -0.1875 to 0.1875
- w_up: bfloat16 [32, 1024, 512], P('dp', None, 'mp'), may hold values from -0.1875 to 0.1875
- w_down: bfloat16 [32, 512, 1024], P('dp', 'mp'), may hold values from -3 to 3
- out_grad: bfloat16 [16384, 1024], P('dp'), may hold values from -6 to 6
Outputs:
- out_hidden: bfloat16 [16384, 1024], P('dp', 'mp')
- grad_hidden: float32 [16384, 1024], P('dp', 'mp')
- grad_w_query: float32 [1024, 1024], P('dp', 'mp')
- grad_w_key: float32 [1024, 512], P('dp', 'mp')
- grad_w_value: float32 [1024, 512], P('dp', 'mp')
- grad_w_out: float32 [1024, 1024], P('mp', 'dp')
- grad_gain_attn: float32 [1024], P('dp')
- grad_gain_moe: float32 [1024], P('dp')
- grad_w_router: float32 [1024, 32], P('dp')
- grad_w_gate: float32 [32, 1024, 512], P('dp', None, 'mp')
- grad_w_up: float32 [32, 1024, 512], P('dp', None, 'mp')
- grad_w_down: float32 [32, 512, 1024], P('dp', 'mp')
The draws below stay inside these ranges and needn't reach their ends.
Inputs may be any that keep to these rules, and one draw needn't show every extreme that they name: lengths count blocks of 512 tokens of the packed sequences; they sum to 32 and the largest is exactly 4. `block_order`: each of 0 to 31 appears once. `routes`: each token names 8 different experts; among the 512 tokens of one index of dp no expert is named by more than 160 tokens, and in some of these aligned blocks one expert is named by exactly 160.
All inputs are finite; a program needn't handle non-finite values.
Results may differ from the reference program's by a relative error of at most 0.034.
Values may be sent and summed in bfloat16 or wider, within the bound.
No kernel may reach another device: no remote copies, remote signals or barrier semaphores. Data moves between devices by JAX's collectives and lax.ppermute only.
A program may use at most 128 MiB of HBM per device.

```python
import math
import jax
import jax.numpy as jnp
import numpy as np
from jax import lax

D = 1024
HEADS = 16
KV_HEADS = 8
HEAD_DIM = 64
EXPERTS = 32
TOP = 8
EFF = 512
TOK_DEV = 512
BLOCK = 512
MAXLEN = 2048
TOKENS = 16384
NBLOCKS = 32
NSEQ = 16
MOST = 4
CAP = 160
N_DP = 32


def level_of(rng, shape, split, least, top_value):
    def one(axis_at, parts):
        heights = jax.random.uniform(jax.random.fold_in(jax.random.fold_in(rng, 6), axis_at), (parts,), jnp.float32, least / len(split), top_value / len(split))
        return jnp.repeat(jnp.exp(heights), shape[axis_at] // parts).reshape((-1,) + (1,) * (len(shape) - axis_at - 1))

    level = one(*split[0])
    for cut in split[1:]:
        level = level * one(*cut)
    return level


def length_profile(count, total, most, lean):
    weights = [(1 << 20) // math.isqrt(rank ** lean) + 1 for rank in range(2, count + 1)]
    rest, given = total - most - (count - 1), [1] * (count - 1)
    while rest > 0:
        candidates = [i for i in range(count - 1) if given[i] < most]
        mass, budget = sum([weights[i] for i in candidates]), rest
        for i in candidates:
            more = min(most - given[i], max(1, budget * weights[i] // mass), rest)
            given[i] = given[i] + more
            rest = rest - more
    return np.array([most] + given)


def uneven(own_key, number_of, total, reach, skew):
    if number_of == 2:
        one = jax.random.randint(own_key, (), max(1, total - reach), min(reach, total - 1) + 1)
        return jnp.stack([one, total - one])
    tallies = jnp.asarray(length_profile(number_of, total, reach, skew), jnp.int32)
    twos = (number_of - 1) // 2
    source_of, receiver = tallies[1:1 + 2 * twos:2], tallies[2:2 + 2 * twos:2]
    slack = jnp.minimum(source_of - 1, reach - receiver)
    moved = jax.random.randint(jax.random.fold_in(own_key, 1), (twos,), 0, 1 << 20) % (slack + 1)
    tallies = tallies.at[1:1 + 2 * twos:2].set(source_of - moved).at[2:2 + 2 * twos:2].set(receiver + moved)
    return tallies[jax.random.permutation(jax.random.fold_in(own_key, 2), number_of)]


def shared_out(key, own, number, rows, number_of, top, bound, slope):
    order = jax.random.permutation(key, number_of)
    heavy_load, usual = load_shares(number_of, rows * top, bound, slope, True), load_shares(number_of, rows * top, bound, slope, False)
    places = jnp.arange(number_of)

    def named(sizes, rotation):
        used = int((sizes > 0).sum())
        fixed = max(1, used // 4)
        passed = fixed + (places - fixed + rotation * (used - fixed)) % max(1, number_of - fixed)
        return jnp.zeros((number_of,), jnp.int32).at[order[jnp.where(places < fixed, places, passed)]].set(jnp.asarray(sizes, jnp.int32))

    sizes = jnp.where(number % 4 == 0, named(heavy_load, number // 4), named(usual, number - number // 4 - 1))
    mixed = jax.random.permutation(jax.random.fold_in(own, 3), number_of)
    donor, taker = mixed[0:number_of // 2 * 2:2], mixed[1:number_of // 2 * 2:2]
    slack = jnp.minimum(sizes[donor] - 1, bound - sizes[taker]) // 2
    slack = jnp.where((donor == order[0]) | (taker == order[0]) | (sizes[taker] == 0), 0, jnp.maximum(slack, 0))
    passed = jax.random.randint(jax.random.fold_in(own, 4), (number_of // 2,), 0, 1 << 20) % (slack + 1)
    sizes = sizes.at[donor].add(-passed).at[taker].add(passed)
    labels = jnp.searchsorted(jnp.cumsum(sizes), jnp.arange(rows * top), side="right").astype(jnp.int32)
    listing = labels.reshape(top, rows).T
    listing = listing[jax.random.permutation(jax.random.fold_in(own, 1), rows)]
    rotation = jax.random.randint(jax.random.fold_in(own, 2), (rows, 1), 0, top)
    return jnp.take_along_axis(listing, (jnp.arange(top)[None, :] + rotation) % top, axis=1)


def load_shares(amount, total, bound, slope, full):
    loads = [(1 << 20) // math.isqrt(rank ** slope) + 1 for rank in range(1, amount + 1)]
    largest = bound if full else min(bound, max(-(-total // amount), total * loads[0] // sum(loads)))
    least = 1 if total - largest >= amount - 1 else 0
    counts, spare = [largest] + [least] * (amount - 1), total - largest - least * (amount - 1)
    while spare > 0:
        movable = [i for i in range(1, amount) if counts[i] < largest] or [i for i in range(1, amount) if counts[i] < bound]
        mass, budget = sum([loads[i] for i in movable]), spare
        for i in movable:
            addition = min(bound - counts[i], max(1, budget * loads[i] // mass), spare)
            counts[i] = counts[i] + addition
            spare = spare - addition
    return np.array(counts)


def bell_draw(stream_key, shape, scale, bound, shards=(), held_as=jnp.bfloat16):
    gain = level_of(stream_key, shape, shards, -0.22, 0.18) if shards else 1.0
    entries = jax.random.normal(stream_key, shape, jnp.float32) * scale * gain
    return jnp.minimum(jnp.maximum(entries, -bound), bound).astype(held_as)


def setup_inputs(seed: int = 0) -> dict:
    seeds = jax.random.split(jax.random.key(seed), 16)
    hidden_in = bell_draw(seeds[0], (TOKENS, D), 1.0, 6.0, ((0, 32),))
    lengths = uneven(seeds[1], NSEQ, NBLOCKS, MOST, 1).astype(jnp.int32)
    block_order = jax.random.permutation(seeds[2], NBLOCKS).astype(jnp.int32)
    routes_keys = jax.random.split(jax.random.fold_in(seeds[3], 1), TOKENS // TOK_DEV)
    routes_turns = jax.random.permutation(jax.random.fold_in(seeds[3], 3), TOKENS // TOK_DEV)
    routes = jax.vmap(lambda own, number: shared_out(jax.random.fold_in(seeds[3], 2), own, number, TOK_DEV, EXPERTS, TOP, CAP, 1))(routes_keys, routes_turns).reshape((TOKENS, TOP))
    norm_gain_attn = jnp.clip(1.0 + 0.15 * jax.random.normal(seeds[4], (D,), jnp.float32), 0.25, 1.75)
    w_query = bell_draw(seeds[5], (D, HEADS * HEAD_DIM), (D // 16) ** -0.5, 0.75, ((1, 4),))
    w_key = bell_draw(seeds[6], (D, KV_HEADS * HEAD_DIM), (D // 16) ** -0.5, 0.75, ((1, 4),))
    w_value = bell_draw(seeds[7], (D, KV_HEADS * HEAD_DIM), D ** -0.5, 0.1875, ((1, 4),))
    w_out = bell_draw(seeds[8], (HEADS * HEAD_DIM, D), (max(HEADS * HEAD_DIM // 256, 1)) ** -0.5, 3.0, ((0, 4),))
    norm_gain_moe = jnp.clip(1.0 + 0.15 * jax.random.normal(seeds[9], (D,), jnp.float32), 0.25, 1.75)
    w_router = bell_draw(seeds[10], (D, EXPERTS), (4 * D) ** -0.5, 0.09375)
    w_gate = bell_draw(seeds[11], (EXPERTS, D, EFF), D ** -0.5, 0.1875, ((0, 32), (2, 4)))
    w_up = bell_draw(seeds[12], (EXPERTS, D, EFF), D ** -0.5, 0.1875, ((0, 32), (2, 4)))
    w_down = bell_draw(seeds[13], (EXPERTS, EFF, D), (max(EFF // 128, 1)) ** -0.5, 3.0, ((0, 32), (1, 4)))
    out_grad = bell_draw(seeds[14], (TOKENS, D), 1.0, 6.0, ((0, 32),))
    return dict(hidden_in=hidden_in, lengths=lengths, block_order=block_order, routes=routes, norm_gain_attn=norm_gain_attn, w_query=w_query, w_key=w_key, w_value=w_value, w_out=w_out, norm_gain_moe=norm_gain_moe, w_router=w_router, w_gate=w_gate, w_up=w_up, w_down=w_down, out_grad=out_grad)


@jax.custom_vjp
def low(v):
    return lax.optimization_barrier(v.astype(jnp.bfloat16)).astype(jnp.float32)

@jax.custom_vjp
def low_back(v):
    return v

def low_keep(v):
    return (low(v), None)

def low_pass(kept, grad):
    return (grad,)

def back_keep(v):
    return (v, None)

def back_low(kept, grad):
    return (low(grad),)
low.defvjp(low_keep, low_pass)
low_back.defvjp(back_keep, back_low)
epsilon = 1e-06
residual_mult = 0.22
score_mult = 0.015625
rope_base = 10000.0
masked_score = -1e+30

def matmul_high(left_side, right_side):
    return jnp.dot(left_side, right_side, precision=lax.Precision.HIGHEST, preferred_element_type=jnp.float32)

def rms_norm(row_values, gain_values):
    norm_scale = lax.rsqrt(lax.optimization_barrier(jnp.mean(row_values * row_values, axis=-1, keepdims=True)) + epsilon)
    return row_values * norm_scale * gain_values

def rope_tables(positions):
    half_dim = HEAD_DIM // 2
    frequency = rope_base ** (-(jnp.arange(half_dim, dtype=jnp.float32) * 2.0) / HEAD_DIM)
    angles = positions.astype(jnp.float32)[:, None] * frequency[None, :]
    return (jnp.cos(angles), jnp.sin(angles))

def rotate(row_values, cosine, sine_table):
    half_dim = HEAD_DIM // 2
    shaped = row_values.reshape(row_values.shape[0], row_values.shape[1] // HEAD_DIM, HEAD_DIM)
    front_half = shaped[:, :, :half_dim]
    back_half = shaped[:, :, half_dim:]
    cosine_wide = cosine[:, None, :]
    sine_wide = sine_table[:, None, :]
    turned = jnp.concatenate([front_half * cosine_wide - back_half * sine_wide, back_half * cosine_wide + front_half * sine_wide], axis=-1)
    return turned.reshape(row_values.shape)

def block_tables(lengths, block_order):
    block_ids = jnp.arange(block_order.shape[0], dtype=jnp.int32)
    sequence_ids = jnp.arange(lengths.shape[0], dtype=jnp.int32)
    sequence_ends = jnp.cumsum(lengths).astype(jnp.int32)
    sequence_starts = (sequence_ends - lengths).astype(jnp.int32)
    sequence_of = lax.optimization_barrier(jnp.sum((sequence_ends[None, :] <= block_ids[:, None]).astype(jnp.int32), axis=1))
    begins = lax.optimization_barrier(jnp.sum(jnp.where(sequence_of[:, None] == sequence_ids[None, :], sequence_starts[None, :], 0), axis=1))
    offsets = (block_ids - begins).astype(jnp.int32)
    inverse = lax.optimization_barrier(jnp.sum(jnp.where(block_order[None, :] == block_ids[:, None], block_ids[None, :], 0), axis=1)).astype(jnp.int32)
    return (offsets, inverse)

def slot_tables(routes):
    expert_ids = jnp.arange(EXPERTS, dtype=jnp.int32)
    chosen = routes[:, :, None] == expert_ids[None, None, :]
    expert_hits = lax.optimization_barrier(jnp.sum(chosen.astype(jnp.int32), axis=1))
    blocked = expert_hits.reshape(N_DP, TOK_DEV, EXPERTS)
    rank_table = (jnp.cumsum(blocked, axis=1) - blocked).reshape(TOKENS, EXPERTS)
    pair_rank = lax.optimization_barrier(jnp.sum(jnp.where(chosen, rank_table[:, None, :], 0), axis=2))
    token_ids = jnp.arange(TOKENS, dtype=jnp.int32)
    slot_of = (routes * (N_DP * CAP) + (token_ids // TOK_DEV)[:, None] * CAP + pair_rank).reshape(-1).astype(jnp.int32)
    token_fill = jnp.broadcast_to(token_ids[:, None], (TOKENS, TOP)).reshape(-1)
    slot_token = jnp.full((EXPERTS * N_DP * CAP,), TOKENS, jnp.int32).at[slot_of].set(token_fill)
    slot_pair = jnp.full((EXPERTS * N_DP * CAP,), TOKENS * TOP, jnp.int32).at[slot_of].set(jnp.arange(TOKENS * TOP, dtype=jnp.int32))
    return (slot_token.reshape(EXPERTS, N_DP * CAP), slot_pair.reshape(EXPERTS, N_DP * CAP))

def attention(queries, key_rows, value_rows, block_order, offsets, inverse):
    window = MAXLEN // BLOCK
    head_group = HEADS // KV_HEADS
    key_blocks = jnp.take(key_rows.reshape(NBLOCKS, BLOCK, KV_HEADS, HEAD_DIM), inverse, axis=0)
    value_blocks = jnp.take(value_rows.reshape(NBLOCKS, BLOCK, KV_HEADS, HEAD_DIM), inverse, axis=0)
    pad_blocks = jnp.zeros((window - 1, BLOCK, KV_HEADS, HEAD_DIM), jnp.float32)
    padded_rows = (NBLOCKS + window - 1) * BLOCK
    key_padded = jnp.concatenate([pad_blocks, key_blocks], axis=0).reshape(padded_rows, KV_HEADS, HEAD_DIM)
    value_padded = jnp.concatenate([pad_blocks, value_blocks], axis=0).reshape(padded_rows, KV_HEADS, HEAD_DIM)
    query_blocks = queries.reshape(NBLOCKS, BLOCK, KV_HEADS, head_group, HEAD_DIM)
    block_reach = jnp.take(offsets, block_order)
    row_ids = jnp.arange(BLOCK, dtype=jnp.int32)
    column_ids = jnp.arange(window * BLOCK, dtype=jnp.int32)
    back_steps = window - 1 - column_ids // BLOCK
    later_keys = jnp.logical_and(back_steps[None, :] == 0, (column_ids % BLOCK)[None, :] > row_ids[:, None])

    def one_block(query_block, packed_block, reach_steps):
        row_start = (packed_block * BLOCK).astype(jnp.int32)
        key_window = lax.dynamic_slice_in_dim(key_padded, row_start, window * BLOCK, 0)
        value_window = lax.dynamic_slice_in_dim(value_padded, row_start, window * BLOCK, 0)
        raw_scores = low_back(jnp.einsum('qhgd,khd->hgqk', query_block, key_window, precision=lax.Precision.HIGHEST) * score_mult)
        allowed = jnp.logical_and(back_steps[None, :] <= reach_steps, jnp.logical_not(later_keys))
        prob_block = low(jax.nn.softmax(jnp.where(allowed, raw_scores, masked_score), axis=-1))
        return jnp.einsum('hgqk,khd->qhgd', prob_block, value_window, precision=lax.Precision.HIGHEST)
    attended = lax.map(lambda scan_items: jax.checkpoint(one_block)(*scan_items), (query_blocks, block_order, block_reach))
    return attended.reshape(TOKENS, HEADS * HEAD_DIM)

def forward(hidden_in, norm_gain_attn, w_query, w_key, w_value, w_out, norm_gain_moe, w_router, w_gate, w_up, w_down, tables):
    cosine, sine_table, block_order, offsets, inverse, routes, slot_token, slot_pair = tables
    normed = low(rms_norm(hidden_in, norm_gain_attn))
    query_pre = low_back(matmul_high(normed, w_query))
    key_pre = low_back(matmul_high(normed, w_key))
    value_pre = low_back(matmul_high(normed, w_value))
    queries = low(rotate(query_pre, cosine, sine_table))
    key_rows = low(rotate(key_pre, cosine, sine_table))
    value_rows = low(value_pre)
    attended = low_back(low(attention(queries, key_rows, value_rows, block_order, offsets, inverse)))
    branch = low_back(matmul_high(attended, w_out))
    residual = hidden_in + residual_mult * branch
    moe_in = low(rms_norm(residual, norm_gain_moe))
    logits = low_back(matmul_high(moe_in, w_router))
    picked = jnp.take_along_axis(logits, routes, axis=1)
    gate_weights = jax.nn.softmax(picked, axis=-1)
    moe_padded = jnp.concatenate([moe_in, jnp.zeros((1, D), jnp.float32)], axis=0)
    gate_padded = jnp.concatenate([gate_weights.reshape(-1), jnp.zeros((1,), jnp.float32)], axis=0)

    def expert_term(gate_matrix, up_matrix, down_matrix, token_index, pair_index):
        rows_in = low_back(jnp.take(moe_padded, token_index, axis=0))
        gate_pre = low_back(matmul_high(rows_in, gate_matrix))
        up_pre = low_back(matmul_high(rows_in, up_matrix))
        hidden_units = low(jax.nn.silu(gate_pre) * up_pre)
        expert_out = low_back(low(matmul_high(hidden_units, down_matrix)))
        return expert_out * jnp.take(gate_padded, pair_index)[:, None]

    def expert_step(mixture_total, scan_items):
        contribution = jax.checkpoint(expert_term)(*scan_items)
        return (mixture_total.at[scan_items[3]].add(contribution), None)
    mixture, unused = lax.scan(expert_step, jnp.zeros((TOKENS + 1, D), jnp.float32), (w_gate, w_up, w_down, slot_token, slot_pair))
    return residual + residual_mult * mixture[:TOKENS]

def reference(hidden_in, lengths, block_order, routes, norm_gain_attn, w_query, w_key, w_value, w_out, norm_gain_moe, w_router, w_gate, w_up, w_down, out_grad):
    offsets, inverse = block_tables(lengths, block_order)
    token_ids = jnp.arange(TOKENS, dtype=jnp.int32)
    token_offsets = jnp.take(jnp.take(offsets, block_order), token_ids // BLOCK)
    positions = (token_offsets * BLOCK + token_ids % BLOCK).astype(jnp.int32)
    cosine, sine_table = rope_tables(positions)
    slot_token, slot_pair = slot_tables(routes)
    tables = (cosine, sine_table, block_order, offsets, inverse, routes, slot_token, slot_pair)
    floats = tuple((array_in.astype(jnp.float32) for array_in in (hidden_in, norm_gain_attn, w_query, w_key, w_value, w_out, norm_gain_moe, w_router, w_gate, w_up, w_down)))
    result, pullback = jax.vjp(lambda *parameters: forward(*parameters, tables), *floats)
    gradients = pullback(out_grad.astype(jnp.float32))
    return (result.astype(jnp.bfloat16), gradients[0], gradients[2], gradients[3], gradients[4], gradients[5], gradients[1], gradients[6], gradients[7], gradients[8], gradients[9], gradients[10])
```

```python
import jax
import jax.numpy as jnp
from jax import lax
from jax.sharding import PartitionSpec as P

HEAD_DIM = 64
EXPERTS = 32
BLOCK = 512
MAXLEN = 2048
CAP = 160


epsilon = 1e-06
residual_mult = 0.22
score_mult = 0.015625
rope_base = 10000.0
masked_score = -1e30


def in_one_piece(arrays, axis, dim, along):
    ends, at = ([], 0)
    for a in arrays[:-1]:
        at += a.shape[along]
        ends.append(at)
    both = jnp.concatenate(arrays, axis=along)
    return tuple(jnp.split(lax.all_gather(both, axis, axis=dim, tiled=True), ends, axis=along))


def gathered_total(x, axis):
    parts = lax.all_gather(x, axis).astype(jnp.float32)
    return parts.sum(axis=0)


def turned_gather(arrays, axis, dims):
    turned = [jnp.moveaxis(a, dim, 0) for a, dim in zip(arrays, dims)]
    both = jnp.concatenate([t.reshape(len(t), -1) for t in turned], axis=1)
    result, at, finished = (lax.all_gather(both, axis, axis=0, tiled=True), 0, [])
    for t, dim in zip(turned, dims):
        share = result[:, at : at + t[0].size].reshape(-1, *t.shape[1:])
        finished.append(jnp.moveaxis(share, 0, dim))
        at += t[0].size
    return tuple(finished)


def in_blocks(x, dim, length):
    before, after = (x.shape[:dim], x.shape[dim + 1 :])
    return jnp.moveaxis(x.reshape(*before, length, -1, *after), dim, 0)


def laid_out(parts, dim):
    dims = list(parts.shape[1:])
    dims[dim] *= parts.shape[0]
    return jnp.moveaxis(parts, 0, dim).reshape(dims)


def exchange_both(x, axis, axes, splits, concats):
    sizes = [lax.axis_size(a) for a in axes]
    parts = in_blocks(x, splits[0], sizes[0])
    parts = jnp.moveaxis(in_blocks(parts, splits[1] + 1, sizes[1]), 0, 1)
    inside = parts.shape[2:]
    parts = parts.reshape(-1, *inside)
    parts = lax.all_to_all(parts, axis, split_axis=0, concat_axis=0, tiled=True)
    parts = laid_out(parts.reshape(*sizes, *inside), concats[0] + 1)
    return laid_out(parts, concats[1])


def in_one_piece_2(arrays, axis, dim, along):
    ends, at = ([], 0)
    for a in arrays[:-1]:
        at += a.shape[along]
        ends.append(at)
    both = jnp.concatenate(arrays, axis=along)
    return tuple(
        jnp.split(lax.psum_scatter(both, axis, scatter_dimension=dim, tiled=True), ends, axis=along)
    )


def sent_to_all(x, axis):
    length = lax.axis_size(axis)
    return lax.all_to_all(jnp.broadcast_to(x[None], (length, *x.shape)), axis, 0, 0, tiled=True)


def gathered_copies(x, axis, dim):
    parts = sent_to_all(x, axis)
    return laid_out(parts, dim)


def in_one_piece_3(arrays, axis, dim, along):
    columns = [a.reshape(*a.shape[:along], -1) for a in arrays]
    both = jnp.concatenate(columns, axis=along)
    result, at, finished = (lax.psum_scatter(both, axis, scatter_dimension=dim, tiled=True), 0, [])
    for a, column in zip(arrays, columns):
        share = result[..., at : at + column.shape[along]]
        finished.append(share.reshape(*share.shape[:along], *a.shape[along:]))
        at += column.shape[along]
    return tuple(finished)


def from_peers(x, axis):
    got = [x]
    for flip in (1, 2, 3):
        got.append(lax.ppermute(x, axis, [(i, i ^ flip) for i in range(4)]))
    return got


def in_mesh_order(parts, rank, dim):
    stacked = jnp.stack(parts)
    order = jnp.arange(4, dtype=jnp.int32) ^ rank
    return laid_out(jnp.take(stacked, order, axis=0), dim)


def reduced_share(x, axis):
    parts = lax.all_to_all(x, axis, 0, 0, tiled=True)
    return jnp.sum(parts.astype(jnp.float32), axis=0)


def rms_scale(row_values):
    return lax.rsqrt(jnp.mean(row_values * row_values, axis=-1, keepdims=True) + epsilon)


def norm_back(row_values, norm_scale, gain_values, incoming):
    weighted = incoming * gain_values
    inner_mean = jnp.mean(weighted * row_values, axis=-1, keepdims=True)
    return norm_scale * weighted - row_values * (norm_scale * norm_scale * norm_scale) * inner_mean


def rope_tables(positions):
    half_dim = HEAD_DIM // 2
    frequency = rope_base ** (-(jnp.arange(half_dim, dtype=jnp.float32) * 2.0) / HEAD_DIM)
    angles = positions.astype(jnp.float32)[:, None] * frequency[None, :]
    return (jnp.cos(angles), jnp.sin(angles))


def rotate(row_values, cosine, sine_table):
    half_dim = HEAD_DIM // 2
    shaped = row_values.reshape(row_values.shape[0], row_values.shape[1] // HEAD_DIM, HEAD_DIM)
    front_half = shaped[:, :, :half_dim]
    back_half = shaped[:, :, half_dim:]
    cosine_wide = cosine[:, None, :]
    sine_wide = sine_table[:, None, :]
    turned = jnp.concatenate(
        [
            front_half * cosine_wide - back_half * sine_wide,
            back_half * cosine_wide + front_half * sine_wide,
        ],
        axis=-1,
    )
    return turned.reshape(row_values.shape)


def rotate_back(row_values, cosine, sine_table):
    half_dim = HEAD_DIM // 2
    shaped = row_values.reshape(row_values.shape[0], row_values.shape[1] // HEAD_DIM, HEAD_DIM)
    front_half = shaped[:, :, :half_dim]
    back_half = shaped[:, :, half_dim:]
    cosine_wide = cosine[:, None, :]
    sine_wide = sine_table[:, None, :]
    turned = jnp.concatenate(
        [
            front_half * cosine_wide + back_half * sine_wide,
            back_half * cosine_wide - front_half * sine_wide,
        ],
        axis=-1,
    )
    return turned.reshape(row_values.shape)


def block_tables(lengths, block_order):
    block_ids = jnp.arange(block_order.shape[0], dtype=jnp.int32)
    sequence_ids = jnp.arange(lengths.shape[0], dtype=jnp.int32)
    sequence_ends = jnp.cumsum(lengths)
    sequence_starts = sequence_ends - lengths
    sequence_of = jnp.sum((sequence_ends[None, :] <= block_ids[:, None]).astype(jnp.int32), axis=1)
    begins = jnp.sum(
        jnp.where(sequence_of[:, None] == sequence_ids[None, :], sequence_starts[None, :], 0),
        axis=1,
    )
    offsets = block_ids - begins
    inverse = jnp.sum(
        jnp.where(block_order[None, :] == block_ids[:, None], block_ids[None, :], 0), axis=1
    )
    return (offsets, inverse)


def row_contract(left_side, right_side):
    return lax.dot_general(
        left_side, right_side, (((0,), (0,)), ((), ())), preferred_element_type=jnp.float32
    )


def times_transposed(left_side, right_side):
    return lax.dot_general(
        left_side, right_side, (((1,), (1,)), ((), ())), preferred_element_type=jnp.float32
    )


def expert_back(grouped_in, grouped_grad, gate_pre, up_pre, gate_mat, up_mat, down_mat):
    sigmoid_gate = jax.nn.sigmoid(gate_pre)
    silu_gate = jax.nn.silu(gate_pre)
    hidden_units = (silu_gate * up_pre).astype(jnp.bfloat16)
    down_grad = jnp.einsum(
        "secf,secd->efd", hidden_units, grouped_grad, preferred_element_type=jnp.float32
    )
    hidden_grad = jnp.einsum(
        "secd,efd->secf", grouped_grad, down_mat, preferred_element_type=jnp.float32
    )
    gate_pre_grad = (
        hidden_grad * up_pre * sigmoid_gate * (1.0 + gate_pre * (1.0 - sigmoid_gate))
    ).astype(jnp.bfloat16)
    up_pre_grad = (hidden_grad * silu_gate).astype(jnp.bfloat16)
    gate_w_grad = jnp.einsum(
        "secd,secf->edf", grouped_in, gate_pre_grad, preferred_element_type=jnp.float32
    )
    up_w_grad = jnp.einsum(
        "secd,secf->edf", grouped_in, up_pre_grad, preferred_element_type=jnp.float32
    )
    input_part = jnp.einsum(
        "secf,edf->secd", gate_pre_grad, gate_mat, preferred_element_type=jnp.float32
    ) + jnp.einsum("secf,edf->secd", up_pre_grad, up_mat, preferred_element_type=jnp.float32)
    return (gate_w_grad, up_w_grad, down_grad, input_part)


def per_device(
    hidden_in,
    lengths,
    block_order,
    routes,
    norm_gain_attn,
    w_query,
    w_key,
    w_value,
    w_out,
    norm_gain_moe,
    w_router,
    w_gate,
    w_up,
    w_down,
    out_grad,
):
    dp_count = lax.axis_size("dp")
    mp_count = lax.axis_size("mp")
    dp_rank = lax.axis_index("dp")
    mp_rank = lax.axis_index("mp")
    tokens_here = hidden_in.shape[0]
    model_width = hidden_in.shape[1]
    column_share = model_width // mp_count
    column_start = mp_rank * column_share
    blocks_here = tokens_here // BLOCK
    window = MAXLEN // BLOCK
    kv_here = w_key.shape[1] // HEAD_DIM
    head_group = w_query.shape[1] // HEAD_DIM // kv_here
    experts_here = w_gate.shape[0]
    route_width = routes.shape[1]
    capacity = CAP
    offsets, inverse = block_tables(lengths, block_order)
    block_ids = jnp.arange(block_order.shape[0], dtype=jnp.int32)
    my_blocks = lax.dynamic_slice_in_dim(block_order, dp_rank * blocks_here, blocks_here)
    my_offsets = jnp.sum(
        jnp.where(my_blocks[:, None] == block_ids[None, :], offsets[None, :], 0), axis=1
    )
    row_ids = jnp.arange(BLOCK, dtype=jnp.int32)
    positions = (my_offsets[:, None] * BLOCK + row_ids[None, :]).reshape(-1)
    cosine, sine_table = rope_tables(positions)
    later_keys = row_ids[None, :] > row_ids[:, None]
    input_full = hidden_in.astype(jnp.float32)
    scale_one = rms_scale(input_full)
    normed = (input_full * scale_one * norm_gain_attn).astype(jnp.bfloat16)
    query_pre = jnp.dot(normed, w_query, preferred_element_type=jnp.float32)
    key_pre = jnp.dot(normed, w_key, preferred_element_type=jnp.float32)
    value_pre = jnp.dot(normed, w_value, preferred_element_type=jnp.float32)
    queries = rotate(query_pre, cosine, sine_table).astype(jnp.bfloat16)
    key_rows = rotate(key_pre, cosine, sine_table).astype(jnp.bfloat16)
    value_rows = value_pre.astype(jnp.bfloat16)
    piece = BLOCK // dp_count
    kv_width = key_rows.shape[1] + value_rows.shape[1]
    key_value = jnp.concatenate([key_rows, value_rows], axis=1)
    spread = lax.all_to_all(
        key_value.reshape(dp_count, piece, kv_width), "dp", 0, 0, tiled=True
    )
    back_steps = jnp.arange(1, window, dtype=jnp.int32)
    wanted = jnp.maximum(block_order[:, None] - back_steps[None, :], 0)
    wanted_from = jnp.sum(
        jnp.where(wanted[:, :, None] == block_ids[None, None, :], inverse[None, None, :], 0), axis=2
    )
    picked_kv = jnp.take(spread, wanted_from.reshape(-1), axis=0)
    earlier = lax.all_to_all(
        picked_kv.reshape(dp_count, (window - 1) * piece, kv_width), "dp", 0, 0, tiled=True
    )
    earlier = jnp.moveaxis(earlier.reshape(dp_count, window - 1, piece, kv_width), 1, 0)
    kv_window = jnp.concatenate(
        [key_value[None], earlier.reshape(window - 1, BLOCK, kv_width)], axis=0
    )
    keys_window = kv_window[:, :, : key_rows.shape[1]]
    values_window = kv_window[:, :, key_rows.shape[1] :]

    def key_block(packed_query, key_step):
        return (
            lax.dynamic_index_in_dim(keys_window, key_step, 0, False),
            lax.dynamic_index_in_dim(values_window, key_step, 0, False),
            key_step,
        )

    def block_scores(query_block, key_block_rows, key_step):
        query_heads = query_block.reshape(BLOCK, kv_here, head_group, HEAD_DIM)
        key_heads = key_block_rows.reshape(BLOCK, kv_here, HEAD_DIM)
        raw_scores = (
            jnp.einsum("qhgd,khd->hgqk", query_heads, key_heads, preferred_element_type=jnp.float32)
            * score_mult
        )
        return jnp.where(jnp.logical_and(key_step == 0, later_keys), masked_score, raw_scores)

    local_block = 0
    packed_query = my_blocks[local_block]
    block_reach = my_offsets[local_block]
    query_block = queries

    def max_step(
        key_step,
        max_state,
        packed_query=packed_query,
        block_reach=block_reach,
        query_block=query_block,
    ):

        def max_live(running):
            running_max, running_sum = running
            key_part, value_part, row_start = key_block(packed_query, key_step)
            scores = block_scores(query_block, key_part, key_step)
            new_max = jnp.maximum(running_max, jnp.max(scores, axis=-1))
            new_sum = running_sum * jnp.exp(running_max - new_max) + jnp.sum(
                jnp.exp(scores - new_max[..., None]), axis=-1
            )
            return (new_max, new_sum)

        return lax.cond(key_step <= block_reach, max_live, lambda running: running, max_state)

    start_state = (
        jnp.full((kv_here, head_group, BLOCK), masked_score, jnp.float32),
        jnp.zeros((kv_here, head_group, BLOCK), jnp.float32),
    )
    running_max, running_sum = lax.fori_loop(0, window, max_step, start_state)
    block_lse = running_max + jnp.log(running_sum)

    def sum_step(
        key_step,
        accumulated,
        packed_query=packed_query,
        block_reach=block_reach,
        query_block=query_block,
        block_lse=block_lse,
    ):

        def sum_live(running_total):
            key_part, value_part, row_start = key_block(packed_query, key_step)
            prob_block = jnp.exp(
                block_scores(query_block, key_part, key_step) - block_lse[..., None]
            ).astype(jnp.bfloat16)
            value_heads = value_part.reshape(BLOCK, kv_here, HEAD_DIM)
            return running_total + jnp.einsum(
                "hgqk,khd->qhgd", prob_block, value_heads, preferred_element_type=jnp.float32
            )

        return lax.cond(
            key_step <= block_reach, sum_live, lambda running_total: running_total, accumulated
        )

    block_out = lax.fori_loop(
        0, window, sum_step, jnp.zeros((BLOCK, kv_here, head_group, HEAD_DIM), jnp.float32)
    )
    attended_blocks = block_out.reshape(BLOCK, kv_here * head_group * HEAD_DIM)
    lse_blocks = [block_lse]
    attended = attended_blocks.astype(jnp.bfloat16)
    branch_part = jnp.dot(attended, w_out, preferred_element_type=jnp.float32)
    branch_sent = jnp.moveaxis(
        branch_part.astype(jnp.bfloat16).reshape(tokens_here, mp_count, column_share), 1, 0
    )
    branch_own = reduced_share(branch_sent, "mp").astype(jnp.bfloat16)
    branch = in_mesh_order(from_peers(branch_own, "mp"), mp_rank, 1).astype(jnp.float32)
    residual = input_full + residual_mult * branch
    scale_two = rms_scale(residual)
    moe_in = (residual * scale_two * norm_gain_moe).astype(jnp.bfloat16)
    logits = jnp.dot(moe_in, w_router, preferred_element_type=jnp.float32)
    expert_ids = jnp.arange(EXPERTS, dtype=jnp.int32)
    chosen = routes[:, :, None] == expert_ids[None, None, :]
    picked = jnp.sum(jnp.where(chosen, logits[:, None, :], 0.0), axis=2)
    gate_weights = jax.nn.softmax(picked, axis=-1)
    expert_hits = jnp.sum(chosen.astype(jnp.int32), axis=1)
    rank_table = jnp.cumsum(expert_hits, axis=0) - expert_hits
    pair_rank = jnp.sum(jnp.where(chosen, rank_table[:, None, :], 0), axis=2)
    pair_slot = (routes * capacity + pair_rank).reshape(-1)
    token_ids = jnp.arange(tokens_here, dtype=jnp.int32)
    token_fill = jnp.broadcast_to(token_ids[:, None], (tokens_here, route_width)).reshape(-1)
    slot_token = (
        jnp.full((EXPERTS * capacity,), tokens_here, jnp.int32).at[pair_slot].set(token_fill)
    )
    slot_gate = (
        jnp.zeros((EXPERTS * capacity,), jnp.float32).at[pair_slot].set(gate_weights.reshape(-1))
    )
    padded_moe = jnp.concatenate([moe_in, jnp.zeros((1, model_width), jnp.bfloat16)], axis=0)
    padded_grad = jnp.concatenate([out_grad, jnp.zeros((1, model_width), jnp.bfloat16)], axis=0)
    quarter = capacity // mp_count
    slot_begin = mp_rank * quarter
    token_part = lax.dynamic_slice_in_dim(
        slot_token.reshape(EXPERTS, capacity), slot_begin, quarter, 1
    ).reshape(-1)
    gate_part_slots = lax.dynamic_slice_in_dim(
        slot_gate.reshape(EXPERTS, capacity), slot_begin, quarter, 1
    ).reshape(-1)
    full_gate, full_up, full_down = turned_gather((w_gate, w_up, w_down), "mp", (2, 2, 1))
    outgoing = jnp.take(padded_moe, token_part, axis=0).reshape(EXPERTS, quarter, model_width)
    arrived = lax.all_to_all(outgoing, "dp", split_axis=0, concat_axis=0, tiled=True)
    held_slots = arrived.shape[1]
    grouped = arrived.reshape(dp_count, experts_here, held_slots, model_width)
    gate_pre = jnp.einsum("secd,edf->secf", grouped, full_gate, preferred_element_type=jnp.float32)
    up_pre = jnp.einsum("secd,edf->secf", grouped, full_up, preferred_element_type=jnp.float32)
    hidden_units = (jax.nn.silu(gate_pre) * up_pre).astype(jnp.bfloat16)
    rows_out = jnp.einsum(
        "secf,efd->secd", hidden_units, full_down, preferred_element_type=jnp.float32
    ).astype(jnp.bfloat16)
    rows_out, expert_in, gate_keep, up_keep = (
        rows_out.reshape(dp_count * experts_here, held_slots, model_width),
        arrived,
        gate_pre.reshape(dp_count * experts_here, held_slots, -1),
        up_pre.reshape(dp_count * experts_here, held_slots, -1),
    )
    returned = exchange_both(rows_out, ("dp", "mp"), ("dp", "mp"), (0, 2), (0, 1))
    slot_factor = (residual_mult * gate_part_slots)[:, None]
    outgoing_grad = (
        (jnp.take(padded_grad, token_part, axis=0).astype(jnp.float32) * slot_factor)
        .astype(jnp.bfloat16)
        .reshape(EXPERTS, quarter, model_width)
    )
    arrived_grad = lax.all_to_all(outgoing_grad, "dp", split_axis=0, concat_axis=0, tiled=True)
    shape_four = (dp_count, experts_here, quarter)
    gate_w_part, up_w_part, down_w_part, input_part = expert_back(
        expert_in.reshape(shape_four + (model_width,)),
        arrived_grad.reshape(shape_four + (model_width,)),
        gate_keep.reshape(shape_four + (gate_keep.shape[2],)),
        up_keep.reshape(shape_four + (up_keep.shape[2],)),
        full_gate,
        full_up,
        full_down,
    )
    grad_w_gate, grad_w_up, grad_w_down = (
        *tuple(
            (
                part.astype(jnp.float32)
                for part in in_one_piece_2(
                    (gate_w_part.astype(jnp.bfloat16), up_w_part.astype(jnp.bfloat16)), "mp", 2, 0
                )
            )
        ),
        lax.psum_scatter(
            down_w_part.astype(jnp.bfloat16), "mp", scatter_dimension=1, tiled=True
        ).astype(jnp.float32),
    )
    input_home = exchange_both(
        input_part.astype(jnp.bfloat16).reshape(dp_count * experts_here, quarter, model_width),
        ("dp", "mp"),
        ("dp", "mp"),
        (0, 2),
        (0, 1),
    )
    picked_rows = (
        jnp.take(returned.reshape(EXPERTS * capacity, column_share), pair_slot, axis=0)
        .reshape(tokens_here, route_width, column_share)
        .astype(jnp.float32)
    )
    mixture = jnp.sum(gate_weights[:, :, None] * picked_rows, axis=1)
    residual_cols = lax.dynamic_slice_in_dim(residual, column_start, column_share, 1)
    out_hidden = (residual_cols + residual_mult * mixture).astype(jnp.bfloat16)
    grad_full = out_grad.astype(jnp.float32)
    grad_own_cols = lax.dynamic_slice_in_dim(grad_full, column_start, column_share, 1)
    gate_part = residual_mult * jnp.sum(grad_own_cols[:, None, :] * picked_rows, axis=2)
    home_rows = jnp.take(
        input_home.reshape(EXPERTS * capacity, column_share), pair_slot, axis=0
    ).reshape(tokens_here, route_width, column_share)
    expert_grad_cols = jnp.sum(home_rows.astype(jnp.float32), axis=1)
    expert_grad = in_mesh_order(
        from_peers(expert_grad_cols.astype(jnp.bfloat16), "mp"), mp_rank, 1
    ).astype(jnp.float32)
    gate_total = sum(
        part.astype(jnp.float32) for part in from_peers(gate_part.astype(jnp.bfloat16), "mp")
    )
    select_grad = gate_weights * (
        gate_total - jnp.sum(gate_weights * gate_total, axis=-1, keepdims=True)
    )
    logit_grad = jnp.sum(jnp.where(chosen, select_grad[:, :, None], 0.0), axis=1).astype(
        jnp.bfloat16
    )
    moe_in_grad = expert_grad + times_transposed(logit_grad, w_router)
    router_grad = row_contract(moe_in, logit_grad)
    moe_gain_grad = jnp.sum(moe_in_grad * residual * scale_two, axis=0)
    residual_grad = grad_full + norm_back(residual, scale_two, norm_gain_moe, moe_in_grad)
    branch_grad = (residual_mult * residual_grad).astype(jnp.bfloat16)
    out_weight_grad = row_contract(attended, branch_grad)
    attended_grad = times_transposed(branch_grad, w_out).astype(jnp.bfloat16)
    key_grad_all = jnp.zeros((window, BLOCK, kv_here * HEAD_DIM), jnp.float32)
    value_grad_all = jnp.zeros((window, BLOCK, kv_here * HEAD_DIM), jnp.float32)
    local_block = 0
    packed_query = my_blocks[local_block]
    block_reach = my_offsets[local_block]
    query_block = queries
    block_lse = lse_blocks[local_block]
    grad_heads = attended_grad.reshape(BLOCK, kv_here, head_group, HEAD_DIM)

    def delta_step(
        key_step,
        accumulated,
        packed_query=packed_query,
        block_reach=block_reach,
        query_block=query_block,
        block_lse=block_lse,
        grad_heads=grad_heads,
    ):

        def delta_live(running_total):
            key_part, value_part, row_start = key_block(packed_query, key_step)
            prob_block = jnp.exp(
                block_scores(query_block, key_part, key_step) - block_lse[..., None]
            )
            value_heads = value_part.reshape(BLOCK, kv_here, HEAD_DIM)
            prob_grad = jnp.einsum(
                "qhgd,khd->hgqk", grad_heads, value_heads, preferred_element_type=jnp.float32
            )
            return running_total + jnp.sum(prob_block * prob_grad, axis=-1)

        return lax.cond(
            key_step <= block_reach, delta_live, lambda running_total: running_total, accumulated
        )

    delta_sum = lax.fori_loop(
        0, window, delta_step, jnp.zeros((kv_here, head_group, BLOCK), jnp.float32)
    )

    def grad_step(
        key_step,
        grad_carry,
        packed_query=packed_query,
        block_reach=block_reach,
        query_block=query_block,
        block_lse=block_lse,
        grad_heads=grad_heads,
        delta_sum=delta_sum,
    ):
        query_acc, key_acc, value_acc = grad_carry
        key_part, value_part, row_start = key_block(packed_query, key_step)

        def grad_live(unused):
            prob_block = jnp.exp(
                block_scores(query_block, key_part, key_step) - block_lse[..., None]
            )
            query_heads = query_block.reshape(BLOCK, kv_here, head_group, HEAD_DIM)
            key_heads = key_part.reshape(BLOCK, kv_here, HEAD_DIM)
            value_heads = value_part.reshape(BLOCK, kv_here, HEAD_DIM)
            prob_grad = jnp.einsum(
                "qhgd,khd->hgqk", grad_heads, value_heads, preferred_element_type=jnp.float32
            )
            score_grad = (prob_block * (prob_grad - delta_sum[..., None])).astype(jnp.bfloat16)
            query_add = (
                jnp.einsum(
                    "hgqk,khd->qhgd", score_grad, key_heads, preferred_element_type=jnp.float32
                )
                * score_mult
            )
            key_add = (
                jnp.einsum(
                    "hgqk,qhgd->khd", score_grad, query_heads, preferred_element_type=jnp.float32
                )
                * score_mult
            )
            value_add = jnp.einsum(
                "hgqk,qhgd->khd",
                prob_block.astype(jnp.bfloat16),
                grad_heads,
                preferred_element_type=jnp.float32,
            )
            return (
                query_add,
                key_add.reshape(BLOCK, kv_here * HEAD_DIM),
                value_add.reshape(BLOCK, kv_here * HEAD_DIM),
            )

        def dead(unused):
            return (
                jnp.zeros((BLOCK, kv_here, head_group, HEAD_DIM), jnp.float32),
                jnp.zeros((BLOCK, kv_here * HEAD_DIM), jnp.float32),
                jnp.zeros((BLOCK, kv_here * HEAD_DIM), jnp.float32),
            )

        query_add, key_add, value_add = lax.cond(key_step <= block_reach, grad_live, dead, 0)
        key_acc = lax.dynamic_update_index_in_dim(key_acc, key_add, row_start, 0)
        value_acc = lax.dynamic_update_index_in_dim(value_acc, value_add, row_start, 0)
        return (query_acc + query_add, key_acc, value_acc)

    start_grads = (
        jnp.zeros((BLOCK, kv_here, head_group, HEAD_DIM), jnp.float32),
        key_grad_all,
        value_grad_all,
    )
    query_acc, key_grad_all, value_grad_all = lax.fori_loop(0, window, grad_step, start_grads)
    query_grad_blocks = query_acc.reshape(BLOCK, kv_here * head_group * HEAD_DIM)
    kv_grads = jnp.concatenate([key_grad_all, value_grad_all], axis=2)
    later_grads = kv_grads[1:].astype(jnp.bfloat16)
    later_grads = later_grads.reshape(window - 1, dp_count, piece, kv_width)
    later_grads = jnp.moveaxis(later_grads, 1, 0).reshape(dp_count, -1, kv_width)
    gathered_grads = lax.all_to_all(later_grads, "dp", 0, 0, tiled=True)
    after = block_order[:, None] + back_steps[None, :]
    after_hit = after[:, :, None] == block_ids[None, None, :]
    after_from = jnp.sum(jnp.where(after_hit, inverse[None, None, :], 0), axis=2)
    after_reach = jnp.sum(jnp.where(after_hit, offsets[None, None, :], 0), axis=2)
    after_live = after_reach >= back_steps[None, :]
    rows_of = (after_from * (window - 1) + back_steps[None, :] - 1).reshape(-1)
    taken = jnp.take(
        gathered_grads.reshape(dp_count * (window - 1), piece, kv_width), rows_of, axis=0
    ).reshape(dp_count, window - 1, piece, kv_width)
    summed = jnp.sum(
        jnp.where(after_live[:, :, None, None], taken.astype(jnp.float32), 0.0), axis=1
    )
    home = lax.all_to_all(summed.astype(jnp.bfloat16), "dp", 0, 0, tiled=True)
    kv_grad_sum = kv_grads[0] + home.reshape(BLOCK, kv_width).astype(jnp.float32)
    key_grad_sum = kv_grad_sum[:, : key_rows.shape[1]]
    value_grad_sum = kv_grad_sum[:, key_rows.shape[1] :]
    query_pre_grad = rotate_back(query_grad_blocks, cosine, sine_table).astype(jnp.bfloat16)
    key_pre_grad = rotate_back(key_grad_sum, cosine, sine_table).astype(jnp.bfloat16)
    value_pre_grad = value_grad_sum.astype(jnp.bfloat16)
    normed_part = (
        times_transposed(query_pre_grad, w_query)
        + times_transposed(key_pre_grad, w_key)
        + times_transposed(value_pre_grad, w_value)
    )
    query_weight_grad = row_contract(normed, query_pre_grad)
    key_weight_grad = row_contract(normed, key_pre_grad)
    value_weight_grad = row_contract(normed, value_pre_grad)
    normed_sent = jnp.moveaxis(
        normed_part.astype(jnp.bfloat16).reshape(tokens_here, mp_count, column_share), 1, 0
    )
    normed_own = reduced_share(normed_sent, "mp").astype(jnp.bfloat16)
    normed_grad = in_mesh_order(from_peers(normed_own, "mp"), mp_rank, 1).astype(jnp.float32)
    attn_gain_grad = jnp.sum(normed_grad * input_full * scale_one, axis=0)
    hidden_grad_full = residual_grad + norm_back(input_full, scale_one, norm_gain_attn, normed_grad)
    grad_hidden = lax.dynamic_slice_in_dim(hidden_grad_full, column_start, column_share, 1)
    def share_rows(x):
        return x.astype(jnp.bfloat16).reshape(dp_count, x.shape[0] // dp_count, -1)

    early = reduced_share(
        jnp.concatenate(
            [
                share_rows(out_weight_grad.T),
                share_rows(router_grad),
                share_rows(moe_gain_grad[:, None]),
            ],
            axis=2,
        ),
        "dp",
    )
    late = reduced_share(
        jnp.concatenate(
            [
                share_rows(query_weight_grad),
                share_rows(key_weight_grad),
                share_rows(value_weight_grad),
                share_rows(attn_gain_grad[:, None]),
            ],
            axis=2,
        ),
        "dp",
    )
    q_end = query_weight_grad.shape[1]
    k_end = q_end + key_weight_grad.shape[1]
    v_end = k_end + value_weight_grad.shape[1]
    o_end = out_weight_grad.shape[0]
    reduced = (
        late[:, :q_end],
        late[:, q_end:k_end],
        late[:, k_end:v_end],
        early[:, :o_end].T,
        early[:, o_end : o_end + EXPERTS],
        late[:, v_end],
        early[:, o_end + EXPERTS],
    )
    (
        query_reduced,
        key_reduced,
        value_reduced,
        out_reduced,
        router_reduced,
        attn_gain_reduced,
        moe_gain_reduced,
    ) = reduced
    return (
        out_hidden,
        grad_hidden,
        query_reduced,
        key_reduced,
        value_reduced,
        out_reduced,
        attn_gain_reduced,
        moe_gain_reduced,
        router_reduced,
        grad_w_gate,
        grad_w_up,
        grad_w_down,
    )


def solution(mesh):
    in_specs = (
        P("dp", None),
        P(),
        P(),
        P("dp", None),
        P(),
        P(None, "mp"),
        P(None, "mp"),
        P(None, "mp"),
        P("mp", None),
        P(),
        P(),
        P("dp", None, "mp"),
        P("dp", None, "mp"),
        P("dp", "mp", None),
        P("dp", None),
    )
    out_specs = (
        P("dp", "mp"),
        P("dp", "mp"),
        P("dp", "mp"),
        P("dp", "mp"),
        P("dp", "mp"),
        P("mp", "dp"),
        P("dp"),
        P("dp"),
        P("dp", None),
        P("dp", None, "mp"),
        P("dp", None, "mp"),
        P("dp", "mp", None),
    )
    return jax.shard_map(
        per_device, mesh=mesh, in_specs=in_specs, out_specs=out_specs, check_vma=False
    )
```

```python
import jax
import jax.numpy as jnp
from jax import lax
from jax.experimental import pallas as pl
from jax.experimental.pallas import tpu as pltpu
from jax.sharding import PartitionSpec as P

HEAD_DIM = 64
EXPERTS = 32
BLOCK = 512
MAXLEN = 2048
CAP = 160


epsilon = 1e-06
residual_mult = 0.22
score_mult = 0.015625
rope_base = 10000.0
masked_score = -1e30


def in_one_piece(arrays, axis, dim, along):
    ends, at = ([], 0)
    for a in arrays[:-1]:
        at += a.shape[along]
        ends.append(at)
    both = jnp.concatenate(arrays, axis=along)
    return tuple(jnp.split(lax.all_gather(both, axis, axis=dim, tiled=True), ends, axis=along))


def gathered_total(x, axis):
    parts = lax.all_gather(x, axis).astype(jnp.float32)
    return parts.sum(axis=0)


def turned_gather(arrays, axis, dims):
    turned = [jnp.moveaxis(a, dim, 0) for a, dim in zip(arrays, dims)]
    both = jnp.concatenate([t.reshape(len(t), -1) for t in turned], axis=1)
    result, at, finished = (lax.all_gather(both, axis, axis=0, tiled=True), 0, [])
    for t, dim in zip(turned, dims):
        share = result[:, at : at + t[0].size].reshape(-1, *t.shape[1:])
        finished.append(jnp.moveaxis(share, 0, dim))
        at += t[0].size
    return tuple(finished)


def in_blocks(x, dim, length):
    before, after = (x.shape[:dim], x.shape[dim + 1 :])
    return jnp.moveaxis(x.reshape(*before, length, -1, *after), dim, 0)


def laid_out(parts, dim):
    dims = list(parts.shape[1:])
    dims[dim] *= parts.shape[0]
    return jnp.moveaxis(parts, 0, dim).reshape(dims)


def exchange_both(x, axis, axes, splits, concats):
    sizes = [lax.axis_size(a) for a in axes]
    parts = in_blocks(x, splits[0], sizes[0])
    parts = jnp.moveaxis(in_blocks(parts, splits[1] + 1, sizes[1]), 0, 1)
    inside = parts.shape[2:]
    parts = parts.reshape(-1, *inside)
    parts = lax.all_to_all(parts, axis, split_axis=0, concat_axis=0, tiled=True)
    parts = laid_out(parts.reshape(*sizes, *inside), concats[0] + 1)
    return laid_out(parts, concats[1])


def in_one_piece_2(arrays, axis, dim, along):
    ends, at = ([], 0)
    for a in arrays[:-1]:
        at += a.shape[along]
        ends.append(at)
    both = jnp.concatenate(arrays, axis=along)
    return tuple(
        jnp.split(lax.psum_scatter(both, axis, scatter_dimension=dim, tiled=True), ends, axis=along)
    )


def sent_to_all(x, axis):
    length = lax.axis_size(axis)
    return lax.all_to_all(jnp.broadcast_to(x[None], (length, *x.shape)), axis, 0, 0, tiled=True)


def gathered_copies(x, axis, dim):
    parts = sent_to_all(x, axis)
    return laid_out(parts, dim)


def in_one_piece_3(arrays, axis, dim, along):
    columns = [a.reshape(*a.shape[:along], -1) for a in arrays]
    both = jnp.concatenate(columns, axis=along)
    result, at, finished = (lax.psum_scatter(both, axis, scatter_dimension=dim, tiled=True), 0, [])
    for a, column in zip(arrays, columns):
        share = result[..., at : at + column.shape[along]]
        finished.append(share.reshape(*share.shape[:along], *a.shape[along:]))
        at += column.shape[along]
    return tuple(finished)


def from_peers(x, axis):
    got = [x]
    for flip in (1, 2, 3):
        got.append(lax.ppermute(x, axis, [(i, i ^ flip) for i in range(4)]))
    return got


def in_mesh_order(parts, rank, dim):
    stacked = jnp.stack(parts)
    order = jnp.arange(4, dtype=jnp.int32) ^ rank
    return laid_out(jnp.take(stacked, order, axis=0), dim)


def reduced_share(x, axis):
    parts = lax.all_to_all(x, axis, 0, 0, tiled=True)
    return jnp.sum(parts.astype(jnp.float32), axis=0)


def rms_scale(row_values):
    return lax.rsqrt(jnp.mean(row_values * row_values, axis=-1, keepdims=True) + epsilon)


def norm_back(row_values, norm_scale, gain_values, incoming):
    weighted = incoming * gain_values
    inner_mean = jnp.mean(weighted * row_values, axis=-1, keepdims=True)
    return norm_scale * weighted - row_values * (norm_scale * norm_scale * norm_scale) * inner_mean


def rope_tables(positions):
    half_dim = HEAD_DIM // 2
    frequency = rope_base ** (-(jnp.arange(half_dim, dtype=jnp.float32) * 2.0) / HEAD_DIM)
    angles = positions.astype(jnp.float32)[:, None] * frequency[None, :]
    return (jnp.cos(angles), jnp.sin(angles))


def rotate(row_values, cosine, sine_table):
    half_dim = HEAD_DIM // 2
    shaped = row_values.reshape(row_values.shape[0], row_values.shape[1] // HEAD_DIM, HEAD_DIM)
    front_half = shaped[:, :, :half_dim]
    back_half = shaped[:, :, half_dim:]
    cosine_wide = cosine[:, None, :]
    sine_wide = sine_table[:, None, :]
    turned = jnp.concatenate(
        [
            front_half * cosine_wide - back_half * sine_wide,
            back_half * cosine_wide + front_half * sine_wide,
        ],
        axis=-1,
    )
    return turned.reshape(row_values.shape)


def rotate_back(row_values, cosine, sine_table):
    half_dim = HEAD_DIM // 2
    shaped = row_values.reshape(row_values.shape[0], row_values.shape[1] // HEAD_DIM, HEAD_DIM)
    front_half = shaped[:, :, :half_dim]
    back_half = shaped[:, :, half_dim:]
    cosine_wide = cosine[:, None, :]
    sine_wide = sine_table[:, None, :]
    turned = jnp.concatenate(
        [
            front_half * cosine_wide + back_half * sine_wide,
            back_half * cosine_wide - front_half * sine_wide,
        ],
        axis=-1,
    )
    return turned.reshape(row_values.shape)


def block_tables(lengths, block_order):
    block_ids = jnp.arange(block_order.shape[0], dtype=jnp.int32)
    sequence_ids = jnp.arange(lengths.shape[0], dtype=jnp.int32)
    sequence_ends = jnp.cumsum(lengths)
    sequence_starts = sequence_ends - lengths
    sequence_of = jnp.sum((sequence_ends[None, :] <= block_ids[:, None]).astype(jnp.int32), axis=1)
    begins = jnp.sum(
        jnp.where(sequence_of[:, None] == sequence_ids[None, :], sequence_starts[None, :], 0),
        axis=1,
    )
    offsets = block_ids - begins
    inverse = jnp.sum(
        jnp.where(block_order[None, :] == block_ids[:, None], block_ids[None, :], 0), axis=1
    )
    return (offsets, inverse)


def row_contract(left_side, right_side):
    return lax.dot_general(
        left_side, right_side, (((0,), (0,)), ((), ())), preferred_element_type=jnp.float32
    )


def times_transposed(left_side, right_side):
    return lax.dot_general(
        left_side, right_side, (((1,), (1,)), ((), ())), preferred_element_type=jnp.float32
    )


def padded_columns(rows_t, out_ref):
    zero = jnp.zeros((HEAD_DIM, rows_t.shape[1]), out_ref.dtype)
    for h in range(4):
        mine = rows_t[h * HEAD_DIM : (h + 1) * HEAD_DIM].astype(out_ref.dtype)
        at = (h // 2) * HEAD_DIM
        out_ref[h, pl.ds(at, HEAD_DIM), :] = mine
        out_ref[h, pl.ds(HEAD_DIM - at, HEAD_DIM), :] = zero


def padded_rows(rows, out_ref):
    n = rows.shape[0]
    lane = lax.broadcasted_iota(jnp.int32, (n, 128), 1)
    for h in range(4):
        pair = rows[:, (h // 2) * 128 : (h // 2) * 128 + 128].astype(jnp.float32)
        if h % 2 != h // 2:
            pair = pltpu.roll(pair, HEAD_DIM, 1)
        own = (lane < HEAD_DIM) if h // 2 == 0 else (lane >= HEAD_DIM)
        out_ref[pl.ds(h * n, n), :] = jnp.where(own, pair, 0.0).astype(out_ref.dtype)


def attend_kernel(reach_ref, q_ref, own_ref, prev_ref, att_ref, out_t_ref, lse_ref, qpad_ref, max_ref, sum_ref):
    q_t = jnp.transpose(q_ref[...].astype(jnp.float32) * score_mult)
    padded_columns(q_t, qpad_ref)
    half = BLOCK // 2

    def block(key_rows, value_rows, first):
        for h in range(4):
            group = (h // 2) * HEAD_DIM
            for t in range(2):
                cols = slice(t * half, (t + 1) * half)
                rows = half if first and t == 0 else BLOCK
                scores = jnp.dot(
                    key_rows[:rows], qpad_ref[h, :, cols], preferred_element_type=jnp.float32
                )
                if first:
                    key_at = lax.broadcasted_iota(jnp.int32, scores.shape, 0)
                    query_at = lax.broadcasted_iota(jnp.int32, scores.shape, 1) + t * half
                    scores = jnp.where(key_at > query_at, masked_score, scores)
                new_max = jnp.max(scores, axis=0, keepdims=True)
                if not first:
                    old_max = max_ref[h : h + 1, cols]
                    new_max = jnp.maximum(new_max, old_max)
                    shrink = jnp.exp(old_max - new_max)
                weights = jnp.exp(scores - new_max)
                total = jnp.sum(weights, axis=0, keepdims=True)
                part = lax.dot_general(
                    value_rows[:rows],
                    weights.astype(jnp.bfloat16),
                    (((0,), (0,)), ((), ())),
                    preferred_element_type=jnp.float32,
                )[group : group + HEAD_DIM]
                mine = pl.ds(h * HEAD_DIM, HEAD_DIM)
                if not first:
                    total = total + sum_ref[h : h + 1, cols] * shrink
                    part = part + out_t_ref[mine, cols] * shrink
                max_ref[h : h + 1, cols] = new_max
                sum_ref[h : h + 1, cols] = total
                out_t_ref[mine, cols] = part

    block(own_ref[:, :128], own_ref[:, 128:], True)

    @pl.loop(1, reach_ref[0] + 1)
    def _(step):
        rows = prev_ref[:, pl.ds(step - 1, 1)].reshape(BLOCK, 256)
        block(rows[:, :128], rows[:, 128:], False)

    lse_ref[...] = jnp.zeros_like(lse_ref)
    lse_ref[0:4, :] = max_ref[0:4, :] + jnp.log(sum_ref[0:4, :])
    for h in range(4):
        mine = pl.ds(h * HEAD_DIM, HEAD_DIM)
        out_t_ref[mine, :] = out_t_ref[mine, :] / sum_ref[h : h + 1, :]
    att_ref[...] = jnp.transpose(out_t_ref[...]).astype(jnp.bfloat16)


def attend(reach, queries, own_kv, earlier):
    vmem = pl.BlockSpec(memory_space=pltpu.VMEM)
    return pl.pallas_call(
        attend_kernel,
        name="attend",
        in_specs=[pl.BlockSpec(memory_space=pltpu.SMEM), vmem, vmem, vmem],
        out_specs=[vmem] * 3,
        out_shape=(
            jax.ShapeDtypeStruct((BLOCK, 256), jnp.bfloat16),
            jax.ShapeDtypeStruct((256, BLOCK), jnp.float32),
            jax.ShapeDtypeStruct((8, BLOCK), jnp.float32),
        ),
        scratch_shapes=[
            pltpu.VMEM((4, 128, BLOCK), jnp.bfloat16),
            pltpu.VMEM((8, BLOCK), jnp.float32),
            pltpu.VMEM((8, BLOCK), jnp.float32),
        ],
        compiler_params=pltpu.CompilerParams(vmem_limit_bytes=40 << 20),
        cost_estimate=pl.CostEstimate(
            flops=5_000_000_000, bytes_accessed=3_000_000, transcendentals=3_000_000
        ),
    )(reach, queries, own_kv, earlier)


def rotated_back(rows, cosine, signed_sine):
    lane = lax.broadcasted_iota(jnp.int32, (rows.shape[0], 128), 1)
    front = (lane % HEAD_DIM) < HEAD_DIM // 2
    done = []
    for at in range(0, rows.shape[1], 128):
        chunk = rows[:, at : at + 128]
        partner = jnp.where(front, pltpu.roll(chunk, 96, 1), pltpu.roll(chunk, 32, 1))
        done.append(chunk * cosine - partner * signed_sine)
    return done


def attend_back_kernel(
    reach_ref, q_ref, own_ref, prev_ref, grad_ref, grad_t_ref, out_t_ref, lse_ref, cos_ref, sin_ref,
    qgrad_ref, own_grad_ref, prev_grad_ref,
    qpad_ref, gpad_ref, qrows_ref, grows_ref, ds_ref, p_ref, delta_ref, dq_ref,
):
    half = BLOCK // 2
    q_scaled = q_ref[...].astype(jnp.float32) * score_mult
    padded_columns(jnp.transpose(q_scaled), qpad_ref)
    padded_rows(q_scaled, qrows_ref)
    padded_columns(grad_t_ref[...], gpad_ref)
    padded_rows(grad_ref[...], grows_ref)
    both = grad_t_ref[...].astype(jnp.float32) * out_t_ref[...]
    for h in range(4):
        delta_ref[h : h + 1, :] = jnp.sum(
            both[h * HEAD_DIM : (h + 1) * HEAD_DIM], axis=0, keepdims=True
        )

    def block(key_rows, value_rows, first):
        for h in range(4):
            for t in range(2):
                cols = slice(t * half, (t + 1) * half)
                wide = slice(h * BLOCK + t * half, h * BLOCK + (t + 1) * half)
                rows = half if first and t == 0 else BLOCK
                scores = jnp.dot(
                    key_rows[:rows], qpad_ref[h, :, cols], preferred_element_type=jnp.float32
                )
                weights = jnp.exp(scores - lse_ref[h : h + 1, cols])
                if first:
                    key_at = lax.broadcasted_iota(jnp.int32, scores.shape, 0)
                    query_at = lax.broadcasted_iota(jnp.int32, scores.shape, 1) + t * half
                    weights = jnp.where(key_at > query_at, 0.0, weights)
                weight_grad = jnp.dot(
                    value_rows[:rows], gpad_ref[h, :, cols], preferred_element_type=jnp.float32
                )
                score_grad = weights * (weight_grad - delta_ref[h : h + 1, cols])
                p_ref[:rows, wide] = weights.astype(jnp.bfloat16)
                ds_ref[:rows, wide] = score_grad.astype(jnp.bfloat16)
                if rows < BLOCK:
                    p_ref[rows:, wide] = jnp.zeros((BLOCK - rows, half), jnp.bfloat16)
                    ds_ref[rows:, wide] = jnp.zeros((BLOCK - rows, half), jnp.bfloat16)
        key_grad = jnp.dot(ds_ref[...], qrows_ref[...], preferred_element_type=jnp.float32)
        value_grad = jnp.dot(p_ref[...], grows_ref[...], preferred_element_type=jnp.float32)
        for h in range(4):
            group = (h // 2) * HEAD_DIM
            mine = pl.ds(h * HEAD_DIM, HEAD_DIM)
            part = lax.dot_general(
                key_rows,
                ds_ref[:, h * BLOCK : (h + 1) * BLOCK],
                (((0,), (0,)), ((), ())),
                preferred_element_type=jnp.float32,
            )[group : group + HEAD_DIM]
            if first:
                dq_ref[mine, :] = part
            else:
                dq_ref[mine, :] = dq_ref[mine, :] + part
        return key_grad, value_grad

    key_grad, value_grad = block(own_ref[:, :128], own_ref[:, 128:], True)
    own_grad_ref[:, :128] = key_grad
    own_grad_ref[:, 128:] = value_grad

    @pl.loop(1, reach_ref[0] + 1)
    def _(step):
        rows = prev_ref[:, pl.ds(step - 1, 1)].reshape(BLOCK, 256)
        key_grad, value_grad = block(rows[:, :128], rows[:, 128:], False)
        parts = prev_grad_ref.shape[0]
        shape = (parts, 1, BLOCK // parts, 128)
        prev_grad_ref[:, pl.ds(step - 1, 1), :, 0:128] = key_grad.astype(jnp.bfloat16).reshape(shape)
        prev_grad_ref[:, pl.ds(step - 1, 1), :, 128:256] = value_grad.astype(jnp.bfloat16).reshape(shape)

    turned = rotated_back(jnp.transpose(dq_ref[...]) * score_mult, cos_ref[...], sin_ref[...])
    for i, chunk in enumerate(turned):
        qgrad_ref[:, i * 128 : (i + 1) * 128] = chunk.astype(jnp.bfloat16)


def attend_back(reach, queries, own_kv, earlier, grad, grad_t, out_t, lse, cosine, signed_sine):
    vmem = pl.BlockSpec(memory_space=pltpu.VMEM)
    return pl.pallas_call(
        attend_back_kernel,
        name="attend_back",
        in_specs=[pl.BlockSpec(memory_space=pltpu.SMEM)] + [vmem] * 9,
        out_specs=[vmem] * 3,
        out_shape=(
            jax.ShapeDtypeStruct((BLOCK, 256), jnp.bfloat16),
            jax.ShapeDtypeStruct((BLOCK, 256), jnp.float32),
            jax.ShapeDtypeStruct(earlier.shape, jnp.bfloat16),
        ),
        scratch_shapes=[
            pltpu.VMEM((4, 128, BLOCK), jnp.bfloat16),
            pltpu.VMEM((4, 128, BLOCK), jnp.bfloat16),
            pltpu.VMEM((4 * BLOCK, 128), jnp.bfloat16),
            pltpu.VMEM((4 * BLOCK, 128), jnp.bfloat16),
            pltpu.VMEM((BLOCK, 4 * BLOCK), jnp.bfloat16),
            pltpu.VMEM((BLOCK, 4 * BLOCK), jnp.bfloat16),
            pltpu.VMEM((8, BLOCK), jnp.float32),
            pltpu.VMEM((256, BLOCK), jnp.float32),
        ],
        compiler_params=pltpu.CompilerParams(vmem_limit_bytes=48 << 20),
        cost_estimate=pl.CostEstimate(
            flops=12_000_000_000, bytes_accessed=5_000_000, transcendentals=3_000_000
        ),
    )(reach, queries, own_kv, earlier, grad, grad_t, out_t, lse, cosine, signed_sine)


def expert_back(grouped_in, grouped_grad, gate_pre, up_pre, gate_mat, up_mat, down_mat):
    sigmoid_gate = jax.nn.sigmoid(gate_pre)
    silu_gate = jax.nn.silu(gate_pre)
    hidden_units = (silu_gate * up_pre).astype(jnp.bfloat16)
    down_grad = jnp.einsum(
        "secf,secd->efd", hidden_units, grouped_grad, preferred_element_type=jnp.float32
    )
    hidden_grad = jnp.einsum(
        "secd,efd->secf", grouped_grad, down_mat, preferred_element_type=jnp.float32
    )
    gate_pre_grad = (
        hidden_grad * up_pre * sigmoid_gate * (1.0 + gate_pre * (1.0 - sigmoid_gate))
    ).astype(jnp.bfloat16)
    up_pre_grad = (hidden_grad * silu_gate).astype(jnp.bfloat16)
    gate_w_grad = jnp.einsum(
        "secd,secf->edf", grouped_in, gate_pre_grad, preferred_element_type=jnp.float32
    )
    up_w_grad = jnp.einsum(
        "secd,secf->edf", grouped_in, up_pre_grad, preferred_element_type=jnp.float32
    )
    input_part = jnp.einsum(
        "secf,edf->secd", gate_pre_grad, gate_mat, preferred_element_type=jnp.float32
    ) + jnp.einsum("secf,edf->secd", up_pre_grad, up_mat, preferred_element_type=jnp.float32)
    return (gate_w_grad, up_w_grad, down_grad, input_part)


def per_device(
    hidden_in,
    lengths,
    block_order,
    routes,
    norm_gain_attn,
    w_query,
    w_key,
    w_value,
    w_out,
    norm_gain_moe,
    w_router,
    w_gate,
    w_up,
    w_down,
    out_grad,
):
    dp_count = lax.axis_size("dp")
    mp_count = lax.axis_size("mp")
    dp_rank = lax.axis_index("dp")
    mp_rank = lax.axis_index("mp")
    tokens_here = hidden_in.shape[0]
    model_width = hidden_in.shape[1]
    column_share = model_width // mp_count
    column_start = mp_rank * column_share
    blocks_here = tokens_here // BLOCK
    window = MAXLEN // BLOCK
    kv_here = w_key.shape[1] // HEAD_DIM
    head_group = w_query.shape[1] // HEAD_DIM // kv_here
    experts_here = w_gate.shape[0]
    route_width = routes.shape[1]
    capacity = CAP
    offsets, inverse = block_tables(lengths, block_order)
    block_ids = jnp.arange(block_order.shape[0], dtype=jnp.int32)
    my_blocks = lax.dynamic_slice_in_dim(block_order, dp_rank * blocks_here, blocks_here)
    my_offsets = jnp.sum(
        jnp.where(my_blocks[:, None] == block_ids[None, :], offsets[None, :], 0), axis=1
    )
    row_ids = jnp.arange(BLOCK, dtype=jnp.int32)
    positions = (my_offsets[:, None] * BLOCK + row_ids[None, :]).reshape(-1)
    cosine, sine_table = rope_tables(positions)
    later_keys = row_ids[None, :] > row_ids[:, None]
    input_full = hidden_in.astype(jnp.float32)
    scale_one = rms_scale(input_full)
    normed = (input_full * scale_one * norm_gain_attn).astype(jnp.bfloat16)
    query_pre = jnp.dot(normed, w_query, preferred_element_type=jnp.float32)
    key_pre = jnp.dot(normed, w_key, preferred_element_type=jnp.float32)
    value_pre = jnp.dot(normed, w_value, preferred_element_type=jnp.float32)
    queries = rotate(query_pre, cosine, sine_table).astype(jnp.bfloat16)
    key_rows = rotate(key_pre, cosine, sine_table).astype(jnp.bfloat16)
    value_rows = value_pre.astype(jnp.bfloat16)
    piece = BLOCK // dp_count
    kv_width = key_rows.shape[1] + value_rows.shape[1]
    key_value = jnp.concatenate([key_rows, value_rows], axis=1)
    spread = lax.all_to_all(
        key_value.reshape(dp_count, piece, kv_width), "dp", 0, 0, tiled=True
    )
    back_steps = jnp.arange(1, window, dtype=jnp.int32)
    wanted = jnp.maximum(block_order[:, None] - back_steps[None, :], 0)
    wanted_from = jnp.sum(
        jnp.where(wanted[:, :, None] == block_ids[None, None, :], inverse[None, None, :], 0), axis=2
    )
    picked_kv = jnp.take(spread, wanted_from.reshape(-1), axis=0)
    earlier = lax.all_to_all(
        picked_kv.reshape(dp_count, (window - 1) * piece, kv_width), "dp", 0, 0, tiled=True
    )
    earlier = earlier.reshape(dp_count, window - 1, piece, kv_width)
    reach = my_offsets
    attended, attended_t, block_lse = attend(reach, queries, key_value, earlier)
    branch_part = jnp.dot(attended, w_out, preferred_element_type=jnp.float32)
    branch_sent = jnp.moveaxis(
        branch_part.astype(jnp.bfloat16).reshape(tokens_here, mp_count, column_share), 1, 0
    )
    branch_own = reduced_share(branch_sent, "mp").astype(jnp.bfloat16)
    branch = in_mesh_order(from_peers(branch_own, "mp"), mp_rank, 1).astype(jnp.float32)
    residual = input_full + residual_mult * branch
    scale_two = rms_scale(residual)
    moe_in = (residual * scale_two * norm_gain_moe).astype(jnp.bfloat16)
    logits = jnp.dot(moe_in, w_router, preferred_element_type=jnp.float32)
    expert_ids = jnp.arange(EXPERTS, dtype=jnp.int32)
    chosen = routes[:, :, None] == expert_ids[None, None, :]
    picked = jnp.sum(jnp.where(chosen, logits[:, None, :], 0.0), axis=2)
    gate_weights = jax.nn.softmax(picked, axis=-1)
    expert_hits = jnp.sum(chosen.astype(jnp.int32), axis=1)
    rank_table = jnp.cumsum(expert_hits, axis=0) - expert_hits
    pair_rank = jnp.sum(jnp.where(chosen, rank_table[:, None, :], 0), axis=2)
    pair_slot = (routes * capacity + pair_rank).reshape(-1)
    token_ids = jnp.arange(tokens_here, dtype=jnp.int32)
    token_fill = jnp.broadcast_to(token_ids[:, None], (tokens_here, route_width)).reshape(-1)
    slot_token = (
        jnp.full((EXPERTS * capacity,), tokens_here, jnp.int32).at[pair_slot].set(token_fill)
    )
    slot_gate = (
        jnp.zeros((EXPERTS * capacity,), jnp.float32).at[pair_slot].set(gate_weights.reshape(-1))
    )
    padded_moe = jnp.concatenate([moe_in, jnp.zeros((1, model_width), jnp.bfloat16)], axis=0)
    padded_grad = jnp.concatenate([out_grad, jnp.zeros((1, model_width), jnp.bfloat16)], axis=0)
    quarter = capacity // mp_count
    slot_begin = mp_rank * quarter
    token_part = lax.dynamic_slice_in_dim(
        slot_token.reshape(EXPERTS, capacity), slot_begin, quarter, 1
    ).reshape(-1)
    gate_part_slots = lax.dynamic_slice_in_dim(
        slot_gate.reshape(EXPERTS, capacity), slot_begin, quarter, 1
    ).reshape(-1)
    full_gate, full_up, full_down = turned_gather((w_gate, w_up, w_down), "mp", (2, 2, 1))
    outgoing = jnp.take(padded_moe, token_part, axis=0).reshape(EXPERTS, quarter, model_width)
    arrived = lax.all_to_all(outgoing, "dp", split_axis=0, concat_axis=0, tiled=True)
    held_slots = arrived.shape[1]
    grouped = arrived.reshape(dp_count, experts_here, held_slots, model_width)
    gate_pre = jnp.einsum("secd,edf->secf", grouped, full_gate, preferred_element_type=jnp.float32)
    up_pre = jnp.einsum("secd,edf->secf", grouped, full_up, preferred_element_type=jnp.float32)
    hidden_units = (jax.nn.silu(gate_pre) * up_pre).astype(jnp.bfloat16)
    rows_out = jnp.einsum(
        "secf,efd->secd", hidden_units, full_down, preferred_element_type=jnp.float32
    ).astype(jnp.bfloat16)
    rows_out, expert_in, gate_keep, up_keep = (
        rows_out.reshape(dp_count * experts_here, held_slots, model_width),
        arrived,
        gate_pre.reshape(dp_count * experts_here, held_slots, -1),
        up_pre.reshape(dp_count * experts_here, held_slots, -1),
    )
    returned = exchange_both(rows_out, ("dp", "mp"), ("dp", "mp"), (0, 2), (0, 1))
    slot_factor = (residual_mult * gate_part_slots)[:, None]
    outgoing_grad = (
        (jnp.take(padded_grad, token_part, axis=0).astype(jnp.float32) * slot_factor)
        .astype(jnp.bfloat16)
        .reshape(EXPERTS, quarter, model_width)
    )
    arrived_grad = lax.all_to_all(outgoing_grad, "dp", split_axis=0, concat_axis=0, tiled=True)
    shape_four = (dp_count, experts_here, quarter)
    gate_w_part, up_w_part, down_w_part, input_part = expert_back(
        expert_in.reshape(shape_four + (model_width,)),
        arrived_grad.reshape(shape_four + (model_width,)),
        gate_keep.reshape(shape_four + (gate_keep.shape[2],)),
        up_keep.reshape(shape_four + (up_keep.shape[2],)),
        full_gate,
        full_up,
        full_down,
    )
    grad_w_gate, grad_w_up, grad_w_down = (
        *tuple(
            (
                part.astype(jnp.float32)
                for part in in_one_piece_2(
                    (gate_w_part.astype(jnp.bfloat16), up_w_part.astype(jnp.bfloat16)), "mp", 2, 0
                )
            )
        ),
        lax.psum_scatter(
            down_w_part.astype(jnp.bfloat16), "mp", scatter_dimension=1, tiled=True
        ).astype(jnp.float32),
    )
    input_home = exchange_both(
        input_part.astype(jnp.bfloat16).reshape(dp_count * experts_here, quarter, model_width),
        ("dp", "mp"),
        ("dp", "mp"),
        (0, 2),
        (0, 1),
    )
    picked_rows = (
        jnp.take(returned.reshape(EXPERTS * capacity, column_share), pair_slot, axis=0)
        .reshape(tokens_here, route_width, column_share)
        .astype(jnp.float32)
    )
    mixture = jnp.sum(gate_weights[:, :, None] * picked_rows, axis=1)
    residual_cols = lax.dynamic_slice_in_dim(residual, column_start, column_share, 1)
    out_hidden = (residual_cols + residual_mult * mixture).astype(jnp.bfloat16)
    grad_full = out_grad.astype(jnp.float32)
    grad_own_cols = lax.dynamic_slice_in_dim(grad_full, column_start, column_share, 1)
    gate_part = residual_mult * jnp.sum(grad_own_cols[:, None, :] * picked_rows, axis=2)
    home_rows = jnp.take(
        input_home.reshape(EXPERTS * capacity, column_share), pair_slot, axis=0
    ).reshape(tokens_here, route_width, column_share)
    expert_grad_cols = jnp.sum(home_rows.astype(jnp.float32), axis=1)
    expert_grad = in_mesh_order(
        from_peers(expert_grad_cols.astype(jnp.bfloat16), "mp"), mp_rank, 1
    ).astype(jnp.float32)
    gate_total = sum(
        part.astype(jnp.float32) for part in from_peers(gate_part.astype(jnp.bfloat16), "mp")
    )
    select_grad = gate_weights * (
        gate_total - jnp.sum(gate_weights * gate_total, axis=-1, keepdims=True)
    )
    logit_grad = jnp.sum(jnp.where(chosen, select_grad[:, :, None], 0.0), axis=1).astype(
        jnp.bfloat16
    )
    moe_in_grad = expert_grad + times_transposed(logit_grad, w_router)
    router_grad = row_contract(moe_in, logit_grad)
    moe_gain_grad = jnp.sum(moe_in_grad * residual * scale_two, axis=0)
    residual_grad = grad_full + norm_back(residual, scale_two, norm_gain_moe, moe_in_grad)
    branch_grad = (residual_mult * residual_grad).astype(jnp.bfloat16)
    out_weight_grad = row_contract(attended, branch_grad)
    attended_grad = times_transposed(branch_grad, w_out).astype(jnp.bfloat16)
    attended_grad_t = times_transposed(w_out, branch_grad).astype(jnp.bfloat16)
    cosine_wide = jnp.tile(cosine, (1, 4))
    sine_wide = jnp.tile(jnp.concatenate([-sine_table, sine_table], axis=1), (1, 2))
    query_pre_grad, own_grads, later_grads = attend_back(
        reach,
        queries,
        key_value,
        earlier,
        attended_grad,
        attended_grad_t,
        attended_t,
        block_lse,
        cosine_wide,
        sine_wide,
    )
    later_grads = later_grads.reshape(dp_count, -1, kv_width)
    gathered_grads = lax.all_to_all(later_grads, "dp", 0, 0, tiled=True)
    after = block_order[:, None] + back_steps[None, :]
    after_hit = after[:, :, None] == block_ids[None, None, :]
    after_from = jnp.sum(jnp.where(after_hit, inverse[None, None, :], 0), axis=2)
    after_reach = jnp.sum(jnp.where(after_hit, offsets[None, None, :], 0), axis=2)
    after_live = after_reach >= back_steps[None, :]
    rows_of = (after_from * (window - 1) + back_steps[None, :] - 1).reshape(-1)
    taken = jnp.take(
        gathered_grads.reshape(dp_count * (window - 1), piece, kv_width), rows_of, axis=0
    ).reshape(dp_count, window - 1, piece, kv_width)
    summed = jnp.sum(
        jnp.where(after_live[:, :, None, None], taken.astype(jnp.float32), 0.0), axis=1
    )
    home = lax.all_to_all(summed.astype(jnp.bfloat16), "dp", 0, 0, tiled=True)
    kv_grad_sum = own_grads + home.reshape(BLOCK, kv_width).astype(jnp.float32)
    key_grad_sum = kv_grad_sum[:, : key_rows.shape[1]]
    value_grad_sum = kv_grad_sum[:, key_rows.shape[1] :]
    key_pre_grad = rotate_back(key_grad_sum, cosine, sine_table).astype(jnp.bfloat16)
    value_pre_grad = value_grad_sum.astype(jnp.bfloat16)
    normed_part = (
        times_transposed(query_pre_grad, w_query)
        + times_transposed(key_pre_grad, w_key)
        + times_transposed(value_pre_grad, w_value)
    )
    query_weight_grad = row_contract(normed, query_pre_grad)
    key_weight_grad = row_contract(normed, key_pre_grad)
    value_weight_grad = row_contract(normed, value_pre_grad)
    normed_sent = jnp.moveaxis(
        normed_part.astype(jnp.bfloat16).reshape(tokens_here, mp_count, column_share), 1, 0
    )
    normed_own = reduced_share(normed_sent, "mp").astype(jnp.bfloat16)
    normed_grad = in_mesh_order(from_peers(normed_own, "mp"), mp_rank, 1).astype(jnp.float32)
    attn_gain_grad = jnp.sum(normed_grad * input_full * scale_one, axis=0)
    hidden_grad_full = residual_grad + norm_back(input_full, scale_one, norm_gain_attn, normed_grad)
    grad_hidden = lax.dynamic_slice_in_dim(hidden_grad_full, column_start, column_share, 1)
    def share_rows(x):
        return x.astype(jnp.bfloat16).reshape(dp_count, x.shape[0] // dp_count, -1)

    early = reduced_share(
        jnp.concatenate(
            [
                share_rows(out_weight_grad.T),
                share_rows(router_grad),
                share_rows(moe_gain_grad[:, None]),
            ],
            axis=2,
        ),
        "dp",
    )
    late = reduced_share(
        jnp.concatenate(
            [
                share_rows(query_weight_grad),
                share_rows(key_weight_grad),
                share_rows(value_weight_grad),
                share_rows(attn_gain_grad[:, None]),
            ],
            axis=2,
        ),
        "dp",
    )
    q_end = query_weight_grad.shape[1]
    k_end = q_end + key_weight_grad.shape[1]
    v_end = k_end + value_weight_grad.shape[1]
    o_end = out_weight_grad.shape[0]
    reduced = (
        late[:, :q_end],
        late[:, q_end:k_end],
        late[:, k_end:v_end],
        early[:, :o_end].T,
        early[:, o_end : o_end + EXPERTS],
        late[:, v_end],
        early[:, o_end + EXPERTS],
    )
    (
        query_reduced,
        key_reduced,
        value_reduced,
        out_reduced,
        router_reduced,
        attn_gain_reduced,
        moe_gain_reduced,
    ) = reduced
    return (
        out_hidden,
        grad_hidden,
        query_reduced,
        key_reduced,
        value_reduced,
        out_reduced,
        attn_gain_reduced,
        moe_gain_reduced,
        router_reduced,
        grad_w_gate,
        grad_w_up,
        grad_w_down,
    )


def solution(mesh):
    in_specs = (
        P("dp", None),
        P(),
        P(),
        P("dp", None),
        P(),
        P(None, "mp"),
        P(None, "mp"),
        P(None, "mp"),
        P("mp", None),
        P(),
        P(),
        P("dp", None, "mp"),
        P("dp", None, "mp"),
        P("dp", "mp", None),
        P("dp", None),
    )
    out_specs = (
        P("dp", "mp"),
        P("dp", "mp"),
        P("dp", "mp"),
        P("dp", "mp"),
        P("dp", "mp"),
        P("mp", "dp"),
        P("dp"),
        P("dp"),
        P("dp", None),
        P("dp", None, "mp"),
        P("dp", None, "mp"),
        P("dp", "mp", None),
    )
    return jax.shard_map(
        per_device, mesh=mesh, in_specs=in_specs, out_specs=out_specs, check_vma=False
    )
```

```python
import jax
import jax.numpy as jnp
import numpy as np
from jax import lax
from jax.experimental import pallas as pl
from jax.experimental.pallas import tpu as pltpu
from jax.sharding import PartitionSpec as P

HEAD_DIM = 64
EXPERTS = 32
BLOCK = 512
MAXLEN = 2048
CAP = 160


epsilon = 1e-06
residual_mult = 0.22
score_mult = 0.015625
rope_base = 10000.0
masked_score = -1e30


def from_peers(x, axis):
    got = [x]
    for flip in (1, 2, 3):
        got.append(lax.ppermute(x, axis, [(i, i ^ flip) for i in range(4)]))
    return got


def to_all(x, axis):
    return lax.all_to_all(x, axis, 0, 0, tiled=True)


def after(x, *others):
    return lax.optimization_barrier((x, *others))[0]


def rope_constants():
    frequency = rope_base ** (-(np.arange(HEAD_DIM // 2, dtype=np.float64) * 2.0) / HEAD_DIM)
    wide = np.tile(frequency, 4)[None, :]
    rows = np.arange(BLOCK, dtype=np.float64)[:, None] * wide
    starts = np.arange(MAXLEN // BLOCK, dtype=np.float64)[:, None] * BLOCK * wide
    return [a.astype(np.float32) for a in (np.cos(rows), np.sin(rows), np.cos(starts), np.sin(starts))]


def rope_wide(offset):
    cos_row, sin_row, cos_start, sin_start = [jnp.asarray(a) for a in rope_constants()]
    cos_at = lax.dynamic_slice_in_dim(cos_start, offset, 1, 0)
    sin_at = lax.dynamic_slice_in_dim(sin_start, offset, 1, 0)
    sign = np.where(np.arange(128) % HEAD_DIM < HEAD_DIM // 2, -1.0, 1.0).astype(np.float32)
    cosine = cos_row * cos_at - sin_row * sin_at
    sine = sin_row * cos_at + cos_row * sin_at
    return cosine, sine * sign[None, :]


def block_tables(lengths, block_order):
    block_ids = jnp.arange(block_order.shape[0], dtype=jnp.int32)
    sequence_ids = jnp.arange(lengths.shape[0], dtype=jnp.int32)
    sequence_ends = jnp.cumsum(lengths)
    sequence_starts = sequence_ends - lengths
    sequence_of = jnp.sum((sequence_ends[None, :] <= block_ids[:, None]).astype(jnp.int32), axis=1)
    begins = jnp.sum(
        jnp.where(sequence_of[:, None] == sequence_ids[None, :], sequence_starts[None, :], 0),
        axis=1,
    )
    offsets = block_ids - begins
    inverse = jnp.sum(
        jnp.where(block_order[None, :] == block_ids[:, None], block_ids[None, :], 0), axis=1
    )
    return (offsets, inverse)


def row_contract(left_side, right_side):
    return lax.dot_general(
        left_side, right_side, (((0,), (0,)), ((), ())), preferred_element_type=jnp.float32
    )


def times_transposed(left_side, right_side):
    return lax.dot_general(
        left_side, right_side, (((1,), (1,)), ((), ())), preferred_element_type=jnp.float32
    )


def padded_columns(rows_t, out_ref):
    zero = jnp.zeros((HEAD_DIM, rows_t.shape[1]), out_ref.dtype)
    for h in range(4):
        mine = rows_t[h * HEAD_DIM : (h + 1) * HEAD_DIM].astype(out_ref.dtype)
        at = (h // 2) * HEAD_DIM
        out_ref[h, pl.ds(at, HEAD_DIM), :] = mine
        out_ref[h, pl.ds(HEAD_DIM - at, HEAD_DIM), :] = zero


def padded_rows(rows, out_ref):
    n = rows.shape[0]
    lane = lax.broadcasted_iota(jnp.int32, (n, 128), 1)
    for h in range(4):
        pair = rows[:, (h // 2) * 128 : (h // 2) * 128 + 128].astype(jnp.float32)
        if h % 2 != h // 2:
            pair = pltpu.roll(pair, HEAD_DIM, 1)
        own = (lane < HEAD_DIM) if h // 2 == 0 else (lane >= HEAD_DIM)
        out_ref[pl.ds(h * n, n), :] = jnp.where(own, pair, 0.0).astype(out_ref.dtype)


def attend_kernel(reach_ref, q_ref, own_ref, prev_ref, att_ref, out_t_ref, lse_ref, qpad_ref, max_ref, sum_ref):
    q_t = jnp.transpose(q_ref[...].astype(jnp.float32) * score_mult)
    padded_columns(q_t, qpad_ref)
    half = BLOCK // 2

    def block(key_rows, value_rows, first):
        for h in range(4):
            group = (h // 2) * HEAD_DIM
            for t in range(2):
                cols = slice(t * half, (t + 1) * half)
                rows = half if first and t == 0 else BLOCK
                scores = jnp.dot(
                    key_rows[:rows], qpad_ref[h, :, cols], preferred_element_type=jnp.float32
                )
                if first:
                    key_at = lax.broadcasted_iota(jnp.int32, scores.shape, 0)
                    query_at = lax.broadcasted_iota(jnp.int32, scores.shape, 1) + t * half
                    scores = jnp.where(key_at > query_at, masked_score, scores)
                new_max = jnp.max(scores, axis=0, keepdims=True)
                if not first:
                    old_max = max_ref[h : h + 1, cols]
                    new_max = jnp.maximum(new_max, old_max)
                    shrink = jnp.exp(old_max - new_max)
                weights = jnp.exp(scores - new_max)
                total = jnp.sum(weights, axis=0, keepdims=True)
                part = lax.dot_general(
                    value_rows[:rows],
                    weights.astype(jnp.bfloat16),
                    (((0,), (0,)), ((), ())),
                    preferred_element_type=jnp.float32,
                )[group : group + HEAD_DIM]
                mine = pl.ds(h * HEAD_DIM, HEAD_DIM)
                if not first:
                    total = total + sum_ref[h : h + 1, cols] * shrink
                    part = part + out_t_ref[mine, cols] * shrink
                max_ref[h : h + 1, cols] = new_max
                sum_ref[h : h + 1, cols] = total
                out_t_ref[mine, cols] = part

    block(own_ref[:, :128], own_ref[:, 128:], True)

    @pl.loop(1, reach_ref[0] + 1)
    def _(step):
        rows = prev_ref[:, pl.ds(step - 1, 1)].reshape(BLOCK, 256)
        block(rows[:, :128], rows[:, 128:], False)

    lse_ref[...] = jnp.zeros_like(lse_ref)
    lse_ref[0:4, :] = max_ref[0:4, :] + jnp.log(sum_ref[0:4, :])
    for h in range(4):
        mine = pl.ds(h * HEAD_DIM, HEAD_DIM)
        out_t_ref[mine, :] = out_t_ref[mine, :] / sum_ref[h : h + 1, :]
    att_ref[...] = jnp.transpose(out_t_ref[...]).astype(jnp.bfloat16)


def attend(reach, queries, own_kv, earlier):
    vmem = pl.BlockSpec(memory_space=pltpu.VMEM)
    return pl.pallas_call(
        attend_kernel,
        name="attend",
        in_specs=[pl.BlockSpec(memory_space=pltpu.SMEM), vmem, vmem, vmem],
        out_specs=[vmem] * 3,
        out_shape=(
            jax.ShapeDtypeStruct((BLOCK, 256), jnp.bfloat16),
            jax.ShapeDtypeStruct((256, BLOCK), jnp.float32),
            jax.ShapeDtypeStruct((8, BLOCK), jnp.float32),
        ),
        scratch_shapes=[
            pltpu.VMEM((4, 128, BLOCK), jnp.bfloat16),
            pltpu.VMEM((8, BLOCK), jnp.float32),
            pltpu.VMEM((8, BLOCK), jnp.float32),
        ],
        compiler_params=pltpu.CompilerParams(vmem_limit_bytes=40 << 20),
        cost_estimate=pl.CostEstimate(
            flops=5_000_000_000, bytes_accessed=3_000_000, transcendentals=3_000_000
        ),
    )(reach, queries, own_kv, earlier)


def rotated_back(rows, cosine, signed_sine):
    lane = lax.broadcasted_iota(jnp.int32, (rows.shape[0], 128), 1)
    front = (lane % HEAD_DIM) < HEAD_DIM // 2
    done = []
    for at in range(0, rows.shape[1], 128):
        chunk = rows[:, at : at + 128]
        partner = jnp.where(front, pltpu.roll(chunk, 96, 1), pltpu.roll(chunk, 32, 1))
        done.append(chunk * cosine - partner * signed_sine)
    return done


def attend_back_kernel(
    reach_ref, q_ref, own_ref, prev_ref, grad_ref, grad_t_ref, out_t_ref, lse_ref, cos_ref, sin_ref,
    qgrad_ref, own_grad_ref, prev_grad_ref,
    qpad_ref, gpad_ref, qrows_ref, grows_ref, ds_ref, p_ref, delta_ref, dq_ref,
):
    half = BLOCK // 2
    q_scaled = q_ref[...].astype(jnp.float32) * score_mult
    padded_columns(jnp.transpose(q_scaled), qpad_ref)
    padded_rows(q_scaled, qrows_ref)
    padded_columns(grad_t_ref[...], gpad_ref)
    padded_rows(grad_ref[...], grows_ref)
    both = grad_t_ref[...].astype(jnp.float32) * out_t_ref[...]
    for h in range(4):
        delta_ref[h : h + 1, :] = jnp.sum(
            both[h * HEAD_DIM : (h + 1) * HEAD_DIM], axis=0, keepdims=True
        )

    def block(key_rows, value_rows, first):
        for h in range(4):
            for t in range(2):
                cols = slice(t * half, (t + 1) * half)
                wide = slice(h * BLOCK + t * half, h * BLOCK + (t + 1) * half)
                rows = half if first and t == 0 else BLOCK
                scores = jnp.dot(
                    key_rows[:rows], qpad_ref[h, :, cols], preferred_element_type=jnp.float32
                )
                weights = jnp.exp(scores - lse_ref[h : h + 1, cols])
                if first:
                    key_at = lax.broadcasted_iota(jnp.int32, scores.shape, 0)
                    query_at = lax.broadcasted_iota(jnp.int32, scores.shape, 1) + t * half
                    weights = jnp.where(key_at > query_at, 0.0, weights)
                weight_grad = jnp.dot(
                    value_rows[:rows], gpad_ref[h, :, cols], preferred_element_type=jnp.float32
                )
                score_grad = weights * (weight_grad - delta_ref[h : h + 1, cols])
                p_ref[:rows, wide] = weights.astype(jnp.bfloat16)
                ds_ref[:rows, wide] = score_grad.astype(jnp.bfloat16)
                if rows < BLOCK:
                    p_ref[rows:, wide] = jnp.zeros((BLOCK - rows, half), jnp.bfloat16)
                    ds_ref[rows:, wide] = jnp.zeros((BLOCK - rows, half), jnp.bfloat16)
        key_grad = jnp.dot(ds_ref[...], qrows_ref[...], preferred_element_type=jnp.float32)
        value_grad = jnp.dot(p_ref[...], grows_ref[...], preferred_element_type=jnp.float32)
        for h in range(4):
            group = (h // 2) * HEAD_DIM
            mine = pl.ds(h * HEAD_DIM, HEAD_DIM)
            part = lax.dot_general(
                key_rows,
                ds_ref[:, h * BLOCK : (h + 1) * BLOCK],
                (((0,), (0,)), ((), ())),
                preferred_element_type=jnp.float32,
            )[group : group + HEAD_DIM]
            if first:
                dq_ref[mine, :] = part
            else:
                dq_ref[mine, :] = dq_ref[mine, :] + part
        return key_grad, value_grad

    key_grad, value_grad = block(own_ref[:, :128], own_ref[:, 128:], True)
    own_grad_ref[:, :128] = key_grad
    own_grad_ref[:, 128:] = value_grad

    @pl.loop(1, reach_ref[0] + 1)
    def _(step):
        rows = prev_ref[:, pl.ds(step - 1, 1)].reshape(BLOCK, 256)
        key_grad, value_grad = block(rows[:, :128], rows[:, 128:], False)
        parts = prev_grad_ref.shape[0]
        shape = (parts, 1, BLOCK // parts, 128)
        prev_grad_ref[:, pl.ds(step - 1, 1), :, 0:128] = key_grad.astype(jnp.bfloat16).reshape(shape)
        prev_grad_ref[:, pl.ds(step - 1, 1), :, 128:256] = value_grad.astype(jnp.bfloat16).reshape(shape)

    turned = rotated_back(jnp.transpose(dq_ref[...]) * score_mult, cos_ref[...], sin_ref[...])
    for i, chunk in enumerate(turned):
        qgrad_ref[:, i * 128 : (i + 1) * 128] = chunk.astype(jnp.bfloat16)


def attend_back(reach, queries, own_kv, earlier, grad, grad_t, out_t, lse, cosine, signed_sine):
    vmem = pl.BlockSpec(memory_space=pltpu.VMEM)
    return pl.pallas_call(
        attend_back_kernel,
        name="attend_back",
        in_specs=[pl.BlockSpec(memory_space=pltpu.SMEM)] + [vmem] * 9,
        out_specs=[vmem] * 3,
        out_shape=(
            jax.ShapeDtypeStruct((BLOCK, 256), jnp.bfloat16),
            jax.ShapeDtypeStruct((BLOCK, 256), jnp.float32),
            jax.ShapeDtypeStruct(earlier.shape, jnp.bfloat16),
        ),
        scratch_shapes=[
            pltpu.VMEM((4, 128, BLOCK), jnp.bfloat16),
            pltpu.VMEM((4, 128, BLOCK), jnp.bfloat16),
            pltpu.VMEM((4 * BLOCK, 128), jnp.bfloat16),
            pltpu.VMEM((4 * BLOCK, 128), jnp.bfloat16),
            pltpu.VMEM((BLOCK, 4 * BLOCK), jnp.bfloat16),
            pltpu.VMEM((BLOCK, 4 * BLOCK), jnp.bfloat16),
            pltpu.VMEM((8, BLOCK), jnp.float32),
            pltpu.VMEM((256, BLOCK), jnp.float32),
        ],
        compiler_params=pltpu.CompilerParams(vmem_limit_bytes=48 << 20),
        cost_estimate=pl.CostEstimate(
            flops=12_000_000_000, bytes_accessed=5_000_000, transcendentals=3_000_000
        ),
    )(reach, queries, own_kv, earlier, grad, grad_t, out_t, lse, cosine, signed_sine)


def whole_vmem():
    return pl.BlockSpec(memory_space=pltpu.VMEM)


def in_smem():
    return pl.BlockSpec(memory_space=pltpu.SMEM)


def rotated(rows, cosine, signed_sine):
    lane = lax.broadcasted_iota(jnp.int32, (rows.shape[0], 128), 1)
    front = (lane % HEAD_DIM) < HEAD_DIM // 2
    done = []
    for at in range(0, rows.shape[1], 128):
        chunk = rows[:, at : at + 128]
        partner = jnp.where(front, pltpu.roll(chunk, 96, 1), pltpu.roll(chunk, 32, 1))
        done.append(chunk * cosine + partner * signed_sine)
    return done


def project_kernel(x_ref, gain_ref, wq_ref, wk_ref, wv_ref, cos_ref, sin_ref, normed_ref, q_ref, kv_ref):
    x = x_ref[...].astype(jnp.float32)
    scale = lax.rsqrt(jnp.mean(x * x, axis=1, keepdims=True) + epsilon)
    normed = (x * scale * gain_ref[...]).astype(jnp.bfloat16)
    normed_ref[...] = normed
    cosine, signed_sine = cos_ref[...], sin_ref[...]
    keys = jnp.dot(normed, wk_ref[...], preferred_element_type=jnp.float32)
    kv_ref[:, :128] = rotated(keys, cosine, signed_sine)[0].astype(jnp.bfloat16)
    kv_ref[:, 128:] = jnp.dot(normed, wv_ref[...], preferred_element_type=jnp.float32).astype(
        jnp.bfloat16
    )
    queries = jnp.dot(normed, wq_ref[...], preferred_element_type=jnp.float32)
    for i, chunk in enumerate(rotated(queries, cosine, signed_sine)):
        q_ref[:, i * 128 : (i + 1) * 128] = chunk.astype(jnp.bfloat16)


def project(x, gain, w_query, w_key, w_value, cosine, signed_sine):
    tile = 256
    rows = x.shape[0]

    def by_rows(width):
        return pl.BlockSpec((tile, width), lambda i: (i, 0))

    def fixed(a):
        return pl.BlockSpec(a.shape, lambda i: (0, 0))

    return pl.pallas_call(
        project_kernel,
        name="project",
        grid=(rows // tile,),
        in_specs=[by_rows(1024), fixed(gain), fixed(w_query), fixed(w_key), fixed(w_value), by_rows(128), by_rows(128)],
        out_specs=[by_rows(1024), by_rows(256), by_rows(256)],
        out_shape=(
            jax.ShapeDtypeStruct((rows, 1024), jnp.bfloat16),
            jax.ShapeDtypeStruct((rows, 256), jnp.bfloat16),
            jax.ShapeDtypeStruct((rows, 256), jnp.bfloat16),
        ),
        cost_estimate=pl.CostEstimate(flops=540_000_000, bytes_accessed=4_000_000, transcendentals=512),
    )(x, gain, w_query, w_key, w_value, cosine, signed_sine)


def route_kernel(begin_ref, routes_ref, picks_ref, ranks_ref):
    tokens = routes_ref.shape[1]
    expert_at = lax.broadcasted_iota(jnp.int32, (128, tokens), 0)
    hits = jnp.zeros((128, tokens), jnp.float32)
    for k in range(routes_ref.shape[0]):
        hits = hits + jnp.where(routes_ref[k : k + 1, :] == expert_at, 1.0, 0.0)
    before_at = lax.broadcasted_iota(jnp.int32, (tokens, tokens), 0)
    after_at = lax.broadcasted_iota(jnp.int32, (tokens, tokens), 1)
    before = jnp.where(before_at < after_at, 1.0, 0.0).astype(jnp.bfloat16)
    counts = jnp.dot(hits.astype(jnp.bfloat16), before, preferred_element_type=jnp.float32)
    ranks = jnp.where(hits > 0.5, counts, -1.0)
    ranks_ref[...] = ranks
    quarter = picks_ref.shape[0] // EXPERTS
    slot_at = lax.broadcasted_iota(jnp.int32, (quarter, tokens), 0) + begin_ref[0]
    slot_at = slot_at.astype(jnp.float32)
    for e in range(EXPERTS):
        picks_ref[e * quarter : (e + 1) * quarter, :] = jnp.where(
            ranks[e : e + 1, :] == slot_at, 1.0, 0.0
        ).astype(jnp.bfloat16)


def route(begin, routes_t, quarter):
    tokens = routes_t.shape[1]
    return pl.pallas_call(
        route_kernel,
        name="route",
        in_specs=[in_smem(), whole_vmem()],
        out_specs=[whole_vmem()] * 2,
        out_shape=(
            jax.ShapeDtypeStruct((EXPERTS * quarter, tokens), jnp.bfloat16),
            jax.ShapeDtypeStruct((128, tokens), jnp.float32),
        ),
        cost_estimate=pl.CostEstimate(flops=100_000_000, bytes_accessed=1_600_000, transcendentals=0),
    )(begin, routes_t)


def residual_kernel(
    a0, a1, a2, a3, w0, w1, w2, w3, x_ref, gain_ref, router_ref, ranks_ref, residual_ref, moe_ref, gates_ref
):
    branch = jnp.dot(a0[...], w0[...], preferred_element_type=jnp.float32)
    for a, w in ((a1, w1), (a2, w2), (a3, w3)):
        branch = branch + jnp.dot(a[...], w[...], preferred_element_type=jnp.float32)
    residual = x_ref[...].astype(jnp.float32) + residual_mult * branch
    residual_ref[...] = residual
    scale = lax.rsqrt(jnp.mean(residual * residual, axis=1, keepdims=True) + epsilon)
    moe_in = (residual * scale * gain_ref[...]).astype(jnp.bfloat16)
    moe_ref[...] = moe_in
    logits = jnp.dot(moe_in, router_ref[...], preferred_element_type=jnp.float32)
    chosen = jnp.transpose(ranks_ref[...]) >= 0.0
    kept = jnp.where(chosen, logits, masked_score)
    top = jnp.max(kept, axis=1, keepdims=True)
    raised = jnp.where(chosen, jnp.exp(kept - top), 0.0)
    gates_ref[...] = raised / jnp.sum(raised, axis=1, keepdims=True)


def residual_step(attended, w_out, x, gain, router, ranks):
    tile = 256
    rows = x.shape[0]

    def by_rows(width):
        return pl.BlockSpec((tile, width), lambda i: (i, 0))

    def fixed(a):
        return pl.BlockSpec(a.shape, lambda i: (0, 0))

    return pl.pallas_call(
        residual_kernel,
        name="residual_step",
        grid=(rows // tile,),
        in_specs=[by_rows(256)] * 4
        + [fixed(w) for w in w_out]
        + [by_rows(1024), fixed(gain), fixed(router), pl.BlockSpec((128, tile), lambda i: (0, i))],
        out_specs=[by_rows(1024), by_rows(1024), by_rows(128)],
        out_shape=(
            jax.ShapeDtypeStruct((rows, 1024), jnp.float32),
            jax.ShapeDtypeStruct((rows, 1024), jnp.bfloat16),
            jax.ShapeDtypeStruct((rows, 128), jnp.float32),
        ),
        compiler_params=pltpu.CompilerParams(vmem_limit_bytes=32 << 20),
        cost_estimate=pl.CostEstimate(flops=1_200_000_000, bytes_accessed=8_000_000, transcendentals=70_000),
    )(*attended, *w_out, x, gain, router, ranks)


def combine_kernel(ranks_ref, gates_ref, picks_ref, mix_ref, slot_gates_ref, ranks_low, gates_low):
    step = pl.program_id(0)
    width = mix_ref.shape[1]
    per = width // CAP

    @pl.when(step == 0)
    def _():
        ranks_low[...] = jnp.transpose(ranks_ref[...]).astype(jnp.bfloat16)
        gates_low[...] = (residual_mult * gates_ref[...]).astype(jnp.bfloat16)

    expert_at = lax.broadcasted_iota(jnp.int32, (128, width), 0) - step * per
    slot_at = lax.broadcasted_iota(jnp.int32, (128, width), 1)
    first = expert_at * CAP
    spread = jnp.where((slot_at >= first) & (slot_at < first + CAP), 1.0, 0.0).astype(jnp.bfloat16)
    rank_here = jnp.dot(ranks_low[...], spread, preferred_element_type=jnp.float32)
    gate_here = jnp.dot(gates_low[...], spread, preferred_element_type=jnp.float32)
    lane = lax.broadcasted_iota(jnp.int32, (1, width), 1)
    within = lane
    for i in range(1, per):
        within = jnp.where(lane >= i * CAP, lane - i * CAP, within)
    mix_ref[...] = jnp.where(rank_here == within.astype(jnp.float32), gate_here, 0.0).astype(
        jnp.bfloat16
    )
    quarter = slot_gates_ref.shape[0] // per
    found = jnp.dot(picks_ref[...], gates_low[...], preferred_element_type=jnp.float32)
    column = lax.broadcasted_iota(jnp.int32, (quarter, 128), 1)
    for i in range(per):
        part = found[i * quarter : (i + 1) * quarter]
        part = jnp.sum(jnp.where(column == step * per + i, part, 0.0), axis=1, keepdims=True)
        slot_gates_ref[i * quarter : (i + 1) * quarter, :] = jnp.broadcast_to(
            part, (quarter, 128)
        ).astype(jnp.bfloat16)


def combine_weights(ranks, gates, picks):
    steps = 8
    tokens = gates.shape[0]
    return pl.pallas_call(
        combine_kernel,
        name="combine_weights",
        grid=(steps,),
        in_specs=[
            pl.BlockSpec(ranks.shape, lambda i: (0, 0)),
            pl.BlockSpec(gates.shape, lambda i: (0, 0)),
            pl.BlockSpec((picks.shape[0] // steps, tokens), lambda i: (i, 0)),
        ],
        out_specs=[
            pl.BlockSpec((tokens, EXPERTS * CAP // steps), lambda i: (0, i)),
            pl.BlockSpec((picks.shape[0] // steps, 128), lambda i: (i, 0)),
        ],
        out_shape=(
            jax.ShapeDtypeStruct((tokens, EXPERTS * CAP), jnp.bfloat16),
            jax.ShapeDtypeStruct((picks.shape[0], 128), jnp.bfloat16),
        ),
        scratch_shapes=[
            pltpu.VMEM((tokens, 128), jnp.bfloat16),
            pltpu.VMEM((tokens, 128), jnp.bfloat16),
        ],
        cost_estimate=pl.CostEstimate(flops=1_500_000_000, bytes_accessed=7_000_000, transcendentals=0),
    )(ranks, gates, picks)


def expert_kernel(
    x_ref, grad_ref, wg_ref, wu_ref, wd_ref, lane_ref,
    out_ref, row_ref, gate_grad_ref, hidden_ref, gate_pre_ref, up_pre_ref, both_ref,
):
    units = wd_ref.shape[0] * wd_ref.shape[1]
    share = wd_ref.shape[1]

    @pl.when(pl.program_id(0) == 0)
    def _():
        for m in range(wd_ref.shape[0]):
            both_ref[:, m * share : (m + 1) * share] = wg_ref[m]
            both_ref[:, units + m * share : units + (m + 1) * share] = wu_ref[m]

    rows = x_ref.shape[0]
    pre = jnp.dot(x_ref[...], both_ref[...], preferred_element_type=jnp.float32)
    gate_pre, up_pre = pre[:, :units], pre[:, units:]
    sigmoid = 1.0 / (1.0 + jnp.exp(-gate_pre))
    silu = gate_pre * sigmoid
    hidden = (silu * up_pre).astype(jnp.bfloat16)
    hidden_ref[...] = hidden
    down = wd_ref[...].reshape(units, wd_ref.shape[2])
    out = jnp.dot(hidden, down, preferred_element_type=jnp.float32)
    out_low = out.astype(jnp.bfloat16).astype(jnp.float32)
    grad = grad_ref[...]
    gate_grad = residual_mult * jnp.sum(grad.astype(jnp.float32) * out_low, axis=1, keepdims=True)
    lane = lax.broadcasted_iota(jnp.int32, (rows, 128), 1)
    gate_grad_ref[...] = jnp.where(lane == lane_ref[0], gate_grad, 0.0).astype(jnp.bfloat16)
    hidden_grad = lax.dot_general(
        grad, down, (((1,), (1,)), ((), ())), preferred_element_type=jnp.float32
    )
    gate_pre_grad = (hidden_grad * up_pre * sigmoid * (1.0 + gate_pre * (1.0 - sigmoid))).astype(
        jnp.bfloat16
    )
    up_pre_grad = (hidden_grad * silu).astype(jnp.bfloat16)
    gate_pre_ref[...] = gate_pre_grad
    up_pre_ref[...] = up_pre_grad
    row = lax.dot_general(
        jnp.concatenate([gate_pre_grad, up_pre_grad], axis=1),
        both_ref[...],
        (((1,), (1,)), ((), ())),
        preferred_element_type=jnp.float32,
    )
    quarter = out_ref.shape[1]
    wide = out_ref.shape[2]
    pieces = out.shape[1] // wide
    for s in range(rows // quarter):
        for m in range(pieces):
            at = (slice(s * quarter, (s + 1) * quarter), slice(m * wide, (m + 1) * wide))
            out_ref[s * pieces + m] = out[at].astype(jnp.bfloat16)
            row_ref[s * pieces + m] = row[at].astype(jnp.bfloat16)


def expert_step(x, grad, w_gate, w_up, w_down, lane, quarter, pieces):
    steps = 4
    slots, width = x.shape
    tile = slots // steps
    units = w_down.shape[0] * w_down.shape[1]
    groups = tile // quarter * pieces

    def by_rows(columns):
        return pl.BlockSpec((tile, columns), lambda i: (i, 0))

    def fixed(a):
        return pl.BlockSpec(a.shape, lambda i: (0, 0, 0), pipeline_mode=pl.Buffered(1))

    grouped = pl.BlockSpec((groups, quarter, width // pieces), lambda i: (i, 0, 0))
    grouped_shape = jax.ShapeDtypeStruct((groups * steps, quarter, width // pieces), jnp.bfloat16)
    unit_shape = jax.ShapeDtypeStruct((slots, units), jnp.bfloat16)
    return pl.pallas_call(
        expert_kernel,
        name="expert_step",
        grid=(steps,),
        in_specs=[by_rows(width), by_rows(width), fixed(w_gate), fixed(w_up), fixed(w_down), in_smem()],
        out_specs=[grouped, grouped, by_rows(128), by_rows(units), by_rows(units), by_rows(units)],
        out_shape=(
            grouped_shape,
            grouped_shape,
            jax.ShapeDtypeStruct((slots, 128), jnp.bfloat16),
            unit_shape,
            unit_shape,
            unit_shape,
        ),
        scratch_shapes=[pltpu.VMEM((width, 2 * units), jnp.bfloat16)],
        compiler_params=pltpu.CompilerParams(vmem_limit_bytes=48 << 20),
        cost_estimate=pl.CostEstimate(
            flops=8_000_000_000, bytes_accessed=18_000_000, transcendentals=700_000
        ),
    )(x, grad, w_gate, w_up, w_down, lane)


def norm_back_kernel(
    column_ref, g0, g1, g2, g3, s0, s1, s2, s3, gates_ref, residual_ref, gain_ref, router_ref, grad_ref, w_ref,
    low_ref, logit_ref, own_ref, att_ref, att_t_ref, gain_grad_ref, u_ref,
):
    rank = column_ref[0]
    share = g0.shape[1]
    for flip, part in enumerate((g0, g1, g2, g3)):
        at = pl.multiple_of(jnp.bitwise_xor(rank, flip) * share, share)
        u_ref[:, pl.ds(at, share)] = part[...].astype(jnp.float32)
    gates = gates_ref[...]
    gate_grad = s0[...].astype(jnp.float32)
    for part in (s1, s2, s3):
        gate_grad = gate_grad + part[...].astype(jnp.float32)
    inner = jnp.sum(gates * gate_grad, axis=1, keepdims=True)
    logit_grad = (gates * (gate_grad - inner)).astype(jnp.bfloat16)
    logit_ref[...] = logit_grad
    u = u_ref[...] + lax.dot_general(
        logit_grad, router_ref[...], (((1,), (1,)), ((), ())), preferred_element_type=jnp.float32
    )
    v = residual_ref[...]
    scale = lax.rsqrt(jnp.mean(v * v, axis=1, keepdims=True) + epsilon)
    weighted = u * gain_ref[...]
    mean = jnp.mean(weighted * v, axis=1, keepdims=True)
    total = grad_ref[...].astype(jnp.float32) + scale * weighted - v * (scale * scale * scale * mean)

    @pl.when(pl.program_id(0) == 0)
    def _():
        gain_grad_ref[...] = jnp.zeros_like(gain_grad_ref)

    gain_grad_ref[0:1, :] += jnp.sum(u * v * scale, axis=0, keepdims=True)
    low = (residual_mult * total).astype(jnp.bfloat16)
    low_ref[...] = low
    u_ref[...] = total
    own_ref[...] = u_ref[:, pl.ds(pl.multiple_of(rank * share, share), share)]
    nt = (((1,), (1,)), ((), ()))
    att_ref[...] = lax.dot_general(low, w_ref[...], nt, preferred_element_type=jnp.float32).astype(
        jnp.bfloat16
    )
    att_t_ref[...] = lax.dot_general(w_ref[...], low, nt, preferred_element_type=jnp.float32).astype(
        jnp.bfloat16
    )


def norm_back_step(rank, grads, gate_grads, gates, residual, gain, router, out_grad, w_out):
    tile = 256
    rows = residual.shape[0]

    def by_rows(width):
        return pl.BlockSpec((tile, width), lambda i: (i, 0))

    def fixed(a):
        return pl.BlockSpec(a.shape, lambda i: (0, 0))

    return pl.pallas_call(
        norm_back_kernel,
        name="norm_back_step",
        grid=(rows // tile,),
        in_specs=[in_smem()]
        + [by_rows(256)] * 4
        + [by_rows(128)] * 5
        + [by_rows(1024), fixed(gain), fixed(router), by_rows(1024), fixed(w_out)],
        out_specs=[
            by_rows(1024),
            by_rows(128),
            by_rows(256),
            by_rows(256),
            pl.BlockSpec((256, tile), lambda i: (0, i)),
            pl.BlockSpec((8, 1024), lambda i: (0, 0)),
        ],
        out_shape=(
            jax.ShapeDtypeStruct((rows, 1024), jnp.bfloat16),
            jax.ShapeDtypeStruct((rows, 128), jnp.bfloat16),
            jax.ShapeDtypeStruct((rows, 256), jnp.float32),
            jax.ShapeDtypeStruct((rows, 256), jnp.bfloat16),
            jax.ShapeDtypeStruct((256, rows), jnp.bfloat16),
            jax.ShapeDtypeStruct((8, 1024), jnp.float32),
        ),
        scratch_shapes=[pltpu.VMEM((tile, 1024), jnp.float32)],
        compiler_params=pltpu.CompilerParams(vmem_limit_bytes=32 << 20),
        cost_estimate=pl.CostEstimate(flops=700_000_000, bytes_accessed=9_000_000, transcendentals=512),
    )(rank, *grads, *gate_grads, gates, residual, gain, router, out_grad, w_out)


def per_device(
    hidden_in,
    lengths,
    block_order,
    routes,
    norm_gain_attn,
    w_query,
    w_key,
    w_value,
    w_out,
    norm_gain_moe,
    w_router,
    w_gate,
    w_up,
    w_down,
    out_grad,
):
    dp_count = lax.axis_size("dp")
    mp_count = lax.axis_size("mp")
    dp_rank = lax.axis_index("dp")
    mp_rank = lax.axis_index("mp")
    rows_here, width = hidden_in.shape
    share = width // mp_count
    column_start = mp_rank * share
    window = MAXLEN // BLOCK
    piece = BLOCK // dp_count
    quarter = CAP // mp_count
    kv_width = w_key.shape[1] + w_value.shape[1]
    offsets, inverse = block_tables(lengths, block_order)
    block_ids = jnp.arange(block_order.shape[0], dtype=jnp.int32)
    my_block = lax.dynamic_slice_in_dim(block_order, dp_rank, 1)
    reach = jnp.sum(jnp.where(my_block[:, None] == block_ids[None, :], offsets[None, :], 0), axis=1)
    cosine, signed_sine = rope_wide(reach[0])
    rank_one = mp_rank.reshape(1).astype(jnp.int32)
    lane_one = dp_rank.reshape(1).astype(jnp.int32)

    full_gate = lax.all_gather(w_gate[0], "mp", axis=0)
    full_up = lax.all_gather(w_up[0], "mp", axis=0)
    full_down = lax.all_gather(w_down[0], "mp", axis=0)
    full_out = from_peers(w_out, "mp")

    gain_attn = norm_gain_attn[None, :]
    gain_moe = norm_gain_moe[None, :]
    normed, queries, key_value = project(
        hidden_in, gain_attn, w_query, w_key, w_value, cosine, signed_sine
    )
    spread = to_all(key_value.reshape(dp_count, piece, kv_width), "dp")
    back_steps = jnp.arange(1, window, dtype=jnp.int32)
    wanted = jnp.maximum(block_order[:, None] - back_steps[None, :], 0)
    wanted_from = jnp.sum(
        jnp.where(wanted[:, :, None] == block_ids[None, None, :], inverse[None, None, :], 0), axis=2
    )
    picked_kv = jnp.take(spread, wanted_from.reshape(-1), axis=0)
    earlier = to_all(picked_kv.reshape(dp_count, (window - 1) * piece, kv_width), "dp")
    earlier = earlier.reshape(dp_count, window - 1, piece, kv_width)

    picks, ranks = route((mp_rank * quarter).reshape(1).astype(jnp.int32), routes.T, quarter)
    grad_rows = jnp.dot(picks, after(out_grad, earlier), preferred_element_type=jnp.bfloat16)
    grad_arrived = to_all(grad_rows.reshape(EXPERTS, quarter, width), "dp")

    attended, attended_t, lse = attend(reach, queries, key_value, earlier)
    router_wide = jnp.pad(w_router, ((0, 0), (0, 128 - EXPERTS)))
    residual, moe_in, gates = residual_step(
        from_peers(attended, "mp"), full_out, hidden_in, gain_moe, router_wide, ranks
    )

    moe_rows = jnp.dot(picks, moe_in, preferred_element_type=jnp.bfloat16)
    moe_arrived = to_all(moe_rows.reshape(EXPERTS, quarter, width), "dp")
    mix, slot_gates = combine_weights(ranks, gates, picks)
    gates_arrived = to_all(slot_gates.reshape(EXPERTS, quarter, 128), "dp")
    slots = dp_count * quarter
    grouped = moe_arrived.reshape(slots, width)
    grouped_grad = grad_arrived.reshape(slots, width)
    rows_out, row_grad, gate_grad_rows, hidden_units, gate_pre_grad, up_pre_grad = expert_step(
        grouped, grouped_grad, full_gate, full_up, full_down, lane_one, quarter, mp_count
    )
    gate_grad_home = to_all(gate_grad_rows.reshape(dp_count, quarter, 128), "dp")
    row_home = lax.all_to_all(row_grad, ("dp", "mp"), 0, 0, tiled=True)
    rows_home = lax.all_to_all(after(rows_out, row_home), ("dp", "mp"), 0, 0, tiled=True)

    slot_factor = gates_arrived.reshape(slots, 128)[:, :1].astype(jnp.float32)
    scaled_grad = (grouped_grad.astype(jnp.float32) * slot_factor).astype(jnp.bfloat16)
    down_part = row_contract(hidden_units, scaled_grad)
    gate_part = row_contract(
        grouped, (gate_pre_grad.astype(jnp.float32) * slot_factor).astype(jnp.bfloat16)
    )
    up_part = row_contract(
        grouped, (up_pre_grad.astype(jnp.float32) * slot_factor).astype(jnp.bfloat16)
    )
    gate_up = jnp.stack([gate_part, up_part]).astype(jnp.bfloat16)
    gate_up = lax.psum_scatter(gate_up, "mp", scatter_dimension=2, tiled=True)
    grad_w_gate = gate_up[:1].astype(jnp.float32)
    grad_w_up = gate_up[1:].astype(jnp.float32)
    grad_w_down = lax.psum_scatter(
        down_part.astype(jnp.bfloat16)[None], "mp", scatter_dimension=1, tiled=True
    ).astype(jnp.float32)

    gate_grad_part = row_contract(picks, gate_grad_home.reshape(EXPERTS * quarter, 128))
    gate_grads = from_peers(gate_grad_part.astype(jnp.bfloat16), "mp")
    expert_grad = jnp.dot(
        mix, row_home.reshape(EXPERTS * CAP, share), preferred_element_type=jnp.float32
    ).astype(jnp.bfloat16)
    branch_grad, logit_grad, residual_grad_own, attended_grad, attended_grad_t, moe_gain = norm_back_step(
        rank_one,
        from_peers(expert_grad, "mp"),
        gate_grads,
        gates,
        residual,
        gain_moe,
        router_wide,
        out_grad,
        w_out,
    )
    query_pre_grad, own_grads, later_grads = attend_back(
        reach,
        queries,
        key_value,
        earlier,
        attended_grad,
        attended_grad_t,
        attended_t,
        lse,
        cosine,
        signed_sine,
    )

    kv_spread = to_all(later_grads.reshape(dp_count, (window - 1) * piece, kv_width), "dp")
    later = block_order[:, None] + back_steps[None, :]
    later_hit = later[:, :, None] == block_ids[None, None, :]
    later_from = jnp.sum(jnp.where(later_hit, inverse[None, None, :], 0), axis=2)
    later_reach = jnp.sum(jnp.where(later_hit, offsets[None, None, :], 0), axis=2)
    later_live = later_reach >= back_steps[None, :]
    rows_of = (later_from * (window - 1) + back_steps[None, :] - 1).reshape(-1)
    taken = jnp.take(
        kv_spread.reshape(dp_count * (window - 1), piece, kv_width), rows_of, axis=0
    ).reshape(dp_count, window - 1, piece, kv_width)
    summed = jnp.sum(
        jnp.where(later_live[:, :, None, None], taken.astype(jnp.float32), 0.0), axis=1
    )
    kv_home = to_all(summed.astype(jnp.bfloat16), "dp")
    kv_grad = own_grads + kv_home.reshape(BLOCK, kv_width).astype(jnp.float32)
    half = w_key.shape[1]
    front = (np.arange(half) % HEAD_DIM < HEAD_DIM // 2)[None, :]
    key_grad = kv_grad[:, :half]
    partner = jnp.where(front, jnp.roll(key_grad, -HEAD_DIM // 2, 1), jnp.roll(key_grad, HEAD_DIM // 2, 1))
    key_pre_grad = (key_grad * cosine - partner * signed_sine).astype(jnp.bfloat16)
    value_pre_grad = kv_grad[:, half:].astype(jnp.bfloat16)

    mixture = jnp.dot(
        mix, rows_home.reshape(EXPERTS * CAP, share), preferred_element_type=jnp.float32
    )
    residual_cols = lax.dynamic_slice_in_dim(residual, column_start, share, 1)
    out_hidden = (residual_cols + mixture).astype(jnp.bfloat16)

    def share_rows(x):
        return x.astype(jnp.bfloat16).reshape(dp_count, x.shape[0] // dp_count, -1)

    def reduced(parts):
        arrived = to_all(jnp.concatenate([share_rows(p) for p in parts], axis=2), "dp")
        return jnp.sum(arrived.astype(jnp.float32), axis=0)

    early = reduced(
        [
            row_contract(branch_grad, attended),
            row_contract(moe_in, logit_grad)[:, :EXPERTS],
            jnp.transpose(moe_gain)[:, :1],
        ]
    )
    query_late = reduced([row_contract(normed, query_pre_grad)])
    normed_part = (
        times_transposed(query_pre_grad, w_query)
        + times_transposed(key_pre_grad, w_key)
        + times_transposed(value_pre_grad, w_value)
    )
    x = hidden_in.astype(jnp.float32)
    scale = lax.rsqrt(jnp.mean(x * x, axis=-1, keepdims=True) + epsilon)
    gain_part = jnp.sum(normed_part * x * scale, axis=0)
    kv_late = reduced(
        [
            row_contract(normed, jnp.concatenate([key_pre_grad, value_pre_grad], axis=1)),
            gain_part[:, None],
        ]
    )
    attn_gain = sum(from_peers(kv_late[:, kv_width], "mp"))

    normed_low = normed_part.astype(jnp.bfloat16)
    own_cols = lax.dynamic_slice_in_dim(normed_part, column_start, share, 1)
    for flip in (1, 2, 3):
        there = jnp.bitwise_xor(mp_rank, flip) * share
        sent = lax.dynamic_slice_in_dim(normed_low, there, share, 1)
        got = lax.ppermute(sent, "mp", [(i, i ^ flip) for i in range(4)])
        own_cols = own_cols + got.astype(jnp.float32)
    x_cols = lax.dynamic_slice_in_dim(x, column_start, share, 1)
    gain_cols = lax.dynamic_slice_in_dim(gain_attn, column_start, share, 1)
    weighted = own_cols * gain_cols
    inner = sum(from_peers(jnp.sum(weighted * x_cols, axis=1), "mp"))[:, None] / width
    grad_hidden = residual_grad_own + scale * weighted - x_cols * (scale * scale * scale * inner)

    out_end = attended.shape[1]
    return (
        out_hidden,
        grad_hidden,
        query_late,
        kv_late[:, :half],
        kv_late[:, half:kv_width],
        early[:, :out_end].T,
        attn_gain,
        early[:, out_end + EXPERTS],
        early[:, out_end : out_end + EXPERTS],
        grad_w_gate,
        grad_w_up,
        grad_w_down,
    )


def solution(mesh):
    in_specs = (
        P("dp", None),
        P(),
        P(),
        P("dp", None),
        P(),
        P(None, "mp"),
        P(None, "mp"),
        P(None, "mp"),
        P("mp", None),
        P(),
        P(),
        P("dp", None, "mp"),
        P("dp", None, "mp"),
        P("dp", "mp", None),
        P("dp", None),
    )
    out_specs = (
        P("dp", "mp"),
        P("dp", "mp"),
        P("dp", "mp"),
        P("dp", "mp"),
        P("dp", "mp"),
        P("mp", "dp"),
        P("dp"),
        P("dp"),
        P("dp", None),
        P("dp", None, "mp"),
        P("dp", None, "mp"),
        P("dp", "mp", None),
    )
    return jax.shard_map(
        per_device, mesh=mesh, in_specs=in_specs, out_specs=out_specs, check_vma=False
    )
```

```python
import jax
import jax.numpy as jnp
import numpy as np
from jax import lax
from jax.experimental import pallas as pl
from jax.experimental.pallas import tpu as pltpu
from jax.sharding import PartitionSpec as P

HEAD_DIM = 64
EXPERTS = 32
BLOCK = 512
MAXLEN = 2048
CAP = 160
WIDTH = 1024
SHARE = 256
QUARTER = 40
SLOTS = 1280
LANES = 128
PACKED = 640

epsilon = 1e-06
residual_mult = 0.22
score_mult = 0.015625
rope_base = 10000.0
masked_score = -1e30

NN = (((1,), (0,)), ((), ()))
NT = (((1,), (1,)), ((), ()))
TN = (((0,), (0,)), ((), ()))


def mm(a, b, dims=NN):
    return lax.dot_general(a, b, dims, preferred_element_type=jnp.float32)


def to_all(x):
    return lax.all_to_all(x, "dp", 0, 0, tiled=True)


def peer(x, flip):
    return lax.ppermute(x, "mp", [(i, i ^ flip) for i in range(4)])


def after(x, *others):
    return lax.optimization_barrier((x, *others))[0]


def vmem():
    return pl.BlockSpec(memory_space=pltpu.VMEM)


def smem():
    return pl.BlockSpec(memory_space=pltpu.SMEM)


def tiles(rows, width, row0=0):
    return pl.BlockSpec((rows, width), lambda i: (i + row0, 0))


def fixed(rows, width):
    return pl.BlockSpec((rows, width), lambda i: (0, 0))


def once(rows, width):
    return pl.BlockSpec((rows, width), lambda i: (0, 0), pipeline_mode=pl.Buffered(1))


def out(shape, dtype):
    return jax.ShapeDtypeStruct(shape, dtype)


def cost(flops, moved, exps=0):
    return pl.CostEstimate(flops=flops, bytes_accessed=moved, transcendentals=exps)


def rope_constants():
    frequency = rope_base ** (-(np.arange(HEAD_DIM // 2, dtype=np.float64) * 2.0) / HEAD_DIM)
    wide = np.tile(frequency, 4)[None, :]
    rows = np.arange(BLOCK, dtype=np.float64)[:, None] * wide
    starts = np.arange(8, dtype=np.float64)[:, None] * BLOCK * wide
    made = (np.cos(rows), np.sin(rows), np.cos(starts), np.sin(starts))
    return [jnp.asarray(a.astype(np.float32)) for a in made]


def half_front(rows):
    lane = lax.broadcasted_iota(jnp.int32, (rows, LANES), 1)
    return (lane % HEAD_DIM) < HEAD_DIM // 2


def turned(chunk, cosine, signed_sine, back=False):
    partner = jnp.where(
        half_front(chunk.shape[0]), pltpu.roll(chunk, 96, 1), pltpu.roll(chunk, 32, 1)
    )
    if back:
        return chunk * cosine - partner * signed_sine
    return chunk * cosine + partner * signed_sine


def block_tables_in(lengths_ref, order_ref, rank_ref, offset_ref, inverse_ref, reach_ref, wanted_ref, later_ref, live_ref):
    count = order_ref.shape[0]
    steps = MAXLEN // BLOCK - 1

    def sequence(s, begin):
        def one(j, at):
            offset_ref[jnp.minimum(at, count - 1)] = j
            return at + 1

        return lax.fori_loop(0, lengths_ref[s], one, begin)

    lax.fori_loop(0, lengths_ref.shape[0], sequence, jnp.int32(0))

    def invert(d, carry):
        inverse_ref[order_ref[d]] = d
        return carry

    lax.fori_loop(0, count, invert, jnp.int32(0))
    reach_ref[0] = offset_ref[order_ref[rank_ref[0]]]

    def look(d, carry):
        packed = order_ref[d]
        for s in range(1, steps + 1):
            wanted_ref[d * steps + s - 1] = inverse_ref[jnp.maximum(packed - s, 0)]
            next_at = jnp.minimum(packed + s, count - 1)
            later_ref[d * steps + s - 1] = inverse_ref[next_at] * steps + s - 1
            is_live = jnp.logical_and(packed + s < count, offset_ref[next_at] >= s)
            live_ref[d * steps + s - 1] = jnp.where(is_live, 1, 0)
        return carry

    lax.fori_loop(0, count, look, jnp.int32(0))


def project_kernel(
    lengths_ref, order_ref, rank_ref, x_ref, gain_ref, wq_ref, wk_ref, wv_ref, cos_ref, sin_ref, cos0_ref, sin0_ref,
    normed_ref, q_ref, kv_ref, cosine_ref, sine_ref, reach_ref, wanted_ref, later_ref, live_ref,
    offset_ref, inverse_ref,
):
    @pl.when(pl.program_id(0) == 0)
    def _():
        block_tables_in(
            lengths_ref, order_ref, rank_ref, offset_ref, inverse_ref, reach_ref, wanted_ref, later_ref, live_ref
        )

    x = x_ref[...].astype(jnp.float32)
    scale = lax.rsqrt(jnp.mean(x * x, axis=1, keepdims=True) + epsilon)
    normed = (x * scale * gain_ref[...]).astype(jnp.bfloat16)
    normed_ref[...] = normed
    at = reach_ref[0]
    cos0, sin0 = cos0_ref[pl.ds(at, 1), :], sin0_ref[pl.ds(at, 1), :]
    cosine = cos_ref[...] * cos0 - sin_ref[...] * sin0
    sine = sin_ref[...] * cos0 + cos_ref[...] * sin0
    sine = jnp.where(half_front(x.shape[0]), -sine, sine)
    cosine_ref[...] = cosine
    sine_ref[...] = sine
    kv_ref[:, :LANES] = turned(mm(normed, wk_ref[...]), cosine, sine).astype(jnp.bfloat16)
    kv_ref[:, LANES:] = mm(normed, wv_ref[...]).astype(jnp.bfloat16)
    queries = mm(normed, wq_ref[...])
    for i in range(0, SHARE, LANES):
        q_ref[:, i : i + LANES] = turned(queries[:, i : i + LANES], cosine, sine).astype(jnp.bfloat16)


def project(lengths, order, rank, x, gain, w_query, w_key, w_value):
    tile = 256
    count = order.shape[0]
    steps = MAXLEN // BLOCK - 1
    tables = [out((1,), jnp.int32)] + [out((count * steps,), jnp.int32)] * 3
    return pl.pallas_call(
        project_kernel,
        name="project",
        grid=(BLOCK // tile,),
        in_specs=[smem()] * 3
        + [tiles(tile, WIDTH), fixed(1, WIDTH), fixed(WIDTH, SHARE), fixed(WIDTH, LANES), fixed(WIDTH, LANES)]
        + [tiles(tile, LANES)] * 2
        + [fixed(8, LANES)] * 2,
        out_specs=[tiles(tile, WIDTH), tiles(tile, SHARE), tiles(tile, SHARE)]
        + [tiles(tile, LANES)] * 2
        + [smem()] * 4,
        out_shape=[
            out((BLOCK, WIDTH), jnp.bfloat16),
            out((BLOCK, SHARE), jnp.bfloat16),
            out((BLOCK, SHARE), jnp.bfloat16),
            out((BLOCK, LANES), jnp.float32),
            out((BLOCK, LANES), jnp.float32),
        ]
        + tables,
        scratch_shapes=[pltpu.SMEM((count,), jnp.int32), pltpu.SMEM((count,), jnp.int32)],
        cost_estimate=cost(540_000_000, 4_000_000, 512),
    )(lengths, order, rank, x, gain, w_query, w_key, w_value, *rope_constants())


def pick_kernel(wanted_ref, pieces_ref, picked_ref):
    def one(i, carry):
        picked_ref[i] = pieces_ref[wanted_ref[i]]
        return carry

    lax.fori_loop(0, picked_ref.shape[0], one, jnp.int32(0), unroll=4)


def pick_pieces(wanted, pieces):
    return pl.pallas_call(
        pick_kernel,
        name="pick_pieces",
        in_specs=[smem(), vmem()],
        out_specs=vmem(),
        out_shape=out((wanted.shape[0], *pieces.shape[1:]), pieces.dtype),
        cost_estimate=cost(0, 1_100_000),
    )(wanted, pieces)


def sum_kernel(later_ref, live_ref, pieces_ref, sum_ref):
    steps = MAXLEN // BLOCK - 1

    def one(d, carry):
        total = jnp.zeros(sum_ref.shape[1:], jnp.float32)
        for s in range(steps):
            part = pieces_ref[later_ref[d * steps + s]].astype(jnp.float32)
            total = total + jnp.where(live_ref[d * steps + s] == 1, part, 0.0)
        sum_ref[d] = total.astype(sum_ref.dtype)
        return carry

    lax.fori_loop(0, sum_ref.shape[0], one, jnp.int32(0), unroll=2)


def sum_pieces(later, live, pieces, count):
    return pl.pallas_call(
        sum_kernel,
        name="sum_pieces",
        in_specs=[smem(), smem(), vmem()],
        out_specs=vmem(),
        out_shape=out((count, *pieces.shape[1:]), pieces.dtype),
        cost_estimate=cost(0, 1_100_000),
    )(later, live, pieces)


def pack_kernel(out_ref, down_ref, gate_ref, up_ref, packed_ref):
    packed_ref[:SHARE, :] = out_ref[...]
    packed_ref[SHARE : SHARE + LANES, :] = down_ref[...]
    for k in range(4):
        rows = slice(k * SHARE, (k + 1) * SHARE)
        packed_ref[SHARE + LANES :, k * SHARE : k * SHARE + LANES] = gate_ref[rows, :]
        packed_ref[SHARE + LANES :, k * SHARE + LANES : (k + 1) * SHARE] = up_ref[rows, :]


def pack_weights(w_out, w_down, w_gate, w_up):
    return pl.pallas_call(
        pack_kernel,
        name="pack_weights",
        in_specs=[vmem()] * 4,
        out_specs=vmem(),
        out_shape=out((PACKED, WIDTH), jnp.bfloat16),
        cost_estimate=cost(0, 2_600_000),
    )(w_out, w_down, w_gate, w_up)


def route_kernel(begin_ref, routes_ref, picks_ref, ranks_ref):
    tokens = routes_ref.shape[1]
    expert_at = lax.broadcasted_iota(jnp.int32, (LANES, tokens), 0)
    hits = jnp.zeros((LANES, tokens), jnp.float32)
    for k in range(routes_ref.shape[0]):
        hits = hits + jnp.where(routes_ref[k : k + 1, :] == expert_at, 1.0, 0.0)
    row_at = lax.broadcasted_iota(jnp.int32, (tokens, tokens), 0)
    column_at = lax.broadcasted_iota(jnp.int32, (tokens, tokens), 1)
    before = jnp.where(row_at < column_at, 1.0, 0.0).astype(jnp.bfloat16)
    ranks = jnp.where(hits > 0.5, mm(hits.astype(jnp.bfloat16), before), -1.0)
    ranks_ref[...] = ranks
    slot_at = lax.broadcasted_iota(jnp.int32, (QUARTER, tokens), 0) + begin_ref[0]
    slot_at = slot_at.astype(jnp.float32)
    for e in range(EXPERTS):
        picks_ref[e * QUARTER : (e + 1) * QUARTER, :] = jnp.where(
            ranks[e : e + 1, :] == slot_at, 1.0, 0.0
        ).astype(jnp.bfloat16)


def route(begin, routes_t):
    return pl.pallas_call(
        route_kernel,
        name="route",
        in_specs=[smem(), vmem()],
        out_specs=[vmem()] * 2,
        out_shape=(out((SLOTS, BLOCK), jnp.bfloat16), out((LANES, BLOCK), jnp.float32)),
        cost_estimate=cost(100_000_000, 1_600_000),
    )(begin, routes_t)


def padded_columns(rows_t, out_ref):
    zero = jnp.zeros((HEAD_DIM, rows_t.shape[1]), out_ref.dtype)
    for h in range(4):
        mine = rows_t[h * HEAD_DIM : (h + 1) * HEAD_DIM].astype(out_ref.dtype)
        at = (h // 2) * HEAD_DIM
        out_ref[h, pl.ds(at, HEAD_DIM), :] = mine
        out_ref[h, pl.ds(HEAD_DIM - at, HEAD_DIM), :] = zero


def padded_rows(rows, out_ref):
    n = rows.shape[0]
    lane = lax.broadcasted_iota(jnp.int32, (n, 128), 1)
    for h in range(4):
        pair = rows[:, (h // 2) * 128 : (h // 2) * 128 + 128].astype(jnp.float32)
        if h % 2 != h // 2:
            pair = pltpu.roll(pair, HEAD_DIM, 1)
        own = (lane < HEAD_DIM) if h // 2 == 0 else (lane >= HEAD_DIM)
        out_ref[pl.ds(h * n, n), :] = jnp.where(own, pair, 0.0).astype(out_ref.dtype)


def attend_kernel(reach_ref, q_ref, own_ref, prev_ref, att_ref, out_t_ref, lse_ref, qpad_ref, max_ref, sum_ref):
    q_t = jnp.transpose(q_ref[...].astype(jnp.float32) * score_mult)
    padded_columns(q_t, qpad_ref)
    half = BLOCK // 2

    def block(key_rows, value_rows, first):
        for h in range(4):
            group = (h // 2) * HEAD_DIM
            for t in range(2):
                cols = slice(t * half, (t + 1) * half)
                rows = half if first and t == 0 else BLOCK
                scores = jnp.dot(
                    key_rows[:rows], qpad_ref[h, :, cols], preferred_element_type=jnp.float32
                )
                if first:
                    key_at = lax.broadcasted_iota(jnp.int32, scores.shape, 0)
                    query_at = lax.broadcasted_iota(jnp.int32, scores.shape, 1) + t * half
                    scores = jnp.where(key_at > query_at, masked_score, scores)
                new_max = jnp.max(scores, axis=0, keepdims=True)
                if not first:
                    old_max = max_ref[h : h + 1, cols]
                    new_max = jnp.maximum(new_max, old_max)
                    shrink = jnp.exp(old_max - new_max)
                weights = jnp.exp(scores - new_max)
                total = jnp.sum(weights, axis=0, keepdims=True)
                part = lax.dot_general(
                    value_rows[:rows],
                    weights.astype(jnp.bfloat16),
                    (((0,), (0,)), ((), ())),
                    preferred_element_type=jnp.float32,
                )[group : group + HEAD_DIM]
                mine = pl.ds(h * HEAD_DIM, HEAD_DIM)
                if not first:
                    total = total + sum_ref[h : h + 1, cols] * shrink
                    part = part + out_t_ref[mine, cols] * shrink
                max_ref[h : h + 1, cols] = new_max
                sum_ref[h : h + 1, cols] = total
                out_t_ref[mine, cols] = part

    block(own_ref[:, :128], own_ref[:, 128:], True)

    @pl.loop(1, reach_ref[0] + 1)
    def _(step):
        rows = prev_ref[:, pl.ds(step - 1, 1)].reshape(BLOCK, 256)
        block(rows[:, :128], rows[:, 128:], False)

    lse_ref[...] = jnp.zeros_like(lse_ref)
    lse_ref[0:4, :] = max_ref[0:4, :] + jnp.log(sum_ref[0:4, :])
    for h in range(4):
        mine = pl.ds(h * HEAD_DIM, HEAD_DIM)
        out_t_ref[mine, :] = out_t_ref[mine, :] / sum_ref[h : h + 1, :]
    att_ref[...] = jnp.transpose(out_t_ref[...]).astype(jnp.bfloat16)


def attend(reach, queries, own_kv, earlier):
    vmem = pl.BlockSpec(memory_space=pltpu.VMEM)
    return pl.pallas_call(
        attend_kernel,
        name="attend",
        in_specs=[pl.BlockSpec(memory_space=pltpu.SMEM), vmem, vmem, vmem],
        out_specs=[vmem] * 3,
        out_shape=(
            jax.ShapeDtypeStruct((BLOCK, 256), jnp.bfloat16),
            jax.ShapeDtypeStruct((256, BLOCK), jnp.float32),
            jax.ShapeDtypeStruct((8, BLOCK), jnp.float32),
        ),
        scratch_shapes=[
            pltpu.VMEM((4, 128, BLOCK), jnp.bfloat16),
            pltpu.VMEM((8, BLOCK), jnp.float32),
            pltpu.VMEM((8, BLOCK), jnp.float32),
        ],
        compiler_params=pltpu.CompilerParams(vmem_limit_bytes=40 << 20),
        cost_estimate=pl.CostEstimate(
            flops=5_000_000_000, bytes_accessed=3_000_000, transcendentals=3_000_000
        ),
    )(reach, queries, own_kv, earlier)


def attend_back_kernel(
    reach_ref, q_ref, own_ref, prev_ref, grad_ref, grad_t_ref, out_t_ref, lse_ref, cos_ref, sin_ref,
    qgrad_ref, own_grad_ref, prev_grad_ref,
    qpad_ref, gpad_ref, qrows_ref, grows_ref, ds_ref, p_ref, delta_ref, dq_ref,
):
    half = BLOCK // 2
    q_scaled = q_ref[...].astype(jnp.float32) * score_mult
    padded_columns(jnp.transpose(q_scaled), qpad_ref)
    padded_rows(q_scaled, qrows_ref)
    padded_columns(grad_t_ref[...], gpad_ref)
    padded_rows(grad_ref[...], grows_ref)
    both = grad_t_ref[...].astype(jnp.float32) * out_t_ref[...]
    for h in range(4):
        delta_ref[h : h + 1, :] = jnp.sum(
            both[h * HEAD_DIM : (h + 1) * HEAD_DIM], axis=0, keepdims=True
        )

    def block(key_rows, value_rows, first):
        for h in range(4):
            for t in range(2):
                cols = slice(t * half, (t + 1) * half)
                wide = slice(h * BLOCK + t * half, h * BLOCK + (t + 1) * half)
                rows = half if first and t == 0 else BLOCK
                scores = jnp.dot(
                    key_rows[:rows], qpad_ref[h, :, cols], preferred_element_type=jnp.float32
                )
                weights = jnp.exp(scores - lse_ref[h : h + 1, cols])
                if first:
                    key_at = lax.broadcasted_iota(jnp.int32, scores.shape, 0)
                    query_at = lax.broadcasted_iota(jnp.int32, scores.shape, 1) + t * half
                    weights = jnp.where(key_at > query_at, 0.0, weights)
                weight_grad = jnp.dot(
                    value_rows[:rows], gpad_ref[h, :, cols], preferred_element_type=jnp.float32
                )
                score_grad = weights * (weight_grad - delta_ref[h : h + 1, cols])
                p_ref[:rows, wide] = weights.astype(jnp.bfloat16)
                ds_ref[:rows, wide] = score_grad.astype(jnp.bfloat16)
                if rows < BLOCK:
                    p_ref[rows:, wide] = jnp.zeros((BLOCK - rows, half), jnp.bfloat16)
                    ds_ref[rows:, wide] = jnp.zeros((BLOCK - rows, half), jnp.bfloat16)
        key_grad = jnp.dot(ds_ref[...], qrows_ref[...], preferred_element_type=jnp.float32)
        value_grad = jnp.dot(p_ref[...], grows_ref[...], preferred_element_type=jnp.float32)
        for h in range(4):
            group = (h // 2) * HEAD_DIM
            mine = pl.ds(h * HEAD_DIM, HEAD_DIM)
            part = lax.dot_general(
                key_rows,
                ds_ref[:, h * BLOCK : (h + 1) * BLOCK],
                (((0,), (0,)), ((), ())),
                preferred_element_type=jnp.float32,
            )[group : group + HEAD_DIM]
            if first:
                dq_ref[mine, :] = part
            else:
                dq_ref[mine, :] = dq_ref[mine, :] + part
        return key_grad, value_grad

    key_grad, value_grad = block(own_ref[:, :128], own_ref[:, 128:], True)
    own_grad_ref[:, :128] = key_grad
    own_grad_ref[:, 128:] = value_grad

    @pl.loop(1, reach_ref[0] + 1)
    def _(step):
        rows = prev_ref[:, pl.ds(step - 1, 1)].reshape(BLOCK, 256)
        key_grad, value_grad = block(rows[:, :128], rows[:, 128:], False)
        parts = prev_grad_ref.shape[0]
        shape = (parts, 1, BLOCK // parts, 128)
        prev_grad_ref[:, pl.ds(step - 1, 1), :, 0:128] = key_grad.astype(jnp.bfloat16).reshape(shape)
        prev_grad_ref[:, pl.ds(step - 1, 1), :, 128:256] = value_grad.astype(jnp.bfloat16).reshape(shape)

    query_grad = jnp.transpose(dq_ref[...]) * score_mult
    for i in range(0, SHARE, LANES):
        qgrad_ref[:, i : i + LANES] = turned(
            query_grad[:, i : i + LANES], cos_ref[...], sin_ref[...], back=True
        ).astype(jnp.bfloat16)


def attend_back(reach, queries, own_kv, earlier, grad, grad_t, out_t, lse, cosine, signed_sine):
    vmem = pl.BlockSpec(memory_space=pltpu.VMEM)
    return pl.pallas_call(
        attend_back_kernel,
        name="attend_back",
        in_specs=[pl.BlockSpec(memory_space=pltpu.SMEM)] + [vmem] * 9,
        out_specs=[vmem] * 3,
        out_shape=(
            jax.ShapeDtypeStruct((BLOCK, 256), jnp.bfloat16),
            jax.ShapeDtypeStruct((BLOCK, 256), jnp.float32),
            jax.ShapeDtypeStruct(earlier.shape, jnp.bfloat16),
        ),
        scratch_shapes=[
            pltpu.VMEM((4, 128, BLOCK), jnp.bfloat16),
            pltpu.VMEM((4, 128, BLOCK), jnp.bfloat16),
            pltpu.VMEM((4 * BLOCK, 128), jnp.bfloat16),
            pltpu.VMEM((4 * BLOCK, 128), jnp.bfloat16),
            pltpu.VMEM((BLOCK, 4 * BLOCK), jnp.bfloat16),
            pltpu.VMEM((BLOCK, 4 * BLOCK), jnp.bfloat16),
            pltpu.VMEM((8, BLOCK), jnp.float32),
            pltpu.VMEM((256, BLOCK), jnp.float32),
        ],
        compiler_params=pltpu.CompilerParams(vmem_limit_bytes=48 << 20),
        cost_estimate=pl.CostEstimate(
            flops=12_000_000_000, bytes_accessed=5_000_000, transcendentals=3_000_000
        ),
    )(reach, queries, own_kv, earlier, grad, grad_t, out_t, lse, cosine, signed_sine)


def residual_kernel(
    a0, a1, a2, a3, w0, w1, w2, w3, x_ref, gain_ref, router_ref, ranks_ref,
    residual_ref, moe_ref, gates_ref,
):
    branch = mm(a0[...], w0[...])
    for a, w in ((a1, w1), (a2, w2), (a3, w3)):
        branch = branch + mm(a[...], w[...])
    residual = x_ref[...].astype(jnp.float32) + residual_mult * branch
    residual_ref[...] = residual
    scale = lax.rsqrt(jnp.mean(residual * residual, axis=1, keepdims=True) + epsilon)
    moe_in = (residual * scale * gain_ref[...]).astype(jnp.bfloat16)
    moe_ref[:, :WIDTH] = moe_in
    logits = mm(router_ref[...], moe_in, NT)
    chosen = ranks_ref[...] >= 0.0
    kept = jnp.where(chosen, logits, masked_score)
    top = jnp.max(kept, axis=0, keepdims=True)
    raised = jnp.where(chosen, jnp.exp(kept - top), 0.0)
    gates = raised / jnp.sum(raised, axis=0, keepdims=True)
    gates_ref[...] = gates
    moe_ref[:, WIDTH:] = (residual_mult * jnp.transpose(gates)).astype(jnp.bfloat16)


def residual_step(attended, packed, x, gain, router_t, ranks):
    tile = 256
    by_columns = pl.BlockSpec((LANES, tile), lambda i: (0, i))
    return pl.pallas_call(
        residual_kernel,
        name="residual_step",
        grid=(BLOCK // tile,),
        in_specs=[tiles(tile, SHARE)] * 4
        + [fixed(SHARE, WIDTH)] * 4
        + [tiles(tile, WIDTH), fixed(1, WIDTH), fixed(LANES, WIDTH), by_columns],
        out_specs=[tiles(tile, WIDTH), tiles(tile, WIDTH + LANES), by_columns],
        out_shape=(
            out((BLOCK, WIDTH), jnp.float32),
            out((BLOCK, WIDTH + LANES), jnp.bfloat16),
            out((LANES, BLOCK), jnp.float32),
        ),
        compiler_params=pltpu.CompilerParams(vmem_limit_bytes=32 << 20),
        cost_estimate=cost(1_200_000_000, 8_000_000, 70_000),
    )(*attended, *packed, x, gain, router_t, ranks)


def mix_kernel(begin_ref, ranks_ref, moe_ref, mix_ref):
    ranks = jnp.transpose(ranks_ref[...]).astype(jnp.bfloat16)
    gates = moe_ref[:, WIDTH:]
    width = 640
    for at in range(0, SLOTS, width):
        expert_at = lax.broadcasted_iota(jnp.int32, (LANES, width), 0)
        first = expert_at * QUARTER - at
        slot_at = lax.broadcasted_iota(jnp.int32, (LANES, width), 1)
        inside = jnp.logical_and(slot_at >= first, slot_at < first + QUARTER)
        spread = jnp.where(inside, 1.0, 0.0).astype(jnp.bfloat16)
        within = jnp.sum(jnp.where(inside, slot_at - first, 0), axis=0, keepdims=True) + begin_ref[0]
        hit = mm(ranks, spread) == within.astype(jnp.float32)
        mix_ref[:, at : at + width] = jnp.where(hit, mm(gates, spread), 0.0).astype(jnp.bfloat16)


def mix_weights(begin, ranks, moe_cat):
    return pl.pallas_call(
        mix_kernel,
        name="mix_weights",
        in_specs=[smem(), vmem(), vmem()],
        out_specs=vmem(),
        out_shape=out((BLOCK, SLOTS), jnp.bfloat16),
        compiler_params=pltpu.CompilerParams(vmem_limit_bytes=32 << 20),
        cost_estimate=cost(350_000_000, 3_000_000),
    )(begin, ranks, moe_cat)


def expert_kernel(
    lane_ref, x_ref, grad_ref, p0, p1, p2, p3,
    out_ref, row_ref, hidden_ref, units_ref,
):
    packed = (p0, p1, p2, p3)
    rows = x_ref.shape[0]
    lane = lax.broadcasted_iota(jnp.int32, (rows, LANES), 1) == lane_ref[0]
    gate = jnp.sum(
        jnp.where(lane, x_ref[:, WIDTH:].astype(jnp.float32), 0.0), axis=1, keepdims=True
    )
    x = x_ref[:, :WIDTH]
    grad = grad_ref[...]
    gates, ups, sigmoids, hidden = [], [], [], []
    for p in packed:
        pre = None
        for k in range(4):
            columns = slice(k * SHARE, (k + 1) * SHARE)
            term = mm(x[:, columns], p[SHARE + LANES :, columns])
            pre = term if pre is None else pre + term
        gate_pre, up_pre = pre[:, :LANES], pre[:, LANES:]
        sigmoid = 1.0 / (1.0 + jnp.exp(-gate_pre))
        gates.append(gate_pre)
        ups.append(up_pre)
        sigmoids.append(sigmoid)
        hidden.append(gate_pre * sigmoid * up_pre)
    hidden_low = jnp.concatenate([h.astype(jnp.bfloat16) for h in hidden], axis=1)
    down = jnp.concatenate([p[SHARE : SHARE + LANES, :] for p in packed], axis=0)
    made = mm(hidden_low, down).astype(jnp.bfloat16)
    out_ref[...] = made
    gate_grad = jnp.sum(grad.astype(jnp.float32) * made.astype(jnp.float32), axis=1, keepdims=True)
    row_ref[:, WIDTH:] = jnp.where(lane, gate_grad, 0.0).astype(jnp.bfloat16)
    hidden_grad = mm(grad, down, NT)
    row = None
    for j, p in enumerate(packed):
        part = hidden_grad[:, j * LANES : (j + 1) * LANES]
        silu = gates[j] * sigmoids[j]
        gate_pre_grad = part * ups[j] * sigmoids[j] * (1.0 + gates[j] * (1.0 - sigmoids[j]))
        up_pre_grad = part * silu
        hidden_ref[:, j * LANES : (j + 1) * LANES] = (hidden[j] * gate).astype(jnp.bfloat16)
        units_ref[:, j * SHARE : j * SHARE + LANES] = (gate_pre_grad * gate).astype(jnp.bfloat16)
        units_ref[:, j * SHARE + LANES : (j + 1) * SHARE] = (up_pre_grad * gate).astype(jnp.bfloat16)
        both = jnp.concatenate([gate_pre_grad, up_pre_grad], axis=1).astype(jnp.bfloat16)
        terms = [
            mm(both, p[SHARE + LANES :, k * SHARE : (k + 1) * SHARE], NT) for k in range(4)
        ]
        row = terms if row is None else [a + b for a, b in zip(row, terms)]
    for k in range(4):
        row_ref[:, k * SHARE : (k + 1) * SHARE] = row[k].astype(jnp.bfloat16)


def expert_step(lane, x, grad, packed):
    tile = 320
    return pl.pallas_call(
        expert_kernel,
        name="expert_step",
        grid=(SLOTS // tile,),
        in_specs=[smem(), tiles(tile, WIDTH + LANES), tiles(tile, WIDTH)] + [once(PACKED, WIDTH)] * 4,
        out_specs=[tiles(tile, WIDTH), tiles(tile, WIDTH + LANES), tiles(tile, 512), tiles(tile, WIDTH)],
        out_shape=(
            out((SLOTS, WIDTH), jnp.bfloat16),
            out((SLOTS, WIDTH + LANES), jnp.bfloat16),
            out((SLOTS, 512), jnp.bfloat16),
            out((SLOTS, WIDTH), jnp.bfloat16),
        ),
        compiler_params=pltpu.CompilerParams(vmem_limit_bytes=48 << 20),
        cost_estimate=cost(8_000_000_000, 18_000_000, 700_000),
    )(lane, x, grad, *packed)


def unit_grads_kernel(x_ref, grad_ref, hidden_ref, units_ref, keep_ref, send_ref, turned_ref):
    step = pl.program_id(0)

    @pl.when(step == 0)
    def _():
        for k in range(4):
            columns = slice(k * SHARE, (k + 1) * SHARE)
            turned_ref[columns, :] = jnp.transpose(x_ref[:, columns])

    def write(to_ref):
        to_ref[0, :LANES, :] = mm(hidden_ref[...], grad_ref[...], TN).astype(jnp.bfloat16)
        for k in range(4):
            columns = slice(k * SHARE, (k + 1) * SHARE)
            to_ref[0, LANES:, columns] = mm(turned_ref[columns, :], units_ref[...]).astype(jnp.bfloat16)

    @pl.when(step < 2)
    def _():
        write(keep_ref)

    @pl.when(step >= 2)
    def _():
        write(send_ref)


def unit_grads(x, grad, hidden, units):
    rows = SHARE + LANES

    def share_of(i):
        return jnp.where(i < 2, 2 * i, 2 * i - 3)

    return pl.pallas_call(
        unit_grads_kernel,
        name="unit_grads",
        grid=(4,),
        in_specs=[
            once(SLOTS, WIDTH),
            once(SLOTS, WIDTH),
            pl.BlockSpec((SLOTS, LANES), lambda i: (0, share_of(i))),
            pl.BlockSpec((SLOTS, SHARE), lambda i: (0, share_of(i))),
        ],
        out_specs=[
            pl.BlockSpec((1, rows, WIDTH), lambda i: (jnp.minimum(i, 1), 0, 0)),
            pl.BlockSpec((1, rows, WIDTH), lambda i: (jnp.maximum(i - 2, 0), 0, 0)),
        ],
        out_shape=(
            out((2, rows, WIDTH), jnp.bfloat16),
            out((2, rows, WIDTH), jnp.bfloat16),
        ),
        scratch_shapes=[pltpu.VMEM((WIDTH, SLOTS), jnp.bfloat16)],
        compiler_params=pltpu.CompilerParams(vmem_limit_bytes=40 << 20),
        cost_estimate=cost(4_000_000_000, 12_000_000),
    )(x, grad, hidden, units)


def unit_finish_kernel(mine_ref, got_ref, gate_ref, up_ref, down_ref):
    total = mine_ref[...].astype(jnp.float32) + got_ref[...].astype(jnp.float32)
    down_ref[0] = total[:LANES, :]
    for k in range(4):
        rows = slice(k * SHARE, (k + 1) * SHARE)
        gate_ref[0, rows, :] = total[LANES:, k * SHARE : k * SHARE + LANES]
        up_ref[0, rows, :] = total[LANES:, k * SHARE + LANES : (k + 1) * SHARE]


def unit_finish(mine, got):
    return pl.pallas_call(
        unit_finish_kernel,
        name="unit_finish",
        in_specs=[vmem()] * 2,
        out_specs=[vmem()] * 3,
        out_shape=(
            out((1, WIDTH, LANES), jnp.float32),
            out((1, WIDTH, LANES), jnp.float32),
            out((1, LANES, WIDTH), jnp.float32),
        ),
        cost_estimate=cost(1_000_000, 3_000_000),
    )(mine, got)


def home_kernel(rank_ref, mix_ref, rows_ref, keep_ref, send_ref):
    rank = rank_ref[0]
    extra = rows_ref.shape[1] > WIDTH
    for j in range(4):
        at = pl.multiple_of(jnp.bitwise_xor(rank, j) * SHARE, SHARE)
        total = mm(mix_ref[...], rows_ref[:, pl.ds(at, SHARE)])
        to_ref = send_ref if j % 2 else keep_ref
        to_ref[(j // 2) * BLOCK : (j // 2 + 1) * BLOCK, :] = total.astype(to_ref.dtype)
    if extra:
        gate_grads = jnp.transpose(mm(mix_ref[...], rows_ref[:, WIDTH:]))[:EXPERTS]
        for to_ref in (keep_ref, send_ref):
            for i in range(2):
                at = 2 * BLOCK + i * EXPERTS
                to_ref[at : at + EXPERTS, :] = gate_grads[:, i * SHARE : (i + 1) * SHARE].astype(
                    to_ref.dtype
                )


def sum_home(rank, mix, rows):
    height = 2 * BLOCK + (2 * EXPERTS if rows.shape[1] > WIDTH else 0)
    return pl.pallas_call(
        home_kernel,
        name="sum_home",
        in_specs=[smem(), vmem(), vmem()],
        out_specs=[vmem()] * 2,
        out_shape=(out((height, SHARE), jnp.float32), out((height, SHARE), jnp.bfloat16)),
        compiler_params=pltpu.CompilerParams(vmem_limit_bytes=32 << 20),
        cost_estimate=cost(1_500_000_000, 6_000_000),
    )(rank, mix, rows)


def swap_kernel(mine_ref, got_ref, total_ref):
    mine, got = mine_ref, got_ref
    half = BLOCK
    total_ref[:half] = (mine[:half] + got[half : 2 * half].astype(jnp.float32)).astype(total_ref.dtype)
    total_ref[half : 2 * half] = (
        mine[half : 2 * half] + got[:half].astype(jnp.float32)
    ).astype(total_ref.dtype)
    total_ref[2 * half :] = (mine[2 * half :] + got[2 * half :].astype(jnp.float32)).astype(
        total_ref.dtype
    )


def swap_sum(mine, got):
    return pl.pallas_call(
        swap_kernel,
        name="swap_sum",
        in_specs=[vmem()] * 2,
        out_specs=vmem(),
        out_shape=out(mine.shape, jnp.bfloat16),
        cost_estimate=cost(1_000_000, 2_500_000),
    )(mine, got)


def norm_back_kernel(
    rank_ref, g0, g2, g1, g3, z_ref, gates_ref, residual_ref, gain_ref, router_ref, grad_ref, w_ref,
    low_ref, logit_ref, own_ref, att_ref, att_t_ref, gain_grad_ref, u_ref,
):
    rank = rank_ref[0]
    for flip, part in enumerate((g0, g1, g2, g3)):
        at = pl.multiple_of(jnp.bitwise_xor(rank, flip) * SHARE, SHARE)
        u_ref[:, pl.ds(at, SHARE)] = part[...].astype(jnp.float32)
    weighted_grads = z_ref[...].astype(jnp.float32)
    gates = gates_ref[:EXPERTS, :]
    inner = jnp.sum(weighted_grads, axis=0, keepdims=True)
    logit_grad = (weighted_grads - gates * inner).astype(jnp.bfloat16)
    logit_ref[...] = logit_grad
    u = u_ref[...] + mm(logit_grad, router_ref[:EXPERTS, :], TN)
    v = residual_ref[...]
    scale = lax.rsqrt(jnp.mean(v * v, axis=1, keepdims=True) + epsilon)
    weighted = u * gain_ref[...]
    mean = jnp.mean(weighted * v, axis=1, keepdims=True)
    total = grad_ref[...].astype(jnp.float32) + scale * weighted - v * (scale * scale * scale * mean)

    @pl.when(pl.program_id(0) == 0)
    def _():
        gain_grad_ref[...] = jnp.zeros_like(gain_grad_ref)

    gain_grad_ref[0:1, :] += jnp.sum(u * v * scale, axis=0, keepdims=True)
    low = (residual_mult * total).astype(jnp.bfloat16)
    low_ref[...] = low
    u_ref[...] = total
    own_ref[...] = u_ref[:, pl.ds(pl.multiple_of(rank * SHARE, SHARE), SHARE)]
    att_ref[...] = mm(low, w_ref[...], NT).astype(jnp.bfloat16)
    att_t_ref[...] = mm(w_ref[...], low, NT).astype(jnp.bfloat16)


def norm_back_step(rank, mine, theirs, gates, residual, gain, router_t, out_grad, w_out):
    tile = 256
    by_columns = pl.BlockSpec((EXPERTS, tile), lambda i: (0, i))
    return pl.pallas_call(
        norm_back_kernel,
        name="norm_back_step",
        grid=(BLOCK // tile,),
        in_specs=[smem()]
        + [tiles(tile, SHARE), tiles(tile, SHARE, BLOCK // tile)] * 2
        + [
            tiles(EXPERTS, SHARE, 2 * BLOCK // EXPERTS),
            pl.BlockSpec((LANES, tile), lambda i: (0, i)),
            tiles(tile, WIDTH),
            fixed(1, WIDTH),
            fixed(LANES, WIDTH),
            tiles(tile, WIDTH),
            fixed(SHARE, WIDTH),
        ],
        out_specs=[
            tiles(tile, WIDTH),
            by_columns,
            tiles(tile, SHARE),
            tiles(tile, SHARE),
            pl.BlockSpec((SHARE, tile), lambda i: (0, i)),
            fixed(8, WIDTH),
        ],
        out_shape=(
            out((BLOCK, WIDTH), jnp.bfloat16),
            out((EXPERTS, BLOCK), jnp.bfloat16),
            out((BLOCK, SHARE), jnp.float32),
            out((BLOCK, SHARE), jnp.bfloat16),
            out((SHARE, BLOCK), jnp.bfloat16),
            out((8, WIDTH), jnp.float32),
        ),
        scratch_shapes=[pltpu.VMEM((tile, WIDTH), jnp.float32)],
        compiler_params=pltpu.CompilerParams(vmem_limit_bytes=32 << 20),
        cost_estimate=cost(700_000_000, 9_000_000, 512),
    )(rank, mine, mine, theirs, theirs, mine, gates, residual, gain, router_t, out_grad, w_out)


def dense_grads_kernel(low_ref, attended_ref, normed_ref, qgrad_ref, logit_ref, moe_ref, gain_ref, made_ref):
    made_ref[:, :SHARE] = mm(low_ref[...], attended_ref[...], TN).astype(jnp.bfloat16)
    made_ref[:, SHARE : 2 * SHARE] = mm(normed_ref[...], qgrad_ref[...], TN).astype(jnp.bfloat16)
    router = mm(logit_ref[...], moe_ref[:, :WIDTH])
    stacked = jnp.concatenate(
        [router, gain_ref[...], jnp.zeros((LANES - EXPERTS - 8, WIDTH), jnp.float32)], axis=0
    )
    made_ref[:, 2 * SHARE :] = jnp.transpose(stacked).astype(jnp.bfloat16)


def dense_grads(low, attended, normed, qgrad, logit, moe_cat, gain_grad):
    return pl.pallas_call(
        dense_grads_kernel,
        name="dense_grads",
        in_specs=[vmem()] * 7,
        out_specs=vmem(),
        out_shape=out((WIDTH, 2 * SHARE + LANES), jnp.bfloat16),
        compiler_params=pltpu.CompilerParams(vmem_limit_bytes=32 << 20),
        cost_estimate=cost(600_000_000, 6_000_000),
    )(low, attended, normed, qgrad, logit, moe_cat, gain_grad)


def last_grads_kernel(
    rank_ref, own_ref, home_ref, qgrad_ref, normed_ref, x_ref, wq_ref, wk_ref, wv_ref, cos_ref, sin_ref, made_ref,
    all_ref, keep_ref, send_ref, part_ref,
):
    rank = rank_ref[0]
    kv = own_ref[...] + home_ref[...].astype(jnp.float32)
    key_grad = turned(kv[:, :LANES], cos_ref[...], sin_ref[...], back=True).astype(jnp.bfloat16)
    value_grad = kv[:, LANES:].astype(jnp.bfloat16)
    both = jnp.concatenate([key_grad, value_grad], axis=1)
    all_ref[:, : 2 * SHARE] = made_ref[:, : 2 * SHARE]
    all_ref[:, 2 * SHARE : 3 * SHARE] = mm(normed_ref[...], both, TN).astype(jnp.bfloat16)
    gain = jnp.zeros((1, WIDTH), jnp.float32)
    tile = 128
    for i in range(0, BLOCK, tile):
        rows = slice(i, i + tile)
        part = mm(qgrad_ref[rows, :], wq_ref[...], NT)
        part = part + mm(key_grad[rows], wk_ref[...], NT) + mm(value_grad[rows], wv_ref[...], NT)
        x = x_ref[rows, :].astype(jnp.float32)
        scale = lax.rsqrt(jnp.mean(x * x, axis=1, keepdims=True) + epsilon)
        gain = gain + jnp.sum(part * x * scale, axis=0, keepdims=True)
        part_ref[rows, :] = part
    for j in range(4):
        at = pl.multiple_of(jnp.bitwise_xor(rank, j) * SHARE, SHARE)
        to_ref = send_ref if j % 2 else keep_ref
        to_ref[(j // 2) * BLOCK : (j // 2 + 1) * BLOCK, :] = part_ref[:, pl.ds(at, SHARE)].astype(to_ref.dtype)
    lane = lax.broadcasted_iota(jnp.int32, (WIDTH, LANES), 1)
    column = jnp.transpose(jnp.broadcast_to(gain, (LANES, WIDTH)))
    rest = jnp.where(lane == EXPERTS + 8, column, made_ref[:, 2 * SHARE :].astype(jnp.float32))
    all_ref[:, 3 * SHARE :] = rest.astype(jnp.bfloat16)


def last_grads(rank, own, home, qgrad, normed, x, w_query, w_key, w_value, cosine, sine, made):
    return pl.pallas_call(
        last_grads_kernel,
        name="last_grads",
        in_specs=[smem()] + [vmem()] * 11,
        out_specs=[vmem()] * 3,
        out_shape=(
            out((WIDTH, 3 * SHARE + LANES), jnp.bfloat16),
            out((2 * BLOCK, SHARE), jnp.float32),
            out((2 * BLOCK, SHARE), jnp.bfloat16),
        ),
        scratch_shapes=[pltpu.VMEM((BLOCK, WIDTH), jnp.float32)],
        compiler_params=pltpu.CompilerParams(vmem_limit_bytes=40 << 20),
        cost_estimate=cost(1_000_000_000, 8_000_000, 512),
    )(rank, own, home, qgrad, normed, x, w_query, w_key, w_value, cosine, sine, made)


def shares_summed(keep, send):
    near = keep + peer(send, 1).astype(jnp.float32)
    half = near.shape[0] // 2
    return near[:half] + peer(near[half:].astype(jnp.bfloat16), 2).astype(jnp.float32)


def per_device(
    hidden_in,
    lengths,
    block_order,
    routes,
    norm_gain_attn,
    w_query,
    w_key,
    w_value,
    w_out,
    norm_gain_moe,
    w_router,
    w_gate,
    w_up,
    w_down,
    out_grad,
):
    dp_count = block_order.shape[0]
    mp_rank = lax.axis_index("mp").astype(jnp.int32)
    column_start = mp_rank * SHARE
    piece = BLOCK // dp_count
    steps = MAXLEN // BLOCK - 1
    rank = mp_rank.reshape(1)
    lane = lax.axis_index("dp").astype(jnp.int32).reshape(1)
    begin = rank * QUARTER
    gain_attn = norm_gain_attn[None, :]
    gain_moe = norm_gain_moe[None, :]
    router_t = jnp.pad(w_router.T, ((0, LANES - EXPERTS), (0, 0)))

    own_pack = pack_weights(w_out, w_down[0], w_gate[0], w_up[0])
    far_pack = peer(own_pack, 2)
    packed = [own_pack, peer(own_pack, 1), far_pack, peer(far_pack, 1)]

    normed, queries, key_value, cosine, sine, reach, wanted, later, live = project(
        lengths, block_order, lane, hidden_in, gain_attn, w_query, w_key, w_value
    )
    pieces = to_all(key_value.reshape(dp_count, piece, SHARE))
    picks, ranks = route(begin, routes.T)
    grad_rows = jnp.dot(picks, out_grad, preferred_element_type=jnp.bfloat16)
    picked = pick_pieces(wanted, pieces)
    earlier = to_all(picked.reshape(dp_count, steps * piece, SHARE))
    earlier = earlier.reshape(dp_count, steps, piece, SHARE)
    grad_arrived = to_all(after(grad_rows, earlier).reshape(EXPERTS, QUARTER, WIDTH))

    attended, attended_t, lse = attend(reach, after(queries, far_pack), key_value, earlier)
    attended_sent = after(attended, *packed)
    far = peer(attended_sent, 2)
    residual, moe_cat, gates = residual_step(
        [attended, peer(attended_sent, 1), far, peer(far, 1)],
        packed,
        hidden_in,
        gain_moe,
        router_t,
        ranks,
    )

    moe_rows = jnp.dot(picks, moe_cat, preferred_element_type=jnp.bfloat16)
    grouped = to_all(moe_rows.reshape(EXPERTS, QUARTER, -1)).reshape(SLOTS, -1)
    mix = mix_weights(begin, ranks, moe_cat)
    grouped_grad = grad_arrived.reshape(SLOTS, WIDTH)
    rows_out, row_grad, hidden_units, unit_grad = expert_step(lane, grouped, grouped_grad, packed)
    row_home = to_all(row_grad.reshape(dp_count, QUARTER, -1)).reshape(SLOTS, -1)
    rows_home = to_all(after(rows_out, row_home).reshape(dp_count, QUARTER, -1)).reshape(SLOTS, -1)

    unit_keep, unit_send = unit_grads(grouped, grouped_grad, hidden_units, unit_grad)

    keep, send = sum_home(rank, mix, row_home)
    near = keep + peer(send, 1).astype(jnp.float32)
    mine = swap_sum(near, peer(near.astype(jnp.bfloat16), 2))
    theirs = peer(mine, 1)
    branch_grad, logit_grad, residual_grad, attended_grad, attended_grad_t, moe_gain = norm_back_step(
        rank, mine, theirs, gates, residual, gain_moe, router_t, out_grad, w_out
    )

    unit_near = unit_keep.astype(jnp.float32) + peer(after(unit_send, mine), 1).astype(jnp.float32)
    unit_far = peer(unit_near[1].astype(jnp.bfloat16), 2)
    grad_w_gate, grad_w_up, grad_w_down = unit_finish(unit_near[0], unit_far)

    query_pre_grad, own_grads, later_grads = attend_back(
        reach,
        queries,
        key_value,
        earlier,
        attended_grad,
        attended_grad_t,
        attended_t,
        lse,
        cosine,
        sine,
    )
    later_pieces = to_all(later_grads.reshape(dp_count, steps * piece, SHARE))
    summed = sum_pieces(
        later, live, later_pieces.reshape(dp_count * steps, piece, SHARE), dp_count
    )
    kv_home = to_all(summed).reshape(BLOCK, SHARE)
    made = dense_grads(
        branch_grad, attended, normed, query_pre_grad, logit_grad, moe_cat, moe_gain
    )

    keep, send = sum_home(rank, mix, rows_home)
    mixture = shares_summed(keep, send)
    residual_cols = lax.dynamic_slice_in_dim(residual, column_start, SHARE, 1)
    out_hidden = (residual_cols + mixture).astype(jnp.bfloat16)

    every, keep, send = last_grads(
        rank,
        own_grads,
        kv_home,
        query_pre_grad,
        normed,
        hidden_in,
        w_query,
        w_key,
        w_value,
        cosine,
        sine,
        made,
    )
    arrived = to_all(every.reshape(dp_count, WIDTH // dp_count, -1))
    dense = jnp.sum(arrived.astype(jnp.float32), axis=0)
    normed_grad = shares_summed(keep, send)
    x = hidden_in.astype(jnp.float32)
    scale = lax.rsqrt(jnp.mean(x * x, axis=-1, keepdims=True) + epsilon)
    x_cols = lax.dynamic_slice_in_dim(x, column_start, SHARE, 1)
    weighted = normed_grad * lax.dynamic_slice_in_dim(gain_attn, column_start, SHARE, 1)
    inner = jnp.sum(weighted * x_cols, axis=1)
    inner = inner + peer(inner, 1) + peer(inner, 2) + peer(inner, 3)
    inner = inner[:, None] / WIDTH
    grad_hidden = residual_grad + scale * weighted - x_cols * (scale * scale * scale * inner)

    at = 3 * SHARE
    attn_gain = dense[:, at + EXPERTS + 8]
    attn_gain = attn_gain + peer(attn_gain, 1) + peer(attn_gain, 2) + peer(attn_gain, 3)
    return (
        out_hidden,
        grad_hidden,
        dense[:, SHARE : 2 * SHARE],
        dense[:, 2 * SHARE : 2 * SHARE + LANES],
        dense[:, 2 * SHARE + LANES : at],
        dense[:, :SHARE].T,
        attn_gain,
        dense[:, at + EXPERTS],
        dense[:, at : at + EXPERTS],
        grad_w_gate,
        grad_w_up,
        grad_w_down,
    )


def solution(mesh):
    in_specs = (
        P("dp", None),
        P(),
        P(),
        P("dp", None),
        P(),
        P(None, "mp"),
        P(None, "mp"),
        P(None, "mp"),
        P("mp", None),
        P(),
        P(),
        P("dp", None, "mp"),
        P("dp", None, "mp"),
        P("dp", "mp", None),
        P("dp", None),
    )
    out_specs = (
        P("dp", "mp"),
        P("dp", "mp"),
        P("dp", "mp"),
        P("dp", "mp"),
        P("dp", "mp"),
        P("mp", "dp"),
        P("dp"),
        P("dp"),
        P("dp", None),
        P("dp", None, "mp"),
        P("dp", None, "mp"),
        P("dp", "mp", None),
    )
    return jax.shard_map(
        per_device, mesh=mesh, in_specs=in_specs, out_specs=out_specs, check_vma=False
    )
```

```python
import jax
import jax.numpy as jnp
import numpy as np
from jax import lax
from jax.experimental import pallas as pl
from jax.experimental.pallas import tpu as pltpu
from jax.sharding import PartitionSpec as P

HEAD_DIM = 64
EXPERTS = 32
BLOCK = 512
MAXLEN = 2048
CAP = 160
WIDTH = 1024
SHARE = 256
QUARTER = 40
SLOTS = 1280
LANES = 128
PACKED = 384

epsilon = 1e-06
residual_mult = 0.22
score_mult = 0.015625
rope_base = 10000.0
masked_score = -1e30

NN = (((1,), (0,)), ((), ()))
NT = (((1,), (1,)), ((), ()))
TN = (((0,), (0,)), ((), ()))


def mm(a, b, dims=NN):
    return lax.dot_general(a, b, dims, preferred_element_type=jnp.float32)


def to_all(x):
    return lax.all_to_all(x, "dp", 0, 0, tiled=True)


def peer(x, flip):
    return lax.ppermute(x, "mp", [(i, i ^ flip) for i in range(4)])


def after(x, *others):
    return lax.optimization_barrier((x, *others))[0]


def smem():
    return pl.BlockSpec(memory_space=pltpu.SMEM)


def tiles(rows, width, row0=0):
    return pl.BlockSpec((rows, width), lambda i: (i + row0, 0))


def fixed(rows, width):
    return pl.BlockSpec((rows, width), lambda i: (0, 0))


def once(*shape):
    return pl.BlockSpec(shape, lambda i: (0,) * len(shape), pipeline_mode=pl.Buffered(1))


def run(kernel, name, steps, in_specs, out_specs, out_shape, args, estimate, scratch=(), free=()):
    in_specs = [once(*a.shape) if s is None else s for s, a in zip(in_specs, args)]
    out_specs = [once(*o.shape) if s is None else s for s, o in zip(out_specs, out_shape)]
    args = [
        a
        if s.memory_space == pltpu.SMEM or i in free
        else pltpu.with_memory_space_constraint(a, pltpu.HBM)
        for i, (s, a) in enumerate(zip(in_specs, args))
    ]
    out_shape = [
        o if s.memory_space == pltpu.SMEM else pltpu.HBM(o.shape, o.dtype)
        for s, o in zip(out_specs, out_shape)
    ]
    return pl.pallas_call(
        kernel,
        name=name,
        grid=(steps,),
        in_specs=in_specs,
        out_specs=out_specs,
        out_shape=out_shape,
        scratch_shapes=list(scratch),
        compiler_params=pltpu.CompilerParams(vmem_limit_bytes=60 << 20),
        cost_estimate=estimate,
    )(*args)


def out(shape, dtype):
    return jax.ShapeDtypeStruct(shape, dtype)


def cost(flops, moved, exps=0):
    return pl.CostEstimate(flops=flops, bytes_accessed=moved, transcendentals=exps)


def rope_constants():
    frequency = rope_base ** (-(np.arange(HEAD_DIM // 2, dtype=np.float64) * 2.0) / HEAD_DIM)
    wide = np.tile(frequency, 4)[None, :]
    made = []
    for count, apart in ((BLOCK // 16, 16), (16, 1), (8, BLOCK)):
        angles = np.arange(count, dtype=np.float64)[:, None] * apart * wide
        made += [np.cos(angles), np.sin(angles)]
    return [jnp.asarray(a.astype(np.float32)) for a in made]


def half_front(rows):
    lane = lax.broadcasted_iota(jnp.int32, (rows, LANES), 1)
    return (lane % HEAD_DIM) < HEAD_DIM // 2


def turned(chunk, cosine, signed_sine, back=False):
    partner = jnp.where(
        half_front(chunk.shape[0]), pltpu.roll(chunk, 96, 1), pltpu.roll(chunk, 32, 1)
    )
    if back:
        return chunk * cosine - partner * signed_sine
    return chunk * cosine + partner * signed_sine


def block_tables_in(lengths_ref, order_ref, rank_ref, offset_ref, inverse_ref, reach_ref, wanted_ref, later_ref, live_ref):
    count = order_ref.shape[0]
    steps = MAXLEN // BLOCK - 1

    def sequence(s, begin):
        def one(j, at):
            offset_ref[jnp.minimum(at, count - 1)] = j
            return at + 1

        return lax.fori_loop(0, lengths_ref[s], one, begin)

    lax.fori_loop(0, lengths_ref.shape[0], sequence, jnp.int32(0))

    def invert(d, carry):
        inverse_ref[order_ref[d]] = d
        return carry

    lax.fori_loop(0, count, invert, jnp.int32(0))
    reach_ref[0] = offset_ref[order_ref[rank_ref[0]]]

    def look(d, carry):
        packed = order_ref[d]
        for s in range(1, steps + 1):
            wanted_ref[d * steps + s - 1] = inverse_ref[jnp.maximum(packed - s, 0)]
            next_at = jnp.minimum(packed + s, count - 1)
            later_ref[d * steps + s - 1] = inverse_ref[next_at] * steps + s - 1
            is_live = jnp.logical_and(packed + s < count, offset_ref[next_at] >= s)
            live_ref[d * steps + s - 1] = jnp.where(is_live, 1, 0)
        return carry

    lax.fori_loop(0, count, look, jnp.int32(0))


def project_kernel(
    lengths_ref, order_ref, rank_ref, x_ref, gain_ref, wq_ref, wk_ref, wv_ref,
    cos16_ref, sin16_ref, cos1_ref, sin1_ref, cos0_ref, sin0_ref,
    normed_ref, q_ref, kv_ref, cosine_ref, sine_ref, reach_ref, wanted_ref, later_ref, live_ref,
    offset_ref, inverse_ref,
):
    @pl.when(pl.program_id(0) == 0)
    def _():
        block_tables_in(
            lengths_ref, order_ref, rank_ref, offset_ref, inverse_ref, reach_ref, wanted_ref, later_ref, live_ref
        )

    x = x_ref[...].astype(jnp.float32)
    scale = lax.rsqrt(jnp.mean(x * x, axis=1, keepdims=True) + epsilon)
    normed = (x * scale * gain_ref[...]).astype(jnp.bfloat16)
    normed_ref[...] = normed
    at = reach_ref[0]
    cos0, sin0 = cos0_ref[pl.ds(at, 1), :], sin0_ref[pl.ds(at, 1), :]
    cos16 = cos16_ref[...] * cos0 - sin16_ref[...] * sin0
    sin16 = sin16_ref[...] * cos0 + cos16_ref[...] * sin0
    cos1, sin1 = cos1_ref[...][None], sin1_ref[...][None]
    cosine = (cos16[:, None, :] * cos1 - sin16[:, None, :] * sin1).reshape(x.shape[0], LANES)
    sine = (sin16[:, None, :] * cos1 + cos16[:, None, :] * sin1).reshape(x.shape[0], LANES)
    sine = jnp.where(half_front(x.shape[0]), -sine, sine)
    cosine_ref[...] = cosine
    sine_ref[...] = sine
    kv_ref[:, :LANES] = turned(mm(normed, wk_ref[...]), cosine, sine).astype(jnp.bfloat16)
    kv_ref[:, LANES:] = mm(normed, wv_ref[...]).astype(jnp.bfloat16)
    queries = mm(normed, wq_ref[...])
    for i in range(0, SHARE, LANES):
        q_ref[:, i : i + LANES] = turned(queries[:, i : i + LANES], cosine, sine).astype(jnp.bfloat16)


def project(lengths, order, rank, x, gain, w_query, w_key, w_value):
    tile = 256
    count = order.shape[0]
    steps = MAXLEN // BLOCK - 1
    bf16, f32 = jnp.bfloat16, jnp.float32
    return run(
        project_kernel,
        "project",
        BLOCK // tile,
        [smem()] * 3
        + [tiles(tile, WIDTH), None, None, None, None]
        + [tiles(tile // 16, LANES)] * 2
        + [None] * 4,
        [tiles(tile, WIDTH), tiles(tile, SHARE), tiles(tile, SHARE)]
        + [tiles(tile, LANES)] * 2
        + [smem()] * 4,
        [out((BLOCK, WIDTH), bf16), out((BLOCK, SHARE), bf16), out((BLOCK, SHARE), bf16)]
        + [out((BLOCK, LANES), f32)] * 2
        + [out((1,), jnp.int32)]
        + [out((count * steps,), jnp.int32)] * 3,
        (lengths, order, rank, x, gain, w_query, w_key, w_value, *rope_constants()),
        cost(540_000_000, 4_000_000, 512),
        [pltpu.SMEM((count,), jnp.int32), pltpu.SMEM((count,), jnp.int32)],
    )


def pick_kernel(wanted_ref, pieces_ref, picked_ref):
    def one(i, carry):
        picked_ref[i] = pieces_ref[wanted_ref[i]]
        return carry

    lax.fori_loop(0, picked_ref.shape[0], one, jnp.int32(0), unroll=4)


def pick_pieces(wanted, pieces):
    shape = out((wanted.shape[0], *pieces.shape[1:]), pieces.dtype)
    return run(
        pick_kernel, "pick_pieces", 1, [smem(), None], [None], [shape], (wanted, pieces), cost(0, 1_100_000), free=(1,)
    )[0]


def sum_kernel(later_ref, live_ref, pieces_ref, sum_ref):
    steps = MAXLEN // BLOCK - 1

    def one(d, carry):
        total = jnp.zeros(sum_ref.shape[1:], jnp.float32)
        for s in range(steps):
            part = pieces_ref[later_ref[d * steps + s]].astype(jnp.float32)
            total = total + jnp.where(live_ref[d * steps + s] == 1, part, 0.0)
        sum_ref[d] = total.astype(sum_ref.dtype)
        return carry

    lax.fori_loop(0, sum_ref.shape[0], one, jnp.int32(0), unroll=2)


def sum_pieces(later, live, pieces, count):
    shape = out((count, *pieces.shape[1:]), pieces.dtype)
    return run(
        sum_kernel,
        "sum_pieces",
        1,
        [smem(), smem(), None],
        [None],
        [shape],
        (later, live, pieces),
        cost(0, 1_100_000),
        free=(2,),
    )[0]


def pack_kernel(down_ref, gate_ref, up_ref, packed_ref):
    packed_ref[:LANES, :] = down_ref[...]
    for k in range(4):
        rows = slice(k * SHARE, (k + 1) * SHARE)
        packed_ref[LANES:, k * SHARE : k * SHARE + LANES] = gate_ref[rows, :]
        packed_ref[LANES:, k * SHARE + LANES : (k + 1) * SHARE] = up_ref[rows, :]


def pack_weights(w_down, w_gate, w_up):
    shape = out((PACKED, WIDTH), jnp.bfloat16)
    return run(
        pack_kernel, "pack_weights", 1, [None] * 3, [None], [shape], (w_down, w_gate, w_up), cost(0, 1_600_000)
    )[0]


def route_kernel(begin_ref, routes_ref, picks_ref, ranks_ref):
    tokens = routes_ref.shape[1]
    expert_at = lax.broadcasted_iota(jnp.int32, (LANES, tokens), 0)
    hits = jnp.zeros((LANES, tokens), jnp.float32)
    for k in range(routes_ref.shape[0]):
        hits = hits + jnp.where(routes_ref[k : k + 1, :] == expert_at, 1.0, 0.0)
    row_at = lax.broadcasted_iota(jnp.int32, (tokens, tokens), 0)
    column_at = lax.broadcasted_iota(jnp.int32, (tokens, tokens), 1)
    before = jnp.where(row_at < column_at, 1.0, 0.0).astype(jnp.bfloat16)
    ranks = jnp.where(hits > 0.5, mm(hits.astype(jnp.bfloat16), before), -1.0)
    ranks_ref[...] = ranks
    slot_at = lax.broadcasted_iota(jnp.int32, (QUARTER, tokens), 0) + begin_ref[0]
    slot_at = slot_at.astype(jnp.float32)
    for e in range(EXPERTS):
        picks_ref[e * QUARTER : (e + 1) * QUARTER, :] = jnp.where(
            ranks[e : e + 1, :] == slot_at, 1.0, 0.0
        ).astype(jnp.bfloat16)


def route(begin, routes_t):
    return run(
        route_kernel,
        "route",
        1,
        [smem(), None],
        [None, None],
        [out((SLOTS, BLOCK), jnp.bfloat16), out((LANES, BLOCK), jnp.float32)],
        (begin, routes_t),
        cost(100_000_000, 1_600_000),
        free=(1,),
    )


def padded_columns(rows_t, out_ref):
    zero = jnp.zeros((HEAD_DIM, rows_t.shape[1]), out_ref.dtype)
    for h in range(4):
        mine = rows_t[h * HEAD_DIM : (h + 1) * HEAD_DIM].astype(out_ref.dtype)
        at = (h // 2) * HEAD_DIM
        out_ref[h, pl.ds(at, HEAD_DIM), :] = mine
        out_ref[h, pl.ds(HEAD_DIM - at, HEAD_DIM), :] = zero


def padded_rows(rows, out_ref):
    n = rows.shape[0]
    lane = lax.broadcasted_iota(jnp.int32, (n, 128), 1)
    for h in range(4):
        pair = rows[:, (h // 2) * 128 : (h // 2) * 128 + 128].astype(jnp.float32)
        if h % 2 != h // 2:
            pair = pltpu.roll(pair, HEAD_DIM, 1)
        own = (lane < HEAD_DIM) if h // 2 == 0 else (lane >= HEAD_DIM)
        out_ref[pl.ds(h * n, n), :] = jnp.where(own, pair, 0.0).astype(out_ref.dtype)


def attend_kernel(
    reach_ref, q_ref, own_ref, prev_ref, att_ref, out_t_ref, lse_ref, qpad_ref, max_ref, sum_ref, kv_ref
):
    q_t = jnp.transpose(q_ref[...].astype(jnp.float32) * score_mult)
    padded_columns(q_t, qpad_ref)
    half = BLOCK // 2
    max_ref[...] = jnp.full_like(max_ref, masked_score)
    sum_ref[...] = jnp.zeros_like(sum_ref)
    out_t_ref[...] = jnp.zeros_like(out_t_ref)
    kv_ref[...] = own_ref[...]

    @pl.loop(0, reach_ref[0] + 1)
    def _(step):
        @pl.when(step > 0)
        def _():
            kv_ref[...] = prev_ref[:, pl.ds(step - 1, 1)].reshape(BLOCK, SHARE)

        key_rows, value_rows = kv_ref[:, :LANES], kv_ref[:, LANES:]
        ahead = jnp.minimum(step, 1) * BLOCK
        for h in range(4):
            group = (h // 2) * HEAD_DIM
            for t in range(2):
                cols = slice(t * half, (t + 1) * half)
                scores = mm(key_rows, qpad_ref[h, :, cols])
                key_at = lax.broadcasted_iota(jnp.int32, scores.shape, 0)
                query_at = lax.broadcasted_iota(jnp.int32, scores.shape, 1) + (t * half + ahead)
                scores = jnp.where(key_at > query_at, masked_score, scores)
                old_max = max_ref[h : h + 1, cols]
                new_max = jnp.maximum(jnp.max(scores, axis=0, keepdims=True), old_max)
                shrink = jnp.exp(old_max - new_max)
                weights = jnp.exp(scores - new_max)
                total = jnp.sum(weights, axis=0, keepdims=True)
                part = mm(value_rows, weights.astype(jnp.bfloat16), TN)[group : group + HEAD_DIM]
                mine = pl.ds(h * HEAD_DIM, HEAD_DIM)
                max_ref[h : h + 1, cols] = new_max
                sum_ref[h : h + 1, cols] = total + sum_ref[h : h + 1, cols] * shrink
                out_t_ref[mine, cols] = part + out_t_ref[mine, cols] * shrink

    lse_ref[...] = jnp.zeros_like(lse_ref)
    lse_ref[0:4, :] = max_ref[0:4, :] + jnp.log(sum_ref[0:4, :])
    for h in range(4):
        mine = pl.ds(h * HEAD_DIM, HEAD_DIM)
        out_t_ref[mine, :] = out_t_ref[mine, :] / sum_ref[h : h + 1, :]
    att_ref[...] = jnp.transpose(out_t_ref[...]).astype(jnp.bfloat16)


def attend(reach, queries, own_kv, earlier):
    return run(
        attend_kernel,
        "attend",
        1,
        [smem(), None, None, None],
        [None] * 3,
        [
            out((BLOCK, SHARE), jnp.bfloat16),
            out((SHARE, BLOCK), jnp.float32),
            out((8, BLOCK), jnp.float32),
        ],
        (reach, queries, own_kv, earlier),
        cost(5_000_000_000, 3_000_000, 3_000_000),
        [
            pltpu.VMEM((4, LANES, BLOCK), jnp.bfloat16),
            pltpu.VMEM((8, BLOCK), jnp.float32),
            pltpu.VMEM((8, BLOCK), jnp.float32),
            pltpu.VMEM((BLOCK, SHARE), jnp.bfloat16),
        ],
        free=(3,),
    )


def attend_back_kernel(
    reach_ref, q_ref, own_ref, prev_ref, grad_ref, grad_t_ref, out_t_ref, lse_ref, cos_ref, sin_ref,
    qgrad_ref, own_grad_ref, prev_grad_ref,
    qpad_ref, gpad_ref, qrows_ref, grows_ref, ds_ref, p_ref, delta_ref, dq_ref, kv_ref,
):
    half = BLOCK // 2
    q_scaled = q_ref[...].astype(jnp.float32) * score_mult
    padded_columns(jnp.transpose(q_scaled), qpad_ref)
    padded_rows(q_scaled, qrows_ref)
    padded_columns(grad_t_ref[...], gpad_ref)
    padded_rows(grad_ref[...], grows_ref)
    both = grad_t_ref[...].astype(jnp.float32) * out_t_ref[...]
    for h in range(4):
        delta_ref[h : h + 1, :] = jnp.sum(
            both[h * HEAD_DIM : (h + 1) * HEAD_DIM], axis=0, keepdims=True
        )

    dq_ref[...] = jnp.zeros_like(dq_ref)
    kv_ref[...] = own_ref[...]

    @pl.loop(0, reach_ref[0] + 1)
    def _(step):
        @pl.when(step > 0)
        def _():
            kv_ref[...] = prev_ref[:, pl.ds(step - 1, 1)].reshape(BLOCK, SHARE)

        key_rows, value_rows = kv_ref[:, :LANES], kv_ref[:, LANES:]
        ahead = jnp.minimum(step, 1) * BLOCK
        for h in range(4):
            for t in range(2):
                cols = slice(t * half, (t + 1) * half)
                wide = slice(h * BLOCK + t * half, h * BLOCK + (t + 1) * half)
                scores = mm(key_rows, qpad_ref[h, :, cols])
                weights = jnp.exp(scores - lse_ref[h : h + 1, cols])
                key_at = lax.broadcasted_iota(jnp.int32, scores.shape, 0)
                query_at = lax.broadcasted_iota(jnp.int32, scores.shape, 1) + (t * half + ahead)
                weights = jnp.where(key_at > query_at, 0.0, weights)
                weight_grad = mm(value_rows, gpad_ref[h, :, cols])
                score_grad = weights * (weight_grad - delta_ref[h : h + 1, cols])
                p_ref[:, wide] = weights.astype(jnp.bfloat16)
                ds_ref[:, wide] = score_grad.astype(jnp.bfloat16)
            group = (h // 2) * HEAD_DIM
            mine = pl.ds(h * HEAD_DIM, HEAD_DIM)
            part = mm(key_rows, ds_ref[:, h * BLOCK : (h + 1) * BLOCK], TN)
            dq_ref[mine, :] = dq_ref[mine, :] + part[group : group + HEAD_DIM]
        key_grad = mm(ds_ref[...], qrows_ref[...])
        value_grad = mm(p_ref[...], grows_ref[...])

        @pl.when(step == 0)
        def _():
            own_grad_ref[:, :LANES] = key_grad
            own_grad_ref[:, LANES:] = value_grad

        @pl.when(step > 0)
        def _():
            parts = prev_grad_ref.shape[0]
            shape = (parts, 1, BLOCK // parts, LANES)
            here = pl.ds(jnp.maximum(step - 1, 0), 1)
            prev_grad_ref[:, here, :, 0:LANES] = key_grad.astype(jnp.bfloat16).reshape(shape)
            prev_grad_ref[:, here, :, LANES:SHARE] = value_grad.astype(jnp.bfloat16).reshape(shape)

    query_grad = jnp.transpose(dq_ref[...]) * score_mult
    for i in range(0, SHARE, LANES):
        qgrad_ref[:, i : i + LANES] = turned(
            query_grad[:, i : i + LANES], cos_ref[...], sin_ref[...], back=True
        ).astype(jnp.bfloat16)


def attend_back(reach, queries, own_kv, earlier, grad, grad_t, out_t, lse, cosine, signed_sine):
    return run(
        attend_back_kernel,
        "attend_back",
        1,
        [smem()] + [None] * 9,
        [None] * 3,
        [
            out((BLOCK, SHARE), jnp.bfloat16),
            out((BLOCK, SHARE), jnp.float32),
            out(earlier.shape, jnp.bfloat16),
        ],
        (reach, queries, own_kv, earlier, grad, grad_t, out_t, lse, cosine, signed_sine),
        cost(12_000_000_000, 5_000_000, 3_000_000),
        [
            pltpu.VMEM((4, LANES, BLOCK), jnp.bfloat16),
            pltpu.VMEM((4, LANES, BLOCK), jnp.bfloat16),
            pltpu.VMEM((4 * BLOCK, LANES), jnp.bfloat16),
            pltpu.VMEM((4 * BLOCK, LANES), jnp.bfloat16),
            pltpu.VMEM((BLOCK, 4 * BLOCK), jnp.bfloat16),
            pltpu.VMEM((BLOCK, 4 * BLOCK), jnp.bfloat16),
            pltpu.VMEM((8, BLOCK), jnp.float32),
            pltpu.VMEM((SHARE, BLOCK), jnp.float32),
            pltpu.VMEM((BLOCK, SHARE), jnp.bfloat16),
        ],
        free=(3,),
    )


def residual_kernel(
    a0, a1, a2, a3, w0, w1, w2, w3, x_ref, gain_ref, router_ref, ranks_ref,
    residual_ref, moe_ref, gates_ref,
):
    branch = mm(a0[...], w0[...])
    for a, w in ((a1, w1), (a2, w2), (a3, w3)):
        branch = branch + mm(a[...], w[...])
    residual = x_ref[...].astype(jnp.float32) + residual_mult * branch
    residual_ref[...] = residual
    scale = lax.rsqrt(jnp.mean(residual * residual, axis=1, keepdims=True) + epsilon)
    moe_in = (residual * scale * gain_ref[...]).astype(jnp.bfloat16)
    moe_ref[:, :WIDTH] = moe_in
    logits = mm(router_ref[...], moe_in, NT)
    chosen = ranks_ref[...] >= 0.0
    kept = jnp.where(chosen, logits, masked_score)
    top = jnp.max(kept, axis=0, keepdims=True)
    raised = jnp.where(chosen, jnp.exp(kept - top), 0.0)
    gates = raised / jnp.sum(raised, axis=0, keepdims=True)
    gates_ref[...] = gates
    moe_ref[:, WIDTH:] = (residual_mult * jnp.transpose(gates)).astype(jnp.bfloat16)


def residual_step(attended, w_out, x, gain, router_t, ranks):
    tile = 256
    by_columns = pl.BlockSpec((LANES, tile), lambda i: (0, i))
    return run(
        residual_kernel,
        "residual_step",
        BLOCK // tile,
        [tiles(tile, SHARE)] * 4 + [None] * 4 + [tiles(tile, WIDTH), None, None, by_columns],
        [tiles(tile, WIDTH), tiles(tile, WIDTH + LANES), by_columns],
        [
            out((BLOCK, WIDTH), jnp.float32),
            out((BLOCK, WIDTH + LANES), jnp.bfloat16),
            out((LANES, BLOCK), jnp.float32),
        ],
        (*attended, *w_out, x, gain, router_t, ranks),
        cost(1_200_000_000, 8_000_000, 70_000),
        free=(1, 2, 3, 5, 6, 7, 10),
    )


def mix_kernel(begin_ref, ranks_ref, moe_ref, mix_ref):
    ranks = jnp.transpose(ranks_ref[...]).astype(jnp.bfloat16)
    gates = moe_ref[:, WIDTH:]
    width = 640
    for at in range(0, SLOTS, width):
        expert_at = lax.broadcasted_iota(jnp.int32, (LANES, width), 0)
        first = expert_at * QUARTER - at
        slot_at = lax.broadcasted_iota(jnp.int32, (LANES, width), 1)
        inside = jnp.logical_and(slot_at >= first, slot_at < first + QUARTER)
        spread = jnp.where(inside, 1.0, 0.0).astype(jnp.bfloat16)
        within = jnp.sum(jnp.where(inside, slot_at - first, 0), axis=0, keepdims=True) + begin_ref[0]
        hit = mm(ranks, spread) == within.astype(jnp.float32)
        mix_ref[:, at : at + width] = jnp.where(hit, mm(gates, spread), 0.0).astype(jnp.bfloat16)


def mix_weights(begin, ranks, moe_cat):
    return run(
        mix_kernel,
        "mix_weights",
        1,
        [smem(), None, None],
        [None],
        [out((BLOCK, SLOTS), jnp.bfloat16)],
        (begin, ranks, moe_cat),
        cost(350_000_000, 3_000_000),
    )[0]


def expert_kernel(
    lane_ref, x_ref, grad_ref, p0, p1, p2, p3,
    out_ref, row_ref, hidden_ref, units_ref,
):
    packed = (p0, p1, p2, p3)
    rows = x_ref.shape[0]
    lane = lax.broadcasted_iota(jnp.int32, (rows, LANES), 1) == lane_ref[0]
    gate = jnp.sum(
        jnp.where(lane, x_ref[:, WIDTH:].astype(jnp.float32), 0.0), axis=1, keepdims=True
    )
    x = x_ref[:, :WIDTH]
    grad = grad_ref[...]
    gates, ups, sigmoids, hidden = [], [], [], []
    for p in packed:
        pre = None
        for k in range(4):
            columns = slice(k * SHARE, (k + 1) * SHARE)
            term = mm(x[:, columns], p[LANES:, columns])
            pre = term if pre is None else pre + term
        gate_pre, up_pre = pre[:, :LANES], pre[:, LANES:]
        sigmoid = 1.0 / (1.0 + jnp.exp(-gate_pre))
        gates.append(gate_pre)
        ups.append(up_pre)
        sigmoids.append(sigmoid)
        hidden.append(gate_pre * sigmoid * up_pre)
    hidden_low = jnp.concatenate([h.astype(jnp.bfloat16) for h in hidden], axis=1)
    down = jnp.concatenate([p[:LANES, :] for p in packed], axis=0)
    made = mm(hidden_low, down).astype(jnp.bfloat16)
    out_ref[...] = made
    gate_grad = jnp.sum(grad.astype(jnp.float32) * made.astype(jnp.float32), axis=1, keepdims=True)
    row_ref[:, WIDTH:] = jnp.where(lane, gate_grad, 0.0).astype(jnp.bfloat16)
    hidden_grad = mm(grad, down, NT)
    row = None
    for j, p in enumerate(packed):
        part = hidden_grad[:, j * LANES : (j + 1) * LANES]
        silu = gates[j] * sigmoids[j]
        gate_pre_grad = part * ups[j] * sigmoids[j] * (1.0 + gates[j] * (1.0 - sigmoids[j]))
        up_pre_grad = part * silu
        hidden_ref[:, j * LANES : (j + 1) * LANES] = (hidden[j] * gate).astype(jnp.bfloat16)
        units_ref[:, j * SHARE : j * SHARE + LANES] = (gate_pre_grad * gate).astype(jnp.bfloat16)
        units_ref[:, j * SHARE + LANES : (j + 1) * SHARE] = (up_pre_grad * gate).astype(jnp.bfloat16)
        both = jnp.concatenate([gate_pre_grad, up_pre_grad], axis=1).astype(jnp.bfloat16)
        terms = [
            mm(both, p[LANES:, k * SHARE : (k + 1) * SHARE], NT) for k in range(4)
        ]
        row = terms if row is None else [a + b for a, b in zip(row, terms)]
    for k in range(4):
        row_ref[:, k * SHARE : (k + 1) * SHARE] = row[k].astype(jnp.bfloat16)


def expert_step(lane, x, grad, packed):
    tile = 320
    return run(
        expert_kernel,
        "expert_step",
        SLOTS // tile,
        [smem(), tiles(tile, WIDTH + LANES), tiles(tile, WIDTH)] + [None] * 4,
        [tiles(tile, WIDTH), tiles(tile, WIDTH + LANES), tiles(tile, 512), tiles(tile, WIDTH)],
        [
            out((SLOTS, WIDTH), jnp.bfloat16),
            out((SLOTS, WIDTH + LANES), jnp.bfloat16),
            out((SLOTS, 512), jnp.bfloat16),
            out((SLOTS, WIDTH), jnp.bfloat16),
        ],
        (lane, x, grad, *packed),
        cost(8_000_000_000, 18_000_000, 700_000),
        free=(1, 2, 4, 5, 6),
    )


def unit_grads_kernel(x_ref, grad_ref, hidden_ref, units_ref, keep_ref, send_ref, turned_ref):
    step = pl.program_id(0)

    @pl.when(step == 0)
    def _():
        for k in range(4):
            columns = slice(k * SHARE, (k + 1) * SHARE)
            turned_ref[columns, :] = jnp.transpose(x_ref[:, columns])

    def write(to_ref):
        to_ref[0, :LANES, :] = mm(hidden_ref[...], grad_ref[...], TN).astype(jnp.bfloat16)
        for k in range(4):
            columns = slice(k * SHARE, (k + 1) * SHARE)
            to_ref[0, LANES:, columns] = mm(turned_ref[columns, :], units_ref[...]).astype(jnp.bfloat16)

    @pl.when(step < 2)
    def _():
        write(keep_ref)

    @pl.when(step >= 2)
    def _():
        write(send_ref)


def unit_grads(x, grad, hidden, units):
    rows = SHARE + LANES

    def share_of(i):
        return jnp.where(i < 2, 2 * i, 2 * i - 3)

    return run(
        unit_grads_kernel,
        "unit_grads",
        4,
        [
            once(SLOTS, WIDTH),
            None,
            pl.BlockSpec((SLOTS, LANES), lambda i: (0, share_of(i))),
            pl.BlockSpec((SLOTS, SHARE), lambda i: (0, share_of(i))),
        ],
        [
            pl.BlockSpec((1, rows, WIDTH), lambda i: (jnp.minimum(i, 1), 0, 0)),
            pl.BlockSpec((1, rows, WIDTH), lambda i: (jnp.maximum(i - 2, 0), 0, 0)),
        ],
        [out((2, rows, WIDTH), jnp.bfloat16), out((2, rows, WIDTH), jnp.bfloat16)],
        (x, grad, hidden, units),
        cost(4_000_000_000, 12_000_000),
        [pltpu.VMEM((WIDTH, SLOTS), jnp.bfloat16)],
        free=(0, 1),
    )


def unit_finish_kernel(mine_ref, got_ref, gate_ref, up_ref, down_ref):
    total = mine_ref[...].astype(jnp.float32) + got_ref[...].astype(jnp.float32)
    down_ref[0] = total[:LANES, :]
    for k in range(4):
        rows = slice(k * SHARE, (k + 1) * SHARE)
        gate_ref[0, rows, :] = total[LANES:, k * SHARE : k * SHARE + LANES]
        up_ref[0, rows, :] = total[LANES:, k * SHARE + LANES : (k + 1) * SHARE]


def unit_finish(mine, got):
    return run(
        unit_finish_kernel,
        "unit_finish",
        1,
        [None] * 2,
        [None] * 3,
        [
            out((1, WIDTH, LANES), jnp.float32),
            out((1, WIDTH, LANES), jnp.float32),
            out((1, LANES, WIDTH), jnp.float32),
        ],
        (mine, got),
        cost(1_000_000, 3_000_000),
        free=(0, 1),
    )


def home_kernel(rank_ref, mix_ref, rows_ref, keep_ref, send_ref):
    rank = rank_ref[0]
    extra = rows_ref.shape[1] > WIDTH
    for j in range(4):
        at = pl.multiple_of(jnp.bitwise_xor(rank, j) * SHARE, SHARE)
        total = mm(mix_ref[...], rows_ref[:, pl.ds(at, SHARE)])
        to_ref = send_ref if j % 2 else keep_ref
        to_ref[(j // 2) * BLOCK : (j // 2 + 1) * BLOCK, :] = total.astype(to_ref.dtype)
    if extra:
        gate_grads = jnp.transpose(mm(mix_ref[...], rows_ref[:, WIDTH:]))[:EXPERTS]
        for to_ref in (keep_ref, send_ref):
            for i in range(2):
                at = 2 * BLOCK + i * EXPERTS
                to_ref[at : at + EXPERTS, :] = gate_grads[:, i * SHARE : (i + 1) * SHARE].astype(
                    to_ref.dtype
                )


def sum_home(rank, mix, rows):
    height = 2 * BLOCK + (2 * EXPERTS if rows.shape[1] > WIDTH else 0)
    return run(
        home_kernel,
        "sum_home",
        1,
        [smem(), None, None],
        [None] * 2,
        [out((height, SHARE), jnp.float32), out((height, SHARE), jnp.bfloat16)],
        (rank, mix, rows),
        cost(1_500_000_000, 6_000_000),
        free=(2,),
    )


def swap_kernel(mine_ref, got_ref, total_ref):
    mine, got = mine_ref, got_ref
    half = BLOCK
    total_ref[:half] = (mine[:half] + got[half : 2 * half].astype(jnp.float32)).astype(total_ref.dtype)
    total_ref[half : 2 * half] = (
        mine[half : 2 * half] + got[:half].astype(jnp.float32)
    ).astype(total_ref.dtype)
    total_ref[2 * half :] = (mine[2 * half :] + got[2 * half :].astype(jnp.float32)).astype(
        total_ref.dtype
    )


def swap_sum(mine, got):
    return run(
        swap_kernel,
        "swap_sum",
        1,
        [None] * 2,
        [None],
        [out(mine.shape, jnp.bfloat16)],
        (mine, got),
        cost(1_000_000, 2_500_000),
        free=(0, 1),
    )[0]


def norm_back_kernel(
    rank_ref, g0, g2, g1, g3, z_ref, gates_ref, residual_ref, gain_ref, router_ref, grad_ref, w_ref,
    low_ref, logit_ref, own_ref, att_ref, att_t_ref, gain_grad_ref, u_ref,
):
    rank = rank_ref[0]
    for flip, part in enumerate((g0, g1, g2, g3)):
        at = pl.multiple_of(jnp.bitwise_xor(rank, flip) * SHARE, SHARE)
        u_ref[:, pl.ds(at, SHARE)] = part[...].astype(jnp.float32)
    weighted_grads = z_ref[...].astype(jnp.float32)
    gates = gates_ref[:EXPERTS, :]
    inner = jnp.sum(weighted_grads, axis=0, keepdims=True)
    logit_grad = (weighted_grads - gates * inner).astype(jnp.bfloat16)
    logit_ref[...] = logit_grad
    u = u_ref[...] + mm(logit_grad, router_ref[:EXPERTS, :], TN)
    v = residual_ref[...]
    scale = lax.rsqrt(jnp.mean(v * v, axis=1, keepdims=True) + epsilon)
    weighted = u * gain_ref[...]
    mean = jnp.mean(weighted * v, axis=1, keepdims=True)
    total = grad_ref[...].astype(jnp.float32) + scale * weighted - v * (scale * scale * scale * mean)

    @pl.when(pl.program_id(0) == 0)
    def _():
        gain_grad_ref[...] = jnp.zeros_like(gain_grad_ref)

    gain_grad_ref[0:1, :] += jnp.sum(u * v * scale, axis=0, keepdims=True)
    low = (residual_mult * total).astype(jnp.bfloat16)
    low_ref[...] = low
    u_ref[...] = total
    own_ref[...] = u_ref[:, pl.ds(pl.multiple_of(rank * SHARE, SHARE), SHARE)]
    att_ref[...] = mm(low, w_ref[...], NT).astype(jnp.bfloat16)
    att_t_ref[...] = mm(w_ref[...], low, NT).astype(jnp.bfloat16)


def norm_back_step(rank, mine, theirs, gates, residual, gain, router_t, out_grad, w_out):
    tile = 256
    by_columns = pl.BlockSpec((EXPERTS, tile), lambda i: (0, i))
    return run(
        norm_back_kernel,
        "norm_back_step",
        BLOCK // tile,
        [smem()]
        + [tiles(tile, SHARE), tiles(tile, SHARE, BLOCK // tile)] * 2
        + [
            tiles(EXPERTS, SHARE, 2 * BLOCK // EXPERTS),
            pl.BlockSpec((LANES, tile), lambda i: (0, i)),
            tiles(tile, WIDTH),
            None,
            None,
            tiles(tile, WIDTH),
            None,
        ],
        [
            tiles(tile, WIDTH),
            by_columns,
            tiles(tile, SHARE),
            tiles(tile, SHARE),
            pl.BlockSpec((SHARE, tile), lambda i: (0, i)),
            fixed(8, WIDTH),
        ],
        [
            out((BLOCK, WIDTH), jnp.bfloat16),
            out((EXPERTS, BLOCK), jnp.bfloat16),
            out((BLOCK, SHARE), jnp.float32),
            out((BLOCK, SHARE), jnp.bfloat16),
            out((SHARE, BLOCK), jnp.bfloat16),
            out((8, WIDTH), jnp.float32),
        ],
        (rank, mine, mine, theirs, theirs, mine, gates, residual, gain, router_t, out_grad, w_out),
        cost(700_000_000, 9_000_000, 512),
        [pltpu.VMEM((tile, WIDTH), jnp.float32)],
        free=(3, 4, 9),
    )


def dense_grads_kernel(low_ref, attended_ref, normed_ref, qgrad_ref, logit_ref, moe_ref, gain_ref, made_ref):
    made_ref[:, :SHARE] = mm(low_ref[...], attended_ref[...], TN).astype(jnp.bfloat16)
    made_ref[:, SHARE : 2 * SHARE] = mm(normed_ref[...], qgrad_ref[...], TN).astype(jnp.bfloat16)
    router = mm(logit_ref[...], moe_ref[:, :WIDTH])
    stacked = jnp.concatenate(
        [router, gain_ref[...], jnp.zeros((LANES - EXPERTS - 8, WIDTH), jnp.float32)], axis=0
    )
    made_ref[:, 2 * SHARE :] = jnp.transpose(stacked).astype(jnp.bfloat16)


def dense_grads(low, attended, normed, qgrad, logit, moe_cat, gain_grad):
    return run(
        dense_grads_kernel,
        "dense_grads",
        1,
        [None] * 7,
        [None],
        [out((WIDTH, 2 * SHARE + LANES), jnp.bfloat16)],
        (low, attended, normed, qgrad, logit, moe_cat, gain_grad),
        cost(600_000_000, 6_000_000),
    )[0]


def last_grads_kernel(
    rank_ref, own_ref, home_ref, qgrad_ref, normed_ref, x_ref, wq_ref, wk_ref, wv_ref, cos_ref, sin_ref, made_ref,
    all_ref, keep_ref, send_ref, part_ref,
):
    rank = rank_ref[0]
    kv = own_ref[...] + home_ref[...].astype(jnp.float32)
    key_grad = turned(kv[:, :LANES], cos_ref[...], sin_ref[...], back=True).astype(jnp.bfloat16)
    value_grad = kv[:, LANES:].astype(jnp.bfloat16)
    both = jnp.concatenate([key_grad, value_grad], axis=1)
    all_ref[:, : 2 * SHARE] = made_ref[:, : 2 * SHARE]
    all_ref[:, 2 * SHARE : 3 * SHARE] = mm(normed_ref[...], both, TN).astype(jnp.bfloat16)
    gain = jnp.zeros((1, WIDTH), jnp.float32)
    tile = 128
    for i in range(0, BLOCK, tile):
        rows = slice(i, i + tile)
        part = mm(qgrad_ref[rows, :], wq_ref[...], NT)
        part = part + mm(key_grad[rows], wk_ref[...], NT) + mm(value_grad[rows], wv_ref[...], NT)
        x = x_ref[rows, :].astype(jnp.float32)
        scale = lax.rsqrt(jnp.mean(x * x, axis=1, keepdims=True) + epsilon)
        gain = gain + jnp.sum(part * x * scale, axis=0, keepdims=True)
        part_ref[rows, :] = part
    for j in range(4):
        at = pl.multiple_of(jnp.bitwise_xor(rank, j) * SHARE, SHARE)
        to_ref = send_ref if j % 2 else keep_ref
        to_ref[(j // 2) * BLOCK : (j // 2 + 1) * BLOCK, :] = part_ref[:, pl.ds(at, SHARE)].astype(to_ref.dtype)
    lane = lax.broadcasted_iota(jnp.int32, (WIDTH, LANES), 1)
    column = jnp.transpose(jnp.broadcast_to(gain, (LANES, WIDTH)))
    rest = jnp.where(lane == EXPERTS + 8, column, made_ref[:, 2 * SHARE :].astype(jnp.float32))
    all_ref[:, 3 * SHARE :] = rest.astype(jnp.bfloat16)


def last_grads(rank, own, home, qgrad, normed, x, w_query, w_key, w_value, cosine, sine, made):
    return run(
        last_grads_kernel,
        "last_grads",
        1,
        [smem()] + [None] * 11,
        [None] * 3,
        [
            out((WIDTH, 3 * SHARE + LANES), jnp.bfloat16),
            out((2 * BLOCK, SHARE), jnp.float32),
            out((2 * BLOCK, SHARE), jnp.bfloat16),
        ],
        (rank, own, home, qgrad, normed, x, w_query, w_key, w_value, cosine, sine, made),
        cost(1_000_000_000, 8_000_000, 512),
        [pltpu.VMEM((BLOCK, WIDTH), jnp.float32)],
        free=(2,),
    )


def shares_summed(keep, send):
    near = keep + peer(send, 1).astype(jnp.float32)
    half = near.shape[0] // 2
    return near[:half] + peer(near[half:].astype(jnp.bfloat16), 2).astype(jnp.float32)


def per_device(
    hidden_in,
    lengths,
    block_order,
    routes,
    norm_gain_attn,
    w_query,
    w_key,
    w_value,
    w_out,
    norm_gain_moe,
    w_router,
    w_gate,
    w_up,
    w_down,
    out_grad,
):
    dp_count = block_order.shape[0]
    mp_rank = lax.axis_index("mp").astype(jnp.int32)
    column_start = mp_rank * SHARE
    piece = BLOCK // dp_count
    steps = MAXLEN // BLOCK - 1
    rank = mp_rank.reshape(1)
    lane = lax.axis_index("dp").astype(jnp.int32).reshape(1)
    begin = rank * QUARTER
    gain_attn = norm_gain_attn[None, :]
    gain_moe = norm_gain_moe[None, :]
    router_t = jnp.pad(w_router.T, ((0, LANES - EXPERTS), (0, 0)))

    normed, queries, key_value, cosine, sine, reach, wanted, later, live = project(
        lengths, block_order, lane, hidden_in, gain_attn, w_query, w_key, w_value
    )
    pieces = to_all(key_value.reshape(dp_count, piece, SHARE))
    picks, ranks = route(begin, after(routes.T, key_value))
    far_out = peer(after(w_out, key_value), 2)
    picked = pick_pieces(wanted, after(pieces, far_out))
    earlier = to_all(picked.reshape(dp_count, steps * piece, SHARE))
    earlier = earlier.reshape(dp_count, steps, piece, SHARE)

    own_pack = pack_weights(after(w_down[0], picked), w_gate[0], w_up[0])
    far_pack = peer(own_pack, 2)
    packed = [own_pack, peer(own_pack, 1), far_pack, peer(far_pack, 1)]
    outs = [w_out, peer(after(w_out, picked), 1), far_out, peer(far_out, 1)]

    grad_rows = jnp.dot(picks, after(out_grad, own_pack), preferred_element_type=jnp.bfloat16)
    grad_arrived = to_all(after(grad_rows, earlier, far_pack).reshape(EXPERTS, QUARTER, WIDTH))
    attended, attended_t, lse = attend(reach, queries, key_value, earlier)
    far = peer(attended, 2)
    residual, moe_cat, gates = residual_step(
        [attended, peer(attended, 1), far, peer(far, 1)],
        outs,
        hidden_in,
        gain_moe,
        router_t,
        ranks,
    )

    moe_rows = jnp.dot(picks, moe_cat, preferred_element_type=jnp.bfloat16)
    grouped = to_all(moe_rows.reshape(EXPERTS, QUARTER, -1)).reshape(SLOTS, -1)
    mix = mix_weights(begin, ranks, moe_cat)
    grouped_grad = grad_arrived.reshape(SLOTS, WIDTH)
    rows_out, row_grad, hidden_units, unit_grad = expert_step(lane, grouped, grouped_grad, packed)
    row_home = to_all(row_grad.reshape(dp_count, QUARTER, -1)).reshape(SLOTS, -1)
    unit_keep, unit_send = unit_grads(grouped, grouped_grad, hidden_units, unit_grad)
    unit_near = unit_keep.astype(jnp.float32) + peer(unit_send, 1).astype(jnp.float32)
    unit_low = unit_near[1].astype(jnp.bfloat16)

    keep, send = sum_home(rank, after(mix, unit_low), row_home)
    near = keep + peer(send, 1).astype(jnp.float32)
    mine = swap_sum(near, peer(near.astype(jnp.bfloat16), 2))
    theirs = peer(mine, 1)
    branch_grad, logit_grad, residual_grad, attended_grad, attended_grad_t, moe_gain = norm_back_step(
        rank, mine, theirs, gates, residual, gain_moe, router_t, out_grad, w_out
    )
    rows_home = to_all(after(rows_out, mine).reshape(dp_count, QUARTER, -1)).reshape(SLOTS, -1)

    query_pre_grad, own_grads, later_grads = attend_back(
        reach,
        queries,
        key_value,
        earlier,
        attended_grad,
        attended_grad_t,
        attended_t,
        lse,
        cosine,
        sine,
    )
    later_pieces = to_all(after(later_grads, rows_home).reshape(dp_count, steps * piece, SHARE))
    summed = sum_pieces(
        later, live, later_pieces.reshape(dp_count * steps, piece, SHARE), dp_count
    )
    kv_home = to_all(summed).reshape(BLOCK, SHARE)
    made = dense_grads(
        branch_grad, attended, normed, query_pre_grad, logit_grad, moe_cat, moe_gain
    )

    unit_far = peer(after(unit_low, summed), 2)
    grad_w_gate, grad_w_up, grad_w_down = unit_finish(unit_near[0], unit_far)
    keep, send = sum_home(rank, mix, rows_home)
    mixture = shares_summed(keep, send)
    residual_cols = lax.dynamic_slice_in_dim(residual, column_start, SHARE, 1)
    out_hidden = (residual_cols + mixture).astype(jnp.bfloat16)

    every, keep, send = last_grads(
        rank,
        own_grads,
        after(kv_home, unit_far),
        query_pre_grad,
        normed,
        hidden_in,
        w_query,
        w_key,
        w_value,
        cosine,
        sine,
        made,
    )
    arrived = to_all(every.reshape(dp_count, WIDTH // dp_count, -1))
    dense = jnp.sum(arrived.astype(jnp.float32), axis=0)
    normed_grad = shares_summed(keep, send)
    x = hidden_in.astype(jnp.float32)
    scale = lax.rsqrt(jnp.mean(x * x, axis=-1, keepdims=True) + epsilon)
    x_cols = lax.dynamic_slice_in_dim(x, column_start, SHARE, 1)
    weighted = normed_grad * lax.dynamic_slice_in_dim(gain_attn, column_start, SHARE, 1)
    inner = jnp.sum(weighted * x_cols, axis=1)
    inner = inner + peer(inner, 1) + peer(inner, 2) + peer(inner, 3)
    inner = inner[:, None] / WIDTH
    grad_hidden = residual_grad + scale * weighted - x_cols * (scale * scale * scale * inner)

    at = 3 * SHARE
    attn_gain = dense[:, at + EXPERTS + 8]
    attn_gain = attn_gain + peer(attn_gain, 1) + peer(attn_gain, 2) + peer(attn_gain, 3)
    return (
        out_hidden,
        grad_hidden,
        dense[:, SHARE : 2 * SHARE],
        dense[:, 2 * SHARE : 2 * SHARE + LANES],
        dense[:, 2 * SHARE + LANES : at],
        dense[:, :SHARE].T,
        attn_gain,
        dense[:, at + EXPERTS],
        dense[:, at : at + EXPERTS],
        grad_w_gate,
        grad_w_up,
        grad_w_down,
    )


def solution(mesh):
    in_specs = (
        P("dp", None),
        P(),
        P(),
        P("dp", None),
        P(),
        P(None, "mp"),
        P(None, "mp"),
        P(None, "mp"),
        P("mp", None),
        P(),
        P(),
        P("dp", None, "mp"),
        P("dp", None, "mp"),
        P("dp", "mp", None),
        P("dp", None),
    )
    out_specs = (
        P("dp", "mp"),
        P("dp", "mp"),
        P("dp", "mp"),
        P("dp", "mp"),
        P("dp", "mp"),
        P("mp", "dp"),
        P("dp"),
        P("dp"),
        P("dp", None),
        P("dp", None, "mp"),
        P("dp", None, "mp"),
        P("dp", "mp", None),
    )
    return jax.shard_map(
        per_device, mesh=mesh, in_specs=in_specs, out_specs=out_specs, check_vma=False
    )
```

```python
import jax
import jax.numpy as jnp
import numpy as np
from jax import lax
from jax.experimental import pallas as pl
from jax.experimental.pallas import tpu as pltpu
from jax.sharding import PartitionSpec as P

HEAD_DIM = 64
EXPERTS = 32
BLOCK = 512
MAXLEN = 2048
CAP = 160
WIDTH = 1024
SHARE = 256
QUARTER = 40
SLOTS = 1280
LANES = 128
PACKED = 384

epsilon = 1e-06
residual_mult = 0.22
score_mult = 0.015625
rope_base = 10000.0
masked_score = -1e30

NN = (((1,), (0,)), ((), ()))
NT = (((1,), (1,)), ((), ()))
TN = (((0,), (0,)), ((), ()))


def mm(a, b, dims=NN):
    return lax.dot_general(a, b, dims, preferred_element_type=jnp.float32)


def to_all(x):
    return lax.all_to_all(x, "dp", 0, 0, tiled=True)


def peer(x, flip):
    return lax.ppermute(x, "mp", [(i, i ^ flip) for i in range(4)])


def after(x, *others):
    return lax.optimization_barrier((x, *others))[0]


def vmem():
    return pl.BlockSpec(memory_space=pltpu.VMEM)


def smem():
    return pl.BlockSpec(memory_space=pltpu.SMEM)


def tiles(rows, width, row0=0):
    return pl.BlockSpec((rows, width), lambda i: (i + row0, 0))


def fixed(rows, width):
    return pl.BlockSpec((rows, width), lambda i: (0, 0))


def once(*shape):
    return pl.BlockSpec(shape, lambda i: (0,) * len(shape), pipeline_mode=pl.Buffered(1))


def run(kernel, name, steps, in_specs, out_specs, out_shape, args, estimate, scratch=(), free=(), limit=60):
    in_specs = [once(*a.shape) if s is None else s for s, a in zip(in_specs, args)]
    out_specs = [once(*o.shape) if s is None else s for s, o in zip(out_specs, out_shape)]
    args = [
        a
        if s.memory_space is not None or i in free
        else pltpu.with_memory_space_constraint(a, pltpu.HBM)
        for i, (s, a) in enumerate(zip(in_specs, args))
    ]
    out_shape = [
        o if s.memory_space == pltpu.SMEM else pltpu.HBM(o.shape, o.dtype)
        for s, o in zip(out_specs, out_shape)
    ]
    return pl.pallas_call(
        kernel,
        name=name,
        grid=(steps,),
        in_specs=in_specs,
        out_specs=out_specs,
        out_shape=out_shape,
        scratch_shapes=list(scratch),
        compiler_params=pltpu.CompilerParams(vmem_limit_bytes=limit << 20),
        cost_estimate=estimate,
    )(*args)


def out(shape, dtype):
    return jax.ShapeDtypeStruct(shape, dtype)


def cost(flops, moved, exps=0):
    return pl.CostEstimate(flops=flops, bytes_accessed=moved, transcendentals=exps)


def rope_constants():
    frequency = rope_base ** (-(np.arange(HEAD_DIM // 2, dtype=np.float64) * 2.0) / HEAD_DIM)
    wide = np.tile(frequency, 4)[None, :]
    made = []
    for count, apart in ((BLOCK // 16, 16), (16, 1), (8, BLOCK)):
        angles = np.arange(count, dtype=np.float64)[:, None] * apart * wide
        made += [np.cos(angles), np.sin(angles)]
    return [jnp.asarray(a.astype(np.float32)) for a in made]


def half_front(rows):
    lane = lax.broadcasted_iota(jnp.int32, (rows, LANES), 1)
    return (lane % HEAD_DIM) < HEAD_DIM // 2


def turned(chunk, cosine, signed_sine, back=False):
    partner = jnp.where(
        half_front(chunk.shape[0]), pltpu.roll(chunk, 96, 1), pltpu.roll(chunk, 32, 1)
    )
    if back:
        return chunk * cosine - partner * signed_sine
    return chunk * cosine + partner * signed_sine


def block_tables_in(lengths_ref, order_ref, rank_ref, offset_ref, inverse_ref, reach_ref, wanted_ref, later_ref, live_ref):
    count = order_ref.shape[0]
    steps = MAXLEN // BLOCK - 1

    def sequence(s, begin):
        def one(j, at):
            offset_ref[jnp.minimum(at, count - 1)] = j
            return at + 1

        return lax.fori_loop(0, lengths_ref[s], one, begin)

    lax.fori_loop(0, lengths_ref.shape[0], sequence, jnp.int32(0))

    def invert(d, carry):
        inverse_ref[order_ref[d]] = d
        return carry

    lax.fori_loop(0, count, invert, jnp.int32(0))
    reach_ref[0] = offset_ref[order_ref[rank_ref[0]]]

    def look(d, carry):
        packed = order_ref[d]
        for s in range(1, steps + 1):
            wanted_ref[d * steps + s - 1] = inverse_ref[jnp.maximum(packed - s, 0)]
            next_at = jnp.minimum(packed + s, count - 1)
            later_ref[d * steps + s - 1] = inverse_ref[next_at] * steps + s - 1
            is_live = jnp.logical_and(packed + s < count, offset_ref[next_at] >= s)
            live_ref[d * steps + s - 1] = jnp.where(is_live, 1, 0)
        return carry

    lax.fori_loop(0, count, look, jnp.int32(0))


def project_kernel(
    lengths_ref, order_ref, rank_ref, x_ref, gain_ref, wq_ref, wk_ref, wv_ref,
    cos16_ref, sin16_ref, cos1_ref, sin1_ref, cos0_ref, sin0_ref,
    normed_ref, q_ref, kv_ref, cosine_ref, sine_ref, reach_ref, wanted_ref, later_ref, live_ref,
    offset_ref, inverse_ref,
):
    @pl.when(pl.program_id(0) == 0)
    def _():
        block_tables_in(
            lengths_ref, order_ref, rank_ref, offset_ref, inverse_ref, reach_ref, wanted_ref, later_ref, live_ref
        )

    x = x_ref[...].astype(jnp.float32)
    scale = lax.rsqrt(jnp.mean(x * x, axis=1, keepdims=True) + epsilon)
    normed = (x * scale * gain_ref[...]).astype(jnp.bfloat16)
    normed_ref[...] = normed
    at = reach_ref[0]
    cos0, sin0 = cos0_ref[pl.ds(at, 1), :], sin0_ref[pl.ds(at, 1), :]
    cos16 = cos16_ref[...] * cos0 - sin16_ref[...] * sin0
    sin16 = sin16_ref[...] * cos0 + cos16_ref[...] * sin0
    cos1, sin1 = cos1_ref[...][None], sin1_ref[...][None]
    cosine = (cos16[:, None, :] * cos1 - sin16[:, None, :] * sin1).reshape(x.shape[0], LANES)
    sine = (sin16[:, None, :] * cos1 + cos16[:, None, :] * sin1).reshape(x.shape[0], LANES)
    sine = jnp.where(half_front(x.shape[0]), -sine, sine)
    cosine_ref[...] = cosine
    sine_ref[...] = sine
    kv_ref[:, :LANES] = turned(mm(normed, wk_ref[...]), cosine, sine).astype(jnp.bfloat16)
    kv_ref[:, LANES:] = mm(normed, wv_ref[...]).astype(jnp.bfloat16)
    queries = mm(normed, wq_ref[...])
    for i in range(0, SHARE, LANES):
        q_ref[:, i : i + LANES] = turned(queries[:, i : i + LANES], cosine, sine).astype(jnp.bfloat16)


def project(lengths, order, rank, x, gain, w_query, w_key, w_value):
    tile = 256
    count = order.shape[0]
    steps = MAXLEN // BLOCK - 1
    bf16, f32 = jnp.bfloat16, jnp.float32
    return run(
        project_kernel,
        "project",
        BLOCK // tile,
        [smem()] * 3
        + [tiles(tile, WIDTH), None, None, None, None]
        + [tiles(tile // 16, LANES)] * 2
        + [None] * 4,
        [tiles(tile, WIDTH), tiles(tile, SHARE), tiles(tile, SHARE)]
        + [tiles(tile, LANES)] * 2
        + [smem()] * 4,
        [out((BLOCK, WIDTH), bf16), out((BLOCK, SHARE), bf16), out((BLOCK, SHARE), bf16)]
        + [out((BLOCK, LANES), f32)] * 2
        + [out((1,), jnp.int32)]
        + [out((count * steps,), jnp.int32)] * 3,
        (lengths, order, rank, x, gain, w_query, w_key, w_value, *rope_constants()),
        cost(540_000_000, 4_000_000, 512),
        [pltpu.SMEM((count,), jnp.int32), pltpu.SMEM((count,), jnp.int32)],
    )


def pick_kernel(wanted_ref, pieces_ref, picked_ref):
    def one(i, carry):
        picked_ref[i] = pieces_ref[wanted_ref[i]]
        return carry

    lax.fori_loop(0, picked_ref.shape[0], one, jnp.int32(0), unroll=4)


def pick_pieces(wanted, pieces):
    shape = out((wanted.shape[0], *pieces.shape[1:]), pieces.dtype)
    return run(
        pick_kernel, "pick_pieces", 1, [smem(), None], [None], [shape], (wanted, pieces), cost(0, 1_100_000), free=(1,)
    )[0]


def sum_kernel(later_ref, live_ref, pieces_ref, sum_ref):
    steps = MAXLEN // BLOCK - 1

    def one(d, carry):
        total = jnp.zeros(sum_ref.shape[1:], jnp.float32)
        for s in range(steps):
            part = pieces_ref[later_ref[d * steps + s]].astype(jnp.float32)
            total = total + jnp.where(live_ref[d * steps + s] == 1, part, 0.0)
        sum_ref[d] = total.astype(sum_ref.dtype)
        return carry

    lax.fori_loop(0, sum_ref.shape[0], one, jnp.int32(0), unroll=2)


def sum_pieces(later, live, pieces, count):
    shape = out((count, *pieces.shape[1:]), pieces.dtype)
    return run(
        sum_kernel,
        "sum_pieces",
        1,
        [smem(), smem(), None],
        [None],
        [shape],
        (later, live, pieces),
        cost(0, 1_100_000),
        free=(2,),
    )[0]


def pack_kernel(down_ref, gate_ref, up_ref, packed_ref):
    packed_ref[:LANES, :] = down_ref[...]
    for k in range(4):
        rows = slice(k * SHARE, (k + 1) * SHARE)
        packed_ref[LANES:, k * SHARE : k * SHARE + LANES] = gate_ref[rows, :]
        packed_ref[LANES:, k * SHARE + LANES : (k + 1) * SHARE] = up_ref[rows, :]


def pack_weights(w_down, w_gate, w_up):
    shape = out((PACKED, WIDTH), jnp.bfloat16)
    return run(
        pack_kernel, "pack_weights", 1, [None] * 3, [None], [shape], (w_down, w_gate, w_up), cost(0, 1_600_000)
    )[0]


def route_kernel(begin_ref, routes_ref, picks_ref, ranks_ref):
    tokens = routes_ref.shape[1]
    expert_at = lax.broadcasted_iota(jnp.int32, (LANES, tokens), 0)
    hits = jnp.zeros((LANES, tokens), jnp.float32)
    for k in range(routes_ref.shape[0]):
        hits = hits + jnp.where(routes_ref[k : k + 1, :] == expert_at, 1.0, 0.0)
    row_at = lax.broadcasted_iota(jnp.int32, (tokens, tokens), 0)
    column_at = lax.broadcasted_iota(jnp.int32, (tokens, tokens), 1)
    before = jnp.where(row_at < column_at, 1.0, 0.0).astype(jnp.bfloat16)
    ranks = jnp.where(hits > 0.5, mm(hits.astype(jnp.bfloat16), before), -1.0)
    ranks_ref[...] = ranks
    slot_at = lax.broadcasted_iota(jnp.int32, (QUARTER, tokens), 0) + begin_ref[0]
    slot_at = slot_at.astype(jnp.float32)
    for e in range(EXPERTS):
        picks_ref[e * QUARTER : (e + 1) * QUARTER, :] = jnp.where(
            ranks[e : e + 1, :] == slot_at, 1.0, 0.0
        ).astype(jnp.bfloat16)


def route(begin, routes_t):
    return run(
        route_kernel,
        "route",
        1,
        [smem(), None],
        [None, None],
        [out((SLOTS, BLOCK), jnp.bfloat16), out((LANES, BLOCK), jnp.float32)],
        (begin, routes_t),
        cost(100_000_000, 1_600_000),
        free=(1,),
    )


def padded_columns(rows_t, out_ref):
    zero = jnp.zeros((HEAD_DIM, rows_t.shape[1]), out_ref.dtype)
    for h in range(4):
        mine = rows_t[h * HEAD_DIM : (h + 1) * HEAD_DIM].astype(out_ref.dtype)
        at = (h // 2) * HEAD_DIM
        out_ref[h, pl.ds(at, HEAD_DIM), :] = mine
        out_ref[h, pl.ds(HEAD_DIM - at, HEAD_DIM), :] = zero


def padded_rows(rows, out_ref):
    n = rows.shape[0]
    lane = lax.broadcasted_iota(jnp.int32, (n, 128), 1)
    for h in range(4):
        pair = rows[:, (h // 2) * 128 : (h // 2) * 128 + 128].astype(jnp.float32)
        if h % 2 != h // 2:
            pair = pltpu.roll(pair, HEAD_DIM, 1)
        own = (lane < HEAD_DIM) if h // 2 == 0 else (lane >= HEAD_DIM)
        out_ref[pl.ds(h * n, n), :] = jnp.where(own, pair, 0.0).astype(out_ref.dtype)


def attend_block(key_rows, value_rows, first, qpad_ref, max_ref, sum_ref, out_t_ref):
    half = BLOCK // 2
    for h in range(4):
        group = (h // 2) * HEAD_DIM
        for t in range(2):
            cols = slice(t * half, (t + 1) * half)
            rows = half if first and t == 0 else BLOCK
            scores = mm(key_rows[:rows], qpad_ref[h, :, cols])
            if first:
                key_at = lax.broadcasted_iota(jnp.int32, scores.shape, 0)
                query_at = lax.broadcasted_iota(jnp.int32, scores.shape, 1) + t * half
                scores = jnp.where(key_at > query_at, masked_score, scores)
            new_max = jnp.max(scores, axis=0, keepdims=True)
            if not first:
                old_max = max_ref[h : h + 1, cols]
                new_max = jnp.maximum(new_max, old_max)
                shrink = jnp.exp(old_max - new_max)
            weights = jnp.exp(scores - new_max)
            total = jnp.sum(weights, axis=0, keepdims=True)
            part = mm(value_rows[:rows], weights.astype(jnp.bfloat16), TN)[group : group + HEAD_DIM]
            mine = pl.ds(h * HEAD_DIM, HEAD_DIM)
            if not first:
                total = total + sum_ref[h : h + 1, cols] * shrink
                part = part + out_t_ref[mine, cols] * shrink
            max_ref[h : h + 1, cols] = new_max
            sum_ref[h : h + 1, cols] = total
            out_t_ref[mine, cols] = part


def attend_own_kernel(q_ref, own_ref, qpad_ref, max_ref, sum_ref, out_t_ref):
    padded_columns(jnp.transpose(q_ref[...].astype(jnp.float32) * score_mult), qpad_ref)
    max_ref[...] = jnp.zeros_like(max_ref)
    sum_ref[...] = jnp.ones_like(sum_ref)
    attend_block(own_ref[:, :LANES], own_ref[:, LANES:], True, qpad_ref, max_ref, sum_ref, out_t_ref)


def attend_own(queries, own_kv):
    return pl.pallas_call(
        attend_own_kernel,
        name="attend_own",
        in_specs=[vmem()] * 2,
        out_specs=[vmem()] * 4,
        out_shape=[
            out((4, LANES, BLOCK), jnp.bfloat16),
            out((8, BLOCK), jnp.float32),
            out((8, BLOCK), jnp.float32),
            out((SHARE, BLOCK), jnp.float32),
        ],
        compiler_params=pltpu.CompilerParams(vmem_limit_bytes=36 << 20),
        cost_estimate=cost(1_000_000_000, 2_000_000, 600_000),
    )(queries, own_kv)


def attend_kernel(
    reach_ref, qpad_ref, max0_ref, sum0_ref, out0_ref, prev_ref, att_ref, out_t_ref, lse_ref, max_ref, sum_ref
):
    max_ref[...] = max0_ref[...]
    sum_ref[...] = sum0_ref[...]
    out_t_ref[...] = out0_ref[...]

    @pl.loop(1, reach_ref[0] + 1)
    def _(step):
        rows = prev_ref[:, pl.ds(step - 1, 1)].reshape(BLOCK, SHARE)
        attend_block(rows[:, :LANES], rows[:, LANES:], False, qpad_ref, max_ref, sum_ref, out_t_ref)

    lse_ref[...] = max_ref[...] + jnp.log(sum_ref[...])
    for h in range(4):
        mine = pl.ds(h * HEAD_DIM, HEAD_DIM)
        out_t_ref[mine, :] = out_t_ref[mine, :] / sum_ref[h : h + 1, :]
    att_ref[...] = jnp.transpose(out_t_ref[...]).astype(jnp.bfloat16)


def attend(reach, begun, earlier):
    return run(
        attend_kernel,
        "attend",
        1,
        [smem()] + [vmem()] * 5,
        [None] * 3,
        [
            out((BLOCK, SHARE), jnp.bfloat16),
            out((SHARE, BLOCK), jnp.float32),
            out((8, BLOCK), jnp.float32),
        ],
        (reach, *begun, earlier),
        cost(4_000_000_000, 3_000_000, 3_000_000),
        [pltpu.VMEM((8, BLOCK), jnp.float32), pltpu.VMEM((8, BLOCK), jnp.float32)],
        limit=36,
    )


def attend_back_kernel(
    reach_ref, q_ref, qpad_ref, own_ref, prev_ref, grad_ref, grad_t_ref, out_t_ref, lse_ref, cos_ref, sin_ref,
    qgrad_ref, own_grad_ref, prev_grad_ref,
    gpad_ref, qrows_ref, grows_ref, ds_ref, p_ref, delta_ref, dq_ref,
):
    half = BLOCK // 2
    q_scaled = q_ref[...].astype(jnp.float32) * score_mult
    padded_rows(q_scaled, qrows_ref)
    padded_columns(grad_t_ref[...], gpad_ref)
    padded_rows(grad_ref[...], grows_ref)
    both = grad_t_ref[...].astype(jnp.float32) * out_t_ref[...]
    for h in range(4):
        delta_ref[h : h + 1, :] = jnp.sum(
            both[h * HEAD_DIM : (h + 1) * HEAD_DIM], axis=0, keepdims=True
        )


    def block(key_rows, value_rows, first):
        for h in range(4):
            for t in range(2):
                cols = slice(t * half, (t + 1) * half)
                wide = slice(h * BLOCK + t * half, h * BLOCK + (t + 1) * half)
                rows = half if first and t == 0 else BLOCK
                scores = mm(key_rows[:rows], qpad_ref[h, :, cols])
                weights = jnp.exp(scores - lse_ref[h : h + 1, cols])
                if first:
                    key_at = lax.broadcasted_iota(jnp.int32, scores.shape, 0)
                    query_at = lax.broadcasted_iota(jnp.int32, scores.shape, 1) + t * half
                    weights = jnp.where(key_at > query_at, 0.0, weights)
                weight_grad = mm(value_rows[:rows], gpad_ref[h, :, cols])
                score_grad = weights * (weight_grad - delta_ref[h : h + 1, cols])
                p_ref[:rows, wide] = weights.astype(jnp.bfloat16)
                ds_ref[:rows, wide] = score_grad.astype(jnp.bfloat16)
                if rows < BLOCK:
                    p_ref[rows:, wide] = jnp.zeros((BLOCK - rows, half), jnp.bfloat16)
                    ds_ref[rows:, wide] = jnp.zeros((BLOCK - rows, half), jnp.bfloat16)
        key_grad = mm(ds_ref[...], qrows_ref[...])
        value_grad = mm(p_ref[...], grows_ref[...])
        for h in range(4):
            group = (h // 2) * HEAD_DIM
            mine = pl.ds(h * HEAD_DIM, HEAD_DIM)
            part = mm(key_rows, ds_ref[:, h * BLOCK : (h + 1) * BLOCK], TN)[group : group + HEAD_DIM]
            dq_ref[mine, :] = part if first else dq_ref[mine, :] + part
        return key_grad, value_grad

    key_grad, value_grad = block(own_ref[:, :LANES], own_ref[:, LANES:], True)
    own_grad_ref[:, :LANES] = key_grad
    own_grad_ref[:, LANES:] = value_grad

    @pl.loop(1, reach_ref[0] + 1)
    def _(step):
        rows = prev_ref[:, pl.ds(step - 1, 1)].reshape(BLOCK, SHARE)
        key_grad, value_grad = block(rows[:, :LANES], rows[:, LANES:], False)
        parts = prev_grad_ref.shape[0]
        shape = (parts, 1, BLOCK // parts, LANES)
        prev_grad_ref[:, pl.ds(step - 1, 1), :, :LANES] = key_grad.astype(jnp.bfloat16).reshape(shape)
        prev_grad_ref[:, pl.ds(step - 1, 1), :, LANES:] = value_grad.astype(jnp.bfloat16).reshape(shape)

    query_grad = jnp.transpose(dq_ref[...]) * score_mult
    for i in range(0, SHARE, LANES):
        qgrad_ref[:, i : i + LANES] = turned(
            query_grad[:, i : i + LANES], cos_ref[...], sin_ref[...], back=True
        ).astype(jnp.bfloat16)


def attend_back(reach, queries, padded, own_kv, earlier, grad, grad_t, out_t, lse, cosine, signed_sine):
    return run(
        attend_back_kernel,
        "attend_back",
        1,
        [smem()] + [vmem()] * 10,
        [None] * 3,
        [
            out((BLOCK, SHARE), jnp.bfloat16),
            out((BLOCK, SHARE), jnp.float32),
            out(earlier.shape, jnp.bfloat16),
        ],
        (reach, queries, padded, own_kv, earlier, grad, grad_t, out_t, lse, cosine, signed_sine),
        cost(12_000_000_000, 5_000_000, 3_000_000),
        [
            pltpu.VMEM((4, LANES, BLOCK), jnp.bfloat16),
            pltpu.VMEM((4 * BLOCK, LANES), jnp.bfloat16),
            pltpu.VMEM((4 * BLOCK, LANES), jnp.bfloat16),
            pltpu.VMEM((BLOCK, 4 * BLOCK), jnp.bfloat16),
            pltpu.VMEM((BLOCK, 4 * BLOCK), jnp.bfloat16),
            pltpu.VMEM((8, BLOCK), jnp.float32),
            pltpu.VMEM((SHARE, BLOCK), jnp.float32),
        ],
        limit=36,
    )


def residual_kernel(
    a0, a1, a2, a3, w0, w1, w2, w3, x_ref, gain_ref, router_ref, ranks_ref,
    residual_ref, moe_ref, gates_ref,
):
    branch = mm(a0[...], w0[...])
    for a, w in ((a1, w1), (a2, w2), (a3, w3)):
        branch = branch + mm(a[...], w[...])
    residual = x_ref[...].astype(jnp.float32) + residual_mult * branch
    residual_ref[...] = residual
    scale = lax.rsqrt(jnp.mean(residual * residual, axis=1, keepdims=True) + epsilon)
    moe_in = (residual * scale * gain_ref[...]).astype(jnp.bfloat16)
    moe_ref[:, :WIDTH] = moe_in
    logits = mm(router_ref[...], moe_in, NT)
    chosen = ranks_ref[...] >= 0.0
    kept = jnp.where(chosen, logits, masked_score)
    top = jnp.max(kept, axis=0, keepdims=True)
    raised = jnp.where(chosen, jnp.exp(kept - top), 0.0)
    gates = raised / jnp.sum(raised, axis=0, keepdims=True)
    gates_ref[...] = gates
    moe_ref[:, WIDTH:] = (residual_mult * jnp.transpose(gates)).astype(jnp.bfloat16)


def residual_step(attended, w_out, x, gain, router_t, ranks):
    tile = 256
    by_columns = pl.BlockSpec((LANES, tile), lambda i: (0, i))
    return run(
        residual_kernel,
        "residual_step",
        BLOCK // tile,
        [tiles(tile, SHARE)] * 4 + [None] * 4 + [tiles(tile, WIDTH), None, None, by_columns],
        [tiles(tile, WIDTH), tiles(tile, WIDTH + LANES), by_columns],
        [
            out((BLOCK, WIDTH), jnp.float32),
            out((BLOCK, WIDTH + LANES), jnp.bfloat16),
            out((LANES, BLOCK), jnp.float32),
        ],
        (*attended, *w_out, x, gain, router_t, ranks),
        cost(1_200_000_000, 8_000_000, 70_000),
        free=(1, 2, 3, 5, 6, 7, 10),
    )


def mix_kernel(begin_ref, ranks_ref, moe_ref, mix_ref):
    ranks = jnp.transpose(ranks_ref[...]).astype(jnp.bfloat16)
    gates = moe_ref[:, WIDTH:]
    width = 640
    for at in range(0, SLOTS, width):
        expert_at = lax.broadcasted_iota(jnp.int32, (LANES, width), 0)
        first = expert_at * QUARTER - at
        slot_at = lax.broadcasted_iota(jnp.int32, (LANES, width), 1)
        inside = jnp.logical_and(slot_at >= first, slot_at < first + QUARTER)
        spread = jnp.where(inside, 1.0, 0.0).astype(jnp.bfloat16)
        within = jnp.sum(jnp.where(inside, slot_at - first, 0), axis=0, keepdims=True) + begin_ref[0]
        hit = mm(ranks, spread) == within.astype(jnp.float32)
        mix_ref[:, at : at + width] = jnp.where(hit, mm(gates, spread), 0.0).astype(jnp.bfloat16)


def mix_weights(begin, ranks, moe_cat):
    return run(
        mix_kernel,
        "mix_weights",
        1,
        [smem(), None, None],
        [None],
        [out((BLOCK, SLOTS), jnp.bfloat16)],
        (begin, ranks, moe_cat),
        cost(350_000_000, 3_000_000),
    )[0]


def expert_kernel(
    lane_ref, x_ref, grad_ref, p0, p1, p2, p3,
    out_ref, row_ref, hidden_ref, units_ref,
):
    packed = (p0, p1, p2, p3)
    rows = out_ref.shape[0]
    here = pl.ds(pl.program_id(0) * rows, rows)
    lane = lax.broadcasted_iota(jnp.int32, (rows, LANES), 1) == lane_ref[0]
    gate = jnp.sum(
        jnp.where(lane, x_ref[here, WIDTH:].astype(jnp.float32), 0.0), axis=1, keepdims=True
    )
    x = x_ref[here, :WIDTH]
    grad = grad_ref[...]
    gates, ups, sigmoids, hidden = [], [], [], []
    for p in packed:
        pre = None
        for k in range(4):
            columns = slice(k * SHARE, (k + 1) * SHARE)
            term = mm(x[:, columns], p[LANES:, columns])
            pre = term if pre is None else pre + term
        gate_pre, up_pre = pre[:, :LANES], pre[:, LANES:]
        sigmoid = 1.0 / (1.0 + jnp.exp(-gate_pre))
        gates.append(gate_pre)
        ups.append(up_pre)
        sigmoids.append(sigmoid)
        hidden.append(gate_pre * sigmoid * up_pre)
    hidden_low = jnp.concatenate([h.astype(jnp.bfloat16) for h in hidden], axis=1)
    down = jnp.concatenate([p[:LANES, :] for p in packed], axis=0)
    made = mm(hidden_low, down).astype(jnp.bfloat16)
    out_ref[...] = made
    gate_grad = jnp.sum(grad.astype(jnp.float32) * made.astype(jnp.float32), axis=1, keepdims=True)
    row_ref[:, WIDTH:] = jnp.where(lane, gate_grad, 0.0).astype(jnp.bfloat16)
    hidden_grad = mm(grad, down, NT)
    row = None
    for j, p in enumerate(packed):
        part = hidden_grad[:, j * LANES : (j + 1) * LANES]
        silu = gates[j] * sigmoids[j]
        gate_pre_grad = part * ups[j] * sigmoids[j] * (1.0 + gates[j] * (1.0 - sigmoids[j]))
        up_pre_grad = part * silu
        hidden_ref[:, j * LANES : (j + 1) * LANES] = (hidden[j] * gate).astype(jnp.bfloat16)
        units_ref[:, j * SHARE : j * SHARE + LANES] = (gate_pre_grad * gate).astype(jnp.bfloat16)
        units_ref[:, j * SHARE + LANES : (j + 1) * SHARE] = (up_pre_grad * gate).astype(jnp.bfloat16)
        both = jnp.concatenate([gate_pre_grad, up_pre_grad], axis=1).astype(jnp.bfloat16)
        terms = [
            mm(both, p[LANES:, k * SHARE : (k + 1) * SHARE], NT) for k in range(4)
        ]
        row = terms if row is None else [a + b for a, b in zip(row, terms)]
    for k in range(4):
        row_ref[:, k * SHARE : (k + 1) * SHARE] = row[k].astype(jnp.bfloat16)


def expert_step(lane, x, grad, packed):
    tile = 320
    return run(
        expert_kernel,
        "expert_step",
        SLOTS // tile,
        [smem(), vmem(), tiles(tile, WIDTH)] + [None] * 4,
        [tiles(tile, WIDTH), tiles(tile, WIDTH + LANES), tiles(tile, 512), tiles(tile, WIDTH)],
        [
            out((SLOTS, WIDTH), jnp.bfloat16),
            out((SLOTS, WIDTH + LANES), jnp.bfloat16),
            out((SLOTS, 512), jnp.bfloat16),
            out((SLOTS, WIDTH), jnp.bfloat16),
        ],
        (lane, x, grad, *packed),
        cost(8_000_000_000, 18_000_000, 700_000),
        limit=40,
    )


def unit_grads_kernel(x_ref, grad_ref, hidden_ref, units_ref, keep_ref, send_ref, turned_ref):
    step = pl.program_id(0)

    @pl.when(step == 0)
    def _():
        for k in range(4):
            columns = slice(k * SHARE, (k + 1) * SHARE)
            turned_ref[columns, :] = jnp.transpose(x_ref[:, columns])

    def write(to_ref):
        to_ref[0, :LANES, :] = mm(hidden_ref[...], grad_ref[...], TN).astype(jnp.bfloat16)
        for k in range(4):
            columns = slice(k * SHARE, (k + 1) * SHARE)
            to_ref[0, LANES:, columns] = mm(turned_ref[columns, :], units_ref[...]).astype(jnp.bfloat16)

    @pl.when(step < 2)
    def _():
        write(keep_ref)

    @pl.when(step >= 2)
    def _():
        write(send_ref)


def unit_grads(x, grad, hidden, units):
    rows = SHARE + LANES

    def share_of(i):
        return jnp.where(i < 2, 2 * i, 2 * i - 3)

    return run(
        unit_grads_kernel,
        "unit_grads",
        4,
        [
            vmem(),
            None,
            pl.BlockSpec((SLOTS, LANES), lambda i: (0, share_of(i))),
            pl.BlockSpec((SLOTS, SHARE), lambda i: (0, share_of(i))),
        ],
        [
            pl.BlockSpec((1, rows, WIDTH), lambda i: (jnp.minimum(i, 1), 0, 0)),
            pl.BlockSpec((1, rows, WIDTH), lambda i: (jnp.maximum(i - 2, 0), 0, 0)),
        ],
        [out((2, rows, WIDTH), jnp.bfloat16), out((2, rows, WIDTH), jnp.bfloat16)],
        (x, grad, hidden, units),
        cost(4_000_000_000, 12_000_000),
        [pltpu.VMEM((WIDTH, SLOTS), jnp.bfloat16)],
        limit=36,
    )


def unit_finish_kernel(mine_ref, got_ref, gate_ref, up_ref, down_ref):
    total = mine_ref[...].astype(jnp.float32) + got_ref[...].astype(jnp.float32)
    down_ref[0] = total[:LANES, :]
    for k in range(4):
        rows = slice(k * SHARE, (k + 1) * SHARE)
        gate_ref[0, rows, :] = total[LANES:, k * SHARE : k * SHARE + LANES]
        up_ref[0, rows, :] = total[LANES:, k * SHARE + LANES : (k + 1) * SHARE]


def unit_finish(mine, got):
    return run(
        unit_finish_kernel,
        "unit_finish",
        1,
        [None] * 2,
        [None] * 3,
        [
            out((1, WIDTH, LANES), jnp.float32),
            out((1, WIDTH, LANES), jnp.float32),
            out((1, LANES, WIDTH), jnp.float32),
        ],
        (mine, got),
        cost(1_000_000, 3_000_000),
        free=(0, 1),
    )


def home_kernel(rank_ref, mix_ref, rows_ref, keep_ref, send_ref):
    rank = rank_ref[0]
    extra = rows_ref.shape[1] > WIDTH
    for j in range(4):
        at = pl.multiple_of(jnp.bitwise_xor(rank, j) * SHARE, SHARE)
        total = mm(mix_ref[...], rows_ref[:, pl.ds(at, SHARE)])
        to_ref = send_ref if j % 2 else keep_ref
        to_ref[(j // 2) * BLOCK : (j // 2 + 1) * BLOCK, :] = total.astype(to_ref.dtype)
    if extra:
        gate_grads = jnp.transpose(mm(mix_ref[...], rows_ref[:, WIDTH:]))[:EXPERTS]
        for to_ref in (keep_ref, send_ref):
            for i in range(2):
                at = 2 * BLOCK + i * EXPERTS
                to_ref[at : at + EXPERTS, :] = gate_grads[:, i * SHARE : (i + 1) * SHARE].astype(
                    to_ref.dtype
                )


def sum_home(rank, mix, rows):
    height = 2 * BLOCK + (2 * EXPERTS if rows.shape[1] > WIDTH else 0)
    return run(
        home_kernel,
        "sum_home",
        1,
        [smem(), vmem(), vmem()],
        [None] * 2,
        [out((height, SHARE), jnp.float32), out((height, SHARE), jnp.bfloat16)],
        (rank, mix, rows),
        cost(1_500_000_000, 6_000_000),
        limit=36,
    )


def swap_kernel(mine_ref, got_ref, total_ref):
    mine, got = mine_ref, got_ref
    half = BLOCK
    total_ref[:half] = (mine[:half] + got[half : 2 * half].astype(jnp.float32)).astype(total_ref.dtype)
    total_ref[half : 2 * half] = (
        mine[half : 2 * half] + got[:half].astype(jnp.float32)
    ).astype(total_ref.dtype)
    total_ref[2 * half :] = (mine[2 * half :] + got[2 * half :].astype(jnp.float32)).astype(
        total_ref.dtype
    )


def swap_sum(mine, got):
    return run(
        swap_kernel,
        "swap_sum",
        1,
        [None] * 2,
        [None],
        [out(mine.shape, jnp.bfloat16)],
        (mine, got),
        cost(1_000_000, 2_500_000),
        free=(0, 1),
    )[0]


def norm_back_kernel(
    rank_ref, g0, g2, g1, g3, z_ref, gates_ref, residual_ref, gain_ref, router_ref, grad_ref, w_ref,
    low_ref, logit_ref, own_ref, att_ref, att_t_ref, gain_grad_ref, u_ref,
):
    rank = rank_ref[0]
    for flip, part in enumerate((g0, g1, g2, g3)):
        at = pl.multiple_of(jnp.bitwise_xor(rank, flip) * SHARE, SHARE)
        u_ref[:, pl.ds(at, SHARE)] = part[...].astype(jnp.float32)
    weighted_grads = z_ref[...].astype(jnp.float32)
    gates = gates_ref[:EXPERTS, :]
    inner = jnp.sum(weighted_grads, axis=0, keepdims=True)
    logit_grad = (weighted_grads - gates * inner).astype(jnp.bfloat16)
    logit_ref[...] = logit_grad
    u = u_ref[...] + mm(logit_grad, router_ref[:EXPERTS, :], TN)
    v = residual_ref[...]
    scale = lax.rsqrt(jnp.mean(v * v, axis=1, keepdims=True) + epsilon)
    weighted = u * gain_ref[...]
    mean = jnp.mean(weighted * v, axis=1, keepdims=True)
    total = grad_ref[...].astype(jnp.float32) + scale * weighted - v * (scale * scale * scale * mean)

    @pl.when(pl.program_id(0) == 0)
    def _():
        gain_grad_ref[...] = jnp.zeros_like(gain_grad_ref)

    gain_grad_ref[0:1, :] += jnp.sum(u * v * scale, axis=0, keepdims=True)
    low = (residual_mult * total).astype(jnp.bfloat16)
    low_ref[...] = low
    u_ref[...] = total
    own_ref[...] = u_ref[:, pl.ds(pl.multiple_of(rank * SHARE, SHARE), SHARE)]
    att_ref[...] = mm(low, w_ref[...], NT).astype(jnp.bfloat16)
    att_t_ref[...] = mm(w_ref[...], low, NT).astype(jnp.bfloat16)


def norm_back_step(rank, mine, theirs, gates, residual, gain, router_t, out_grad, w_out):
    tile = 256
    by_columns = pl.BlockSpec((EXPERTS, tile), lambda i: (0, i))
    return run(
        norm_back_kernel,
        "norm_back_step",
        BLOCK // tile,
        [smem()]
        + [tiles(tile, SHARE), tiles(tile, SHARE, BLOCK // tile)] * 2
        + [
            tiles(EXPERTS, SHARE, 2 * BLOCK // EXPERTS),
            pl.BlockSpec((LANES, tile), lambda i: (0, i)),
            tiles(tile, WIDTH),
            None,
            None,
            tiles(tile, WIDTH),
            None,
        ],
        [
            tiles(tile, WIDTH),
            by_columns,
            tiles(tile, SHARE),
            tiles(tile, SHARE),
            pl.BlockSpec((SHARE, tile), lambda i: (0, i)),
            fixed(8, WIDTH),
        ],
        [
            out((BLOCK, WIDTH), jnp.bfloat16),
            out((EXPERTS, BLOCK), jnp.bfloat16),
            out((BLOCK, SHARE), jnp.float32),
            out((BLOCK, SHARE), jnp.bfloat16),
            out((SHARE, BLOCK), jnp.bfloat16),
            out((8, WIDTH), jnp.float32),
        ],
        (rank, mine, mine, theirs, theirs, mine, gates, residual, gain, router_t, out_grad, w_out),
        cost(700_000_000, 9_000_000, 512),
        [pltpu.VMEM((tile, WIDTH), jnp.float32)],
        free=(3, 4, 9),
    )


def dense_grads_kernel(low_ref, attended_ref, normed_ref, qgrad_ref, logit_ref, moe_ref, gain_ref, made_ref):
    made_ref[:, :SHARE] = mm(low_ref[...], attended_ref[...], TN).astype(jnp.bfloat16)
    made_ref[:, SHARE : 2 * SHARE] = mm(normed_ref[...], qgrad_ref[...], TN).astype(jnp.bfloat16)
    router = mm(logit_ref[...], moe_ref[:, :WIDTH])
    stacked = jnp.concatenate(
        [router, gain_ref[...], jnp.zeros((LANES - EXPERTS - 8, WIDTH), jnp.float32)], axis=0
    )
    made_ref[:, 2 * SHARE :] = jnp.transpose(stacked).astype(jnp.bfloat16)


def dense_grads(low, attended, normed, qgrad, logit, moe_cat, gain_grad):
    return run(
        dense_grads_kernel,
        "dense_grads",
        1,
        [None] * 7,
        [None],
        [out((WIDTH, 2 * SHARE + LANES), jnp.bfloat16)],
        (low, attended, normed, qgrad, logit, moe_cat, gain_grad),
        cost(600_000_000, 6_000_000),
    )[0]


def last_grads_kernel(
    rank_ref, own_ref, home_ref, qgrad_ref, normed_ref, x_ref, wq_ref, wk_ref, wv_ref, cos_ref, sin_ref, made_ref,
    all_ref, keep_ref, send_ref, part_ref,
):
    rank = rank_ref[0]
    kv = own_ref[...] + home_ref[...].astype(jnp.float32)
    key_grad = turned(kv[:, :LANES], cos_ref[...], sin_ref[...], back=True).astype(jnp.bfloat16)
    value_grad = kv[:, LANES:].astype(jnp.bfloat16)
    both = jnp.concatenate([key_grad, value_grad], axis=1)
    all_ref[:, : 2 * SHARE] = made_ref[:, : 2 * SHARE]
    all_ref[:, 2 * SHARE : 3 * SHARE] = mm(normed_ref[...], both, TN).astype(jnp.bfloat16)
    gain = jnp.zeros((1, WIDTH), jnp.float32)
    tile = 128
    for i in range(0, BLOCK, tile):
        rows = slice(i, i + tile)
        part = mm(qgrad_ref[rows, :], wq_ref[...], NT)
        part = part + mm(key_grad[rows], wk_ref[...], NT) + mm(value_grad[rows], wv_ref[...], NT)
        x = x_ref[rows, :].astype(jnp.float32)
        scale = lax.rsqrt(jnp.mean(x * x, axis=1, keepdims=True) + epsilon)
        gain = gain + jnp.sum(part * x * scale, axis=0, keepdims=True)
        part_ref[rows, :] = part
    for j in range(4):
        at = pl.multiple_of(jnp.bitwise_xor(rank, j) * SHARE, SHARE)
        to_ref = send_ref if j % 2 else keep_ref
        to_ref[(j // 2) * BLOCK : (j // 2 + 1) * BLOCK, :] = part_ref[:, pl.ds(at, SHARE)].astype(to_ref.dtype)
    lane = lax.broadcasted_iota(jnp.int32, (WIDTH, LANES), 1)
    column = jnp.transpose(jnp.broadcast_to(gain, (LANES, WIDTH)))
    rest = jnp.where(lane == EXPERTS + 8, column, made_ref[:, 2 * SHARE :].astype(jnp.float32))
    all_ref[:, 3 * SHARE :] = rest.astype(jnp.bfloat16)


def last_grads(rank, own, home, qgrad, normed, x, w_query, w_key, w_value, cosine, sine, made):
    return run(
        last_grads_kernel,
        "last_grads",
        1,
        [smem()] + [None] * 11,
        [None] * 3,
        [
            out((WIDTH, 3 * SHARE + LANES), jnp.bfloat16),
            out((2 * BLOCK, SHARE), jnp.float32),
            out((2 * BLOCK, SHARE), jnp.bfloat16),
        ],
        (rank, own, home, qgrad, normed, x, w_query, w_key, w_value, cosine, sine, made),
        cost(1_000_000_000, 8_000_000, 512),
        [pltpu.VMEM((BLOCK, WIDTH), jnp.float32)],
        free=(2,),
    )


def per_device(
    hidden_in,
    lengths,
    block_order,
    routes,
    norm_gain_attn,
    w_query,
    w_key,
    w_value,
    w_out,
    norm_gain_moe,
    w_router,
    w_gate,
    w_up,
    w_down,
    out_grad,
):
    dp_count = block_order.shape[0]
    mp_rank = lax.axis_index("mp").astype(jnp.int32)
    column_start = mp_rank * SHARE
    piece = BLOCK // dp_count
    steps = MAXLEN // BLOCK - 1
    rank = mp_rank.reshape(1)
    lane = lax.axis_index("dp").astype(jnp.int32).reshape(1)
    begin = rank * QUARTER
    gain_attn = norm_gain_attn[None, :]
    gain_moe = norm_gain_moe[None, :]
    router_t = jnp.pad(w_router.T, ((0, LANES - EXPERTS), (0, 0)))

    normed, queries, key_value, cosine, sine, reach, wanted, later, live = project(
        lengths, block_order, lane, hidden_in, gain_attn, w_query, w_key, w_value
    )
    pieces = to_all(key_value.reshape(dp_count, piece, SHARE))
    picks, ranks = route(begin, after(routes.T, key_value))
    far_out = peer(after(w_out, key_value), 2)
    begun = attend_own(queries, after(key_value, picks))
    picked = pick_pieces(wanted, after(pieces, far_out))
    earlier = to_all(picked.reshape(dp_count, steps * piece, SHARE))
    earlier = earlier.reshape(dp_count, steps, piece, SHARE)

    outs = [w_out, peer(after(w_out, picked), 1), far_out, peer(far_out, 1)]

    grad_rows = jnp.dot(picks, after(out_grad, picked), preferred_element_type=jnp.bfloat16)
    grad_arrived = to_all(after(grad_rows, earlier, begun[1]).reshape(EXPERTS, QUARTER, WIDTH))
    attended, attended_t, lse = attend(reach, begun, earlier)
    far = peer(attended, 2)
    residual, moe_cat, gates = residual_step(
        [attended, peer(attended, 1), far, peer(far, 1)],
        outs,
        hidden_in,
        gain_moe,
        router_t,
        ranks,
    )
    own_pack = pack_weights(after(w_down[0], attended), w_gate[0], w_up[0])
    far_pack = peer(after(own_pack, far), 2)
    packed = [own_pack, peer(own_pack, 1), far_pack, peer(far_pack, 1)]

    moe_rows = jnp.dot(picks, moe_cat, preferred_element_type=jnp.bfloat16)
    grouped = to_all(after(moe_rows, far_pack).reshape(EXPERTS, QUARTER, -1)).reshape(SLOTS, -1)
    mix = mix_weights(begin, ranks, moe_cat)
    grouped_grad = grad_arrived.reshape(SLOTS, WIDTH)
    rows_out, row_grad, hidden_units, unit_grad = expert_step(lane, grouped, grouped_grad, packed)
    row_home = to_all(row_grad.reshape(dp_count, QUARTER, -1)).reshape(SLOTS, -1)
    unit_keep, unit_send = unit_grads(grouped, grouped_grad, hidden_units, unit_grad)
    unit_got = peer(unit_send, 1)
    keep, send = sum_home(rank, after(mix, unit_got), row_home)
    near = keep + peer(send, 1).astype(jnp.float32)
    near_low = near.astype(jnp.bfloat16)
    mine = swap_sum(near, peer(near_low, 2))
    unit_near = unit_keep.astype(jnp.float32) + after(unit_got, near_low).astype(jnp.float32)
    unit_low = unit_near[1].astype(jnp.bfloat16)
    theirs = peer(mine, 1)
    rows_home = to_all(after(rows_out, theirs).reshape(dp_count, QUARTER, -1)).reshape(SLOTS, -1)
    branch_grad, logit_grad, residual_grad, attended_grad, attended_grad_t, moe_gain = norm_back_step(
        rank, mine, theirs, gates, residual, gain_moe, router_t, out_grad, w_out
    )

    query_pre_grad, own_grads, later_grads = attend_back(
        reach,
        queries,
        begun[0],
        key_value,
        earlier,
        attended_grad,
        attended_grad_t,
        attended_t,
        lse,
        cosine,
        sine,
    )
    unit_far = peer(after(unit_low, later_grads), 2)
    later_pieces = to_all(after(later_grads, rows_home).reshape(dp_count, steps * piece, SHARE))
    summed = sum_pieces(
        later, live, after(later_pieces, unit_far).reshape(dp_count * steps, piece, SHARE), dp_count
    )
    kv_home = to_all(summed).reshape(BLOCK, SHARE)
    made = dense_grads(
        branch_grad, attended, normed, query_pre_grad, logit_grad, moe_cat, moe_gain
    )

    keep, send = sum_home(rank, mix, after(rows_home, summed))
    near_mix = keep + peer(send, 1).astype(jnp.float32)
    far_mix = peer(near_mix[BLOCK:].astype(jnp.bfloat16), 2)

    every, keep, send = last_grads(
        rank,
        own_grads,
        after(kv_home, far_mix),
        query_pre_grad,
        normed,
        hidden_in,
        w_query,
        w_key,
        w_value,
        cosine,
        sine,
        made,
    )
    near_norm = keep + peer(send, 1).astype(jnp.float32)
    sent_norm = near_norm[BLOCK:].astype(jnp.bfloat16)
    far_norm = peer(sent_norm, 2)
    arrived = to_all(every.reshape(dp_count, WIDTH // dp_count, -1))
    normed_grad = near_norm[:BLOCK] + far_norm.astype(jnp.float32)
    x = hidden_in.astype(jnp.float32)
    scale = lax.rsqrt(jnp.mean(x * x, axis=-1, keepdims=True) + epsilon)
    x_cols = lax.dynamic_slice_in_dim(x, column_start, SHARE, 1)
    weighted = normed_grad * lax.dynamic_slice_in_dim(gain_attn, column_start, SHARE, 1)
    inner = jnp.sum(weighted * x_cols, axis=1)
    inner = inner + peer(inner, 1) + peer(inner, 2) + peer(inner, 3)
    inner = inner[:, None] / WIDTH
    grad_hidden = residual_grad + scale * weighted - x_cols * (scale * scale * scale * inner)
    grad_w_gate, grad_w_up, grad_w_down = unit_finish(unit_near[0], unit_far)
    mixture = near_mix[:BLOCK] + far_mix.astype(jnp.float32)
    residual_cols = lax.dynamic_slice_in_dim(residual, column_start, SHARE, 1)
    out_hidden = (residual_cols + mixture).astype(jnp.bfloat16)

    dense = jnp.sum(arrived.astype(jnp.float32), axis=0)
    at = 3 * SHARE
    attn_gain = dense[:, at + EXPERTS + 8]
    attn_gain = attn_gain + peer(attn_gain, 1) + peer(attn_gain, 2) + peer(attn_gain, 3)
    return (
        out_hidden,
        grad_hidden,
        dense[:, SHARE : 2 * SHARE],
        dense[:, 2 * SHARE : 2 * SHARE + LANES],
        dense[:, 2 * SHARE + LANES : at],
        dense[:, :SHARE].T,
        attn_gain,
        dense[:, at + EXPERTS],
        dense[:, at : at + EXPERTS],
        grad_w_gate,
        grad_w_up,
        grad_w_down,
    )


def solution(mesh):
    in_specs = (
        P("dp", None),
        P(),
        P(),
        P("dp", None),
        P(),
        P(None, "mp"),
        P(None, "mp"),
        P(None, "mp"),
        P("mp", None),
        P(),
        P(),
        P("dp", None, "mp"),
        P("dp", None, "mp"),
        P("dp", "mp", None),
        P("dp", None),
    )
    out_specs = (
        P("dp", "mp"),
        P("dp", "mp"),
        P("dp", "mp"),
        P("dp", "mp"),
        P("dp", "mp"),
        P("mp", "dp"),
        P("dp"),
        P("dp"),
        P("dp", None),
        P("dp", None, "mp"),
        P("dp", None, "mp"),
        P("dp", "mp", None),
    )
    return jax.shard_map(
        per_device, mesh=mesh, in_specs=in_specs, out_specs=out_specs, check_vma=False
    )
```

```python
import jax
import jax.numpy as jnp
import numpy as np
from jax import lax
from jax.experimental import pallas as pl
from jax.experimental.pallas import tpu as pltpu
from jax.sharding import PartitionSpec as P

HEAD_DIM = 64
EXPERTS = 32
BLOCK = 512
MAXLEN = 2048
CAP = 160
WIDTH = 1024
SHARE = 256
QUARTER = 40
SLOTS = 1280
LANES = 128
PACKED = 384

epsilon = 1e-06
residual_mult = 0.22
score_mult = 0.015625
rope_base = 10000.0
masked_score = -1e30

NN = (((1,), (0,)), ((), ()))
NT = (((1,), (1,)), ((), ()))
TN = (((0,), (0,)), ((), ()))


def mm(a, b, dims=NN):
    return lax.dot_general(a, b, dims, preferred_element_type=jnp.float32)


def to_all(x):
    return lax.all_to_all(x, "dp", 0, 0, tiled=True)


def peer(x, flip):
    return lax.ppermute(x, "mp", [(i, i ^ flip) for i in range(4)])


def after(x, *others):
    return lax.optimization_barrier((x, *others))[0]


def vmem():
    return pl.BlockSpec(memory_space=pltpu.VMEM)


def smem():
    return pl.BlockSpec(memory_space=pltpu.SMEM)


def tiles(rows, width, row0=0):
    return pl.BlockSpec((rows, width), lambda i: (i + row0, 0))


def fixed(rows, width):
    return pl.BlockSpec((rows, width), lambda i: (0, 0))


def once(*shape):
    return pl.BlockSpec(shape, lambda i: (0,) * len(shape), pipeline_mode=pl.Buffered(1))


def run(kernel, name, steps, in_specs, out_specs, out_shape, args, estimate, scratch=(), free=(), limit=32):
    in_specs = [once(*a.shape) if s is None else s for s, a in zip(in_specs, args)]
    out_specs = [once(*o.shape) if s is None else s for s, o in zip(out_specs, out_shape)]
    args = [
        a
        if s.memory_space is not None or i in free
        else pltpu.with_memory_space_constraint(a, pltpu.HBM)
        for i, (s, a) in enumerate(zip(in_specs, args))
    ]
    out_shape = [
        o if s.memory_space == pltpu.SMEM else pltpu.HBM(o.shape, o.dtype)
        for s, o in zip(out_specs, out_shape)
    ]
    return pl.pallas_call(
        kernel,
        name=name,
        grid=(steps,),
        in_specs=in_specs,
        out_specs=out_specs,
        out_shape=out_shape,
        scratch_shapes=list(scratch),
        compiler_params=pltpu.CompilerParams(vmem_limit_bytes=limit << 20),
        cost_estimate=estimate,
    )(*args)


def out(shape, dtype):
    return jax.ShapeDtypeStruct(shape, dtype)


def cost(flops, moved, exps=0):
    return pl.CostEstimate(flops=flops, bytes_accessed=moved, transcendentals=exps)


def rope_constants():
    frequency = rope_base ** (-(np.arange(HEAD_DIM // 2, dtype=np.float64) * 2.0) / HEAD_DIM)
    wide = np.tile(frequency, 4)[None, :]
    made = []
    for count, apart in ((BLOCK // 16, 16), (16, 1), (8, BLOCK)):
        angles = np.arange(count, dtype=np.float64)[:, None] * apart * wide
        made += [np.cos(angles), np.sin(angles)]
    return [jnp.asarray(a.astype(np.float32)) for a in made]


def half_front(rows):
    lane = lax.broadcasted_iota(jnp.int32, (rows, LANES), 1)
    return (lane % HEAD_DIM) < HEAD_DIM // 2


def turned(chunk, cosine, signed_sine, back=False):
    partner = jnp.where(
        half_front(chunk.shape[0]), pltpu.roll(chunk, 96, 1), pltpu.roll(chunk, 32, 1)
    )
    if back:
        return chunk * cosine - partner * signed_sine
    return chunk * cosine + partner * signed_sine


def block_tables_in(lengths_ref, order_ref, rank_ref, offset_ref, inverse_ref, reach_ref, wanted_ref, later_ref, live_ref):
    count = order_ref.shape[0]
    steps = MAXLEN // BLOCK - 1

    def sequence(s, begin):
        def one(j, at):
            offset_ref[jnp.minimum(at, count - 1)] = j
            return at + 1

        return lax.fori_loop(0, lengths_ref[s], one, begin)

    lax.fori_loop(0, lengths_ref.shape[0], sequence, jnp.int32(0))

    def invert(d, carry):
        inverse_ref[order_ref[d]] = d
        return carry

    lax.fori_loop(0, count, invert, jnp.int32(0))
    reach_ref[0] = offset_ref[order_ref[rank_ref[0]]]

    def look(d, carry):
        packed = order_ref[d]
        for s in range(1, steps + 1):
            wanted_ref[d * steps + s - 1] = inverse_ref[jnp.maximum(packed - s, 0)]
            next_at = jnp.minimum(packed + s, count - 1)
            later_ref[d * steps + s - 1] = inverse_ref[next_at] * steps + s - 1
            is_live = jnp.logical_and(packed + s < count, offset_ref[next_at] >= s)
            live_ref[d * steps + s - 1] = jnp.where(is_live, 1, 0)
        return carry

    lax.fori_loop(0, count, look, jnp.int32(0))


def project_kernel(
    lengths_ref, order_ref, rank_ref, x_ref, gain_ref, wq_ref, wk_ref, wv_ref,
    cos16_ref, sin16_ref, cos1_ref, sin1_ref, cos0_ref, sin0_ref,
    normed_ref, q_ref, kv_ref, cosine_ref, sine_ref, reach_ref, wanted_ref, later_ref, live_ref,
    offset_ref, inverse_ref,
):
    @pl.when(pl.program_id(0) == 0)
    def _():
        block_tables_in(
            lengths_ref, order_ref, rank_ref, offset_ref, inverse_ref, reach_ref, wanted_ref, later_ref, live_ref
        )

    x = x_ref[...].astype(jnp.float32)
    scale = lax.rsqrt(jnp.mean(x * x, axis=1, keepdims=True) + epsilon)
    normed = (x * scale * gain_ref[...]).astype(jnp.bfloat16)
    normed_ref[...] = normed
    at = reach_ref[0]
    cos0, sin0 = cos0_ref[pl.ds(at, 1), :], sin0_ref[pl.ds(at, 1), :]
    cos16 = cos16_ref[...] * cos0 - sin16_ref[...] * sin0
    sin16 = sin16_ref[...] * cos0 + cos16_ref[...] * sin0
    cos1, sin1 = cos1_ref[...][None], sin1_ref[...][None]
    cosine = (cos16[:, None, :] * cos1 - sin16[:, None, :] * sin1).reshape(x.shape[0], LANES)
    sine = (sin16[:, None, :] * cos1 + cos16[:, None, :] * sin1).reshape(x.shape[0], LANES)
    sine = jnp.where(half_front(x.shape[0]), -sine, sine)
    cosine_ref[...] = cosine
    sine_ref[...] = sine
    kv_ref[:, :LANES] = turned(mm(normed, wk_ref[...]), cosine, sine).astype(jnp.bfloat16)
    kv_ref[:, LANES:] = mm(normed, wv_ref[...]).astype(jnp.bfloat16)
    queries = mm(normed, wq_ref[...])
    for i in range(0, SHARE, LANES):
        q_ref[:, i : i + LANES] = turned(queries[:, i : i + LANES], cosine, sine).astype(jnp.bfloat16)


def project(lengths, order, rank, x, gain, w_query, w_key, w_value):
    tile = 256
    count = order.shape[0]
    steps = MAXLEN // BLOCK - 1
    bf16, f32 = jnp.bfloat16, jnp.float32
    return run(
        project_kernel,
        "project",
        BLOCK // tile,
        [smem()] * 3
        + [tiles(tile, WIDTH), None, None, None, None]
        + [tiles(tile // 16, LANES)] * 2
        + [None] * 4,
        [tiles(tile, WIDTH), tiles(tile, SHARE), tiles(tile, SHARE)]
        + [tiles(tile, LANES)] * 2
        + [smem()] * 4,
        [out((BLOCK, WIDTH), bf16), out((BLOCK, SHARE), bf16), out((BLOCK, SHARE), bf16)]
        + [out((BLOCK, LANES), f32)] * 2
        + [out((1,), jnp.int32)]
        + [out((count * steps,), jnp.int32)] * 3,
        (lengths, order, rank, x, gain, w_query, w_key, w_value, *rope_constants()),
        cost(540_000_000, 4_000_000, 512),
        [pltpu.SMEM((count,), jnp.int32), pltpu.SMEM((count,), jnp.int32)],
    )


def pick_kernel(wanted_ref, pieces_ref, picked_ref):
    def one(i, carry):
        picked_ref[i] = pieces_ref[wanted_ref[i]]
        return carry

    lax.fori_loop(0, picked_ref.shape[0], one, jnp.int32(0), unroll=4)


def pick_pieces(wanted, pieces):
    shape = out((wanted.shape[0], *pieces.shape[1:]), pieces.dtype)
    return run(
        pick_kernel, "pick_pieces", 1, [smem(), None], [None], [shape], (wanted, pieces), cost(0, 1_100_000), free=(1,)
    )[0]


def sum_kernel(later_ref, live_ref, pieces_ref, sum_ref):
    steps = MAXLEN // BLOCK - 1

    def one(d, carry):
        total = jnp.zeros(sum_ref.shape[1:], jnp.float32)
        for s in range(steps):
            part = pieces_ref[later_ref[d * steps + s]].astype(jnp.float32)
            total = total + jnp.where(live_ref[d * steps + s] == 1, part, 0.0)
        sum_ref[d] = total.astype(sum_ref.dtype)
        return carry

    lax.fori_loop(0, sum_ref.shape[0], one, jnp.int32(0), unroll=2)


def sum_pieces(later, live, pieces, count):
    shape = out((count, *pieces.shape[1:]), pieces.dtype)
    return run(
        sum_kernel,
        "sum_pieces",
        1,
        [smem(), smem(), None],
        [None],
        [shape],
        (later, live, pieces),
        cost(0, 1_100_000),
        free=(2,),
    )[0]


def pack_kernel(down_ref, gate_ref, up_ref, packed_ref):
    packed_ref[:LANES, :] = down_ref[...]
    for k in range(4):
        rows = slice(k * SHARE, (k + 1) * SHARE)
        packed_ref[LANES:, k * SHARE : k * SHARE + LANES] = gate_ref[rows, :]
        packed_ref[LANES:, k * SHARE + LANES : (k + 1) * SHARE] = up_ref[rows, :]


def pack_weights(w_down, w_gate, w_up):
    shape = out((PACKED, WIDTH), jnp.bfloat16)
    return run(
        pack_kernel, "pack_weights", 1, [None] * 3, [None], [shape], (w_down, w_gate, w_up), cost(0, 1_600_000)
    )[0]


def route_kernel(begin_ref, routes_ref, picks_ref, ranks_ref):
    tokens = routes_ref.shape[1]
    expert_at = lax.broadcasted_iota(jnp.int32, (LANES, tokens), 0)
    hits = jnp.zeros((LANES, tokens), jnp.float32)
    for k in range(routes_ref.shape[0]):
        hits = hits + jnp.where(routes_ref[k : k + 1, :] == expert_at, 1.0, 0.0)
    row_at = lax.broadcasted_iota(jnp.int32, (tokens, tokens), 0)
    column_at = lax.broadcasted_iota(jnp.int32, (tokens, tokens), 1)
    before = jnp.where(row_at < column_at, 1.0, 0.0).astype(jnp.bfloat16)
    ranks = jnp.where(hits > 0.5, mm(hits.astype(jnp.bfloat16), before), -1.0)
    ranks_ref[...] = ranks
    slot_at = lax.broadcasted_iota(jnp.int32, (QUARTER, tokens), 0) + begin_ref[0]
    slot_at = slot_at.astype(jnp.float32)
    for e in range(EXPERTS):
        picks_ref[e * QUARTER : (e + 1) * QUARTER, :] = jnp.where(
            ranks[e : e + 1, :] == slot_at, 1.0, 0.0
        ).astype(jnp.bfloat16)


def route(begin, routes_t):
    return run(
        route_kernel,
        "route",
        1,
        [smem(), None],
        [None, None],
        [out((SLOTS, BLOCK), jnp.bfloat16), out((LANES, BLOCK), jnp.float32)],
        (begin, routes_t),
        cost(100_000_000, 1_600_000),
        free=(1,),
    )


def padded_columns(rows_t, out_ref):
    zero = jnp.zeros((HEAD_DIM, rows_t.shape[1]), out_ref.dtype)
    for h in range(4):
        mine = rows_t[h * HEAD_DIM : (h + 1) * HEAD_DIM].astype(out_ref.dtype)
        at = (h // 2) * HEAD_DIM
        out_ref[h, pl.ds(at, HEAD_DIM), :] = mine
        out_ref[h, pl.ds(HEAD_DIM - at, HEAD_DIM), :] = zero


def padded_rows(rows, out_ref):
    n = rows.shape[0]
    lane = lax.broadcasted_iota(jnp.int32, (n, 128), 1)
    for h in range(4):
        pair = rows[:, (h // 2) * 128 : (h // 2) * 128 + 128].astype(jnp.float32)
        if h % 2 != h // 2:
            pair = pltpu.roll(pair, HEAD_DIM, 1)
        own = (lane < HEAD_DIM) if h // 2 == 0 else (lane >= HEAD_DIM)
        out_ref[pl.ds(h * n, n), :] = jnp.where(own, pair, 0.0).astype(out_ref.dtype)


def attend_block(key_rows, value_rows, first, qpad_ref, max_ref, sum_ref, out_t_ref):
    half = BLOCK // 2
    for h in range(4):
        group = (h // 2) * HEAD_DIM
        for t in range(2):
            cols = slice(t * half, (t + 1) * half)
            rows = half if first and t == 0 else BLOCK
            scores = mm(key_rows[:rows], qpad_ref[h, :, cols])
            if first:
                key_at = lax.broadcasted_iota(jnp.int32, scores.shape, 0)
                query_at = lax.broadcasted_iota(jnp.int32, scores.shape, 1) + t * half
                scores = jnp.where(key_at > query_at, masked_score, scores)
            new_max = jnp.max(scores, axis=0, keepdims=True)
            if not first:
                old_max = max_ref[h : h + 1, cols]
                new_max = jnp.maximum(new_max, old_max)
                shrink = jnp.exp(old_max - new_max)
            weights = jnp.exp(scores - new_max)
            total = jnp.sum(weights, axis=0, keepdims=True)
            part = mm(value_rows[:rows], weights.astype(jnp.bfloat16), TN)[group : group + HEAD_DIM]
            mine = pl.ds(h * HEAD_DIM, HEAD_DIM)
            if not first:
                total = total + sum_ref[h : h + 1, cols] * shrink
                part = part + out_t_ref[mine, cols] * shrink
            max_ref[h : h + 1, cols] = new_max
            sum_ref[h : h + 1, cols] = total
            out_t_ref[mine, cols] = part


def attend_own_kernel(q_ref, own_ref, qpad_ref, max_ref, sum_ref, out_t_ref):
    padded_columns(jnp.transpose(q_ref[...].astype(jnp.float32) * score_mult), qpad_ref)
    max_ref[...] = jnp.zeros_like(max_ref)
    sum_ref[...] = jnp.ones_like(sum_ref)
    attend_block(own_ref[:, :LANES], own_ref[:, LANES:], True, qpad_ref, max_ref, sum_ref, out_t_ref)


def attend_own(queries, own_kv):
    return pl.pallas_call(
        attend_own_kernel,
        name="attend_own",
        in_specs=[vmem()] * 2,
        out_specs=[vmem()] * 4,
        out_shape=[
            out((4, LANES, BLOCK), jnp.bfloat16),
            out((8, BLOCK), jnp.float32),
            out((8, BLOCK), jnp.float32),
            out((SHARE, BLOCK), jnp.float32),
        ],
        compiler_params=pltpu.CompilerParams(vmem_limit_bytes=36 << 20),
        cost_estimate=cost(1_000_000_000, 2_000_000, 600_000),
    )(queries, own_kv)


def attend_kernel(
    reach_ref, qpad_ref, max0_ref, sum0_ref, out0_ref, prev_ref, att_ref, out_t_ref, lse_ref, max_ref, sum_ref
):
    max_ref[...] = max0_ref[...]
    sum_ref[...] = sum0_ref[...]
    out_t_ref[...] = out0_ref[...]

    @pl.loop(1, reach_ref[0] + 1)
    def _(step):
        rows = prev_ref[:, pl.ds(step - 1, 1)].reshape(BLOCK, SHARE)
        attend_block(rows[:, :LANES], rows[:, LANES:], False, qpad_ref, max_ref, sum_ref, out_t_ref)

    lse_ref[...] = max_ref[...] + jnp.log(sum_ref[...])
    for h in range(4):
        mine = pl.ds(h * HEAD_DIM, HEAD_DIM)
        out_t_ref[mine, :] = out_t_ref[mine, :] / sum_ref[h : h + 1, :]
    att_ref[...] = jnp.transpose(out_t_ref[...]).astype(jnp.bfloat16)


def attend(reach, begun, earlier):
    return run(
        attend_kernel,
        "attend",
        1,
        [smem()] + [vmem()] * 5,
        [None] * 3,
        [
            out((BLOCK, SHARE), jnp.bfloat16),
            out((SHARE, BLOCK), jnp.float32),
            out((8, BLOCK), jnp.float32),
        ],
        (reach, *begun, earlier),
        cost(4_000_000_000, 3_000_000, 3_000_000),
        [pltpu.VMEM((8, BLOCK), jnp.float32), pltpu.VMEM((8, BLOCK), jnp.float32)],
        limit=36,
    )


def attend_back_kernel(
    reach_ref, q_ref, qpad_ref, own_ref, prev_ref, grad_ref, grad_t_ref, out_t_ref, lse_ref, cos_ref, sin_ref,
    qgrad_ref, own_grad_ref, prev_grad_ref,
    gpad_ref, qrows_ref, grows_ref, ds_ref, p_ref, delta_ref, dq_ref,
):
    half = BLOCK // 2
    q_scaled = q_ref[...].astype(jnp.float32) * score_mult
    padded_rows(q_scaled, qrows_ref)
    padded_columns(grad_t_ref[...], gpad_ref)
    padded_rows(grad_ref[...], grows_ref)
    both = grad_t_ref[...].astype(jnp.float32) * out_t_ref[...]
    for h in range(4):
        delta_ref[h : h + 1, :] = jnp.sum(
            both[h * HEAD_DIM : (h + 1) * HEAD_DIM], axis=0, keepdims=True
        )


    def block(key_rows, value_rows, first):
        for h in range(4):
            for t in range(2):
                cols = slice(t * half, (t + 1) * half)
                wide = slice(h * BLOCK + t * half, h * BLOCK + (t + 1) * half)
                rows = half if first and t == 0 else BLOCK
                scores = mm(key_rows[:rows], qpad_ref[h, :, cols])
                weights = jnp.exp(scores - lse_ref[h : h + 1, cols])
                if first:
                    key_at = lax.broadcasted_iota(jnp.int32, scores.shape, 0)
                    query_at = lax.broadcasted_iota(jnp.int32, scores.shape, 1) + t * half
                    weights = jnp.where(key_at > query_at, 0.0, weights)
                weight_grad = mm(value_rows[:rows], gpad_ref[h, :, cols])
                score_grad = weights * (weight_grad - delta_ref[h : h + 1, cols])
                p_ref[:rows, wide] = weights.astype(jnp.bfloat16)
                ds_ref[:rows, wide] = score_grad.astype(jnp.bfloat16)
                if rows < BLOCK:
                    p_ref[rows:, wide] = jnp.zeros((BLOCK - rows, half), jnp.bfloat16)
                    ds_ref[rows:, wide] = jnp.zeros((BLOCK - rows, half), jnp.bfloat16)
        key_grad = mm(ds_ref[...], qrows_ref[...])
        value_grad = mm(p_ref[...], grows_ref[...])
        for h in range(4):
            group = (h // 2) * HEAD_DIM
            mine = pl.ds(h * HEAD_DIM, HEAD_DIM)
            part = mm(key_rows, ds_ref[:, h * BLOCK : (h + 1) * BLOCK], TN)[group : group + HEAD_DIM]
            dq_ref[mine, :] = part if first else dq_ref[mine, :] + part
        return key_grad, value_grad

    key_grad, value_grad = block(own_ref[:, :LANES], own_ref[:, LANES:], True)
    own_grad_ref[:, :LANES] = key_grad
    own_grad_ref[:, LANES:] = value_grad

    @pl.loop(1, reach_ref[0] + 1)
    def _(step):
        rows = prev_ref[:, pl.ds(step - 1, 1)].reshape(BLOCK, SHARE)
        key_grad, value_grad = block(rows[:, :LANES], rows[:, LANES:], False)
        parts = prev_grad_ref.shape[0]
        shape = (parts, 1, BLOCK // parts, LANES)
        prev_grad_ref[:, pl.ds(step - 1, 1), :, :LANES] = key_grad.astype(jnp.bfloat16).reshape(shape)
        prev_grad_ref[:, pl.ds(step - 1, 1), :, LANES:] = value_grad.astype(jnp.bfloat16).reshape(shape)

    query_grad = jnp.transpose(dq_ref[...]) * score_mult
    for i in range(0, SHARE, LANES):
        qgrad_ref[:, i : i + LANES] = turned(
            query_grad[:, i : i + LANES], cos_ref[...], sin_ref[...], back=True
        ).astype(jnp.bfloat16)


def attend_back(reach, queries, padded, own_kv, earlier, grad, grad_t, out_t, lse, cosine, signed_sine):
    return run(
        attend_back_kernel,
        "attend_back",
        1,
        [smem()] + [vmem()] * 10,
        [None] * 3,
        [
            out((BLOCK, SHARE), jnp.bfloat16),
            out((BLOCK, SHARE), jnp.float32),
            out(earlier.shape, jnp.bfloat16),
        ],
        (reach, queries, padded, own_kv, earlier, grad, grad_t, out_t, lse, cosine, signed_sine),
        cost(12_000_000_000, 5_000_000, 3_000_000),
        [
            pltpu.VMEM((4, LANES, BLOCK), jnp.bfloat16),
            pltpu.VMEM((4 * BLOCK, LANES), jnp.bfloat16),
            pltpu.VMEM((4 * BLOCK, LANES), jnp.bfloat16),
            pltpu.VMEM((BLOCK, 4 * BLOCK), jnp.bfloat16),
            pltpu.VMEM((BLOCK, 4 * BLOCK), jnp.bfloat16),
            pltpu.VMEM((8, BLOCK), jnp.float32),
            pltpu.VMEM((SHARE, BLOCK), jnp.float32),
        ],
        limit=36,
    )


def residual_kernel(
    a0, a1, a2, a3, w0, w1, w2, w3, x_ref, gain_ref, router_ref, ranks_ref, picks_ref,
    residual_ref, moe_ref, gates_ref, rows_ref, held_ref,
):
    step = pl.program_id(0)
    tile = x_ref.shape[0]

    @pl.when(step < BLOCK // tile)
    def _():
        branch = mm(a0[...], w0[...])
        for a, w in ((a1, w1), (a2, w2), (a3, w3)):
            branch = branch + mm(a[...], w[...])
        residual = x_ref[...].astype(jnp.float32) + residual_mult * branch
        residual_ref[...] = residual
        scale = lax.rsqrt(jnp.mean(residual * residual, axis=1, keepdims=True) + epsilon)
        moe_in = (residual * scale * gain_ref[...]).astype(jnp.bfloat16)
        moe_ref[:, :WIDTH] = moe_in
        logits = mm(router_ref[...], moe_in, NT)
        chosen = ranks_ref[...] >= 0.0
        kept = jnp.where(chosen, logits, masked_score)
        top = jnp.max(kept, axis=0, keepdims=True)
        raised = jnp.where(chosen, jnp.exp(kept - top), 0.0)
        gates = raised / jnp.sum(raised, axis=0, keepdims=True)
        gates_ref[...] = gates
        low = (residual_mult * jnp.transpose(gates)).astype(jnp.bfloat16)
        moe_ref[:, WIDTH:] = low
        held_ref[pl.ds(step * tile, tile), :WIDTH] = moe_in
        held_ref[pl.ds(step * tile, tile), WIDTH:] = low

    @pl.when(step >= BLOCK // tile)
    def _():
        rows_ref[...] = mm(picks_ref[...], held_ref[...]).astype(jnp.bfloat16)


def residual_step(attended, w_out, x, gain, router_t, ranks, picks):
    tile = 256
    first = BLOCK // tile
    slot_tile = SLOTS // 4

    def early(rows, width):
        return pl.BlockSpec((rows, width), lambda i: (jnp.minimum(i, first - 1), 0))

    def late(rows, width):
        return pl.BlockSpec((rows, width), lambda i: (jnp.maximum(i - first, 0), 0))

    by_columns = pl.BlockSpec((LANES, tile), lambda i: (0, jnp.minimum(i, first - 1)))
    return run(
        residual_kernel,
        "residual_step",
        first + 4,
        [early(tile, SHARE)] * 4
        + [None] * 4
        + [early(tile, WIDTH), None, None, by_columns, late(slot_tile, BLOCK)],
        [early(tile, WIDTH), early(tile, WIDTH + LANES), by_columns, late(slot_tile, WIDTH + LANES)],
        [
            out((BLOCK, WIDTH), jnp.float32),
            out((BLOCK, WIDTH + LANES), jnp.bfloat16),
            out((LANES, BLOCK), jnp.float32),
            out((SLOTS, WIDTH + LANES), jnp.bfloat16),
        ],
        (*attended, *w_out, x, gain, router_t, ranks, picks),
        cost(2_700_000_000, 12_000_000, 70_000),
        [pltpu.VMEM((BLOCK, WIDTH + LANES), jnp.bfloat16)],
        free=(1, 2, 3, 5, 6, 7, 10),
    )


def mix_kernel(begin_ref, ranks_ref, moe_ref, mix_ref):
    ranks = jnp.transpose(ranks_ref[...]).astype(jnp.bfloat16)
    gates = moe_ref[:, WIDTH:]
    width = 640
    for at in range(0, SLOTS, width):
        expert_at = lax.broadcasted_iota(jnp.int32, (LANES, width), 0)
        first = expert_at * QUARTER - at
        slot_at = lax.broadcasted_iota(jnp.int32, (LANES, width), 1)
        inside = jnp.logical_and(slot_at >= first, slot_at < first + QUARTER)
        spread = jnp.where(inside, 1.0, 0.0).astype(jnp.bfloat16)
        within = jnp.sum(jnp.where(inside, slot_at - first, 0), axis=0, keepdims=True) + begin_ref[0]
        hit = mm(ranks, spread) == within.astype(jnp.float32)
        mix_ref[:, at : at + width] = jnp.where(hit, mm(gates, spread), 0.0).astype(jnp.bfloat16)


def mix_weights(begin, ranks, moe_cat):
    return run(
        mix_kernel,
        "mix_weights",
        1,
        [smem(), None, None],
        [None],
        [out((BLOCK, SLOTS), jnp.bfloat16)],
        (begin, ranks, moe_cat),
        cost(350_000_000, 3_000_000),
    )[0]


def expert_kernel(
    lane_ref, x_ref, grad_ref, p0, p1, p2, p3,
    out_ref, row_ref, hidden_ref, units_ref,
):
    packed = (p0, p1, p2, p3)
    rows = out_ref.shape[0]
    here = pl.ds(pl.program_id(0) * rows, rows)
    lane = lax.broadcasted_iota(jnp.int32, (rows, LANES), 1) == lane_ref[0]
    gate = jnp.sum(
        jnp.where(lane, x_ref[here, WIDTH:].astype(jnp.float32), 0.0), axis=1, keepdims=True
    )
    x = x_ref[here, :WIDTH]
    grad = grad_ref[...]
    gates, ups, sigmoids, hidden = [], [], [], []
    for p in packed:
        pre = None
        for k in range(4):
            columns = slice(k * SHARE, (k + 1) * SHARE)
            term = mm(x[:, columns], p[LANES:, columns])
            pre = term if pre is None else pre + term
        gate_pre, up_pre = pre[:, :LANES], pre[:, LANES:]
        sigmoid = 1.0 / (1.0 + jnp.exp(-gate_pre))
        gates.append(gate_pre)
        ups.append(up_pre)
        sigmoids.append(sigmoid)
        hidden.append(gate_pre * sigmoid * up_pre)
    hidden_low = jnp.concatenate([h.astype(jnp.bfloat16) for h in hidden], axis=1)
    down = jnp.concatenate([p[:LANES, :] for p in packed], axis=0)
    made = mm(hidden_low, down).astype(jnp.bfloat16)
    out_ref[...] = made
    gate_grad = jnp.sum(grad.astype(jnp.float32) * made.astype(jnp.float32), axis=1, keepdims=True)
    row_ref[:, WIDTH:] = jnp.where(lane, gate_grad, 0.0).astype(jnp.bfloat16)
    hidden_grad = mm(grad, down, NT)
    row = None
    for j, p in enumerate(packed):
        part = hidden_grad[:, j * LANES : (j + 1) * LANES]
        silu = gates[j] * sigmoids[j]
        gate_pre_grad = part * ups[j] * sigmoids[j] * (1.0 + gates[j] * (1.0 - sigmoids[j]))
        up_pre_grad = part * silu
        hidden_ref[:, j * LANES : (j + 1) * LANES] = (hidden[j] * gate).astype(jnp.bfloat16)
        units_ref[:, j * SHARE : j * SHARE + LANES] = (gate_pre_grad * gate).astype(jnp.bfloat16)
        units_ref[:, j * SHARE + LANES : (j + 1) * SHARE] = (up_pre_grad * gate).astype(jnp.bfloat16)
        both = jnp.concatenate([gate_pre_grad, up_pre_grad], axis=1).astype(jnp.bfloat16)
        terms = [
            mm(both, p[LANES:, k * SHARE : (k + 1) * SHARE], NT) for k in range(4)
        ]
        row = terms if row is None else [a + b for a, b in zip(row, terms)]
    for k in range(4):
        row_ref[:, k * SHARE : (k + 1) * SHARE] = row[k].astype(jnp.bfloat16)


def expert_step(lane, x, grad, packed):
    tile = 320
    return run(
        expert_kernel,
        "expert_step",
        SLOTS // tile,
        [smem(), vmem(), tiles(tile, WIDTH)] + [None] * 4,
        [tiles(tile, WIDTH), tiles(tile, WIDTH + LANES), tiles(tile, 512), tiles(tile, WIDTH)],
        [
            out((SLOTS, WIDTH), jnp.bfloat16),
            out((SLOTS, WIDTH + LANES), jnp.bfloat16),
            out((SLOTS, 512), jnp.bfloat16),
            out((SLOTS, WIDTH), jnp.bfloat16),
        ],
        (lane, x, grad, *packed),
        cost(8_000_000_000, 18_000_000, 700_000),
        limit=40,
    )


def unit_grads_kernel(x_ref, grad_ref, hidden_ref, units_ref, keep_ref, send_ref, turned_ref):
    step = pl.program_id(0)

    @pl.when(step == 0)
    def _():
        for k in range(4):
            columns = slice(k * SHARE, (k + 1) * SHARE)
            turned_ref[columns, :] = jnp.transpose(x_ref[:, columns])

    def write(to_ref):
        to_ref[0, :LANES, :] = mm(hidden_ref[...], grad_ref[...], TN).astype(jnp.bfloat16)
        for k in range(4):
            columns = slice(k * SHARE, (k + 1) * SHARE)
            to_ref[0, LANES:, columns] = mm(turned_ref[columns, :], units_ref[...]).astype(jnp.bfloat16)

    @pl.when(step < 2)
    def _():
        write(keep_ref)

    @pl.when(step >= 2)
    def _():
        write(send_ref)


def unit_grads(x, grad, hidden, units):
    rows = SHARE + LANES

    def share_of(i):
        return jnp.where(i < 2, 2 * i, 2 * i - 3)

    return run(
        unit_grads_kernel,
        "unit_grads",
        4,
        [
            vmem(),
            None,
            pl.BlockSpec((SLOTS, LANES), lambda i: (0, share_of(i))),
            pl.BlockSpec((SLOTS, SHARE), lambda i: (0, share_of(i))),
        ],
        [
            pl.BlockSpec((1, rows, WIDTH), lambda i: (jnp.minimum(i, 1), 0, 0)),
            pl.BlockSpec((1, rows, WIDTH), lambda i: (jnp.maximum(i - 2, 0), 0, 0)),
        ],
        [out((2, rows, WIDTH), jnp.bfloat16), out((2, rows, WIDTH), jnp.bfloat16)],
        (x, grad, hidden, units),
        cost(4_000_000_000, 12_000_000),
        [pltpu.VMEM((WIDTH, SLOTS), jnp.bfloat16)],
        limit=36,
    )


def unit_finish_kernel(mine_ref, got_ref, gate_ref, up_ref, down_ref):
    total = mine_ref[...].astype(jnp.float32) + got_ref[...].astype(jnp.float32)
    down_ref[0] = total[:LANES, :]
    for k in range(4):
        rows = slice(k * SHARE, (k + 1) * SHARE)
        gate_ref[0, rows, :] = total[LANES:, k * SHARE : k * SHARE + LANES]
        up_ref[0, rows, :] = total[LANES:, k * SHARE + LANES : (k + 1) * SHARE]


def unit_finish(mine, got):
    return run(
        unit_finish_kernel,
        "unit_finish",
        1,
        [None] * 2,
        [None] * 3,
        [
            out((1, WIDTH, LANES), jnp.float32),
            out((1, WIDTH, LANES), jnp.float32),
            out((1, LANES, WIDTH), jnp.float32),
        ],
        (mine, got),
        cost(1_000_000, 3_000_000),
        free=(0, 1),
    )


def home_kernel(rank_ref, mix_ref, rows_ref, keep_ref, send_ref):
    rank = rank_ref[0]
    extra = rows_ref.shape[1] > WIDTH
    for j in range(4):
        at = pl.multiple_of(jnp.bitwise_xor(rank, j) * SHARE, SHARE)
        total = mm(mix_ref[...], rows_ref[:, pl.ds(at, SHARE)])
        to_ref = send_ref if j % 2 else keep_ref
        to_ref[(j // 2) * BLOCK : (j // 2 + 1) * BLOCK, :] = total.astype(to_ref.dtype)
    if extra:
        gate_grads = jnp.transpose(mm(mix_ref[...], rows_ref[:, WIDTH:]))[:EXPERTS]
        for to_ref in (keep_ref, send_ref):
            for i in range(2):
                at = 2 * BLOCK + i * EXPERTS
                to_ref[at : at + EXPERTS, :] = gate_grads[:, i * SHARE : (i + 1) * SHARE].astype(
                    to_ref.dtype
                )


def sum_home(rank, mix, rows):
    height = 2 * BLOCK + (2 * EXPERTS if rows.shape[1] > WIDTH else 0)
    return run(
        home_kernel,
        "sum_home",
        1,
        [smem(), None, vmem()],
        [None] * 2,
        [out((height, SHARE), jnp.float32), out((height, SHARE), jnp.bfloat16)],
        (rank, mix, rows),
        cost(1_500_000_000, 6_000_000),
        limit=36,
    )


def swap_kernel(mine_ref, got_ref, total_ref):
    mine, got = mine_ref, got_ref
    half = BLOCK
    total_ref[:half] = (mine[:half] + got[half : 2 * half].astype(jnp.float32)).astype(total_ref.dtype)
    total_ref[half : 2 * half] = (
        mine[half : 2 * half] + got[:half].astype(jnp.float32)
    ).astype(total_ref.dtype)
    total_ref[2 * half :] = (mine[2 * half :] + got[2 * half :].astype(jnp.float32)).astype(
        total_ref.dtype
    )


def swap_sum(mine, got):
    return run(
        swap_kernel,
        "swap_sum",
        1,
        [None] * 2,
        [None],
        [out(mine.shape, jnp.bfloat16)],
        (mine, got),
        cost(1_000_000, 2_500_000),
        free=(0, 1),
    )[0]


def norm_back_kernel(
    rank_ref, g0, g2, g1, g3, z_ref, gates_ref, residual_ref, gain_ref, router_ref, grad_ref, w_ref,
    low_ref, logit_ref, own_ref, att_ref, att_t_ref, gain_grad_ref, u_ref,
):
    rank = rank_ref[0]
    for flip, part in enumerate((g0, g1, g2, g3)):
        at = pl.multiple_of(jnp.bitwise_xor(rank, flip) * SHARE, SHARE)
        u_ref[:, pl.ds(at, SHARE)] = part[...].astype(jnp.float32)
    weighted_grads = z_ref[...].astype(jnp.float32)
    gates = gates_ref[:EXPERTS, :]
    inner = jnp.sum(weighted_grads, axis=0, keepdims=True)
    logit_grad = (weighted_grads - gates * inner).astype(jnp.bfloat16)
    logit_ref[...] = logit_grad
    u = u_ref[...] + mm(logit_grad, router_ref[:EXPERTS, :], TN)
    v = residual_ref[...]
    scale = lax.rsqrt(jnp.mean(v * v, axis=1, keepdims=True) + epsilon)
    weighted = u * gain_ref[...]
    mean = jnp.mean(weighted * v, axis=1, keepdims=True)
    total = grad_ref[...].astype(jnp.float32) + scale * weighted - v * (scale * scale * scale * mean)

    @pl.when(pl.program_id(0) == 0)
    def _():
        gain_grad_ref[...] = jnp.zeros_like(gain_grad_ref)

    gain_grad_ref[0:1, :] += jnp.sum(u * v * scale, axis=0, keepdims=True)
    low = (residual_mult * total).astype(jnp.bfloat16)
    low_ref[...] = low
    u_ref[...] = total
    own_ref[...] = u_ref[:, pl.ds(pl.multiple_of(rank * SHARE, SHARE), SHARE)]
    att_ref[...] = mm(low, w_ref[...], NT).astype(jnp.bfloat16)
    att_t_ref[...] = mm(w_ref[...], low, NT).astype(jnp.bfloat16)


def norm_back_step(rank, mine, theirs, gates, residual, gain, router_t, out_grad, w_out):
    tile = 256
    by_columns = pl.BlockSpec((EXPERTS, tile), lambda i: (0, i))
    return run(
        norm_back_kernel,
        "norm_back_step",
        BLOCK // tile,
        [smem()]
        + [tiles(tile, SHARE), tiles(tile, SHARE, BLOCK // tile)] * 2
        + [
            tiles(EXPERTS, SHARE, 2 * BLOCK // EXPERTS),
            pl.BlockSpec((LANES, tile), lambda i: (0, i)),
            tiles(tile, WIDTH),
            None,
            None,
            tiles(tile, WIDTH),
            None,
        ],
        [
            tiles(tile, WIDTH),
            by_columns,
            tiles(tile, SHARE),
            tiles(tile, SHARE),
            pl.BlockSpec((SHARE, tile), lambda i: (0, i)),
            fixed(8, WIDTH),
        ],
        [
            out((BLOCK, WIDTH), jnp.bfloat16),
            out((EXPERTS, BLOCK), jnp.bfloat16),
            out((BLOCK, SHARE), jnp.float32),
            out((BLOCK, SHARE), jnp.bfloat16),
            out((SHARE, BLOCK), jnp.bfloat16),
            out((8, WIDTH), jnp.float32),
        ],
        (rank, mine, mine, theirs, theirs, mine, gates, residual, gain, router_t, out_grad, w_out),
        cost(700_000_000, 9_000_000, 512),
        [pltpu.VMEM((tile, WIDTH), jnp.float32)],
        free=(3, 4, 9),
    )


def dense_grads_kernel(low_ref, attended_ref, normed_ref, qgrad_ref, logit_ref, moe_ref, gain_ref, made_ref):
    made_ref[:, :SHARE] = mm(low_ref[...], attended_ref[...], TN).astype(jnp.bfloat16)
    made_ref[:, SHARE : 2 * SHARE] = mm(normed_ref[...], qgrad_ref[...], TN).astype(jnp.bfloat16)
    router = mm(logit_ref[...], moe_ref[:, :WIDTH])
    stacked = jnp.concatenate(
        [router, gain_ref[...], jnp.zeros((LANES - EXPERTS - 8, WIDTH), jnp.float32)], axis=0
    )
    made_ref[:, 2 * SHARE :] = jnp.transpose(stacked).astype(jnp.bfloat16)


def dense_grads(low, attended, normed, qgrad, logit, moe_cat, gain_grad):
    return run(
        dense_grads_kernel,
        "dense_grads",
        1,
        [None] * 7,
        [None],
        [out((WIDTH, 2 * SHARE + LANES), jnp.bfloat16)],
        (low, attended, normed, qgrad, logit, moe_cat, gain_grad),
        cost(600_000_000, 6_000_000),
    )[0]


def last_grads_kernel(
    rank_ref, own_ref, home_ref, qgrad_ref, normed_ref, x_ref, wq_ref, wk_ref, wv_ref, cos_ref, sin_ref, made_ref,
    gain_ref, all_ref, keep_ref, send_ref, inner_ref, part_ref,
):
    rank = rank_ref[0]
    kv = own_ref[...] + home_ref[...].astype(jnp.float32)
    key_grad = turned(kv[:, :LANES], cos_ref[...], sin_ref[...], back=True).astype(jnp.bfloat16)
    value_grad = kv[:, LANES:].astype(jnp.bfloat16)
    both = jnp.concatenate([key_grad, value_grad], axis=1)
    all_ref[:, : 2 * SHARE] = made_ref[:, : 2 * SHARE]
    all_ref[:, 2 * SHARE : 3 * SHARE] = mm(normed_ref[...], both, TN).astype(jnp.bfloat16)
    gain = jnp.zeros((1, WIDTH), jnp.float32)
    tile = 128
    for i in range(0, BLOCK, tile):
        rows = slice(i, i + tile)
        part = mm(qgrad_ref[rows, :], wq_ref[...], NT)
        part = part + mm(key_grad[rows], wk_ref[...], NT) + mm(value_grad[rows], wv_ref[...], NT)
        x = x_ref[rows, :].astype(jnp.float32)
        scale = lax.rsqrt(jnp.mean(x * x, axis=1, keepdims=True) + epsilon)
        along = part * x
        gain = gain + jnp.sum(along * scale, axis=0, keepdims=True)
        inner = jnp.sum(along * gain_ref[...], axis=1, keepdims=True)
        inner_ref[:, rows] = jnp.transpose(jnp.broadcast_to(inner, (tile, LANES)))[:8]
        part_ref[rows, :] = part
    for j in range(4):
        at = pl.multiple_of(jnp.bitwise_xor(rank, j) * SHARE, SHARE)
        to_ref = send_ref if j % 2 else keep_ref
        to_ref[(j // 2) * BLOCK : (j // 2 + 1) * BLOCK, :] = part_ref[:, pl.ds(at, SHARE)].astype(to_ref.dtype)
    lane = lax.broadcasted_iota(jnp.int32, (WIDTH, LANES), 1)
    column = jnp.transpose(jnp.broadcast_to(gain, (LANES, WIDTH)))
    rest = jnp.where(lane == EXPERTS + 8, column, made_ref[:, 2 * SHARE :].astype(jnp.float32))
    all_ref[:, 3 * SHARE :] = rest.astype(jnp.bfloat16)


def last_grads(rank, own, home, qgrad, normed, x, w_query, w_key, w_value, cosine, sine, made, gain):
    return run(
        last_grads_kernel,
        "last_grads",
        1,
        [smem()] + [None] * 12,
        [None] * 4,
        [
            out((WIDTH, 3 * SHARE + LANES), jnp.bfloat16),
            out((2 * BLOCK, SHARE), jnp.float32),
            out((2 * BLOCK, SHARE), jnp.bfloat16),
            out((8, BLOCK), jnp.float32),
        ],
        (rank, own, home, qgrad, normed, x, w_query, w_key, w_value, cosine, sine, made, gain),
        cost(1_000_000_000, 8_000_000, 512),
        [pltpu.VMEM((BLOCK, WIDTH), jnp.float32)],
        free=(2,),
    )


def per_device(
    hidden_in,
    lengths,
    block_order,
    routes,
    norm_gain_attn,
    w_query,
    w_key,
    w_value,
    w_out,
    norm_gain_moe,
    w_router,
    w_gate,
    w_up,
    w_down,
    out_grad,
):
    dp_count = block_order.shape[0]
    mp_rank = lax.axis_index("mp").astype(jnp.int32)
    column_start = mp_rank * SHARE
    piece = BLOCK // dp_count
    steps = MAXLEN // BLOCK - 1
    rank = mp_rank.reshape(1)
    lane = lax.axis_index("dp").astype(jnp.int32).reshape(1)
    begin = rank * QUARTER
    gain_attn = norm_gain_attn[None, :]
    gain_moe = norm_gain_moe[None, :]
    router_t = jnp.pad(w_router.T, ((0, LANES - EXPERTS), (0, 0)))

    normed, queries, key_value, cosine, sine, reach, wanted, later, live = project(
        lengths, block_order, lane, hidden_in, gain_attn, w_query, w_key, w_value
    )
    pieces = to_all(key_value.reshape(dp_count, piece, SHARE))
    picks, ranks = route(begin, after(routes.T, key_value))
    far_out = peer(after(w_out, key_value), 2)
    begun = attend_own(queries, after(key_value, picks))
    picked = pick_pieces(wanted, after(pieces, far_out))
    earlier = to_all(picked.reshape(dp_count, steps * piece, SHARE))
    earlier = earlier.reshape(dp_count, steps, piece, SHARE)

    outs = [w_out, peer(after(w_out, picked), 1), far_out, peer(far_out, 1)]

    grad_rows = jnp.dot(picks, after(out_grad, picked), preferred_element_type=jnp.bfloat16)
    grad_arrived = to_all(after(grad_rows, earlier, begun[1]).reshape(EXPERTS, QUARTER, WIDTH))
    attended, attended_t, lse = attend(reach, begun, earlier)
    far = peer(attended, 2)
    residual, moe_cat, gates, moe_rows = residual_step(
        [attended, peer(attended, 1), far, peer(far, 1)],
        outs,
        hidden_in,
        gain_moe,
        router_t,
        ranks,
        picks,
    )
    own_pack = pack_weights(after(w_down[0], attended), w_gate[0], w_up[0])
    far_pack = peer(after(own_pack, far), 2)
    packed = [own_pack, peer(own_pack, 1), far_pack, peer(far_pack, 1)]

    grouped = to_all(after(moe_rows, far_pack).reshape(EXPERTS, QUARTER, -1)).reshape(SLOTS, -1)
    mix = mix_weights(begin, ranks, moe_cat)
    grouped_grad = grad_arrived.reshape(SLOTS, WIDTH)
    rows_out, row_grad, hidden_units, unit_grad = expert_step(lane, grouped, grouped_grad, packed)
    row_home = to_all(row_grad.reshape(dp_count, QUARTER, -1)).reshape(SLOTS, -1)
    unit_keep, unit_send = unit_grads(grouped, grouped_grad, hidden_units, unit_grad)
    unit_near = unit_keep.astype(jnp.float32) + peer(unit_send, 1).astype(jnp.float32)
    unit_low = unit_near[1].astype(jnp.bfloat16)
    cut = PACKED // 2
    unit_far_a = peer(unit_low[:cut], 2)
    keep, send = sum_home(rank, after(mix, unit_far_a), row_home)
    near = keep + peer(send, 1).astype(jnp.float32)
    mine = swap_sum(near, peer(near.astype(jnp.bfloat16), 2))
    theirs = peer(mine, 1)
    rows_home = to_all(after(rows_out, theirs).reshape(dp_count, QUARTER, -1)).reshape(SLOTS, -1)
    branch_grad, logit_grad, residual_grad, attended_grad, attended_grad_t, moe_gain = norm_back_step(
        rank, mine, theirs, gates, residual, gain_moe, router_t, out_grad, w_out
    )

    query_pre_grad, own_grads, later_grads = attend_back(
        reach,
        queries,
        begun[0],
        key_value,
        earlier,
        attended_grad,
        attended_grad_t,
        attended_t,
        lse,
        cosine,
        sine,
    )
    unit_far_b = peer(after(unit_low[cut:], later_grads), 2)
    later_pieces = to_all(after(later_grads, rows_home).reshape(dp_count, steps * piece, SHARE))
    summed = sum_pieces(
        later, live, after(later_pieces, unit_far_b).reshape(dp_count * steps, piece, SHARE), dp_count
    )
    kv_home = to_all(summed).reshape(BLOCK, SHARE)
    made = dense_grads(
        branch_grad, attended, normed, query_pre_grad, logit_grad, moe_cat, moe_gain
    )

    every, keep, send, inner = last_grads(
        rank,
        own_grads,
        kv_home,
        query_pre_grad,
        normed,
        hidden_in,
        w_query,
        w_key,
        w_value,
        cosine,
        sine,
        made,
        gain_attn,
    )
    near_norm = keep + peer(send, 1).astype(jnp.float32)
    far_norm = peer(near_norm[BLOCK:].astype(jnp.bfloat16), 2)
    inner = inner[0] + peer(inner[0], 1) + peer(inner[0], 2) + peer(inner[0], 3)
    arrived = to_all(every.reshape(dp_count, WIDTH // dp_count, -1))

    keep, send = sum_home(rank, mix, after(rows_home, every))
    near_mix = keep + peer(send, 1).astype(jnp.float32)
    far_mix = peer(near_mix[BLOCK:].astype(jnp.bfloat16), 2)
    unit_far = jnp.concatenate([unit_far_a, unit_far_b], axis=0)
    grad_w_gate, grad_w_up, grad_w_down = unit_finish(unit_near[0], unit_far)

    dense = jnp.sum(arrived.astype(jnp.float32), axis=0)
    normed_grad = near_norm[:BLOCK] + after(far_norm, dense).astype(jnp.float32)
    x = hidden_in.astype(jnp.float32)
    scale = lax.rsqrt(jnp.mean(x * x, axis=-1, keepdims=True) + epsilon)
    x_cols = lax.dynamic_slice_in_dim(x, column_start, SHARE, 1)
    weighted = normed_grad * lax.dynamic_slice_in_dim(gain_attn, column_start, SHARE, 1)
    inner = inner[:, None] / WIDTH
    grad_hidden = residual_grad + scale * weighted - x_cols * (scale * scale * scale * inner)
    mixture = near_mix[:BLOCK] + far_mix.astype(jnp.float32)
    residual_cols = lax.dynamic_slice_in_dim(residual, column_start, SHARE, 1)
    out_hidden = (residual_cols + mixture).astype(jnp.bfloat16)

    at = 3 * SHARE
    attn_gain = dense[:, at + EXPERTS + 8]
    attn_gain = attn_gain + peer(attn_gain, 1) + peer(attn_gain, 2) + peer(attn_gain, 3)
    return (
        out_hidden,
        grad_hidden,
        dense[:, SHARE : 2 * SHARE],
        dense[:, 2 * SHARE : 2 * SHARE + LANES],
        dense[:, 2 * SHARE + LANES : at],
        dense[:, :SHARE].T,
        attn_gain,
        dense[:, at + EXPERTS],
        dense[:, at : at + EXPERTS],
        grad_w_gate,
        grad_w_up,
        grad_w_down,
    )


def solution(mesh):
    in_specs = (
        P("dp", None),
        P(),
        P(),
        P("dp", None),
        P(),
        P(None, "mp"),
        P(None, "mp"),
        P(None, "mp"),
        P("mp", None),
        P(),
        P(),
        P("dp", None, "mp"),
        P("dp", None, "mp"),
        P("dp", "mp", None),
        P("dp", None),
    )
    out_specs = (
        P("dp", "mp"),
        P("dp", "mp"),
        P("dp", "mp"),
        P("dp", "mp"),
        P("dp", "mp"),
        P("mp", "dp"),
        P("dp"),
        P("dp"),
        P("dp", None),
        P("dp", None, "mp"),
        P("dp", None, "mp"),
        P("dp", "mp", None),
    )
    return jax.shard_map(
        per_device, mesh=mesh, in_specs=in_specs, out_specs=out_specs, check_vma=False
    )
```

```python
import jax
import jax.numpy as jnp
import numpy as np
from jax import lax
from jax.experimental import pallas as pl
from jax.experimental.pallas import tpu as pltpu
from jax.sharding import PartitionSpec as P

HEAD_DIM = 64
EXPERTS = 32
BLOCK = 512
MAXLEN = 2048
CAP = 160
WIDTH = 1024
SHARE = 256
QUARTER = 40
SLOTS = 1280
LANES = 128
PACKED = 384

epsilon = 1e-06
residual_mult = 0.22
score_mult = 0.015625
rope_base = 10000.0
masked_score = -1e30

NN = (((1,), (0,)), ((), ()))
NT = (((1,), (1,)), ((), ()))
TN = (((0,), (0,)), ((), ()))


def mm(a, b, dims=NN):
    return lax.dot_general(a, b, dims, preferred_element_type=jnp.float32)


def to_all(x):
    return lax.all_to_all(x, "dp", 0, 0, tiled=True)


def peer(x, flip):
    return lax.ppermute(x, "mp", [(i, i ^ flip) for i in range(4)])


def after(x, *others):
    return lax.optimization_barrier((x, *others))[0]


def vmem():
    return pl.BlockSpec(memory_space=pltpu.VMEM)


def smem():
    return pl.BlockSpec(memory_space=pltpu.SMEM)


def tiles(rows, width, row0=0):
    return pl.BlockSpec((rows, width), lambda i: (i + row0, 0))


def fixed(rows, width):
    return pl.BlockSpec((rows, width), lambda i: (0, 0))


def once(*shape):
    return pl.BlockSpec(shape, lambda i: (0,) * len(shape), pipeline_mode=pl.Buffered(1))


def run(kernel, name, steps, in_specs, out_specs, out_shape, args, estimate, scratch=(), free=(), limit=32):
    in_specs = [once(*a.shape) if s is None else s for s, a in zip(in_specs, args)]
    out_specs = [once(*o.shape) if s is None else s for s, o in zip(out_specs, out_shape)]
    args = [
        a
        if s.memory_space is not None or i in free
        else pltpu.with_memory_space_constraint(a, pltpu.HBM)
        for i, (s, a) in enumerate(zip(in_specs, args))
    ]
    out_shape = [
        o if s.memory_space == pltpu.SMEM else pltpu.HBM(o.shape, o.dtype)
        for s, o in zip(out_specs, out_shape)
    ]
    return pl.pallas_call(
        kernel,
        name=name,
        grid=(steps,),
        in_specs=in_specs,
        out_specs=out_specs,
        out_shape=out_shape,
        scratch_shapes=list(scratch),
        compiler_params=pltpu.CompilerParams(vmem_limit_bytes=limit << 20),
        cost_estimate=estimate,
    )(*args)


def out(shape, dtype):
    return jax.ShapeDtypeStruct(shape, dtype)


def cost(flops, moved, exps=0):
    return pl.CostEstimate(flops=flops, bytes_accessed=moved, transcendentals=exps)


def rope_constants():
    frequency = rope_base ** (-(np.arange(HEAD_DIM // 2, dtype=np.float64) * 2.0) / HEAD_DIM)
    wide = np.tile(frequency, 4)[None, :]
    made = []
    for count, apart in ((BLOCK // 16, 16), (16, 1), (8, BLOCK)):
        angles = np.arange(count, dtype=np.float64)[:, None] * apart * wide
        made += [np.cos(angles), np.sin(angles)]
    return [jnp.asarray(a.astype(np.float32)) for a in made]


def half_front(rows):
    lane = lax.broadcasted_iota(jnp.int32, (rows, LANES), 1)
    return (lane % HEAD_DIM) < HEAD_DIM // 2


def turned(chunk, cosine, signed_sine, back=False):
    partner = jnp.where(
        half_front(chunk.shape[0]), pltpu.roll(chunk, 96, 1), pltpu.roll(chunk, 32, 1)
    )
    if back:
        return chunk * cosine - partner * signed_sine
    return chunk * cosine + partner * signed_sine


def block_tables_in(lengths_ref, order_ref, rank_ref, offset_ref, inverse_ref, reach_ref, wanted_ref, later_ref, live_ref):
    count = order_ref.shape[0]
    steps = MAXLEN // BLOCK - 1

    def sequence(s, begin):
        def one(j, at):
            offset_ref[jnp.minimum(at, count - 1)] = j
            return at + 1

        return lax.fori_loop(0, lengths_ref[s], one, begin)

    lax.fori_loop(0, lengths_ref.shape[0], sequence, jnp.int32(0))

    def invert(d, carry):
        inverse_ref[order_ref[d]] = d
        return carry

    lax.fori_loop(0, count, invert, jnp.int32(0))
    reach_ref[0] = offset_ref[order_ref[rank_ref[0]]]

    def look(d, carry):
        packed = order_ref[d]
        for s in range(1, steps + 1):
            wanted_ref[d * steps + s - 1] = inverse_ref[jnp.maximum(packed - s, 0)]
            next_at = jnp.minimum(packed + s, count - 1)
            later_ref[d * steps + s - 1] = inverse_ref[next_at] * steps + s - 1
            is_live = jnp.logical_and(packed + s < count, offset_ref[next_at] >= s)
            live_ref[d * steps + s - 1] = jnp.where(is_live, 1, 0)
        return carry

    lax.fori_loop(0, count, look, jnp.int32(0))


def project_kernel(
    lengths_ref, order_ref, rank_ref, x_ref, gain_ref, wq_ref, wk_ref, wv_ref,
    cos16_ref, sin16_ref, cos1_ref, sin1_ref, cos0_ref, sin0_ref,
    normed_ref, q_ref, kv_ref, cosine_ref, sine_ref, reach_ref, wanted_ref, later_ref, live_ref,
    offset_ref, inverse_ref,
):
    @pl.when(pl.program_id(0) == 0)
    def _():
        block_tables_in(
            lengths_ref, order_ref, rank_ref, offset_ref, inverse_ref, reach_ref, wanted_ref, later_ref, live_ref
        )

    x = x_ref[...].astype(jnp.float32)
    scale = lax.rsqrt(jnp.mean(x * x, axis=1, keepdims=True) + epsilon)
    normed = (x * scale * gain_ref[...]).astype(jnp.bfloat16)
    normed_ref[...] = normed
    at = reach_ref[0]
    cos0, sin0 = cos0_ref[pl.ds(at, 1), :], sin0_ref[pl.ds(at, 1), :]
    cos16 = cos16_ref[...] * cos0 - sin16_ref[...] * sin0
    sin16 = sin16_ref[...] * cos0 + cos16_ref[...] * sin0
    cos1, sin1 = cos1_ref[...][None], sin1_ref[...][None]
    cosine = (cos16[:, None, :] * cos1 - sin16[:, None, :] * sin1).reshape(x.shape[0], LANES)
    sine = (sin16[:, None, :] * cos1 + cos16[:, None, :] * sin1).reshape(x.shape[0], LANES)
    sine = jnp.where(half_front(x.shape[0]), -sine, sine)
    cosine_ref[...] = cosine
    sine_ref[...] = sine
    kv_ref[:, :LANES] = turned(mm(normed, wk_ref[...]), cosine, sine).astype(jnp.bfloat16)
    kv_ref[:, LANES:] = mm(normed, wv_ref[...]).astype(jnp.bfloat16)
    queries = mm(normed, wq_ref[...])
    for i in range(0, SHARE, LANES):
        q_ref[:, i : i + LANES] = turned(queries[:, i : i + LANES], cosine, sine).astype(jnp.bfloat16)


def project(lengths, order, rank, x, gain, w_query, w_key, w_value):
    tile = 256
    count = order.shape[0]
    steps = MAXLEN // BLOCK - 1
    bf16, f32 = jnp.bfloat16, jnp.float32
    return run(
        project_kernel,
        "project",
        BLOCK // tile,
        [smem()] * 3
        + [tiles(tile, WIDTH), None, None, None, None]
        + [tiles(tile // 16, LANES)] * 2
        + [None] * 4,
        [tiles(tile, WIDTH), tiles(tile, SHARE), tiles(tile, SHARE)]
        + [tiles(tile, LANES)] * 2
        + [smem()] * 4,
        [out((BLOCK, WIDTH), bf16), out((BLOCK, SHARE), bf16), out((BLOCK, SHARE), bf16)]
        + [out((BLOCK, LANES), f32)] * 2
        + [out((1,), jnp.int32)]
        + [out((count * steps,), jnp.int32)] * 3,
        (lengths, order, rank, x, gain, w_query, w_key, w_value, *rope_constants()),
        cost(540_000_000, 4_000_000, 512),
        [pltpu.SMEM((count,), jnp.int32), pltpu.SMEM((count,), jnp.int32)],
    )


def pick_kernel(wanted_ref, pieces_ref, picked_ref):
    def one(i, carry):
        picked_ref[i] = pieces_ref[wanted_ref[i]]
        return carry

    lax.fori_loop(0, picked_ref.shape[0], one, jnp.int32(0), unroll=4)


def pick_pieces(wanted, pieces):
    shape = out((wanted.shape[0], *pieces.shape[1:]), pieces.dtype)
    return run(
        pick_kernel, "pick_pieces", 1, [smem(), None], [None], [shape], (wanted, pieces), cost(0, 1_100_000), free=(1,)
    )[0]


def sum_kernel(later_ref, live_ref, pieces_ref, sum_ref):
    steps = MAXLEN // BLOCK - 1

    def one(d, carry):
        total = jnp.zeros(sum_ref.shape[1:], jnp.float32)
        for s in range(steps):
            part = pieces_ref[later_ref[d * steps + s]].astype(jnp.float32)
            total = total + jnp.where(live_ref[d * steps + s] == 1, part, 0.0)
        sum_ref[d] = total.astype(sum_ref.dtype)
        return carry

    lax.fori_loop(0, sum_ref.shape[0], one, jnp.int32(0), unroll=2)


def sum_pieces(later, live, pieces, count):
    shape = out((count, *pieces.shape[1:]), pieces.dtype)
    return run(
        sum_kernel,
        "sum_pieces",
        1,
        [smem(), smem(), None],
        [None],
        [shape],
        (later, live, pieces),
        cost(0, 1_100_000),
        free=(2,),
    )[0]


def pack_kernel(down_ref, gate_ref, up_ref, packed_ref):
    packed_ref[:LANES, :] = down_ref[...]
    for k in range(4):
        rows = slice(k * SHARE, (k + 1) * SHARE)
        packed_ref[LANES:, k * SHARE : k * SHARE + LANES] = gate_ref[rows, :]
        packed_ref[LANES:, k * SHARE + LANES : (k + 1) * SHARE] = up_ref[rows, :]


def pack_weights(w_down, w_gate, w_up):
    shape = out((PACKED, WIDTH), jnp.bfloat16)
    return run(
        pack_kernel, "pack_weights", 1, [None] * 3, [None], [shape], (w_down, w_gate, w_up), cost(0, 1_600_000)
    )[0]


def route_kernel(begin_ref, routes_ref, picks_ref, ranks_ref):
    tokens = routes_ref.shape[1]
    expert_at = lax.broadcasted_iota(jnp.int32, (LANES, tokens), 0)
    hits = jnp.zeros((LANES, tokens), jnp.float32)
    for k in range(routes_ref.shape[0]):
        hits = hits + jnp.where(routes_ref[k : k + 1, :] == expert_at, 1.0, 0.0)
    row_at = lax.broadcasted_iota(jnp.int32, (tokens, tokens), 0)
    column_at = lax.broadcasted_iota(jnp.int32, (tokens, tokens), 1)
    before = jnp.where(row_at < column_at, 1.0, 0.0).astype(jnp.bfloat16)
    ranks = jnp.where(hits > 0.5, mm(hits.astype(jnp.bfloat16), before), -1.0)
    ranks_ref[...] = ranks
    slot_at = lax.broadcasted_iota(jnp.int32, (QUARTER, tokens), 0) + begin_ref[0]
    slot_at = slot_at.astype(jnp.float32)
    for e in range(EXPERTS):
        picks_ref[e * QUARTER : (e + 1) * QUARTER, :] = jnp.where(
            ranks[e : e + 1, :] == slot_at, 1.0, 0.0
        ).astype(jnp.bfloat16)


def route(begin, routes_t):
    return run(
        route_kernel,
        "route",
        1,
        [smem(), None],
        [None, None],
        [out((SLOTS, BLOCK), jnp.bfloat16), out((LANES, BLOCK), jnp.float32)],
        (begin, routes_t),
        cost(100_000_000, 1_600_000),
        free=(1,),
    )


def padded_columns(rows_t, out_ref):
    zero = jnp.zeros((HEAD_DIM, rows_t.shape[1]), out_ref.dtype)
    for h in range(4):
        mine = rows_t[h * HEAD_DIM : (h + 1) * HEAD_DIM].astype(out_ref.dtype)
        at = (h // 2) * HEAD_DIM
        out_ref[h, pl.ds(at, HEAD_DIM), :] = mine
        out_ref[h, pl.ds(HEAD_DIM - at, HEAD_DIM), :] = zero


def padded_rows(rows, out_ref):
    n = rows.shape[0]
    lane = lax.broadcasted_iota(jnp.int32, (n, 128), 1)
    for h in range(4):
        pair = rows[:, (h // 2) * 128 : (h // 2) * 128 + 128].astype(jnp.float32)
        if h % 2 != h // 2:
            pair = pltpu.roll(pair, HEAD_DIM, 1)
        own = (lane < HEAD_DIM) if h // 2 == 0 else (lane >= HEAD_DIM)
        out_ref[pl.ds(h * n, n), :] = jnp.where(own, pair, 0.0).astype(out_ref.dtype)


def attend_block(key_rows, value_rows, first, qpad_ref, max_ref, sum_ref, out_t_ref):
    half = BLOCK // 2
    for h in range(4):
        group = (h // 2) * HEAD_DIM
        for t in range(2):
            cols = slice(t * half, (t + 1) * half)
            rows = half if first and t == 0 else BLOCK
            scores = mm(key_rows[:rows], qpad_ref[h, :, cols])
            if first:
                key_at = lax.broadcasted_iota(jnp.int32, scores.shape, 0)
                query_at = lax.broadcasted_iota(jnp.int32, scores.shape, 1) + t * half
                scores = jnp.where(key_at > query_at, masked_score, scores)
            new_max = jnp.max(scores, axis=0, keepdims=True)
            if not first:
                old_max = max_ref[h : h + 1, cols]
                new_max = jnp.maximum(new_max, old_max)
                shrink = jnp.exp(old_max - new_max)
            weights = jnp.exp(scores - new_max)
            total = jnp.sum(weights, axis=0, keepdims=True)
            part = mm(value_rows[:rows], weights.astype(jnp.bfloat16), TN)[group : group + HEAD_DIM]
            mine = pl.ds(h * HEAD_DIM, HEAD_DIM)
            if not first:
                total = total + sum_ref[h : h + 1, cols] * shrink
                part = part + out_t_ref[mine, cols] * shrink
            max_ref[h : h + 1, cols] = new_max
            sum_ref[h : h + 1, cols] = total
            out_t_ref[mine, cols] = part


def attend_own_kernel(q_ref, own_ref, qpad_ref, max_ref, sum_ref, out_t_ref):
    padded_columns(jnp.transpose(q_ref[...].astype(jnp.float32) * score_mult), qpad_ref)
    max_ref[...] = jnp.zeros_like(max_ref)
    sum_ref[...] = jnp.ones_like(sum_ref)
    attend_block(own_ref[:, :LANES], own_ref[:, LANES:], True, qpad_ref, max_ref, sum_ref, out_t_ref)


def attend_own(queries, own_kv):
    return pl.pallas_call(
        attend_own_kernel,
        name="attend_own",
        in_specs=[vmem()] * 2,
        out_specs=[vmem()] * 4,
        out_shape=[
            out((4, LANES, BLOCK), jnp.bfloat16),
            out((8, BLOCK), jnp.float32),
            out((8, BLOCK), jnp.float32),
            out((SHARE, BLOCK), jnp.float32),
        ],
        compiler_params=pltpu.CompilerParams(vmem_limit_bytes=36 << 20),
        cost_estimate=cost(1_000_000_000, 2_000_000, 600_000),
    )(queries, own_kv)


def attend_kernel(
    reach_ref, qpad_ref, max0_ref, sum0_ref, out0_ref, prev_ref, att_ref, out_t_ref, lse_ref, max_ref, sum_ref
):
    max_ref[...] = max0_ref[...]
    sum_ref[...] = sum0_ref[...]
    out_t_ref[...] = out0_ref[...]

    @pl.loop(1, reach_ref[0] + 1)
    def _(step):
        rows = prev_ref[:, pl.ds(step - 1, 1)].reshape(BLOCK, SHARE)
        attend_block(rows[:, :LANES], rows[:, LANES:], False, qpad_ref, max_ref, sum_ref, out_t_ref)

    lse_ref[...] = max_ref[...] + jnp.log(sum_ref[...])
    for h in range(4):
        mine = pl.ds(h * HEAD_DIM, HEAD_DIM)
        out_t_ref[mine, :] = out_t_ref[mine, :] / sum_ref[h : h + 1, :]
    att_ref[...] = jnp.transpose(out_t_ref[...]).astype(jnp.bfloat16)


def attend(reach, begun, earlier):
    return run(
        attend_kernel,
        "attend",
        1,
        [smem()] + [vmem()] * 5,
        [None] * 3,
        [
            out((BLOCK, SHARE), jnp.bfloat16),
            out((SHARE, BLOCK), jnp.float32),
            out((8, BLOCK), jnp.float32),
        ],
        (reach, *begun, earlier),
        cost(4_000_000_000, 3_000_000, 3_000_000),
        [pltpu.VMEM((8, BLOCK), jnp.float32), pltpu.VMEM((8, BLOCK), jnp.float32)],
        limit=36,
    )


def attend_back_kernel(
    reach_ref, q_ref, qpad_ref, own_ref, prev_ref, grad_ref, grad_t_ref, out_t_ref, lse_ref, cos_ref, sin_ref,
    qgrad_ref, own_grad_ref, prev_grad_ref,
    gpad_ref, qrows_ref, grows_ref, ds_ref, p_ref, delta_ref, dq_ref,
):
    half = BLOCK // 2
    q_scaled = q_ref[...].astype(jnp.float32) * score_mult
    padded_rows(q_scaled, qrows_ref)
    padded_columns(grad_t_ref[...], gpad_ref)
    padded_rows(grad_ref[...], grows_ref)
    both = grad_t_ref[...].astype(jnp.float32) * out_t_ref[...]
    for h in range(4):
        delta_ref[h : h + 1, :] = jnp.sum(
            both[h * HEAD_DIM : (h + 1) * HEAD_DIM], axis=0, keepdims=True
        )


    def block(key_rows, value_rows, first):
        for h in range(4):
            for t in range(2):
                cols = slice(t * half, (t + 1) * half)
                wide = slice(h * BLOCK + t * half, h * BLOCK + (t + 1) * half)
                rows = half if first and t == 0 else BLOCK
                scores = mm(key_rows[:rows], qpad_ref[h, :, cols])
                weights = jnp.exp(scores - lse_ref[h : h + 1, cols])
                if first:
                    key_at = lax.broadcasted_iota(jnp.int32, scores.shape, 0)
                    query_at = lax.broadcasted_iota(jnp.int32, scores.shape, 1) + t * half
                    weights = jnp.where(key_at > query_at, 0.0, weights)
                weight_grad = mm(value_rows[:rows], gpad_ref[h, :, cols])
                score_grad = weights * (weight_grad - delta_ref[h : h + 1, cols])
                p_ref[:rows, wide] = weights.astype(jnp.bfloat16)
                ds_ref[:rows, wide] = score_grad.astype(jnp.bfloat16)
                if rows < BLOCK:
                    p_ref[rows:, wide] = jnp.zeros((BLOCK - rows, half), jnp.bfloat16)
                    ds_ref[rows:, wide] = jnp.zeros((BLOCK - rows, half), jnp.bfloat16)
        key_grad = mm(ds_ref[...], qrows_ref[...])
        value_grad = mm(p_ref[...], grows_ref[...])
        for h in range(4):
            group = (h // 2) * HEAD_DIM
            mine = pl.ds(h * HEAD_DIM, HEAD_DIM)
            part = mm(key_rows, ds_ref[:, h * BLOCK : (h + 1) * BLOCK], TN)[group : group + HEAD_DIM]
            dq_ref[mine, :] = part if first else dq_ref[mine, :] + part
        return key_grad, value_grad

    key_grad, value_grad = block(own_ref[:, :LANES], own_ref[:, LANES:], True)
    own_grad_ref[:, :LANES] = key_grad
    own_grad_ref[:, LANES:] = value_grad

    @pl.loop(1, reach_ref[0] + 1)
    def _(step):
        rows = prev_ref[:, pl.ds(step - 1, 1)].reshape(BLOCK, SHARE)
        key_grad, value_grad = block(rows[:, :LANES], rows[:, LANES:], False)
        parts = prev_grad_ref.shape[0]
        shape = (parts, 1, BLOCK // parts, LANES)
        prev_grad_ref[:, pl.ds(step - 1, 1), :, :LANES] = key_grad.astype(jnp.bfloat16).reshape(shape)
        prev_grad_ref[:, pl.ds(step - 1, 1), :, LANES:] = value_grad.astype(jnp.bfloat16).reshape(shape)

    query_grad = jnp.transpose(dq_ref[...]) * score_mult
    for i in range(0, SHARE, LANES):
        qgrad_ref[:, i : i + LANES] = turned(
            query_grad[:, i : i + LANES], cos_ref[...], sin_ref[...], back=True
        ).astype(jnp.bfloat16)


def attend_back(reach, queries, padded, own_kv, earlier, grad, grad_t, out_t, lse, cosine, signed_sine):
    return run(
        attend_back_kernel,
        "attend_back",
        1,
        [smem()] + [vmem()] * 10,
        [None] * 3,
        [
            out((BLOCK, SHARE), jnp.bfloat16),
            out((BLOCK, SHARE), jnp.float32),
            out(earlier.shape, jnp.bfloat16),
        ],
        (reach, queries, padded, own_kv, earlier, grad, grad_t, out_t, lse, cosine, signed_sine),
        cost(12_000_000_000, 5_000_000, 3_000_000),
        [
            pltpu.VMEM((4, LANES, BLOCK), jnp.bfloat16),
            pltpu.VMEM((4 * BLOCK, LANES), jnp.bfloat16),
            pltpu.VMEM((4 * BLOCK, LANES), jnp.bfloat16),
            pltpu.VMEM((BLOCK, 4 * BLOCK), jnp.bfloat16),
            pltpu.VMEM((BLOCK, 4 * BLOCK), jnp.bfloat16),
            pltpu.VMEM((8, BLOCK), jnp.float32),
            pltpu.VMEM((SHARE, BLOCK), jnp.float32),
        ],
        limit=36,
    )


def residual_kernel(
    a0, a1, a2, a3, w0, w1, w2, w3, x_ref, gain_ref, router_ref, ranks_ref, picks_ref,
    residual_ref, moe_ref, gates_ref, rows_ref, held_ref,
):
    step = pl.program_id(0)
    tile = x_ref.shape[0]

    @pl.when(step < BLOCK // tile)
    def _():
        branch = mm(a0[...], w0[...])
        for a, w in ((a1, w1), (a2, w2), (a3, w3)):
            branch = branch + mm(a[...], w[...])
        residual = x_ref[...].astype(jnp.float32) + residual_mult * branch
        residual_ref[...] = residual
        scale = lax.rsqrt(jnp.mean(residual * residual, axis=1, keepdims=True) + epsilon)
        moe_in = (residual * scale * gain_ref[...]).astype(jnp.bfloat16)
        moe_ref[:, :WIDTH] = moe_in
        logits = mm(router_ref[...], moe_in, NT)
        chosen = ranks_ref[...] >= 0.0
        kept = jnp.where(chosen, logits, masked_score)
        top = jnp.max(kept, axis=0, keepdims=True)
        raised = jnp.where(chosen, jnp.exp(kept - top), 0.0)
        gates = raised / jnp.sum(raised, axis=0, keepdims=True)
        gates_ref[...] = gates
        low = (residual_mult * jnp.transpose(gates)).astype(jnp.bfloat16)
        moe_ref[:, WIDTH:] = low
        held_ref[pl.ds(step * tile, tile), :WIDTH] = moe_in
        held_ref[pl.ds(step * tile, tile), WIDTH:] = low

    @pl.when(step >= BLOCK // tile)
    def _():
        rows_ref[...] = mm(picks_ref[...], held_ref[...]).astype(jnp.bfloat16)


def residual_step(attended, w_out, x, gain, router_t, ranks, picks):
    tile = 256
    first = BLOCK // tile
    slot_tile = SLOTS // 4

    def early(rows, width):
        return pl.BlockSpec((rows, width), lambda i: (jnp.minimum(i, first - 1), 0))

    def late(rows, width):
        return pl.BlockSpec((rows, width), lambda i: (jnp.maximum(i - first, 0), 0))

    by_columns = pl.BlockSpec((LANES, tile), lambda i: (0, jnp.minimum(i, first - 1)))
    return run(
        residual_kernel,
        "residual_step",
        first + 4,
        [early(tile, SHARE)] * 4
        + [None] * 4
        + [early(tile, WIDTH), None, None, by_columns, late(slot_tile, BLOCK)],
        [early(tile, WIDTH), early(tile, WIDTH + LANES), by_columns, late(slot_tile, WIDTH + LANES)],
        [
            out((BLOCK, WIDTH), jnp.float32),
            out((BLOCK, WIDTH + LANES), jnp.bfloat16),
            out((LANES, BLOCK), jnp.float32),
            out((SLOTS, WIDTH + LANES), jnp.bfloat16),
        ],
        (*attended, *w_out, x, gain, router_t, ranks, picks),
        cost(2_700_000_000, 12_000_000, 70_000),
        [pltpu.VMEM((BLOCK, WIDTH + LANES), jnp.bfloat16)],
        free=(1, 2, 3, 5, 6, 7, 10),
    )


def mix_kernel(begin_ref, ranks_ref, moe_ref, mix_ref):
    ranks = jnp.transpose(ranks_ref[...]).astype(jnp.bfloat16)
    gates = moe_ref[:, WIDTH:]
    width = 640
    for at in range(0, SLOTS, width):
        expert_at = lax.broadcasted_iota(jnp.int32, (LANES, width), 0)
        first = expert_at * QUARTER - at
        slot_at = lax.broadcasted_iota(jnp.int32, (LANES, width), 1)
        inside = jnp.logical_and(slot_at >= first, slot_at < first + QUARTER)
        spread = jnp.where(inside, 1.0, 0.0).astype(jnp.bfloat16)
        within = jnp.sum(jnp.where(inside, slot_at - first, 0), axis=0, keepdims=True) + begin_ref[0]
        hit = mm(ranks, spread) == within.astype(jnp.float32)
        mix_ref[:, at : at + width] = jnp.where(hit, mm(gates, spread), 0.0).astype(jnp.bfloat16)


def mix_weights(begin, ranks, moe_cat):
    return run(
        mix_kernel,
        "mix_weights",
        1,
        [smem(), None, None],
        [None],
        [out((BLOCK, SLOTS), jnp.bfloat16)],
        (begin, ranks, moe_cat),
        cost(350_000_000, 3_000_000),
    )[0]


def expert_kernel(
    lane_ref, x_ref, grad_ref, p0, p1, p2, p3,
    out_ref, row_ref, hidden_ref, units_ref,
):
    packed = (p0, p1, p2, p3)
    rows = out_ref.shape[0]
    here = pl.ds(pl.program_id(0) * rows, rows)
    lane = lax.broadcasted_iota(jnp.int32, (rows, LANES), 1) == lane_ref[0]
    gate = jnp.sum(
        jnp.where(lane, x_ref[here, WIDTH:].astype(jnp.float32), 0.0), axis=1, keepdims=True
    )
    x = x_ref[here, :WIDTH]
    grad = grad_ref[...]
    gates, ups, sigmoids, hidden = [], [], [], []
    for p in packed:
        pre = None
        for k in range(4):
            columns = slice(k * SHARE, (k + 1) * SHARE)
            term = mm(x[:, columns], p[LANES:, columns])
            pre = term if pre is None else pre + term
        gate_pre, up_pre = pre[:, :LANES], pre[:, LANES:]
        sigmoid = 1.0 / (1.0 + jnp.exp(-gate_pre))
        gates.append(gate_pre)
        ups.append(up_pre)
        sigmoids.append(sigmoid)
        hidden.append(gate_pre * sigmoid * up_pre)
    hidden_low = jnp.concatenate([h.astype(jnp.bfloat16) for h in hidden], axis=1)
    down = jnp.concatenate([p[:LANES, :] for p in packed], axis=0)
    made = mm(hidden_low, down).astype(jnp.bfloat16)
    out_ref[...] = made
    gate_grad = jnp.sum(grad.astype(jnp.float32) * made.astype(jnp.float32), axis=1, keepdims=True)
    row_ref[:, WIDTH:] = jnp.where(lane, gate_grad, 0.0).astype(jnp.bfloat16)
    hidden_grad = mm(grad, down, NT)
    row = None
    for j, p in enumerate(packed):
        part = hidden_grad[:, j * LANES : (j + 1) * LANES]
        silu = gates[j] * sigmoids[j]
        gate_pre_grad = part * ups[j] * sigmoids[j] * (1.0 + gates[j] * (1.0 - sigmoids[j]))
        up_pre_grad = part * silu
        hidden_ref[:, j * LANES : (j + 1) * LANES] = (hidden[j] * gate).astype(jnp.bfloat16)
        units_ref[:, j * SHARE : j * SHARE + LANES] = (gate_pre_grad * gate).astype(jnp.bfloat16)
        units_ref[:, j * SHARE + LANES : (j + 1) * SHARE] = (up_pre_grad * gate).astype(jnp.bfloat16)
        both = jnp.concatenate([gate_pre_grad, up_pre_grad], axis=1).astype(jnp.bfloat16)
        terms = [
            mm(both, p[LANES:, k * SHARE : (k + 1) * SHARE], NT) for k in range(4)
        ]
        row = terms if row is None else [a + b for a, b in zip(row, terms)]
    for k in range(4):
        row_ref[:, k * SHARE : (k + 1) * SHARE] = row[k].astype(jnp.bfloat16)


def expert_step(lane, x, grad, packed):
    tile = 320
    return run(
        expert_kernel,
        "expert_step",
        SLOTS // tile,
        [smem(), vmem(), tiles(tile, WIDTH)] + [None] * 4,
        [tiles(tile, WIDTH), tiles(tile, WIDTH + LANES), tiles(tile, 512), tiles(tile, WIDTH)],
        [
            out((SLOTS, WIDTH), jnp.bfloat16),
            out((SLOTS, WIDTH + LANES), jnp.bfloat16),
            out((SLOTS, 512), jnp.bfloat16),
            out((SLOTS, WIDTH), jnp.bfloat16),
        ],
        (lane, x, grad, *packed),
        cost(8_000_000_000, 18_000_000, 700_000),
        limit=40,
    )


def unit_grads_kernel(x_ref, grad_ref, hidden_ref, units_ref, keep_ref, send_ref, turned_ref):
    step = pl.program_id(0)

    @pl.when(step == 0)
    def _():
        for k in range(4):
            columns = slice(k * SHARE, (k + 1) * SHARE)
            turned_ref[columns, :] = jnp.transpose(x_ref[:, columns])

    def write(to_ref):
        to_ref[0, :LANES, :] = mm(hidden_ref[...], grad_ref[...], TN).astype(jnp.bfloat16)
        for k in range(4):
            columns = slice(k * SHARE, (k + 1) * SHARE)
            to_ref[0, LANES:, columns] = mm(turned_ref[columns, :], units_ref[...]).astype(jnp.bfloat16)

    @pl.when(step < 2)
    def _():
        write(keep_ref)

    @pl.when(step >= 2)
    def _():
        write(send_ref)


def unit_grads(x, grad, hidden, units):
    rows = SHARE + LANES

    def share_of(i):
        return jnp.where(i < 2, 2 * i, 2 * i - 3)

    return run(
        unit_grads_kernel,
        "unit_grads",
        4,
        [
            vmem(),
            None,
            pl.BlockSpec((SLOTS, LANES), lambda i: (0, share_of(i))),
            pl.BlockSpec((SLOTS, SHARE), lambda i: (0, share_of(i))),
        ],
        [
            pl.BlockSpec((1, rows, WIDTH), lambda i: (jnp.minimum(i, 1), 0, 0)),
            pl.BlockSpec((1, rows, WIDTH), lambda i: (jnp.maximum(i - 2, 0), 0, 0)),
        ],
        [out((2, rows, WIDTH), jnp.bfloat16), out((2, rows, WIDTH), jnp.bfloat16)],
        (x, grad, hidden, units),
        cost(4_000_000_000, 12_000_000),
        [pltpu.VMEM((WIDTH, SLOTS), jnp.bfloat16)],
        limit=36,
    )


def unit_finish_kernel(mine_ref, got_ref, gate_ref, up_ref, down_ref):
    total = mine_ref[...].astype(jnp.float32) + got_ref[...].astype(jnp.float32)
    down_ref[0] = total[:LANES, :]
    for k in range(4):
        rows = slice(k * SHARE, (k + 1) * SHARE)
        gate_ref[0, rows, :] = total[LANES:, k * SHARE : k * SHARE + LANES]
        up_ref[0, rows, :] = total[LANES:, k * SHARE + LANES : (k + 1) * SHARE]


def unit_finish(mine, got):
    return run(
        unit_finish_kernel,
        "unit_finish",
        1,
        [None] * 2,
        [None] * 3,
        [
            out((1, WIDTH, LANES), jnp.float32),
            out((1, WIDTH, LANES), jnp.float32),
            out((1, LANES, WIDTH), jnp.float32),
        ],
        (mine, got),
        cost(1_000_000, 3_000_000),
        free=(0, 1),
    )


def home_kernel(rank_ref, mix_ref, rows_ref, keep_ref, send_ref):
    rank = rank_ref[0]
    extra = rows_ref.shape[1] > WIDTH
    for j in range(4):
        at = pl.multiple_of(jnp.bitwise_xor(rank, j) * SHARE, SHARE)
        total = mm(mix_ref[...], rows_ref[:, pl.ds(at, SHARE)])
        to_ref = send_ref if j % 2 else keep_ref
        to_ref[(j // 2) * BLOCK : (j // 2 + 1) * BLOCK, :] = total.astype(to_ref.dtype)
    if extra:
        gate_grads = jnp.transpose(mm(mix_ref[...], rows_ref[:, WIDTH:]))[:EXPERTS]
        for to_ref in (keep_ref, send_ref):
            for i in range(2):
                at = 2 * BLOCK + i * EXPERTS
                to_ref[at : at + EXPERTS, :] = gate_grads[:, i * SHARE : (i + 1) * SHARE].astype(
                    to_ref.dtype
                )


def sum_home(rank, mix, rows):
    height = 2 * BLOCK + (2 * EXPERTS if rows.shape[1] > WIDTH else 0)
    return run(
        home_kernel,
        "sum_home",
        1,
        [smem(), None, vmem()],
        [None] * 2,
        [out((height, SHARE), jnp.float32), out((height, SHARE), jnp.bfloat16)],
        (rank, mix, rows),
        cost(1_500_000_000, 6_000_000),
        limit=36,
    )


def swap_kernel(mine_ref, got_ref, total_ref):
    mine, got = mine_ref, got_ref
    half = BLOCK
    total_ref[:half] = (mine[:half] + got[half : 2 * half].astype(jnp.float32)).astype(total_ref.dtype)
    total_ref[half : 2 * half] = (
        mine[half : 2 * half] + got[:half].astype(jnp.float32)
    ).astype(total_ref.dtype)
    total_ref[2 * half :] = (mine[2 * half :] + got[2 * half :].astype(jnp.float32)).astype(
        total_ref.dtype
    )


def swap_sum(mine, got):
    return run(
        swap_kernel,
        "swap_sum",
        1,
        [None] * 2,
        [None],
        [out(mine.shape, jnp.bfloat16)],
        (mine, got),
        cost(1_000_000, 2_500_000),
        free=(0, 1),
    )[0]


def norm_back_kernel(
    rank_ref, g0, g2, g1, g3, z_ref, gates_ref, residual_ref, gain_ref, router_ref, grad_ref, w_ref,
    low_ref, logit_ref, own_ref, att_ref, att_t_ref, gain_grad_ref, u_ref,
):
    rank = rank_ref[0]
    for flip, part in enumerate((g0, g1, g2, g3)):
        at = pl.multiple_of(jnp.bitwise_xor(rank, flip) * SHARE, SHARE)
        u_ref[:, pl.ds(at, SHARE)] = part[...].astype(jnp.float32)
    weighted_grads = z_ref[...].astype(jnp.float32)
    gates = gates_ref[:EXPERTS, :]
    inner = jnp.sum(weighted_grads, axis=0, keepdims=True)
    logit_grad = (weighted_grads - gates * inner).astype(jnp.bfloat16)
    logit_ref[...] = logit_grad
    u = u_ref[...] + mm(logit_grad, router_ref[:EXPERTS, :], TN)
    v = residual_ref[...]
    scale = lax.rsqrt(jnp.mean(v * v, axis=1, keepdims=True) + epsilon)
    weighted = u * gain_ref[...]
    mean = jnp.mean(weighted * v, axis=1, keepdims=True)
    total = grad_ref[...].astype(jnp.float32) + scale * weighted - v * (scale * scale * scale * mean)

    @pl.when(pl.program_id(0) == 0)
    def _():
        gain_grad_ref[...] = jnp.zeros_like(gain_grad_ref)

    gain_grad_ref[0:1, :] += jnp.sum(u * v * scale, axis=0, keepdims=True)
    low = (residual_mult * total).astype(jnp.bfloat16)
    low_ref[...] = low
    u_ref[...] = total
    own_ref[...] = u_ref[:, pl.ds(pl.multiple_of(rank * SHARE, SHARE), SHARE)]
    att_ref[...] = mm(low, w_ref[...], NT).astype(jnp.bfloat16)
    att_t_ref[...] = mm(w_ref[...], low, NT).astype(jnp.bfloat16)


def norm_back_step(rank, mine, theirs, gates, residual, gain, router_t, out_grad, w_out):
    tile = 256
    by_columns = pl.BlockSpec((EXPERTS, tile), lambda i: (0, i))
    return run(
        norm_back_kernel,
        "norm_back_step",
        BLOCK // tile,
        [smem()]
        + [tiles(tile, SHARE), tiles(tile, SHARE, BLOCK // tile)] * 2
        + [
            tiles(EXPERTS, SHARE, 2 * BLOCK // EXPERTS),
            pl.BlockSpec((LANES, tile), lambda i: (0, i)),
            tiles(tile, WIDTH),
            None,
            None,
            tiles(tile, WIDTH),
            None,
        ],
        [
            tiles(tile, WIDTH),
            by_columns,
            tiles(tile, SHARE),
            tiles(tile, SHARE),
            pl.BlockSpec((SHARE, tile), lambda i: (0, i)),
            fixed(8, WIDTH),
        ],
        [
            out((BLOCK, WIDTH), jnp.bfloat16),
            out((EXPERTS, BLOCK), jnp.bfloat16),
            out((BLOCK, SHARE), jnp.float32),
            out((BLOCK, SHARE), jnp.bfloat16),
            out((SHARE, BLOCK), jnp.bfloat16),
            out((8, WIDTH), jnp.float32),
        ],
        (rank, mine, mine, theirs, theirs, mine, gates, residual, gain, router_t, out_grad, w_out),
        cost(700_000_000, 9_000_000, 512),
        [pltpu.VMEM((tile, WIDTH), jnp.float32)],
        free=(3, 4, 9),
    )


def dense_grads_kernel(low_ref, attended_ref, normed_ref, qgrad_ref, logit_ref, moe_ref, gain_ref, made_ref):
    made_ref[:, :SHARE] = mm(low_ref[...], attended_ref[...], TN).astype(jnp.bfloat16)
    made_ref[:, SHARE : 2 * SHARE] = mm(normed_ref[...], qgrad_ref[...], TN).astype(jnp.bfloat16)
    router = mm(logit_ref[...], moe_ref[:, :WIDTH])
    stacked = jnp.concatenate(
        [router, gain_ref[...], jnp.zeros((LANES - EXPERTS - 8, WIDTH), jnp.float32)], axis=0
    )
    made_ref[:, 2 * SHARE :] = jnp.transpose(stacked).astype(jnp.bfloat16)


def dense_grads(low, attended, normed, qgrad, logit, moe_cat, gain_grad):
    return run(
        dense_grads_kernel,
        "dense_grads",
        1,
        [None] * 7,
        [None],
        [out((WIDTH, 2 * SHARE + LANES), jnp.bfloat16)],
        (low, attended, normed, qgrad, logit, moe_cat, gain_grad),
        cost(600_000_000, 6_000_000),
    )[0]


def last_grads_kernel(
    rank_ref, own_ref, home_ref, qgrad_ref, normed_ref, x_ref, wq_ref, wk_ref, wv_ref, cos_ref, sin_ref, made_ref,
    gain_ref, all_ref, keep_ref, send_ref, inner_ref, part_ref,
):
    rank = rank_ref[0]
    kv = own_ref[...] + home_ref[...].astype(jnp.float32)
    key_grad = turned(kv[:, :LANES], cos_ref[...], sin_ref[...], back=True).astype(jnp.bfloat16)
    value_grad = kv[:, LANES:].astype(jnp.bfloat16)
    both = jnp.concatenate([key_grad, value_grad], axis=1)
    all_ref[:, : 2 * SHARE] = made_ref[:, : 2 * SHARE]
    all_ref[:, 2 * SHARE : 3 * SHARE] = mm(normed_ref[...], both, TN).astype(jnp.bfloat16)
    gain = jnp.zeros((1, WIDTH), jnp.float32)
    tile = 128
    for i in range(0, BLOCK, tile):
        rows = slice(i, i + tile)
        part = mm(qgrad_ref[rows, :], wq_ref[...], NT)
        part = part + mm(key_grad[rows], wk_ref[...], NT) + mm(value_grad[rows], wv_ref[...], NT)
        x = x_ref[rows, :].astype(jnp.float32)
        scale = lax.rsqrt(jnp.mean(x * x, axis=1, keepdims=True) + epsilon)
        along = part * x
        gain = gain + jnp.sum(along * scale, axis=0, keepdims=True)
        inner = jnp.sum(along * gain_ref[...], axis=1, keepdims=True)
        inner_ref[:, rows] = jnp.transpose(jnp.broadcast_to(inner, (tile, LANES)))[:8]
        part_ref[rows, :] = part
    for j in range(4):
        at = pl.multiple_of(jnp.bitwise_xor(rank, j) * SHARE, SHARE)
        to_ref = send_ref if j % 2 else keep_ref
        to_ref[(j // 2) * BLOCK : (j // 2 + 1) * BLOCK, :] = part_ref[:, pl.ds(at, SHARE)].astype(to_ref.dtype)
    lane = lax.broadcasted_iota(jnp.int32, (WIDTH, LANES), 1)
    column = jnp.transpose(jnp.broadcast_to(gain, (LANES, WIDTH)))
    rest = jnp.where(lane == EXPERTS + 8, column, made_ref[:, 2 * SHARE :].astype(jnp.float32))
    all_ref[:, 3 * SHARE :] = rest.astype(jnp.bfloat16)


def last_grads(rank, own, home, qgrad, normed, x, w_query, w_key, w_value, cosine, sine, made, gain):
    return run(
        last_grads_kernel,
        "last_grads",
        1,
        [smem()] + [None] * 12,
        [None] * 4,
        [
            out((WIDTH, 3 * SHARE + LANES), jnp.bfloat16),
            out((2 * BLOCK, SHARE), jnp.float32),
            out((2 * BLOCK, SHARE), jnp.bfloat16),
            out((8, BLOCK), jnp.float32),
        ],
        (rank, own, home, qgrad, normed, x, w_query, w_key, w_value, cosine, sine, made, gain),
        cost(1_000_000_000, 8_000_000, 512),
        [pltpu.VMEM((BLOCK, WIDTH), jnp.float32)],
        free=(2,),
    )


def per_device(
    hidden_in,
    lengths,
    block_order,
    routes,
    norm_gain_attn,
    w_query,
    w_key,
    w_value,
    w_out,
    norm_gain_moe,
    w_router,
    w_gate,
    w_up,
    w_down,
    out_grad,
):
    dp_count = block_order.shape[0]
    mp_rank = lax.axis_index("mp").astype(jnp.int32)
    column_start = mp_rank * SHARE
    piece = BLOCK // dp_count
    steps = MAXLEN // BLOCK - 1
    rank = mp_rank.reshape(1)
    lane = lax.axis_index("dp").astype(jnp.int32).reshape(1)
    begin = rank * QUARTER
    gain_attn = norm_gain_attn[None, :]
    gain_moe = norm_gain_moe[None, :]
    router_t = jnp.pad(w_router.T, ((0, LANES - EXPERTS), (0, 0)))

    normed, queries, key_value, cosine, sine, reach, wanted, later, live = project(
        lengths, block_order, lane, hidden_in, gain_attn, w_query, w_key, w_value
    )
    pieces = to_all(key_value.reshape(dp_count, piece, SHARE))
    picks, ranks = route(begin, after(routes.T, key_value))
    far_out = peer(after(w_out, key_value), 2)
    begun = attend_own(queries, after(key_value, picks))
    picked = pick_pieces(wanted, after(pieces, far_out))
    earlier = to_all(picked.reshape(dp_count, steps * piece, SHARE))
    earlier = earlier.reshape(dp_count, steps, piece, SHARE)

    outs = [w_out, peer(after(w_out, picked), 1), far_out, peer(far_out, 1)]

    grad_rows = jnp.dot(picks, after(out_grad, picked), preferred_element_type=jnp.bfloat16)
    grad_arrived = to_all(after(grad_rows, earlier, begun[1]).reshape(EXPERTS, QUARTER, WIDTH))
    attended, attended_t, lse = attend(reach, begun, earlier)
    far = peer(attended, 2)
    residual, moe_cat, gates, moe_rows = residual_step(
        [attended, peer(attended, 1), far, peer(far, 1)],
        outs,
        hidden_in,
        gain_moe,
        router_t,
        ranks,
        picks,
    )
    own_pack = pack_weights(after(w_down[0], attended), w_gate[0], w_up[0])
    far_pack = peer(after(own_pack, far), 2)
    packed = [own_pack, peer(own_pack, 1), far_pack, peer(far_pack, 1)]

    grouped = to_all(after(moe_rows, far_pack).reshape(EXPERTS, QUARTER, -1)).reshape(SLOTS, -1)
    mix = mix_weights(begin, ranks, moe_cat)
    grouped_grad = grad_arrived.reshape(SLOTS, WIDTH)
    rows_out, row_grad, hidden_units, unit_grad = expert_step(lane, grouped, grouped_grad, packed)
    row_home = to_all(row_grad.reshape(dp_count, QUARTER, -1)).reshape(SLOTS, -1)
    rows_home = to_all(after(rows_out, row_home).reshape(dp_count, QUARTER, -1)).reshape(SLOTS, -1)

    unit_keep, unit_send = unit_grads(grouped, grouped_grad, hidden_units, unit_grad)
    unit_near = unit_keep.astype(jnp.float32) + peer(unit_send, 1).astype(jnp.float32)
    unit_low = unit_near[1].astype(jnp.bfloat16)
    cut = PACKED // 2
    unit_far_a = peer(unit_low[:cut], 2)
    keep, send = sum_home(rank, after(mix, unit_far_a), row_home)
    near = keep + peer(send, 1).astype(jnp.float32)
    mine = swap_sum(near, peer(near.astype(jnp.bfloat16), 2))
    theirs = peer(mine, 1)
    branch_grad, logit_grad, residual_grad, attended_grad, attended_grad_t, moe_gain = norm_back_step(
        rank, mine, theirs, gates, residual, gain_moe, router_t, out_grad, w_out
    )

    query_pre_grad, own_grads, later_grads = attend_back(
        reach,
        queries,
        begun[0],
        key_value,
        earlier,
        attended_grad,
        attended_grad_t,
        attended_t,
        lse,
        cosine,
        sine,
    )
    later_pieces = to_all(after(later_grads, rows_home).reshape(dp_count, steps * piece, SHARE))
    summed = sum_pieces(
        later, live, later_pieces.reshape(dp_count * steps, piece, SHARE), dp_count
    )
    kv_home = to_all(summed).reshape(BLOCK, SHARE)
    made = dense_grads(
        branch_grad, attended, normed, query_pre_grad, logit_grad, moe_cat, moe_gain
    )

    every, keep, send, inner = last_grads(
        rank,
        own_grads,
        kv_home,
        query_pre_grad,
        normed,
        hidden_in,
        w_query,
        w_key,
        w_value,
        cosine,
        sine,
        made,
        gain_attn,
    )
    near_norm = keep + peer(send, 1).astype(jnp.float32)
    far_norm = peer(near_norm[BLOCK:].astype(jnp.bfloat16), 2)
    inner = inner[0] + peer(inner[0], 1) + peer(inner[0], 2) + peer(inner[0], 3)
    arrived = to_all(every.reshape(dp_count, WIDTH // dp_count, -1))

    keep, send = sum_home(rank, mix, after(rows_home, every))
    near_mix = keep + peer(send, 1).astype(jnp.float32)
    far_mix = peer(near_mix[BLOCK:].astype(jnp.bfloat16), 2)
    dense = jnp.sum(arrived.astype(jnp.float32), axis=0)
    unit_far_b = peer(after(unit_low[cut:], far_norm), 2)
    normed_grad = near_norm[:BLOCK] + after(far_norm, dense).astype(jnp.float32)
    x = hidden_in.astype(jnp.float32)
    scale = lax.rsqrt(jnp.mean(x * x, axis=-1, keepdims=True) + epsilon)
    x_cols = lax.dynamic_slice_in_dim(x, column_start, SHARE, 1)
    weighted = normed_grad * lax.dynamic_slice_in_dim(gain_attn, column_start, SHARE, 1)
    inner = inner[:, None] / WIDTH
    grad_hidden = residual_grad + scale * weighted - x_cols * (scale * scale * scale * inner)
    mixture = near_mix[:BLOCK] + after(far_mix, dense).astype(jnp.float32)
    residual_cols = lax.dynamic_slice_in_dim(residual, column_start, SHARE, 1)
    out_hidden = (residual_cols + mixture).astype(jnp.bfloat16)

    at = 3 * SHARE
    attn_gain = dense[:, at + EXPERTS + 8]
    unit_far = jnp.concatenate([unit_far_a, after(unit_far_b, attn_gain)], axis=0)
    grad_w_gate, grad_w_up, grad_w_down = unit_finish(unit_near[0], unit_far)
    attn_gain = attn_gain + peer(attn_gain, 1) + peer(attn_gain, 2) + peer(attn_gain, 3)
    return (
        out_hidden,
        grad_hidden,
        dense[:, SHARE : 2 * SHARE],
        dense[:, 2 * SHARE : 2 * SHARE + LANES],
        dense[:, 2 * SHARE + LANES : at],
        dense[:, :SHARE].T,
        attn_gain,
        dense[:, at + EXPERTS],
        dense[:, at : at + EXPERTS],
        grad_w_gate,
        grad_w_up,
        grad_w_down,
    )


def solution(mesh):
    in_specs = (
        P("dp", None),
        P(),
        P(),
        P("dp", None),
        P(),
        P(None, "mp"),
        P(None, "mp"),
        P(None, "mp"),
        P("mp", None),
        P(),
        P(),
        P("dp", None, "mp"),
        P("dp", None, "mp"),
        P("dp", "mp", None),
        P("dp", None),
    )
    out_specs = (
        P("dp", "mp"),
        P("dp", "mp"),
        P("dp", "mp"),
        P("dp", "mp"),
        P("dp", "mp"),
        P("mp", "dp"),
        P("dp"),
        P("dp"),
        P("dp", None),
        P("dp", None, "mp"),
        P("dp", None, "mp"),
        P("dp", "mp", None),
    )
    return jax.shard_map(
        per_device, mesh=mesh, in_specs=in_specs, out_specs=out_specs, check_vma=False
    )
```

```python
import jax
import jax.numpy as jnp
import numpy as np
from jax import lax
from jax.experimental import pallas as pl
from jax.experimental.pallas import tpu as pltpu
from jax.sharding import PartitionSpec as P

HEAD_DIM = 64
EXPERTS = 32
BLOCK = 512
MAXLEN = 2048
CAP = 160
WIDTH = 1024
SHARE = 256
QUARTER = 40
SLOTS = 1280
LANES = 128
PACKED = 384

epsilon = 1e-06
residual_mult = 0.22
score_mult = 0.015625
rope_base = 10000.0
masked_score = -1e30

NN = (((1,), (0,)), ((), ()))
NT = (((1,), (1,)), ((), ()))
TN = (((0,), (0,)), ((), ()))


def mm(a, b, dims=NN):
    return lax.dot_general(a, b, dims, preferred_element_type=jnp.float32)


def to_all(x):
    return lax.all_to_all(x, "dp", 0, 0, tiled=True)


def crossed_groups(dp_count=32):
    groups = []
    for chip in range(2):
        for core in range(2):
            groups.append([i * 4 + ((chip ^ (core & i & 1)) * 2 + core) for i in range(dp_count)])
    return groups


def to_experts(x):
    return lax.all_to_all(
        x, ("dp", "mp"), 0, 0, axis_index_groups=crossed_groups(x.shape[0]), tiled=True
    )


def peer(x, flip):
    return lax.ppermute(x, "mp", [(i, i ^ flip) for i in range(4)])


def after(x, *others):
    return lax.optimization_barrier((x, *others))[0]


def vmem():
    return pl.BlockSpec(memory_space=pltpu.VMEM)


def smem():
    return pl.BlockSpec(memory_space=pltpu.SMEM)


def tiles(rows, width, row0=0):
    return pl.BlockSpec((rows, width), lambda i: (i + row0, 0))


def fixed(rows, width):
    return pl.BlockSpec((rows, width), lambda i: (0, 0))


def once(*shape):
    return pl.BlockSpec(shape, lambda i: (0,) * len(shape), pipeline_mode=pl.Buffered(1))


def run(kernel, name, steps, in_specs, out_specs, out_shape, args, estimate, scratch=(), free=(), limit=32):
    in_specs = [once(*a.shape) if s is None else s for s, a in zip(in_specs, args)]
    out_specs = [once(*o.shape) if s is None else s for s, o in zip(out_specs, out_shape)]
    args = [
        a
        if s.memory_space is not None or i in free
        else pltpu.with_memory_space_constraint(a, pltpu.HBM)
        for i, (s, a) in enumerate(zip(in_specs, args))
    ]
    out_shape = [
        o if s.memory_space == pltpu.SMEM else pltpu.HBM(o.shape, o.dtype)
        for s, o in zip(out_specs, out_shape)
    ]
    return pl.pallas_call(
        kernel,
        name=name,
        grid=(steps,),
        in_specs=in_specs,
        out_specs=out_specs,
        out_shape=out_shape,
        scratch_shapes=list(scratch),
        compiler_params=pltpu.CompilerParams(vmem_limit_bytes=limit << 20),
        cost_estimate=estimate,
    )(*args)


def out(shape, dtype):
    return jax.ShapeDtypeStruct(shape, dtype)


def cost(flops, moved, exps=0):
    return pl.CostEstimate(flops=flops, bytes_accessed=moved, transcendentals=exps)


def rope_constants():
    frequency = rope_base ** (-(np.arange(HEAD_DIM // 2, dtype=np.float64) * 2.0) / HEAD_DIM)
    wide = np.tile(frequency, 4)[None, :]
    made = []
    for count, apart in ((BLOCK // 16, 16), (16, 1), (8, BLOCK)):
        angles = np.arange(count, dtype=np.float64)[:, None] * apart * wide
        made += [np.cos(angles), np.sin(angles)]
    return [jnp.asarray(a.astype(np.float32)) for a in made]


def half_front(rows):
    lane = lax.broadcasted_iota(jnp.int32, (rows, LANES), 1)
    return (lane % HEAD_DIM) < HEAD_DIM // 2


def turned(chunk, cosine, signed_sine, back=False):
    partner = jnp.where(
        half_front(chunk.shape[0]), pltpu.roll(chunk, 96, 1), pltpu.roll(chunk, 32, 1)
    )
    if back:
        return chunk * cosine - partner * signed_sine
    return chunk * cosine + partner * signed_sine


def block_tables_in(lengths_ref, order_ref, rank_ref, offset_ref, inverse_ref, reach_ref, wanted_ref, later_ref, live_ref):
    count = order_ref.shape[0]
    steps = MAXLEN // BLOCK - 1

    def sequence(s, begin):
        def one(j, at):
            offset_ref[jnp.minimum(at, count - 1)] = j
            return at + 1

        return lax.fori_loop(0, lengths_ref[s], one, begin)

    lax.fori_loop(0, lengths_ref.shape[0], sequence, jnp.int32(0))

    def invert(d, carry):
        inverse_ref[order_ref[d]] = d
        return carry

    lax.fori_loop(0, count, invert, jnp.int32(0))
    reach_ref[0] = offset_ref[order_ref[rank_ref[0]]]

    def look(d, carry):
        packed = order_ref[d]
        for s in range(1, steps + 1):
            wanted_ref[d * steps + s - 1] = inverse_ref[jnp.maximum(packed - s, 0)]
            next_at = jnp.minimum(packed + s, count - 1)
            later_ref[d * steps + s - 1] = inverse_ref[next_at] * steps + s - 1
            is_live = jnp.logical_and(packed + s < count, offset_ref[next_at] >= s)
            live_ref[d * steps + s - 1] = jnp.where(is_live, 1, 0)
        return carry

    lax.fori_loop(0, count, look, jnp.int32(0))


def project_kernel(
    lengths_ref, order_ref, rank_ref, x_ref, gain_ref, wq_ref, wk_ref, wv_ref,
    cos16_ref, sin16_ref, cos1_ref, sin1_ref, cos0_ref, sin0_ref,
    normed_ref, q_ref, kv_ref, cosine_ref, sine_ref, reach_ref, wanted_ref, later_ref, live_ref,
    offset_ref, inverse_ref,
):
    @pl.when(pl.program_id(0) == 0)
    def _():
        block_tables_in(
            lengths_ref, order_ref, rank_ref, offset_ref, inverse_ref, reach_ref, wanted_ref, later_ref, live_ref
        )

    x = x_ref[...].astype(jnp.float32)
    scale = lax.rsqrt(jnp.mean(x * x, axis=1, keepdims=True) + epsilon)
    normed = (x * scale * gain_ref[...]).astype(jnp.bfloat16)
    normed_ref[...] = normed
    at = reach_ref[0]
    cos0, sin0 = cos0_ref[pl.ds(at, 1), :], sin0_ref[pl.ds(at, 1), :]
    cos16 = cos16_ref[...] * cos0 - sin16_ref[...] * sin0
    sin16 = sin16_ref[...] * cos0 + cos16_ref[...] * sin0
    cos1, sin1 = cos1_ref[...][None], sin1_ref[...][None]
    cosine = (cos16[:, None, :] * cos1 - sin16[:, None, :] * sin1).reshape(x.shape[0], LANES)
    sine = (sin16[:, None, :] * cos1 + cos16[:, None, :] * sin1).reshape(x.shape[0], LANES)
    sine = jnp.where(half_front(x.shape[0]), -sine, sine)
    cosine_ref[...] = cosine
    sine_ref[...] = sine
    kv_ref[:, :LANES] = turned(mm(normed, wk_ref[...]), cosine, sine).astype(jnp.bfloat16)
    kv_ref[:, LANES:] = mm(normed, wv_ref[...]).astype(jnp.bfloat16)
    queries = mm(normed, wq_ref[...])
    for i in range(0, SHARE, LANES):
        q_ref[:, i : i + LANES] = turned(queries[:, i : i + LANES], cosine, sine).astype(jnp.bfloat16)


def project(lengths, order, rank, x, gain, w_query, w_key, w_value):
    tile = 256
    count = order.shape[0]
    steps = MAXLEN // BLOCK - 1
    bf16, f32 = jnp.bfloat16, jnp.float32
    return run(
        project_kernel,
        "project",
        BLOCK // tile,
        [smem()] * 3
        + [tiles(tile, WIDTH), None, None, None, None]
        + [tiles(tile // 16, LANES)] * 2
        + [None] * 4,
        [tiles(tile, WIDTH), tiles(tile, SHARE), tiles(tile, SHARE)]
        + [tiles(tile, LANES)] * 2
        + [smem()] * 4,
        [out((BLOCK, WIDTH), bf16), out((BLOCK, SHARE), bf16), out((BLOCK, SHARE), bf16)]
        + [out((BLOCK, LANES), f32)] * 2
        + [out((1,), jnp.int32)]
        + [out((count * steps,), jnp.int32)] * 3,
        (lengths, order, rank, x, gain, w_query, w_key, w_value, *rope_constants()),
        cost(540_000_000, 4_000_000, 512),
        [pltpu.SMEM((count,), jnp.int32), pltpu.SMEM((count,), jnp.int32)],
    )


def pick_kernel(wanted_ref, pieces_ref, picked_ref):
    def one(i, carry):
        picked_ref[i] = pieces_ref[wanted_ref[i]]
        return carry

    lax.fori_loop(0, picked_ref.shape[0], one, jnp.int32(0), unroll=4)


def pick_pieces(wanted, pieces):
    shape = out((wanted.shape[0], *pieces.shape[1:]), pieces.dtype)
    return run(
        pick_kernel, "pick_pieces", 1, [smem(), None], [None], [shape], (wanted, pieces), cost(0, 1_100_000), free=(1,)
    )[0]


def sum_kernel(later_ref, live_ref, pieces_ref, sum_ref):
    steps = MAXLEN // BLOCK - 1

    def one(d, carry):
        total = jnp.zeros(sum_ref.shape[1:], jnp.float32)
        for s in range(steps):
            part = pieces_ref[later_ref[d * steps + s]].astype(jnp.float32)
            total = total + jnp.where(live_ref[d * steps + s] == 1, part, 0.0)
        sum_ref[d] = total.astype(sum_ref.dtype)
        return carry

    lax.fori_loop(0, sum_ref.shape[0], one, jnp.int32(0), unroll=2)


def sum_pieces(later, live, pieces, count):
    shape = out((count, *pieces.shape[1:]), pieces.dtype)
    return run(
        sum_kernel,
        "sum_pieces",
        1,
        [smem(), smem(), None],
        [None],
        [shape],
        (later, live, pieces),
        cost(0, 1_100_000),
        free=(2,),
    )[0]


def pack_kernel(down_ref, gate_ref, up_ref, packed_ref):
    packed_ref[:LANES, :] = down_ref[...]
    for k in range(4):
        rows = slice(k * SHARE, (k + 1) * SHARE)
        packed_ref[LANES:, k * SHARE : k * SHARE + LANES] = gate_ref[rows, :]
        packed_ref[LANES:, k * SHARE + LANES : (k + 1) * SHARE] = up_ref[rows, :]


def pack_weights(w_down, w_gate, w_up):
    shape = out((PACKED, WIDTH), jnp.bfloat16)
    return run(
        pack_kernel, "pack_weights", 1, [None] * 3, [None], [shape], (w_down, w_gate, w_up), cost(0, 1_600_000)
    )[0]


def route_kernel(begin_ref, routes_ref, picks_ref, ranks_ref):
    tokens = routes_ref.shape[1]
    expert_at = lax.broadcasted_iota(jnp.int32, (LANES, tokens), 0)
    hits = jnp.zeros((LANES, tokens), jnp.float32)
    for k in range(routes_ref.shape[0]):
        hits = hits + jnp.where(routes_ref[k : k + 1, :] == expert_at, 1.0, 0.0)
    row_at = lax.broadcasted_iota(jnp.int32, (tokens, tokens), 0)
    column_at = lax.broadcasted_iota(jnp.int32, (tokens, tokens), 1)
    before = jnp.where(row_at < column_at, 1.0, 0.0).astype(jnp.bfloat16)
    ranks = jnp.where(hits > 0.5, mm(hits.astype(jnp.bfloat16), before), -1.0)
    ranks_ref[...] = ranks
    slot_at = lax.broadcasted_iota(jnp.int32, (QUARTER, tokens), 0) + begin_ref[0]
    slot_at = slot_at.astype(jnp.float32)
    for e in range(EXPERTS):
        picks_ref[e * QUARTER : (e + 1) * QUARTER, :] = jnp.where(
            ranks[e : e + 1, :] == slot_at, 1.0, 0.0
        ).astype(jnp.bfloat16)


def route(begin, routes_t):
    return run(
        route_kernel,
        "route",
        1,
        [smem(), None],
        [None, None],
        [out((SLOTS, BLOCK), jnp.bfloat16), out((LANES, BLOCK), jnp.float32)],
        (begin, routes_t),
        cost(100_000_000, 1_600_000),
        free=(1,),
    )


def padded_columns(rows_t, out_ref):
    zero = jnp.zeros((HEAD_DIM, rows_t.shape[1]), out_ref.dtype)
    for h in range(4):
        mine = rows_t[h * HEAD_DIM : (h + 1) * HEAD_DIM].astype(out_ref.dtype)
        at = (h // 2) * HEAD_DIM
        out_ref[h, pl.ds(at, HEAD_DIM), :] = mine
        out_ref[h, pl.ds(HEAD_DIM - at, HEAD_DIM), :] = zero


def padded_rows(rows, out_ref):
    n = rows.shape[0]
    lane = lax.broadcasted_iota(jnp.int32, (n, 128), 1)
    for h in range(4):
        pair = rows[:, (h // 2) * 128 : (h // 2) * 128 + 128].astype(jnp.float32)
        if h % 2 != h // 2:
            pair = pltpu.roll(pair, HEAD_DIM, 1)
        own = (lane < HEAD_DIM) if h // 2 == 0 else (lane >= HEAD_DIM)
        out_ref[pl.ds(h * n, n), :] = jnp.where(own, pair, 0.0).astype(out_ref.dtype)


def attend_block(key_rows, value_rows, first, qpad_ref, max_ref, sum_ref, out_t_ref):
    half = BLOCK // 2
    for h in range(4):
        group = (h // 2) * HEAD_DIM
        for t in range(2):
            cols = slice(t * half, (t + 1) * half)
            rows = half if first and t == 0 else BLOCK
            scores = mm(key_rows[:rows], qpad_ref[h, :, cols])
            if first:
                key_at = lax.broadcasted_iota(jnp.int32, scores.shape, 0)
                query_at = lax.broadcasted_iota(jnp.int32, scores.shape, 1) + t * half
                scores = jnp.where(key_at > query_at, masked_score, scores)
            new_max = jnp.max(scores, axis=0, keepdims=True)
            if not first:
                old_max = max_ref[h : h + 1, cols]
                new_max = jnp.maximum(new_max, old_max)
                shrink = jnp.exp(old_max - new_max)
            weights = jnp.exp(scores - new_max)
            total = jnp.sum(weights, axis=0, keepdims=True)
            part = mm(value_rows[:rows], weights.astype(jnp.bfloat16), TN)[group : group + HEAD_DIM]
            mine = pl.ds(h * HEAD_DIM, HEAD_DIM)
            if not first:
                total = total + sum_ref[h : h + 1, cols] * shrink
                part = part + out_t_ref[mine, cols] * shrink
            max_ref[h : h + 1, cols] = new_max
            sum_ref[h : h + 1, cols] = total
            out_t_ref[mine, cols] = part


def attend_own_kernel(q_ref, own_ref, qpad_ref, max_ref, sum_ref, out_t_ref):
    padded_columns(jnp.transpose(q_ref[...].astype(jnp.float32) * score_mult), qpad_ref)
    max_ref[...] = jnp.zeros_like(max_ref)
    sum_ref[...] = jnp.ones_like(sum_ref)
    attend_block(own_ref[:, :LANES], own_ref[:, LANES:], True, qpad_ref, max_ref, sum_ref, out_t_ref)


def attend_own(queries, own_kv):
    return pl.pallas_call(
        attend_own_kernel,
        name="attend_own",
        in_specs=[vmem()] * 2,
        out_specs=[vmem()] * 4,
        out_shape=[
            out((4, LANES, BLOCK), jnp.bfloat16),
            out((8, BLOCK), jnp.float32),
            out((8, BLOCK), jnp.float32),
            out((SHARE, BLOCK), jnp.float32),
        ],
        compiler_params=pltpu.CompilerParams(vmem_limit_bytes=36 << 20),
        cost_estimate=cost(1_000_000_000, 2_000_000, 600_000),
    )(queries, own_kv)


def attend_kernel(
    reach_ref, qpad_ref, max0_ref, sum0_ref, out0_ref, prev_ref, att_ref, out_t_ref, lse_ref, max_ref, sum_ref
):
    max_ref[...] = max0_ref[...]
    sum_ref[...] = sum0_ref[...]
    out_t_ref[...] = out0_ref[...]

    @pl.loop(1, reach_ref[0] + 1)
    def _(step):
        rows = prev_ref[:, pl.ds(step - 1, 1)].reshape(BLOCK, SHARE)
        attend_block(rows[:, :LANES], rows[:, LANES:], False, qpad_ref, max_ref, sum_ref, out_t_ref)

    lse_ref[...] = max_ref[...] + jnp.log(sum_ref[...])
    for h in range(4):
        mine = pl.ds(h * HEAD_DIM, HEAD_DIM)
        out_t_ref[mine, :] = out_t_ref[mine, :] / sum_ref[h : h + 1, :]
    att_ref[...] = jnp.transpose(out_t_ref[...]).astype(jnp.bfloat16)


def attend(reach, begun, earlier):
    return run(
        attend_kernel,
        "attend",
        1,
        [smem()] + [vmem()] * 5,
        [None] * 3,
        [
            out((BLOCK, SHARE), jnp.bfloat16),
            out((SHARE, BLOCK), jnp.float32),
            out((8, BLOCK), jnp.float32),
        ],
        (reach, *begun, earlier),
        cost(4_000_000_000, 3_000_000, 3_000_000),
        [pltpu.VMEM((8, BLOCK), jnp.float32), pltpu.VMEM((8, BLOCK), jnp.float32)],
        limit=36,
    )


def attend_back_kernel(
    reach_ref, q_ref, qpad_ref, own_ref, prev_ref, grad_ref, grad_t_ref, out_t_ref, lse_ref, cos_ref, sin_ref,
    qgrad_ref, own_grad_ref, prev_grad_ref,
    gpad_ref, qrows_ref, grows_ref, ds_ref, p_ref, delta_ref, dq_ref,
):
    half = BLOCK // 2
    q_scaled = q_ref[...].astype(jnp.float32) * score_mult
    padded_rows(q_scaled, qrows_ref)
    padded_columns(grad_t_ref[...], gpad_ref)
    padded_rows(grad_ref[...], grows_ref)
    both = grad_t_ref[...].astype(jnp.float32) * out_t_ref[...]
    for h in range(4):
        delta_ref[h : h + 1, :] = jnp.sum(
            both[h * HEAD_DIM : (h + 1) * HEAD_DIM], axis=0, keepdims=True
        )


    def block(key_rows, value_rows, first):
        for h in range(4):
            for t in range(2):
                cols = slice(t * half, (t + 1) * half)
                wide = slice(h * BLOCK + t * half, h * BLOCK + (t + 1) * half)
                rows = half if first and t == 0 else BLOCK
                scores = mm(key_rows[:rows], qpad_ref[h, :, cols])
                weights = jnp.exp(scores - lse_ref[h : h + 1, cols])
                if first:
                    key_at = lax.broadcasted_iota(jnp.int32, scores.shape, 0)
                    query_at = lax.broadcasted_iota(jnp.int32, scores.shape, 1) + t * half
                    weights = jnp.where(key_at > query_at, 0.0, weights)
                weight_grad = mm(value_rows[:rows], gpad_ref[h, :, cols])
                score_grad = weights * (weight_grad - delta_ref[h : h + 1, cols])
                p_ref[:rows, wide] = weights.astype(jnp.bfloat16)
                ds_ref[:rows, wide] = score_grad.astype(jnp.bfloat16)
                if rows < BLOCK:
                    p_ref[rows:, wide] = jnp.zeros((BLOCK - rows, half), jnp.bfloat16)
                    ds_ref[rows:, wide] = jnp.zeros((BLOCK - rows, half), jnp.bfloat16)
        key_grad = mm(ds_ref[...], qrows_ref[...])
        value_grad = mm(p_ref[...], grows_ref[...])
        for h in range(4):
            group = (h // 2) * HEAD_DIM
            mine = pl.ds(h * HEAD_DIM, HEAD_DIM)
            part = mm(key_rows, ds_ref[:, h * BLOCK : (h + 1) * BLOCK], TN)[group : group + HEAD_DIM]
            dq_ref[mine, :] = part if first else dq_ref[mine, :] + part
        return key_grad, value_grad

    key_grad, value_grad = block(own_ref[:, :LANES], own_ref[:, LANES:], True)
    own_grad_ref[:, :LANES] = key_grad
    own_grad_ref[:, LANES:] = value_grad

    @pl.loop(1, reach_ref[0] + 1)
    def _(step):
        rows = prev_ref[:, pl.ds(step - 1, 1)].reshape(BLOCK, SHARE)
        key_grad, value_grad = block(rows[:, :LANES], rows[:, LANES:], False)
        parts = prev_grad_ref.shape[0]
        shape = (parts, 1, BLOCK // parts, LANES)
        prev_grad_ref[:, pl.ds(step - 1, 1), :, :LANES] = key_grad.astype(jnp.bfloat16).reshape(shape)
        prev_grad_ref[:, pl.ds(step - 1, 1), :, LANES:] = value_grad.astype(jnp.bfloat16).reshape(shape)

    query_grad = jnp.transpose(dq_ref[...]) * score_mult
    for i in range(0, SHARE, LANES):
        qgrad_ref[:, i : i + LANES] = turned(
            query_grad[:, i : i + LANES], cos_ref[...], sin_ref[...], back=True
        ).astype(jnp.bfloat16)


def attend_back(reach, queries, padded, own_kv, earlier, grad, grad_t, out_t, lse, cosine, signed_sine):
    return run(
        attend_back_kernel,
        "attend_back",
        1,
        [smem()] + [vmem()] * 10,
        [None] * 3,
        [
            out((BLOCK, SHARE), jnp.bfloat16),
            out((BLOCK, SHARE), jnp.float32),
            out(earlier.shape, jnp.bfloat16),
        ],
        (reach, queries, padded, own_kv, earlier, grad, grad_t, out_t, lse, cosine, signed_sine),
        cost(12_000_000_000, 5_000_000, 3_000_000),
        [
            pltpu.VMEM((4, LANES, BLOCK), jnp.bfloat16),
            pltpu.VMEM((4 * BLOCK, LANES), jnp.bfloat16),
            pltpu.VMEM((4 * BLOCK, LANES), jnp.bfloat16),
            pltpu.VMEM((BLOCK, 4 * BLOCK), jnp.bfloat16),
            pltpu.VMEM((BLOCK, 4 * BLOCK), jnp.bfloat16),
            pltpu.VMEM((8, BLOCK), jnp.float32),
            pltpu.VMEM((SHARE, BLOCK), jnp.float32),
        ],
        limit=36,
    )


def residual_kernel(
    a0, a1, a2, a3, w0, w1, w2, w3, x_ref, gain_ref, router_ref, ranks_ref, picks_ref,
    residual_ref, moe_ref, gates_ref, rows_ref, held_ref,
):
    step = pl.program_id(0)
    tile = x_ref.shape[0]

    @pl.when(step < BLOCK // tile)
    def _():
        branch = mm(a0[...], w0[...])
        for a, w in ((a1, w1), (a2, w2), (a3, w3)):
            branch = branch + mm(a[...], w[...])
        residual = x_ref[...].astype(jnp.float32) + residual_mult * branch
        residual_ref[...] = residual
        scale = lax.rsqrt(jnp.mean(residual * residual, axis=1, keepdims=True) + epsilon)
        moe_in = (residual * scale * gain_ref[...]).astype(jnp.bfloat16)
        moe_ref[:, :WIDTH] = moe_in
        logits = mm(router_ref[...], moe_in, NT)
        chosen = ranks_ref[...] >= 0.0
        kept = jnp.where(chosen, logits, masked_score)
        top = jnp.max(kept, axis=0, keepdims=True)
        raised = jnp.where(chosen, jnp.exp(kept - top), 0.0)
        gates = raised / jnp.sum(raised, axis=0, keepdims=True)
        gates_ref[...] = gates
        low = (residual_mult * jnp.transpose(gates)).astype(jnp.bfloat16)
        moe_ref[:, WIDTH:] = low
        held_ref[pl.ds(step * tile, tile), :WIDTH] = moe_in
        held_ref[pl.ds(step * tile, tile), WIDTH:] = low

    @pl.when(step >= BLOCK // tile)
    def _():
        rows_ref[...] = mm(picks_ref[...], held_ref[...]).astype(jnp.bfloat16)


def residual_step(attended, w_out, x, gain, router_t, ranks, picks):
    tile = 256
    first = BLOCK // tile
    slot_tile = SLOTS // 4

    def early(rows, width):
        return pl.BlockSpec((rows, width), lambda i: (jnp.minimum(i, first - 1), 0))

    def late(rows, width):
        return pl.BlockSpec((rows, width), lambda i: (jnp.maximum(i - first, 0), 0))

    by_columns = pl.BlockSpec((LANES, tile), lambda i: (0, jnp.minimum(i, first - 1)))
    return run(
        residual_kernel,
        "residual_step",
        first + 4,
        [early(tile, SHARE)] * 4
        + [None] * 4
        + [early(tile, WIDTH), None, None, by_columns, late(slot_tile, BLOCK)],
        [early(tile, WIDTH), early(tile, WIDTH + LANES), by_columns, late(slot_tile, WIDTH + LANES)],
        [
            out((BLOCK, WIDTH), jnp.float32),
            out((BLOCK, WIDTH + LANES), jnp.bfloat16),
            out((LANES, BLOCK), jnp.float32),
            out((SLOTS, WIDTH + LANES), jnp.bfloat16),
        ],
        (*attended, *w_out, x, gain, router_t, ranks, picks),
        cost(2_700_000_000, 12_000_000, 70_000),
        [pltpu.VMEM((BLOCK, WIDTH + LANES), jnp.bfloat16)],
        free=(1, 2, 3, 5, 6, 7, 10),
    )


def mix_kernel(begin_ref, ranks_ref, moe_ref, mix_ref):
    ranks = jnp.transpose(ranks_ref[...]).astype(jnp.bfloat16)
    gates = moe_ref[:, WIDTH:]
    width = 640
    for at in range(0, SLOTS, width):
        expert_at = lax.broadcasted_iota(jnp.int32, (LANES, width), 0)
        first = expert_at * QUARTER - at
        slot_at = lax.broadcasted_iota(jnp.int32, (LANES, width), 1)
        inside = jnp.logical_and(slot_at >= first, slot_at < first + QUARTER)
        spread = jnp.where(inside, 1.0, 0.0).astype(jnp.bfloat16)
        within = jnp.sum(jnp.where(inside, slot_at - first, 0), axis=0, keepdims=True) + begin_ref[0]
        hit = mm(ranks, spread) == within.astype(jnp.float32)
        mix_ref[:, at : at + width] = jnp.where(hit, mm(gates, spread), 0.0).astype(jnp.bfloat16)


def mix_weights(begin, ranks, moe_cat):
    return run(
        mix_kernel,
        "mix_weights",
        1,
        [smem(), None, None],
        [None],
        [out((BLOCK, SLOTS), jnp.bfloat16)],
        (begin, ranks, moe_cat),
        cost(350_000_000, 3_000_000),
    )[0]


def expert_kernel(
    lane_ref, x_ref, grad_ref, p0, p1, p2, p3,
    out_ref, row_ref, hidden_ref, units_ref,
):
    packed = (p0, p1, p2, p3)
    rows = out_ref.shape[0]
    here = pl.ds(pl.program_id(0) * rows, rows)
    lane = lax.broadcasted_iota(jnp.int32, (rows, LANES), 1) == lane_ref[0]
    gate = jnp.sum(
        jnp.where(lane, x_ref[here, WIDTH:].astype(jnp.float32), 0.0), axis=1, keepdims=True
    )
    x = x_ref[here, :WIDTH]
    grad = grad_ref[...]
    gates, ups, sigmoids, hidden = [], [], [], []
    for p in packed:
        pre = None
        for k in range(4):
            columns = slice(k * SHARE, (k + 1) * SHARE)
            term = mm(x[:, columns], p[LANES:, columns])
            pre = term if pre is None else pre + term
        gate_pre, up_pre = pre[:, :LANES], pre[:, LANES:]
        sigmoid = 1.0 / (1.0 + jnp.exp(-gate_pre))
        gates.append(gate_pre)
        ups.append(up_pre)
        sigmoids.append(sigmoid)
        hidden.append(gate_pre * sigmoid * up_pre)
    hidden_low = jnp.concatenate([h.astype(jnp.bfloat16) for h in hidden], axis=1)
    down = jnp.concatenate([p[:LANES, :] for p in packed], axis=0)
    made = mm(hidden_low, down).astype(jnp.bfloat16)
    out_ref[...] = made
    gate_grad = jnp.sum(grad.astype(jnp.float32) * made.astype(jnp.float32), axis=1, keepdims=True)
    row_ref[:, WIDTH:] = jnp.where(lane, gate_grad, 0.0).astype(jnp.bfloat16)
    hidden_grad = mm(grad, down, NT)
    row = None
    for j, p in enumerate(packed):
        part = hidden_grad[:, j * LANES : (j + 1) * LANES]
        silu = gates[j] * sigmoids[j]
        gate_pre_grad = part * ups[j] * sigmoids[j] * (1.0 + gates[j] * (1.0 - sigmoids[j]))
        up_pre_grad = part * silu
        hidden_ref[:, j * LANES : (j + 1) * LANES] = (hidden[j] * gate).astype(jnp.bfloat16)
        units_ref[:, j * SHARE : j * SHARE + LANES] = (gate_pre_grad * gate).astype(jnp.bfloat16)
        units_ref[:, j * SHARE + LANES : (j + 1) * SHARE] = (up_pre_grad * gate).astype(jnp.bfloat16)
        both = jnp.concatenate([gate_pre_grad, up_pre_grad], axis=1).astype(jnp.bfloat16)
        terms = [
            mm(both, p[LANES:, k * SHARE : (k + 1) * SHARE], NT) for k in range(4)
        ]
        row = terms if row is None else [a + b for a, b in zip(row, terms)]
    for k in range(4):
        row_ref[:, k * SHARE : (k + 1) * SHARE] = row[k].astype(jnp.bfloat16)


def expert_step(lane, x, grad, packed):
    tile = 320
    return run(
        expert_kernel,
        "expert_step",
        SLOTS // tile,
        [smem(), vmem(), tiles(tile, WIDTH)] + [None] * 4,
        [tiles(tile, WIDTH), tiles(tile, WIDTH + LANES), tiles(tile, 512), tiles(tile, WIDTH)],
        [
            out((SLOTS, WIDTH), jnp.bfloat16),
            out((SLOTS, WIDTH + LANES), jnp.bfloat16),
            out((SLOTS, 512), jnp.bfloat16),
            out((SLOTS, WIDTH), jnp.bfloat16),
        ],
        (lane, x, grad, *packed),
        cost(8_000_000_000, 18_000_000, 700_000),
        limit=40,
    )


def unit_grads_kernel(x_ref, grad_ref, hidden_ref, units_ref, keep_ref, send_ref, turned_ref):
    step = pl.program_id(0)

    @pl.when(step == 0)
    def _():
        for k in range(4):
            columns = slice(k * SHARE, (k + 1) * SHARE)
            turned_ref[columns, :] = jnp.transpose(x_ref[:, columns])

    def write(to_ref):
        to_ref[0, :LANES, :] = mm(hidden_ref[...], grad_ref[...], TN).astype(jnp.bfloat16)
        for k in range(4):
            columns = slice(k * SHARE, (k + 1) * SHARE)
            to_ref[0, LANES:, columns] = mm(turned_ref[columns, :], units_ref[...]).astype(jnp.bfloat16)

    @pl.when(step < 2)
    def _():
        write(keep_ref)

    @pl.when(step >= 2)
    def _():
        write(send_ref)


def unit_grads(x, grad, hidden, units):
    rows = SHARE + LANES

    def share_of(i):
        return jnp.where(i < 2, 2 * i, 2 * i - 3)

    return run(
        unit_grads_kernel,
        "unit_grads",
        4,
        [
            vmem(),
            None,
            pl.BlockSpec((SLOTS, LANES), lambda i: (0, share_of(i))),
            pl.BlockSpec((SLOTS, SHARE), lambda i: (0, share_of(i))),
        ],
        [
            pl.BlockSpec((1, rows, WIDTH), lambda i: (jnp.minimum(i, 1), 0, 0)),
            pl.BlockSpec((1, rows, WIDTH), lambda i: (jnp.maximum(i - 2, 0), 0, 0)),
        ],
        [out((2, rows, WIDTH), jnp.bfloat16), out((2, rows, WIDTH), jnp.bfloat16)],
        (x, grad, hidden, units),
        cost(4_000_000_000, 12_000_000),
        [pltpu.VMEM((WIDTH, SLOTS), jnp.bfloat16)],
        limit=36,
    )


def unit_finish_kernel(mine_ref, got_ref, gate_ref, up_ref, down_ref):
    total = mine_ref[...].astype(jnp.float32) + got_ref[...].astype(jnp.float32)
    down_ref[0] = total[:LANES, :]
    for k in range(4):
        rows = slice(k * SHARE, (k + 1) * SHARE)
        gate_ref[0, rows, :] = total[LANES:, k * SHARE : k * SHARE + LANES]
        up_ref[0, rows, :] = total[LANES:, k * SHARE + LANES : (k + 1) * SHARE]


def unit_finish(mine, got):
    return run(
        unit_finish_kernel,
        "unit_finish",
        1,
        [None] * 2,
        [None] * 3,
        [
            out((1, WIDTH, LANES), jnp.float32),
            out((1, WIDTH, LANES), jnp.float32),
            out((1, LANES, WIDTH), jnp.float32),
        ],
        (mine, got),
        cost(1_000_000, 3_000_000),
        free=(0, 1),
    )


def home_kernel(rank_ref, mix_ref, rows_ref, keep_ref, send_ref):
    rank = rank_ref[0]
    extra = rows_ref.shape[1] > WIDTH
    for j in range(4):
        at = pl.multiple_of(jnp.bitwise_xor(rank, j) * SHARE, SHARE)
        total = mm(mix_ref[...], rows_ref[:, pl.ds(at, SHARE)])
        to_ref = send_ref if j % 2 else keep_ref
        to_ref[(j // 2) * BLOCK : (j // 2 + 1) * BLOCK, :] = total.astype(to_ref.dtype)
    if extra:
        gate_grads = jnp.transpose(mm(mix_ref[...], rows_ref[:, WIDTH:]))[:EXPERTS]
        for to_ref in (keep_ref, send_ref):
            for i in range(2):
                at = 2 * BLOCK + i * EXPERTS
                to_ref[at : at + EXPERTS, :] = gate_grads[:, i * SHARE : (i + 1) * SHARE].astype(
                    to_ref.dtype
                )


def sum_home(rank, mix, rows):
    height = 2 * BLOCK + (2 * EXPERTS if rows.shape[1] > WIDTH else 0)
    return run(
        home_kernel,
        "sum_home",
        1,
        [smem(), None, vmem()],
        [None] * 2,
        [out((height, SHARE), jnp.float32), out((height, SHARE), jnp.bfloat16)],
        (rank, mix, rows),
        cost(1_500_000_000, 6_000_000),
        limit=36,
    )


def swap_kernel(mine_ref, got_ref, total_ref):
    mine, got = mine_ref, got_ref
    half = BLOCK
    total_ref[:half] = (mine[:half] + got[half : 2 * half].astype(jnp.float32)).astype(total_ref.dtype)
    total_ref[half : 2 * half] = (
        mine[half : 2 * half] + got[:half].astype(jnp.float32)
    ).astype(total_ref.dtype)
    total_ref[2 * half :] = (mine[2 * half :] + got[2 * half :].astype(jnp.float32)).astype(
        total_ref.dtype
    )


def swap_sum(mine, got):
    return run(
        swap_kernel,
        "swap_sum",
        1,
        [None] * 2,
        [None],
        [out(mine.shape, jnp.bfloat16)],
        (mine, got),
        cost(1_000_000, 2_500_000),
        free=(0, 1),
    )[0]


def norm_back_kernel(
    rank_ref, g0, g2, g1, g3, z_ref, gates_ref, residual_ref, gain_ref, router_ref, grad_ref, w_ref,
    low_ref, logit_ref, own_ref, att_ref, att_t_ref, gain_grad_ref, u_ref,
):
    rank = rank_ref[0]
    for flip, part in enumerate((g0, g1, g2, g3)):
        at = pl.multiple_of(jnp.bitwise_xor(rank, flip) * SHARE, SHARE)
        u_ref[:, pl.ds(at, SHARE)] = part[...].astype(jnp.float32)
    weighted_grads = z_ref[...].astype(jnp.float32)
    gates = gates_ref[:EXPERTS, :]
    inner = jnp.sum(weighted_grads, axis=0, keepdims=True)
    logit_grad = (weighted_grads - gates * inner).astype(jnp.bfloat16)
    logit_ref[...] = logit_grad
    u = u_ref[...] + mm(logit_grad, router_ref[:EXPERTS, :], TN)
    v = residual_ref[...]
    scale = lax.rsqrt(jnp.mean(v * v, axis=1, keepdims=True) + epsilon)
    weighted = u * gain_ref[...]
    mean = jnp.mean(weighted * v, axis=1, keepdims=True)
    total = grad_ref[...].astype(jnp.float32) + scale * weighted - v * (scale * scale * scale * mean)

    @pl.when(pl.program_id(0) == 0)
    def _():
        gain_grad_ref[...] = jnp.zeros_like(gain_grad_ref)

    gain_grad_ref[0:1, :] += jnp.sum(u * v * scale, axis=0, keepdims=True)
    low = (residual_mult * total).astype(jnp.bfloat16)
    low_ref[...] = low
    u_ref[...] = total
    own_ref[...] = u_ref[:, pl.ds(pl.multiple_of(rank * SHARE, SHARE), SHARE)]
    att_ref[...] = mm(low, w_ref[...], NT).astype(jnp.bfloat16)
    att_t_ref[...] = mm(w_ref[...], low, NT).astype(jnp.bfloat16)


def norm_back_step(rank, mine, theirs, gates, residual, gain, router_t, out_grad, w_out):
    tile = 256
    by_columns = pl.BlockSpec((EXPERTS, tile), lambda i: (0, i))
    return run(
        norm_back_kernel,
        "norm_back_step",
        BLOCK // tile,
        [smem()]
        + [tiles(tile, SHARE), tiles(tile, SHARE, BLOCK // tile)] * 2
        + [
            tiles(EXPERTS, SHARE, 2 * BLOCK // EXPERTS),
            pl.BlockSpec((LANES, tile), lambda i: (0, i)),
            tiles(tile, WIDTH),
            None,
            None,
            tiles(tile, WIDTH),
            None,
        ],
        [
            tiles(tile, WIDTH),
            by_columns,
            tiles(tile, SHARE),
            tiles(tile, SHARE),
            pl.BlockSpec((SHARE, tile), lambda i: (0, i)),
            fixed(8, WIDTH),
        ],
        [
            out((BLOCK, WIDTH), jnp.bfloat16),
            out((EXPERTS, BLOCK), jnp.bfloat16),
            out((BLOCK, SHARE), jnp.float32),
            out((BLOCK, SHARE), jnp.bfloat16),
            out((SHARE, BLOCK), jnp.bfloat16),
            out((8, WIDTH), jnp.float32),
        ],
        (rank, mine, mine, theirs, theirs, mine, gates, residual, gain, router_t, out_grad, w_out),
        cost(700_000_000, 9_000_000, 512),
        [pltpu.VMEM((tile, WIDTH), jnp.float32)],
        free=(3, 4, 9),
    )


def dense_grads_kernel(low_ref, attended_ref, normed_ref, qgrad_ref, logit_ref, moe_ref, gain_ref, made_ref):
    made_ref[:, :SHARE] = mm(low_ref[...], attended_ref[...], TN).astype(jnp.bfloat16)
    made_ref[:, SHARE : 2 * SHARE] = mm(normed_ref[...], qgrad_ref[...], TN).astype(jnp.bfloat16)
    router = mm(logit_ref[...], moe_ref[:, :WIDTH])
    stacked = jnp.concatenate(
        [router, gain_ref[...], jnp.zeros((LANES - EXPERTS - 8, WIDTH), jnp.float32)], axis=0
    )
    made_ref[:, 2 * SHARE :] = jnp.transpose(stacked).astype(jnp.bfloat16)


def dense_grads(low, attended, normed, qgrad, logit, moe_cat, gain_grad):
    return run(
        dense_grads_kernel,
        "dense_grads",
        1,
        [None] * 7,
        [None],
        [out((WIDTH, 2 * SHARE + LANES), jnp.bfloat16)],
        (low, attended, normed, qgrad, logit, moe_cat, gain_grad),
        cost(600_000_000, 6_000_000),
    )[0]


def last_grads_kernel(
    rank_ref, own_ref, home_ref, qgrad_ref, normed_ref, x_ref, wq_ref, wk_ref, wv_ref, cos_ref, sin_ref, made_ref,
    gain_ref, all_ref, keep_ref, send_ref, inner_ref, part_ref,
):
    rank = rank_ref[0]
    kv = own_ref[...] + home_ref[...].astype(jnp.float32)
    key_grad = turned(kv[:, :LANES], cos_ref[...], sin_ref[...], back=True).astype(jnp.bfloat16)
    value_grad = kv[:, LANES:].astype(jnp.bfloat16)
    both = jnp.concatenate([key_grad, value_grad], axis=1)
    all_ref[:, : 2 * SHARE] = made_ref[:, : 2 * SHARE]
    all_ref[:, 2 * SHARE : 3 * SHARE] = mm(normed_ref[...], both, TN).astype(jnp.bfloat16)
    gain = jnp.zeros((1, WIDTH), jnp.float32)
    tile = 128
    for i in range(0, BLOCK, tile):
        rows = slice(i, i + tile)
        part = mm(qgrad_ref[rows, :], wq_ref[...], NT)
        part = part + mm(key_grad[rows], wk_ref[...], NT) + mm(value_grad[rows], wv_ref[...], NT)
        x = x_ref[rows, :].astype(jnp.float32)
        scale = lax.rsqrt(jnp.mean(x * x, axis=1, keepdims=True) + epsilon)
        along = part * x
        gain = gain + jnp.sum(along * scale, axis=0, keepdims=True)
        inner = jnp.sum(along * gain_ref[...], axis=1, keepdims=True)
        inner_ref[:, rows] = jnp.transpose(jnp.broadcast_to(inner, (tile, LANES)))[:8]
        part_ref[rows, :] = part
    for j in range(4):
        at = pl.multiple_of(jnp.bitwise_xor(rank, j) * SHARE, SHARE)
        to_ref = send_ref if j % 2 else keep_ref
        to_ref[(j // 2) * BLOCK : (j // 2 + 1) * BLOCK, :] = part_ref[:, pl.ds(at, SHARE)].astype(to_ref.dtype)
    lane = lax.broadcasted_iota(jnp.int32, (WIDTH, LANES), 1)
    column = jnp.transpose(jnp.broadcast_to(gain, (LANES, WIDTH)))
    rest = jnp.where(lane == EXPERTS + 8, column, made_ref[:, 2 * SHARE :].astype(jnp.float32))
    all_ref[:, 3 * SHARE :] = rest.astype(jnp.bfloat16)


def last_grads(rank, own, home, qgrad, normed, x, w_query, w_key, w_value, cosine, sine, made, gain):
    return run(
        last_grads_kernel,
        "last_grads",
        1,
        [smem()] + [None] * 12,
        [None] * 4,
        [
            out((WIDTH, 3 * SHARE + LANES), jnp.bfloat16),
            out((2 * BLOCK, SHARE), jnp.float32),
            out((2 * BLOCK, SHARE), jnp.bfloat16),
            out((8, BLOCK), jnp.float32),
        ],
        (rank, own, home, qgrad, normed, x, w_query, w_key, w_value, cosine, sine, made, gain),
        cost(1_000_000_000, 8_000_000, 512),
        [pltpu.VMEM((BLOCK, WIDTH), jnp.float32)],
        free=(2,),
    )


def per_device(
    hidden_in,
    lengths,
    block_order,
    routes,
    norm_gain_attn,
    w_query,
    w_key,
    w_value,
    w_out,
    norm_gain_moe,
    w_router,
    w_gate,
    w_up,
    w_down,
    out_grad,
):
    dp_count = block_order.shape[0]
    mp_rank = lax.axis_index("mp").astype(jnp.int32)
    column_start = mp_rank * SHARE
    piece = BLOCK // dp_count
    steps = MAXLEN // BLOCK - 1
    rank = mp_rank.reshape(1)
    lane = lax.axis_index("dp").astype(jnp.int32).reshape(1)
    begin = rank * QUARTER
    gain_attn = norm_gain_attn[None, :]
    gain_moe = norm_gain_moe[None, :]
    router_t = jnp.pad(w_router.T, ((0, LANES - EXPERTS), (0, 0)))

    normed, queries, key_value, cosine, sine, reach, wanted, later, live = project(
        lengths, block_order, lane, hidden_in, gain_attn, w_query, w_key, w_value
    )
    pieces = to_all(key_value.reshape(dp_count, piece, SHARE))
    picks, ranks = route(begin, after(routes.T, key_value))
    far_out = peer(after(w_out, key_value), 2)
    begun = attend_own(queries, after(key_value, picks))
    picked = pick_pieces(wanted, after(pieces, far_out))
    earlier = to_all(picked.reshape(dp_count, steps * piece, SHARE))
    earlier = earlier.reshape(dp_count, steps, piece, SHARE)

    outs = [w_out, peer(after(w_out, picked), 1), far_out, peer(far_out, 1)]

    grad_rows = jnp.dot(picks, after(out_grad, picked), preferred_element_type=jnp.bfloat16)
    grad_arrived = to_experts(after(grad_rows, earlier, begun[1]).reshape(EXPERTS, QUARTER, WIDTH))
    attended, attended_t, lse = attend(reach, begun, earlier)
    far = peer(attended, 2)
    residual, moe_cat, gates, moe_rows = residual_step(
        [attended, peer(attended, 1), far, peer(far, 1)],
        outs,
        hidden_in,
        gain_moe,
        router_t,
        ranks,
        picks,
    )
    own_pack = pack_weights(after(w_down[0], attended), w_gate[0], w_up[0])
    far_pack = peer(after(own_pack, far), 2)
    packed = [own_pack, peer(own_pack, 1), far_pack, peer(far_pack, 1)]

    grouped = to_experts(after(moe_rows, far_pack).reshape(EXPERTS, QUARTER, -1)).reshape(SLOTS, -1)
    mix = mix_weights(begin, ranks, moe_cat)
    grouped_grad = grad_arrived.reshape(SLOTS, WIDTH)
    rows_out, row_grad, hidden_units, unit_grad = expert_step(lane, grouped, grouped_grad, packed)
    row_home = to_experts(row_grad.reshape(dp_count, QUARTER, -1)).reshape(SLOTS, -1)
    unit_keep, unit_send = unit_grads(grouped, grouped_grad, hidden_units, unit_grad)
    unit_near = unit_keep.astype(jnp.float32) + peer(unit_send, 1).astype(jnp.float32)
    unit_low = unit_near[1].astype(jnp.bfloat16)
    cut = PACKED // 2
    unit_far_a = peer(unit_low[:cut], 2)
    keep, send = sum_home(rank, after(mix, unit_far_a), row_home)
    near = keep + peer(send, 1).astype(jnp.float32)
    mine = swap_sum(near, peer(near.astype(jnp.bfloat16), 2))
    theirs = peer(mine, 1)
    rows_home = to_experts(after(rows_out, theirs).reshape(dp_count, QUARTER, -1)).reshape(SLOTS, -1)
    branch_grad, logit_grad, residual_grad, attended_grad, attended_grad_t, moe_gain = norm_back_step(
        rank, mine, theirs, gates, residual, gain_moe, router_t, out_grad, w_out
    )

    query_pre_grad, own_grads, later_grads = attend_back(
        reach,
        queries,
        begun[0],
        key_value,
        earlier,
        attended_grad,
        attended_grad_t,
        attended_t,
        lse,
        cosine,
        sine,
    )
    unit_far_b = peer(after(unit_low[cut:], later_grads), 2)
    later_pieces = to_all(after(later_grads, rows_home).reshape(dp_count, steps * piece, SHARE))
    summed = sum_pieces(
        later, live, after(later_pieces, unit_far_b).reshape(dp_count * steps, piece, SHARE), dp_count
    )
    kv_home = to_all(summed).reshape(BLOCK, SHARE)
    made = dense_grads(
        branch_grad, attended, normed, query_pre_grad, logit_grad, moe_cat, moe_gain
    )

    every, keep, send, inner = last_grads(
        rank,
        own_grads,
        kv_home,
        query_pre_grad,
        normed,
        hidden_in,
        w_query,
        w_key,
        w_value,
        cosine,
        sine,
        made,
        gain_attn,
    )
    near_norm = keep + peer(send, 1).astype(jnp.float32)
    far_norm = peer(near_norm[BLOCK:].astype(jnp.bfloat16), 2)
    inner = inner[0] + peer(inner[0], 1) + peer(inner[0], 2) + peer(inner[0], 3)
    arrived = to_all(every.reshape(dp_count, WIDTH // dp_count, -1))

    keep, send = sum_home(rank, mix, after(rows_home, every))
    near_mix = keep + peer(send, 1).astype(jnp.float32)
    far_mix = peer(near_mix[BLOCK:].astype(jnp.bfloat16), 2)
    unit_far = jnp.concatenate([unit_far_a, unit_far_b], axis=0)
    grad_w_gate, grad_w_up, grad_w_down = unit_finish(unit_near[0], unit_far)

    dense = jnp.sum(arrived.astype(jnp.float32), axis=0)
    normed_grad = near_norm[:BLOCK] + after(far_norm, dense).astype(jnp.float32)
    x = hidden_in.astype(jnp.float32)
    scale = lax.rsqrt(jnp.mean(x * x, axis=-1, keepdims=True) + epsilon)
    x_cols = lax.dynamic_slice_in_dim(x, column_start, SHARE, 1)
    weighted = normed_grad * lax.dynamic_slice_in_dim(gain_attn, column_start, SHARE, 1)
    inner = inner[:, None] / WIDTH
    grad_hidden = residual_grad + scale * weighted - x_cols * (scale * scale * scale * inner)
    mixture = near_mix[:BLOCK] + after(far_mix, dense).astype(jnp.float32)
    residual_cols = lax.dynamic_slice_in_dim(residual, column_start, SHARE, 1)
    out_hidden = (residual_cols + mixture).astype(jnp.bfloat16)

    at = 3 * SHARE
    attn_gain = dense[:, at + EXPERTS + 8]
    attn_gain = attn_gain + peer(attn_gain, 1) + peer(attn_gain, 2) + peer(attn_gain, 3)
    return (
        out_hidden,
        grad_hidden,
        dense[:, SHARE : 2 * SHARE],
        dense[:, 2 * SHARE : 2 * SHARE + LANES],
        dense[:, 2 * SHARE + LANES : at],
        dense[:, :SHARE].T,
        attn_gain,
        dense[:, at + EXPERTS],
        dense[:, at : at + EXPERTS],
        grad_w_gate,
        grad_w_up,
        grad_w_down,
    )


def solution(mesh):
    in_specs = (
        P("dp", None),
        P(),
        P(),
        P("dp", None),
        P(),
        P(None, "mp"),
        P(None, "mp"),
        P(None, "mp"),
        P("mp", None),
        P(),
        P(),
        P("dp", None, "mp"),
        P("dp", None, "mp"),
        P("dp", "mp", None),
        P("dp", None),
    )
    out_specs = (
        P("dp", "mp"),
        P("dp", "mp"),
        P("dp", "mp"),
        P("dp", "mp"),
        P("dp", "mp"),
        P("mp", "dp"),
        P("dp"),
        P("dp"),
        P("dp", None),
        P("dp", None, "mp"),
        P("dp", None, "mp"),
        P("dp", "mp", None),
    )
    return jax.shard_map(
        per_device, mesh=mesh, in_specs=in_specs, out_specs=out_specs, check_vma=False
    )
```

```python
import jax
import jax.numpy as jnp
import numpy as np
from jax import lax
from jax.experimental import pallas as pl
from jax.experimental.pallas import tpu as pltpu
from jax.sharding import PartitionSpec as P

HEAD_DIM = 64
EXPERTS = 32
BLOCK = 512
MAXLEN = 2048
CAP = 160
WIDTH = 1024
SHARE = 256
QUARTER = 40
SLOTS = 1280
LANES = 128
PACKED = 384

epsilon = 1e-06
residual_mult = 0.22
score_mult = 0.015625
rope_base = 10000.0
masked_score = -1e30

NN = (((1,), (0,)), ((), ()))
NT = (((1,), (1,)), ((), ()))
TN = (((0,), (0,)), ((), ()))


def mm(a, b, dims=NN):
    return lax.dot_general(a, b, dims, preferred_element_type=jnp.float32)


def to_all(x):
    return lax.all_to_all(x, "dp", 0, 0, tiled=True)


def crossed_groups(dp_count=32):
    groups = []
    for chip in range(2):
        for core in range(2):
            groups.append([i * 4 + ((chip ^ (core & i & 1)) * 2 + core) for i in range(dp_count)])
    return groups


def to_experts(x):
    return lax.all_to_all(
        x, ("dp", "mp"), 0, 0, axis_index_groups=crossed_groups(x.shape[0]), tiled=True
    )


def peer(x, flip):
    return lax.ppermute(x, "mp", [(i, i ^ flip) for i in range(4)])


def after(x, *others):
    return lax.optimization_barrier((x, *others))[0]


def vmem():
    return pl.BlockSpec(memory_space=pltpu.VMEM)


def smem():
    return pl.BlockSpec(memory_space=pltpu.SMEM)


def tiles(rows, width, row0=0):
    return pl.BlockSpec((rows, width), lambda i: (i + row0, 0))


def fixed(rows, width):
    return pl.BlockSpec((rows, width), lambda i: (0, 0))


def once(*shape):
    return pl.BlockSpec(shape, lambda i: (0,) * len(shape), pipeline_mode=pl.Buffered(1))


def run(kernel, name, steps, in_specs, out_specs, out_shape, args, estimate, scratch=(), free=(), limit=32):
    in_specs = [once(*a.shape) if s is None else s for s, a in zip(in_specs, args)]
    out_specs = [once(*o.shape) if s is None else s for s, o in zip(out_specs, out_shape)]
    args = [
        a
        if s.memory_space is not None or i in free
        else pltpu.with_memory_space_constraint(a, pltpu.HBM)
        for i, (s, a) in enumerate(zip(in_specs, args))
    ]
    out_shape = [
        o if s.memory_space == pltpu.SMEM else pltpu.HBM(o.shape, o.dtype)
        for s, o in zip(out_specs, out_shape)
    ]
    return pl.pallas_call(
        kernel,
        name=name,
        grid=(steps,),
        in_specs=in_specs,
        out_specs=out_specs,
        out_shape=out_shape,
        scratch_shapes=list(scratch),
        compiler_params=pltpu.CompilerParams(vmem_limit_bytes=limit << 20),
        cost_estimate=estimate,
    )(*args)


def out(shape, dtype):
    return jax.ShapeDtypeStruct(shape, dtype)


def cost(flops, moved, exps=0):
    return pl.CostEstimate(flops=flops, bytes_accessed=moved, transcendentals=exps)


def rope_constants():
    frequency = rope_base ** (-(np.arange(HEAD_DIM // 2, dtype=np.float64) * 2.0) / HEAD_DIM)
    wide = np.tile(frequency, 4)[None, :]
    made = []
    for count, apart in ((BLOCK // 16, 16), (16, 1), (8, BLOCK)):
        angles = np.arange(count, dtype=np.float64)[:, None] * apart * wide
        made += [np.cos(angles), np.sin(angles)]
    return [jnp.asarray(a.astype(np.float32)) for a in made]


def half_front(rows):
    lane = lax.broadcasted_iota(jnp.int32, (rows, LANES), 1)
    return (lane % HEAD_DIM) < HEAD_DIM // 2


def turned(chunk, cosine, signed_sine, back=False):
    partner = jnp.where(
        half_front(chunk.shape[0]), pltpu.roll(chunk, 96, 1), pltpu.roll(chunk, 32, 1)
    )
    if back:
        return chunk * cosine - partner * signed_sine
    return chunk * cosine + partner * signed_sine


def block_tables_in(lengths_ref, order_ref, rank_ref, offset_ref, inverse_ref, reach_ref, wanted_ref, later_ref, live_ref):
    count = order_ref.shape[0]
    steps = MAXLEN // BLOCK - 1

    def sequence(s, begin):
        def one(j, at):
            offset_ref[jnp.minimum(at, count - 1)] = j
            return at + 1

        return lax.fori_loop(0, lengths_ref[s], one, begin)

    lax.fori_loop(0, lengths_ref.shape[0], sequence, jnp.int32(0))

    def invert(d, carry):
        inverse_ref[order_ref[d]] = d
        return carry

    lax.fori_loop(0, count, invert, jnp.int32(0))
    reach_ref[0] = offset_ref[order_ref[rank_ref[0]]]

    def look(d, carry):
        packed = order_ref[d]
        for s in range(1, steps + 1):
            wanted_ref[d * steps + s - 1] = inverse_ref[jnp.maximum(packed - s, 0)]
            next_at = jnp.minimum(packed + s, count - 1)
            later_ref[d * steps + s - 1] = inverse_ref[next_at] * steps + s - 1
            is_live = jnp.logical_and(packed + s < count, offset_ref[next_at] >= s)
            live_ref[d * steps + s - 1] = jnp.where(is_live, 1, 0)
        return carry

    lax.fori_loop(0, count, look, jnp.int32(0))


def project_kernel(
    lengths_ref, order_ref, rank_ref, x_ref, gain_ref, wk_ref, wv_ref,
    cos16_ref, sin16_ref, cos1_ref, sin1_ref, cos0_ref, sin0_ref,
    normed_ref, kv_ref, cosine_ref, sine_ref, reach_ref, wanted_ref, later_ref, live_ref,
    offset_ref, inverse_ref,
):
    @pl.when(pl.program_id(0) == 0)
    def _():
        block_tables_in(
            lengths_ref, order_ref, rank_ref, offset_ref, inverse_ref, reach_ref, wanted_ref, later_ref, live_ref
        )

    x = x_ref[...].astype(jnp.float32)
    scale = lax.rsqrt(jnp.mean(x * x, axis=1, keepdims=True) + epsilon)
    normed = (x * scale * gain_ref[...]).astype(jnp.bfloat16)
    normed_ref[...] = normed
    at = reach_ref[0]
    cos0, sin0 = cos0_ref[pl.ds(at, 1), :], sin0_ref[pl.ds(at, 1), :]
    cos16 = cos16_ref[...] * cos0 - sin16_ref[...] * sin0
    sin16 = sin16_ref[...] * cos0 + cos16_ref[...] * sin0
    cos1, sin1 = cos1_ref[...][None], sin1_ref[...][None]
    cosine = (cos16[:, None, :] * cos1 - sin16[:, None, :] * sin1).reshape(x.shape[0], LANES)
    sine = (sin16[:, None, :] * cos1 + cos16[:, None, :] * sin1).reshape(x.shape[0], LANES)
    sine = jnp.where(half_front(x.shape[0]), -sine, sine)
    cosine_ref[...] = cosine
    sine_ref[...] = sine
    kv_ref[:, :LANES] = turned(mm(normed, wk_ref[...]), cosine, sine).astype(jnp.bfloat16)
    kv_ref[:, LANES:] = mm(normed, wv_ref[...]).astype(jnp.bfloat16)


def query_kernel(normed_ref, wq_ref, cosine_ref, sine_ref, q_ref):
    queries = mm(normed_ref[...], wq_ref[...])
    for i in range(0, SHARE, LANES):
        q_ref[:, i : i + LANES] = turned(
            queries[:, i : i + LANES], cosine_ref[...], sine_ref[...]
        ).astype(jnp.bfloat16)


def project_queries(normed, w_query, cosine, sine):
    tile = 256
    return run(
        query_kernel,
        "project_queries",
        BLOCK // tile,
        [tiles(tile, WIDTH), None, tiles(tile, LANES), tiles(tile, LANES)],
        [tiles(tile, SHARE)],
        [out((BLOCK, SHARE), jnp.bfloat16)],
        (normed, w_query, cosine, sine),
        cost(270_000_000, 2_500_000),
    )[0]


def project(lengths, order, rank, x, gain, w_key, w_value):
    tile = 256
    count = order.shape[0]
    steps = MAXLEN // BLOCK - 1
    bf16, f32 = jnp.bfloat16, jnp.float32
    return run(
        project_kernel,
        "project",
        BLOCK // tile,
        [smem()] * 3
        + [tiles(tile, WIDTH), None, None, None]
        + [tiles(tile // 16, LANES)] * 2
        + [None] * 4,
        [tiles(tile, WIDTH), tiles(tile, SHARE)] + [tiles(tile, LANES)] * 2 + [smem()] * 4,
        [out((BLOCK, WIDTH), bf16), out((BLOCK, SHARE), bf16)]
        + [out((BLOCK, LANES), f32)] * 2
        + [out((1,), jnp.int32)]
        + [out((count * steps,), jnp.int32)] * 3,
        (lengths, order, rank, x, gain, w_key, w_value, *rope_constants()),
        cost(540_000_000, 4_000_000, 512),
        [pltpu.SMEM((count,), jnp.int32), pltpu.SMEM((count,), jnp.int32)],
    )


def pick_kernel(wanted_ref, pieces_ref, picked_ref):
    def one(i, carry):
        picked_ref[i] = pieces_ref[wanted_ref[i]]
        return carry

    lax.fori_loop(0, picked_ref.shape[0], one, jnp.int32(0), unroll=4)


def pick_pieces(wanted, pieces):
    shape = out((wanted.shape[0], *pieces.shape[1:]), pieces.dtype)
    return run(
        pick_kernel, "pick_pieces", 1, [smem(), None], [None], [shape], (wanted, pieces), cost(0, 1_100_000), free=(1,)
    )[0]


def sum_kernel(later_ref, live_ref, pieces_ref, sum_ref):
    steps = MAXLEN // BLOCK - 1

    def one(d, carry):
        total = jnp.zeros(sum_ref.shape[1:], jnp.float32)
        for s in range(steps):
            part = pieces_ref[later_ref[d * steps + s]].astype(jnp.float32)
            total = total + jnp.where(live_ref[d * steps + s] == 1, part, 0.0)
        sum_ref[d] = total.astype(sum_ref.dtype)
        return carry

    lax.fori_loop(0, sum_ref.shape[0], one, jnp.int32(0), unroll=2)


def sum_pieces(later, live, pieces, count):
    shape = out((count, *pieces.shape[1:]), pieces.dtype)
    return run(
        sum_kernel,
        "sum_pieces",
        1,
        [smem(), smem(), None],
        [None],
        [shape],
        (later, live, pieces),
        cost(0, 1_100_000),
        free=(2,),
    )[0]


def pack_kernel(down_ref, gate_ref, up_ref, packed_ref):
    packed_ref[:LANES, :] = down_ref[...]
    for k in range(4):
        rows = slice(k * SHARE, (k + 1) * SHARE)
        packed_ref[LANES:, k * SHARE : k * SHARE + LANES] = gate_ref[rows, :]
        packed_ref[LANES:, k * SHARE + LANES : (k + 1) * SHARE] = up_ref[rows, :]


def pack_weights(w_down, w_gate, w_up):
    shape = out((PACKED, WIDTH), jnp.bfloat16)
    return run(
        pack_kernel, "pack_weights", 1, [None] * 3, [None], [shape], (w_down, w_gate, w_up), cost(0, 1_600_000)
    )[0]


def route_kernel(begin_ref, routes_ref, picks_ref, ranks_ref):
    tokens = routes_ref.shape[1]
    expert_at = lax.broadcasted_iota(jnp.int32, (LANES, tokens), 0)
    hits = jnp.zeros((LANES, tokens), jnp.float32)
    for k in range(routes_ref.shape[0]):
        hits = hits + jnp.where(routes_ref[k : k + 1, :] == expert_at, 1.0, 0.0)
    row_at = lax.broadcasted_iota(jnp.int32, (tokens, tokens), 0)
    column_at = lax.broadcasted_iota(jnp.int32, (tokens, tokens), 1)
    before = jnp.where(row_at < column_at, 1.0, 0.0).astype(jnp.bfloat16)
    ranks = jnp.where(hits > 0.5, mm(hits.astype(jnp.bfloat16), before), -1.0)
    ranks_ref[...] = ranks
    slot_at = lax.broadcasted_iota(jnp.int32, (QUARTER, tokens), 0) + begin_ref[0]
    slot_at = slot_at.astype(jnp.float32)
    for e in range(EXPERTS):
        picks_ref[e * QUARTER : (e + 1) * QUARTER, :] = jnp.where(
            ranks[e : e + 1, :] == slot_at, 1.0, 0.0
        ).astype(jnp.bfloat16)


def route(begin, routes_t):
    return run(
        route_kernel,
        "route",
        1,
        [smem(), None],
        [None, None],
        [out((SLOTS, BLOCK), jnp.bfloat16), out((LANES, BLOCK), jnp.float32)],
        (begin, routes_t),
        cost(100_000_000, 1_600_000),
        free=(1,),
    )


def padded_columns(rows_t, out_ref):
    zero = jnp.zeros((HEAD_DIM, rows_t.shape[1]), out_ref.dtype)
    for h in range(4):
        mine = rows_t[h * HEAD_DIM : (h + 1) * HEAD_DIM].astype(out_ref.dtype)
        at = (h // 2) * HEAD_DIM
        out_ref[h, pl.ds(at, HEAD_DIM), :] = mine
        out_ref[h, pl.ds(HEAD_DIM - at, HEAD_DIM), :] = zero


def padded_rows(rows, out_ref):
    n = rows.shape[0]
    lane = lax.broadcasted_iota(jnp.int32, (n, 128), 1)
    for h in range(4):
        pair = rows[:, (h // 2) * 128 : (h // 2) * 128 + 128].astype(jnp.float32)
        if h % 2 != h // 2:
            pair = pltpu.roll(pair, HEAD_DIM, 1)
        own = (lane < HEAD_DIM) if h // 2 == 0 else (lane >= HEAD_DIM)
        out_ref[pl.ds(h * n, n), :] = jnp.where(own, pair, 0.0).astype(out_ref.dtype)


def attend_block(key_rows, value_rows, first, qpad_ref, max_ref, sum_ref, out_t_ref):
    half = BLOCK // 2
    for h in range(4):
        group = (h // 2) * HEAD_DIM
        for t in range(2):
            cols = slice(t * half, (t + 1) * half)
            rows = half if first and t == 0 else BLOCK
            scores = mm(key_rows[:rows], qpad_ref[h, :, cols])
            if first:
                key_at = lax.broadcasted_iota(jnp.int32, scores.shape, 0)
                query_at = lax.broadcasted_iota(jnp.int32, scores.shape, 1) + t * half
                scores = jnp.where(key_at > query_at, masked_score, scores)
            new_max = jnp.max(scores, axis=0, keepdims=True)
            if not first:
                old_max = max_ref[h : h + 1, cols]
                new_max = jnp.maximum(new_max, old_max)
                shrink = jnp.exp(old_max - new_max)
            weights = jnp.exp(scores - new_max)
            total = jnp.sum(weights, axis=0, keepdims=True)
            part = mm(value_rows[:rows], weights.astype(jnp.bfloat16), TN)[group : group + HEAD_DIM]
            mine = pl.ds(h * HEAD_DIM, HEAD_DIM)
            if not first:
                total = total + sum_ref[h : h + 1, cols] * shrink
                part = part + out_t_ref[mine, cols] * shrink
            max_ref[h : h + 1, cols] = new_max
            sum_ref[h : h + 1, cols] = total
            out_t_ref[mine, cols] = part


def attend_own_kernel(q_ref, own_ref, qpad_ref, max_ref, sum_ref, out_t_ref):
    padded_columns(jnp.transpose(q_ref[...].astype(jnp.float32) * score_mult), qpad_ref)
    max_ref[...] = jnp.zeros_like(max_ref)
    sum_ref[...] = jnp.ones_like(sum_ref)
    attend_block(own_ref[:, :LANES], own_ref[:, LANES:], True, qpad_ref, max_ref, sum_ref, out_t_ref)


def attend_own(queries, own_kv):
    return pl.pallas_call(
        attend_own_kernel,
        name="attend_own",
        in_specs=[vmem()] * 2,
        out_specs=[vmem()] * 4,
        out_shape=[
            out((4, LANES, BLOCK), jnp.bfloat16),
            out((8, BLOCK), jnp.float32),
            out((8, BLOCK), jnp.float32),
            out((SHARE, BLOCK), jnp.float32),
        ],
        compiler_params=pltpu.CompilerParams(vmem_limit_bytes=36 << 20),
        cost_estimate=cost(1_000_000_000, 2_000_000, 600_000),
    )(queries, own_kv)


def attend_kernel(
    reach_ref, qpad_ref, max0_ref, sum0_ref, out0_ref, prev_ref, att_ref, out_t_ref, lse_ref, max_ref, sum_ref
):
    max_ref[...] = max0_ref[...]
    sum_ref[...] = sum0_ref[...]
    out_t_ref[...] = out0_ref[...]

    @pl.loop(1, reach_ref[0] + 1)
    def _(step):
        rows = prev_ref[:, pl.ds(step - 1, 1)].reshape(BLOCK, SHARE)
        attend_block(rows[:, :LANES], rows[:, LANES:], False, qpad_ref, max_ref, sum_ref, out_t_ref)

    lse_ref[...] = max_ref[...] + jnp.log(sum_ref[...])
    for h in range(4):
        mine = pl.ds(h * HEAD_DIM, HEAD_DIM)
        out_t_ref[mine, :] = out_t_ref[mine, :] / sum_ref[h : h + 1, :]
    att_ref[...] = jnp.transpose(out_t_ref[...]).astype(jnp.bfloat16)


def attend(reach, begun, earlier):
    return run(
        attend_kernel,
        "attend",
        1,
        [smem()] + [vmem()] * 5,
        [None] * 3,
        [
            out((BLOCK, SHARE), jnp.bfloat16),
            out((SHARE, BLOCK), jnp.float32),
            out((8, BLOCK), jnp.float32),
        ],
        (reach, *begun, earlier),
        cost(4_000_000_000, 3_000_000, 3_000_000),
        [pltpu.VMEM((8, BLOCK), jnp.float32), pltpu.VMEM((8, BLOCK), jnp.float32)],
        limit=36,
    )


def attend_back_kernel(
    reach_ref, q_ref, qpad_ref, own_ref, prev_ref, grad_ref, grad_t_ref, out_t_ref, lse_ref, cos_ref, sin_ref,
    qgrad_ref, own_grad_ref, prev_grad_ref,
    gpad_ref, qrows_ref, grows_ref, ds_ref, p_ref, delta_ref, dq_ref,
):
    half = BLOCK // 2
    q_scaled = q_ref[...].astype(jnp.float32) * score_mult
    padded_rows(q_scaled, qrows_ref)
    padded_columns(grad_t_ref[...], gpad_ref)
    padded_rows(grad_ref[...], grows_ref)
    both = grad_t_ref[...].astype(jnp.float32) * out_t_ref[...]
    for h in range(4):
        delta_ref[h : h + 1, :] = jnp.sum(
            both[h * HEAD_DIM : (h + 1) * HEAD_DIM], axis=0, keepdims=True
        )


    def block(key_rows, value_rows, first):
        for h in range(4):
            for t in range(2):
                cols = slice(t * half, (t + 1) * half)
                wide = slice(h * BLOCK + t * half, h * BLOCK + (t + 1) * half)
                rows = half if first and t == 0 else BLOCK
                scores = mm(key_rows[:rows], qpad_ref[h, :, cols])
                weights = jnp.exp(scores - lse_ref[h : h + 1, cols])
                if first:
                    key_at = lax.broadcasted_iota(jnp.int32, scores.shape, 0)
                    query_at = lax.broadcasted_iota(jnp.int32, scores.shape, 1) + t * half
                    weights = jnp.where(key_at > query_at, 0.0, weights)
                weight_grad = mm(value_rows[:rows], gpad_ref[h, :, cols])
                score_grad = weights * (weight_grad - delta_ref[h : h + 1, cols])
                p_ref[:rows, wide] = weights.astype(jnp.bfloat16)
                ds_ref[:rows, wide] = score_grad.astype(jnp.bfloat16)
                if rows < BLOCK:
                    p_ref[rows:, wide] = jnp.zeros((BLOCK - rows, half), jnp.bfloat16)
                    ds_ref[rows:, wide] = jnp.zeros((BLOCK - rows, half), jnp.bfloat16)
        key_grad = mm(ds_ref[...], qrows_ref[...])
        value_grad = mm(p_ref[...], grows_ref[...])
        for h in range(4):
            group = (h // 2) * HEAD_DIM
            mine = pl.ds(h * HEAD_DIM, HEAD_DIM)
            part = mm(key_rows, ds_ref[:, h * BLOCK : (h + 1) * BLOCK], TN)[group : group + HEAD_DIM]
            dq_ref[mine, :] = part if first else dq_ref[mine, :] + part
        return key_grad, value_grad

    key_grad, value_grad = block(own_ref[:, :LANES], own_ref[:, LANES:], True)
    own_grad_ref[:, :LANES] = key_grad
    own_grad_ref[:, LANES:] = value_grad

    @pl.loop(1, reach_ref[0] + 1)
    def _(step):
        rows = prev_ref[:, pl.ds(step - 1, 1)].reshape(BLOCK, SHARE)
        key_grad, value_grad = block(rows[:, :LANES], rows[:, LANES:], False)
        parts = prev_grad_ref.shape[0]
        shape = (parts, 1, BLOCK // parts, LANES)
        prev_grad_ref[:, pl.ds(step - 1, 1), :, :LANES] = key_grad.astype(jnp.bfloat16).reshape(shape)
        prev_grad_ref[:, pl.ds(step - 1, 1), :, LANES:] = value_grad.astype(jnp.bfloat16).reshape(shape)

    query_grad = jnp.transpose(dq_ref[...]) * score_mult
    for i in range(0, SHARE, LANES):
        qgrad_ref[:, i : i + LANES] = turned(
            query_grad[:, i : i + LANES], cos_ref[...], sin_ref[...], back=True
        ).astype(jnp.bfloat16)


def attend_back(reach, queries, padded, own_kv, earlier, grad, grad_t, out_t, lse, cosine, signed_sine):
    return run(
        attend_back_kernel,
        "attend_back",
        1,
        [smem()] + [vmem()] * 10,
        [None] * 3,
        [
            out((BLOCK, SHARE), jnp.bfloat16),
            out((BLOCK, SHARE), jnp.float32),
            out(earlier.shape, jnp.bfloat16),
        ],
        (reach, queries, padded, own_kv, earlier, grad, grad_t, out_t, lse, cosine, signed_sine),
        cost(12_000_000_000, 5_000_000, 3_000_000),
        [
            pltpu.VMEM((4, LANES, BLOCK), jnp.bfloat16),
            pltpu.VMEM((4 * BLOCK, LANES), jnp.bfloat16),
            pltpu.VMEM((4 * BLOCK, LANES), jnp.bfloat16),
            pltpu.VMEM((BLOCK, 4 * BLOCK), jnp.bfloat16),
            pltpu.VMEM((BLOCK, 4 * BLOCK), jnp.bfloat16),
            pltpu.VMEM((8, BLOCK), jnp.float32),
            pltpu.VMEM((SHARE, BLOCK), jnp.float32),
        ],
        limit=36,
    )


def residual_kernel(
    a0, a1, a2, a3, w0, w1, w2, w3, x_ref, gain_ref, router_ref, ranks_ref, picks_ref,
    residual_ref, moe_ref, gates_ref, rows_ref, held_ref,
):
    step = pl.program_id(0)
    tile = x_ref.shape[0]

    @pl.when(step < BLOCK // tile)
    def _():
        branch = mm(a0[...], w0[...])
        for a, w in ((a1, w1), (a2, w2), (a3, w3)):
            branch = branch + mm(a[...], w[...])
        residual = x_ref[...].astype(jnp.float32) + residual_mult * branch
        residual_ref[...] = residual
        scale = lax.rsqrt(jnp.mean(residual * residual, axis=1, keepdims=True) + epsilon)
        moe_in = (residual * scale * gain_ref[...]).astype(jnp.bfloat16)
        moe_ref[:, :WIDTH] = moe_in
        logits = mm(router_ref[...], moe_in, NT)
        chosen = ranks_ref[...] >= 0.0
        kept = jnp.where(chosen, logits, masked_score)
        top = jnp.max(kept, axis=0, keepdims=True)
        raised = jnp.where(chosen, jnp.exp(kept - top), 0.0)
        gates = raised / jnp.sum(raised, axis=0, keepdims=True)
        gates_ref[...] = gates
        low = (residual_mult * jnp.transpose(gates)).astype(jnp.bfloat16)
        moe_ref[:, WIDTH:] = low
        held_ref[pl.ds(step * tile, tile), :WIDTH] = moe_in
        held_ref[pl.ds(step * tile, tile), WIDTH:] = low

    @pl.when(step >= BLOCK // tile)
    def _():
        rows_ref[...] = mm(picks_ref[...], held_ref[...]).astype(jnp.bfloat16)


def residual_step(attended, w_out, x, gain, router_t, ranks, picks):
    tile = 256
    first = BLOCK // tile
    slot_tile = SLOTS // 4

    def early(rows, width):
        return pl.BlockSpec((rows, width), lambda i: (jnp.minimum(i, first - 1), 0))

    def late(rows, width):
        return pl.BlockSpec((rows, width), lambda i: (jnp.maximum(i - first, 0), 0))

    by_columns = pl.BlockSpec((LANES, tile), lambda i: (0, jnp.minimum(i, first - 1)))
    return run(
        residual_kernel,
        "residual_step",
        first + 4,
        [early(tile, SHARE)] * 4
        + [None] * 4
        + [early(tile, WIDTH), None, None, by_columns, late(slot_tile, BLOCK)],
        [early(tile, WIDTH), early(tile, WIDTH + LANES), by_columns, late(slot_tile, WIDTH + LANES)],
        [
            out((BLOCK, WIDTH), jnp.float32),
            out((BLOCK, WIDTH + LANES), jnp.bfloat16),
            out((LANES, BLOCK), jnp.float32),
            out((SLOTS, WIDTH + LANES), jnp.bfloat16),
        ],
        (*attended, *w_out, x, gain, router_t, ranks, picks),
        cost(2_700_000_000, 12_000_000, 70_000),
        [pltpu.VMEM((BLOCK, WIDTH + LANES), jnp.bfloat16)],
        free=(1, 2, 3, 5, 6, 7, 10),
    )


def mix_kernel(begin_ref, ranks_ref, moe_ref, mix_ref):
    ranks = jnp.transpose(ranks_ref[...]).astype(jnp.bfloat16)
    gates = moe_ref[:, WIDTH:]
    width = 640
    for at in range(0, SLOTS, width):
        expert_at = lax.broadcasted_iota(jnp.int32, (LANES, width), 0)
        first = expert_at * QUARTER - at
        slot_at = lax.broadcasted_iota(jnp.int32, (LANES, width), 1)
        inside = jnp.logical_and(slot_at >= first, slot_at < first + QUARTER)
        spread = jnp.where(inside, 1.0, 0.0).astype(jnp.bfloat16)
        within = jnp.sum(jnp.where(inside, slot_at - first, 0), axis=0, keepdims=True) + begin_ref[0]
        hit = mm(ranks, spread) == within.astype(jnp.float32)
        mix_ref[:, at : at + width] = jnp.where(hit, mm(gates, spread), 0.0).astype(jnp.bfloat16)


def mix_weights(begin, ranks, moe_cat):
    return run(
        mix_kernel,
        "mix_weights",
        1,
        [smem(), None, None],
        [None],
        [out((BLOCK, SLOTS), jnp.bfloat16)],
        (begin, ranks, moe_cat),
        cost(350_000_000, 3_000_000),
    )[0]


def expert_kernel(
    lane_ref, x_ref, grad_ref, p0, p1, p2, p3,
    out_ref, row_ref, hidden_ref, units_ref,
):
    packed = (p0, p1, p2, p3)
    rows = out_ref.shape[0]
    here = pl.ds(pl.program_id(0) * rows, rows)
    lane = lax.broadcasted_iota(jnp.int32, (rows, LANES), 1) == lane_ref[0]
    gate = jnp.sum(
        jnp.where(lane, x_ref[here, WIDTH:].astype(jnp.float32), 0.0), axis=1, keepdims=True
    )
    x = x_ref[here, :WIDTH]
    grad = grad_ref[...]
    gates, ups, sigmoids, hidden = [], [], [], []
    for p in packed:
        pre = None
        for k in range(4):
            columns = slice(k * SHARE, (k + 1) * SHARE)
            term = mm(x[:, columns], p[LANES:, columns])
            pre = term if pre is None else pre + term
        gate_pre, up_pre = pre[:, :LANES], pre[:, LANES:]
        sigmoid = 1.0 / (1.0 + jnp.exp(-gate_pre))
        gates.append(gate_pre)
        ups.append(up_pre)
        sigmoids.append(sigmoid)
        hidden.append(gate_pre * sigmoid * up_pre)
    hidden_low = jnp.concatenate([h.astype(jnp.bfloat16) for h in hidden], axis=1)
    down = jnp.concatenate([p[:LANES, :] for p in packed], axis=0)
    made = mm(hidden_low, down).astype(jnp.bfloat16)
    out_ref[...] = made
    gate_grad = jnp.sum(grad.astype(jnp.float32) * made.astype(jnp.float32), axis=1, keepdims=True)
    row_ref[:, WIDTH:] = jnp.where(lane, gate_grad, 0.0).astype(jnp.bfloat16)
    hidden_grad = mm(grad, down, NT)
    row = None
    for j, p in enumerate(packed):
        part = hidden_grad[:, j * LANES : (j + 1) * LANES]
        silu = gates[j] * sigmoids[j]
        gate_pre_grad = part * ups[j] * sigmoids[j] * (1.0 + gates[j] * (1.0 - sigmoids[j]))
        up_pre_grad = part * silu
        hidden_ref[:, j * LANES : (j + 1) * LANES] = (hidden[j] * gate).astype(jnp.bfloat16)
        units_ref[:, j * SHARE : j * SHARE + LANES] = (gate_pre_grad * gate).astype(jnp.bfloat16)
        units_ref[:, j * SHARE + LANES : (j + 1) * SHARE] = (up_pre_grad * gate).astype(jnp.bfloat16)
        both = jnp.concatenate([gate_pre_grad, up_pre_grad], axis=1).astype(jnp.bfloat16)
        terms = [
            mm(both, p[LANES:, k * SHARE : (k + 1) * SHARE], NT) for k in range(4)
        ]
        row = terms if row is None else [a + b for a, b in zip(row, terms)]
    for k in range(4):
        row_ref[:, k * SHARE : (k + 1) * SHARE] = row[k].astype(jnp.bfloat16)


def expert_step(lane, x, grad, packed):
    tile = 320
    return run(
        expert_kernel,
        "expert_step",
        SLOTS // tile,
        [smem(), vmem(), tiles(tile, WIDTH)] + [None] * 4,
        [tiles(tile, WIDTH), tiles(tile, WIDTH + LANES), tiles(tile, 512), tiles(tile, WIDTH)],
        [
            out((SLOTS, WIDTH), jnp.bfloat16),
            out((SLOTS, WIDTH + LANES), jnp.bfloat16),
            out((SLOTS, 512), jnp.bfloat16),
            out((SLOTS, WIDTH), jnp.bfloat16),
        ],
        (lane, x, grad, *packed),
        cost(8_000_000_000, 18_000_000, 700_000),
        limit=40,
    )


def unit_grads_kernel(x_ref, grad_ref, hidden_ref, units_ref, keep_ref, send_ref, turned_ref):
    step = pl.program_id(0)

    @pl.when(step == 0)
    def _():
        for k in range(4):
            columns = slice(k * SHARE, (k + 1) * SHARE)
            turned_ref[columns, :] = jnp.transpose(x_ref[:, columns])

    def write(to_ref):
        to_ref[0, :LANES, :] = mm(hidden_ref[...], grad_ref[...], TN).astype(jnp.bfloat16)
        for k in range(4):
            columns = slice(k * SHARE, (k + 1) * SHARE)
            to_ref[0, LANES:, columns] = mm(turned_ref[columns, :], units_ref[...]).astype(jnp.bfloat16)

    @pl.when(step < 2)
    def _():
        write(keep_ref)

    @pl.when(step >= 2)
    def _():
        write(send_ref)


def unit_grads(x, grad, hidden, units):
    rows = SHARE + LANES

    def share_of(i):
        return jnp.where(i < 2, 2 * i, 2 * i - 3)

    return run(
        unit_grads_kernel,
        "unit_grads",
        4,
        [
            vmem(),
            None,
            pl.BlockSpec((SLOTS, LANES), lambda i: (0, share_of(i))),
            pl.BlockSpec((SLOTS, SHARE), lambda i: (0, share_of(i))),
        ],
        [
            pl.BlockSpec((1, rows, WIDTH), lambda i: (jnp.minimum(i, 1), 0, 0)),
            pl.BlockSpec((1, rows, WIDTH), lambda i: (jnp.maximum(i - 2, 0), 0, 0)),
        ],
        [out((2, rows, WIDTH), jnp.bfloat16), out((2, rows, WIDTH), jnp.bfloat16)],
        (x, grad, hidden, units),
        cost(4_000_000_000, 12_000_000),
        [pltpu.VMEM((WIDTH, SLOTS), jnp.bfloat16)],
        limit=36,
    )


def unit_finish_kernel(mine_ref, first_ref, second_ref, gate_ref, up_ref, down_ref):
    got = jnp.concatenate([first_ref[...], second_ref[...]], axis=0)
    total = mine_ref[0] + got.astype(jnp.float32)
    down_ref[0] = total[:LANES, :]
    for k in range(4):
        rows = slice(k * SHARE, (k + 1) * SHARE)
        gate_ref[0, rows, :] = total[LANES:, k * SHARE : k * SHARE + LANES]
        up_ref[0, rows, :] = total[LANES:, k * SHARE + LANES : (k + 1) * SHARE]


def unit_finish(mine, first, second):
    return run(
        unit_finish_kernel,
        "unit_finish",
        1,
        [once(1, PACKED, WIDTH), None, None],
        [None] * 3,
        [
            out((1, WIDTH, LANES), jnp.float32),
            out((1, WIDTH, LANES), jnp.float32),
            out((1, LANES, WIDTH), jnp.float32),
        ],
        (mine, first, second),
        cost(1_000_000, 3_000_000),
        free=(0, 1, 2),
    )


def home_kernel(rank_ref, mix_ref, rows_ref, keep_ref, send_ref):
    rank = rank_ref[0]
    extra = rows_ref.shape[1] > WIDTH
    for j in range(4):
        at = pl.multiple_of(jnp.bitwise_xor(rank, j) * SHARE, SHARE)
        total = mm(mix_ref[...], rows_ref[:, pl.ds(at, SHARE)])
        to_ref = send_ref if j % 2 else keep_ref
        to_ref[(j // 2) * BLOCK : (j // 2 + 1) * BLOCK, :] = total.astype(to_ref.dtype)
    if extra:
        gate_grads = jnp.transpose(mm(mix_ref[...], rows_ref[:, WIDTH:]))[:EXPERTS]
        for to_ref in (keep_ref, send_ref):
            for i in range(2):
                at = 2 * BLOCK + i * EXPERTS
                to_ref[at : at + EXPERTS, :] = gate_grads[:, i * SHARE : (i + 1) * SHARE].astype(
                    to_ref.dtype
                )


def sum_home(rank, mix, rows):
    height = 2 * BLOCK + (2 * EXPERTS if rows.shape[1] > WIDTH else 0)
    return run(
        home_kernel,
        "sum_home",
        1,
        [smem(), None, vmem()],
        [None] * 2,
        [out((height, SHARE), jnp.float32), out((height, SHARE), jnp.bfloat16)],
        (rank, mix, rows),
        cost(1_500_000_000, 6_000_000),
        limit=36,
    )


def swap_kernel(mine_ref, got_ref, total_ref):
    mine, got = mine_ref, got_ref
    half = BLOCK
    total_ref[:half] = (mine[:half] + got[half : 2 * half].astype(jnp.float32)).astype(total_ref.dtype)
    total_ref[half : 2 * half] = (
        mine[half : 2 * half] + got[:half].astype(jnp.float32)
    ).astype(total_ref.dtype)
    total_ref[2 * half :] = (mine[2 * half :] + got[2 * half :].astype(jnp.float32)).astype(
        total_ref.dtype
    )


def swap_sum(mine, got):
    return run(
        swap_kernel,
        "swap_sum",
        1,
        [None] * 2,
        [None],
        [out(mine.shape, jnp.bfloat16)],
        (mine, got),
        cost(1_000_000, 2_500_000),
        free=(0, 1),
    )[0]


def norm_back_kernel(
    rank_ref, g0, g2, g1, g3, z_ref, gates_ref, residual_ref, gain_ref, router_ref, grad_ref, w_ref,
    low_ref, logit_ref, own_ref, att_ref, att_t_ref, gain_grad_ref, u_ref,
):
    rank = rank_ref[0]
    for flip, part in enumerate((g0, g1, g2, g3)):
        at = pl.multiple_of(jnp.bitwise_xor(rank, flip) * SHARE, SHARE)
        u_ref[:, pl.ds(at, SHARE)] = part[...].astype(jnp.float32)
    weighted_grads = z_ref[...].astype(jnp.float32)
    gates = gates_ref[:EXPERTS, :]
    inner = jnp.sum(weighted_grads, axis=0, keepdims=True)
    logit_grad = (weighted_grads - gates * inner).astype(jnp.bfloat16)
    logit_ref[...] = logit_grad
    u = u_ref[...] + mm(logit_grad, router_ref[:EXPERTS, :], TN)
    v = residual_ref[...]
    scale = lax.rsqrt(jnp.mean(v * v, axis=1, keepdims=True) + epsilon)
    weighted = u * gain_ref[...]
    mean = jnp.mean(weighted * v, axis=1, keepdims=True)
    total = grad_ref[...].astype(jnp.float32) + scale * weighted - v * (scale * scale * scale * mean)

    @pl.when(pl.program_id(0) == 0)
    def _():
        gain_grad_ref[...] = jnp.zeros_like(gain_grad_ref)

    gain_grad_ref[0:1, :] += jnp.sum(u * v * scale, axis=0, keepdims=True)
    low = (residual_mult * total).astype(jnp.bfloat16)
    low_ref[...] = low
    u_ref[...] = total
    own_ref[...] = u_ref[:, pl.ds(pl.multiple_of(rank * SHARE, SHARE), SHARE)]
    att_ref[...] = mm(low, w_ref[...], NT).astype(jnp.bfloat16)
    att_t_ref[...] = mm(w_ref[...], low, NT).astype(jnp.bfloat16)


def norm_back_step(rank, mine, theirs, gates, residual, gain, router_t, out_grad, w_out):
    tile = 256
    by_columns = pl.BlockSpec((EXPERTS, tile), lambda i: (0, i))
    return run(
        norm_back_kernel,
        "norm_back_step",
        BLOCK // tile,
        [smem()]
        + [tiles(tile, SHARE), tiles(tile, SHARE, BLOCK // tile)] * 2
        + [
            tiles(EXPERTS, SHARE, 2 * BLOCK // EXPERTS),
            pl.BlockSpec((LANES, tile), lambda i: (0, i)),
            tiles(tile, WIDTH),
            None,
            None,
            tiles(tile, WIDTH),
            None,
        ],
        [
            tiles(tile, WIDTH),
            by_columns,
            tiles(tile, SHARE),
            tiles(tile, SHARE),
            pl.BlockSpec((SHARE, tile), lambda i: (0, i)),
            fixed(8, WIDTH),
        ],
        [
            out((BLOCK, WIDTH), jnp.bfloat16),
            out((EXPERTS, BLOCK), jnp.bfloat16),
            out((BLOCK, SHARE), jnp.float32),
            out((BLOCK, SHARE), jnp.bfloat16),
            out((SHARE, BLOCK), jnp.bfloat16),
            out((8, WIDTH), jnp.float32),
        ],
        (rank, mine, mine, theirs, theirs, mine, gates, residual, gain, router_t, out_grad, w_out),
        cost(700_000_000, 9_000_000, 512),
        [pltpu.VMEM((tile, WIDTH), jnp.float32)],
        free=(3, 4, 9),
    )


def dense_grads_kernel(low_ref, attended_ref, normed_ref, qgrad_ref, logit_ref, moe_ref, gain_ref, made_ref):
    made_ref[:, :SHARE] = mm(low_ref[...], attended_ref[...], TN).astype(jnp.bfloat16)
    made_ref[:, SHARE : 2 * SHARE] = mm(normed_ref[...], qgrad_ref[...], TN).astype(jnp.bfloat16)
    router = mm(logit_ref[...], moe_ref[:, :WIDTH])
    stacked = jnp.concatenate(
        [router, gain_ref[...], jnp.zeros((LANES - EXPERTS - 8, WIDTH), jnp.float32)], axis=0
    )
    made_ref[:, 2 * SHARE :] = jnp.transpose(stacked).astype(jnp.bfloat16)


def dense_grads(low, attended, normed, qgrad, logit, moe_cat, gain_grad):
    return run(
        dense_grads_kernel,
        "dense_grads",
        1,
        [None] * 7,
        [None],
        [out((WIDTH, 2 * SHARE + LANES), jnp.bfloat16)],
        (low, attended, normed, qgrad, logit, moe_cat, gain_grad),
        cost(600_000_000, 6_000_000),
    )[0]


def last_grads_kernel(
    rank_ref, own_ref, home_ref, qgrad_ref, normed_ref, x_ref, wq_ref, wk_ref, wv_ref, cos_ref, sin_ref, made_ref,
    gain_ref, all_ref, keep_ref, send_ref, inner_ref, part_ref,
):
    rank = rank_ref[0]
    kv = own_ref[...] + home_ref[...].astype(jnp.float32)
    key_grad = turned(kv[:, :LANES], cos_ref[...], sin_ref[...], back=True).astype(jnp.bfloat16)
    value_grad = kv[:, LANES:].astype(jnp.bfloat16)
    both = jnp.concatenate([key_grad, value_grad], axis=1)
    all_ref[:, : 2 * SHARE] = made_ref[:, : 2 * SHARE]
    all_ref[:, 2 * SHARE : 3 * SHARE] = mm(normed_ref[...], both, TN).astype(jnp.bfloat16)
    gain = jnp.zeros((1, WIDTH), jnp.float32)
    tile = 128
    for i in range(0, BLOCK, tile):
        rows = slice(i, i + tile)
        part = mm(qgrad_ref[rows, :], wq_ref[...], NT)
        part = part + mm(key_grad[rows], wk_ref[...], NT) + mm(value_grad[rows], wv_ref[...], NT)
        x = x_ref[rows, :].astype(jnp.float32)
        scale = lax.rsqrt(jnp.mean(x * x, axis=1, keepdims=True) + epsilon)
        along = part * x
        gain = gain + jnp.sum(along * scale, axis=0, keepdims=True)
        inner = jnp.sum(along * gain_ref[...], axis=1, keepdims=True)
        inner_ref[:, rows] = jnp.transpose(jnp.broadcast_to(inner, (tile, LANES)))[:8]
        part_ref[rows, :] = part
    for j in range(4):
        at = pl.multiple_of(jnp.bitwise_xor(rank, j) * SHARE, SHARE)
        to_ref = send_ref if j % 2 else keep_ref
        to_ref[(j // 2) * BLOCK : (j // 2 + 1) * BLOCK, :] = part_ref[:, pl.ds(at, SHARE)].astype(to_ref.dtype)
    lane = lax.broadcasted_iota(jnp.int32, (WIDTH, LANES), 1)
    column = jnp.transpose(jnp.broadcast_to(gain, (LANES, WIDTH)))
    rest = jnp.where(lane == EXPERTS + 8, column, made_ref[:, 2 * SHARE :].astype(jnp.float32))
    all_ref[:, 3 * SHARE :] = rest.astype(jnp.bfloat16)


def last_grads(rank, own, home, qgrad, normed, x, w_query, w_key, w_value, cosine, sine, made, gain):
    return run(
        last_grads_kernel,
        "last_grads",
        1,
        [smem()] + [None] * 12,
        [None] * 4,
        [
            out((WIDTH, 3 * SHARE + LANES), jnp.bfloat16),
            out((2 * BLOCK, SHARE), jnp.float32),
            out((2 * BLOCK, SHARE), jnp.bfloat16),
            out((8, BLOCK), jnp.float32),
        ],
        (rank, own, home, qgrad, normed, x, w_query, w_key, w_value, cosine, sine, made, gain),
        cost(1_000_000_000, 8_000_000, 512),
        [pltpu.VMEM((BLOCK, WIDTH), jnp.float32)],
        free=(2,),
    )


def input_finish_kernel(
    rank_ref, near_ref, far_ref, i0, i1, i2, i3, x_ref, gain_ref, residual_ref, made_ref
):
    mine = pl.ds(pl.multiple_of(rank_ref[0] * SHARE, SHARE), SHARE)
    x = x_ref[...].astype(jnp.float32)
    scale = lax.rsqrt(jnp.mean(x * x, axis=1, keepdims=True) + epsilon)
    inner = (i0[...] + i1[...] + i2[...] + i3[...]) * (1.0 / WIDTH)
    inner = jnp.transpose(jnp.broadcast_to(inner[:1], (LANES, BLOCK)))[:, :1]
    weighted = (near_ref[...] + far_ref[...].astype(jnp.float32)) * gain_ref[:, mine]
    x_own = x_ref[:, mine].astype(jnp.float32)
    made_ref[...] = residual_ref[...] + scale * weighted - x_own * (scale * scale * scale * inner)


def input_finish(rank, near, far, inners, x, gain, residual):
    return run(
        input_finish_kernel,
        "input_finish",
        1,
        [smem(), once(BLOCK, SHARE), None] + [None] * 7,
        [None],
        [out((BLOCK, SHARE), jnp.float32)],
        (rank, near, far, *inners, x, gain, residual),
        cost(3_000_000, 3_000_000, 512),
        free=(1, 2, 3, 4, 5, 6),
    )[0]


def per_device(
    hidden_in,
    lengths,
    block_order,
    routes,
    norm_gain_attn,
    w_query,
    w_key,
    w_value,
    w_out,
    norm_gain_moe,
    w_router,
    w_gate,
    w_up,
    w_down,
    out_grad,
):
    dp_count = block_order.shape[0]
    mp_rank = lax.axis_index("mp").astype(jnp.int32)
    column_start = mp_rank * SHARE
    piece = BLOCK // dp_count
    steps = MAXLEN // BLOCK - 1
    rank = mp_rank.reshape(1)
    lane = lax.axis_index("dp").astype(jnp.int32).reshape(1)
    begin = rank * QUARTER
    gain_attn = norm_gain_attn[None, :]
    gain_moe = norm_gain_moe[None, :]
    router_t = jnp.pad(w_router.T, ((0, LANES - EXPERTS), (0, 0)))

    normed, key_value, cosine, sine, reach, wanted, later, live = project(
        lengths, block_order, lane, hidden_in, gain_attn, w_key, w_value
    )
    queries = project_queries(normed, w_query, cosine, sine)
    pieces = to_all(key_value.reshape(dp_count, piece, SHARE))
    picks, ranks = route(begin, after(routes.T, key_value))
    far_out = peer(after(w_out, key_value), 2)
    begun = attend_own(queries, after(key_value, picks))
    picked = pick_pieces(wanted, after(pieces, far_out))
    earlier = to_all(picked.reshape(dp_count, steps * piece, SHARE))
    earlier = earlier.reshape(dp_count, steps, piece, SHARE)

    outs = [w_out, peer(after(w_out, picked), 1), far_out, peer(far_out, 1)]

    grad_rows = jnp.dot(picks, after(out_grad, picked), preferred_element_type=jnp.bfloat16)
    grad_arrived = to_experts(after(grad_rows, earlier, begun[1]).reshape(EXPERTS, QUARTER, WIDTH))
    attended, attended_t, lse = attend(reach, begun, earlier)
    far = peer(attended, 2)
    residual, moe_cat, gates, moe_rows = residual_step(
        [attended, peer(attended, 1), far, peer(far, 1)],
        outs,
        hidden_in,
        gain_moe,
        router_t,
        ranks,
        picks,
    )
    own_pack = pack_weights(after(w_down[0], attended), w_gate[0], w_up[0])
    far_pack = peer(after(own_pack, far), 2)
    packed = [own_pack, peer(own_pack, 1), far_pack, peer(far_pack, 1)]

    grouped = to_experts(after(moe_rows, far_pack).reshape(EXPERTS, QUARTER, -1)).reshape(SLOTS, -1)
    mix = mix_weights(begin, ranks, moe_cat)
    grouped_grad = grad_arrived.reshape(SLOTS, WIDTH)
    rows_out, row_grad, hidden_units, unit_grad = expert_step(lane, grouped, grouped_grad, packed)
    row_home = to_experts(row_grad.reshape(dp_count, QUARTER, -1)).reshape(SLOTS, -1)
    unit_keep, unit_send = unit_grads(grouped, grouped_grad, hidden_units, unit_grad)
    unit_near = unit_keep.astype(jnp.float32) + peer(unit_send, 1).astype(jnp.float32)
    unit_low = unit_near[1].astype(jnp.bfloat16)
    cut = PACKED // 2
    unit_far_a = peer(unit_low[:cut], 2)
    keep, send = sum_home(rank, after(mix, unit_far_a), row_home)
    near = keep + peer(send, 1).astype(jnp.float32)
    mine = swap_sum(near, peer(near.astype(jnp.bfloat16), 2))
    theirs = peer(mine, 1)
    rows_home = to_experts(after(rows_out, theirs).reshape(dp_count, QUARTER, -1)).reshape(SLOTS, -1)
    branch_grad, logit_grad, residual_grad, attended_grad, attended_grad_t, moe_gain = norm_back_step(
        rank, mine, theirs, gates, residual, gain_moe, router_t, out_grad, w_out
    )

    query_pre_grad, own_grads, later_grads = attend_back(
        reach,
        queries,
        begun[0],
        key_value,
        earlier,
        attended_grad,
        attended_grad_t,
        attended_t,
        lse,
        cosine,
        sine,
    )
    unit_far_b = peer(after(unit_low[cut:], later_grads), 2)
    unit_far_b = peer(after(unit_low[cut:], branch_grad), 2)
    later_pieces = to_all(after(later_grads, rows_home, unit_far_b).reshape(dp_count, steps * piece, SHARE))
    summed = sum_pieces(
        later, live, later_pieces.reshape(dp_count * steps, piece, SHARE), dp_count
    )
    kv_home = to_all(summed).reshape(BLOCK, SHARE)
    made = dense_grads(
        branch_grad, attended, normed, query_pre_grad, logit_grad, moe_cat, moe_gain
    )

    every, keep, send, inner = last_grads(
        rank,
        own_grads,
        kv_home,
        query_pre_grad,
        normed,
        hidden_in,
        w_query,
        w_key,
        w_value,
        cosine,
        sine,
        made,
        gain_attn,
    )
    near_norm = keep + peer(send, 1).astype(jnp.float32)
    far_norm = peer(near_norm[BLOCK:].astype(jnp.bfloat16), 2)
    inners = [inner] + [peer(inner, flip) for flip in (1, 2, 3)]
    arrived = to_all(every.reshape(dp_count, WIDTH // dp_count, -1))
    keep, send = sum_home(rank, mix, after(rows_home, every))
    near_mix = keep + peer(send, 1).astype(jnp.float32)
    far_mix = peer(near_mix[BLOCK:].astype(jnp.bfloat16), 2)
    grad_w_gate, grad_w_up, grad_w_down = unit_finish(unit_near, unit_far_a, after(unit_far_b, every))
    dense = jnp.sum(arrived.astype(jnp.float32), axis=0)
    residual_cols = lax.dynamic_slice_in_dim(residual, column_start, SHARE, 1)
    mixture = near_mix[:BLOCK] + after(far_mix, dense).astype(jnp.float32)
    out_hidden = (residual_cols + mixture).astype(jnp.bfloat16)

    grad_hidden = input_finish(
        rank, near_norm, after(far_norm, dense), inners, hidden_in, gain_attn, residual_grad
    )
    at = 3 * SHARE
    attn_gain = dense[:, at + EXPERTS + 8]
    attn_gain = attn_gain + peer(attn_gain, 1) + peer(attn_gain, 2) + peer(attn_gain, 3)
    return (
        out_hidden,
        grad_hidden,
        dense[:, SHARE : 2 * SHARE],
        dense[:, 2 * SHARE : 2 * SHARE + LANES],
        dense[:, 2 * SHARE + LANES : at],
        dense[:, :SHARE].T,
        attn_gain,
        dense[:, at + EXPERTS],
        dense[:, at : at + EXPERTS],
        grad_w_gate,
        grad_w_up,
        grad_w_down,
    )


def solution(mesh):
    in_specs = (
        P("dp", None),
        P(),
        P(),
        P("dp", None),
        P(),
        P(None, "mp"),
        P(None, "mp"),
        P(None, "mp"),
        P("mp", None),
        P(),
        P(),
        P("dp", None, "mp"),
        P("dp", None, "mp"),
        P("dp", "mp", None),
        P("dp", None),
    )
    out_specs = (
        P("dp", "mp"),
        P("dp", "mp"),
        P("dp", "mp"),
        P("dp", "mp"),
        P("dp", "mp"),
        P("mp", "dp"),
        P("dp"),
        P("dp"),
        P("dp", None),
        P("dp", None, "mp"),
        P("dp", None, "mp"),
        P("dp", "mp", None),
    )
    return jax.shard_map(
        per_device, mesh=mesh, in_specs=in_specs, out_specs=out_specs, check_vma=False
    )
```

```python
import jax
import jax.numpy as jnp
import numpy as np
from jax import lax
from jax.experimental import pallas as pl
from jax.experimental.pallas import tpu as pltpu
from jax.sharding import PartitionSpec as P

HEAD_DIM = 64
EXPERTS = 32
BLOCK = 512
MAXLEN = 2048
CAP = 160
WIDTH = 1024
SHARE = 256
QUARTER = 40
SLOTS = 1280
LANES = 128
PACKED = 384

epsilon = 1e-06
residual_mult = 0.22
score_mult = 0.015625
rope_base = 10000.0
masked_score = -1e30

NN = (((1,), (0,)), ((), ()))
NT = (((1,), (1,)), ((), ()))
TN = (((0,), (0,)), ((), ()))


def mm(a, b, dims=NN):
    return lax.dot_general(a, b, dims, preferred_element_type=jnp.float32)


def to_all(x):
    return lax.all_to_all(x, "dp", 0, 0, tiled=True)


def crossed_groups(dp_count=32):
    groups = []
    for chip in range(2):
        for core in range(2):
            groups.append([i * 4 + (chip ^ (i & 1)) * 2 + core for i in range(dp_count)])
    return groups


def to_experts(x):
    return lax.all_to_all(
        x, ("dp", "mp"), 0, 0, axis_index_groups=crossed_groups(x.shape[0]), tiled=True
    )


def peer(x, flip):
    return lax.ppermute(x, "mp", [(i, i ^ flip) for i in range(4)])


def after(x, *others):
    return lax.optimization_barrier((x, *others))[0]


def vmem():
    return pl.BlockSpec(memory_space=pltpu.VMEM)


def smem():
    return pl.BlockSpec(memory_space=pltpu.SMEM)


def tiles(rows, width, row0=0):
    return pl.BlockSpec((rows, width), lambda i: (i + row0, 0))


def fixed(rows, width):
    return pl.BlockSpec((rows, width), lambda i: (0, 0))


def once(*shape):
    return pl.BlockSpec(shape, lambda i: (0,) * len(shape), pipeline_mode=pl.Buffered(1))


def run(kernel, name, steps, in_specs, out_specs, out_shape, args, estimate, scratch=(), free=(), limit=32):
    in_specs = [once(*a.shape) if s is None else s for s, a in zip(in_specs, args)]
    out_specs = [once(*o.shape) if s is None else s for s, o in zip(out_specs, out_shape)]
    args = [
        a
        if s.memory_space is not None or i in free
        else pltpu.with_memory_space_constraint(a, pltpu.HBM)
        for i, (s, a) in enumerate(zip(in_specs, args))
    ]
    out_shape = [
        o if s.memory_space == pltpu.SMEM else pltpu.HBM(o.shape, o.dtype)
        for s, o in zip(out_specs, out_shape)
    ]
    return pl.pallas_call(
        kernel,
        name=name,
        grid=(steps,),
        in_specs=in_specs,
        out_specs=out_specs,
        out_shape=out_shape,
        scratch_shapes=list(scratch),
        compiler_params=pltpu.CompilerParams(vmem_limit_bytes=limit << 20),
        cost_estimate=estimate,
    )(*args)


def out(shape, dtype):
    return jax.ShapeDtypeStruct(shape, dtype)


def cost(flops, moved, exps=0):
    return pl.CostEstimate(flops=flops, bytes_accessed=moved, transcendentals=exps)


def rope_constants():
    frequency = rope_base ** (-(np.arange(HEAD_DIM // 2, dtype=np.float64) * 2.0) / HEAD_DIM)
    wide = np.tile(frequency, 4)[None, :]
    made = []
    for count, apart in ((BLOCK // 16, 16), (16, 1), (8, BLOCK)):
        angles = np.arange(count, dtype=np.float64)[:, None] * apart * wide
        made += [np.cos(angles), np.sin(angles)]
    return [jnp.asarray(a.astype(np.float32)) for a in made]


def half_front(rows):
    lane = lax.broadcasted_iota(jnp.int32, (rows, LANES), 1)
    return (lane % HEAD_DIM) < HEAD_DIM // 2


def turned(chunk, cosine, signed_sine, back=False):
    partner = jnp.where(
        half_front(chunk.shape[0]), pltpu.roll(chunk, 96, 1), pltpu.roll(chunk, 32, 1)
    )
    if back:
        return chunk * cosine - partner * signed_sine
    return chunk * cosine + partner * signed_sine


def block_tables_in(lengths_ref, order_ref, rank_ref, offset_ref, inverse_ref, reach_ref, wanted_ref, later_ref, live_ref):
    count = order_ref.shape[0]
    steps = MAXLEN // BLOCK - 1

    def sequence(s, begin):
        def one(j, at):
            offset_ref[jnp.minimum(at, count - 1)] = j
            return at + 1

        return lax.fori_loop(0, lengths_ref[s], one, begin)

    lax.fori_loop(0, lengths_ref.shape[0], sequence, jnp.int32(0))

    def invert(d, carry):
        inverse_ref[order_ref[d]] = d
        return carry

    lax.fori_loop(0, count, invert, jnp.int32(0))
    reach_ref[0] = offset_ref[order_ref[rank_ref[0]]]

    def look(d, carry):
        packed = order_ref[d]
        for s in range(1, steps + 1):
            wanted_ref[d * steps + s - 1] = inverse_ref[jnp.maximum(packed - s, 0)]
            next_at = jnp.minimum(packed + s, count - 1)
            later_ref[d * steps + s - 1] = inverse_ref[next_at] * steps + s - 1
            is_live = jnp.logical_and(packed + s < count, offset_ref[next_at] >= s)
            live_ref[d * steps + s - 1] = jnp.where(is_live, 1, 0)
        return carry

    lax.fori_loop(0, count, look, jnp.int32(0))


def project_kernel(
    lengths_ref, order_ref, rank_ref, x_ref, gain_ref, wk_ref, wv_ref,
    cos16_ref, sin16_ref, cos1_ref, sin1_ref, cos0_ref, sin0_ref,
    normed_ref, kv_ref, cosine_ref, sine_ref, reach_ref, wanted_ref, later_ref, live_ref,
    offset_ref, inverse_ref,
):
    @pl.when(pl.program_id(0) == 0)
    def _():
        block_tables_in(
            lengths_ref, order_ref, rank_ref, offset_ref, inverse_ref, reach_ref, wanted_ref, later_ref, live_ref
        )

    x = x_ref[...].astype(jnp.float32)
    scale = lax.rsqrt(jnp.mean(x * x, axis=1, keepdims=True) + epsilon)
    normed = (x * scale * gain_ref[...]).astype(jnp.bfloat16)
    normed_ref[...] = normed
    at = reach_ref[0]
    cos0, sin0 = cos0_ref[pl.ds(at, 1), :], sin0_ref[pl.ds(at, 1), :]
    cos16 = cos16_ref[...] * cos0 - sin16_ref[...] * sin0
    sin16 = sin16_ref[...] * cos0 + cos16_ref[...] * sin0
    cos1, sin1 = cos1_ref[...][None], sin1_ref[...][None]
    cosine = (cos16[:, None, :] * cos1 - sin16[:, None, :] * sin1).reshape(x.shape[0], LANES)
    sine = (sin16[:, None, :] * cos1 + cos16[:, None, :] * sin1).reshape(x.shape[0], LANES)
    sine = jnp.where(half_front(x.shape[0]), -sine, sine)
    cosine_ref[...] = cosine
    sine_ref[...] = sine
    kv_ref[:, :LANES] = turned(mm(normed, wk_ref[...]), cosine, sine).astype(jnp.bfloat16)
    kv_ref[:, LANES:] = mm(normed, wv_ref[...]).astype(jnp.bfloat16)


def query_kernel(normed_ref, wq_ref, cosine_ref, sine_ref, q_ref):
    queries = mm(normed_ref[...], wq_ref[...])
    for i in range(0, SHARE, LANES):
        q_ref[:, i : i + LANES] = turned(
            queries[:, i : i + LANES], cosine_ref[...], sine_ref[...]
        ).astype(jnp.bfloat16)


def project_queries(normed, w_query, cosine, sine):
    tile = 256
    return run(
        query_kernel,
        "project_queries",
        BLOCK // tile,
        [tiles(tile, WIDTH), None, tiles(tile, LANES), tiles(tile, LANES)],
        [tiles(tile, SHARE)],
        [out((BLOCK, SHARE), jnp.bfloat16)],
        (normed, w_query, cosine, sine),
        cost(270_000_000, 2_500_000),
    )[0]


def project(lengths, order, rank, x, gain, w_key, w_value):
    tile = 256
    count = order.shape[0]
    steps = MAXLEN // BLOCK - 1
    bf16, f32 = jnp.bfloat16, jnp.float32
    return run(
        project_kernel,
        "project",
        BLOCK // tile,
        [smem()] * 3
        + [tiles(tile, WIDTH), None, None, None]
        + [tiles(tile // 16, LANES)] * 2
        + [None] * 4,
        [tiles(tile, WIDTH), tiles(tile, SHARE)] + [tiles(tile, LANES)] * 2 + [smem()] * 4,
        [out((BLOCK, WIDTH), bf16), out((BLOCK, SHARE), bf16)]
        + [out((BLOCK, LANES), f32)] * 2
        + [out((1,), jnp.int32)]
        + [out((count * steps,), jnp.int32)] * 3,
        (lengths, order, rank, x, gain, w_key, w_value, *rope_constants()),
        cost(540_000_000, 4_000_000, 512),
        [pltpu.SMEM((count,), jnp.int32), pltpu.SMEM((count,), jnp.int32)],
    )


def pick_kernel(wanted_ref, pieces_ref, picked_ref):
    def one(i, carry):
        picked_ref[i] = pieces_ref[wanted_ref[i]]
        return carry

    lax.fori_loop(0, picked_ref.shape[0], one, jnp.int32(0), unroll=4)


def pick_pieces(wanted, pieces):
    shape = out((wanted.shape[0], *pieces.shape[1:]), pieces.dtype)
    return run(
        pick_kernel, "pick_pieces", 1, [smem(), None], [None], [shape], (wanted, pieces), cost(0, 1_100_000), free=(1,)
    )[0]


def sum_kernel(later_ref, live_ref, pieces_ref, sum_ref):
    steps = MAXLEN // BLOCK - 1

    def one(d, carry):
        total = jnp.zeros(sum_ref.shape[1:], jnp.float32)
        for s in range(steps):
            part = pieces_ref[later_ref[d * steps + s]].astype(jnp.float32)
            total = total + jnp.where(live_ref[d * steps + s] == 1, part, 0.0)
        sum_ref[d] = total.astype(sum_ref.dtype)
        return carry

    lax.fori_loop(0, sum_ref.shape[0], one, jnp.int32(0), unroll=2)


def sum_pieces(later, live, pieces, count):
    shape = out((count, *pieces.shape[1:]), pieces.dtype)
    return run(
        sum_kernel,
        "sum_pieces",
        1,
        [smem(), smem(), None],
        [None],
        [shape],
        (later, live, pieces),
        cost(0, 1_100_000),
        free=(2,),
    )[0]


def pack_kernel(down_ref, gate_ref, up_ref, packed_ref):
    packed_ref[:LANES, :] = down_ref[...]
    for k in range(4):
        rows = slice(k * SHARE, (k + 1) * SHARE)
        packed_ref[LANES:, k * SHARE : k * SHARE + LANES] = gate_ref[rows, :]
        packed_ref[LANES:, k * SHARE + LANES : (k + 1) * SHARE] = up_ref[rows, :]


def pack_weights(w_down, w_gate, w_up):
    shape = out((PACKED, WIDTH), jnp.bfloat16)
    return run(
        pack_kernel, "pack_weights", 1, [None] * 3, [None], [shape], (w_down, w_gate, w_up), cost(0, 1_600_000)
    )[0]


def route_kernel(begin_ref, routes_ref, picks_ref, ranks_ref):
    tokens = routes_ref.shape[1]
    expert_at = lax.broadcasted_iota(jnp.int32, (LANES, tokens), 0)
    hits = jnp.zeros((LANES, tokens), jnp.float32)
    for k in range(routes_ref.shape[0]):
        hits = hits + jnp.where(routes_ref[k : k + 1, :] == expert_at, 1.0, 0.0)
    row_at = lax.broadcasted_iota(jnp.int32, (tokens, tokens), 0)
    column_at = lax.broadcasted_iota(jnp.int32, (tokens, tokens), 1)
    before = jnp.where(row_at < column_at, 1.0, 0.0).astype(jnp.bfloat16)
    ranks = jnp.where(hits > 0.5, mm(hits.astype(jnp.bfloat16), before), -1.0)
    ranks_ref[...] = ranks
    slot_at = lax.broadcasted_iota(jnp.int32, (QUARTER, tokens), 0) + begin_ref[0]
    slot_at = slot_at.astype(jnp.float32)
    for e in range(EXPERTS):
        picks_ref[e * QUARTER : (e + 1) * QUARTER, :] = jnp.where(
            ranks[e : e + 1, :] == slot_at, 1.0, 0.0
        ).astype(jnp.bfloat16)


def route(begin, routes_t):
    return run(
        route_kernel,
        "route",
        1,
        [smem(), None],
        [None, None],
        [out((SLOTS, BLOCK), jnp.bfloat16), out((LANES, BLOCK), jnp.float32)],
        (begin, routes_t),
        cost(100_000_000, 1_600_000),
        free=(1,),
    )


def padded_columns(rows_t, out_ref):
    zero = jnp.zeros((HEAD_DIM, rows_t.shape[1]), out_ref.dtype)
    for h in range(4):
        mine = rows_t[h * HEAD_DIM : (h + 1) * HEAD_DIM].astype(out_ref.dtype)
        at = (h // 2) * HEAD_DIM
        out_ref[h, pl.ds(at, HEAD_DIM), :] = mine
        out_ref[h, pl.ds(HEAD_DIM - at, HEAD_DIM), :] = zero


def padded_rows(rows, out_ref):
    n = rows.shape[0]
    lane = lax.broadcasted_iota(jnp.int32, (n, 128), 1)
    for h in range(4):
        pair = rows[:, (h // 2) * 128 : (h // 2) * 128 + 128].astype(jnp.float32)
        if h % 2 != h // 2:
            pair = pltpu.roll(pair, HEAD_DIM, 1)
        own = (lane < HEAD_DIM) if h // 2 == 0 else (lane >= HEAD_DIM)
        out_ref[pl.ds(h * n, n), :] = jnp.where(own, pair, 0.0).astype(out_ref.dtype)


def attend_block(key_rows, value_rows, first, qpad_ref, max_ref, sum_ref, out_t_ref):
    half = BLOCK // 2
    for h in range(4):
        group = (h // 2) * HEAD_DIM
        for t in range(2):
            cols = slice(t * half, (t + 1) * half)
            rows = half if first and t == 0 else BLOCK
            scores = mm(key_rows[:rows], qpad_ref[h, :, cols])
            if first:
                key_at = lax.broadcasted_iota(jnp.int32, scores.shape, 0)
                query_at = lax.broadcasted_iota(jnp.int32, scores.shape, 1) + t * half
                scores = jnp.where(key_at > query_at, masked_score, scores)
            new_max = jnp.max(scores, axis=0, keepdims=True)
            if not first:
                old_max = max_ref[h : h + 1, cols]
                new_max = jnp.maximum(new_max, old_max)
                shrink = jnp.exp(old_max - new_max)
            weights = jnp.exp(scores - new_max)
            total = jnp.sum(weights, axis=0, keepdims=True)
            part = mm(value_rows[:rows], weights.astype(jnp.bfloat16), TN)[group : group + HEAD_DIM]
            mine = pl.ds(h * HEAD_DIM, HEAD_DIM)
            if not first:
                total = total + sum_ref[h : h + 1, cols] * shrink
                part = part + out_t_ref[mine, cols] * shrink
            max_ref[h : h + 1, cols] = new_max
            sum_ref[h : h + 1, cols] = total
            out_t_ref[mine, cols] = part


def attend_own_kernel(q_ref, own_ref, qpad_ref, max_ref, sum_ref, out_t_ref):
    padded_columns(jnp.transpose(q_ref[...].astype(jnp.float32) * score_mult), qpad_ref)
    max_ref[...] = jnp.zeros_like(max_ref)
    sum_ref[...] = jnp.ones_like(sum_ref)
    attend_block(own_ref[:, :LANES], own_ref[:, LANES:], True, qpad_ref, max_ref, sum_ref, out_t_ref)


def attend_own(queries, own_kv):
    return pl.pallas_call(
        attend_own_kernel,
        name="attend_own",
        in_specs=[vmem()] * 2,
        out_specs=[vmem()] * 4,
        out_shape=[
            out((4, LANES, BLOCK), jnp.bfloat16),
            out((8, BLOCK), jnp.float32),
            out((8, BLOCK), jnp.float32),
            out((SHARE, BLOCK), jnp.float32),
        ],
        compiler_params=pltpu.CompilerParams(vmem_limit_bytes=36 << 20),
        cost_estimate=cost(1_000_000_000, 2_000_000, 600_000),
    )(queries, own_kv)


def attend_kernel(
    reach_ref, qpad_ref, max0_ref, sum0_ref, out0_ref, prev_ref, att_ref, out_t_ref, lse_ref, max_ref, sum_ref
):
    max_ref[...] = max0_ref[...]
    sum_ref[...] = sum0_ref[...]
    out_t_ref[...] = out0_ref[...]

    @pl.loop(1, reach_ref[0] + 1)
    def _(step):
        rows = prev_ref[:, pl.ds(step - 1, 1)].reshape(BLOCK, SHARE)
        attend_block(rows[:, :LANES], rows[:, LANES:], False, qpad_ref, max_ref, sum_ref, out_t_ref)

    lse_ref[...] = max_ref[...] + jnp.log(sum_ref[...])
    for h in range(4):
        mine = pl.ds(h * HEAD_DIM, HEAD_DIM)
        out_t_ref[mine, :] = out_t_ref[mine, :] / sum_ref[h : h + 1, :]
    att_ref[...] = jnp.transpose(out_t_ref[...]).astype(jnp.bfloat16)


def attend(reach, begun, earlier):
    return run(
        attend_kernel,
        "attend",
        1,
        [smem()] + [vmem()] * 5,
        [None] * 3,
        [
            out((BLOCK, SHARE), jnp.bfloat16),
            out((SHARE, BLOCK), jnp.float32),
            out((8, BLOCK), jnp.float32),
        ],
        (reach, *begun, earlier),
        cost(4_000_000_000, 3_000_000, 3_000_000),
        [pltpu.VMEM((8, BLOCK), jnp.float32), pltpu.VMEM((8, BLOCK), jnp.float32)],
        limit=36,
    )


def attend_back_kernel(
    reach_ref, q_ref, qpad_ref, own_ref, prev_ref, grad_ref, grad_t_ref, out_t_ref, lse_ref, cos_ref, sin_ref,
    qgrad_ref, own_grad_ref, prev_grad_ref,
    gpad_ref, qrows_ref, grows_ref, ds_ref, p_ref, delta_ref, dq_ref,
):
    half = BLOCK // 2
    q_scaled = q_ref[...].astype(jnp.float32) * score_mult
    padded_rows(q_scaled, qrows_ref)
    padded_columns(grad_t_ref[...], gpad_ref)
    padded_rows(grad_ref[...], grows_ref)
    both = grad_t_ref[...].astype(jnp.float32) * out_t_ref[...]
    for h in range(4):
        delta_ref[h : h + 1, :] = jnp.sum(
            both[h * HEAD_DIM : (h + 1) * HEAD_DIM], axis=0, keepdims=True
        )


    def block(key_rows, value_rows, first):
        for h in range(4):
            for t in range(2):
                cols = slice(t * half, (t + 1) * half)
                wide = slice(h * BLOCK + t * half, h * BLOCK + (t + 1) * half)
                rows = half if first and t == 0 else BLOCK
                scores = mm(key_rows[:rows], qpad_ref[h, :, cols])
                weights = jnp.exp(scores - lse_ref[h : h + 1, cols])
                if first:
                    key_at = lax.broadcasted_iota(jnp.int32, scores.shape, 0)
                    query_at = lax.broadcasted_iota(jnp.int32, scores.shape, 1) + t * half
                    weights = jnp.where(key_at > query_at, 0.0, weights)
                weight_grad = mm(value_rows[:rows], gpad_ref[h, :, cols])
                score_grad = weights * (weight_grad - delta_ref[h : h + 1, cols])
                p_ref[:rows, wide] = weights.astype(jnp.bfloat16)
                ds_ref[:rows, wide] = score_grad.astype(jnp.bfloat16)
                if rows < BLOCK:
                    p_ref[rows:, wide] = jnp.zeros((BLOCK - rows, half), jnp.bfloat16)
                    ds_ref[rows:, wide] = jnp.zeros((BLOCK - rows, half), jnp.bfloat16)
        key_grad = mm(ds_ref[...], qrows_ref[...])
        value_grad = mm(p_ref[...], grows_ref[...])
        for h in range(4):
            group = (h // 2) * HEAD_DIM
            mine = pl.ds(h * HEAD_DIM, HEAD_DIM)
            part = mm(key_rows, ds_ref[:, h * BLOCK : (h + 1) * BLOCK], TN)[group : group + HEAD_DIM]
            dq_ref[mine, :] = part if first else dq_ref[mine, :] + part
        return key_grad, value_grad

    key_grad, value_grad = block(own_ref[:, :LANES], own_ref[:, LANES:], True)
    own_grad_ref[:, :LANES] = key_grad
    own_grad_ref[:, LANES:] = value_grad

    @pl.loop(1, reach_ref[0] + 1)
    def _(step):
        rows = prev_ref[:, pl.ds(step - 1, 1)].reshape(BLOCK, SHARE)
        key_grad, value_grad = block(rows[:, :LANES], rows[:, LANES:], False)
        parts = prev_grad_ref.shape[0]
        shape = (parts, 1, BLOCK // parts, LANES)
        prev_grad_ref[:, pl.ds(step - 1, 1), :, :LANES] = key_grad.astype(jnp.bfloat16).reshape(shape)
        prev_grad_ref[:, pl.ds(step - 1, 1), :, LANES:] = value_grad.astype(jnp.bfloat16).reshape(shape)

    query_grad = jnp.transpose(dq_ref[...]) * score_mult
    for i in range(0, SHARE, LANES):
        qgrad_ref[:, i : i + LANES] = turned(
            query_grad[:, i : i + LANES], cos_ref[...], sin_ref[...], back=True
        ).astype(jnp.bfloat16)


def attend_back(reach, queries, padded, own_kv, earlier, grad, grad_t, out_t, lse, cosine, signed_sine):
    return run(
        attend_back_kernel,
        "attend_back",
        1,
        [smem()] + [vmem()] * 10,
        [None] * 3,
        [
            out((BLOCK, SHARE), jnp.bfloat16),
            out((BLOCK, SHARE), jnp.float32),
            out(earlier.shape, jnp.bfloat16),
        ],
        (reach, queries, padded, own_kv, earlier, grad, grad_t, out_t, lse, cosine, signed_sine),
        cost(12_000_000_000, 5_000_000, 3_000_000),
        [
            pltpu.VMEM((4, LANES, BLOCK), jnp.bfloat16),
            pltpu.VMEM((4 * BLOCK, LANES), jnp.bfloat16),
            pltpu.VMEM((4 * BLOCK, LANES), jnp.bfloat16),
            pltpu.VMEM((BLOCK, 4 * BLOCK), jnp.bfloat16),
            pltpu.VMEM((BLOCK, 4 * BLOCK), jnp.bfloat16),
            pltpu.VMEM((8, BLOCK), jnp.float32),
            pltpu.VMEM((SHARE, BLOCK), jnp.float32),
        ],
        limit=36,
    )


def residual_kernel(
    a0, a1, a2, a3, w0, w1, w2, w3, x_ref, gain_ref, router_ref, ranks_ref, picks_ref,
    residual_ref, moe_ref, gates_ref, rows_ref, held_ref,
):
    step = pl.program_id(0)
    tile = x_ref.shape[0]

    @pl.when(step < BLOCK // tile)
    def _():
        branch = mm(a0[...], w0[...])
        for a, w in ((a1, w1), (a2, w2), (a3, w3)):
            branch = branch + mm(a[...], w[...])
        residual = x_ref[...].astype(jnp.float32) + residual_mult * branch
        residual_ref[...] = residual
        scale = lax.rsqrt(jnp.mean(residual * residual, axis=1, keepdims=True) + epsilon)
        moe_in = (residual * scale * gain_ref[...]).astype(jnp.bfloat16)
        moe_ref[:, :WIDTH] = moe_in
        logits = mm(router_ref[...], moe_in, NT)
        chosen = ranks_ref[...] >= 0.0
        kept = jnp.where(chosen, logits, masked_score)
        top = jnp.max(kept, axis=0, keepdims=True)
        raised = jnp.where(chosen, jnp.exp(kept - top), 0.0)
        gates = raised / jnp.sum(raised, axis=0, keepdims=True)
        gates_ref[...] = gates
        low = (residual_mult * jnp.transpose(gates)).astype(jnp.bfloat16)
        moe_ref[:, WIDTH:] = low
        held_ref[pl.ds(step * tile, tile), :WIDTH] = moe_in
        held_ref[pl.ds(step * tile, tile), WIDTH:] = low

    @pl.when(step >= BLOCK // tile)
    def _():
        rows_ref[...] = mm(picks_ref[...], held_ref[...]).astype(jnp.bfloat16)


def residual_step(attended, w_out, x, gain, router_t, ranks, picks):
    tile = 256
    first = BLOCK // tile
    slot_tile = SLOTS // 4

    def early(rows, width):
        return pl.BlockSpec((rows, width), lambda i: (jnp.minimum(i, first - 1), 0))

    def late(rows, width):
        return pl.BlockSpec((rows, width), lambda i: (jnp.maximum(i - first, 0), 0))

    by_columns = pl.BlockSpec((LANES, tile), lambda i: (0, jnp.minimum(i, first - 1)))
    return run(
        residual_kernel,
        "residual_step",
        first + 4,
        [early(tile, SHARE)] * 4
        + [None] * 4
        + [early(tile, WIDTH), None, None, by_columns, late(slot_tile, BLOCK)],
        [early(tile, WIDTH), early(tile, WIDTH + LANES), by_columns, late(slot_tile, WIDTH + LANES)],
        [
            out((BLOCK, WIDTH), jnp.float32),
            out((BLOCK, WIDTH + LANES), jnp.bfloat16),
            out((LANES, BLOCK), jnp.float32),
            out((SLOTS, WIDTH + LANES), jnp.bfloat16),
        ],
        (*attended, *w_out, x, gain, router_t, ranks, picks),
        cost(2_700_000_000, 12_000_000, 70_000),
        [pltpu.VMEM((BLOCK, WIDTH + LANES), jnp.bfloat16)],
        free=(1, 2, 3, 5, 6, 7, 10),
    )


def mix_kernel(begin_ref, ranks_ref, moe_ref, mix_ref):
    ranks = jnp.transpose(ranks_ref[...]).astype(jnp.bfloat16)
    gates = moe_ref[:, WIDTH:]
    width = 640
    for at in range(0, SLOTS, width):
        expert_at = lax.broadcasted_iota(jnp.int32, (LANES, width), 0)
        first = expert_at * QUARTER - at
        slot_at = lax.broadcasted_iota(jnp.int32, (LANES, width), 1)
        inside = jnp.logical_and(slot_at >= first, slot_at < first + QUARTER)
        spread = jnp.where(inside, 1.0, 0.0).astype(jnp.bfloat16)
        within = jnp.sum(jnp.where(inside, slot_at - first, 0), axis=0, keepdims=True) + begin_ref[0]
        hit = mm(ranks, spread) == within.astype(jnp.float32)
        mix_ref[:, at : at + width] = jnp.where(hit, mm(gates, spread), 0.0).astype(jnp.bfloat16)


def mix_weights(begin, ranks, moe_cat):
    return run(
        mix_kernel,
        "mix_weights",
        1,
        [smem(), None, None],
        [None],
        [out((BLOCK, SLOTS), jnp.bfloat16)],
        (begin, ranks, moe_cat),
        cost(350_000_000, 3_000_000),
    )[0]


def expert_kernel(
    lane_ref, x_ref, grad_ref, p0, p1, p2, p3,
    out_ref, row_ref, hidden_ref, units_ref,
):
    packed = (p0, p1, p2, p3)
    rows = out_ref.shape[0]
    here = pl.ds(pl.program_id(0) * rows, rows)
    lane = lax.broadcasted_iota(jnp.int32, (rows, LANES), 1) == lane_ref[0]
    gate = jnp.sum(
        jnp.where(lane, x_ref[here, WIDTH:].astype(jnp.float32), 0.0), axis=1, keepdims=True
    )
    x = x_ref[here, :WIDTH]
    grad = grad_ref[...]
    gates, ups, sigmoids, hidden = [], [], [], []
    for p in packed:
        pre = None
        for k in range(4):
            columns = slice(k * SHARE, (k + 1) * SHARE)
            term = mm(x[:, columns], p[LANES:, columns])
            pre = term if pre is None else pre + term
        gate_pre, up_pre = pre[:, :LANES], pre[:, LANES:]
        sigmoid = 1.0 / (1.0 + jnp.exp(-gate_pre))
        gates.append(gate_pre)
        ups.append(up_pre)
        sigmoids.append(sigmoid)
        hidden.append(gate_pre * sigmoid * up_pre)
    hidden_low = jnp.concatenate([h.astype(jnp.bfloat16) for h in hidden], axis=1)
    down = jnp.concatenate([p[:LANES, :] for p in packed], axis=0)
    made = mm(hidden_low, down).astype(jnp.bfloat16)
    out_ref[...] = made
    gate_grad = jnp.sum(grad.astype(jnp.float32) * made.astype(jnp.float32), axis=1, keepdims=True)
    row_ref[:, WIDTH:] = jnp.where(lane, gate_grad, 0.0).astype(jnp.bfloat16)
    hidden_grad = mm(grad, down, NT)
    row = None
    for j, p in enumerate(packed):
        part = hidden_grad[:, j * LANES : (j + 1) * LANES]
        silu = gates[j] * sigmoids[j]
        gate_pre_grad = part * ups[j] * sigmoids[j] * (1.0 + gates[j] * (1.0 - sigmoids[j]))
        up_pre_grad = part * silu
        hidden_ref[:, j * LANES : (j + 1) * LANES] = (hidden[j] * gate).astype(jnp.bfloat16)
        units_ref[:, j * SHARE : j * SHARE + LANES] = (gate_pre_grad * gate).astype(jnp.bfloat16)
        units_ref[:, j * SHARE + LANES : (j + 1) * SHARE] = (up_pre_grad * gate).astype(jnp.bfloat16)
        both = jnp.concatenate([gate_pre_grad, up_pre_grad], axis=1).astype(jnp.bfloat16)
        terms = [
            mm(both, p[LANES:, k * SHARE : (k + 1) * SHARE], NT) for k in range(4)
        ]
        row = terms if row is None else [a + b for a, b in zip(row, terms)]
    for k in range(4):
        row_ref[:, k * SHARE : (k + 1) * SHARE] = row[k].astype(jnp.bfloat16)


def expert_step(lane, x, grad, packed):
    tile = 320
    return run(
        expert_kernel,
        "expert_step",
        SLOTS // tile,
        [smem(), vmem(), tiles(tile, WIDTH)] + [None] * 4,
        [tiles(tile, WIDTH), tiles(tile, WIDTH + LANES), tiles(tile, 512), tiles(tile, WIDTH)],
        [
            out((SLOTS, WIDTH), jnp.bfloat16),
            out((SLOTS, WIDTH + LANES), jnp.bfloat16),
            out((SLOTS, 512), jnp.bfloat16),
            out((SLOTS, WIDTH), jnp.bfloat16),
        ],
        (lane, x, grad, *packed),
        cost(8_000_000_000, 18_000_000, 700_000),
        limit=40,
    )


def unit_grads_kernel(x_ref, grad_ref, hidden_ref, units_ref, keep_ref, send_ref, turned_ref):
    step = pl.program_id(0)

    @pl.when(step == 0)
    def _():
        for k in range(4):
            columns = slice(k * SHARE, (k + 1) * SHARE)
            turned_ref[columns, :] = jnp.transpose(x_ref[:, columns])

    def write(to_ref):
        to_ref[0, :LANES, :] = mm(hidden_ref[...], grad_ref[...], TN).astype(jnp.bfloat16)
        for k in range(4):
            columns = slice(k * SHARE, (k + 1) * SHARE)
            to_ref[0, LANES:, columns] = mm(turned_ref[columns, :], units_ref[...]).astype(jnp.bfloat16)

    @pl.when(step < 2)
    def _():
        write(keep_ref)

    @pl.when(step >= 2)
    def _():
        write(send_ref)


def unit_grads(x, grad, hidden, units):
    rows = SHARE + LANES

    def share_of(i):
        return jnp.where(i < 2, 2 * i, 2 * i - 3)

    return run(
        unit_grads_kernel,
        "unit_grads",
        4,
        [
            vmem(),
            None,
            pl.BlockSpec((SLOTS, LANES), lambda i: (0, share_of(i))),
            pl.BlockSpec((SLOTS, SHARE), lambda i: (0, share_of(i))),
        ],
        [
            pl.BlockSpec((1, rows, WIDTH), lambda i: (jnp.minimum(i, 1), 0, 0)),
            pl.BlockSpec((1, rows, WIDTH), lambda i: (jnp.maximum(i - 2, 0), 0, 0)),
        ],
        [out((2, rows, WIDTH), jnp.bfloat16), out((2, rows, WIDTH), jnp.bfloat16)],
        (x, grad, hidden, units),
        cost(4_000_000_000, 12_000_000),
        [pltpu.VMEM((WIDTH, SLOTS), jnp.bfloat16)],
        limit=36,
    )


def unit_finish_kernel(mine_ref, first_ref, second_ref, gate_ref, up_ref, down_ref):
    got = jnp.concatenate([first_ref[...], second_ref[...]], axis=0)
    total = mine_ref[0] + got.astype(jnp.float32)
    down_ref[0] = total[:LANES, :]
    for k in range(4):
        rows = slice(k * SHARE, (k + 1) * SHARE)
        gate_ref[0, rows, :] = total[LANES:, k * SHARE : k * SHARE + LANES]
        up_ref[0, rows, :] = total[LANES:, k * SHARE + LANES : (k + 1) * SHARE]


def unit_finish(mine, first, second):
    return run(
        unit_finish_kernel,
        "unit_finish",
        1,
        [once(1, PACKED, WIDTH), None, None],
        [None] * 3,
        [
            out((1, WIDTH, LANES), jnp.float32),
            out((1, WIDTH, LANES), jnp.float32),
            out((1, LANES, WIDTH), jnp.float32),
        ],
        (mine, first, second),
        cost(1_000_000, 3_000_000),
        free=(0, 1, 2),
    )


def home_kernel(rank_ref, mix_ref, rows_ref, keep_ref, send_ref):
    rank = rank_ref[0]
    extra = rows_ref.shape[1] > WIDTH
    for j in range(4):
        at = pl.multiple_of(jnp.bitwise_xor(rank, j) * SHARE, SHARE)
        total = mm(mix_ref[...], rows_ref[:, pl.ds(at, SHARE)])
        to_ref = send_ref if j % 2 else keep_ref
        to_ref[(j // 2) * BLOCK : (j // 2 + 1) * BLOCK, :] = total.astype(to_ref.dtype)
    if extra:
        gate_grads = jnp.transpose(mm(mix_ref[...], rows_ref[:, WIDTH:]))[:EXPERTS]
        for to_ref in (keep_ref, send_ref):
            for i in range(2):
                at = 2 * BLOCK + i * EXPERTS
                to_ref[at : at + EXPERTS, :] = gate_grads[:, i * SHARE : (i + 1) * SHARE].astype(
                    to_ref.dtype
                )


def sum_home(rank, mix, rows):
    height = 2 * BLOCK + (2 * EXPERTS if rows.shape[1] > WIDTH else 0)
    return run(
        home_kernel,
        "sum_home",
        1,
        [smem(), None, vmem()],
        [None] * 2,
        [out((height, SHARE), jnp.float32), out((height, SHARE), jnp.bfloat16)],
        (rank, mix, rows),
        cost(1_500_000_000, 6_000_000),
        limit=36,
    )


def swap_kernel(mine_ref, got_ref, total_ref):
    mine, got = mine_ref, got_ref
    half = BLOCK
    total_ref[:half] = (mine[:half] + got[half : 2 * half].astype(jnp.float32)).astype(total_ref.dtype)
    total_ref[half : 2 * half] = (
        mine[half : 2 * half] + got[:half].astype(jnp.float32)
    ).astype(total_ref.dtype)
    total_ref[2 * half :] = (mine[2 * half :] + got[2 * half :].astype(jnp.float32)).astype(
        total_ref.dtype
    )


def swap_sum(mine, got):
    return run(
        swap_kernel,
        "swap_sum",
        1,
        [None] * 2,
        [None],
        [out(mine.shape, jnp.bfloat16)],
        (mine, got),
        cost(1_000_000, 2_500_000),
        free=(0, 1),
    )[0]


def norm_back_kernel(
    rank_ref, g0, g2, g1, g3, z_ref, gates_ref, residual_ref, gain_ref, router_ref, grad_ref, w_ref,
    low_ref, logit_ref, own_ref, att_ref, att_t_ref, gain_grad_ref, u_ref,
):
    rank = rank_ref[0]
    for flip, part in enumerate((g0, g1, g2, g3)):
        at = pl.multiple_of(jnp.bitwise_xor(rank, flip) * SHARE, SHARE)
        u_ref[:, pl.ds(at, SHARE)] = part[...].astype(jnp.float32)
    weighted_grads = z_ref[...].astype(jnp.float32)
    gates = gates_ref[:EXPERTS, :]
    inner = jnp.sum(weighted_grads, axis=0, keepdims=True)
    logit_grad = (weighted_grads - gates * inner).astype(jnp.bfloat16)
    logit_ref[...] = logit_grad
    u = u_ref[...] + mm(logit_grad, router_ref[:EXPERTS, :], TN)
    v = residual_ref[...]
    scale = lax.rsqrt(jnp.mean(v * v, axis=1, keepdims=True) + epsilon)
    weighted = u * gain_ref[...]
    mean = jnp.mean(weighted * v, axis=1, keepdims=True)
    total = grad_ref[...].astype(jnp.float32) + scale * weighted - v * (scale * scale * scale * mean)

    @pl.when(pl.program_id(0) == 0)
    def _():
        gain_grad_ref[...] = jnp.zeros_like(gain_grad_ref)

    gain_grad_ref[0:1, :] += jnp.sum(u * v * scale, axis=0, keepdims=True)
    low = (residual_mult * total).astype(jnp.bfloat16)
    low_ref[...] = low
    u_ref[...] = total
    own_ref[...] = u_ref[:, pl.ds(pl.multiple_of(rank * SHARE, SHARE), SHARE)]
    att_ref[...] = mm(low, w_ref[...], NT).astype(jnp.bfloat16)
    att_t_ref[...] = mm(w_ref[...], low, NT).astype(jnp.bfloat16)


def norm_back_step(rank, mine, theirs, gates, residual, gain, router_t, out_grad, w_out):
    tile = 256
    by_columns = pl.BlockSpec((EXPERTS, tile), lambda i: (0, i))
    return run(
        norm_back_kernel,
        "norm_back_step",
        BLOCK // tile,
        [smem()]
        + [tiles(tile, SHARE), tiles(tile, SHARE, BLOCK // tile)] * 2
        + [
            tiles(EXPERTS, SHARE, 2 * BLOCK // EXPERTS),
            pl.BlockSpec((LANES, tile), lambda i: (0, i)),
            tiles(tile, WIDTH),
            None,
            None,
            tiles(tile, WIDTH),
            None,
        ],
        [
            tiles(tile, WIDTH),
            by_columns,
            tiles(tile, SHARE),
            tiles(tile, SHARE),
            pl.BlockSpec((SHARE, tile), lambda i: (0, i)),
            fixed(8, WIDTH),
        ],
        [
            out((BLOCK, WIDTH), jnp.bfloat16),
            out((EXPERTS, BLOCK), jnp.bfloat16),
            out((BLOCK, SHARE), jnp.float32),
            out((BLOCK, SHARE), jnp.bfloat16),
            out((SHARE, BLOCK), jnp.bfloat16),
            out((8, WIDTH), jnp.float32),
        ],
        (rank, mine, mine, theirs, theirs, mine, gates, residual, gain, router_t, out_grad, w_out),
        cost(700_000_000, 9_000_000, 512),
        [pltpu.VMEM((tile, WIDTH), jnp.float32)],
        free=(3, 4, 9),
    )


def dense_grads_kernel(low_ref, attended_ref, normed_ref, qgrad_ref, logit_ref, moe_ref, gain_ref, made_ref):
    made_ref[:, :SHARE] = mm(low_ref[...], attended_ref[...], TN).astype(jnp.bfloat16)
    made_ref[:, SHARE : 2 * SHARE] = mm(normed_ref[...], qgrad_ref[...], TN).astype(jnp.bfloat16)
    router = mm(logit_ref[...], moe_ref[:, :WIDTH])
    stacked = jnp.concatenate(
        [router, gain_ref[...], jnp.zeros((LANES - EXPERTS - 8, WIDTH), jnp.float32)], axis=0
    )
    made_ref[:, 2 * SHARE :] = jnp.transpose(stacked).astype(jnp.bfloat16)


def dense_grads(low, attended, normed, qgrad, logit, moe_cat, gain_grad):
    return run(
        dense_grads_kernel,
        "dense_grads",
        1,
        [None] * 7,
        [None],
        [out((WIDTH, 2 * SHARE + LANES), jnp.bfloat16)],
        (low, attended, normed, qgrad, logit, moe_cat, gain_grad),
        cost(600_000_000, 6_000_000),
    )[0]


def last_grads_kernel(
    rank_ref, own_ref, home_ref, qgrad_ref, normed_ref, x_ref, wq_ref, wk_ref, wv_ref, cos_ref, sin_ref, made_ref,
    gain_ref, all_ref, keep_ref, send_ref, inner_ref, part_ref,
):
    rank = rank_ref[0]
    kv = own_ref[...] + home_ref[...].astype(jnp.float32)
    key_grad = turned(kv[:, :LANES], cos_ref[...], sin_ref[...], back=True).astype(jnp.bfloat16)
    value_grad = kv[:, LANES:].astype(jnp.bfloat16)
    both = jnp.concatenate([key_grad, value_grad], axis=1)
    all_ref[:, : 2 * SHARE] = made_ref[:, : 2 * SHARE]
    all_ref[:, 2 * SHARE : 3 * SHARE] = mm(normed_ref[...], both, TN).astype(jnp.bfloat16)
    gain = jnp.zeros((1, WIDTH), jnp.float32)
    tile = 128
    for i in range(0, BLOCK, tile):
        rows = slice(i, i + tile)
        part = mm(qgrad_ref[rows, :], wq_ref[...], NT)
        part = part + mm(key_grad[rows], wk_ref[...], NT) + mm(value_grad[rows], wv_ref[...], NT)
        x = x_ref[rows, :].astype(jnp.float32)
        scale = lax.rsqrt(jnp.mean(x * x, axis=1, keepdims=True) + epsilon)
        along = part * x
        gain = gain + jnp.sum(along * scale, axis=0, keepdims=True)
        inner = jnp.sum(along * gain_ref[...], axis=1, keepdims=True)
        inner_ref[:, rows] = jnp.transpose(jnp.broadcast_to(inner, (tile, LANES)))[:8]
        part_ref[rows, :] = part
    for j in range(4):
        at = pl.multiple_of(jnp.bitwise_xor(rank, j) * SHARE, SHARE)
        to_ref = send_ref if j % 2 else keep_ref
        to_ref[(j // 2) * BLOCK : (j // 2 + 1) * BLOCK, :] = part_ref[:, pl.ds(at, SHARE)].astype(to_ref.dtype)
    lane = lax.broadcasted_iota(jnp.int32, (WIDTH, LANES), 1)
    column = jnp.transpose(jnp.broadcast_to(gain, (LANES, WIDTH)))
    rest = jnp.where(lane == EXPERTS + 8, column, made_ref[:, 2 * SHARE :].astype(jnp.float32))
    all_ref[:, 3 * SHARE :] = rest.astype(jnp.bfloat16)


def last_grads(rank, own, home, qgrad, normed, x, w_query, w_key, w_value, cosine, sine, made, gain):
    return run(
        last_grads_kernel,
        "last_grads",
        1,
        [smem()] + [None] * 12,
        [None] * 4,
        [
            out((WIDTH, 3 * SHARE + LANES), jnp.bfloat16),
            out((2 * BLOCK, SHARE), jnp.float32),
            out((2 * BLOCK, SHARE), jnp.bfloat16),
            out((8, BLOCK), jnp.float32),
        ],
        (rank, own, home, qgrad, normed, x, w_query, w_key, w_value, cosine, sine, made, gain),
        cost(1_000_000_000, 8_000_000, 512),
        [pltpu.VMEM((BLOCK, WIDTH), jnp.float32)],
        free=(2,),
    )


def input_finish_kernel(
    rank_ref, near_ref, far_ref, i0, i1, i2, i3, x_ref, gain_ref, residual_ref, made_ref
):
    mine = pl.ds(pl.multiple_of(rank_ref[0] * SHARE, SHARE), SHARE)
    x = x_ref[...].astype(jnp.float32)
    scale = lax.rsqrt(jnp.mean(x * x, axis=1, keepdims=True) + epsilon)
    inner = (i0[...] + i1[...] + i2[...] + i3[...]) * (1.0 / WIDTH)
    inner = jnp.transpose(jnp.broadcast_to(inner[:1], (LANES, BLOCK)))[:, :1]
    weighted = (near_ref[...] + far_ref[...].astype(jnp.float32)) * gain_ref[:, mine]
    x_own = x_ref[:, mine].astype(jnp.float32)
    made_ref[...] = residual_ref[...] + scale * weighted - x_own * (scale * scale * scale * inner)


def input_finish(rank, near, far, inners, x, gain, residual):
    return run(
        input_finish_kernel,
        "input_finish",
        1,
        [smem(), once(BLOCK, SHARE), None] + [None] * 7,
        [None],
        [out((BLOCK, SHARE), jnp.float32)],
        (rank, near, far, *inners, x, gain, residual),
        cost(3_000_000, 3_000_000, 512),
        free=(1, 2, 3, 4, 5, 6),
    )[0]


def per_device(
    hidden_in,
    lengths,
    block_order,
    routes,
    norm_gain_attn,
    w_query,
    w_key,
    w_value,
    w_out,
    norm_gain_moe,
    w_router,
    w_gate,
    w_up,
    w_down,
    out_grad,
):
    dp_count = block_order.shape[0]
    mp_rank = lax.axis_index("mp").astype(jnp.int32)
    column_start = mp_rank * SHARE
    piece = BLOCK // dp_count
    steps = MAXLEN // BLOCK - 1
    rank = mp_rank.reshape(1)
    lane = lax.axis_index("dp").astype(jnp.int32).reshape(1)
    begin = rank * QUARTER
    gain_attn = norm_gain_attn[None, :]
    gain_moe = norm_gain_moe[None, :]
    router_t = jnp.pad(w_router.T, ((0, LANES - EXPERTS), (0, 0)))

    normed, key_value, cosine, sine, reach, wanted, later, live = project(
        lengths, block_order, lane, hidden_in, gain_attn, w_key, w_value
    )
    queries = project_queries(normed, w_query, cosine, sine)
    pieces = to_all(key_value.reshape(dp_count, piece, SHARE))
    picks, ranks = route(begin, after(routes.T, key_value))
    far_out = peer(after(w_out, key_value), 2)
    begun = attend_own(queries, after(key_value, picks))
    picked = pick_pieces(wanted, after(pieces, far_out))
    earlier = to_all(picked.reshape(dp_count, steps * piece, SHARE))
    earlier = earlier.reshape(dp_count, steps, piece, SHARE)

    outs = [w_out, peer(after(w_out, picked), 1), far_out, peer(far_out, 1)]

    grad_rows = jnp.dot(picks, after(out_grad, picked), preferred_element_type=jnp.bfloat16)
    grad_arrived = to_experts(after(grad_rows, earlier, begun[1]).reshape(EXPERTS, QUARTER, WIDTH))
    attended, attended_t, lse = attend(reach, begun, earlier)
    far = peer(attended, 2)
    residual, moe_cat, gates, moe_rows = residual_step(
        [attended, peer(attended, 1), far, peer(far, 1)],
        outs,
        hidden_in,
        gain_moe,
        router_t,
        ranks,
        picks,
    )
    own_pack = pack_weights(after(w_down[0], attended), w_gate[0], w_up[0])
    far_pack = peer(after(own_pack, far), 2)
    packed = [own_pack, peer(own_pack, 1), far_pack, peer(far_pack, 1)]

    grouped = to_experts(after(moe_rows, far_pack).reshape(EXPERTS, QUARTER, -1)).reshape(SLOTS, -1)
    mix = mix_weights(begin, ranks, moe_cat)
    grouped_grad = grad_arrived.reshape(SLOTS, WIDTH)
    rows_out, row_grad, hidden_units, unit_grad = expert_step(lane, grouped, grouped_grad, packed)
    row_home = to_experts(row_grad.reshape(dp_count, QUARTER, -1)).reshape(SLOTS, -1)
    rows_home = to_experts(after(rows_out, row_home).reshape(dp_count, QUARTER, -1)).reshape(SLOTS, -1)

    unit_keep, unit_send = unit_grads(grouped, grouped_grad, hidden_units, unit_grad)
    unit_near = unit_keep.astype(jnp.float32) + peer(unit_send, 1).astype(jnp.float32)
    unit_low = unit_near[1].astype(jnp.bfloat16)
    cut = PACKED // 2
    unit_far_a = peer(unit_low[:cut], 2)
    keep, send = sum_home(rank, after(mix, unit_far_a), row_home)
    near = keep + peer(send, 1).astype(jnp.float32)
    mine = swap_sum(near, peer(near.astype(jnp.bfloat16), 2))
    theirs = peer(mine, 1)
    branch_grad, logit_grad, residual_grad, attended_grad, attended_grad_t, moe_gain = norm_back_step(
        rank, mine, theirs, gates, residual, gain_moe, router_t, out_grad, w_out
    )

    query_pre_grad, own_grads, later_grads = attend_back(
        reach,
        queries,
        begun[0],
        key_value,
        earlier,
        attended_grad,
        attended_grad_t,
        attended_t,
        lse,
        cosine,
        sine,
    )
    unit_far_b = peer(after(unit_low[cut:], later_grads), 2)
    unit_far_b = peer(after(unit_low[cut:], branch_grad), 2)
    later_pieces = to_all(after(later_grads, rows_home, unit_far_b).reshape(dp_count, steps * piece, SHARE))
    summed = sum_pieces(
        later, live, later_pieces.reshape(dp_count * steps, piece, SHARE), dp_count
    )
    kv_home = to_all(summed).reshape(BLOCK, SHARE)
    made = dense_grads(
        branch_grad, attended, normed, query_pre_grad, logit_grad, moe_cat, moe_gain
    )

    every, keep, send, inner = last_grads(
        rank,
        own_grads,
        kv_home,
        query_pre_grad,
        normed,
        hidden_in,
        w_query,
        w_key,
        w_value,
        cosine,
        sine,
        made,
        gain_attn,
    )
    near_norm = keep + peer(send, 1).astype(jnp.float32)
    far_norm = peer(near_norm[BLOCK:].astype(jnp.bfloat16), 2)
    inners = [inner] + [peer(inner, flip) for flip in (1, 2, 3)]
    arrived = to_all(every.reshape(dp_count, WIDTH // dp_count, -1))
    keep, send = sum_home(rank, mix, after(rows_home, every))
    near_mix = keep + peer(send, 1).astype(jnp.float32)
    far_mix = peer(near_mix[BLOCK:].astype(jnp.bfloat16), 2)
    grad_w_gate, grad_w_up, grad_w_down = unit_finish(unit_near, unit_far_a, after(unit_far_b, every))
    dense = jnp.sum(arrived.astype(jnp.float32), axis=0)
    residual_cols = lax.dynamic_slice_in_dim(residual, column_start, SHARE, 1)
    mixture = near_mix[:BLOCK] + after(far_mix, dense).astype(jnp.float32)
    out_hidden = (residual_cols + mixture).astype(jnp.bfloat16)

    grad_hidden = input_finish(
        rank, near_norm, after(far_norm, dense), inners, hidden_in, gain_attn, residual_grad
    )
    at = 3 * SHARE
    attn_gain = dense[:, at + EXPERTS + 8]
    attn_gain = attn_gain + peer(attn_gain, 1) + peer(attn_gain, 2) + peer(attn_gain, 3)
    return (
        out_hidden,
        grad_hidden,
        dense[:, SHARE : 2 * SHARE],
        dense[:, 2 * SHARE : 2 * SHARE + LANES],
        dense[:, 2 * SHARE + LANES : at],
        dense[:, :SHARE].T,
        attn_gain,
        dense[:, at + EXPERTS],
        dense[:, at : at + EXPERTS],
        grad_w_gate,
        grad_w_up,
        grad_w_down,
    )


def solution(mesh):
    in_specs = (
        P("dp", None),
        P(),
        P(),
        P("dp", None),
        P(),
        P(None, "mp"),
        P(None, "mp"),
        P(None, "mp"),
        P("mp", None),
        P(),
        P(),
        P("dp", None, "mp"),
        P("dp", None, "mp"),
        P("dp", "mp", None),
        P("dp", None),
    )
    out_specs = (
        P("dp", "mp"),
        P("dp", "mp"),
        P("dp", "mp"),
        P("dp", "mp"),
        P("dp", "mp"),
        P("mp", "dp"),
        P("dp"),
        P("dp"),
        P("dp", None),
        P("dp", None, "mp"),
        P("dp", None, "mp"),
        P("dp", "mp", None),
    )
    return jax.shard_map(
        per_device, mesh=mesh, in_specs=in_specs, out_specs=out_specs, check_vma=False
    )
```

```python
import jax
import jax.numpy as jnp
import numpy as np
from jax import lax
from jax.experimental import pallas as pl
from jax.experimental.pallas import tpu as pltpu
from jax.sharding import PartitionSpec as P

HEAD_DIM = 64
EXPERTS = 32
BLOCK = 512
MAXLEN = 2048
CAP = 160
WIDTH = 1024
SHARE = 256
QUARTER = 40
SLOTS = 1280
LANES = 128
PACKED = 384

epsilon = 1e-06
residual_mult = 0.22
score_mult = 0.015625
rope_base = 10000.0
masked_score = -1e30

NN = (((1,), (0,)), ((), ()))
NT = (((1,), (1,)), ((), ()))
TN = (((0,), (0,)), ((), ()))


def mm(a, b, dims=NN):
    return lax.dot_general(a, b, dims, preferred_element_type=jnp.float32)


def to_all(x):
    return lax.all_to_all(x, "dp", 0, 0, tiled=True)


def crossed_groups(dp_count=32):
    groups = []
    for chip in range(2):
        for core in range(2):
            groups.append([i * 4 + (chip ^ (i & 1)) * 2 + core for i in range(dp_count)])
    return groups


def to_experts(x):
    return lax.all_to_all(
        x, ("dp", "mp"), 0, 0, axis_index_groups=crossed_groups(x.shape[0]), tiled=True
    )


def peer(x, flip):
    return lax.ppermute(x, "mp", [(i, i ^ flip) for i in range(4)])


def after(x, *others):
    return lax.optimization_barrier((x, *others))[0]


def vmem():
    return pl.BlockSpec(memory_space=pltpu.VMEM)


def smem():
    return pl.BlockSpec(memory_space=pltpu.SMEM)


def tiles(rows, width, row0=0):
    return pl.BlockSpec((rows, width), lambda i: (i + row0, 0))


def fixed(rows, width):
    return pl.BlockSpec((rows, width), lambda i: (0, 0))


def once(*shape):
    return pl.BlockSpec(shape, lambda i: (0,) * len(shape), pipeline_mode=pl.Buffered(1))


def run(kernel, name, steps, in_specs, out_specs, out_shape, args, estimate, scratch=(), free=(), limit=32):
    in_specs = [once(*a.shape) if s is None else s for s, a in zip(in_specs, args)]
    out_specs = [once(*o.shape) if s is None else s for s, o in zip(out_specs, out_shape)]
    args = [
        a
        if s.memory_space is not None or i in free
        else pltpu.with_memory_space_constraint(a, pltpu.HBM)
        for i, (s, a) in enumerate(zip(in_specs, args))
    ]
    out_shape = [
        o if s.memory_space == pltpu.SMEM else pltpu.HBM(o.shape, o.dtype)
        for s, o in zip(out_specs, out_shape)
    ]
    return pl.pallas_call(
        kernel,
        name=name,
        grid=(steps,),
        in_specs=in_specs,
        out_specs=out_specs,
        out_shape=out_shape,
        scratch_shapes=list(scratch),
        compiler_params=pltpu.CompilerParams(vmem_limit_bytes=limit << 20),
        cost_estimate=estimate,
    )(*args)


def out(shape, dtype):
    return jax.ShapeDtypeStruct(shape, dtype)


def cost(flops, moved, exps=0):
    return pl.CostEstimate(flops=flops, bytes_accessed=moved, transcendentals=exps)


def rope_constants():
    frequency = rope_base ** (-(np.arange(HEAD_DIM // 2, dtype=np.float64) * 2.0) / HEAD_DIM)
    wide = np.tile(frequency, 4)[None, :]
    made = []
    for count, apart in ((BLOCK // 16, 16), (16, 1), (8, BLOCK)):
        angles = np.arange(count, dtype=np.float64)[:, None] * apart * wide
        made += [np.cos(angles), np.sin(angles)]
    return [jnp.asarray(a.astype(np.float32)) for a in made]


def half_front(rows):
    lane = lax.broadcasted_iota(jnp.int32, (rows, LANES), 1)
    return (lane % HEAD_DIM) < HEAD_DIM // 2


def turned(chunk, cosine, signed_sine, back=False):
    partner = jnp.where(
        half_front(chunk.shape[0]), pltpu.roll(chunk, 96, 1), pltpu.roll(chunk, 32, 1)
    )
    if back:
        return chunk * cosine - partner * signed_sine
    return chunk * cosine + partner * signed_sine


def block_tables_in(lengths_ref, order_ref, rank_ref, offset_ref, inverse_ref, reach_ref, wanted_ref, later_ref, live_ref):
    count = order_ref.shape[0]
    steps = MAXLEN // BLOCK - 1

    def sequence(s, begin):
        def one(j, at):
            offset_ref[jnp.minimum(at, count - 1)] = j
            return at + 1

        return lax.fori_loop(0, lengths_ref[s], one, begin)

    lax.fori_loop(0, lengths_ref.shape[0], sequence, jnp.int32(0))

    def invert(d, carry):
        inverse_ref[order_ref[d]] = d
        return carry

    lax.fori_loop(0, count, invert, jnp.int32(0))
    reach_ref[0] = offset_ref[order_ref[rank_ref[0]]]

    def look(d, carry):
        packed = order_ref[d]
        for s in range(1, steps + 1):
            wanted_ref[d * steps + s - 1] = inverse_ref[jnp.maximum(packed - s, 0)]
            next_at = jnp.minimum(packed + s, count - 1)
            later_ref[d * steps + s - 1] = inverse_ref[next_at] * steps + s - 1
            is_live = jnp.logical_and(packed + s < count, offset_ref[next_at] >= s)
            live_ref[d * steps + s - 1] = jnp.where(is_live, 1, 0)
        return carry

    lax.fori_loop(0, count, look, jnp.int32(0))


def project_kernel(
    lengths_ref, order_ref, rank_ref, x_ref, gain_ref, wk_ref, wv_ref,
    cos16_ref, sin16_ref, cos1_ref, sin1_ref, cos0_ref, sin0_ref,
    normed_ref, kv_ref, cosine_ref, sine_ref, reach_ref, wanted_ref, later_ref, live_ref,
    offset_ref, inverse_ref,
):
    @pl.when(pl.program_id(0) == 0)
    def _():
        block_tables_in(
            lengths_ref, order_ref, rank_ref, offset_ref, inverse_ref, reach_ref, wanted_ref, later_ref, live_ref
        )

    x = x_ref[...].astype(jnp.float32)
    scale = lax.rsqrt(jnp.mean(x * x, axis=1, keepdims=True) + epsilon)
    normed = (x * scale * gain_ref[...]).astype(jnp.bfloat16)
    normed_ref[...] = normed
    at = reach_ref[0]
    cos0, sin0 = cos0_ref[pl.ds(at, 1), :], sin0_ref[pl.ds(at, 1), :]
    cos16 = cos16_ref[...] * cos0 - sin16_ref[...] * sin0
    sin16 = sin16_ref[...] * cos0 + cos16_ref[...] * sin0
    cos1, sin1 = cos1_ref[...][None], sin1_ref[...][None]
    cosine = (cos16[:, None, :] * cos1 - sin16[:, None, :] * sin1).reshape(x.shape[0], LANES)
    sine = (sin16[:, None, :] * cos1 + cos16[:, None, :] * sin1).reshape(x.shape[0], LANES)
    sine = jnp.where(half_front(x.shape[0]), -sine, sine)
    cosine_ref[...] = cosine
    sine_ref[...] = sine
    kv_ref[:, :LANES] = turned(mm(normed, wk_ref[...]), cosine, sine).astype(jnp.bfloat16)
    kv_ref[:, LANES:] = mm(normed, wv_ref[...]).astype(jnp.bfloat16)


def query_kernel(normed_ref, wq_ref, cosine_ref, sine_ref, q_ref):
    queries = mm(normed_ref[...], wq_ref[...])
    for i in range(0, SHARE, LANES):
        q_ref[:, i : i + LANES] = turned(
            queries[:, i : i + LANES], cosine_ref[...], sine_ref[...]
        ).astype(jnp.bfloat16)


def project_queries(normed, w_query, cosine, sine):
    tile = 256
    return run(
        query_kernel,
        "project_queries",
        BLOCK // tile,
        [tiles(tile, WIDTH), None, tiles(tile, LANES), tiles(tile, LANES)],
        [tiles(tile, SHARE)],
        [out((BLOCK, SHARE), jnp.bfloat16)],
        (normed, w_query, cosine, sine),
        cost(270_000_000, 2_500_000),
    )[0]


def project(lengths, order, rank, x, gain, w_key, w_value):
    tile = 256
    count = order.shape[0]
    steps = MAXLEN // BLOCK - 1
    bf16, f32 = jnp.bfloat16, jnp.float32
    return run(
        project_kernel,
        "project",
        BLOCK // tile,
        [smem()] * 3
        + [tiles(tile, WIDTH), None, None, None]
        + [tiles(tile // 16, LANES)] * 2
        + [None] * 4,
        [tiles(tile, WIDTH), tiles(tile, SHARE)] + [tiles(tile, LANES)] * 2 + [smem()] * 4,
        [out((BLOCK, WIDTH), bf16), out((BLOCK, SHARE), bf16)]
        + [out((BLOCK, LANES), f32)] * 2
        + [out((1,), jnp.int32)]
        + [out((count * steps,), jnp.int32)] * 3,
        (lengths, order, rank, x, gain, w_key, w_value, *rope_constants()),
        cost(540_000_000, 4_000_000, 512),
        [pltpu.SMEM((count,), jnp.int32), pltpu.SMEM((count,), jnp.int32)],
    )


def pick_kernel(wanted_ref, pieces_ref, picked_ref):
    def one(i, carry):
        picked_ref[i] = pieces_ref[wanted_ref[i]]
        return carry

    lax.fori_loop(0, picked_ref.shape[0], one, jnp.int32(0), unroll=4)


def pick_pieces(wanted, pieces):
    shape = out((wanted.shape[0], *pieces.shape[1:]), pieces.dtype)
    return run(
        pick_kernel, "pick_pieces", 1, [smem(), None], [None], [shape], (wanted, pieces), cost(0, 1_100_000), free=(1,)
    )[0]


def sum_kernel(later_ref, live_ref, pieces_ref, sum_ref):
    steps = MAXLEN // BLOCK - 1

    def one(d, carry):
        total = jnp.zeros(sum_ref.shape[1:], jnp.float32)
        for s in range(steps):
            part = pieces_ref[later_ref[d * steps + s]].astype(jnp.float32)
            total = total + jnp.where(live_ref[d * steps + s] == 1, part, 0.0)
        sum_ref[d] = total.astype(sum_ref.dtype)
        return carry

    lax.fori_loop(0, sum_ref.shape[0], one, jnp.int32(0), unroll=2)


def sum_pieces(later, live, pieces, count):
    shape = out((count, *pieces.shape[1:]), pieces.dtype)
    return run(
        sum_kernel,
        "sum_pieces",
        1,
        [smem(), smem(), None],
        [None],
        [shape],
        (later, live, pieces),
        cost(0, 1_100_000),
        free=(2,),
    )[0]


def pack_kernel(down_ref, gate_ref, up_ref, first_ref, second_ref):
    for k in range(4):
        rows = slice(k * SHARE, (k + 1) * SHARE)
        to_ref = (first_ref, second_ref)[k // 2]
        at = (k % 2) * SHARE
        to_ref[:LANES, at : at + SHARE] = down_ref[:, rows]
        to_ref[LANES:, at : at + LANES] = gate_ref[rows, :]
        to_ref[LANES:, at + LANES : at + SHARE] = up_ref[rows, :]


def pack_weights(w_down, w_gate, w_up):
    shape = out((PACKED, 2 * SHARE), jnp.bfloat16)
    return run(
        pack_kernel,
        "pack_weights",
        1,
        [None] * 3,
        [None] * 2,
        [shape] * 2,
        (w_down, w_gate, w_up),
        cost(0, 1_600_000),
    )


def route_kernel(begin_ref, routes_ref, picks_ref, ranks_ref):
    tokens = routes_ref.shape[1]
    expert_at = lax.broadcasted_iota(jnp.int32, (LANES, tokens), 0)
    hits = jnp.zeros((LANES, tokens), jnp.float32)
    for k in range(routes_ref.shape[0]):
        hits = hits + jnp.where(routes_ref[k : k + 1, :] == expert_at, 1.0, 0.0)
    row_at = lax.broadcasted_iota(jnp.int32, (tokens, tokens), 0)
    column_at = lax.broadcasted_iota(jnp.int32, (tokens, tokens), 1)
    before = jnp.where(row_at < column_at, 1.0, 0.0).astype(jnp.bfloat16)
    ranks = jnp.where(hits > 0.5, mm(hits.astype(jnp.bfloat16), before), -1.0)
    ranks_ref[...] = ranks
    slot_at = lax.broadcasted_iota(jnp.int32, (QUARTER, tokens), 0) + begin_ref[0]
    slot_at = slot_at.astype(jnp.float32)
    for e in range(EXPERTS):
        picks_ref[e * QUARTER : (e + 1) * QUARTER, :] = jnp.where(
            ranks[e : e + 1, :] == slot_at, 1.0, 0.0
        ).astype(jnp.bfloat16)


def route(begin, routes_t):
    return run(
        route_kernel,
        "route",
        1,
        [smem(), None],
        [None, None],
        [out((SLOTS, BLOCK), jnp.bfloat16), out((LANES, BLOCK), jnp.float32)],
        (begin, routes_t),
        cost(100_000_000, 1_600_000),
        free=(1,),
    )


def padded_columns(rows_t, out_ref):
    zero = jnp.zeros((HEAD_DIM, rows_t.shape[1]), out_ref.dtype)
    for h in range(4):
        mine = rows_t[h * HEAD_DIM : (h + 1) * HEAD_DIM].astype(out_ref.dtype)
        at = (h // 2) * HEAD_DIM
        out_ref[h, pl.ds(at, HEAD_DIM), :] = mine
        out_ref[h, pl.ds(HEAD_DIM - at, HEAD_DIM), :] = zero


def padded_rows(rows, out_ref):
    n = rows.shape[0]
    lane = lax.broadcasted_iota(jnp.int32, (n, 128), 1)
    for h in range(4):
        pair = rows[:, (h // 2) * 128 : (h // 2) * 128 + 128].astype(jnp.float32)
        if h % 2 != h // 2:
            pair = pltpu.roll(pair, HEAD_DIM, 1)
        own = (lane < HEAD_DIM) if h // 2 == 0 else (lane >= HEAD_DIM)
        out_ref[pl.ds(h * n, n), :] = jnp.where(own, pair, 0.0).astype(out_ref.dtype)


def attend_block(key_rows, value_rows, first, qpad_ref, max_ref, sum_ref, out_t_ref):
    half = BLOCK // 2
    for h in range(4):
        group = (h // 2) * HEAD_DIM
        for t in range(2):
            cols = slice(t * half, (t + 1) * half)
            rows = half if first and t == 0 else BLOCK
            scores = mm(key_rows[:rows], qpad_ref[h, :, cols])
            if first:
                key_at = lax.broadcasted_iota(jnp.int32, scores.shape, 0)
                query_at = lax.broadcasted_iota(jnp.int32, scores.shape, 1) + t * half
                scores = jnp.where(key_at > query_at, masked_score, scores)
            new_max = jnp.max(scores, axis=0, keepdims=True)
            if not first:
                old_max = max_ref[h : h + 1, cols]
                new_max = jnp.maximum(new_max, old_max)
                shrink = jnp.exp(old_max - new_max)
            weights = jnp.exp(scores - new_max)
            total = jnp.sum(weights, axis=0, keepdims=True)
            part = mm(value_rows[:rows], weights.astype(jnp.bfloat16), TN)[group : group + HEAD_DIM]
            mine = pl.ds(h * HEAD_DIM, HEAD_DIM)
            if not first:
                total = total + sum_ref[h : h + 1, cols] * shrink
                part = part + out_t_ref[mine, cols] * shrink
            max_ref[h : h + 1, cols] = new_max
            sum_ref[h : h + 1, cols] = total
            out_t_ref[mine, cols] = part


def attend_own_kernel(q_ref, own_ref, qpad_ref, max_ref, sum_ref, out_t_ref):
    padded_columns(jnp.transpose(q_ref[...].astype(jnp.float32) * score_mult), qpad_ref)
    max_ref[...] = jnp.zeros_like(max_ref)
    sum_ref[...] = jnp.ones_like(sum_ref)
    attend_block(own_ref[:, :LANES], own_ref[:, LANES:], True, qpad_ref, max_ref, sum_ref, out_t_ref)


def attend_own(queries, own_kv):
    return pl.pallas_call(
        attend_own_kernel,
        name="attend_own",
        in_specs=[vmem()] * 2,
        out_specs=[vmem()] * 4,
        out_shape=[
            out((4, LANES, BLOCK), jnp.bfloat16),
            out((8, BLOCK), jnp.float32),
            out((8, BLOCK), jnp.float32),
            out((SHARE, BLOCK), jnp.float32),
        ],
        compiler_params=pltpu.CompilerParams(vmem_limit_bytes=36 << 20),
        cost_estimate=cost(1_000_000_000, 2_000_000, 600_000),
    )(queries, own_kv)


def attend_kernel(
    reach_ref, qpad_ref, max0_ref, sum0_ref, out0_ref, prev_ref, att_ref, out_t_ref, lse_ref, max_ref, sum_ref
):
    max_ref[...] = max0_ref[...]
    sum_ref[...] = sum0_ref[...]
    out_t_ref[...] = out0_ref[...]

    @pl.loop(1, reach_ref[0] + 1)
    def _(step):
        rows = prev_ref[:, pl.ds(step - 1, 1)].reshape(BLOCK, SHARE)
        attend_block(rows[:, :LANES], rows[:, LANES:], False, qpad_ref, max_ref, sum_ref, out_t_ref)

    lse_ref[...] = max_ref[...] + jnp.log(sum_ref[...])
    for h in range(4):
        mine = pl.ds(h * HEAD_DIM, HEAD_DIM)
        out_t_ref[mine, :] = out_t_ref[mine, :] / sum_ref[h : h + 1, :]
    att_ref[...] = jnp.transpose(out_t_ref[...]).astype(jnp.bfloat16)


def attend(reach, begun, earlier):
    return run(
        attend_kernel,
        "attend",
        1,
        [smem()] + [vmem()] * 5,
        [None] * 3,
        [
            out((BLOCK, SHARE), jnp.bfloat16),
            out((SHARE, BLOCK), jnp.float32),
            out((8, BLOCK), jnp.float32),
        ],
        (reach, *begun, earlier),
        cost(4_000_000_000, 3_000_000, 3_000_000),
        [pltpu.VMEM((8, BLOCK), jnp.float32), pltpu.VMEM((8, BLOCK), jnp.float32)],
        limit=36,
    )


def attend_back_kernel(
    reach_ref, q_ref, qpad_ref, own_ref, prev_ref, grad_ref, grad_t_ref, out_t_ref, lse_ref, cos_ref, sin_ref,
    qgrad_ref, own_grad_ref, prev_grad_ref,
    gpad_ref, qrows_ref, grows_ref, ds_ref, p_ref, delta_ref, dq_ref,
):
    half = BLOCK // 2
    q_scaled = q_ref[...].astype(jnp.float32) * score_mult
    padded_rows(q_scaled, qrows_ref)
    padded_columns(grad_t_ref[...], gpad_ref)
    padded_rows(grad_ref[...], grows_ref)
    both = grad_t_ref[...].astype(jnp.float32) * out_t_ref[...]
    for h in range(4):
        delta_ref[h : h + 1, :] = jnp.sum(
            both[h * HEAD_DIM : (h + 1) * HEAD_DIM], axis=0, keepdims=True
        )


    def block(key_rows, value_rows, first):
        for h in range(4):
            for t in range(2):
                cols = slice(t * half, (t + 1) * half)
                wide = slice(h * BLOCK + t * half, h * BLOCK + (t + 1) * half)
                rows = half if first and t == 0 else BLOCK
                scores = mm(key_rows[:rows], qpad_ref[h, :, cols])
                weights = jnp.exp(scores - lse_ref[h : h + 1, cols])
                if first:
                    key_at = lax.broadcasted_iota(jnp.int32, scores.shape, 0)
                    query_at = lax.broadcasted_iota(jnp.int32, scores.shape, 1) + t * half
                    weights = jnp.where(key_at > query_at, 0.0, weights)
                weight_grad = mm(value_rows[:rows], gpad_ref[h, :, cols])
                score_grad = weights * (weight_grad - delta_ref[h : h + 1, cols])
                p_ref[:rows, wide] = weights.astype(jnp.bfloat16)
                ds_ref[:rows, wide] = score_grad.astype(jnp.bfloat16)
                if rows < BLOCK:
                    p_ref[rows:, wide] = jnp.zeros((BLOCK - rows, half), jnp.bfloat16)
                    ds_ref[rows:, wide] = jnp.zeros((BLOCK - rows, half), jnp.bfloat16)
        key_grad = mm(ds_ref[...], qrows_ref[...])
        value_grad = mm(p_ref[...], grows_ref[...])
        for h in range(4):
            group = (h // 2) * HEAD_DIM
            mine = pl.ds(h * HEAD_DIM, HEAD_DIM)
            part = mm(key_rows, ds_ref[:, h * BLOCK : (h + 1) * BLOCK], TN)[group : group + HEAD_DIM]
            dq_ref[mine, :] = part if first else dq_ref[mine, :] + part
        return key_grad, value_grad

    key_grad, value_grad = block(own_ref[:, :LANES], own_ref[:, LANES:], True)
    own_grad_ref[:, :LANES] = key_grad
    own_grad_ref[:, LANES:] = value_grad

    @pl.loop(1, reach_ref[0] + 1)
    def _(step):
        rows = prev_ref[:, pl.ds(step - 1, 1)].reshape(BLOCK, SHARE)
        key_grad, value_grad = block(rows[:, :LANES], rows[:, LANES:], False)
        parts = prev_grad_ref.shape[0]
        shape = (parts, 1, BLOCK // parts, LANES)
        prev_grad_ref[:, pl.ds(step - 1, 1), :, :LANES] = key_grad.astype(jnp.bfloat16).reshape(shape)
        prev_grad_ref[:, pl.ds(step - 1, 1), :, LANES:] = value_grad.astype(jnp.bfloat16).reshape(shape)

    query_grad = jnp.transpose(dq_ref[...]) * score_mult
    for i in range(0, SHARE, LANES):
        qgrad_ref[:, i : i + LANES] = turned(
            query_grad[:, i : i + LANES], cos_ref[...], sin_ref[...], back=True
        ).astype(jnp.bfloat16)


def attend_back(reach, queries, padded, own_kv, earlier, grad, grad_t, out_t, lse, cosine, signed_sine):
    return run(
        attend_back_kernel,
        "attend_back",
        1,
        [smem()] + [vmem()] * 10,
        [None] * 3,
        [
            out((BLOCK, SHARE), jnp.bfloat16),
            out((BLOCK, SHARE), jnp.float32),
            out(earlier.shape, jnp.bfloat16),
        ],
        (reach, queries, padded, own_kv, earlier, grad, grad_t, out_t, lse, cosine, signed_sine),
        cost(12_000_000_000, 5_000_000, 3_000_000),
        [
            pltpu.VMEM((4, LANES, BLOCK), jnp.bfloat16),
            pltpu.VMEM((4 * BLOCK, LANES), jnp.bfloat16),
            pltpu.VMEM((4 * BLOCK, LANES), jnp.bfloat16),
            pltpu.VMEM((BLOCK, 4 * BLOCK), jnp.bfloat16),
            pltpu.VMEM((BLOCK, 4 * BLOCK), jnp.bfloat16),
            pltpu.VMEM((8, BLOCK), jnp.float32),
            pltpu.VMEM((SHARE, BLOCK), jnp.float32),
        ],
        limit=36,
    )


def residual_kernel(
    a0, a1, a2, a3, w0, w1, w2, w3, x_ref, gain_ref, router_ref, ranks_ref, picks_ref,
    residual_ref, moe_ref, gates_ref, rows_ref, held_ref,
):
    step = pl.program_id(0)
    tile = x_ref.shape[0]

    @pl.when(step < BLOCK // tile)
    def _():
        branch = mm(a0[...], w0[...])
        for a, w in ((a1, w1), (a2, w2), (a3, w3)):
            branch = branch + mm(a[...], w[...])
        residual = x_ref[...].astype(jnp.float32) + residual_mult * branch
        residual_ref[...] = residual
        scale = lax.rsqrt(jnp.mean(residual * residual, axis=1, keepdims=True) + epsilon)
        moe_in = (residual * scale * gain_ref[...]).astype(jnp.bfloat16)
        moe_ref[:, :WIDTH] = moe_in
        logits = mm(router_ref[...], moe_in, NT)
        chosen = ranks_ref[...] >= 0.0
        kept = jnp.where(chosen, logits, masked_score)
        top = jnp.max(kept, axis=0, keepdims=True)
        raised = jnp.where(chosen, jnp.exp(kept - top), 0.0)
        gates = raised / jnp.sum(raised, axis=0, keepdims=True)
        gates_ref[...] = gates
        low = (residual_mult * jnp.transpose(gates)).astype(jnp.bfloat16)
        moe_ref[:, WIDTH:] = low
        held_ref[pl.ds(step * tile, tile), :WIDTH] = moe_in
        held_ref[pl.ds(step * tile, tile), WIDTH:] = low

    @pl.when(step >= BLOCK // tile)
    def _():
        rows_ref[...] = mm(picks_ref[...], held_ref[...]).astype(jnp.bfloat16)


def residual_step(attended, w_out, x, gain, router_t, ranks, picks):
    tile = 256
    first = BLOCK // tile
    slot_tile = SLOTS // 4

    def early(rows, width):
        return pl.BlockSpec((rows, width), lambda i: (jnp.minimum(i, first - 1), 0))

    def late(rows, width):
        return pl.BlockSpec((rows, width), lambda i: (jnp.maximum(i - first, 0), 0))

    by_columns = pl.BlockSpec((LANES, tile), lambda i: (0, jnp.minimum(i, first - 1)))
    return run(
        residual_kernel,
        "residual_step",
        first + 4,
        [early(tile, SHARE)] * 4
        + [None] * 4
        + [early(tile, WIDTH), None, None, by_columns, late(slot_tile, BLOCK)],
        [early(tile, WIDTH), early(tile, WIDTH + LANES), by_columns, late(slot_tile, WIDTH + LANES)],
        [
            out((BLOCK, WIDTH), jnp.float32),
            out((BLOCK, WIDTH + LANES), jnp.bfloat16),
            out((LANES, BLOCK), jnp.float32),
            out((SLOTS, WIDTH + LANES), jnp.bfloat16),
        ],
        (*attended, *w_out, x, gain, router_t, ranks, picks),
        cost(2_700_000_000, 12_000_000, 70_000),
        [pltpu.VMEM((BLOCK, WIDTH + LANES), jnp.bfloat16)],
        free=(1, 2, 3, 5, 6, 7, 10),
    )


def mix_kernel(begin_ref, ranks_ref, moe_ref, mix_ref):
    ranks = jnp.transpose(ranks_ref[...]).astype(jnp.bfloat16)
    gates = moe_ref[:, WIDTH:]
    width = 640
    for at in range(0, SLOTS, width):
        expert_at = lax.broadcasted_iota(jnp.int32, (LANES, width), 0)
        first = expert_at * QUARTER - at
        slot_at = lax.broadcasted_iota(jnp.int32, (LANES, width), 1)
        inside = jnp.logical_and(slot_at >= first, slot_at < first + QUARTER)
        spread = jnp.where(inside, 1.0, 0.0).astype(jnp.bfloat16)
        within = jnp.sum(jnp.where(inside, slot_at - first, 0), axis=0, keepdims=True) + begin_ref[0]
        hit = mm(ranks, spread) == within.astype(jnp.float32)
        mix_ref[:, at : at + width] = jnp.where(hit, mm(gates, spread), 0.0).astype(jnp.bfloat16)


def mix_weights(begin, ranks, moe_cat):
    return run(
        mix_kernel,
        "mix_weights",
        1,
        [smem(), None, None],
        [None],
        [out((BLOCK, SLOTS), jnp.bfloat16)],
        (begin, ranks, moe_cat),
        cost(350_000_000, 3_000_000),
    )[0]


def expert_kernel(lane_ref, x_ref, grad_ref, *refs):
    packed = [refs[2 * j : 2 * j + 2] for j in range(4)]
    out_ref, row_ref, hidden_ref, units_ref = refs[8:]

    def block(j, k):
        return packed[j][k // 2], slice((k % 2) * SHARE, (k % 2 + 1) * SHARE)

    rows = out_ref.shape[0]
    here = pl.ds(pl.program_id(0) * rows, rows)
    lane = lax.broadcasted_iota(jnp.int32, (rows, LANES), 1) == lane_ref[0]
    gate = jnp.sum(
        jnp.where(lane, x_ref[here, WIDTH:].astype(jnp.float32), 0.0), axis=1, keepdims=True
    )
    x = x_ref[here, :WIDTH]
    grad = grad_ref[...]
    gates, ups, sigmoids, hidden = [], [], [], []
    for j in range(4):
        pre = None
        for k in range(4):
            p, columns = block(j, k)
            term = mm(x[:, k * SHARE : (k + 1) * SHARE], p[LANES:, columns])
            pre = term if pre is None else pre + term
        gate_pre, up_pre = pre[:, :LANES], pre[:, LANES:]
        sigmoid = 1.0 / (1.0 + jnp.exp(-gate_pre))
        gates.append(gate_pre)
        ups.append(up_pre)
        sigmoids.append(sigmoid)
        hidden.append(gate_pre * sigmoid * up_pre)
    hidden_low = jnp.concatenate([h.astype(jnp.bfloat16) for h in hidden], axis=1)
    down = jnp.concatenate(
        [jnp.concatenate([p[:LANES, :] for p in pair], axis=1) for pair in packed], axis=0
    )
    made = mm(hidden_low, down).astype(jnp.bfloat16)
    out_ref[...] = made
    gate_grad = jnp.sum(grad.astype(jnp.float32) * made.astype(jnp.float32), axis=1, keepdims=True)
    row_ref[:, WIDTH:] = jnp.where(lane, gate_grad, 0.0).astype(jnp.bfloat16)
    hidden_grad = mm(grad, down, NT)
    row = None
    for j in range(4):
        part = hidden_grad[:, j * LANES : (j + 1) * LANES]
        silu = gates[j] * sigmoids[j]
        gate_pre_grad = part * ups[j] * sigmoids[j] * (1.0 + gates[j] * (1.0 - sigmoids[j]))
        up_pre_grad = part * silu
        hidden_ref[:, j * LANES : (j + 1) * LANES] = (hidden[j] * gate).astype(jnp.bfloat16)
        units_ref[:, j * SHARE : j * SHARE + LANES] = (gate_pre_grad * gate).astype(jnp.bfloat16)
        units_ref[:, j * SHARE + LANES : (j + 1) * SHARE] = (up_pre_grad * gate).astype(jnp.bfloat16)
        both = jnp.concatenate([gate_pre_grad, up_pre_grad], axis=1).astype(jnp.bfloat16)
        terms = []
        for k in range(4):
            p, columns = block(j, k)
            terms.append(mm(both, p[LANES:, columns], NT))
        row = terms if row is None else [a + b for a, b in zip(row, terms)]
    for k in range(4):
        row_ref[:, k * SHARE : (k + 1) * SHARE] = row[k].astype(jnp.bfloat16)


def expert_step(lane, x, grad, packed):
    tile = 320
    return run(
        expert_kernel,
        "expert_step",
        SLOTS // tile,
        [smem(), vmem(), tiles(tile, WIDTH)] + [None] * 8,
        [tiles(tile, WIDTH), tiles(tile, WIDTH + LANES), tiles(tile, 512), tiles(tile, WIDTH)],
        [
            out((SLOTS, WIDTH), jnp.bfloat16),
            out((SLOTS, WIDTH + LANES), jnp.bfloat16),
            out((SLOTS, 512), jnp.bfloat16),
            out((SLOTS, WIDTH), jnp.bfloat16),
        ],
        (lane, x, grad, *packed),
        cost(8_000_000_000, 18_000_000, 700_000),
        limit=40,
    )


def unit_grads_kernel(x_ref, grad_ref, hidden_ref, units_ref, keep_ref, send_ref, turned_ref):
    step = pl.program_id(0)

    @pl.when(step == 0)
    def _():
        for k in range(4):
            columns = slice(k * SHARE, (k + 1) * SHARE)
            turned_ref[columns, :] = jnp.transpose(x_ref[:, columns])

    def write(to_ref):
        to_ref[0, :LANES, :] = mm(hidden_ref[...], grad_ref[...], TN).astype(jnp.bfloat16)
        for k in range(4):
            columns = slice(k * SHARE, (k + 1) * SHARE)
            to_ref[0, LANES:, columns] = mm(turned_ref[columns, :], units_ref[...]).astype(jnp.bfloat16)

    @pl.when(step < 2)
    def _():
        write(keep_ref)

    @pl.when(step >= 2)
    def _():
        write(send_ref)


def unit_grads(x, grad, hidden, units):
    rows = SHARE + LANES

    def share_of(i):
        return jnp.where(i < 2, 2 * i, 2 * i - 3)

    return run(
        unit_grads_kernel,
        "unit_grads",
        4,
        [
            vmem(),
            None,
            pl.BlockSpec((SLOTS, LANES), lambda i: (0, share_of(i))),
            pl.BlockSpec((SLOTS, SHARE), lambda i: (0, share_of(i))),
        ],
        [
            pl.BlockSpec((1, rows, WIDTH), lambda i: (jnp.minimum(i, 1), 0, 0)),
            pl.BlockSpec((1, rows, WIDTH), lambda i: (jnp.maximum(i - 2, 0), 0, 0)),
        ],
        [out((2, rows, WIDTH), jnp.bfloat16), out((2, rows, WIDTH), jnp.bfloat16)],
        (x, grad, hidden, units),
        cost(4_000_000_000, 12_000_000),
        [pltpu.VMEM((WIDTH, SLOTS), jnp.bfloat16)],
        limit=36,
    )


def unit_finish_kernel(mine_ref, first_ref, second_ref, third_ref, gate_ref, up_ref, down_ref):
    got = jnp.concatenate([first_ref[...], second_ref[...], third_ref[...]], axis=0)
    total = mine_ref[0] + got.astype(jnp.float32)
    down_ref[0] = total[:LANES, :]
    for k in range(4):
        rows = slice(k * SHARE, (k + 1) * SHARE)
        gate_ref[0, rows, :] = total[LANES:, k * SHARE : k * SHARE + LANES]
        up_ref[0, rows, :] = total[LANES:, k * SHARE + LANES : (k + 1) * SHARE]


def unit_finish(mine, first, second, third):
    return run(
        unit_finish_kernel,
        "unit_finish",
        1,
        [once(1, PACKED, WIDTH), None, None, None],
        [None] * 3,
        [
            out((1, WIDTH, LANES), jnp.float32),
            out((1, WIDTH, LANES), jnp.float32),
            out((1, LANES, WIDTH), jnp.float32),
        ],
        (mine, first, second, third),
        cost(1_000_000, 3_000_000),
        free=(0, 1, 2, 3),
    )


def home_kernel(rank_ref, mix_ref, rows_ref, keep_ref, send_ref):
    rank = rank_ref[0]
    extra = rows_ref.shape[1] > WIDTH
    for j in range(4):
        at = pl.multiple_of(jnp.bitwise_xor(rank, j) * SHARE, SHARE)
        total = mm(mix_ref[...], rows_ref[:, pl.ds(at, SHARE)])
        to_ref = send_ref if j % 2 else keep_ref
        to_ref[(j // 2) * BLOCK : (j // 2 + 1) * BLOCK, :] = total.astype(to_ref.dtype)
    if extra:
        gate_grads = jnp.transpose(mm(mix_ref[...], rows_ref[:, WIDTH:]))[:EXPERTS]
        for to_ref in (keep_ref, send_ref):
            for i in range(2):
                at = 2 * BLOCK + i * EXPERTS
                to_ref[at : at + EXPERTS, :] = gate_grads[:, i * SHARE : (i + 1) * SHARE].astype(
                    to_ref.dtype
                )


def sum_home(rank, mix, rows):
    height = 2 * BLOCK + (2 * EXPERTS if rows.shape[1] > WIDTH else 0)
    return run(
        home_kernel,
        "sum_home",
        1,
        [smem(), None, vmem()],
        [None] * 2,
        [out((height, SHARE), jnp.float32), out((height, SHARE), jnp.bfloat16)],
        (rank, mix, rows),
        cost(1_500_000_000, 6_000_000),
        limit=36,
    )


def swap_kernel(mine_ref, got_ref, total_ref):
    mine, got = mine_ref, got_ref
    half = BLOCK
    total_ref[:half] = (mine[:half] + got[half : 2 * half].astype(jnp.float32)).astype(total_ref.dtype)
    total_ref[half : 2 * half] = (
        mine[half : 2 * half] + got[:half].astype(jnp.float32)
    ).astype(total_ref.dtype)
    total_ref[2 * half :] = (mine[2 * half :] + got[2 * half :].astype(jnp.float32)).astype(
        total_ref.dtype
    )


def swap_sum(mine, got):
    return run(
        swap_kernel,
        "swap_sum",
        1,
        [None] * 2,
        [None],
        [out(mine.shape, jnp.bfloat16)],
        (mine, got),
        cost(1_000_000, 2_500_000),
        free=(0, 1),
    )[0]


def norm_back_kernel(
    rank_ref, g0, g2, g1, g3, z_ref, gates_ref, residual_ref, gain_ref, router_ref, grad_ref, w_ref,
    low_ref, logit_ref, own_ref, att_ref, att_t_ref, gain_grad_ref, u_ref,
):
    rank = rank_ref[0]
    for flip, part in enumerate((g0, g1, g2, g3)):
        at = pl.multiple_of(jnp.bitwise_xor(rank, flip) * SHARE, SHARE)
        u_ref[:, pl.ds(at, SHARE)] = part[...].astype(jnp.float32)
    weighted_grads = z_ref[...].astype(jnp.float32)
    gates = gates_ref[:EXPERTS, :]
    inner = jnp.sum(weighted_grads, axis=0, keepdims=True)
    logit_grad = (weighted_grads - gates * inner).astype(jnp.bfloat16)
    logit_ref[...] = logit_grad
    u = u_ref[...] + mm(logit_grad, router_ref[:EXPERTS, :], TN)
    v = residual_ref[...]
    scale = lax.rsqrt(jnp.mean(v * v, axis=1, keepdims=True) + epsilon)
    weighted = u * gain_ref[...]
    mean = jnp.mean(weighted * v, axis=1, keepdims=True)
    total = grad_ref[...].astype(jnp.float32) + scale * weighted - v * (scale * scale * scale * mean)

    @pl.when(pl.program_id(0) == 0)
    def _():
        gain_grad_ref[...] = jnp.zeros_like(gain_grad_ref)

    gain_grad_ref[0:1, :] += jnp.sum(u * v * scale, axis=0, keepdims=True)
    low = (residual_mult * total).astype(jnp.bfloat16)
    low_ref[...] = low
    u_ref[...] = total
    own_ref[...] = u_ref[:, pl.ds(pl.multiple_of(rank * SHARE, SHARE), SHARE)]
    att_ref[...] = mm(low, w_ref[...], NT).astype(jnp.bfloat16)
    att_t_ref[...] = mm(w_ref[...], low, NT).astype(jnp.bfloat16)


def norm_back_step(rank, mine, theirs, gates, residual, gain, router_t, out_grad, w_out):
    tile = 256
    by_columns = pl.BlockSpec((EXPERTS, tile), lambda i: (0, i))
    return run(
        norm_back_kernel,
        "norm_back_step",
        BLOCK // tile,
        [smem()]
        + [tiles(tile, SHARE), tiles(tile, SHARE, BLOCK // tile)] * 2
        + [
            tiles(EXPERTS, SHARE, 2 * BLOCK // EXPERTS),
            pl.BlockSpec((LANES, tile), lambda i: (0, i)),
            tiles(tile, WIDTH),
            None,
            None,
            tiles(tile, WIDTH),
            None,
        ],
        [
            tiles(tile, WIDTH),
            by_columns,
            tiles(tile, SHARE),
            tiles(tile, SHARE),
            pl.BlockSpec((SHARE, tile), lambda i: (0, i)),
            fixed(8, WIDTH),
        ],
        [
            out((BLOCK, WIDTH), jnp.bfloat16),
            out((EXPERTS, BLOCK), jnp.bfloat16),
            out((BLOCK, SHARE), jnp.float32),
            out((BLOCK, SHARE), jnp.bfloat16),
            out((SHARE, BLOCK), jnp.bfloat16),
            out((8, WIDTH), jnp.float32),
        ],
        (rank, mine, mine, theirs, theirs, mine, gates, residual, gain, router_t, out_grad, w_out),
        cost(700_000_000, 9_000_000, 512),
        [pltpu.VMEM((tile, WIDTH), jnp.float32)],
        free=(3, 4, 9),
    )


def dense_grads_kernel(low_ref, attended_ref, normed_ref, qgrad_ref, logit_ref, moe_ref, gain_ref, made_ref):
    made_ref[:, :SHARE] = mm(low_ref[...], attended_ref[...], TN).astype(jnp.bfloat16)
    made_ref[:, SHARE : 2 * SHARE] = mm(normed_ref[...], qgrad_ref[...], TN).astype(jnp.bfloat16)
    router = mm(logit_ref[...], moe_ref[:, :WIDTH])
    stacked = jnp.concatenate(
        [router, gain_ref[...], jnp.zeros((LANES - EXPERTS - 8, WIDTH), jnp.float32)], axis=0
    )
    made_ref[:, 2 * SHARE :] = jnp.transpose(stacked).astype(jnp.bfloat16)


def dense_grads(low, attended, normed, qgrad, logit, moe_cat, gain_grad):
    return run(
        dense_grads_kernel,
        "dense_grads",
        1,
        [None] * 7,
        [None],
        [out((WIDTH, 2 * SHARE + LANES), jnp.bfloat16)],
        (low, attended, normed, qgrad, logit, moe_cat, gain_grad),
        cost(600_000_000, 6_000_000),
    )[0]


def last_grads_kernel(
    rank_ref, own_ref, home_ref, qgrad_ref, normed_ref, x_ref, wq_ref, wk_ref, wv_ref, cos_ref, sin_ref, made_ref,
    gain_ref, all_ref, keep_ref, send_ref, inner_ref, part_ref,
):
    rank = rank_ref[0]
    kv = own_ref[...] + home_ref[...].astype(jnp.float32)
    key_grad = turned(kv[:, :LANES], cos_ref[...], sin_ref[...], back=True).astype(jnp.bfloat16)
    value_grad = kv[:, LANES:].astype(jnp.bfloat16)
    both = jnp.concatenate([key_grad, value_grad], axis=1)
    all_ref[:, : 2 * SHARE] = made_ref[:, : 2 * SHARE]
    all_ref[:, 2 * SHARE : 3 * SHARE] = mm(normed_ref[...], both, TN).astype(jnp.bfloat16)
    gain = jnp.zeros((1, WIDTH), jnp.float32)
    tile = 128
    for i in range(0, BLOCK, tile):
        rows = slice(i, i + tile)
        part = mm(qgrad_ref[rows, :], wq_ref[...], NT)
        part = part + mm(key_grad[rows], wk_ref[...], NT) + mm(value_grad[rows], wv_ref[...], NT)
        x = x_ref[rows, :].astype(jnp.float32)
        scale = lax.rsqrt(jnp.mean(x * x, axis=1, keepdims=True) + epsilon)
        along = part * x
        gain = gain + jnp.sum(along * scale, axis=0, keepdims=True)
        inner = jnp.sum(along * gain_ref[...], axis=1, keepdims=True)
        inner_ref[:, rows] = jnp.transpose(jnp.broadcast_to(inner, (tile, LANES)))[:8]
        part_ref[rows, :] = part
    for j in range(4):
        at = pl.multiple_of(jnp.bitwise_xor(rank, j) * SHARE, SHARE)
        to_ref = send_ref if j % 2 else keep_ref
        to_ref[(j // 2) * BLOCK : (j // 2 + 1) * BLOCK, :] = part_ref[:, pl.ds(at, SHARE)].astype(to_ref.dtype)
    lane = lax.broadcasted_iota(jnp.int32, (WIDTH, LANES), 1)
    column = jnp.transpose(jnp.broadcast_to(gain, (LANES, WIDTH)))
    rest = jnp.where(lane == EXPERTS + 8, column, made_ref[:, 2 * SHARE :].astype(jnp.float32))
    all_ref[:, 3 * SHARE :] = rest.astype(jnp.bfloat16)


def last_grads(rank, own, home, qgrad, normed, x, w_query, w_key, w_value, cosine, sine, made, gain):
    return run(
        last_grads_kernel,
        "last_grads",
        1,
        [smem()] + [None] * 12,
        [None] * 4,
        [
            out((WIDTH, 3 * SHARE + LANES), jnp.bfloat16),
            out((2 * BLOCK, SHARE), jnp.float32),
            out((2 * BLOCK, SHARE), jnp.bfloat16),
            out((8, BLOCK), jnp.float32),
        ],
        (rank, own, home, qgrad, normed, x, w_query, w_key, w_value, cosine, sine, made, gain),
        cost(1_000_000_000, 8_000_000, 512),
        [pltpu.VMEM((BLOCK, WIDTH), jnp.float32)],
        free=(2,),
    )


def input_finish_kernel(
    rank_ref, near_ref, far_ref, i0, i1, i2, i3, x_ref, gain_ref, residual_ref, made_ref
):
    mine = pl.ds(pl.multiple_of(rank_ref[0] * SHARE, SHARE), SHARE)
    x = x_ref[...].astype(jnp.float32)
    scale = lax.rsqrt(jnp.mean(x * x, axis=1, keepdims=True) + epsilon)
    inner = (i0[...] + i1[...] + i2[...] + i3[...]) * (1.0 / WIDTH)
    inner = jnp.transpose(jnp.broadcast_to(inner[:1], (LANES, BLOCK)))[:, :1]
    weighted = (near_ref[...] + far_ref[...].astype(jnp.float32)) * gain_ref[:, mine]
    x_own = x_ref[:, mine].astype(jnp.float32)
    made_ref[...] = residual_ref[...] + scale * weighted - x_own * (scale * scale * scale * inner)


def input_finish(rank, near, far, inners, x, gain, residual):
    return run(
        input_finish_kernel,
        "input_finish",
        1,
        [smem(), once(BLOCK, SHARE), None] + [None] * 7,
        [None],
        [out((BLOCK, SHARE), jnp.float32)],
        (rank, near, far, *inners, x, gain, residual),
        cost(3_000_000, 3_000_000, 512),
        free=(1, 2, 3, 4, 5, 6),
    )[0]


def per_device(
    hidden_in,
    lengths,
    block_order,
    routes,
    norm_gain_attn,
    w_query,
    w_key,
    w_value,
    w_out,
    norm_gain_moe,
    w_router,
    w_gate,
    w_up,
    w_down,
    out_grad,
):
    dp_count = block_order.shape[0]
    mp_rank = lax.axis_index("mp").astype(jnp.int32)
    column_start = mp_rank * SHARE
    piece = BLOCK // dp_count
    steps = MAXLEN // BLOCK - 1
    rank = mp_rank.reshape(1)
    lane = lax.axis_index("dp").astype(jnp.int32).reshape(1)
    begin = rank * QUARTER
    gain_attn = norm_gain_attn[None, :]
    gain_moe = norm_gain_moe[None, :]
    router_t = jnp.pad(w_router.T, ((0, LANES - EXPERTS), (0, 0)))

    far_out = peer(w_out, 2)
    own_pack = pack_weights(w_down[0], w_gate[0], w_up[0])

    normed, key_value, cosine, sine, reach, wanted, later, live = project(
        lengths, block_order, lane, hidden_in, gain_attn, w_key, w_value
    )
    queries = project_queries(normed, w_query, cosine, sine)
    pieces = to_all(key_value.reshape(dp_count, piece, SHARE))
    picks, ranks = route(begin, after(routes.T, key_value))
    begun = attend_own(queries, after(key_value, picks))
    picked = pick_pieces(wanted, after(pieces, far_out))
    far_first = peer(after(own_pack[0], picked), 2)
    earlier = to_all(picked.reshape(dp_count, steps * piece, SHARE))
    earlier = earlier.reshape(dp_count, steps, piece, SHARE)

    outs = [w_out, peer(after(w_out, picked), 1), far_out, peer(far_out, 1)]

    grad_rows = jnp.dot(picks, after(out_grad, picked), preferred_element_type=jnp.bfloat16)
    grad_arrived = to_experts(after(grad_rows, earlier, begun[1], far_first).reshape(EXPERTS, QUARTER, WIDTH))
    attended, attended_t, lse = attend(reach, begun, earlier)
    far = peer(attended, 2)
    residual, moe_cat, gates, moe_rows = residual_step(
        [attended, peer(attended, 1), far, peer(far, 1)],
        outs,
        hidden_in,
        gain_moe,
        router_t,
        ranks,
        picks,
    )
    far_second = peer(after(own_pack[1], moe_rows), 2)
    far_pack = [far_first, far_second]
    packed = [*own_pack, *[peer(a, 1) for a in own_pack], *far_pack, *[peer(a, 1) for a in far_pack]]
    grouped = to_experts(moe_rows.reshape(EXPERTS, QUARTER, -1)).reshape(SLOTS, -1)
    mix = mix_weights(begin, ranks, moe_cat)
    grouped_grad = grad_arrived.reshape(SLOTS, WIDTH)
    rows_out, row_grad, hidden_units, unit_grad = expert_step(lane, grouped, grouped_grad, packed)
    row_home = to_experts(row_grad.reshape(dp_count, QUARTER, -1)).reshape(SLOTS, -1)
    rows_home = to_experts(after(rows_out, row_home).reshape(dp_count, QUARTER, -1)).reshape(SLOTS, -1)

    unit_keep, unit_send = unit_grads(grouped, grouped_grad, hidden_units, unit_grad)
    unit_near = unit_keep.astype(jnp.float32) + peer(unit_send, 1).astype(jnp.float32)
    unit_low = unit_near[1].astype(jnp.bfloat16)
    cut = PACKED // 2
    unit_far_a = peer(unit_low[:cut], 2)
    keep, send = sum_home(rank, after(mix, unit_far_a), row_home)
    near = keep + peer(send, 1).astype(jnp.float32)
    mine = swap_sum(near, peer(near.astype(jnp.bfloat16), 2))
    theirs = peer(mine, 1)
    branch_grad, logit_grad, residual_grad, attended_grad, attended_grad_t, moe_gain = norm_back_step(
        rank, mine, theirs, gates, residual, gain_moe, router_t, out_grad, w_out
    )

    query_pre_grad, own_grads, later_grads = attend_back(
        reach,
        queries,
        begun[0],
        key_value,
        earlier,
        attended_grad,
        attended_grad_t,
        attended_t,
        lse,
        cosine,
        sine,
    )
    unit_far_b = peer(after(unit_low[cut:], later_grads), 2)
    unit_far_b = peer(after(unit_low[cut : cut + cut // 2], branch_grad), 2)
    later_pieces = to_all(after(later_grads, rows_home, unit_far_b).reshape(dp_count, steps * piece, SHARE))
    summed = sum_pieces(
        later, live, later_pieces.reshape(dp_count * steps, piece, SHARE), dp_count
    )
    kv_home = to_all(summed).reshape(BLOCK, SHARE)
    made = dense_grads(
        branch_grad, attended, normed, query_pre_grad, logit_grad, moe_cat, moe_gain
    )

    unit_far_c = peer(after(unit_low[cut + cut // 2 :], kv_home, made), 2)

    every, keep, send, inner = last_grads(
        rank,
        own_grads,
        kv_home,
        query_pre_grad,
        normed,
        hidden_in,
        w_query,
        w_key,
        w_value,
        cosine,
        sine,
        made,
        gain_attn,
    )
    near_norm = keep + peer(send, 1).astype(jnp.float32)
    far_norm = peer(near_norm[BLOCK:].astype(jnp.bfloat16), 2)
    inners = [inner] + [peer(inner, flip) for flip in (1, 2, 3)]
    every = after(every, unit_far_c)
    arrived = to_all(every.reshape(dp_count, WIDTH // dp_count, -1))
    keep, send = sum_home(rank, mix, after(rows_home, every))
    near_mix = keep + peer(send, 1).astype(jnp.float32)
    far_mix = peer(near_mix[BLOCK:].astype(jnp.bfloat16), 2)
    grad_w_gate, grad_w_up, grad_w_down = unit_finish(
        unit_near, unit_far_a, after(unit_far_b, every), unit_far_c
    )
    dense = jnp.sum(arrived.astype(jnp.float32), axis=0)
    at = 3 * SHARE
    attn_gain = dense[:, at + EXPERTS + 8]
    attn_gain = attn_gain + peer(attn_gain, 1) + peer(attn_gain, 2) + peer(attn_gain, 3)
    residual_cols = lax.dynamic_slice_in_dim(residual, column_start, SHARE, 1)
    mixture = near_mix[:BLOCK] + after(far_mix, attn_gain).astype(jnp.float32)
    out_hidden = (residual_cols + mixture).astype(jnp.bfloat16)

    grad_hidden = input_finish(
        rank, near_norm, after(far_norm, dense), inners, hidden_in, gain_attn, residual_grad
    )
    return (
        out_hidden,
        grad_hidden,
        dense[:, SHARE : 2 * SHARE],
        dense[:, 2 * SHARE : 2 * SHARE + LANES],
        dense[:, 2 * SHARE + LANES : at],
        dense[:, :SHARE].T,
        attn_gain,
        dense[:, at + EXPERTS],
        dense[:, at : at + EXPERTS],
        grad_w_gate,
        grad_w_up,
        grad_w_down,
    )


def solution(mesh):
    in_specs = (
        P("dp", None),
        P(),
        P(),
        P("dp", None),
        P(),
        P(None, "mp"),
        P(None, "mp"),
        P(None, "mp"),
        P("mp", None),
        P(),
        P(),
        P("dp", None, "mp"),
        P("dp", None, "mp"),
        P("dp", "mp", None),
        P("dp", None),
    )
    out_specs = (
        P("dp", "mp"),
        P("dp", "mp"),
        P("dp", "mp"),
        P("dp", "mp"),
        P("dp", "mp"),
        P("mp", "dp"),
        P("dp"),
        P("dp"),
        P("dp", None),
        P("dp", None, "mp"),
        P("dp", None, "mp"),
        P("dp", "mp", None),
    )
    return jax.shard_map(
        per_device, mesh=mesh, in_specs=in_specs, out_specs=out_specs, check_vma=False
    )
```

```python
import jax
import jax.numpy as jnp
import numpy as np
from jax import lax
from jax.experimental import pallas as pl
from jax.experimental.pallas import tpu as pltpu
from jax.sharding import PartitionSpec as P

HEAD_DIM = 64
EXPERTS = 32
BLOCK = 512
MAXLEN = 2048
CAP = 160
WIDTH = 1024
SHARE = 256
QUARTER = 40
SLOTS = 1280
LANES = 128
PACKED = 384

epsilon = 1e-06
residual_mult = 0.22
score_mult = 0.015625
rope_base = 10000.0
masked_score = -1e30

NN = (((1,), (0,)), ((), ()))
NT = (((1,), (1,)), ((), ()))
TN = (((0,), (0,)), ((), ()))


def mm(a, b, dims=NN):
    return lax.dot_general(a, b, dims, preferred_element_type=jnp.float32)


def to_all(x):
    return lax.all_to_all(x, "dp", 0, 0, tiled=True)


def crossed_groups(dp_count=32):
    groups = []
    for chip in range(2):
        for core in range(2):
            groups.append([i * 4 + (chip ^ (i & 1)) * 2 + core for i in range(dp_count)])
    return groups


def to_experts(x):
    return lax.all_to_all(
        x, ("dp", "mp"), 0, 0, axis_index_groups=crossed_groups(x.shape[0]), tiled=True
    )


def peer(x, flip):
    return lax.ppermute(x, "mp", [(i, i ^ flip) for i in range(4)])


def after(x, *others):
    return lax.optimization_barrier((x, *others))[0]


def vmem():
    return pl.BlockSpec(memory_space=pltpu.VMEM)


def smem():
    return pl.BlockSpec(memory_space=pltpu.SMEM)


def tiles(rows, width, row0=0):
    return pl.BlockSpec((rows, width), lambda i: (i + row0, 0))


def fixed(rows, width):
    return pl.BlockSpec((rows, width), lambda i: (0, 0))


def once(*shape):
    return pl.BlockSpec(shape, lambda i: (0,) * len(shape), pipeline_mode=pl.Buffered(1))


def run(kernel, name, steps, in_specs, out_specs, out_shape, args, estimate, scratch=(), free=(), limit=32):
    in_specs = [once(*a.shape) if s is None else s for s, a in zip(in_specs, args)]
    out_specs = [once(*o.shape) if s is None else s for s, o in zip(out_specs, out_shape)]
    args = [
        a
        if s.memory_space is not None or i in free
        else pltpu.with_memory_space_constraint(a, pltpu.HBM)
        for i, (s, a) in enumerate(zip(in_specs, args))
    ]
    out_shape = [
        o if s.memory_space == pltpu.SMEM else pltpu.HBM(o.shape, o.dtype)
        for s, o in zip(out_specs, out_shape)
    ]
    return pl.pallas_call(
        kernel,
        name=name,
        grid=(steps,),
        in_specs=in_specs,
        out_specs=out_specs,
        out_shape=out_shape,
        scratch_shapes=list(scratch),
        compiler_params=pltpu.CompilerParams(vmem_limit_bytes=limit << 20),
        cost_estimate=estimate,
    )(*args)


def out(shape, dtype):
    return jax.ShapeDtypeStruct(shape, dtype)


def cost(flops, moved, exps=0):
    return pl.CostEstimate(flops=flops, bytes_accessed=moved, transcendentals=exps)


def rope_constants():
    frequency = rope_base ** (-(np.arange(HEAD_DIM // 2, dtype=np.float64) * 2.0) / HEAD_DIM)
    wide = np.tile(frequency, 4)[None, :]
    made = []
    for count, apart in ((BLOCK // 16, 16), (16, 1), (8, BLOCK)):
        angles = np.arange(count, dtype=np.float64)[:, None] * apart * wide
        made += [np.cos(angles), np.sin(angles)]
    return [jnp.asarray(a.astype(np.float32)) for a in made]


def half_front(rows):
    lane = lax.broadcasted_iota(jnp.int32, (rows, LANES), 1)
    return (lane % HEAD_DIM) < HEAD_DIM // 2


def turned(chunk, cosine, signed_sine, back=False):
    partner = jnp.where(
        half_front(chunk.shape[0]), pltpu.roll(chunk, 96, 1), pltpu.roll(chunk, 32, 1)
    )
    if back:
        return chunk * cosine - partner * signed_sine
    return chunk * cosine + partner * signed_sine


def block_tables_in(lengths_ref, order_ref, rank_ref, offset_ref, inverse_ref, reach_ref, wanted_ref, later_ref, live_ref):
    count = order_ref.shape[0]
    steps = MAXLEN // BLOCK - 1

    def sequence(s, begin):
        def one(j, at):
            offset_ref[jnp.minimum(at, count - 1)] = j
            return at + 1

        return lax.fori_loop(0, lengths_ref[s], one, begin)

    lax.fori_loop(0, lengths_ref.shape[0], sequence, jnp.int32(0))

    def invert(d, carry):
        inverse_ref[order_ref[d]] = d
        return carry

    lax.fori_loop(0, count, invert, jnp.int32(0))
    reach_ref[0] = offset_ref[order_ref[rank_ref[0]]]

    def look(d, carry):
        packed = order_ref[d]
        for s in range(1, steps + 1):
            wanted_ref[d * steps + s - 1] = inverse_ref[jnp.maximum(packed - s, 0)]
            next_at = jnp.minimum(packed + s, count - 1)
            later_ref[d * steps + s - 1] = inverse_ref[next_at] * steps + s - 1
            is_live = jnp.logical_and(packed + s < count, offset_ref[next_at] >= s)
            live_ref[d * steps + s - 1] = jnp.where(is_live, 1, 0)
        return carry

    lax.fori_loop(0, count, look, jnp.int32(0))


def project_kernel(
    lengths_ref, order_ref, rank_ref, x_ref, gain_ref, wk_ref, wv_ref,
    cos16_ref, sin16_ref, cos1_ref, sin1_ref, cos0_ref, sin0_ref,
    normed_ref, kv_ref, cosine_ref, sine_ref, reach_ref, wanted_ref, later_ref, live_ref,
    offset_ref, inverse_ref,
):
    @pl.when(pl.program_id(0) == 0)
    def _():
        block_tables_in(
            lengths_ref, order_ref, rank_ref, offset_ref, inverse_ref, reach_ref, wanted_ref, later_ref, live_ref
        )

    x = x_ref[...].astype(jnp.float32)
    scale = lax.rsqrt(jnp.mean(x * x, axis=1, keepdims=True) + epsilon)
    normed = (x * scale * gain_ref[...]).astype(jnp.bfloat16)
    normed_ref[...] = normed
    at = reach_ref[0]
    cos0, sin0 = cos0_ref[pl.ds(at, 1), :], sin0_ref[pl.ds(at, 1), :]
    cos16 = cos16_ref[...] * cos0 - sin16_ref[...] * sin0
    sin16 = sin16_ref[...] * cos0 + cos16_ref[...] * sin0
    cos1, sin1 = cos1_ref[...][None], sin1_ref[...][None]
    cosine = (cos16[:, None, :] * cos1 - sin16[:, None, :] * sin1).reshape(x.shape[0], LANES)
    sine = (sin16[:, None, :] * cos1 + cos16[:, None, :] * sin1).reshape(x.shape[0], LANES)
    sine = jnp.where(half_front(x.shape[0]), -sine, sine)
    cosine_ref[...] = cosine
    sine_ref[...] = sine
    kv_ref[:, :LANES] = turned(mm(normed, wk_ref[...]), cosine, sine).astype(jnp.bfloat16)
    kv_ref[:, LANES:] = mm(normed, wv_ref[...]).astype(jnp.bfloat16)


def query_kernel(normed_ref, wq_ref, cosine_ref, sine_ref, q_ref):
    queries = mm(normed_ref[...], wq_ref[...])
    for i in range(0, SHARE, LANES):
        q_ref[:, i : i + LANES] = turned(
            queries[:, i : i + LANES], cosine_ref[...], sine_ref[...]
        ).astype(jnp.bfloat16)


def project_queries(normed, w_query, cosine, sine):
    tile = 256
    return run(
        query_kernel,
        "project_queries",
        BLOCK // tile,
        [tiles(tile, WIDTH), None, tiles(tile, LANES), tiles(tile, LANES)],
        [tiles(tile, SHARE)],
        [out((BLOCK, SHARE), jnp.bfloat16)],
        (normed, w_query, cosine, sine),
        cost(270_000_000, 2_500_000),
    )[0]


def project(lengths, order, rank, x, gain, w_key, w_value):
    tile = 256
    count = order.shape[0]
    steps = MAXLEN // BLOCK - 1
    bf16, f32 = jnp.bfloat16, jnp.float32
    return run(
        project_kernel,
        "project",
        BLOCK // tile,
        [smem()] * 3
        + [tiles(tile, WIDTH), None, None, None]
        + [tiles(tile // 16, LANES)] * 2
        + [None] * 4,
        [tiles(tile, WIDTH), tiles(tile, SHARE)] + [tiles(tile, LANES)] * 2 + [smem()] * 4,
        [out((BLOCK, WIDTH), bf16), out((BLOCK, SHARE), bf16)]
        + [out((BLOCK, LANES), f32)] * 2
        + [out((1,), jnp.int32)]
        + [out((count * steps,), jnp.int32)] * 3,
        (lengths, order, rank, x, gain, w_key, w_value, *rope_constants()),
        cost(540_000_000, 4_000_000, 512),
        [pltpu.SMEM((count,), jnp.int32), pltpu.SMEM((count,), jnp.int32)],
    )


def pick_kernel(wanted_ref, pieces_ref, picked_ref):
    def one(i, carry):
        picked_ref[i] = pieces_ref[wanted_ref[i]]
        return carry

    lax.fori_loop(0, picked_ref.shape[0], one, jnp.int32(0), unroll=4)


def pick_pieces(wanted, pieces):
    shape = out((wanted.shape[0], *pieces.shape[1:]), pieces.dtype)
    return run(
        pick_kernel, "pick_pieces", 1, [smem(), None], [None], [shape], (wanted, pieces), cost(0, 1_100_000), free=(1,)
    )[0]


def sum_kernel(later_ref, live_ref, pieces_ref, sum_ref):
    steps = MAXLEN // BLOCK - 1

    def one(d, carry):
        total = jnp.zeros(sum_ref.shape[1:], jnp.float32)
        for s in range(steps):
            part = pieces_ref[later_ref[d * steps + s]].astype(jnp.float32)
            total = total + jnp.where(live_ref[d * steps + s] == 1, part, 0.0)
        sum_ref[d] = total.astype(sum_ref.dtype)
        return carry

    lax.fori_loop(0, sum_ref.shape[0], one, jnp.int32(0), unroll=2)


def sum_pieces(later, live, pieces, count):
    shape = out((count, *pieces.shape[1:]), pieces.dtype)
    return run(
        sum_kernel,
        "sum_pieces",
        1,
        [smem(), smem(), None],
        [None],
        [shape],
        (later, live, pieces),
        cost(0, 1_100_000),
        free=(2,),
    )[0]


def route_kernel(begin_ref, routes_ref, picks_ref, ranks_ref):
    tokens = routes_ref.shape[1]
    expert_at = lax.broadcasted_iota(jnp.int32, (LANES, tokens), 0)
    hits = jnp.zeros((LANES, tokens), jnp.float32)
    for k in range(routes_ref.shape[0]):
        hits = hits + jnp.where(routes_ref[k : k + 1, :] == expert_at, 1.0, 0.0)
    row_at = lax.broadcasted_iota(jnp.int32, (tokens, tokens), 0)
    column_at = lax.broadcasted_iota(jnp.int32, (tokens, tokens), 1)
    before = jnp.where(row_at < column_at, 1.0, 0.0).astype(jnp.bfloat16)
    ranks = jnp.where(hits > 0.5, mm(hits.astype(jnp.bfloat16), before), -1.0)
    ranks_ref[...] = ranks
    slot_at = lax.broadcasted_iota(jnp.int32, (QUARTER, tokens), 0) + begin_ref[0]
    slot_at = slot_at.astype(jnp.float32)
    for e in range(EXPERTS):
        picks_ref[e * QUARTER : (e + 1) * QUARTER, :] = jnp.where(
            ranks[e : e + 1, :] == slot_at, 1.0, 0.0
        ).astype(jnp.bfloat16)


def route(begin, routes_t):
    return run(
        route_kernel,
        "route",
        1,
        [smem(), None],
        [None, None],
        [out((SLOTS, BLOCK), jnp.bfloat16), out((LANES, BLOCK), jnp.float32)],
        (begin, routes_t),
        cost(100_000_000, 1_600_000),
        free=(1,),
    )


def padded_columns(rows_t, out_ref):
    zero = jnp.zeros((HEAD_DIM, rows_t.shape[1]), out_ref.dtype)
    for h in range(4):
        mine = rows_t[h * HEAD_DIM : (h + 1) * HEAD_DIM].astype(out_ref.dtype)
        at = (h // 2) * HEAD_DIM
        out_ref[h, pl.ds(at, HEAD_DIM), :] = mine
        out_ref[h, pl.ds(HEAD_DIM - at, HEAD_DIM), :] = zero


def padded_rows(rows, out_ref):
    n = rows.shape[0]
    lane = lax.broadcasted_iota(jnp.int32, (n, 128), 1)
    for h in range(4):
        pair = rows[:, (h // 2) * 128 : (h // 2) * 128 + 128].astype(jnp.float32)
        if h % 2 != h // 2:
            pair = pltpu.roll(pair, HEAD_DIM, 1)
        own = (lane < HEAD_DIM) if h // 2 == 0 else (lane >= HEAD_DIM)
        out_ref[pl.ds(h * n, n), :] = jnp.where(own, pair, 0.0).astype(out_ref.dtype)


def attend_block(key_rows, value_rows, first, qpad_ref, max_ref, sum_ref, out_t_ref):
    half = BLOCK // 2
    for h in range(4):
        group = (h // 2) * HEAD_DIM
        for t in range(2):
            cols = slice(t * half, (t + 1) * half)
            rows = half if first and t == 0 else BLOCK
            scores = mm(key_rows[:rows], qpad_ref[h, :, cols])
            if first:
                key_at = lax.broadcasted_iota(jnp.int32, scores.shape, 0)
                query_at = lax.broadcasted_iota(jnp.int32, scores.shape, 1) + t * half
                scores = jnp.where(key_at > query_at, masked_score, scores)
            new_max = jnp.max(scores, axis=0, keepdims=True)
            if not first:
                old_max = max_ref[h : h + 1, cols]
                new_max = jnp.maximum(new_max, old_max)
                shrink = jnp.exp(old_max - new_max)
            weights = jnp.exp(scores - new_max)
            total = jnp.sum(weights, axis=0, keepdims=True)
            part = mm(value_rows[:rows], weights.astype(jnp.bfloat16), TN)[group : group + HEAD_DIM]
            mine = pl.ds(h * HEAD_DIM, HEAD_DIM)
            if not first:
                total = total + sum_ref[h : h + 1, cols] * shrink
                part = part + out_t_ref[mine, cols] * shrink
            max_ref[h : h + 1, cols] = new_max
            sum_ref[h : h + 1, cols] = total
            out_t_ref[mine, cols] = part


def attend_own_kernel(q_ref, own_ref, qpad_ref, max_ref, sum_ref, out_t_ref):
    padded_columns(jnp.transpose(q_ref[...].astype(jnp.float32) * score_mult), qpad_ref)
    max_ref[...] = jnp.zeros_like(max_ref)
    sum_ref[...] = jnp.ones_like(sum_ref)
    attend_block(own_ref[:, :LANES], own_ref[:, LANES:], True, qpad_ref, max_ref, sum_ref, out_t_ref)


def attend_own(queries, own_kv):
    return pl.pallas_call(
        attend_own_kernel,
        name="attend_own",
        in_specs=[vmem()] * 2,
        out_specs=[vmem()] * 4,
        out_shape=[
            out((4, LANES, BLOCK), jnp.bfloat16),
            out((8, BLOCK), jnp.float32),
            out((8, BLOCK), jnp.float32),
            out((SHARE, BLOCK), jnp.float32),
        ],
        compiler_params=pltpu.CompilerParams(vmem_limit_bytes=36 << 20),
        cost_estimate=cost(1_000_000_000, 2_000_000, 600_000),
    )(queries, own_kv)


def attend_kernel(
    reach_ref, qpad_ref, max0_ref, sum0_ref, out0_ref, prev_ref, att_ref, out_t_ref, lse_ref, max_ref, sum_ref
):
    max_ref[...] = max0_ref[...]
    sum_ref[...] = sum0_ref[...]
    out_t_ref[...] = out0_ref[...]

    @pl.loop(1, reach_ref[0] + 1)
    def _(step):
        rows = prev_ref[:, pl.ds(step - 1, 1)].reshape(BLOCK, SHARE)
        attend_block(rows[:, :LANES], rows[:, LANES:], False, qpad_ref, max_ref, sum_ref, out_t_ref)

    lse_ref[...] = max_ref[...] + jnp.log(sum_ref[...])
    for h in range(4):
        mine = pl.ds(h * HEAD_DIM, HEAD_DIM)
        out_t_ref[mine, :] = out_t_ref[mine, :] / sum_ref[h : h + 1, :]
    att_ref[...] = jnp.transpose(out_t_ref[...]).astype(jnp.bfloat16)


def attend(reach, begun, earlier):
    return run(
        attend_kernel,
        "attend",
        1,
        [smem()] + [vmem()] * 5,
        [None] * 3,
        [
            out((BLOCK, SHARE), jnp.bfloat16),
            out((SHARE, BLOCK), jnp.float32),
            out((8, BLOCK), jnp.float32),
        ],
        (reach, *begun, earlier),
        cost(4_000_000_000, 3_000_000, 3_000_000),
        [pltpu.VMEM((8, BLOCK), jnp.float32), pltpu.VMEM((8, BLOCK), jnp.float32)],
        limit=36,
    )


def attend_back_kernel(
    reach_ref, q_ref, qpad_ref, own_ref, prev_ref, grad_ref, grad_t_ref, out_t_ref, lse_ref, cos_ref, sin_ref,
    qgrad_ref, own_grad_ref, prev_grad_ref,
    gpad_ref, qrows_ref, grows_ref, ds_ref, p_ref, delta_ref, dq_ref,
):
    half = BLOCK // 2
    q_scaled = q_ref[...].astype(jnp.float32) * score_mult
    padded_rows(q_scaled, qrows_ref)
    padded_columns(grad_t_ref[...], gpad_ref)
    padded_rows(grad_ref[...], grows_ref)
    both = grad_t_ref[...].astype(jnp.float32) * out_t_ref[...]
    for h in range(4):
        delta_ref[h : h + 1, :] = jnp.sum(
            both[h * HEAD_DIM : (h + 1) * HEAD_DIM], axis=0, keepdims=True
        )


    def block(key_rows, value_rows, first):
        for h in range(4):
            for t in range(2):
                cols = slice(t * half, (t + 1) * half)
                wide = slice(h * BLOCK + t * half, h * BLOCK + (t + 1) * half)
                rows = half if first and t == 0 else BLOCK
                scores = mm(key_rows[:rows], qpad_ref[h, :, cols])
                weights = jnp.exp(scores - lse_ref[h : h + 1, cols])
                if first:
                    key_at = lax.broadcasted_iota(jnp.int32, scores.shape, 0)
                    query_at = lax.broadcasted_iota(jnp.int32, scores.shape, 1) + t * half
                    weights = jnp.where(key_at > query_at, 0.0, weights)
                weight_grad = mm(value_rows[:rows], gpad_ref[h, :, cols])
                score_grad = weights * (weight_grad - delta_ref[h : h + 1, cols])
                p_ref[:rows, wide] = weights.astype(jnp.bfloat16)
                ds_ref[:rows, wide] = score_grad.astype(jnp.bfloat16)
                if rows < BLOCK:
                    p_ref[rows:, wide] = jnp.zeros((BLOCK - rows, half), jnp.bfloat16)
                    ds_ref[rows:, wide] = jnp.zeros((BLOCK - rows, half), jnp.bfloat16)
        key_grad = mm(ds_ref[...], qrows_ref[...])
        value_grad = mm(p_ref[...], grows_ref[...])
        for h in range(4):
            group = (h // 2) * HEAD_DIM
            mine = pl.ds(h * HEAD_DIM, HEAD_DIM)
            part = mm(key_rows, ds_ref[:, h * BLOCK : (h + 1) * BLOCK], TN)[group : group + HEAD_DIM]
            dq_ref[mine, :] = part if first else dq_ref[mine, :] + part
        return key_grad, value_grad

    key_grad, value_grad = block(own_ref[:, :LANES], own_ref[:, LANES:], True)
    own_grad_ref[:, :LANES] = key_grad
    own_grad_ref[:, LANES:] = value_grad

    @pl.loop(1, reach_ref[0] + 1)
    def _(step):
        rows = prev_ref[:, pl.ds(step - 1, 1)].reshape(BLOCK, SHARE)
        key_grad, value_grad = block(rows[:, :LANES], rows[:, LANES:], False)
        parts = prev_grad_ref.shape[0]
        shape = (parts, 1, BLOCK // parts, LANES)
        prev_grad_ref[:, pl.ds(step - 1, 1), :, :LANES] = key_grad.astype(jnp.bfloat16).reshape(shape)
        prev_grad_ref[:, pl.ds(step - 1, 1), :, LANES:] = value_grad.astype(jnp.bfloat16).reshape(shape)

    query_grad = jnp.transpose(dq_ref[...]) * score_mult
    for i in range(0, SHARE, LANES):
        qgrad_ref[:, i : i + LANES] = turned(
            query_grad[:, i : i + LANES], cos_ref[...], sin_ref[...], back=True
        ).astype(jnp.bfloat16)


def attend_back(reach, queries, padded, own_kv, earlier, grad, grad_t, out_t, lse, cosine, signed_sine):
    return run(
        attend_back_kernel,
        "attend_back",
        1,
        [smem()] + [vmem()] * 10,
        [None] * 3,
        [
            out((BLOCK, SHARE), jnp.bfloat16),
            out((BLOCK, SHARE), jnp.float32),
            out(earlier.shape, jnp.bfloat16),
        ],
        (reach, queries, padded, own_kv, earlier, grad, grad_t, out_t, lse, cosine, signed_sine),
        cost(12_000_000_000, 5_000_000, 3_000_000),
        [
            pltpu.VMEM((4, LANES, BLOCK), jnp.bfloat16),
            pltpu.VMEM((4 * BLOCK, LANES), jnp.bfloat16),
            pltpu.VMEM((4 * BLOCK, LANES), jnp.bfloat16),
            pltpu.VMEM((BLOCK, 4 * BLOCK), jnp.bfloat16),
            pltpu.VMEM((BLOCK, 4 * BLOCK), jnp.bfloat16),
            pltpu.VMEM((8, BLOCK), jnp.float32),
            pltpu.VMEM((SHARE, BLOCK), jnp.float32),
        ],
        limit=36,
    )


def residual_kernel(
    a0, a1, a2, a3, w0, w1, w2, w3, x_ref, gain_ref, router_ref, ranks_ref, picks_ref,
    residual_ref, moe_ref, gates_ref, rows_ref, held_ref,
):
    step = pl.program_id(0)
    tile = x_ref.shape[0]

    @pl.when(step < BLOCK // tile)
    def _():
        branch = mm(a0[...], w0[...])
        for a, w in ((a1, w1), (a2, w2), (a3, w3)):
            branch = branch + mm(a[...], w[...])
        residual = x_ref[...].astype(jnp.float32) + residual_mult * branch
        residual_ref[...] = residual
        scale = lax.rsqrt(jnp.mean(residual * residual, axis=1, keepdims=True) + epsilon)
        moe_in = (residual * scale * gain_ref[...]).astype(jnp.bfloat16)
        moe_ref[:, :WIDTH] = moe_in
        logits = mm(router_ref[...], moe_in, NT)
        chosen = ranks_ref[...] >= 0.0
        kept = jnp.where(chosen, logits, masked_score)
        top = jnp.max(kept, axis=0, keepdims=True)
        raised = jnp.where(chosen, jnp.exp(kept - top), 0.0)
        gates = raised / jnp.sum(raised, axis=0, keepdims=True)
        gates_ref[...] = gates
        low = (residual_mult * jnp.transpose(gates)).astype(jnp.bfloat16)
        moe_ref[:, WIDTH:] = low
        held_ref[pl.ds(step * tile, tile), :WIDTH] = moe_in
        held_ref[pl.ds(step * tile, tile), WIDTH:] = low

    @pl.when(step >= BLOCK // tile)
    def _():
        rows_ref[...] = mm(picks_ref[...], held_ref[...]).astype(jnp.bfloat16)


def residual_step(attended, w_out, x, gain, router_t, ranks, picks):
    tile = 256
    first = BLOCK // tile
    slot_tile = SLOTS // 4

    def early(rows, width):
        return pl.BlockSpec((rows, width), lambda i: (jnp.minimum(i, first - 1), 0))

    def late(rows, width):
        return pl.BlockSpec((rows, width), lambda i: (jnp.maximum(i - first, 0), 0))

    by_columns = pl.BlockSpec((LANES, tile), lambda i: (0, jnp.minimum(i, first - 1)))
    return run(
        residual_kernel,
        "residual_step",
        first + 4,
        [early(tile, SHARE)] * 4
        + [None] * 4
        + [early(tile, WIDTH), None, None, by_columns, late(slot_tile, BLOCK)],
        [early(tile, WIDTH), early(tile, WIDTH + LANES), by_columns, late(slot_tile, WIDTH + LANES)],
        [
            out((BLOCK, WIDTH), jnp.float32),
            out((BLOCK, WIDTH + LANES), jnp.bfloat16),
            out((LANES, BLOCK), jnp.float32),
            out((SLOTS, WIDTH + LANES), jnp.bfloat16),
        ],
        (*attended, *w_out, x, gain, router_t, ranks, picks),
        cost(2_700_000_000, 12_000_000, 70_000),
        [pltpu.VMEM((BLOCK, WIDTH + LANES), jnp.bfloat16)],
        free=(1, 2, 3, 5, 6, 7, 10),
    )


def mix_kernel(begin_ref, ranks_ref, moe_ref, mix_ref):
    ranks = jnp.transpose(ranks_ref[...]).astype(jnp.bfloat16)
    gates = moe_ref[:, WIDTH:]
    width = 640
    for at in range(0, SLOTS, width):
        expert_at = lax.broadcasted_iota(jnp.int32, (LANES, width), 0)
        first = expert_at * QUARTER - at
        slot_at = lax.broadcasted_iota(jnp.int32, (LANES, width), 1)
        inside = jnp.logical_and(slot_at >= first, slot_at < first + QUARTER)
        spread = jnp.where(inside, 1.0, 0.0).astype(jnp.bfloat16)
        within = jnp.sum(jnp.where(inside, slot_at - first, 0), axis=0, keepdims=True) + begin_ref[0]
        hit = mm(ranks, spread) == within.astype(jnp.float32)
        mix_ref[:, at : at + width] = jnp.where(hit, mm(gates, spread), 0.0).astype(jnp.bfloat16)


def mix_weights(begin, ranks, moe_cat):
    return run(
        mix_kernel,
        "mix_weights",
        1,
        [smem(), None, None],
        [None],
        [out((BLOCK, SLOTS), jnp.bfloat16)],
        (begin, ranks, moe_cat),
        cost(350_000_000, 3_000_000),
    )[0]


def expert_kernel(lane_ref, x_ref, grad_ref, *refs):
    downs, gate_refs, up_refs = refs[:4], refs[4:8], refs[8:12]
    out_ref, row_ref, hidden_ref, units_ref = refs[12:]
    rows = out_ref.shape[0]
    here = pl.ds(pl.program_id(0) * rows, rows)
    lane = lax.broadcasted_iota(jnp.int32, (rows, LANES), 1) == lane_ref[0]
    gate = jnp.sum(
        jnp.where(lane, x_ref[here, WIDTH:].astype(jnp.float32), 0.0), axis=1, keepdims=True
    )
    x = x_ref[here, :WIDTH]
    grad = grad_ref[...]
    gates, ups, sigmoids, hidden = [], [], [], []
    for j in range(4):
        pre = mm(x, jnp.concatenate([gate_refs[j][...], up_refs[j][...]], axis=1))
        gate_pre, up_pre = pre[:, :LANES], pre[:, LANES:]
        sigmoid = 1.0 / (1.0 + jnp.exp(-gate_pre))
        gates.append(gate_pre)
        ups.append(up_pre)
        sigmoids.append(sigmoid)
        hidden.append(gate_pre * sigmoid * up_pre)
    hidden_low = jnp.concatenate([h.astype(jnp.bfloat16) for h in hidden], axis=1)
    down = jnp.concatenate([p[...] for p in downs], axis=0)
    made = mm(hidden_low, down).astype(jnp.bfloat16)
    out_ref[...] = made
    gate_grad = jnp.sum(grad.astype(jnp.float32) * made.astype(jnp.float32), axis=1, keepdims=True)
    row_ref[:, WIDTH:] = jnp.where(lane, gate_grad, 0.0).astype(jnp.bfloat16)
    hidden_grad = mm(grad, down, NT)
    row = None
    for j in range(4):
        part = hidden_grad[:, j * LANES : (j + 1) * LANES]
        silu = gates[j] * sigmoids[j]
        gate_pre_grad = part * ups[j] * sigmoids[j] * (1.0 + gates[j] * (1.0 - sigmoids[j]))
        up_pre_grad = part * silu
        hidden_ref[:, j * LANES : (j + 1) * LANES] = (hidden[j] * gate).astype(jnp.bfloat16)
        units_ref[:, j * SHARE : j * SHARE + LANES] = (gate_pre_grad * gate).astype(jnp.bfloat16)
        units_ref[:, j * SHARE + LANES : (j + 1) * SHARE] = (up_pre_grad * gate).astype(jnp.bfloat16)
        both = jnp.concatenate([gate_pre_grad, up_pre_grad], axis=1).astype(jnp.bfloat16)
        term = mm(both, jnp.concatenate([gate_refs[j][...], up_refs[j][...]], axis=1), NT)
        row = term if row is None else row + term
    row_ref[:, :WIDTH] = row.astype(jnp.bfloat16)


def expert_step(lane, x, grad, downs, gates, ups):
    tile = 320
    return run(
        expert_kernel,
        "expert_step",
        SLOTS // tile,
        [smem(), vmem(), tiles(tile, WIDTH)] + [None] * 12,
        [tiles(tile, WIDTH), tiles(tile, WIDTH + LANES), tiles(tile, 512), tiles(tile, WIDTH)],
        [
            out((SLOTS, WIDTH), jnp.bfloat16),
            out((SLOTS, WIDTH + LANES), jnp.bfloat16),
            out((SLOTS, 512), jnp.bfloat16),
            out((SLOTS, WIDTH), jnp.bfloat16),
        ],
        (lane, x, grad, *downs, *gates, *ups),
        cost(8_000_000_000, 18_000_000, 700_000),
        limit=40,
    )


def unit_grads_kernel(x_ref, grad_ref, hidden_ref, units_ref, keep_ref, send_ref, turned_ref):
    step = pl.program_id(0)

    @pl.when(step == 0)
    def _():
        for k in range(4):
            columns = slice(k * SHARE, (k + 1) * SHARE)
            turned_ref[columns, :] = jnp.transpose(x_ref[:, columns])

    def write(to_ref):
        to_ref[0, :LANES, :] = mm(hidden_ref[...], grad_ref[...], TN).astype(jnp.bfloat16)
        for k in range(4):
            columns = slice(k * SHARE, (k + 1) * SHARE)
            to_ref[0, LANES:, columns] = mm(turned_ref[columns, :], units_ref[...]).astype(jnp.bfloat16)

    @pl.when(step < 2)
    def _():
        write(keep_ref)

    @pl.when(step >= 2)
    def _():
        write(send_ref)


def unit_grads(x, grad, hidden, units):
    rows = SHARE + LANES

    def share_of(i):
        return jnp.where(i < 2, 2 * i, 2 * i - 3)

    return run(
        unit_grads_kernel,
        "unit_grads",
        4,
        [
            vmem(),
            None,
            pl.BlockSpec((SLOTS, LANES), lambda i: (0, share_of(i))),
            pl.BlockSpec((SLOTS, SHARE), lambda i: (0, share_of(i))),
        ],
        [
            pl.BlockSpec((1, rows, WIDTH), lambda i: (jnp.minimum(i, 1), 0, 0)),
            pl.BlockSpec((1, rows, WIDTH), lambda i: (jnp.maximum(i - 2, 0), 0, 0)),
        ],
        [out((2, rows, WIDTH), jnp.bfloat16), out((2, rows, WIDTH), jnp.bfloat16)],
        (x, grad, hidden, units),
        cost(4_000_000_000, 12_000_000),
        [pltpu.VMEM((WIDTH, SLOTS), jnp.bfloat16)],
        limit=36,
    )


def unit_finish_kernel(mine_ref, first_ref, second_ref, third_ref, gate_ref, up_ref, down_ref):
    got = jnp.concatenate([first_ref[...], second_ref[...], third_ref[...]], axis=0)
    total = mine_ref[0] + got.astype(jnp.float32)
    down_ref[0] = total[:LANES, :]
    for k in range(4):
        rows = slice(k * SHARE, (k + 1) * SHARE)
        gate_ref[0, rows, :] = total[LANES:, k * SHARE : k * SHARE + LANES]
        up_ref[0, rows, :] = total[LANES:, k * SHARE + LANES : (k + 1) * SHARE]


def unit_finish(mine, first, second, third):
    return run(
        unit_finish_kernel,
        "unit_finish",
        1,
        [once(1, PACKED, WIDTH), None, None, None],
        [None] * 3,
        [
            out((1, WIDTH, LANES), jnp.float32),
            out((1, WIDTH, LANES), jnp.float32),
            out((1, LANES, WIDTH), jnp.float32),
        ],
        (mine, first, second, third),
        cost(1_000_000, 3_000_000),
        free=(0, 1, 2, 3),
    )


def home_kernel(rank_ref, mix_ref, rows_ref, keep_ref, send_ref):
    rank = rank_ref[0]
    extra = rows_ref.shape[1] > WIDTH
    for j in range(4):
        at = pl.multiple_of(jnp.bitwise_xor(rank, j) * SHARE, SHARE)
        total = mm(mix_ref[...], rows_ref[:, pl.ds(at, SHARE)])
        to_ref = send_ref if j % 2 else keep_ref
        to_ref[(j // 2) * BLOCK : (j // 2 + 1) * BLOCK, :] = total.astype(to_ref.dtype)
    if extra:
        gate_grads = jnp.transpose(mm(mix_ref[...], rows_ref[:, WIDTH:]))[:EXPERTS]
        for to_ref in (keep_ref, send_ref):
            for i in range(2):
                at = 2 * BLOCK + i * EXPERTS
                to_ref[at : at + EXPERTS, :] = gate_grads[:, i * SHARE : (i + 1) * SHARE].astype(
                    to_ref.dtype
                )


def sum_home(rank, mix, rows):
    height = 2 * BLOCK + (2 * EXPERTS if rows.shape[1] > WIDTH else 0)
    return run(
        home_kernel,
        "sum_home",
        1,
        [smem(), None, vmem()],
        [None] * 2,
        [out((height, SHARE), jnp.float32), out((height, SHARE), jnp.bfloat16)],
        (rank, mix, rows),
        cost(1_500_000_000, 6_000_000),
        limit=36,
    )


def swap_kernel(mine_ref, got_ref, total_ref):
    mine, got = mine_ref, got_ref
    half = BLOCK
    total_ref[:half] = (mine[:half] + got[half : 2 * half].astype(jnp.float32)).astype(total_ref.dtype)
    total_ref[half : 2 * half] = (
        mine[half : 2 * half] + got[:half].astype(jnp.float32)
    ).astype(total_ref.dtype)
    total_ref[2 * half :] = (mine[2 * half :] + got[2 * half :].astype(jnp.float32)).astype(
        total_ref.dtype
    )


def swap_sum(mine, got):
    return run(
        swap_kernel,
        "swap_sum",
        1,
        [None] * 2,
        [None],
        [out(mine.shape, jnp.bfloat16)],
        (mine, got),
        cost(1_000_000, 2_500_000),
        free=(0, 1),
    )[0]


def norm_back_kernel(
    rank_ref, g0, g2, g1, g3, z_ref, gates_ref, residual_ref, gain_ref, router_ref, grad_ref, w_ref,
    low_ref, logit_ref, own_ref, att_ref, att_t_ref, gain_grad_ref, u_ref,
):
    rank = rank_ref[0]
    for flip, part in enumerate((g0, g1, g2, g3)):
        at = pl.multiple_of(jnp.bitwise_xor(rank, flip) * SHARE, SHARE)
        u_ref[:, pl.ds(at, SHARE)] = part[...].astype(jnp.float32)
    weighted_grads = z_ref[...].astype(jnp.float32)
    gates = gates_ref[:EXPERTS, :]
    inner = jnp.sum(weighted_grads, axis=0, keepdims=True)
    logit_grad = (weighted_grads - gates * inner).astype(jnp.bfloat16)
    logit_ref[...] = logit_grad
    u = u_ref[...] + mm(logit_grad, router_ref[:EXPERTS, :], TN)
    v = residual_ref[...]
    scale = lax.rsqrt(jnp.mean(v * v, axis=1, keepdims=True) + epsilon)
    weighted = u * gain_ref[...]
    mean = jnp.mean(weighted * v, axis=1, keepdims=True)
    total = grad_ref[...].astype(jnp.float32) + scale * weighted - v * (scale * scale * scale * mean)

    @pl.when(pl.program_id(0) == 0)
    def _():
        gain_grad_ref[...] = jnp.zeros_like(gain_grad_ref)

    gain_grad_ref[0:1, :] += jnp.sum(u * v * scale, axis=0, keepdims=True)
    low = (residual_mult * total).astype(jnp.bfloat16)
    low_ref[...] = low
    u_ref[...] = total
    own_ref[...] = u_ref[:, pl.ds(pl.multiple_of(rank * SHARE, SHARE), SHARE)]
    att_ref[...] = mm(low, w_ref[...], NT).astype(jnp.bfloat16)
    att_t_ref[...] = mm(w_ref[...], low, NT).astype(jnp.bfloat16)


def norm_back_step(rank, mine, theirs, gates, residual, gain, router_t, out_grad, w_out):
    tile = 256
    by_columns = pl.BlockSpec((EXPERTS, tile), lambda i: (0, i))
    return run(
        norm_back_kernel,
        "norm_back_step",
        BLOCK // tile,
        [smem()]
        + [tiles(tile, SHARE), tiles(tile, SHARE, BLOCK // tile)] * 2
        + [
            tiles(EXPERTS, SHARE, 2 * BLOCK // EXPERTS),
            pl.BlockSpec((LANES, tile), lambda i: (0, i)),
            tiles(tile, WIDTH),
            None,
            None,
            tiles(tile, WIDTH),
            None,
        ],
        [
            tiles(tile, WIDTH),
            by_columns,
            tiles(tile, SHARE),
            tiles(tile, SHARE),
            pl.BlockSpec((SHARE, tile), lambda i: (0, i)),
            fixed(8, WIDTH),
        ],
        [
            out((BLOCK, WIDTH), jnp.bfloat16),
            out((EXPERTS, BLOCK), jnp.bfloat16),
            out((BLOCK, SHARE), jnp.float32),
            out((BLOCK, SHARE), jnp.bfloat16),
            out((SHARE, BLOCK), jnp.bfloat16),
            out((8, WIDTH), jnp.float32),
        ],
        (rank, mine, mine, theirs, theirs, mine, gates, residual, gain, router_t, out_grad, w_out),
        cost(700_000_000, 9_000_000, 512),
        [pltpu.VMEM((tile, WIDTH), jnp.float32)],
        free=(3, 4, 9),
    )


def dense_grads_kernel(low_ref, attended_ref, normed_ref, qgrad_ref, logit_ref, moe_ref, gain_ref, made_ref):
    made_ref[:, :SHARE] = mm(low_ref[...], attended_ref[...], TN).astype(jnp.bfloat16)
    made_ref[:, SHARE : 2 * SHARE] = mm(normed_ref[...], qgrad_ref[...], TN).astype(jnp.bfloat16)
    router = mm(logit_ref[...], moe_ref[:, :WIDTH])
    stacked = jnp.concatenate(
        [router, gain_ref[...], jnp.zeros((LANES - EXPERTS - 8, WIDTH), jnp.float32)], axis=0
    )
    made_ref[:, 2 * SHARE :] = jnp.transpose(stacked).astype(jnp.bfloat16)


def dense_grads(low, attended, normed, qgrad, logit, moe_cat, gain_grad):
    return run(
        dense_grads_kernel,
        "dense_grads",
        1,
        [None] * 7,
        [None],
        [out((WIDTH, 2 * SHARE + LANES), jnp.bfloat16)],
        (low, attended, normed, qgrad, logit, moe_cat, gain_grad),
        cost(600_000_000, 6_000_000),
    )[0]


def last_grads_kernel(
    rank_ref, own_ref, home_ref, qgrad_ref, normed_ref, x_ref, wq_ref, wk_ref, wv_ref, cos_ref, sin_ref, made_ref,
    gain_ref, all_ref, keep_ref, send_ref, inner_ref, part_ref,
):
    rank = rank_ref[0]
    kv = own_ref[...] + home_ref[...].astype(jnp.float32)
    key_grad = turned(kv[:, :LANES], cos_ref[...], sin_ref[...], back=True).astype(jnp.bfloat16)
    value_grad = kv[:, LANES:].astype(jnp.bfloat16)
    both = jnp.concatenate([key_grad, value_grad], axis=1)
    all_ref[:, : 2 * SHARE] = made_ref[:, : 2 * SHARE]
    all_ref[:, 2 * SHARE : 3 * SHARE] = mm(normed_ref[...], both, TN).astype(jnp.bfloat16)
    gain = jnp.zeros((1, WIDTH), jnp.float32)
    tile = 128
    for i in range(0, BLOCK, tile):
        rows = slice(i, i + tile)
        part = mm(qgrad_ref[rows, :], wq_ref[...], NT)
        part = part + mm(key_grad[rows], wk_ref[...], NT) + mm(value_grad[rows], wv_ref[...], NT)
        x = x_ref[rows, :].astype(jnp.float32)
        scale = lax.rsqrt(jnp.mean(x * x, axis=1, keepdims=True) + epsilon)
        along = part * x
        gain = gain + jnp.sum(along * scale, axis=0, keepdims=True)
        inner = jnp.sum(along * gain_ref[...], axis=1, keepdims=True)
        inner_ref[:, rows] = jnp.transpose(jnp.broadcast_to(inner, (tile, LANES)))[:8]
        part_ref[rows, :] = part
    for j in range(4):
        at = pl.multiple_of(jnp.bitwise_xor(rank, j) * SHARE, SHARE)
        to_ref = send_ref if j % 2 else keep_ref
        to_ref[(j // 2) * BLOCK : (j // 2 + 1) * BLOCK, :] = part_ref[:, pl.ds(at, SHARE)].astype(to_ref.dtype)
    lane = lax.broadcasted_iota(jnp.int32, (WIDTH, LANES), 1)
    column = jnp.transpose(jnp.broadcast_to(gain, (LANES, WIDTH)))
    rest = jnp.where(lane == EXPERTS + 8, column, made_ref[:, 2 * SHARE :].astype(jnp.float32))
    all_ref[:, 3 * SHARE :] = rest.astype(jnp.bfloat16)


def last_grads(rank, own, home, qgrad, normed, x, w_query, w_key, w_value, cosine, sine, made, gain):
    return run(
        last_grads_kernel,
        "last_grads",
        1,
        [smem()] + [None] * 12,
        [None] * 4,
        [
            out((WIDTH, 3 * SHARE + LANES), jnp.bfloat16),
            out((2 * BLOCK, SHARE), jnp.float32),
            out((2 * BLOCK, SHARE), jnp.bfloat16),
            out((8, BLOCK), jnp.float32),
        ],
        (rank, own, home, qgrad, normed, x, w_query, w_key, w_value, cosine, sine, made, gain),
        cost(1_000_000_000, 8_000_000, 512),
        [pltpu.VMEM((BLOCK, WIDTH), jnp.float32)],
        free=(2,),
    )


def input_finish_kernel(
    rank_ref, near_ref, far_ref, i0, i1, i2, i3, x_ref, gain_ref, residual_ref, made_ref
):
    mine = pl.ds(pl.multiple_of(rank_ref[0] * SHARE, SHARE), SHARE)
    x = x_ref[...].astype(jnp.float32)
    scale = lax.rsqrt(jnp.mean(x * x, axis=1, keepdims=True) + epsilon)
    inner = (i0[...] + i1[...] + i2[...] + i3[...]) * (1.0 / WIDTH)
    inner = jnp.transpose(jnp.broadcast_to(inner[:1], (LANES, BLOCK)))[:, :1]
    weighted = (near_ref[...] + far_ref[...].astype(jnp.float32)) * gain_ref[:, mine]
    x_own = x_ref[:, mine].astype(jnp.float32)
    made_ref[...] = residual_ref[...] + scale * weighted - x_own * (scale * scale * scale * inner)


def input_finish(rank, near, far, inners, x, gain, residual):
    return run(
        input_finish_kernel,
        "input_finish",
        1,
        [smem(), once(BLOCK, SHARE), None] + [None] * 7,
        [None],
        [out((BLOCK, SHARE), jnp.float32)],
        (rank, near, far, *inners, x, gain, residual),
        cost(3_000_000, 3_000_000, 512),
        free=(1, 2, 3, 4, 5, 6),
    )[0]


def per_device(
    hidden_in,
    lengths,
    block_order,
    routes,
    norm_gain_attn,
    w_query,
    w_key,
    w_value,
    w_out,
    norm_gain_moe,
    w_router,
    w_gate,
    w_up,
    w_down,
    out_grad,
):
    dp_count = block_order.shape[0]
    mp_rank = lax.axis_index("mp").astype(jnp.int32)
    column_start = mp_rank * SHARE
    piece = BLOCK // dp_count
    steps = MAXLEN // BLOCK - 1
    rank = mp_rank.reshape(1)
    lane = lax.axis_index("dp").astype(jnp.int32).reshape(1)
    begin = rank * QUARTER
    gain_attn = norm_gain_attn[None, :]
    gain_moe = norm_gain_moe[None, :]
    router_t = jnp.pad(w_router.T, ((0, LANES - EXPERTS), (0, 0)))

    far_out = peer(w_out, 2)
    far_down = peer(w_down[0], 2)

    normed, key_value, cosine, sine, reach, wanted, later, live = project(
        lengths, block_order, lane, hidden_in, gain_attn, w_key, w_value
    )
    queries = project_queries(normed, w_query, cosine, sine)
    pieces = to_all(key_value.reshape(dp_count, piece, SHARE))
    picks, ranks = route(begin, after(routes.T, key_value))
    begun = attend_own(queries, after(key_value, picks))
    picked = pick_pieces(wanted, after(pieces, far_out, far_down, queries, picks))
    far_gate = peer(after(w_gate[0], picked), 2)
    far_up = peer(after(w_up[0], picked), 2)
    earlier = to_all(picked.reshape(dp_count, steps * piece, SHARE))
    earlier = earlier.reshape(dp_count, steps, piece, SHARE)

    outs = [w_out, peer(after(w_out, picked), 1), far_out, peer(far_out, 1)]

    grad_rows = jnp.dot(picks, after(out_grad, picked), preferred_element_type=jnp.bfloat16)
    grad_arrived = to_experts(after(grad_rows, earlier, begun[1], far_gate, far_up).reshape(EXPERTS, QUARTER, WIDTH))
    attended, attended_t, lse = attend(reach, begun, earlier)
    far = peer(attended, 2)
    residual, moe_cat, gates, moe_rows = residual_step(
        [attended, peer(attended, 1), far, peer(far, 1)],
        outs,
        hidden_in,
        gain_moe,
        router_t,
        ranks,
        picks,
    )
    own = [after(w[0], moe_rows) for w in (w_down, w_gate, w_up)]
    far = [after(w, moe_rows) for w in (far_down, far_gate, far_up)]
    downs, gates_all, ups = [[w, peer(w, 1), v, peer(v, 1)] for w, v in zip(own, far)]
    grouped = to_experts(moe_rows.reshape(EXPERTS, QUARTER, -1)).reshape(SLOTS, -1)
    mix = mix_weights(begin, ranks, moe_cat)
    grouped_grad = grad_arrived.reshape(SLOTS, WIDTH)
    rows_out, row_grad, hidden_units, unit_grad = expert_step(
        lane, grouped, grouped_grad, downs, gates_all, ups
    )
    row_home = to_experts(row_grad.reshape(dp_count, QUARTER, -1)).reshape(SLOTS, -1)
    rows_home = to_experts(after(rows_out, row_home).reshape(dp_count, QUARTER, -1)).reshape(SLOTS, -1)

    unit_keep, unit_send = unit_grads(grouped, grouped_grad, hidden_units, unit_grad)
    unit_near = unit_keep.astype(jnp.float32) + peer(unit_send, 1).astype(jnp.float32)
    unit_low = unit_near[1].astype(jnp.bfloat16)
    cut = PACKED // 2
    unit_far_a = peer(unit_low[:cut], 2)
    keep, send = sum_home(rank, after(mix, unit_far_a), row_home)
    near = keep + peer(send, 1).astype(jnp.float32)
    mine = swap_sum(near, peer(near.astype(jnp.bfloat16), 2))
    theirs = peer(mine, 1)
    branch_grad, logit_grad, residual_grad, attended_grad, attended_grad_t, moe_gain = norm_back_step(
        rank, mine, theirs, gates, residual, gain_moe, router_t, out_grad, w_out
    )

    query_pre_grad, own_grads, later_grads = attend_back(
        reach,
        queries,
        begun[0],
        key_value,
        earlier,
        attended_grad,
        attended_grad_t,
        attended_t,
        lse,
        cosine,
        sine,
    )
    unit_far_b = peer(after(unit_low[cut:], later_grads), 2)
    unit_far_b = peer(after(unit_low[cut : cut + cut // 2], branch_grad), 2)
    later_pieces = to_all(after(later_grads, rows_home, unit_far_b).reshape(dp_count, steps * piece, SHARE))
    summed = sum_pieces(
        later, live, later_pieces.reshape(dp_count * steps, piece, SHARE), dp_count
    )
    kv_home = to_all(summed).reshape(BLOCK, SHARE)
    made = dense_grads(
        branch_grad, attended, normed, query_pre_grad, logit_grad, moe_cat, moe_gain
    )

    unit_far_c = peer(after(unit_low[cut + cut // 2 :], kv_home, made), 2)

    every, keep, send, inner = last_grads(
        rank,
        own_grads,
        kv_home,
        query_pre_grad,
        normed,
        hidden_in,
        w_query,
        w_key,
        w_value,
        cosine,
        sine,
        made,
        gain_attn,
    )
    near_norm = keep + peer(send, 1).astype(jnp.float32)
    far_norm = peer(near_norm[BLOCK:].astype(jnp.bfloat16), 2)
    inners = [inner] + [peer(inner, flip) for flip in (1, 2, 3)]
    every = after(every, unit_far_c)
    arrived = to_all(every.reshape(dp_count, WIDTH // dp_count, -1))
    keep, send = sum_home(rank, mix, after(rows_home, every))
    near_mix = keep + peer(send, 1).astype(jnp.float32)
    far_mix = peer(near_mix[BLOCK:].astype(jnp.bfloat16), 2)
    grad_w_gate, grad_w_up, grad_w_down = unit_finish(
        unit_near, unit_far_a, after(unit_far_b, every), unit_far_c
    )
    dense = jnp.sum(arrived.astype(jnp.float32), axis=0)
    at = 3 * SHARE
    attn_gain = dense[:, at + EXPERTS + 8]
    attn_gain = attn_gain + peer(attn_gain, 1) + peer(attn_gain, 2) + peer(attn_gain, 3)
    residual_cols = lax.dynamic_slice_in_dim(residual, column_start, SHARE, 1)
    mixture = near_mix[:BLOCK] + after(far_mix, attn_gain).astype(jnp.float32)
    out_hidden = (residual_cols + mixture).astype(jnp.bfloat16)

    grad_hidden = input_finish(
        rank, near_norm, after(far_norm, dense), inners, hidden_in, gain_attn, residual_grad
    )
    return (
        out_hidden,
        grad_hidden,
        dense[:, SHARE : 2 * SHARE],
        dense[:, 2 * SHARE : 2 * SHARE + LANES],
        dense[:, 2 * SHARE + LANES : at],
        dense[:, :SHARE].T,
        attn_gain,
        dense[:, at + EXPERTS],
        dense[:, at : at + EXPERTS],
        grad_w_gate,
        grad_w_up,
        grad_w_down,
    )


def solution(mesh):
    in_specs = (
        P("dp", None),
        P(),
        P(),
        P("dp", None),
        P(),
        P(None, "mp"),
        P(None, "mp"),
        P(None, "mp"),
        P("mp", None),
        P(),
        P(),
        P("dp", None, "mp"),
        P("dp", None, "mp"),
        P("dp", "mp", None),
        P("dp", None),
    )
    out_specs = (
        P("dp", "mp"),
        P("dp", "mp"),
        P("dp", "mp"),
        P("dp", "mp"),
        P("dp", "mp"),
        P("mp", "dp"),
        P("dp"),
        P("dp"),
        P("dp", None),
        P("dp", None, "mp"),
        P("dp", None, "mp"),
        P("dp", "mp", None),
    )
    return jax.shard_map(
        per_device, mesh=mesh, in_specs=in_specs, out_specs=out_specs, check_vma=False
    )
```

```python
import jax
import jax.numpy as jnp
import numpy as np
from jax import lax
from jax.experimental import pallas as pl
from jax.experimental.pallas import tpu as pltpu
from jax.sharding import PartitionSpec as P

HEAD_DIM = 64
EXPERTS = 32
BLOCK = 512
MAXLEN = 2048
CAP = 160
WIDTH = 1024
SHARE = 256
QUARTER = 40
SLOTS = 1280
LANES = 128
PACKED = 384

epsilon = 1e-06
residual_mult = 0.22
score_mult = 0.015625
rope_base = 10000.0
masked_score = -1e30

NN = (((1,), (0,)), ((), ()))
NT = (((1,), (1,)), ((), ()))
TN = (((0,), (0,)), ((), ()))


def mm(a, b, dims=NN):
    return lax.dot_general(a, b, dims, preferred_element_type=jnp.float32)


def to_all(x):
    return lax.all_to_all(x, "dp", 0, 0, tiled=True)


def crossed_groups(dp_count=32):
    groups = []
    for chip in range(2):
        for core in range(2):
            groups.append([i * 4 + (chip ^ (i & 1)) * 2 + core for i in range(dp_count)])
    return groups


def to_experts(x):
    return lax.all_to_all(
        x, ("dp", "mp"), 0, 0, axis_index_groups=crossed_groups(x.shape[0]), tiled=True
    )


def peer(x, flip):
    return lax.ppermute(x, "mp", [(i, i ^ flip) for i in range(4)])


def after(x, *others):
    return lax.optimization_barrier((x, *others))[0]


def vmem():
    return pl.BlockSpec(memory_space=pltpu.VMEM)


def smem():
    return pl.BlockSpec(memory_space=pltpu.SMEM)


def tiles(rows, width, row0=0):
    return pl.BlockSpec((rows, width), lambda i: (i + row0, 0))


def fixed(rows, width):
    return pl.BlockSpec((rows, width), lambda i: (0, 0))


def once(*shape):
    return pl.BlockSpec(shape, lambda i: (0,) * len(shape), pipeline_mode=pl.Buffered(1))


def run(kernel, name, steps, in_specs, out_specs, out_shape, args, estimate, scratch=(), free=(), limit=32):
    in_specs = [once(*a.shape) if s is None else s for s, a in zip(in_specs, args)]
    out_specs = [once(*o.shape) if s is None else s for s, o in zip(out_specs, out_shape)]
    args = [
        a
        if s.memory_space is not None or i in free
        else pltpu.with_memory_space_constraint(a, pltpu.HBM)
        for i, (s, a) in enumerate(zip(in_specs, args))
    ]
    out_shape = [
        o if s.memory_space == pltpu.SMEM else pltpu.HBM(o.shape, o.dtype)
        for s, o in zip(out_specs, out_shape)
    ]
    return pl.pallas_call(
        kernel,
        name=name,
        grid=(steps,),
        in_specs=in_specs,
        out_specs=out_specs,
        out_shape=out_shape,
        scratch_shapes=list(scratch),
        compiler_params=pltpu.CompilerParams(vmem_limit_bytes=limit << 20),
        cost_estimate=estimate,
    )(*args)


def out(shape, dtype):
    return jax.ShapeDtypeStruct(shape, dtype)


def cost(flops, moved, exps=0):
    return pl.CostEstimate(flops=flops, bytes_accessed=moved, transcendentals=exps)


def rope_constants():
    frequency = rope_base ** (-(np.arange(HEAD_DIM // 2, dtype=np.float64) * 2.0) / HEAD_DIM)
    wide = np.tile(frequency, 4)[None, :]
    made = []
    for count, apart in ((BLOCK // 16, 16), (16, 1), (8, BLOCK)):
        angles = np.arange(count, dtype=np.float64)[:, None] * apart * wide
        made += [np.cos(angles), np.sin(angles)]
    return [jnp.asarray(a.astype(np.float32)) for a in made]


def half_front(rows):
    lane = lax.broadcasted_iota(jnp.int32, (rows, LANES), 1)
    return (lane % HEAD_DIM) < HEAD_DIM // 2


def turned(chunk, cosine, signed_sine, back=False):
    partner = jnp.where(
        half_front(chunk.shape[0]), pltpu.roll(chunk, 96, 1), pltpu.roll(chunk, 32, 1)
    )
    if back:
        return chunk * cosine - partner * signed_sine
    return chunk * cosine + partner * signed_sine


def block_tables_in(lengths_ref, order_ref, rank_ref, offset_ref, inverse_ref, reach_ref, wanted_ref, later_ref, live_ref):
    count = order_ref.shape[0]
    steps = MAXLEN // BLOCK - 1

    def sequence(s, begin):
        def one(j, at):
            offset_ref[jnp.minimum(at, count - 1)] = j
            return at + 1

        return lax.fori_loop(0, lengths_ref[s], one, begin)

    lax.fori_loop(0, lengths_ref.shape[0], sequence, jnp.int32(0))

    def invert(d, carry):
        inverse_ref[order_ref[d]] = d
        return carry

    lax.fori_loop(0, count, invert, jnp.int32(0))
    reach_ref[0] = offset_ref[order_ref[rank_ref[0]]]

    def look(d, carry):
        packed = order_ref[d]
        for s in range(1, steps + 1):
            wanted_ref[d * steps + s - 1] = inverse_ref[jnp.maximum(packed - s, 0)]
            next_at = jnp.minimum(packed + s, count - 1)
            later_ref[d * steps + s - 1] = inverse_ref[next_at] * steps + s - 1
            is_live = jnp.logical_and(packed + s < count, offset_ref[next_at] >= s)
            live_ref[d * steps + s - 1] = jnp.where(is_live, 1, 0)
        return carry

    lax.fori_loop(0, count, look, jnp.int32(0))


def project_kernel(
    lengths_ref, order_ref, rank_ref, x_ref, gain_ref, wk_ref, wv_ref,
    cos16_ref, sin16_ref, cos1_ref, sin1_ref, cos0_ref, sin0_ref,
    normed_ref, kv_ref, cosine_ref, sine_ref, reach_ref, wanted_ref, later_ref, live_ref,
    offset_ref, inverse_ref,
):
    @pl.when(pl.program_id(0) == 0)
    def _():
        block_tables_in(
            lengths_ref, order_ref, rank_ref, offset_ref, inverse_ref, reach_ref, wanted_ref, later_ref, live_ref
        )

    x = x_ref[...].astype(jnp.float32)
    scale = lax.rsqrt(jnp.mean(x * x, axis=1, keepdims=True) + epsilon)
    normed = (x * scale * gain_ref[...]).astype(jnp.bfloat16)
    normed_ref[...] = normed
    at = reach_ref[0]
    cos0, sin0 = cos0_ref[pl.ds(at, 1), :], sin0_ref[pl.ds(at, 1), :]
    cos16 = cos16_ref[...] * cos0 - sin16_ref[...] * sin0
    sin16 = sin16_ref[...] * cos0 + cos16_ref[...] * sin0
    cos1, sin1 = cos1_ref[...][None], sin1_ref[...][None]
    cosine = (cos16[:, None, :] * cos1 - sin16[:, None, :] * sin1).reshape(x.shape[0], LANES)
    sine = (sin16[:, None, :] * cos1 + cos16[:, None, :] * sin1).reshape(x.shape[0], LANES)
    sine = jnp.where(half_front(x.shape[0]), -sine, sine)
    cosine_ref[...] = cosine
    sine_ref[...] = sine
    kv_ref[:, :LANES] = turned(mm(normed, wk_ref[...]), cosine, sine).astype(jnp.bfloat16)
    kv_ref[:, LANES:] = mm(normed, wv_ref[...]).astype(jnp.bfloat16)


def query_kernel(normed_ref, wq_ref, cosine_ref, sine_ref, q_ref):
    queries = mm(normed_ref[...], wq_ref[...])
    for i in range(0, SHARE, LANES):
        q_ref[:, i : i + LANES] = turned(
            queries[:, i : i + LANES], cosine_ref[...], sine_ref[...]
        ).astype(jnp.bfloat16)


def project_queries(normed, w_query, cosine, sine):
    tile = 256
    return run(
        query_kernel,
        "project_queries",
        BLOCK // tile,
        [tiles(tile, WIDTH), None, tiles(tile, LANES), tiles(tile, LANES)],
        [tiles(tile, SHARE)],
        [out((BLOCK, SHARE), jnp.bfloat16)],
        (normed, w_query, cosine, sine),
        cost(270_000_000, 2_500_000),
    )[0]


def project(lengths, order, rank, x, gain, w_key, w_value):
    tile = 256
    count = order.shape[0]
    steps = MAXLEN // BLOCK - 1
    bf16, f32 = jnp.bfloat16, jnp.float32
    return run(
        project_kernel,
        "project",
        BLOCK // tile,
        [smem()] * 3
        + [tiles(tile, WIDTH), None, None, None]
        + [tiles(tile // 16, LANES)] * 2
        + [None] * 4,
        [tiles(tile, WIDTH), tiles(tile, SHARE)] + [tiles(tile, LANES)] * 2 + [smem()] * 4,
        [out((BLOCK, WIDTH), bf16), out((BLOCK, SHARE), bf16)]
        + [out((BLOCK, LANES), f32)] * 2
        + [out((1,), jnp.int32)]
        + [out((count * steps,), jnp.int32)] * 3,
        (lengths, order, rank, x, gain, w_key, w_value, *rope_constants()),
        cost(540_000_000, 4_000_000, 512),
        [pltpu.SMEM((count,), jnp.int32), pltpu.SMEM((count,), jnp.int32)],
    )


def pick_kernel(wanted_ref, pieces_ref, picked_ref):
    def one(i, carry):
        picked_ref[i] = pieces_ref[wanted_ref[i]]
        return carry

    lax.fori_loop(0, picked_ref.shape[0], one, jnp.int32(0), unroll=4)


def pick_pieces(wanted, pieces):
    shape = out((wanted.shape[0], *pieces.shape[1:]), pieces.dtype)
    return run(
        pick_kernel, "pick_pieces", 1, [smem(), None], [None], [shape], (wanted, pieces), cost(0, 1_100_000), free=(1,)
    )[0]


def sum_kernel(later_ref, live_ref, pieces_ref, sum_ref):
    steps = MAXLEN // BLOCK - 1

    def one(d, carry):
        total = jnp.zeros(sum_ref.shape[1:], jnp.float32)
        for s in range(steps):
            part = pieces_ref[later_ref[d * steps + s]].astype(jnp.float32)
            total = total + jnp.where(live_ref[d * steps + s] == 1, part, 0.0)
        sum_ref[d] = total.astype(sum_ref.dtype)
        return carry

    lax.fori_loop(0, sum_ref.shape[0], one, jnp.int32(0), unroll=2)


def sum_pieces(later, live, pieces, count):
    shape = out((count, *pieces.shape[1:]), pieces.dtype)
    return run(
        sum_kernel,
        "sum_pieces",
        1,
        [smem(), smem(), None],
        [None],
        [shape],
        (later, live, pieces),
        cost(0, 1_100_000),
        free=(2,),
    )[0]


def route_kernel(begin_ref, routes_ref, picks_ref, ranks_ref):
    tokens = routes_ref.shape[1]
    expert_at = lax.broadcasted_iota(jnp.int32, (LANES, tokens), 0)
    hits = jnp.zeros((LANES, tokens), jnp.float32)
    for k in range(routes_ref.shape[0]):
        hits = hits + jnp.where(routes_ref[k : k + 1, :] == expert_at, 1.0, 0.0)
    row_at = lax.broadcasted_iota(jnp.int32, (tokens, tokens), 0)
    column_at = lax.broadcasted_iota(jnp.int32, (tokens, tokens), 1)
    before = jnp.where(row_at < column_at, 1.0, 0.0).astype(jnp.bfloat16)
    ranks = jnp.where(hits > 0.5, mm(hits.astype(jnp.bfloat16), before), -1.0)
    ranks_ref[...] = ranks
    slot_at = lax.broadcasted_iota(jnp.int32, (QUARTER, tokens), 0) + begin_ref[0]
    slot_at = slot_at.astype(jnp.float32)
    for e in range(EXPERTS):
        picks_ref[e * QUARTER : (e + 1) * QUARTER, :] = jnp.where(
            ranks[e : e + 1, :] == slot_at, 1.0, 0.0
        ).astype(jnp.bfloat16)


def route(begin, routes_t):
    return run(
        route_kernel,
        "route",
        1,
        [smem(), None],
        [None, None],
        [out((SLOTS, BLOCK), jnp.bfloat16), out((LANES, BLOCK), jnp.float32)],
        (begin, routes_t),
        cost(100_000_000, 1_600_000),
        free=(1,),
    )


def padded_columns(rows_t, out_ref):
    zero = jnp.zeros((HEAD_DIM, rows_t.shape[1]), out_ref.dtype)
    for h in range(4):
        mine = rows_t[h * HEAD_DIM : (h + 1) * HEAD_DIM].astype(out_ref.dtype)
        at = (h // 2) * HEAD_DIM
        out_ref[h, pl.ds(at, HEAD_DIM), :] = mine
        out_ref[h, pl.ds(HEAD_DIM - at, HEAD_DIM), :] = zero


def padded_rows(rows, out_ref):
    n = rows.shape[0]
    lane = lax.broadcasted_iota(jnp.int32, (n, 128), 1)
    for h in range(4):
        pair = rows[:, (h // 2) * 128 : (h // 2) * 128 + 128].astype(jnp.float32)
        if h % 2 != h // 2:
            pair = pltpu.roll(pair, HEAD_DIM, 1)
        own = (lane < HEAD_DIM) if h // 2 == 0 else (lane >= HEAD_DIM)
        out_ref[pl.ds(h * n, n), :] = jnp.where(own, pair, 0.0).astype(out_ref.dtype)


def attend_block(key_rows, value_rows, first, qpad_ref, max_ref, sum_ref, out_t_ref):
    half = BLOCK // 2
    for h in range(4):
        group = (h // 2) * HEAD_DIM
        for t in range(2):
            cols = slice(t * half, (t + 1) * half)
            rows = half if first and t == 0 else BLOCK
            scores = mm(key_rows[:rows], qpad_ref[h, :, cols])
            if first:
                key_at = lax.broadcasted_iota(jnp.int32, scores.shape, 0)
                query_at = lax.broadcasted_iota(jnp.int32, scores.shape, 1) + t * half
                scores = jnp.where(key_at > query_at, masked_score, scores)
            new_max = jnp.max(scores, axis=0, keepdims=True)
            if not first:
                old_max = max_ref[h : h + 1, cols]
                new_max = jnp.maximum(new_max, old_max)
                shrink = jnp.exp(old_max - new_max)
            weights = jnp.exp(scores - new_max)
            total = jnp.sum(weights, axis=0, keepdims=True)
            part = mm(value_rows[:rows], weights.astype(jnp.bfloat16), TN)[group : group + HEAD_DIM]
            mine = pl.ds(h * HEAD_DIM, HEAD_DIM)
            if not first:
                total = total + sum_ref[h : h + 1, cols] * shrink
                part = part + out_t_ref[mine, cols] * shrink
            max_ref[h : h + 1, cols] = new_max
            sum_ref[h : h + 1, cols] = total
            out_t_ref[mine, cols] = part


def attend_own_kernel(q_ref, own_ref, qpad_ref, max_ref, sum_ref, out_t_ref):
    padded_columns(jnp.transpose(q_ref[...].astype(jnp.float32) * score_mult), qpad_ref)
    max_ref[...] = jnp.zeros_like(max_ref)
    sum_ref[...] = jnp.ones_like(sum_ref)
    attend_block(own_ref[:, :LANES], own_ref[:, LANES:], True, qpad_ref, max_ref, sum_ref, out_t_ref)


def attend_own(queries, own_kv):
    return pl.pallas_call(
        attend_own_kernel,
        name="attend_own",
        in_specs=[vmem()] * 2,
        out_specs=[vmem()] * 4,
        out_shape=[
            out((4, LANES, BLOCK), jnp.bfloat16),
            out((8, BLOCK), jnp.float32),
            out((8, BLOCK), jnp.float32),
            out((SHARE, BLOCK), jnp.float32),
        ],
        compiler_params=pltpu.CompilerParams(vmem_limit_bytes=36 << 20),
        cost_estimate=cost(1_000_000_000, 2_000_000, 600_000),
    )(queries, own_kv)


def attend_kernel(
    reach_ref, qpad_ref, max0_ref, sum0_ref, out0_ref, prev_ref, att_ref, out_t_ref, lse_ref, max_ref, sum_ref
):
    max_ref[...] = max0_ref[...]
    sum_ref[...] = sum0_ref[...]
    out_t_ref[...] = out0_ref[...]

    @pl.loop(1, reach_ref[0] + 1)
    def _(step):
        rows = prev_ref[:, pl.ds(step - 1, 1)].reshape(BLOCK, SHARE)
        attend_block(rows[:, :LANES], rows[:, LANES:], False, qpad_ref, max_ref, sum_ref, out_t_ref)

    lse_ref[...] = max_ref[...] + jnp.log(sum_ref[...])
    for h in range(4):
        mine = pl.ds(h * HEAD_DIM, HEAD_DIM)
        out_t_ref[mine, :] = out_t_ref[mine, :] / sum_ref[h : h + 1, :]
    att_ref[...] = jnp.transpose(out_t_ref[...]).astype(jnp.bfloat16)


def attend(reach, begun, earlier):
    return run(
        attend_kernel,
        "attend",
        1,
        [smem()] + [vmem()] * 5,
        [None] * 3,
        [
            out((BLOCK, SHARE), jnp.bfloat16),
            out((SHARE, BLOCK), jnp.float32),
            out((8, BLOCK), jnp.float32),
        ],
        (reach, *begun, earlier),
        cost(4_000_000_000, 3_000_000, 3_000_000),
        [pltpu.VMEM((8, BLOCK), jnp.float32), pltpu.VMEM((8, BLOCK), jnp.float32)],
        limit=36,
    )


def attend_back_kernel(
    reach_ref, q_ref, qpad_ref, own_ref, prev_ref, grad_ref, grad_t_ref, out_t_ref, lse_ref, cos_ref, sin_ref,
    qgrad_ref, own_grad_ref, prev_grad_ref,
    gpad_ref, qrows_ref, grows_ref, ds_ref, p_ref, delta_ref, dq_ref,
):
    half = BLOCK // 2
    q_scaled = q_ref[...].astype(jnp.float32) * score_mult
    padded_rows(q_scaled, qrows_ref)
    padded_columns(grad_t_ref[...], gpad_ref)
    padded_rows(grad_ref[...], grows_ref)
    both = grad_t_ref[...].astype(jnp.float32) * out_t_ref[...]
    for h in range(4):
        delta_ref[h : h + 1, :] = jnp.sum(
            both[h * HEAD_DIM : (h + 1) * HEAD_DIM], axis=0, keepdims=True
        )


    def block(key_rows, value_rows, first):
        for h in range(4):
            for t in range(2):
                cols = slice(t * half, (t + 1) * half)
                wide = slice(h * BLOCK + t * half, h * BLOCK + (t + 1) * half)
                rows = half if first and t == 0 else BLOCK
                scores = mm(key_rows[:rows], qpad_ref[h, :, cols])
                weights = jnp.exp(scores - lse_ref[h : h + 1, cols])
                if first:
                    key_at = lax.broadcasted_iota(jnp.int32, scores.shape, 0)
                    query_at = lax.broadcasted_iota(jnp.int32, scores.shape, 1) + t * half
                    weights = jnp.where(key_at > query_at, 0.0, weights)
                weight_grad = mm(value_rows[:rows], gpad_ref[h, :, cols])
                score_grad = weights * (weight_grad - delta_ref[h : h + 1, cols])
                p_ref[:rows, wide] = weights.astype(jnp.bfloat16)
                ds_ref[:rows, wide] = score_grad.astype(jnp.bfloat16)
                if rows < BLOCK:
                    p_ref[rows:, wide] = jnp.zeros((BLOCK - rows, half), jnp.bfloat16)
                    ds_ref[rows:, wide] = jnp.zeros((BLOCK - rows, half), jnp.bfloat16)
        key_grad = mm(ds_ref[...], qrows_ref[...])
        value_grad = mm(p_ref[...], grows_ref[...])
        for h in range(4):
            group = (h // 2) * HEAD_DIM
            mine = pl.ds(h * HEAD_DIM, HEAD_DIM)
            part = mm(key_rows, ds_ref[:, h * BLOCK : (h + 1) * BLOCK], TN)[group : group + HEAD_DIM]
            dq_ref[mine, :] = part if first else dq_ref[mine, :] + part
        return key_grad, value_grad

    key_grad, value_grad = block(own_ref[:, :LANES], own_ref[:, LANES:], True)
    own_grad_ref[:, :LANES] = key_grad
    own_grad_ref[:, LANES:] = value_grad

    @pl.loop(1, reach_ref[0] + 1)
    def _(step):
        rows = prev_ref[:, pl.ds(step - 1, 1)].reshape(BLOCK, SHARE)
        key_grad, value_grad = block(rows[:, :LANES], rows[:, LANES:], False)
        parts = prev_grad_ref.shape[0]
        shape = (parts, 1, BLOCK // parts, LANES)
        prev_grad_ref[:, pl.ds(step - 1, 1), :, :LANES] = key_grad.astype(jnp.bfloat16).reshape(shape)
        prev_grad_ref[:, pl.ds(step - 1, 1), :, LANES:] = value_grad.astype(jnp.bfloat16).reshape(shape)

    query_grad = jnp.transpose(dq_ref[...]) * score_mult
    for i in range(0, SHARE, LANES):
        qgrad_ref[:, i : i + LANES] = turned(
            query_grad[:, i : i + LANES], cos_ref[...], sin_ref[...], back=True
        ).astype(jnp.bfloat16)


def attend_back(reach, queries, padded, own_kv, earlier, grad, grad_t, out_t, lse, cosine, signed_sine):
    return run(
        attend_back_kernel,
        "attend_back",
        1,
        [smem()] + [vmem()] * 10,
        [None] * 3,
        [
            out((BLOCK, SHARE), jnp.bfloat16),
            out((BLOCK, SHARE), jnp.float32),
            out(earlier.shape, jnp.bfloat16),
        ],
        (reach, queries, padded, own_kv, earlier, grad, grad_t, out_t, lse, cosine, signed_sine),
        cost(12_000_000_000, 5_000_000, 3_000_000),
        [
            pltpu.VMEM((4, LANES, BLOCK), jnp.bfloat16),
            pltpu.VMEM((4 * BLOCK, LANES), jnp.bfloat16),
            pltpu.VMEM((4 * BLOCK, LANES), jnp.bfloat16),
            pltpu.VMEM((BLOCK, 4 * BLOCK), jnp.bfloat16),
            pltpu.VMEM((BLOCK, 4 * BLOCK), jnp.bfloat16),
            pltpu.VMEM((8, BLOCK), jnp.float32),
            pltpu.VMEM((SHARE, BLOCK), jnp.float32),
        ],
        limit=36,
    )


def residual_kernel(
    a0, a1, a2, a3, w0, w1, w2, w3, x_ref, gain_ref, router_ref, ranks_ref, picks_ref,
    residual_ref, moe_ref, gates_ref, rows_ref, held_ref,
):
    step = pl.program_id(0)
    tile = x_ref.shape[0]

    @pl.when(step < BLOCK // tile)
    def _():
        branch = mm(a0[...], w0[...])
        for a, w in ((a1, w1), (a2, w2), (a3, w3)):
            branch = branch + mm(a[...], w[...])
        residual = x_ref[...].astype(jnp.float32) + residual_mult * branch
        residual_ref[...] = residual
        scale = lax.rsqrt(jnp.mean(residual * residual, axis=1, keepdims=True) + epsilon)
        moe_in = (residual * scale * gain_ref[...]).astype(jnp.bfloat16)
        moe_ref[:, :WIDTH] = moe_in
        logits = mm(router_ref[...], moe_in, NT)
        chosen = ranks_ref[...] >= 0.0
        kept = jnp.where(chosen, logits, masked_score)
        top = jnp.max(kept, axis=0, keepdims=True)
        raised = jnp.where(chosen, jnp.exp(kept - top), 0.0)
        gates = raised / jnp.sum(raised, axis=0, keepdims=True)
        gates_ref[...] = gates
        low = (residual_mult * jnp.transpose(gates)).astype(jnp.bfloat16)
        moe_ref[:, WIDTH:] = low
        held_ref[pl.ds(step * tile, tile), :WIDTH] = moe_in
        held_ref[pl.ds(step * tile, tile), WIDTH:] = low

    @pl.when(step >= BLOCK // tile)
    def _():
        rows_ref[...] = mm(picks_ref[...], held_ref[...]).astype(jnp.bfloat16)


def residual_step(attended, w_out, x, gain, router_t, ranks, picks):
    tile = 256
    first = BLOCK // tile
    slot_tile = SLOTS // 4

    def early(rows, width):
        return pl.BlockSpec((rows, width), lambda i: (jnp.minimum(i, first - 1), 0))

    def late(rows, width):
        return pl.BlockSpec((rows, width), lambda i: (jnp.maximum(i - first, 0), 0))

    by_columns = pl.BlockSpec((LANES, tile), lambda i: (0, jnp.minimum(i, first - 1)))
    return run(
        residual_kernel,
        "residual_step",
        first + 4,
        [early(tile, SHARE)] * 4
        + [None] * 4
        + [early(tile, WIDTH), None, None, by_columns, late(slot_tile, BLOCK)],
        [early(tile, WIDTH), early(tile, WIDTH + LANES), by_columns, late(slot_tile, WIDTH + LANES)],
        [
            out((BLOCK, WIDTH), jnp.float32),
            out((BLOCK, WIDTH + LANES), jnp.bfloat16),
            out((LANES, BLOCK), jnp.float32),
            out((SLOTS, WIDTH + LANES), jnp.bfloat16),
        ],
        (*attended, *w_out, x, gain, router_t, ranks, picks),
        cost(2_700_000_000, 12_000_000, 70_000),
        [pltpu.VMEM((BLOCK, WIDTH + LANES), jnp.bfloat16)],
        free=(1, 2, 3, 5, 6, 7, 10),
    )


def mix_kernel(begin_ref, ranks_ref, moe_ref, mix_ref):
    ranks = jnp.transpose(ranks_ref[...]).astype(jnp.bfloat16)
    gates = moe_ref[:, WIDTH:]
    width = 640
    for at in range(0, SLOTS, width):
        expert_at = lax.broadcasted_iota(jnp.int32, (LANES, width), 0)
        first = expert_at * QUARTER - at
        slot_at = lax.broadcasted_iota(jnp.int32, (LANES, width), 1)
        inside = jnp.logical_and(slot_at >= first, slot_at < first + QUARTER)
        spread = jnp.where(inside, 1.0, 0.0).astype(jnp.bfloat16)
        within = jnp.sum(jnp.where(inside, slot_at - first, 0), axis=0, keepdims=True) + begin_ref[0]
        hit = mm(ranks, spread) == within.astype(jnp.float32)
        mix_ref[:, at : at + width] = jnp.where(hit, mm(gates, spread), 0.0).astype(jnp.bfloat16)


def mix_weights(begin, ranks, moe_cat):
    return run(
        mix_kernel,
        "mix_weights",
        1,
        [smem(), None, None],
        [None],
        [out((BLOCK, SLOTS), jnp.bfloat16)],
        (begin, ranks, moe_cat),
        cost(350_000_000, 3_000_000),
    )[0]


def expert_kernel(lane_ref, x_ref, grad_ref, *refs):
    downs, gate_refs, up_refs = refs[:4], refs[4:8], refs[8:12]
    out_ref, row_ref, hidden_ref, units_ref = refs[12:]
    rows = out_ref.shape[0]
    here = pl.ds(pl.program_id(0) * rows, rows)
    lane = lax.broadcasted_iota(jnp.int32, (rows, LANES), 1) == lane_ref[0]
    gate = jnp.sum(
        jnp.where(lane, x_ref[here, WIDTH:].astype(jnp.float32), 0.0), axis=1, keepdims=True
    )
    x = x_ref[here, :WIDTH]
    grad = grad_ref[...]
    gates, ups, sigmoids, hidden = [], [], [], []
    for j in range(4):
        pre = mm(x, jnp.concatenate([gate_refs[j][...], up_refs[j][...]], axis=1))
        gate_pre, up_pre = pre[:, :LANES], pre[:, LANES:]
        sigmoid = 1.0 / (1.0 + jnp.exp(-gate_pre))
        gates.append(gate_pre)
        ups.append(up_pre)
        sigmoids.append(sigmoid)
        hidden.append(gate_pre * sigmoid * up_pre)
    hidden_low = jnp.concatenate([h.astype(jnp.bfloat16) for h in hidden], axis=1)
    down = jnp.concatenate([p[...] for p in downs], axis=0)
    made = mm(hidden_low, down).astype(jnp.bfloat16)
    out_ref[...] = made
    gate_grad = jnp.sum(grad.astype(jnp.float32) * made.astype(jnp.float32), axis=1, keepdims=True)
    row_ref[:, WIDTH:] = jnp.where(lane, gate_grad, 0.0).astype(jnp.bfloat16)
    hidden_grad = mm(grad, down, NT)
    row = None
    for j in range(4):
        part = hidden_grad[:, j * LANES : (j + 1) * LANES]
        silu = gates[j] * sigmoids[j]
        gate_pre_grad = part * ups[j] * sigmoids[j] * (1.0 + gates[j] * (1.0 - sigmoids[j]))
        up_pre_grad = part * silu
        hidden_ref[:, j * LANES : (j + 1) * LANES] = (hidden[j] * gate).astype(jnp.bfloat16)
        units_ref[:, j * SHARE : j * SHARE + LANES] = (gate_pre_grad * gate).astype(jnp.bfloat16)
        units_ref[:, j * SHARE + LANES : (j + 1) * SHARE] = (up_pre_grad * gate).astype(jnp.bfloat16)
        both = jnp.concatenate([gate_pre_grad, up_pre_grad], axis=1).astype(jnp.bfloat16)
        term = mm(both, jnp.concatenate([gate_refs[j][...], up_refs[j][...]], axis=1), NT)
        row = term if row is None else row + term
    row_ref[:, :WIDTH] = row.astype(jnp.bfloat16)


def expert_step(lane, x, grad, downs, gates, ups):
    tile = 320
    return run(
        expert_kernel,
        "expert_step",
        SLOTS // tile,
        [smem(), vmem(), tiles(tile, WIDTH)] + [None] * 12,
        [tiles(tile, WIDTH), tiles(tile, WIDTH + LANES), tiles(tile, 512), tiles(tile, WIDTH)],
        [
            out((SLOTS, WIDTH), jnp.bfloat16),
            out((SLOTS, WIDTH + LANES), jnp.bfloat16),
            out((SLOTS, 512), jnp.bfloat16),
            out((SLOTS, WIDTH), jnp.bfloat16),
        ],
        (lane, x, grad, *downs, *gates, *ups),
        cost(8_000_000_000, 18_000_000, 700_000),
        limit=40,
    )


def unit_grads_kernel(x_ref, grad_ref, hidden_ref, units_ref, keep_ref, send_ref, turned_ref):
    step = pl.program_id(0)

    @pl.when(step == 0)
    def _():
        for k in range(4):
            columns = slice(k * SHARE, (k + 1) * SHARE)
            turned_ref[columns, :] = jnp.transpose(x_ref[:, columns])

    def write(to_ref):
        to_ref[0, :LANES, :] = mm(hidden_ref[...], grad_ref[...], TN).astype(jnp.bfloat16)
        for k in range(4):
            columns = slice(k * SHARE, (k + 1) * SHARE)
            to_ref[0, LANES:, columns] = mm(turned_ref[columns, :], units_ref[...]).astype(jnp.bfloat16)

    @pl.when(step < 2)
    def _():
        write(keep_ref)

    @pl.when(step >= 2)
    def _():
        write(send_ref)


def unit_grads(x, grad, hidden, units):
    rows = SHARE + LANES

    def share_of(i):
        return jnp.where(i < 2, 2 * i, 2 * i - 3)

    return run(
        unit_grads_kernel,
        "unit_grads",
        4,
        [
            vmem(),
            None,
            pl.BlockSpec((SLOTS, LANES), lambda i: (0, share_of(i))),
            pl.BlockSpec((SLOTS, SHARE), lambda i: (0, share_of(i))),
        ],
        [
            pl.BlockSpec((1, rows, WIDTH), lambda i: (jnp.minimum(i, 1), 0, 0)),
            pl.BlockSpec((1, rows, WIDTH), lambda i: (jnp.maximum(i - 2, 0), 0, 0)),
        ],
        [out((2, rows, WIDTH), jnp.bfloat16), out((2, rows, WIDTH), jnp.bfloat16)],
        (x, grad, hidden, units),
        cost(4_000_000_000, 12_000_000),
        [pltpu.VMEM((WIDTH, SLOTS), jnp.bfloat16)],
        limit=36,
    )


def unit_finish_kernel(mine_ref, first_ref, second_ref, gate_ref, up_ref, down_ref):
    got = jnp.concatenate([first_ref[...], second_ref[...]], axis=0)
    total = mine_ref[0] + got.astype(jnp.float32)
    down_ref[0] = total[:LANES, :]
    for k in range(4):
        rows = slice(k * SHARE, (k + 1) * SHARE)
        gate_ref[0, rows, :] = total[LANES:, k * SHARE : k * SHARE + LANES]
        up_ref[0, rows, :] = total[LANES:, k * SHARE + LANES : (k + 1) * SHARE]


def unit_finish(mine, first, second):
    return run(
        unit_finish_kernel,
        "unit_finish",
        1,
        [once(1, PACKED, WIDTH), None, None],
        [None] * 3,
        [
            out((1, WIDTH, LANES), jnp.float32),
            out((1, WIDTH, LANES), jnp.float32),
            out((1, LANES, WIDTH), jnp.float32),
        ],
        (mine, first, second),
        cost(1_000_000, 3_000_000),
        free=(0, 1, 2),
    )


def home_kernel(rank_ref, mix_ref, rows_ref, keep_ref, send_ref):
    rank = rank_ref[0]
    extra = rows_ref.shape[1] > WIDTH
    for j in range(4):
        at = pl.multiple_of(jnp.bitwise_xor(rank, j) * SHARE, SHARE)
        total = mm(mix_ref[...], rows_ref[:, pl.ds(at, SHARE)])
        to_ref = send_ref if j % 2 else keep_ref
        to_ref[(j // 2) * BLOCK : (j // 2 + 1) * BLOCK, :] = total.astype(to_ref.dtype)
    if extra:
        gate_grads = jnp.transpose(mm(mix_ref[...], rows_ref[:, WIDTH:]))[:EXPERTS]
        for to_ref in (keep_ref, send_ref):
            for i in range(2):
                at = 2 * BLOCK + i * EXPERTS
                to_ref[at : at + EXPERTS, :] = gate_grads[:, i * SHARE : (i + 1) * SHARE].astype(
                    to_ref.dtype
                )


def sum_home(rank, mix, rows):
    height = 2 * BLOCK + (2 * EXPERTS if rows.shape[1] > WIDTH else 0)
    return run(
        home_kernel,
        "sum_home",
        1,
        [smem(), None, vmem()],
        [None] * 2,
        [out((height, SHARE), jnp.float32), out((height, SHARE), jnp.bfloat16)],
        (rank, mix, rows),
        cost(1_500_000_000, 6_000_000),
        limit=36,
    )


def swap_kernel(mine_ref, got_ref, total_ref):
    mine, got = mine_ref, got_ref
    half = BLOCK
    total_ref[:half] = (mine[:half] + got[half : 2 * half].astype(jnp.float32)).astype(total_ref.dtype)
    total_ref[half : 2 * half] = (
        mine[half : 2 * half] + got[:half].astype(jnp.float32)
    ).astype(total_ref.dtype)
    total_ref[2 * half :] = (mine[2 * half :] + got[2 * half :].astype(jnp.float32)).astype(
        total_ref.dtype
    )


def swap_sum(mine, got):
    return run(
        swap_kernel,
        "swap_sum",
        1,
        [None] * 2,
        [None],
        [out(mine.shape, jnp.bfloat16)],
        (mine, got),
        cost(1_000_000, 2_500_000),
        free=(0, 1),
    )[0]


def norm_back_kernel(
    rank_ref, g0, g2, g1, g3, z_ref, gates_ref, residual_ref, gain_ref, router_ref, grad_ref, w_ref,
    low_ref, logit_ref, own_ref, att_ref, att_t_ref, gain_grad_ref, u_ref,
):
    rank = rank_ref[0]
    for flip, part in enumerate((g0, g1, g2, g3)):
        at = pl.multiple_of(jnp.bitwise_xor(rank, flip) * SHARE, SHARE)
        u_ref[:, pl.ds(at, SHARE)] = part[...].astype(jnp.float32)
    weighted_grads = z_ref[...].astype(jnp.float32)
    gates = gates_ref[:EXPERTS, :]
    inner = jnp.sum(weighted_grads, axis=0, keepdims=True)
    logit_grad = (weighted_grads - gates * inner).astype(jnp.bfloat16)
    logit_ref[...] = logit_grad
    u = u_ref[...] + mm(logit_grad, router_ref[:EXPERTS, :], TN)
    v = residual_ref[...]
    scale = lax.rsqrt(jnp.mean(v * v, axis=1, keepdims=True) + epsilon)
    weighted = u * gain_ref[...]
    mean = jnp.mean(weighted * v, axis=1, keepdims=True)
    total = grad_ref[...].astype(jnp.float32) + scale * weighted - v * (scale * scale * scale * mean)

    @pl.when(pl.program_id(0) == 0)
    def _():
        gain_grad_ref[...] = jnp.zeros_like(gain_grad_ref)

    gain_grad_ref[0:1, :] += jnp.sum(u * v * scale, axis=0, keepdims=True)
    low = (residual_mult * total).astype(jnp.bfloat16)
    low_ref[...] = low
    u_ref[...] = total
    own_ref[...] = u_ref[:, pl.ds(pl.multiple_of(rank * SHARE, SHARE), SHARE)]
    att_ref[...] = mm(low, w_ref[...], NT).astype(jnp.bfloat16)
    att_t_ref[...] = mm(w_ref[...], low, NT).astype(jnp.bfloat16)


def norm_back_step(rank, mine, theirs, gates, residual, gain, router_t, out_grad, w_out):
    tile = 256
    by_columns = pl.BlockSpec((EXPERTS, tile), lambda i: (0, i))
    return run(
        norm_back_kernel,
        "norm_back_step",
        BLOCK // tile,
        [smem()]
        + [tiles(tile, SHARE), tiles(tile, SHARE, BLOCK // tile)] * 2
        + [
            tiles(EXPERTS, SHARE, 2 * BLOCK // EXPERTS),
            pl.BlockSpec((LANES, tile), lambda i: (0, i)),
            tiles(tile, WIDTH),
            None,
            None,
            tiles(tile, WIDTH),
            None,
        ],
        [
            tiles(tile, WIDTH),
            by_columns,
            tiles(tile, SHARE),
            tiles(tile, SHARE),
            pl.BlockSpec((SHARE, tile), lambda i: (0, i)),
            fixed(8, WIDTH),
        ],
        [
            out((BLOCK, WIDTH), jnp.bfloat16),
            out((EXPERTS, BLOCK), jnp.bfloat16),
            out((BLOCK, SHARE), jnp.float32),
            out((BLOCK, SHARE), jnp.bfloat16),
            out((SHARE, BLOCK), jnp.bfloat16),
            out((8, WIDTH), jnp.float32),
        ],
        (rank, mine, mine, theirs, theirs, mine, gates, residual, gain, router_t, out_grad, w_out),
        cost(700_000_000, 9_000_000, 512),
        [pltpu.VMEM((tile, WIDTH), jnp.float32)],
        free=(3, 4, 9),
    )


def dense_grads_kernel(low_ref, attended_ref, normed_ref, qgrad_ref, logit_ref, moe_ref, gain_ref, made_ref):
    made_ref[:, :SHARE] = mm(low_ref[...], attended_ref[...], TN).astype(jnp.bfloat16)
    made_ref[:, SHARE : 2 * SHARE] = mm(normed_ref[...], qgrad_ref[...], TN).astype(jnp.bfloat16)
    router = mm(logit_ref[...], moe_ref[:, :WIDTH])
    stacked = jnp.concatenate(
        [router, gain_ref[...], jnp.zeros((LANES - EXPERTS - 8, WIDTH), jnp.float32)], axis=0
    )
    made_ref[:, 2 * SHARE :] = jnp.transpose(stacked).astype(jnp.bfloat16)


def dense_grads(low, attended, normed, qgrad, logit, moe_cat, gain_grad):
    return run(
        dense_grads_kernel,
        "dense_grads",
        1,
        [None] * 7,
        [None],
        [out((WIDTH, 2 * SHARE + LANES), jnp.bfloat16)],
        (low, attended, normed, qgrad, logit, moe_cat, gain_grad),
        cost(600_000_000, 6_000_000),
    )[0]


def last_grads_kernel(
    rank_ref, own_ref, home_ref, qgrad_ref, normed_ref, x_ref, wq_ref, wk_ref, wv_ref, cos_ref, sin_ref, made_ref,
    gain_ref, all_ref, keep_ref, send_ref, inner_ref, part_ref,
):
    rank = rank_ref[0]
    kv = own_ref[...] + home_ref[...].astype(jnp.float32)
    key_grad = turned(kv[:, :LANES], cos_ref[...], sin_ref[...], back=True).astype(jnp.bfloat16)
    value_grad = kv[:, LANES:].astype(jnp.bfloat16)
    both = jnp.concatenate([key_grad, value_grad], axis=1)
    all_ref[:, : 2 * SHARE] = made_ref[:, : 2 * SHARE]
    all_ref[:, 2 * SHARE : 3 * SHARE] = mm(normed_ref[...], both, TN).astype(jnp.bfloat16)
    gain = jnp.zeros((1, WIDTH), jnp.float32)
    tile = 128
    for i in range(0, BLOCK, tile):
        rows = slice(i, i + tile)
        part = mm(qgrad_ref[rows, :], wq_ref[...], NT)
        part = part + mm(key_grad[rows], wk_ref[...], NT) + mm(value_grad[rows], wv_ref[...], NT)
        x = x_ref[rows, :].astype(jnp.float32)
        scale = lax.rsqrt(jnp.mean(x * x, axis=1, keepdims=True) + epsilon)
        along = part * x
        gain = gain + jnp.sum(along * scale, axis=0, keepdims=True)
        inner = jnp.sum(along * gain_ref[...], axis=1, keepdims=True)
        inner_ref[:, rows] = jnp.transpose(jnp.broadcast_to(inner, (tile, LANES)))[:8]
        part_ref[rows, :] = part
    for j in range(4):
        at = pl.multiple_of(jnp.bitwise_xor(rank, j) * SHARE, SHARE)
        to_ref = send_ref if j % 2 else keep_ref
        to_ref[(j // 2) * BLOCK : (j // 2 + 1) * BLOCK, :] = part_ref[:, pl.ds(at, SHARE)].astype(to_ref.dtype)
    lane = lax.broadcasted_iota(jnp.int32, (WIDTH, LANES), 1)
    column = jnp.transpose(jnp.broadcast_to(gain, (LANES, WIDTH)))
    rest = jnp.where(lane == EXPERTS + 8, column, made_ref[:, 2 * SHARE :].astype(jnp.float32))
    all_ref[:, 3 * SHARE :] = rest.astype(jnp.bfloat16)


def last_grads(rank, own, home, qgrad, normed, x, w_query, w_key, w_value, cosine, sine, made, gain):
    return run(
        last_grads_kernel,
        "last_grads",
        1,
        [smem()] + [None] * 12,
        [None] * 4,
        [
            out((WIDTH, 3 * SHARE + LANES), jnp.bfloat16),
            out((2 * BLOCK, SHARE), jnp.float32),
            out((2 * BLOCK, SHARE), jnp.bfloat16),
            out((8, BLOCK), jnp.float32),
        ],
        (rank, own, home, qgrad, normed, x, w_query, w_key, w_value, cosine, sine, made, gain),
        cost(1_000_000_000, 8_000_000, 512),
        [pltpu.VMEM((BLOCK, WIDTH), jnp.float32)],
        free=(2,),
    )


def input_finish_kernel(
    rank_ref, near_ref, far_ref, i0, i1, i2, i3, x_ref, gain_ref, residual_ref, made_ref
):
    mine = pl.ds(pl.multiple_of(rank_ref[0] * SHARE, SHARE), SHARE)
    x = x_ref[...].astype(jnp.float32)
    scale = lax.rsqrt(jnp.mean(x * x, axis=1, keepdims=True) + epsilon)
    inner = (i0[...] + i1[...] + i2[...] + i3[...]) * (1.0 / WIDTH)
    inner = jnp.transpose(jnp.broadcast_to(inner[:1], (LANES, BLOCK)))[:, :1]
    weighted = (near_ref[...] + far_ref[...].astype(jnp.float32)) * gain_ref[:, mine]
    x_own = x_ref[:, mine].astype(jnp.float32)
    made_ref[...] = residual_ref[...] + scale * weighted - x_own * (scale * scale * scale * inner)


def input_finish(rank, near, far, inners, x, gain, residual):
    return run(
        input_finish_kernel,
        "input_finish",
        1,
        [smem(), once(BLOCK, SHARE), None] + [None] * 7,
        [None],
        [out((BLOCK, SHARE), jnp.float32)],
        (rank, near, far, *inners, x, gain, residual),
        cost(3_000_000, 3_000_000, 512),
        free=(1, 2, 3, 4, 5, 6),
    )[0]


def per_device(
    hidden_in,
    lengths,
    block_order,
    routes,
    norm_gain_attn,
    w_query,
    w_key,
    w_value,
    w_out,
    norm_gain_moe,
    w_router,
    w_gate,
    w_up,
    w_down,
    out_grad,
):
    dp_count = block_order.shape[0]
    mp_rank = lax.axis_index("mp").astype(jnp.int32)
    column_start = mp_rank * SHARE
    piece = BLOCK // dp_count
    steps = MAXLEN // BLOCK - 1
    rank = mp_rank.reshape(1)
    lane = lax.axis_index("dp").astype(jnp.int32).reshape(1)
    begin = rank * QUARTER
    gain_attn = norm_gain_attn[None, :]
    gain_moe = norm_gain_moe[None, :]
    router_t = jnp.pad(w_router.T, ((0, LANES - EXPERTS), (0, 0)))

    far_out = peer(w_out, 2)
    far_down = peer(w_down[0], 2)

    normed, key_value, cosine, sine, reach, wanted, later, live = project(
        lengths, block_order, lane, hidden_in, gain_attn, w_key, w_value
    )
    queries = project_queries(normed, w_query, cosine, sine)
    pieces = to_all(key_value.reshape(dp_count, piece, SHARE))
    picks, ranks = route(begin, after(routes.T, key_value))
    begun = attend_own(queries, key_value)
    far_gate = peer(after(w_gate[0], key_value), 2)
    picked = pick_pieces(wanted, after(pieces, far_out, far_down, begun[1], picks, far_gate))
    far_up = peer(after(w_up[0], picked), 2)
    earlier = to_all(picked.reshape(dp_count, steps * piece, SHARE))
    earlier = earlier.reshape(dp_count, steps, piece, SHARE)

    outs = [w_out, peer(after(w_out, picked), 1), far_out, peer(far_out, 1)]

    grad_rows = jnp.dot(picks, after(out_grad, picked), preferred_element_type=jnp.bfloat16)
    grad_arrived = to_experts(after(grad_rows, earlier, far_up).reshape(EXPERTS, QUARTER, WIDTH))
    attended, attended_t, lse = attend(reach, begun, earlier)
    far = peer(attended, 2)
    residual, moe_cat, gates, moe_rows = residual_step(
        [attended, peer(attended, 1), far, peer(far, 1)],
        outs,
        hidden_in,
        gain_moe,
        router_t,
        ranks,
        picks,
    )
    own = [after(w[0], moe_rows) for w in (w_down, w_gate, w_up)]
    far = [after(w, moe_rows) for w in (far_down, far_gate, far_up)]
    downs, gates_all, ups = [[w, peer(w, 1), v, peer(v, 1)] for w, v in zip(own, far)]
    grouped = to_experts(moe_rows.reshape(EXPERTS, QUARTER, -1)).reshape(SLOTS, -1)
    mix = mix_weights(begin, ranks, moe_cat)
    grouped_grad = grad_arrived.reshape(SLOTS, WIDTH)
    rows_out, row_grad, hidden_units, unit_grad = expert_step(
        lane, grouped, grouped_grad, downs, gates_all, ups
    )
    row_home = to_experts(row_grad.reshape(dp_count, QUARTER, -1)).reshape(SLOTS, -1)
    rows_home = to_experts(after(rows_out, row_home).reshape(dp_count, QUARTER, -1)).reshape(SLOTS, -1)

    unit_keep, unit_send = unit_grads(grouped, grouped_grad, hidden_units, unit_grad)
    unit_near = unit_keep.astype(jnp.float32) + peer(unit_send, 1).astype(jnp.float32)
    unit_low = unit_near[1].astype(jnp.bfloat16)
    cut = PACKED * 3 // 4
    unit_far_a = peer(unit_low[:cut], 2)
    keep, send = sum_home(rank, after(mix, unit_far_a), row_home)
    near = keep + peer(send, 1).astype(jnp.float32)
    mine = swap_sum(near, peer(near.astype(jnp.bfloat16), 2))
    theirs = peer(mine, 1)
    branch_grad, logit_grad, residual_grad, attended_grad, attended_grad_t, moe_gain = norm_back_step(
        rank, mine, theirs, gates, residual, gain_moe, router_t, out_grad, w_out
    )

    query_pre_grad, own_grads, later_grads = attend_back(
        reach,
        queries,
        begun[0],
        key_value,
        earlier,
        attended_grad,
        attended_grad_t,
        attended_t,
        lse,
        cosine,
        sine,
    )
    unit_far_b = peer(after(unit_low[cut:], later_grads), 2)
    later_pieces = to_all(after(later_grads, rows_home).reshape(dp_count, steps * piece, SHARE))
    summed = sum_pieces(
        later, live, later_pieces.reshape(dp_count * steps, piece, SHARE), dp_count
    )
    kv_home = to_all(summed).reshape(BLOCK, SHARE)
    made = dense_grads(
        branch_grad, attended, normed, query_pre_grad, logit_grad, moe_cat, moe_gain
    )

    unit_far_c = peer(after(unit_low[cut:], kv_home, made), 2)

    every, keep, send, inner = last_grads(
        rank,
        own_grads,
        kv_home,
        query_pre_grad,
        normed,
        hidden_in,
        w_query,
        w_key,
        w_value,
        cosine,
        sine,
        made,
        gain_attn,
    )
    near_norm = keep + peer(send, 1).astype(jnp.float32)
    far_norm = peer(near_norm[BLOCK:].astype(jnp.bfloat16), 2)
    inners = [inner] + [peer(inner, flip) for flip in (1, 2, 3)]
    every = after(every, unit_far_c)
    arrived = to_all(every.reshape(dp_count, WIDTH // dp_count, -1))
    keep, send = sum_home(rank, mix, after(rows_home, every))
    near_mix = keep + peer(send, 1).astype(jnp.float32)
    far_mix = peer(near_mix[BLOCK:].astype(jnp.bfloat16), 2)
    grad_w_gate, grad_w_up, grad_w_down = unit_finish(
        unit_near, unit_far_a, after(unit_far_c, every)
    )
    dense = jnp.sum(arrived.astype(jnp.float32), axis=0)
    at = 3 * SHARE
    attn_gain = dense[:, at + EXPERTS + 8]
    attn_gain = attn_gain + peer(attn_gain, 1) + peer(attn_gain, 2) + peer(attn_gain, 3)
    residual_cols = lax.dynamic_slice_in_dim(residual, column_start, SHARE, 1)
    mixture = near_mix[:BLOCK] + after(far_mix, attn_gain).astype(jnp.float32)
    out_hidden = (residual_cols + mixture).astype(jnp.bfloat16)

    grad_hidden = input_finish(
        rank, near_norm, after(far_norm, dense), inners, hidden_in, gain_attn, residual_grad
    )
    return (
        out_hidden,
        grad_hidden,
        dense[:, SHARE : 2 * SHARE],
        dense[:, 2 * SHARE : 2 * SHARE + LANES],
        dense[:, 2 * SHARE + LANES : at],
        dense[:, :SHARE].T,
        attn_gain,
        dense[:, at + EXPERTS],
        dense[:, at : at + EXPERTS],
        grad_w_gate,
        grad_w_up,
        grad_w_down,
    )


def solution(mesh):
    in_specs = (
        P("dp", None),
        P(),
        P(),
        P("dp", None),
        P(),
        P(None, "mp"),
        P(None, "mp"),
        P(None, "mp"),
        P("mp", None),
        P(),
        P(),
        P("dp", None, "mp"),
        P("dp", None, "mp"),
        P("dp", "mp", None),
        P("dp", None),
    )
    out_specs = (
        P("dp", "mp"),
        P("dp", "mp"),
        P("dp", "mp"),
        P("dp", "mp"),
        P("dp", "mp"),
        P("mp", "dp"),
        P("dp"),
        P("dp"),
        P("dp", None),
        P("dp", None, "mp"),
        P("dp", None, "mp"),
        P("dp", "mp", None),
    )
    return jax.shard_map(
        per_device, mesh=mesh, in_specs=in_specs, out_specs=out_specs, check_vma=False
    )
```

```python
import jax
import jax.numpy as jnp
import numpy as np
from jax import lax
from jax.experimental import pallas as pl
from jax.experimental.pallas import tpu as pltpu
from jax.sharding import PartitionSpec as P

HEAD_DIM = 64
EXPERTS = 32
BLOCK = 512
MAXLEN = 2048
CAP = 160
WIDTH = 1024
SHARE = 256
QUARTER = 40
SLOTS = 1280
LANES = 128
PACKED = 384

epsilon = 1e-06
residual_mult = 0.22
score_mult = 0.015625
rope_base = 10000.0
masked_score = -1e30

NN = (((1,), (0,)), ((), ()))
NT = (((1,), (1,)), ((), ()))
TN = (((0,), (0,)), ((), ()))


def mm(a, b, dims=NN):
    return lax.dot_general(a, b, dims, preferred_element_type=jnp.float32)


def to_all(x):
    return lax.all_to_all(x, "dp", 0, 0, tiled=True)


def crossed_groups(dp_count=32):
    groups = []
    for chip in range(2):
        for core in range(2):
            groups.append([i * 4 + (chip ^ (i & 1)) * 2 + core for i in range(dp_count)])
    return groups


def to_experts(x):
    return lax.all_to_all(
        x, ("dp", "mp"), 0, 0, axis_index_groups=crossed_groups(x.shape[0]), tiled=True
    )


def peer(x, flip):
    return lax.ppermute(x, "mp", [(i, i ^ flip) for i in range(4)])


def after(x, *others):
    return lax.optimization_barrier((x, *others))[0]


def vmem():
    return pl.BlockSpec(memory_space=pltpu.VMEM)


def smem():
    return pl.BlockSpec(memory_space=pltpu.SMEM)


def tiles(rows, width, row0=0):
    return pl.BlockSpec((rows, width), lambda i: (i + row0, 0))


def fixed(rows, width):
    return pl.BlockSpec((rows, width), lambda i: (0, 0))


def once(*shape):
    return pl.BlockSpec(shape, lambda i: (0,) * len(shape), pipeline_mode=pl.Buffered(1))


def run(kernel, name, steps, in_specs, out_specs, out_shape, args, estimate, scratch=(), free=(), limit=32):
    in_specs = [once(*a.shape) if s is None else s for s, a in zip(in_specs, args)]
    out_specs = [once(*o.shape) if s is None else s for s, o in zip(out_specs, out_shape)]
    args = [
        a
        if s.memory_space is not None or i in free
        else pltpu.with_memory_space_constraint(a, pltpu.HBM)
        for i, (s, a) in enumerate(zip(in_specs, args))
    ]
    out_shape = [
        o if s.memory_space == pltpu.SMEM else pltpu.HBM(o.shape, o.dtype)
        for s, o in zip(out_specs, out_shape)
    ]
    return pl.pallas_call(
        kernel,
        name=name,
        grid=(steps,),
        in_specs=in_specs,
        out_specs=out_specs,
        out_shape=out_shape,
        scratch_shapes=list(scratch),
        compiler_params=pltpu.CompilerParams(vmem_limit_bytes=limit << 20),
        cost_estimate=estimate,
    )(*args)


def out(shape, dtype):
    return jax.ShapeDtypeStruct(shape, dtype)


def cost(flops, moved, exps=0):
    return pl.CostEstimate(flops=flops, bytes_accessed=moved, transcendentals=exps)


def rope_constants():
    frequency = rope_base ** (-(np.arange(HEAD_DIM // 2, dtype=np.float64) * 2.0) / HEAD_DIM)
    wide = np.tile(frequency, 4)[None, :]
    made = []
    for count, apart in ((BLOCK // 16, 16), (16, 1), (8, BLOCK)):
        angles = np.arange(count, dtype=np.float64)[:, None] * apart * wide
        made += [np.cos(angles), np.sin(angles)]
    return [jnp.asarray(a.astype(np.float32)) for a in made]


def half_front(rows):
    lane = lax.broadcasted_iota(jnp.int32, (rows, LANES), 1)
    return (lane % HEAD_DIM) < HEAD_DIM // 2


def turned(chunk, cosine, signed_sine, back=False):
    partner = jnp.where(
        half_front(chunk.shape[0]), pltpu.roll(chunk, 96, 1), pltpu.roll(chunk, 32, 1)
    )
    if back:
        return chunk * cosine - partner * signed_sine
    return chunk * cosine + partner * signed_sine


def block_tables_in(lengths_ref, order_ref, rank_ref, offset_ref, inverse_ref, reach_ref, wanted_ref, later_ref, live_ref):
    count = order_ref.shape[0]
    steps = MAXLEN // BLOCK - 1

    def sequence(s, begin):
        def one(j, at):
            offset_ref[jnp.minimum(at, count - 1)] = j
            return at + 1

        return lax.fori_loop(0, lengths_ref[s], one, begin)

    lax.fori_loop(0, lengths_ref.shape[0], sequence, jnp.int32(0))

    def invert(d, carry):
        inverse_ref[order_ref[d]] = d
        return carry

    lax.fori_loop(0, count, invert, jnp.int32(0))
    reach_ref[0] = offset_ref[order_ref[rank_ref[0]]]

    def look(d, carry):
        packed = order_ref[d]
        for s in range(1, steps + 1):
            wanted_ref[d * steps + s - 1] = inverse_ref[jnp.maximum(packed - s, 0)]
            next_at = jnp.minimum(packed + s, count - 1)
            later_ref[d * steps + s - 1] = inverse_ref[next_at] * steps + s - 1
            is_live = jnp.logical_and(packed + s < count, offset_ref[next_at] >= s)
            live_ref[d * steps + s - 1] = jnp.where(is_live, 1, 0)
        return carry

    lax.fori_loop(0, count, look, jnp.int32(0))


def project_kernel(
    lengths_ref, order_ref, rank_ref, x_ref, gain_ref, wk_ref, wv_ref,
    cos16_ref, sin16_ref, cos1_ref, sin1_ref, cos0_ref, sin0_ref,
    normed_ref, kv_ref, cosine_ref, sine_ref, reach_ref, wanted_ref, later_ref, live_ref,
    offset_ref, inverse_ref,
):
    @pl.when(pl.program_id(0) == 0)
    def _():
        block_tables_in(
            lengths_ref, order_ref, rank_ref, offset_ref, inverse_ref, reach_ref, wanted_ref, later_ref, live_ref
        )

    x = x_ref[...].astype(jnp.float32)
    scale = lax.rsqrt(jnp.mean(x * x, axis=1, keepdims=True) + epsilon)
    normed = (x * scale * gain_ref[...]).astype(jnp.bfloat16)
    normed_ref[...] = normed
    at = reach_ref[0]
    cos0, sin0 = cos0_ref[pl.ds(at, 1), :], sin0_ref[pl.ds(at, 1), :]
    cos16 = cos16_ref[...] * cos0 - sin16_ref[...] * sin0
    sin16 = sin16_ref[...] * cos0 + cos16_ref[...] * sin0
    cos1, sin1 = cos1_ref[...][None], sin1_ref[...][None]
    cosine = (cos16[:, None, :] * cos1 - sin16[:, None, :] * sin1).reshape(x.shape[0], LANES)
    sine = (sin16[:, None, :] * cos1 + cos16[:, None, :] * sin1).reshape(x.shape[0], LANES)
    sine = jnp.where(half_front(x.shape[0]), -sine, sine)
    cosine_ref[...] = cosine
    sine_ref[...] = sine
    kv_ref[:, :LANES] = turned(mm(normed, wk_ref[...]), cosine, sine).astype(jnp.bfloat16)
    kv_ref[:, LANES:] = mm(normed, wv_ref[...]).astype(jnp.bfloat16)


def query_kernel(normed_ref, wq_ref, cosine_ref, sine_ref, q_ref):
    queries = mm(normed_ref[...], wq_ref[...])
    for i in range(0, SHARE, LANES):
        q_ref[:, i : i + LANES] = turned(
            queries[:, i : i + LANES], cosine_ref[...], sine_ref[...]
        ).astype(jnp.bfloat16)


def project_queries(normed, w_query, cosine, sine):
    tile = 256
    return run(
        query_kernel,
        "project_queries",
        BLOCK // tile,
        [tiles(tile, WIDTH), None, tiles(tile, LANES), tiles(tile, LANES)],
        [tiles(tile, SHARE)],
        [out((BLOCK, SHARE), jnp.bfloat16)],
        (normed, w_query, cosine, sine),
        cost(270_000_000, 2_500_000),
    )[0]


def project(lengths, order, rank, x, gain, w_key, w_value):
    tile = 256
    count = order.shape[0]
    steps = MAXLEN // BLOCK - 1
    bf16, f32 = jnp.bfloat16, jnp.float32
    return run(
        project_kernel,
        "project",
        BLOCK // tile,
        [smem()] * 3
        + [tiles(tile, WIDTH), None, None, None]
        + [tiles(tile // 16, LANES)] * 2
        + [None] * 4,
        [tiles(tile, WIDTH), tiles(tile, SHARE)] + [tiles(tile, LANES)] * 2 + [smem()] * 4,
        [out((BLOCK, WIDTH), bf16), out((BLOCK, SHARE), bf16)]
        + [out((BLOCK, LANES), f32)] * 2
        + [out((1,), jnp.int32)]
        + [out((count * steps,), jnp.int32)] * 3,
        (lengths, order, rank, x, gain, w_key, w_value, *rope_constants()),
        cost(540_000_000, 4_000_000, 512),
        [pltpu.SMEM((count,), jnp.int32), pltpu.SMEM((count,), jnp.int32)],
    )


def pick_kernel(wanted_ref, pieces_ref, picked_ref):
    def one(i, carry):
        picked_ref[i] = pieces_ref[wanted_ref[i]]
        return carry

    lax.fori_loop(0, picked_ref.shape[0], one, jnp.int32(0), unroll=4)


def pick_pieces(wanted, pieces):
    shape = out((wanted.shape[0], *pieces.shape[1:]), pieces.dtype)
    return run(
        pick_kernel, "pick_pieces", 1, [smem(), None], [None], [shape], (wanted, pieces), cost(0, 1_100_000), free=(1,)
    )[0]


def sum_kernel(later_ref, live_ref, pieces_ref, sum_ref):
    steps = MAXLEN // BLOCK - 1

    def one(d, carry):
        total = jnp.zeros(sum_ref.shape[1:], jnp.float32)
        for s in range(steps):
            part = pieces_ref[later_ref[d * steps + s]].astype(jnp.float32)
            total = total + jnp.where(live_ref[d * steps + s] == 1, part, 0.0)
        sum_ref[d] = total.astype(sum_ref.dtype)
        return carry

    lax.fori_loop(0, sum_ref.shape[0], one, jnp.int32(0), unroll=2)


def sum_pieces(later, live, pieces, count):
    shape = out((count, *pieces.shape[1:]), pieces.dtype)
    return run(
        sum_kernel,
        "sum_pieces",
        1,
        [smem(), smem(), None],
        [None],
        [shape],
        (later, live, pieces),
        cost(0, 1_100_000),
        free=(2,),
    )[0]


def route_kernel(begin_ref, routes_ref, picks_ref, ranks_ref):
    tokens = routes_ref.shape[1]
    expert_at = lax.broadcasted_iota(jnp.int32, (LANES, tokens), 0)
    hits = jnp.zeros((LANES, tokens), jnp.float32)
    for k in range(routes_ref.shape[0]):
        hits = hits + jnp.where(routes_ref[k : k + 1, :] == expert_at, 1.0, 0.0)
    row_at = lax.broadcasted_iota(jnp.int32, (tokens, tokens), 0)
    column_at = lax.broadcasted_iota(jnp.int32, (tokens, tokens), 1)
    before = jnp.where(row_at < column_at, 1.0, 0.0).astype(jnp.bfloat16)
    ranks = jnp.where(hits > 0.5, mm(hits.astype(jnp.bfloat16), before), -1.0)
    ranks_ref[...] = ranks
    slot_at = lax.broadcasted_iota(jnp.int32, (QUARTER, tokens), 0) + begin_ref[0]
    slot_at = slot_at.astype(jnp.float32)
    for e in range(EXPERTS):
        picks_ref[e * QUARTER : (e + 1) * QUARTER, :] = jnp.where(
            ranks[e : e + 1, :] == slot_at, 1.0, 0.0
        ).astype(jnp.bfloat16)


def route(begin, routes_t):
    return run(
        route_kernel,
        "route",
        1,
        [smem(), None],
        [None, None],
        [out((SLOTS, BLOCK), jnp.bfloat16), out((LANES, BLOCK), jnp.float32)],
        (begin, routes_t),
        cost(100_000_000, 1_600_000),
        free=(1,),
    )


def padded_columns(rows_t, out_ref):
    zero = jnp.zeros((HEAD_DIM, rows_t.shape[1]), out_ref.dtype)
    for h in range(4):
        mine = rows_t[h * HEAD_DIM : (h + 1) * HEAD_DIM].astype(out_ref.dtype)
        at = (h // 2) * HEAD_DIM
        out_ref[h, pl.ds(at, HEAD_DIM), :] = mine
        out_ref[h, pl.ds(HEAD_DIM - at, HEAD_DIM), :] = zero


def padded_rows(rows, out_ref):
    n = rows.shape[0]
    lane = lax.broadcasted_iota(jnp.int32, (n, 128), 1)
    for h in range(4):
        pair = rows[:, (h // 2) * 128 : (h // 2) * 128 + 128].astype(jnp.float32)
        if h % 2 != h // 2:
            pair = pltpu.roll(pair, HEAD_DIM, 1)
        own = (lane < HEAD_DIM) if h // 2 == 0 else (lane >= HEAD_DIM)
        out_ref[pl.ds(h * n, n), :] = jnp.where(own, pair, 0.0).astype(out_ref.dtype)


def attend_block(key_rows, value_rows, first, qpad_ref, max_ref, sum_ref, out_t_ref, vt_ref):
    half = BLOCK // 2
    vt_ref[...] = jnp.transpose(value_rows)
    for h in range(4):
        group = (h // 2) * HEAD_DIM
        for t in range(2):
            cols = slice(t * half, (t + 1) * half)
            rows = half if first and t == 0 else BLOCK
            scores = mm(key_rows[:rows], qpad_ref[h, :, cols])
            if first:
                key_at = lax.broadcasted_iota(jnp.int32, scores.shape, 0)
                query_at = lax.broadcasted_iota(jnp.int32, scores.shape, 1) + t * half
                scores = jnp.where(key_at > query_at, masked_score, scores)
            new_max = jnp.max(scores, axis=0, keepdims=True)
            if not first:
                old_max = max_ref[h : h + 1, cols]
                new_max = jnp.maximum(new_max, old_max)
                shrink = jnp.exp(old_max - new_max)
            weights = jnp.exp(scores - new_max)
            total = jnp.sum(weights, axis=0, keepdims=True)
            part = mm(vt_ref[group : group + HEAD_DIM, :rows], weights.astype(jnp.bfloat16))
            mine = pl.ds(h * HEAD_DIM, HEAD_DIM)
            if not first:
                total = total + sum_ref[h : h + 1, cols] * shrink
                part = part + out_t_ref[mine, cols] * shrink
            max_ref[h : h + 1, cols] = new_max
            sum_ref[h : h + 1, cols] = total
            out_t_ref[mine, cols] = part


def attend_own_kernel(q_ref, own_ref, qpad_ref, max_ref, sum_ref, out_t_ref, vt_ref):
    padded_columns(jnp.transpose(q_ref[...].astype(jnp.float32) * score_mult), qpad_ref)
    max_ref[...] = jnp.zeros_like(max_ref)
    sum_ref[...] = jnp.ones_like(sum_ref)
    attend_block(own_ref[:, :LANES], own_ref[:, LANES:], True, qpad_ref, max_ref, sum_ref, out_t_ref, vt_ref)


def attend_own(queries, own_kv):
    return pl.pallas_call(
        attend_own_kernel,
        name="attend_own",
        in_specs=[vmem()] * 2,
        out_specs=[vmem()] * 4,
        out_shape=[
            out((4, LANES, BLOCK), jnp.bfloat16),
            out((8, BLOCK), jnp.float32),
            out((8, BLOCK), jnp.float32),
            out((SHARE, BLOCK), jnp.float32),
        ],
        scratch_shapes=[pltpu.VMEM((LANES, BLOCK), jnp.bfloat16)],
        compiler_params=pltpu.CompilerParams(vmem_limit_bytes=36 << 20),
        cost_estimate=cost(1_000_000_000, 2_000_000, 600_000),
    )(queries, own_kv)


def attend_kernel(
    reach_ref, qpad_ref, max0_ref, sum0_ref, out0_ref, prev_ref, att_ref, out_t_ref, lse_ref, max_ref, sum_ref, vt_ref
):
    max_ref[...] = max0_ref[...]
    sum_ref[...] = sum0_ref[...]
    out_t_ref[...] = out0_ref[...]

    @pl.loop(1, reach_ref[0] + 1)
    def _(step):
        rows = prev_ref[:, pl.ds(step - 1, 1)].reshape(BLOCK, SHARE)
        attend_block(rows[:, :LANES], rows[:, LANES:], False, qpad_ref, max_ref, sum_ref, out_t_ref, vt_ref)

    lse_ref[...] = max_ref[...] + jnp.log(sum_ref[...])
    for h in range(4):
        mine = pl.ds(h * HEAD_DIM, HEAD_DIM)
        out_t_ref[mine, :] = out_t_ref[mine, :] / sum_ref[h : h + 1, :]
    att_ref[...] = jnp.transpose(out_t_ref[...]).astype(jnp.bfloat16)


def attend(reach, begun, earlier):
    return run(
        attend_kernel,
        "attend",
        1,
        [smem()] + [vmem()] * 5,
        [None] * 3,
        [
            out((BLOCK, SHARE), jnp.bfloat16),
            out((SHARE, BLOCK), jnp.float32),
            out((8, BLOCK), jnp.float32),
        ],
        (reach, *begun, earlier),
        cost(4_000_000_000, 3_000_000, 3_000_000),
        [
            pltpu.VMEM((8, BLOCK), jnp.float32),
            pltpu.VMEM((8, BLOCK), jnp.float32),
            pltpu.VMEM((LANES, BLOCK), jnp.bfloat16),
        ],
        limit=36,
    )


def attend_back_kernel(
    reach_ref, q_ref, qpad_ref, own_ref, prev_ref, grad_ref, grad_t_ref, out_t_ref, lse_ref, cos_ref, sin_ref,
    qgrad_ref, own_grad_ref, prev_grad_ref,
    gpad_ref, qrows_ref, grows_ref, ds_ref, p_ref, delta_ref, dq_ref, kt_ref,
):
    half = BLOCK // 2
    q_scaled = q_ref[...].astype(jnp.float32) * score_mult
    padded_rows(q_scaled, qrows_ref)
    padded_columns(grad_t_ref[...], gpad_ref)
    padded_rows(grad_ref[...], grows_ref)
    both = grad_t_ref[...].astype(jnp.float32) * out_t_ref[...]
    for h in range(4):
        delta_ref[h : h + 1, :] = jnp.sum(
            both[h * HEAD_DIM : (h + 1) * HEAD_DIM], axis=0, keepdims=True
        )


    def block(key_rows, value_rows, first):
        for h in range(4):
            for t in range(2):
                cols = slice(t * half, (t + 1) * half)
                wide = slice(h * BLOCK + t * half, h * BLOCK + (t + 1) * half)
                rows = half if first and t == 0 else BLOCK
                scores = mm(key_rows[:rows], qpad_ref[h, :, cols])
                weights = jnp.exp(scores - lse_ref[h : h + 1, cols])
                if first:
                    key_at = lax.broadcasted_iota(jnp.int32, scores.shape, 0)
                    query_at = lax.broadcasted_iota(jnp.int32, scores.shape, 1) + t * half
                    weights = jnp.where(key_at > query_at, 0.0, weights)
                weight_grad = mm(value_rows[:rows], gpad_ref[h, :, cols])
                score_grad = weights * (weight_grad - delta_ref[h : h + 1, cols])
                p_ref[:rows, wide] = weights.astype(jnp.bfloat16)
                ds_ref[:rows, wide] = score_grad.astype(jnp.bfloat16)
                if rows < BLOCK:
                    p_ref[rows:, wide] = jnp.zeros((BLOCK - rows, half), jnp.bfloat16)
                    ds_ref[rows:, wide] = jnp.zeros((BLOCK - rows, half), jnp.bfloat16)
        key_grad = mm(ds_ref[...], qrows_ref[...])
        value_grad = mm(p_ref[...], grows_ref[...])
        kt_ref[...] = jnp.transpose(key_rows)
        for h in range(4):
            group = (h // 2) * HEAD_DIM
            mine = pl.ds(h * HEAD_DIM, HEAD_DIM)
            part = mm(kt_ref[group : group + HEAD_DIM, :], ds_ref[:, h * BLOCK : (h + 1) * BLOCK])
            dq_ref[mine, :] = part if first else dq_ref[mine, :] + part
        return key_grad, value_grad

    key_grad, value_grad = block(own_ref[:, :LANES], own_ref[:, LANES:], True)
    own_grad_ref[:, :LANES] = key_grad
    own_grad_ref[:, LANES:] = value_grad

    @pl.loop(1, reach_ref[0] + 1)
    def _(step):
        rows = prev_ref[:, pl.ds(step - 1, 1)].reshape(BLOCK, SHARE)
        key_grad, value_grad = block(rows[:, :LANES], rows[:, LANES:], False)
        parts = prev_grad_ref.shape[0]
        shape = (parts, 1, BLOCK // parts, LANES)
        prev_grad_ref[:, pl.ds(step - 1, 1), :, :LANES] = key_grad.astype(jnp.bfloat16).reshape(shape)
        prev_grad_ref[:, pl.ds(step - 1, 1), :, LANES:] = value_grad.astype(jnp.bfloat16).reshape(shape)

    query_grad = jnp.transpose(dq_ref[...]) * score_mult
    for i in range(0, SHARE, LANES):
        qgrad_ref[:, i : i + LANES] = turned(
            query_grad[:, i : i + LANES], cos_ref[...], sin_ref[...], back=True
        ).astype(jnp.bfloat16)


def attend_back(reach, queries, padded, own_kv, earlier, grad, grad_t, out_t, lse, cosine, signed_sine):
    return run(
        attend_back_kernel,
        "attend_back",
        1,
        [smem()] + [vmem()] * 10,
        [None] * 3,
        [
            out((BLOCK, SHARE), jnp.bfloat16),
            out((BLOCK, SHARE), jnp.float32),
            out(earlier.shape, jnp.bfloat16),
        ],
        (reach, queries, padded, own_kv, earlier, grad, grad_t, out_t, lse, cosine, signed_sine),
        cost(12_000_000_000, 5_000_000, 3_000_000),
        [
            pltpu.VMEM((4, LANES, BLOCK), jnp.bfloat16),
            pltpu.VMEM((4 * BLOCK, LANES), jnp.bfloat16),
            pltpu.VMEM((4 * BLOCK, LANES), jnp.bfloat16),
            pltpu.VMEM((BLOCK, 4 * BLOCK), jnp.bfloat16),
            pltpu.VMEM((BLOCK, 4 * BLOCK), jnp.bfloat16),
            pltpu.VMEM((8, BLOCK), jnp.float32),
            pltpu.VMEM((SHARE, BLOCK), jnp.float32),
            pltpu.VMEM((LANES, BLOCK), jnp.bfloat16),
        ],
        limit=36,
    )


def residual_kernel(
    a0, a1, a2, a3, w0, w1, w2, w3, x_ref, gain_ref, router_ref, ranks_ref, picks_ref,
    residual_ref, moe_ref, gates_ref, rows_ref, held_ref,
):
    step = pl.program_id(0)
    tile = x_ref.shape[0]

    @pl.when(step < BLOCK // tile)
    def _():
        branch = mm(a0[...], w0[...])
        for a, w in ((a1, w1), (a2, w2), (a3, w3)):
            branch = branch + mm(a[...], w[...])
        residual = x_ref[...].astype(jnp.float32) + residual_mult * branch
        residual_ref[...] = residual
        scale = lax.rsqrt(jnp.mean(residual * residual, axis=1, keepdims=True) + epsilon)
        moe_in = (residual * scale * gain_ref[...]).astype(jnp.bfloat16)
        moe_ref[:, :WIDTH] = moe_in
        logits = mm(router_ref[...], moe_in, NT)
        chosen = ranks_ref[...] >= 0.0
        kept = jnp.where(chosen, logits, masked_score)
        top = jnp.max(kept, axis=0, keepdims=True)
        raised = jnp.where(chosen, jnp.exp(kept - top), 0.0)
        gates = raised / jnp.sum(raised, axis=0, keepdims=True)
        gates_ref[...] = gates
        low = (residual_mult * jnp.transpose(gates)).astype(jnp.bfloat16)
        moe_ref[:, WIDTH:] = low
        held_ref[pl.ds(step * tile, tile), :WIDTH] = moe_in
        held_ref[pl.ds(step * tile, tile), WIDTH:] = low

    @pl.when(step >= BLOCK // tile)
    def _():
        rows_ref[...] = mm(picks_ref[...], held_ref[...]).astype(jnp.bfloat16)


def residual_step(attended, w_out, x, gain, router_t, ranks, picks):
    tile = 256
    first = BLOCK // tile
    slot_tile = SLOTS // 4

    def early(rows, width):
        return pl.BlockSpec((rows, width), lambda i: (jnp.minimum(i, first - 1), 0))

    def late(rows, width):
        return pl.BlockSpec((rows, width), lambda i: (jnp.maximum(i - first, 0), 0))

    by_columns = pl.BlockSpec((LANES, tile), lambda i: (0, jnp.minimum(i, first - 1)))
    return run(
        residual_kernel,
        "residual_step",
        first + 4,
        [early(tile, SHARE)] * 4
        + [None] * 4
        + [early(tile, WIDTH), None, None, by_columns, late(slot_tile, BLOCK)],
        [early(tile, WIDTH), early(tile, WIDTH + LANES), by_columns, late(slot_tile, WIDTH + LANES)],
        [
            out((BLOCK, WIDTH), jnp.float32),
            out((BLOCK, WIDTH + LANES), jnp.bfloat16),
            out((LANES, BLOCK), jnp.float32),
            out((SLOTS, WIDTH + LANES), jnp.bfloat16),
        ],
        (*attended, *w_out, x, gain, router_t, ranks, picks),
        cost(2_700_000_000, 12_000_000, 70_000),
        [pltpu.VMEM((BLOCK, WIDTH + LANES), jnp.bfloat16)],
        free=(1, 2, 3, 5, 6, 7, 10),
    )


def mix_kernel(begin_ref, ranks_ref, moe_ref, mix_ref):
    ranks = jnp.transpose(ranks_ref[...]).astype(jnp.bfloat16)
    gates = moe_ref[:, WIDTH:]
    width = 640
    for at in range(0, SLOTS, width):
        expert_at = lax.broadcasted_iota(jnp.int32, (LANES, width), 0)
        first = expert_at * QUARTER - at
        slot_at = lax.broadcasted_iota(jnp.int32, (LANES, width), 1)
        inside = jnp.logical_and(slot_at >= first, slot_at < first + QUARTER)
        spread = jnp.where(inside, 1.0, 0.0).astype(jnp.bfloat16)
        within = jnp.sum(jnp.where(inside, slot_at - first, 0), axis=0, keepdims=True) + begin_ref[0]
        hit = mm(ranks, spread) == within.astype(jnp.float32)
        mix_ref[:, at : at + width] = jnp.where(hit, mm(gates, spread), 0.0).astype(jnp.bfloat16)


def mix_weights(begin, ranks, moe_cat):
    return run(
        mix_kernel,
        "mix_weights",
        1,
        [smem(), None, None],
        [None],
        [out((BLOCK, SLOTS), jnp.bfloat16)],
        (begin, ranks, moe_cat),
        cost(350_000_000, 3_000_000),
    )[0]


def expert_kernel(lane_ref, x_ref, grad_ref, *refs):
    downs, gate_refs, up_refs = refs[:4], refs[4:8], refs[8:12]
    out_ref, row_ref, hidden_ref, units_ref = refs[12:]
    rows = out_ref.shape[0]
    here = pl.ds(pl.program_id(0) * rows, rows)
    lane = lax.broadcasted_iota(jnp.int32, (rows, LANES), 1) == lane_ref[0]
    gate = jnp.sum(
        jnp.where(lane, x_ref[here, WIDTH:].astype(jnp.float32), 0.0), axis=1, keepdims=True
    )
    x = x_ref[here, :WIDTH]
    grad = grad_ref[...]
    gates, ups, sigmoids, hidden = [], [], [], []
    for j in range(4):
        pre = mm(x, jnp.concatenate([gate_refs[j][...], up_refs[j][...]], axis=1))
        gate_pre, up_pre = pre[:, :LANES], pre[:, LANES:]
        sigmoid = 1.0 / (1.0 + jnp.exp(-gate_pre))
        gates.append(gate_pre)
        ups.append(up_pre)
        sigmoids.append(sigmoid)
        hidden.append(gate_pre * sigmoid * up_pre)
    hidden_low = jnp.concatenate([h.astype(jnp.bfloat16) for h in hidden], axis=1)
    down = jnp.concatenate([p[...] for p in downs], axis=0)
    made = mm(hidden_low, down).astype(jnp.bfloat16)
    out_ref[...] = made
    gate_grad = jnp.sum(grad.astype(jnp.float32) * made.astype(jnp.float32), axis=1, keepdims=True)
    row_ref[:, WIDTH:] = jnp.where(lane, gate_grad, 0.0).astype(jnp.bfloat16)
    hidden_grad = mm(grad, down, NT)
    row = None
    for j in range(4):
        part = hidden_grad[:, j * LANES : (j + 1) * LANES]
        silu = gates[j] * sigmoids[j]
        gate_pre_grad = part * ups[j] * sigmoids[j] * (1.0 + gates[j] * (1.0 - sigmoids[j]))
        up_pre_grad = part * silu
        hidden_ref[:, j * LANES : (j + 1) * LANES] = (hidden[j] * gate).astype(jnp.bfloat16)
        units_ref[:, j * SHARE : j * SHARE + LANES] = (gate_pre_grad * gate).astype(jnp.bfloat16)
        units_ref[:, j * SHARE + LANES : (j + 1) * SHARE] = (up_pre_grad * gate).astype(jnp.bfloat16)
        both = jnp.concatenate([gate_pre_grad, up_pre_grad], axis=1).astype(jnp.bfloat16)
        term = mm(both, jnp.concatenate([gate_refs[j][...], up_refs[j][...]], axis=1), NT)
        row = term if row is None else row + term
    row_ref[:, :WIDTH] = row.astype(jnp.bfloat16)


def expert_step(lane, x, grad, downs, gates, ups):
    tile = 320
    return run(
        expert_kernel,
        "expert_step",
        SLOTS // tile,
        [smem(), vmem(), tiles(tile, WIDTH)] + [None] * 12,
        [tiles(tile, WIDTH), tiles(tile, WIDTH + LANES), tiles(tile, 512), tiles(tile, WIDTH)],
        [
            out((SLOTS, WIDTH), jnp.bfloat16),
            out((SLOTS, WIDTH + LANES), jnp.bfloat16),
            out((SLOTS, 512), jnp.bfloat16),
            out((SLOTS, WIDTH), jnp.bfloat16),
        ],
        (lane, x, grad, *downs, *gates, *ups),
        cost(8_000_000_000, 18_000_000, 700_000),
        limit=40,
    )


def unit_grads_kernel(x_ref, grad_ref, hidden_ref, units_ref, keep_ref, send_ref, turned_ref):
    step = pl.program_id(0)

    @pl.when(step == 0)
    def _():
        for k in range(4):
            columns = slice(k * SHARE, (k + 1) * SHARE)
            turned_ref[columns, :] = jnp.transpose(x_ref[:, columns])

    def write(to_ref):
        to_ref[0, :LANES, :] = mm(hidden_ref[...], grad_ref[...], TN).astype(jnp.bfloat16)
        for k in range(4):
            columns = slice(k * SHARE, (k + 1) * SHARE)
            to_ref[0, LANES:, columns] = mm(turned_ref[columns, :], units_ref[...]).astype(jnp.bfloat16)

    @pl.when(step < 2)
    def _():
        write(keep_ref)

    @pl.when(step >= 2)
    def _():
        write(send_ref)


def unit_grads(x, grad, hidden, units):
    rows = SHARE + LANES

    def share_of(i):
        return jnp.where(i < 2, 2 * i, 2 * i - 3)

    return run(
        unit_grads_kernel,
        "unit_grads",
        4,
        [
            vmem(),
            None,
            pl.BlockSpec((SLOTS, LANES), lambda i: (0, share_of(i))),
            pl.BlockSpec((SLOTS, SHARE), lambda i: (0, share_of(i))),
        ],
        [
            pl.BlockSpec((1, rows, WIDTH), lambda i: (jnp.minimum(i, 1), 0, 0)),
            pl.BlockSpec((1, rows, WIDTH), lambda i: (jnp.maximum(i - 2, 0), 0, 0)),
        ],
        [out((2, rows, WIDTH), jnp.bfloat16), out((2, rows, WIDTH), jnp.bfloat16)],
        (x, grad, hidden, units),
        cost(4_000_000_000, 12_000_000),
        [pltpu.VMEM((WIDTH, SLOTS), jnp.bfloat16)],
        limit=36,
    )


def unit_finish_kernel(mine_ref, first_ref, second_ref, third_ref, gate_ref, up_ref, down_ref):
    got = jnp.concatenate([first_ref[...], second_ref[...], third_ref[...]], axis=0)
    total = mine_ref[0] + got.astype(jnp.float32)
    down_ref[0] = total[:LANES, :]
    for k in range(4):
        rows = slice(k * SHARE, (k + 1) * SHARE)
        gate_ref[0, rows, :] = total[LANES:, k * SHARE : k * SHARE + LANES]
        up_ref[0, rows, :] = total[LANES:, k * SHARE + LANES : (k + 1) * SHARE]


def unit_finish(mine, first, second, third):
    return run(
        unit_finish_kernel,
        "unit_finish",
        1,
        [once(1, PACKED, WIDTH), None, None, None],
        [None] * 3,
        [
            out((1, WIDTH, LANES), jnp.float32),
            out((1, WIDTH, LANES), jnp.float32),
            out((1, LANES, WIDTH), jnp.float32),
        ],
        (mine, first, second, third),
        cost(1_000_000, 3_000_000),
        free=(0, 1, 2, 3),
    )


def home_kernel(rank_ref, mix_ref, rows_ref, keep_ref, send_ref):
    rank = rank_ref[0]
    extra = rows_ref.shape[1] > WIDTH
    for j in range(4):
        at = pl.multiple_of(jnp.bitwise_xor(rank, j) * SHARE, SHARE)
        total = mm(mix_ref[...], rows_ref[:, pl.ds(at, SHARE)])
        to_ref = send_ref if j % 2 else keep_ref
        to_ref[(j // 2) * BLOCK : (j // 2 + 1) * BLOCK, :] = total.astype(to_ref.dtype)
    if extra:
        gate_grads = jnp.transpose(mm(mix_ref[...], rows_ref[:, WIDTH:]))[:EXPERTS]
        for to_ref in (keep_ref, send_ref):
            for i in range(2):
                at = 2 * BLOCK + i * EXPERTS
                to_ref[at : at + EXPERTS, :] = gate_grads[:, i * SHARE : (i + 1) * SHARE].astype(
                    to_ref.dtype
                )


def sum_home(rank, mix, rows):
    height = 2 * BLOCK + (2 * EXPERTS if rows.shape[1] > WIDTH else 0)
    return run(
        home_kernel,
        "sum_home",
        1,
        [smem(), None, vmem()],
        [None] * 2,
        [out((height, SHARE), jnp.float32), out((height, SHARE), jnp.bfloat16)],
        (rank, mix, rows),
        cost(1_500_000_000, 6_000_000),
        limit=36,
    )


def swap_kernel(mine_ref, got_ref, total_ref):
    mine, got = mine_ref, got_ref
    half = BLOCK
    total_ref[:half] = (mine[:half] + got[half : 2 * half].astype(jnp.float32)).astype(total_ref.dtype)
    total_ref[half : 2 * half] = (
        mine[half : 2 * half] + got[:half].astype(jnp.float32)
    ).astype(total_ref.dtype)
    total_ref[2 * half :] = (mine[2 * half :] + got[2 * half :].astype(jnp.float32)).astype(
        total_ref.dtype
    )


def swap_sum(mine, got):
    return run(
        swap_kernel,
        "swap_sum",
        1,
        [None] * 2,
        [None],
        [out(mine.shape, jnp.bfloat16)],
        (mine, got),
        cost(1_000_000, 2_500_000),
        free=(0, 1),
    )[0]


def norm_back_kernel(
    rank_ref, g0, g2, g1, g3, z_ref, gates_ref, residual_ref, gain_ref, router_ref, grad_ref, w_ref,
    low_ref, logit_ref, own_ref, att_ref, att_t_ref, gain_grad_ref, u_ref,
):
    rank = rank_ref[0]
    for flip, part in enumerate((g0, g1, g2, g3)):
        at = pl.multiple_of(jnp.bitwise_xor(rank, flip) * SHARE, SHARE)
        u_ref[:, pl.ds(at, SHARE)] = part[...].astype(jnp.float32)
    weighted_grads = z_ref[...].astype(jnp.float32)
    gates = gates_ref[:EXPERTS, :]
    inner = jnp.sum(weighted_grads, axis=0, keepdims=True)
    logit_grad = (weighted_grads - gates * inner).astype(jnp.bfloat16)
    logit_ref[...] = logit_grad
    u = u_ref[...] + mm(logit_grad, router_ref[:EXPERTS, :], TN)
    v = residual_ref[...]
    scale = lax.rsqrt(jnp.mean(v * v, axis=1, keepdims=True) + epsilon)
    weighted = u * gain_ref[...]
    mean = jnp.mean(weighted * v, axis=1, keepdims=True)
    total = grad_ref[...].astype(jnp.float32) + scale * weighted - v * (scale * scale * scale * mean)

    @pl.when(pl.program_id(0) == 0)
    def _():
        gain_grad_ref[...] = jnp.zeros_like(gain_grad_ref)

    gain_grad_ref[0:1, :] += jnp.sum(u * v * scale, axis=0, keepdims=True)
    low = (residual_mult * total).astype(jnp.bfloat16)
    low_ref[...] = low
    u_ref[...] = total
    own_ref[...] = u_ref[:, pl.ds(pl.multiple_of(rank * SHARE, SHARE), SHARE)]
    att_ref[...] = mm(low, w_ref[...], NT).astype(jnp.bfloat16)
    att_t_ref[...] = mm(w_ref[...], low, NT).astype(jnp.bfloat16)


def norm_back_step(rank, mine, theirs, gates, residual, gain, router_t, out_grad, w_out):
    tile = 256
    by_columns = pl.BlockSpec((EXPERTS, tile), lambda i: (0, i))
    return run(
        norm_back_kernel,
        "norm_back_step",
        BLOCK // tile,
        [smem()]
        + [tiles(tile, SHARE), tiles(tile, SHARE, BLOCK // tile)] * 2
        + [
            tiles(EXPERTS, SHARE, 2 * BLOCK // EXPERTS),
            pl.BlockSpec((LANES, tile), lambda i: (0, i)),
            tiles(tile, WIDTH),
            None,
            None,
            tiles(tile, WIDTH),
            None,
        ],
        [
            tiles(tile, WIDTH),
            by_columns,
            tiles(tile, SHARE),
            tiles(tile, SHARE),
            pl.BlockSpec((SHARE, tile), lambda i: (0, i)),
            fixed(8, WIDTH),
        ],
        [
            out((BLOCK, WIDTH), jnp.bfloat16),
            out((EXPERTS, BLOCK), jnp.bfloat16),
            out((BLOCK, SHARE), jnp.float32),
            out((BLOCK, SHARE), jnp.bfloat16),
            out((SHARE, BLOCK), jnp.bfloat16),
            out((8, WIDTH), jnp.float32),
        ],
        (rank, mine, mine, theirs, theirs, mine, gates, residual, gain, router_t, out_grad, w_out),
        cost(700_000_000, 9_000_000, 512),
        [pltpu.VMEM((tile, WIDTH), jnp.float32)],
        free=(3, 4, 9),
    )


def dense_grads_kernel(low_ref, attended_ref, normed_ref, qgrad_ref, logit_ref, moe_ref, gain_ref, made_ref):
    made_ref[:, :SHARE] = mm(low_ref[...], attended_ref[...], TN).astype(jnp.bfloat16)
    made_ref[:, SHARE : 2 * SHARE] = mm(normed_ref[...], qgrad_ref[...], TN).astype(jnp.bfloat16)
    router = mm(logit_ref[...], moe_ref[:, :WIDTH])
    stacked = jnp.concatenate(
        [router, gain_ref[...], jnp.zeros((LANES - EXPERTS - 8, WIDTH), jnp.float32)], axis=0
    )
    made_ref[:, 2 * SHARE :] = jnp.transpose(stacked).astype(jnp.bfloat16)


def dense_grads(low, attended, normed, qgrad, logit, moe_cat, gain_grad):
    return run(
        dense_grads_kernel,
        "dense_grads",
        1,
        [None] * 7,
        [None],
        [out((WIDTH, 2 * SHARE + LANES), jnp.bfloat16)],
        (low, attended, normed, qgrad, logit, moe_cat, gain_grad),
        cost(600_000_000, 6_000_000),
    )[0]


def last_grads_kernel(
    rank_ref, own_ref, home_ref, qgrad_ref, normed_ref, x_ref, wq_ref, wk_ref, wv_ref, cos_ref, sin_ref, made_ref,
    gain_ref, all_ref, keep_ref, send_ref, inner_ref, part_ref,
):
    rank = rank_ref[0]
    kv = own_ref[...] + home_ref[...].astype(jnp.float32)
    key_grad = turned(kv[:, :LANES], cos_ref[...], sin_ref[...], back=True).astype(jnp.bfloat16)
    value_grad = kv[:, LANES:].astype(jnp.bfloat16)
    both = jnp.concatenate([key_grad, value_grad], axis=1)
    all_ref[:, : 2 * SHARE] = made_ref[:, : 2 * SHARE]
    all_ref[:, 2 * SHARE : 3 * SHARE] = mm(normed_ref[...], both, TN).astype(jnp.bfloat16)
    gain = jnp.zeros((1, WIDTH), jnp.float32)
    tile = 128
    for i in range(0, BLOCK, tile):
        rows = slice(i, i + tile)
        part = mm(qgrad_ref[rows, :], wq_ref[...], NT)
        part = part + mm(key_grad[rows], wk_ref[...], NT) + mm(value_grad[rows], wv_ref[...], NT)
        x = x_ref[rows, :].astype(jnp.float32)
        scale = lax.rsqrt(jnp.mean(x * x, axis=1, keepdims=True) + epsilon)
        along = part * x
        gain = gain + jnp.sum(along * scale, axis=0, keepdims=True)
        inner = jnp.sum(along * gain_ref[...], axis=1, keepdims=True)
        inner_ref[:, rows] = jnp.transpose(jnp.broadcast_to(inner, (tile, LANES)))[:8]
        part_ref[rows, :] = part
    for j in range(4):
        at = pl.multiple_of(jnp.bitwise_xor(rank, j) * SHARE, SHARE)
        to_ref = send_ref if j % 2 else keep_ref
        to_ref[(j // 2) * BLOCK : (j // 2 + 1) * BLOCK, :] = part_ref[:, pl.ds(at, SHARE)].astype(to_ref.dtype)
    lane = lax.broadcasted_iota(jnp.int32, (WIDTH, LANES), 1)
    column = jnp.transpose(jnp.broadcast_to(gain, (LANES, WIDTH)))
    rest = jnp.where(lane == EXPERTS + 8, column, made_ref[:, 2 * SHARE :].astype(jnp.float32))
    all_ref[:, 3 * SHARE :] = rest.astype(jnp.bfloat16)


def last_grads(rank, own, home, qgrad, normed, x, w_query, w_key, w_value, cosine, sine, made, gain):
    return run(
        last_grads_kernel,
        "last_grads",
        1,
        [smem()] + [None] * 12,
        [None] * 4,
        [
            out((WIDTH, 3 * SHARE + LANES), jnp.bfloat16),
            out((2 * BLOCK, SHARE), jnp.float32),
            out((2 * BLOCK, SHARE), jnp.bfloat16),
            out((8, BLOCK), jnp.float32),
        ],
        (rank, own, home, qgrad, normed, x, w_query, w_key, w_value, cosine, sine, made, gain),
        cost(1_000_000_000, 8_000_000, 512),
        [pltpu.VMEM((BLOCK, WIDTH), jnp.float32)],
        free=(2,),
    )


def input_finish_kernel(
    rank_ref, near_ref, far_ref, i0, i1, i2, i3, x_ref, gain_ref, residual_ref, made_ref
):
    mine = pl.ds(pl.multiple_of(rank_ref[0] * SHARE, SHARE), SHARE)
    x = x_ref[...].astype(jnp.float32)
    scale = lax.rsqrt(jnp.mean(x * x, axis=1, keepdims=True) + epsilon)
    inner = (i0[...] + i1[...] + i2[...] + i3[...]) * (1.0 / WIDTH)
    inner = jnp.transpose(jnp.broadcast_to(inner[:1], (LANES, BLOCK)))[:, :1]
    weighted = (near_ref[...] + far_ref[...].astype(jnp.float32)) * gain_ref[:, mine]
    x_own = x_ref[:, mine].astype(jnp.float32)
    made_ref[...] = residual_ref[...] + scale * weighted - x_own * (scale * scale * scale * inner)


def input_finish(rank, near, far, inners, x, gain, residual):
    return run(
        input_finish_kernel,
        "input_finish",
        1,
        [smem(), once(BLOCK, SHARE), None] + [None] * 7,
        [None],
        [out((BLOCK, SHARE), jnp.float32)],
        (rank, near, far, *inners, x, gain, residual),
        cost(3_000_000, 3_000_000, 512),
        free=(1, 2, 3, 4, 5, 6),
    )[0]


def per_device(
    hidden_in,
    lengths,
    block_order,
    routes,
    norm_gain_attn,
    w_query,
    w_key,
    w_value,
    w_out,
    norm_gain_moe,
    w_router,
    w_gate,
    w_up,
    w_down,
    out_grad,
):
    dp_count = block_order.shape[0]
    mp_rank = lax.axis_index("mp").astype(jnp.int32)
    column_start = mp_rank * SHARE
    piece = BLOCK // dp_count
    steps = MAXLEN // BLOCK - 1
    rank = mp_rank.reshape(1)
    lane = lax.axis_index("dp").astype(jnp.int32).reshape(1)
    begin = rank * QUARTER
    gain_attn = norm_gain_attn[None, :]
    gain_moe = norm_gain_moe[None, :]
    router_t = jnp.pad(w_router.T, ((0, LANES - EXPERTS), (0, 0)))

    far_out = peer(w_out, 2)
    far_down, far_gate, far_up = [peer(w[0], 2) for w in (w_down, w_gate, w_up)]

    normed, key_value, cosine, sine, reach, wanted, later, live = project(
        lengths, block_order, lane, hidden_in, gain_attn, w_key, w_value
    )
    queries = project_queries(normed, w_query, cosine, sine)
    pieces = to_all(key_value.reshape(dp_count, piece, SHARE))
    picks, ranks = route(begin, after(routes.T, key_value))
    begun = attend_own(queries, after(key_value, picks))
    picked = pick_pieces(wanted, after(pieces, far_out, far_down, far_gate, far_up, queries, picks))
    earlier = to_all(picked.reshape(dp_count, steps * piece, SHARE))
    earlier = earlier.reshape(dp_count, steps, piece, SHARE)

    outs = [w_out, peer(after(w_out, picked), 1), far_out, peer(far_out, 1)]

    grad_rows = jnp.dot(picks, after(out_grad, picked), preferred_element_type=jnp.bfloat16)
    grad_arrived = to_experts(after(grad_rows, earlier, begun[1]).reshape(EXPERTS, QUARTER, WIDTH))
    attended, attended_t, lse = attend(reach, begun, earlier)
    far = peer(attended, 2)
    residual, moe_cat, gates, moe_rows = residual_step(
        [attended, peer(attended, 1), far, peer(far, 1)],
        outs,
        hidden_in,
        gain_moe,
        router_t,
        ranks,
        picks,
    )
    own = [after(w[0], moe_rows) for w in (w_down, w_gate, w_up)]
    far = [after(w, moe_rows) for w in (far_down, far_gate, far_up)]
    downs, gates_all, ups = [[w, peer(w, 1), v, peer(v, 1)] for w, v in zip(own, far)]
    grouped = to_experts(moe_rows.reshape(EXPERTS, QUARTER, -1)).reshape(SLOTS, -1)
    mix = mix_weights(begin, ranks, moe_cat)
    grouped_grad = grad_arrived.reshape(SLOTS, WIDTH)
    rows_out, row_grad, hidden_units, unit_grad = expert_step(
        lane, grouped, grouped_grad, downs, gates_all, ups
    )
    row_home = to_experts(row_grad.reshape(dp_count, QUARTER, -1)).reshape(SLOTS, -1)
    rows_home = to_experts(after(rows_out, row_home).reshape(dp_count, QUARTER, -1)).reshape(SLOTS, -1)

    unit_keep, unit_send = unit_grads(grouped, grouped_grad, hidden_units, unit_grad)
    unit_near = unit_keep.astype(jnp.float32) + peer(unit_send, 1).astype(jnp.float32)
    unit_low = unit_near[1].astype(jnp.bfloat16)
    cut = PACKED // 2
    unit_far_a = peer(unit_low[:cut], 2)
    keep, send = sum_home(rank, after(mix, unit_far_a), row_home)
    near = keep + peer(send, 1).astype(jnp.float32)
    mine = swap_sum(near, peer(near.astype(jnp.bfloat16), 2))
    theirs = peer(mine, 1)
    branch_grad, logit_grad, residual_grad, attended_grad, attended_grad_t, moe_gain = norm_back_step(
        rank, mine, theirs, gates, residual, gain_moe, router_t, out_grad, w_out
    )

    query_pre_grad, own_grads, later_grads = attend_back(
        reach,
        queries,
        begun[0],
        key_value,
        earlier,
        attended_grad,
        attended_grad_t,
        attended_t,
        lse,
        cosine,
        sine,
    )
    unit_far_b = peer(after(unit_low[cut:], later_grads), 2)
    unit_far_b = peer(after(unit_low[cut : cut + cut // 2], branch_grad), 2)
    later_pieces = to_all(after(later_grads, rows_home, unit_far_b).reshape(dp_count, steps * piece, SHARE))
    summed = sum_pieces(
        later, live, later_pieces.reshape(dp_count * steps, piece, SHARE), dp_count
    )
    kv_home = to_all(summed).reshape(BLOCK, SHARE)
    made = dense_grads(
        branch_grad, attended, normed, query_pre_grad, logit_grad, moe_cat, moe_gain
    )

    unit_far_c = peer(after(unit_low[cut + cut // 2 :], kv_home, made), 2)

    every, keep, send, inner = last_grads(
        rank,
        own_grads,
        kv_home,
        query_pre_grad,
        normed,
        hidden_in,
        w_query,
        w_key,
        w_value,
        cosine,
        sine,
        made,
        gain_attn,
    )
    near_norm = keep + peer(send, 1).astype(jnp.float32)
    far_norm = peer(near_norm[BLOCK:].astype(jnp.bfloat16), 2)
    inners = [inner] + [peer(inner, flip) for flip in (1, 2, 3)]
    every = after(every, unit_far_c)
    arrived = to_all(every.reshape(dp_count, WIDTH // dp_count, -1))
    keep, send = sum_home(rank, mix, after(rows_home, every))
    near_mix = keep + peer(send, 1).astype(jnp.float32)
    far_mix = peer(near_mix[BLOCK:].astype(jnp.bfloat16), 2)
    grad_w_gate, grad_w_up, grad_w_down = unit_finish(
        unit_near, unit_far_a, after(unit_far_b, every), unit_far_c
    )
    dense = jnp.sum(arrived.astype(jnp.float32), axis=0)
    at = 3 * SHARE
    attn_gain = dense[:, at + EXPERTS + 8]
    attn_gain = attn_gain + peer(attn_gain, 1) + peer(attn_gain, 2) + peer(attn_gain, 3)
    grad_hidden = input_finish(
        rank, near_norm, after(far_norm, dense), inners, hidden_in, gain_attn, residual_grad
    )
    residual_cols = lax.dynamic_slice_in_dim(residual, column_start, SHARE, 1)
    mixture = near_mix[:BLOCK] + after(far_mix, grad_hidden).astype(jnp.float32)
    out_hidden = (residual_cols + mixture).astype(jnp.bfloat16)

    return (
        out_hidden,
        grad_hidden,
        dense[:, SHARE : 2 * SHARE],
        dense[:, 2 * SHARE : 2 * SHARE + LANES],
        dense[:, 2 * SHARE + LANES : at],
        dense[:, :SHARE].T,
        attn_gain,
        dense[:, at + EXPERTS],
        dense[:, at : at + EXPERTS],
        grad_w_gate,
        grad_w_up,
        grad_w_down,
    )


def solution(mesh):
    in_specs = (
        P("dp", None),
        P(),
        P(),
        P("dp", None),
        P(),
        P(None, "mp"),
        P(None, "mp"),
        P(None, "mp"),
        P("mp", None),
        P(),
        P(),
        P("dp", None, "mp"),
        P("dp", None, "mp"),
        P("dp", "mp", None),
        P("dp", None),
    )
    out_specs = (
        P("dp", "mp"),
        P("dp", "mp"),
        P("dp", "mp"),
        P("dp", "mp"),
        P("dp", "mp"),
        P("mp", "dp"),
        P("dp"),
        P("dp"),
        P("dp", None),
        P("dp", None, "mp"),
        P("dp", None, "mp"),
        P("dp", "mp", None),
    )
    return jax.shard_map(
        per_device, mesh=mesh, in_specs=in_specs, out_specs=out_specs, check_vma=False
    )
```

```python
import jax
import jax.numpy as jnp
import numpy as np
from jax import lax
from jax.experimental import pallas as pl
from jax.experimental.pallas import tpu as pltpu
from jax.sharding import PartitionSpec as P

HEAD_DIM = 64
EXPERTS = 32
BLOCK = 512
MAXLEN = 2048
CAP = 160
WIDTH = 1024
SHARE = 256
QUARTER = 40
SLOTS = 1280
LANES = 128
PACKED = 384

epsilon = 1e-06
residual_mult = 0.22
score_mult = 0.015625
rope_base = 10000.0
masked_score = -1e30

NN = (((1,), (0,)), ((), ()))
NT = (((1,), (1,)), ((), ()))
TN = (((0,), (0,)), ((), ()))


def mm(a, b, dims=NN):
    return lax.dot_general(a, b, dims, preferred_element_type=jnp.float32)


def to_all(x):
    return lax.all_to_all(x, "dp", 0, 0, tiled=True)


def crossed_groups(dp_count=32):
    groups = []
    for chip in range(2):
        for core in range(2):
            groups.append([i * 4 + (chip ^ (i & 1)) * 2 + core for i in range(dp_count)])
    return groups


def to_experts(x):
    return lax.all_to_all(
        x, ("dp", "mp"), 0, 0, axis_index_groups=crossed_groups(x.shape[0]), tiled=True
    )


def peer(x, flip):
    return lax.ppermute(x, "mp", [(i, i ^ flip) for i in range(4)])


def after(x, *others):
    return lax.optimization_barrier((x, *others))[0]


def vmem():
    return pl.BlockSpec(memory_space=pltpu.VMEM)


def smem():
    return pl.BlockSpec(memory_space=pltpu.SMEM)


def tiles(rows, width, row0=0):
    return pl.BlockSpec((rows, width), lambda i: (i + row0, 0))


def fixed(rows, width):
    return pl.BlockSpec((rows, width), lambda i: (0, 0))


def once(*shape):
    return pl.BlockSpec(shape, lambda i: (0,) * len(shape), pipeline_mode=pl.Buffered(1))


def run(kernel, name, steps, in_specs, out_specs, out_shape, args, estimate, scratch=(), free=(), limit=32):
    in_specs = [once(*a.shape) if s is None else s for s, a in zip(in_specs, args)]
    out_specs = [once(*o.shape) if s is None else s for s, o in zip(out_specs, out_shape)]
    args = [
        a
        if s.memory_space is not None or i in free
        else pltpu.with_memory_space_constraint(a, pltpu.HBM)
        for i, (s, a) in enumerate(zip(in_specs, args))
    ]
    out_shape = [
        o if s.memory_space == pltpu.SMEM else pltpu.HBM(o.shape, o.dtype)
        for s, o in zip(out_specs, out_shape)
    ]
    return pl.pallas_call(
        kernel,
        name=name,
        grid=(steps,),
        in_specs=in_specs,
        out_specs=out_specs,
        out_shape=out_shape,
        scratch_shapes=list(scratch),
        compiler_params=pltpu.CompilerParams(vmem_limit_bytes=limit << 20),
        cost_estimate=estimate,
    )(*args)


def out(shape, dtype):
    return jax.ShapeDtypeStruct(shape, dtype)


def cost(flops, moved, exps=0):
    return pl.CostEstimate(flops=flops, bytes_accessed=moved, transcendentals=exps)


def rope_constants():
    frequency = rope_base ** (-(np.arange(HEAD_DIM // 2, dtype=np.float64) * 2.0) / HEAD_DIM)
    wide = np.tile(frequency, 4)[None, :]
    made = []
    for count, apart in ((BLOCK // 16, 16), (16, 1), (8, BLOCK)):
        angles = np.arange(count, dtype=np.float64)[:, None] * apart * wide
        made += [np.cos(angles), np.sin(angles)]
    return [jnp.asarray(a.astype(np.float32)) for a in made]


def half_front(rows):
    lane = lax.broadcasted_iota(jnp.int32, (rows, LANES), 1)
    return (lane % HEAD_DIM) < HEAD_DIM // 2


def turned(chunk, cosine, signed_sine, back=False):
    partner = jnp.where(
        half_front(chunk.shape[0]), pltpu.roll(chunk, 96, 1), pltpu.roll(chunk, 32, 1)
    )
    if back:
        return chunk * cosine - partner * signed_sine
    return chunk * cosine + partner * signed_sine


def block_tables_in(lengths_ref, order_ref, rank_ref, offset_ref, inverse_ref, reach_ref, wanted_ref, later_ref, live_ref):
    count = order_ref.shape[0]
    steps = MAXLEN // BLOCK - 1

    def sequence(s, begin):
        def one(j, at):
            offset_ref[jnp.minimum(at, count - 1)] = j
            return at + 1

        return lax.fori_loop(0, lengths_ref[s], one, begin)

    lax.fori_loop(0, lengths_ref.shape[0], sequence, jnp.int32(0))

    def invert(d, carry):
        inverse_ref[order_ref[d]] = d
        return carry

    lax.fori_loop(0, count, invert, jnp.int32(0))
    reach_ref[0] = offset_ref[order_ref[rank_ref[0]]]

    def look(d, carry):
        packed = order_ref[d]
        for s in range(1, steps + 1):
            wanted_ref[d * steps + s - 1] = inverse_ref[jnp.maximum(packed - s, 0)]
            next_at = jnp.minimum(packed + s, count - 1)
            later_ref[d * steps + s - 1] = inverse_ref[next_at] * steps + s - 1
            is_live = jnp.logical_and(packed + s < count, offset_ref[next_at] >= s)
            live_ref[d * steps + s - 1] = jnp.where(is_live, 1, 0)
        return carry

    lax.fori_loop(0, count, look, jnp.int32(0))


def project_kernel(
    lengths_ref, order_ref, rank_ref, x_ref, gain_ref, wk_ref, wv_ref,
    cos16_ref, sin16_ref, cos1_ref, sin1_ref, cos0_ref, sin0_ref,
    normed_ref, kv_ref, cosine_ref, sine_ref, reach_ref, wanted_ref, later_ref, live_ref,
    offset_ref, inverse_ref,
):
    @pl.when(pl.program_id(0) == 0)
    def _():
        block_tables_in(
            lengths_ref, order_ref, rank_ref, offset_ref, inverse_ref, reach_ref, wanted_ref, later_ref, live_ref
        )

    x = x_ref[...].astype(jnp.float32)
    scale = lax.rsqrt(jnp.mean(x * x, axis=1, keepdims=True) + epsilon)
    normed = (x * scale * gain_ref[...]).astype(jnp.bfloat16)
    normed_ref[...] = normed
    at = reach_ref[0]
    cos0, sin0 = cos0_ref[pl.ds(at, 1), :], sin0_ref[pl.ds(at, 1), :]
    cos16 = cos16_ref[...] * cos0 - sin16_ref[...] * sin0
    sin16 = sin16_ref[...] * cos0 + cos16_ref[...] * sin0
    cos1, sin1 = cos1_ref[...][None], sin1_ref[...][None]
    cosine = (cos16[:, None, :] * cos1 - sin16[:, None, :] * sin1).reshape(x.shape[0], LANES)
    sine = (sin16[:, None, :] * cos1 + cos16[:, None, :] * sin1).reshape(x.shape[0], LANES)
    sine = jnp.where(half_front(x.shape[0]), -sine, sine)
    cosine_ref[...] = cosine
    sine_ref[...] = sine
    kv_ref[:, :LANES] = turned(mm(normed, wk_ref[...]), cosine, sine).astype(jnp.bfloat16)
    kv_ref[:, LANES:] = mm(normed, wv_ref[...]).astype(jnp.bfloat16)


def query_kernel(normed_ref, wq_ref, cosine_ref, sine_ref, q_ref):
    queries = mm(normed_ref[...], wq_ref[...])
    for i in range(0, SHARE, LANES):
        q_ref[:, i : i + LANES] = turned(
            queries[:, i : i + LANES], cosine_ref[...], sine_ref[...]
        ).astype(jnp.bfloat16)


def project_queries(normed, w_query, cosine, sine):
    tile = 256
    return run(
        query_kernel,
        "project_queries",
        BLOCK // tile,
        [tiles(tile, WIDTH), None, tiles(tile, LANES), tiles(tile, LANES)],
        [tiles(tile, SHARE)],
        [out((BLOCK, SHARE), jnp.bfloat16)],
        (normed, w_query, cosine, sine),
        cost(270_000_000, 2_500_000),
    )[0]


def project(lengths, order, rank, x, gain, w_key, w_value):
    tile = 256
    count = order.shape[0]
    steps = MAXLEN // BLOCK - 1
    bf16, f32 = jnp.bfloat16, jnp.float32
    return run(
        project_kernel,
        "project",
        BLOCK // tile,
        [smem()] * 3
        + [tiles(tile, WIDTH), None, None, None]
        + [tiles(tile // 16, LANES)] * 2
        + [None] * 4,
        [tiles(tile, WIDTH), tiles(tile, SHARE)] + [tiles(tile, LANES)] * 2 + [smem()] * 4,
        [out((BLOCK, WIDTH), bf16), out((BLOCK, SHARE), bf16)]
        + [out((BLOCK, LANES), f32)] * 2
        + [out((1,), jnp.int32)]
        + [out((count * steps,), jnp.int32)] * 3,
        (lengths, order, rank, x, gain, w_key, w_value, *rope_constants()),
        cost(540_000_000, 4_000_000, 512),
        [pltpu.SMEM((count,), jnp.int32), pltpu.SMEM((count,), jnp.int32)],
    )


def pick_kernel(wanted_ref, pieces_ref, picked_ref):
    def one(i, carry):
        picked_ref[i] = pieces_ref[wanted_ref[i]]
        return carry

    lax.fori_loop(0, picked_ref.shape[0], one, jnp.int32(0), unroll=4)


def pick_pieces(wanted, pieces):
    shape = out((wanted.shape[0], *pieces.shape[1:]), pieces.dtype)
    return run(
        pick_kernel, "pick_pieces", 1, [smem(), None], [None], [shape], (wanted, pieces), cost(0, 1_100_000), free=(1,)
    )[0]


def sum_kernel(later_ref, live_ref, pieces_ref, sum_ref):
    steps = MAXLEN // BLOCK - 1

    def one(d, carry):
        total = jnp.zeros(sum_ref.shape[1:], jnp.float32)
        for s in range(steps):
            part = pieces_ref[later_ref[d * steps + s]].astype(jnp.float32)
            total = total + jnp.where(live_ref[d * steps + s] == 1, part, 0.0)
        sum_ref[d] = total.astype(sum_ref.dtype)
        return carry

    lax.fori_loop(0, sum_ref.shape[0], one, jnp.int32(0), unroll=2)


def sum_pieces(later, live, pieces, count):
    shape = out((count, *pieces.shape[1:]), pieces.dtype)
    return run(
        sum_kernel,
        "sum_pieces",
        1,
        [smem(), smem(), None],
        [None],
        [shape],
        (later, live, pieces),
        cost(0, 1_100_000),
        free=(2,),
    )[0]


def route_kernel(begin_ref, routes_ref, picks_ref, ranks_ref):
    tokens = routes_ref.shape[1]
    expert_at = lax.broadcasted_iota(jnp.int32, (LANES, tokens), 0)
    hits = jnp.zeros((LANES, tokens), jnp.float32)
    for k in range(routes_ref.shape[0]):
        hits = hits + jnp.where(routes_ref[k : k + 1, :] == expert_at, 1.0, 0.0)
    row_at = lax.broadcasted_iota(jnp.int32, (tokens, tokens), 0)
    column_at = lax.broadcasted_iota(jnp.int32, (tokens, tokens), 1)
    before = jnp.where(row_at < column_at, 1.0, 0.0).astype(jnp.bfloat16)
    ranks = jnp.where(hits > 0.5, mm(hits.astype(jnp.bfloat16), before), -1.0)
    ranks_ref[...] = ranks
    slot_at = lax.broadcasted_iota(jnp.int32, (QUARTER, tokens), 0) + begin_ref[0]
    slot_at = slot_at.astype(jnp.float32)
    for e in range(EXPERTS):
        picks_ref[e * QUARTER : (e + 1) * QUARTER, :] = jnp.where(
            ranks[e : e + 1, :] == slot_at, 1.0, 0.0
        ).astype(jnp.bfloat16)


def route(begin, routes_t):
    return run(
        route_kernel,
        "route",
        1,
        [smem(), None],
        [None, None],
        [out((SLOTS, BLOCK), jnp.bfloat16), out((LANES, BLOCK), jnp.float32)],
        (begin, routes_t),
        cost(100_000_000, 1_600_000),
        free=(1,),
    )


def padded_columns(rows_t, out_ref):
    zero = jnp.zeros((HEAD_DIM, rows_t.shape[1]), out_ref.dtype)
    for h in range(4):
        mine = rows_t[h * HEAD_DIM : (h + 1) * HEAD_DIM].astype(out_ref.dtype)
        at = (h // 2) * HEAD_DIM
        out_ref[h, pl.ds(at, HEAD_DIM), :] = mine
        out_ref[h, pl.ds(HEAD_DIM - at, HEAD_DIM), :] = zero


def padded_rows(rows, out_ref):
    n = rows.shape[0]
    lane = lax.broadcasted_iota(jnp.int32, (n, 128), 1)
    for h in range(4):
        pair = rows[:, (h // 2) * 128 : (h // 2) * 128 + 128].astype(jnp.float32)
        if h % 2 != h // 2:
            pair = pltpu.roll(pair, HEAD_DIM, 1)
        own = (lane < HEAD_DIM) if h // 2 == 0 else (lane >= HEAD_DIM)
        out_ref[pl.ds(h * n, n), :] = jnp.where(own, pair, 0.0).astype(out_ref.dtype)


def attend_block(key_rows, value_rows, first, qpad_ref, max_ref, sum_ref, out_t_ref):
    half = BLOCK // 2
    for h in range(4):
        group = (h // 2) * HEAD_DIM
        for t in range(2):
            cols = slice(t * half, (t + 1) * half)
            rows = half if first and t == 0 else BLOCK
            scores = mm(key_rows[:rows], qpad_ref[h, :, cols])
            if first:
                key_at = lax.broadcasted_iota(jnp.int32, scores.shape, 0)
                query_at = lax.broadcasted_iota(jnp.int32, scores.shape, 1) + t * half
                scores = jnp.where(key_at > query_at, masked_score, scores)
            new_max = jnp.max(scores, axis=0, keepdims=True)
            if not first:
                old_max = max_ref[h : h + 1, cols]
                new_max = jnp.maximum(new_max, old_max)
                shrink = jnp.exp(old_max - new_max)
            weights = jnp.exp(scores - new_max)
            total = jnp.sum(weights, axis=0, keepdims=True)
            part = mm(value_rows[:rows], weights.astype(jnp.bfloat16), TN)[group : group + HEAD_DIM]
            mine = pl.ds(h * HEAD_DIM, HEAD_DIM)
            if not first:
                total = total + sum_ref[h : h + 1, cols] * shrink
                part = part + out_t_ref[mine, cols] * shrink
            max_ref[h : h + 1, cols] = new_max
            sum_ref[h : h + 1, cols] = total
            out_t_ref[mine, cols] = part


def attend_own_kernel(q_ref, own_ref, qpad_ref, max_ref, sum_ref, out_t_ref):
    padded_columns(jnp.transpose(q_ref[...].astype(jnp.float32) * score_mult), qpad_ref)
    max_ref[...] = jnp.zeros_like(max_ref)
    sum_ref[...] = jnp.ones_like(sum_ref)
    attend_block(own_ref[:, :LANES], own_ref[:, LANES:], True, qpad_ref, max_ref, sum_ref, out_t_ref)


def attend_own(queries, own_kv):
    return pl.pallas_call(
        attend_own_kernel,
        name="attend_own",
        in_specs=[vmem()] * 2,
        out_specs=[vmem()] * 4,
        out_shape=[
            out((4, LANES, BLOCK), jnp.bfloat16),
            out((8, BLOCK), jnp.float32),
            out((8, BLOCK), jnp.float32),
            out((SHARE, BLOCK), jnp.float32),
        ],
        compiler_params=pltpu.CompilerParams(vmem_limit_bytes=36 << 20),
        cost_estimate=cost(1_000_000_000, 2_000_000, 600_000),
    )(queries, own_kv)


def attend_kernel(
    reach_ref, qpad_ref, max0_ref, sum0_ref, out0_ref, prev_ref, att_ref, out_t_ref, lse_ref, max_ref, sum_ref
):
    max_ref[...] = max0_ref[...]
    sum_ref[...] = sum0_ref[...]
    out_t_ref[...] = out0_ref[...]

    @pl.loop(1, reach_ref[0] + 1)
    def _(step):
        rows = prev_ref[:, pl.ds(step - 1, 1)].reshape(BLOCK, SHARE)
        attend_block(rows[:, :LANES], rows[:, LANES:], False, qpad_ref, max_ref, sum_ref, out_t_ref)

    lse_ref[...] = max_ref[...] + jnp.log(sum_ref[...])
    for h in range(4):
        mine = pl.ds(h * HEAD_DIM, HEAD_DIM)
        out_t_ref[mine, :] = out_t_ref[mine, :] / sum_ref[h : h + 1, :]
    att_ref[...] = jnp.transpose(out_t_ref[...]).astype(jnp.bfloat16)


def attend(reach, begun, earlier):
    return run(
        attend_kernel,
        "attend",
        1,
        [smem()] + [vmem()] * 5,
        [None] * 3,
        [
            out((BLOCK, SHARE), jnp.bfloat16),
            out((SHARE, BLOCK), jnp.float32),
            out((8, BLOCK), jnp.float32),
        ],
        (reach, *begun, earlier),
        cost(4_000_000_000, 3_000_000, 3_000_000),
        [pltpu.VMEM((8, BLOCK), jnp.float32), pltpu.VMEM((8, BLOCK), jnp.float32)],
        limit=36,
    )


def attend_back_kernel(
    reach_ref, q_ref, qpad_ref, own_ref, prev_ref, grad_ref, grad_t_ref, out_t_ref, lse_ref, cos_ref, sin_ref,
    qgrad_ref, own_grad_ref, prev_grad_ref,
    gpad_ref, qrows_ref, grows_ref, ds_ref, p_ref, delta_ref, dq_ref,
):
    half = BLOCK // 2
    q_scaled = q_ref[...].astype(jnp.float32) * score_mult
    padded_rows(q_scaled, qrows_ref)
    padded_columns(grad_t_ref[...], gpad_ref)
    padded_rows(grad_ref[...], grows_ref)
    both = grad_t_ref[...].astype(jnp.float32) * out_t_ref[...]
    for h in range(4):
        delta_ref[h : h + 1, :] = jnp.sum(
            both[h * HEAD_DIM : (h + 1) * HEAD_DIM], axis=0, keepdims=True
        )


    def block(key_rows, value_rows, first):
        for h in range(4):
            for t in range(2):
                cols = slice(t * half, (t + 1) * half)
                wide = slice(h * BLOCK + t * half, h * BLOCK + (t + 1) * half)
                rows = half if first and t == 0 else BLOCK
                scores = mm(key_rows[:rows], qpad_ref[h, :, cols])
                weights = jnp.exp(scores - lse_ref[h : h + 1, cols])
                if first:
                    key_at = lax.broadcasted_iota(jnp.int32, scores.shape, 0)
                    query_at = lax.broadcasted_iota(jnp.int32, scores.shape, 1) + t * half
                    weights = jnp.where(key_at > query_at, 0.0, weights)
                weight_grad = mm(value_rows[:rows], gpad_ref[h, :, cols])
                score_grad = weights * (weight_grad - delta_ref[h : h + 1, cols])
                p_ref[:rows, wide] = weights.astype(jnp.bfloat16)
                ds_ref[:rows, wide] = score_grad.astype(jnp.bfloat16)
                if rows < BLOCK:
                    p_ref[rows:, wide] = jnp.zeros((BLOCK - rows, half), jnp.bfloat16)
                    ds_ref[rows:, wide] = jnp.zeros((BLOCK - rows, half), jnp.bfloat16)
        key_grad = mm(ds_ref[...], qrows_ref[...])
        value_grad = mm(p_ref[...], grows_ref[...])
        for h in range(4):
            group = (h // 2) * HEAD_DIM
            mine = pl.ds(h * HEAD_DIM, HEAD_DIM)
            part = mm(key_rows, ds_ref[:, h * BLOCK : (h + 1) * BLOCK], TN)[group : group + HEAD_DIM]
            dq_ref[mine, :] = part if first else dq_ref[mine, :] + part
        return key_grad, value_grad

    key_grad, value_grad = block(own_ref[:, :LANES], own_ref[:, LANES:], True)
    own_grad_ref[:, :LANES] = key_grad
    own_grad_ref[:, LANES:] = value_grad

    @pl.loop(1, reach_ref[0] + 1)
    def _(step):
        rows = prev_ref[:, pl.ds(step - 1, 1)].reshape(BLOCK, SHARE)
        key_grad, value_grad = block(rows[:, :LANES], rows[:, LANES:], False)
        parts = prev_grad_ref.shape[0]
        shape = (parts, 1, BLOCK // parts, LANES)
        prev_grad_ref[:, pl.ds(step - 1, 1), :, :LANES] = key_grad.astype(jnp.bfloat16).reshape(shape)
        prev_grad_ref[:, pl.ds(step - 1, 1), :, LANES:] = value_grad.astype(jnp.bfloat16).reshape(shape)

    query_grad = jnp.transpose(dq_ref[...]) * score_mult
    for i in range(0, SHARE, LANES):
        qgrad_ref[:, i : i + LANES] = turned(
            query_grad[:, i : i + LANES], cos_ref[...], sin_ref[...], back=True
        ).astype(jnp.bfloat16)


def attend_back(reach, queries, padded, own_kv, earlier, grad, grad_t, out_t, lse, cosine, signed_sine):
    return run(
        attend_back_kernel,
        "attend_back",
        1,
        [smem()] + [vmem()] * 10,
        [None] * 3,
        [
            out((BLOCK, SHARE), jnp.bfloat16),
            out((BLOCK, SHARE), jnp.float32),
            out(earlier.shape, jnp.bfloat16),
        ],
        (reach, queries, padded, own_kv, earlier, grad, grad_t, out_t, lse, cosine, signed_sine),
        cost(12_000_000_000, 5_000_000, 3_000_000),
        [
            pltpu.VMEM((4, LANES, BLOCK), jnp.bfloat16),
            pltpu.VMEM((4 * BLOCK, LANES), jnp.bfloat16),
            pltpu.VMEM((4 * BLOCK, LANES), jnp.bfloat16),
            pltpu.VMEM((BLOCK, 4 * BLOCK), jnp.bfloat16),
            pltpu.VMEM((BLOCK, 4 * BLOCK), jnp.bfloat16),
            pltpu.VMEM((8, BLOCK), jnp.float32),
            pltpu.VMEM((SHARE, BLOCK), jnp.float32),
        ],
        limit=36,
    )


def residual_kernel(
    a0, a1, a2, a3, w0, w1, w2, w3, x_ref, gain_ref, router_ref, ranks_ref, picks_ref,
    residual_ref, moe_ref, gates_ref, rows_ref, held_ref,
):
    step = pl.program_id(0)
    tile = x_ref.shape[0]

    @pl.when(step < BLOCK // tile)
    def _():
        branch = mm(a0[...], w0[...])
        for a, w in ((a1, w1), (a2, w2), (a3, w3)):
            branch = branch + mm(a[...], w[...])
        residual = x_ref[...].astype(jnp.float32) + residual_mult * branch
        residual_ref[...] = residual
        scale = lax.rsqrt(jnp.mean(residual * residual, axis=1, keepdims=True) + epsilon)
        moe_in = (residual * scale * gain_ref[...]).astype(jnp.bfloat16)
        moe_ref[:, :WIDTH] = moe_in
        logits = mm(router_ref[...], moe_in, NT)
        chosen = ranks_ref[...] >= 0.0
        kept = jnp.where(chosen, logits, masked_score)
        top = jnp.max(kept, axis=0, keepdims=True)
        raised = jnp.where(chosen, jnp.exp(kept - top), 0.0)
        gates = raised / jnp.sum(raised, axis=0, keepdims=True)
        gates_ref[...] = gates
        low = (residual_mult * jnp.transpose(gates)).astype(jnp.bfloat16)
        moe_ref[:, WIDTH:] = low
        held_ref[pl.ds(step * tile, tile), :WIDTH] = moe_in
        held_ref[pl.ds(step * tile, tile), WIDTH:] = low

    @pl.when(step >= BLOCK // tile)
    def _():
        rows_ref[...] = mm(picks_ref[...], held_ref[...]).astype(jnp.bfloat16)


def residual_step(attended, w_out, x, gain, router_t, ranks, picks):
    tile = 256
    first = BLOCK // tile
    slot_tile = SLOTS // 2

    def early(rows, width):
        return pl.BlockSpec((rows, width), lambda i: (jnp.minimum(i, first - 1), 0))

    def late(rows, width):
        return pl.BlockSpec((rows, width), lambda i: (jnp.maximum(i - first, 0), 0))

    by_columns = pl.BlockSpec((LANES, tile), lambda i: (0, jnp.minimum(i, first - 1)))
    return run(
        residual_kernel,
        "residual_step",
        first + 2,
        [early(tile, SHARE)] * 4
        + [None] * 4
        + [early(tile, WIDTH), None, None, by_columns, late(slot_tile, BLOCK)],
        [early(tile, WIDTH), early(tile, WIDTH + LANES), by_columns, late(slot_tile, WIDTH + LANES)],
        [
            out((BLOCK, WIDTH), jnp.float32),
            out((BLOCK, WIDTH + LANES), jnp.bfloat16),
            out((LANES, BLOCK), jnp.float32),
            out((SLOTS, WIDTH + LANES), jnp.bfloat16),
        ],
        (*attended, *w_out, x, gain, router_t, ranks, picks),
        cost(2_700_000_000, 12_000_000, 70_000),
        [pltpu.VMEM((BLOCK, WIDTH + LANES), jnp.bfloat16)],
        free=(1, 2, 3, 5, 6, 7, 10),
    )


def mix_kernel(begin_ref, ranks_ref, moe_ref, mix_ref):
    ranks = jnp.transpose(ranks_ref[...]).astype(jnp.bfloat16)
    gates = moe_ref[:, WIDTH:]
    width = 640
    for at in range(0, SLOTS, width):
        expert_at = lax.broadcasted_iota(jnp.int32, (LANES, width), 0)
        first = expert_at * QUARTER - at
        slot_at = lax.broadcasted_iota(jnp.int32, (LANES, width), 1)
        inside = jnp.logical_and(slot_at >= first, slot_at < first + QUARTER)
        spread = jnp.where(inside, 1.0, 0.0).astype(jnp.bfloat16)
        within = jnp.sum(jnp.where(inside, slot_at - first, 0), axis=0, keepdims=True) + begin_ref[0]
        hit = mm(ranks, spread) == within.astype(jnp.float32)
        mix_ref[:, at : at + width] = jnp.where(hit, mm(gates, spread), 0.0).astype(jnp.bfloat16)


def mix_weights(begin, ranks, moe_cat):
    return run(
        mix_kernel,
        "mix_weights",
        1,
        [smem(), None, None],
        [None],
        [out((BLOCK, SLOTS), jnp.bfloat16)],
        (begin, ranks, moe_cat),
        cost(350_000_000, 3_000_000),
    )[0]


def expert_kernel(lane_ref, x_ref, grad_ref, *refs):
    downs, gate_refs, up_refs = refs[:4], refs[4:8], refs[8:12]
    row_ref, hidden_ref, units_ref = refs[12:]
    rows = row_ref.shape[0]
    here = pl.ds(pl.program_id(0) * rows, rows)
    lane = lax.broadcasted_iota(jnp.int32, (rows, LANES), 1) == lane_ref[0]
    gate = jnp.sum(
        jnp.where(lane, x_ref[here, WIDTH:].astype(jnp.float32), 0.0), axis=1, keepdims=True
    )
    x = x_ref[here, :WIDTH]
    gates, ups, sigmoids = [], [], []
    for j in range(4):
        pre = mm(x, jnp.concatenate([gate_refs[j][...], up_refs[j][...]], axis=1))
        gate_pre, up_pre = pre[:, :LANES], pre[:, LANES:]
        gates.append(gate_pre)
        ups.append(up_pre)
        sigmoids.append(1.0 / (1.0 + jnp.exp(-gate_pre)))
    down = jnp.concatenate([p[...] for p in downs], axis=0)
    hidden_grad = mm(grad_ref[...], down, NT)
    gate_grad = jnp.zeros((rows, LANES), jnp.float32)
    row = None
    for j in range(4):
        part = hidden_grad[:, j * LANES : (j + 1) * LANES]
        silu = gates[j] * sigmoids[j]
        hidden = (silu * ups[j]).astype(jnp.bfloat16)
        hidden_ref[:, j * LANES : (j + 1) * LANES] = hidden
        gate_grad = gate_grad + hidden.astype(jnp.float32) * part
        gate_pre_grad = part * ups[j] * sigmoids[j] * (1.0 + gates[j] * (1.0 - sigmoids[j]))
        up_pre_grad = part * silu
        units_ref[:, j * SHARE : j * SHARE + LANES] = (gate_pre_grad * gate).astype(jnp.bfloat16)
        units_ref[:, j * SHARE + LANES : (j + 1) * SHARE] = (up_pre_grad * gate).astype(jnp.bfloat16)
        both = jnp.concatenate([gate_pre_grad, up_pre_grad], axis=1).astype(jnp.bfloat16)
        term = mm(both, jnp.concatenate([gate_refs[j][...], up_refs[j][...]], axis=1), NT)
        row = term if row is None else row + term
    row_ref[:, :WIDTH] = row.astype(jnp.bfloat16)
    gate_grad = jnp.sum(gate_grad, axis=1, keepdims=True)
    row_ref[:, WIDTH:] = jnp.where(lane, gate_grad, 0.0).astype(jnp.bfloat16)


def output_kernel(hidden_ref, d0, d1, d2, d3, out_ref):
    down = jnp.concatenate([p[...] for p in (d0, d1, d2, d3)], axis=0)
    out_ref[...] = mm(hidden_ref[...], down).astype(jnp.bfloat16)


def output_rows(hidden, downs):
    tile = 320
    return run(
        output_kernel,
        "output_rows",
        SLOTS // tile,
        [tiles(tile, 512)] + [None] * 4,
        [tiles(tile, WIDTH)],
        [out((SLOTS, WIDTH), jnp.bfloat16)],
        (hidden, *downs),
        cost(1_300_000_000, 5_000_000),
    )[0]


def expert_step(lane, x, grad, downs, gates, ups):
    tile = 320
    return run(
        expert_kernel,
        "expert_step",
        SLOTS // tile,
        [smem(), vmem(), tiles(tile, WIDTH)] + [None] * 12,
        [tiles(tile, WIDTH + LANES), tiles(tile, 512), tiles(tile, WIDTH)],
        [
            out((SLOTS, WIDTH + LANES), jnp.bfloat16),
            out((SLOTS, 512), jnp.bfloat16),
            out((SLOTS, WIDTH), jnp.bfloat16),
        ],
        (lane, x, grad, *downs, *gates, *ups),
        cost(6_700_000_000, 15_000_000, 700_000),
        limit=40,
    )


def unit_grads_kernel(lane_ref, x_ref, grad_ref, hidden_ref, units_ref, keep_ref, send_ref, turned_ref, gate_ref):
    step = pl.program_id(0)

    @pl.when(step == 0)
    def _():
        for k in range(4):
            columns = slice(k * SHARE, (k + 1) * SHARE)
            turned_ref[columns, :] = jnp.transpose(x_ref[:, columns])
        lane = lax.broadcasted_iota(jnp.int32, (SLOTS, LANES), 1) == lane_ref[0]
        gate = jnp.where(lane, x_ref[:, WIDTH:].astype(jnp.float32), 0.0)
        gate_ref[...] = jnp.broadcast_to(jnp.sum(gate, axis=1, keepdims=True), (SLOTS, LANES))

    def write(to_ref):
        scaled = (hidden_ref[...].astype(jnp.float32) * gate_ref[...]).astype(jnp.bfloat16)
        to_ref[0, :LANES, :] = mm(scaled, grad_ref[...], TN).astype(jnp.bfloat16)
        for k in range(4):
            columns = slice(k * SHARE, (k + 1) * SHARE)
            to_ref[0, LANES:, columns] = mm(turned_ref[columns, :], units_ref[...]).astype(jnp.bfloat16)

    @pl.when(step < 2)
    def _():
        write(keep_ref)

    @pl.when(step >= 2)
    def _():
        write(send_ref)


def unit_grads(lane, x, grad, hidden, units):
    rows = SHARE + LANES

    def share_of(i):
        return jnp.where(i < 2, 2 * i, 2 * i - 3)

    return run(
        unit_grads_kernel,
        "unit_grads",
        4,
        [
            smem(),
            vmem(),
            None,
            pl.BlockSpec((SLOTS, LANES), lambda i: (0, share_of(i))),
            pl.BlockSpec((SLOTS, SHARE), lambda i: (0, share_of(i))),
        ],
        [
            pl.BlockSpec((1, rows, WIDTH), lambda i: (jnp.minimum(i, 1), 0, 0)),
            pl.BlockSpec((1, rows, WIDTH), lambda i: (jnp.maximum(i - 2, 0), 0, 0)),
        ],
        [out((2, rows, WIDTH), jnp.bfloat16), out((2, rows, WIDTH), jnp.bfloat16)],
        (lane, x, grad, hidden, units),
        cost(4_000_000_000, 12_000_000),
        [pltpu.VMEM((WIDTH, SLOTS), jnp.bfloat16), pltpu.VMEM((SLOTS, LANES), jnp.float32)],
        limit=36,
    )


def unit_finish_kernel(mine_ref, first_ref, second_ref, third_ref, gate_ref, up_ref, down_ref):
    got = jnp.concatenate([first_ref[...], second_ref[...], third_ref[...]], axis=0)
    total = mine_ref[0] + got.astype(jnp.float32)
    down_ref[0] = total[:LANES, :]
    for k in range(4):
        rows = slice(k * SHARE, (k + 1) * SHARE)
        gate_ref[0, rows, :] = total[LANES:, k * SHARE : k * SHARE + LANES]
        up_ref[0, rows, :] = total[LANES:, k * SHARE + LANES : (k + 1) * SHARE]


def unit_finish(mine, first, second, third):
    return run(
        unit_finish_kernel,
        "unit_finish",
        1,
        [once(1, PACKED, WIDTH), None, None, None],
        [None] * 3,
        [
            out((1, WIDTH, LANES), jnp.float32),
            out((1, WIDTH, LANES), jnp.float32),
            out((1, LANES, WIDTH), jnp.float32),
        ],
        (mine, first, second, third),
        cost(1_000_000, 3_000_000),
        free=(0, 1, 2, 3),
    )


def home_kernel(rank_ref, mix_ref, rows_ref, keep_ref, send_ref):
    rank = rank_ref[0]
    extra = rows_ref.shape[1] > WIDTH
    for j in range(4):
        at = pl.multiple_of(jnp.bitwise_xor(rank, j) * SHARE, SHARE)
        total = mm(mix_ref[...], rows_ref[:, pl.ds(at, SHARE)])
        to_ref = send_ref if j % 2 else keep_ref
        to_ref[(j // 2) * BLOCK : (j // 2 + 1) * BLOCK, :] = total.astype(to_ref.dtype)
    if extra:
        gate_grads = jnp.transpose(mm(mix_ref[...], rows_ref[:, WIDTH:]))[:EXPERTS]
        for to_ref in (keep_ref, send_ref):
            for i in range(2):
                at = 2 * BLOCK + i * EXPERTS
                to_ref[at : at + EXPERTS, :] = gate_grads[:, i * SHARE : (i + 1) * SHARE].astype(
                    to_ref.dtype
                )


def sum_home(rank, mix, rows):
    height = 2 * BLOCK + (2 * EXPERTS if rows.shape[1] > WIDTH else 0)
    return run(
        home_kernel,
        "sum_home",
        1,
        [smem(), None, vmem()],
        [None] * 2,
        [out((height, SHARE), jnp.float32), out((height, SHARE), jnp.bfloat16)],
        (rank, mix, rows),
        cost(1_500_000_000, 6_000_000),
        limit=36,
    )


def swap_kernel(mine_ref, got_ref, total_ref):
    mine, got = mine_ref, got_ref
    half = BLOCK
    total_ref[:half] = (mine[:half] + got[half : 2 * half].astype(jnp.float32)).astype(total_ref.dtype)
    total_ref[half : 2 * half] = (
        mine[half : 2 * half] + got[:half].astype(jnp.float32)
    ).astype(total_ref.dtype)
    total_ref[2 * half :] = (mine[2 * half :] + got[2 * half :].astype(jnp.float32)).astype(
        total_ref.dtype
    )


def swap_sum(mine, got):
    return run(
        swap_kernel,
        "swap_sum",
        1,
        [None] * 2,
        [None],
        [out(mine.shape, jnp.bfloat16)],
        (mine, got),
        cost(1_000_000, 2_500_000),
        free=(0, 1),
    )[0]


def norm_back_kernel(
    rank_ref, g0, g2, g1, g3, z_ref, gates_ref, residual_ref, gain_ref, router_ref, grad_ref, w_ref,
    low_ref, logit_ref, own_ref, att_ref, att_t_ref, gain_grad_ref, u_ref,
):
    rank = rank_ref[0]
    for flip, part in enumerate((g0, g1, g2, g3)):
        at = pl.multiple_of(jnp.bitwise_xor(rank, flip) * SHARE, SHARE)
        u_ref[:, pl.ds(at, SHARE)] = part[...].astype(jnp.float32)
    weighted_grads = z_ref[...].astype(jnp.float32)
    gates = gates_ref[:EXPERTS, :]
    inner = jnp.sum(weighted_grads, axis=0, keepdims=True)
    logit_grad = (weighted_grads - gates * inner).astype(jnp.bfloat16)
    logit_ref[...] = logit_grad
    u = u_ref[...] + mm(logit_grad, router_ref[:EXPERTS, :], TN)
    v = residual_ref[...]
    scale = lax.rsqrt(jnp.mean(v * v, axis=1, keepdims=True) + epsilon)
    weighted = u * gain_ref[...]
    mean = jnp.mean(weighted * v, axis=1, keepdims=True)
    total = grad_ref[...].astype(jnp.float32) + scale * weighted - v * (scale * scale * scale * mean)

    @pl.when(pl.program_id(0) == 0)
    def _():
        gain_grad_ref[...] = jnp.zeros_like(gain_grad_ref)

    gain_grad_ref[0:1, :] += jnp.sum(u * v * scale, axis=0, keepdims=True)
    low = (residual_mult * total).astype(jnp.bfloat16)
    low_ref[...] = low
    u_ref[...] = total
    own_ref[...] = u_ref[:, pl.ds(pl.multiple_of(rank * SHARE, SHARE), SHARE)]
    att_ref[...] = mm(low, w_ref[...], NT).astype(jnp.bfloat16)
    att_t_ref[...] = mm(w_ref[...], low, NT).astype(jnp.bfloat16)


def norm_back_step(rank, mine, theirs, gates, residual, gain, router_t, out_grad, w_out):
    tile = 256
    by_columns = pl.BlockSpec((EXPERTS, tile), lambda i: (0, i))
    return run(
        norm_back_kernel,
        "norm_back_step",
        BLOCK // tile,
        [smem()]
        + [tiles(tile, SHARE), tiles(tile, SHARE, BLOCK // tile)] * 2
        + [
            tiles(EXPERTS, SHARE, 2 * BLOCK // EXPERTS),
            pl.BlockSpec((LANES, tile), lambda i: (0, i)),
            tiles(tile, WIDTH),
            None,
            None,
            tiles(tile, WIDTH),
            None,
        ],
        [
            tiles(tile, WIDTH),
            by_columns,
            tiles(tile, SHARE),
            tiles(tile, SHARE),
            pl.BlockSpec((SHARE, tile), lambda i: (0, i)),
            fixed(8, WIDTH),
        ],
        [
            out((BLOCK, WIDTH), jnp.bfloat16),
            out((EXPERTS, BLOCK), jnp.bfloat16),
            out((BLOCK, SHARE), jnp.float32),
            out((BLOCK, SHARE), jnp.bfloat16),
            out((SHARE, BLOCK), jnp.bfloat16),
            out((8, WIDTH), jnp.float32),
        ],
        (rank, mine, mine, theirs, theirs, mine, gates, residual, gain, router_t, out_grad, w_out),
        cost(700_000_000, 9_000_000, 512),
        [pltpu.VMEM((tile, WIDTH), jnp.float32)],
        free=(3, 4, 9),
    )


def dense_grads_kernel(low_ref, attended_ref, normed_ref, qgrad_ref, logit_ref, moe_ref, gain_ref, made_ref):
    made_ref[:, :SHARE] = mm(low_ref[...], attended_ref[...], TN).astype(jnp.bfloat16)
    made_ref[:, SHARE : 2 * SHARE] = mm(normed_ref[...], qgrad_ref[...], TN).astype(jnp.bfloat16)
    router = mm(logit_ref[...], moe_ref[:, :WIDTH])
    stacked = jnp.concatenate(
        [router, gain_ref[...], jnp.zeros((LANES - EXPERTS - 8, WIDTH), jnp.float32)], axis=0
    )
    made_ref[:, 2 * SHARE :] = jnp.transpose(stacked).astype(jnp.bfloat16)


def dense_grads(low, attended, normed, qgrad, logit, moe_cat, gain_grad):
    return run(
        dense_grads_kernel,
        "dense_grads",
        1,
        [None] * 7,
        [None],
        [out((WIDTH, 2 * SHARE + LANES), jnp.bfloat16)],
        (low, attended, normed, qgrad, logit, moe_cat, gain_grad),
        cost(600_000_000, 6_000_000),
    )[0]


def last_grads_kernel(
    rank_ref, own_ref, home_ref, qgrad_ref, normed_ref, x_ref, wq_ref, wk_ref, wv_ref, cos_ref, sin_ref, made_ref,
    gain_ref, all_ref, keep_ref, send_ref, inner_ref, part_ref,
):
    rank = rank_ref[0]
    kv = own_ref[...] + home_ref[...].astype(jnp.float32)
    key_grad = turned(kv[:, :LANES], cos_ref[...], sin_ref[...], back=True).astype(jnp.bfloat16)
    value_grad = kv[:, LANES:].astype(jnp.bfloat16)
    both = jnp.concatenate([key_grad, value_grad], axis=1)
    all_ref[:, : 2 * SHARE] = made_ref[:, : 2 * SHARE]
    all_ref[:, 2 * SHARE : 3 * SHARE] = mm(normed_ref[...], both, TN).astype(jnp.bfloat16)
    gain = jnp.zeros((1, WIDTH), jnp.float32)
    tile = 128
    for i in range(0, BLOCK, tile):
        rows = slice(i, i + tile)
        part = mm(qgrad_ref[rows, :], wq_ref[...], NT)
        part = part + mm(key_grad[rows], wk_ref[...], NT) + mm(value_grad[rows], wv_ref[...], NT)
        x = x_ref[rows, :].astype(jnp.float32)
        scale = lax.rsqrt(jnp.mean(x * x, axis=1, keepdims=True) + epsilon)
        along = part * x
        gain = gain + jnp.sum(along * scale, axis=0, keepdims=True)
        inner = jnp.sum(along * gain_ref[...], axis=1, keepdims=True)
        inner_ref[:, rows] = jnp.transpose(jnp.broadcast_to(inner, (tile, LANES)))[:8]
        part_ref[rows, :] = part
    for j in range(4):
        at = pl.multiple_of(jnp.bitwise_xor(rank, j) * SHARE, SHARE)
        to_ref = send_ref if j % 2 else keep_ref
        to_ref[(j // 2) * BLOCK : (j // 2 + 1) * BLOCK, :] = part_ref[:, pl.ds(at, SHARE)].astype(to_ref.dtype)
    lane = lax.broadcasted_iota(jnp.int32, (WIDTH, LANES), 1)
    column = jnp.transpose(jnp.broadcast_to(gain, (LANES, WIDTH)))
    rest = jnp.where(lane == EXPERTS + 8, column, made_ref[:, 2 * SHARE :].astype(jnp.float32))
    all_ref[:, 3 * SHARE :] = rest.astype(jnp.bfloat16)


def last_grads(rank, own, home, qgrad, normed, x, w_query, w_key, w_value, cosine, sine, made, gain):
    return run(
        last_grads_kernel,
        "last_grads",
        1,
        [smem()] + [None] * 12,
        [None] * 4,
        [
            out((WIDTH, 3 * SHARE + LANES), jnp.bfloat16),
            out((2 * BLOCK, SHARE), jnp.float32),
            out((2 * BLOCK, SHARE), jnp.bfloat16),
            out((8, BLOCK), jnp.float32),
        ],
        (rank, own, home, qgrad, normed, x, w_query, w_key, w_value, cosine, sine, made, gain),
        cost(1_000_000_000, 8_000_000, 512),
        [pltpu.VMEM((BLOCK, WIDTH), jnp.float32)],
        free=(2,),
    )


def input_finish_kernel(
    rank_ref, near_ref, far_ref, i0, i1, i2, i3, x_ref, gain_ref, residual_ref, made_ref
):
    mine = pl.ds(pl.multiple_of(rank_ref[0] * SHARE, SHARE), SHARE)
    x = x_ref[...].astype(jnp.float32)
    scale = lax.rsqrt(jnp.mean(x * x, axis=1, keepdims=True) + epsilon)
    inner = (i0[...] + i1[...] + i2[...] + i3[...]) * (1.0 / WIDTH)
    inner = jnp.transpose(jnp.broadcast_to(inner[:1], (LANES, BLOCK)))[:, :1]
    weighted = (near_ref[...] + far_ref[...].astype(jnp.float32)) * gain_ref[:, mine]
    x_own = x_ref[:, mine].astype(jnp.float32)
    made_ref[...] = residual_ref[...] + scale * weighted - x_own * (scale * scale * scale * inner)


def input_finish(rank, near, far, inners, x, gain, residual):
    return run(
        input_finish_kernel,
        "input_finish",
        1,
        [smem(), once(BLOCK, SHARE), None] + [None] * 7,
        [None],
        [out((BLOCK, SHARE), jnp.float32)],
        (rank, near, far, *inners, x, gain, residual),
        cost(3_000_000, 3_000_000, 512),
        free=(1, 2, 3, 4, 5, 6),
    )[0]


def per_device(
    hidden_in,
    lengths,
    block_order,
    routes,
    norm_gain_attn,
    w_query,
    w_key,
    w_value,
    w_out,
    norm_gain_moe,
    w_router,
    w_gate,
    w_up,
    w_down,
    out_grad,
):
    dp_count = block_order.shape[0]
    mp_rank = lax.axis_index("mp").astype(jnp.int32)
    column_start = mp_rank * SHARE
    piece = BLOCK // dp_count
    steps = MAXLEN // BLOCK - 1
    rank = mp_rank.reshape(1)
    lane = lax.axis_index("dp").astype(jnp.int32).reshape(1)
    begin = rank * QUARTER
    gain_attn = norm_gain_attn[None, :]
    gain_moe = norm_gain_moe[None, :]
    router_t = jnp.pad(w_router.T, ((0, LANES - EXPERTS), (0, 0)))

    far_out = peer(w_out, 2)
    far_down = peer(w_down[0], 2)

    normed, key_value, cosine, sine, reach, wanted, later, live = project(
        lengths, block_order, lane, hidden_in, gain_attn, w_key, w_value
    )
    queries = project_queries(normed, w_query, cosine, sine)
    pieces = to_all(key_value.reshape(dp_count, piece, SHARE))
    picks, ranks = route(begin, after(routes.T, key_value))
    begun = attend_own(queries, after(key_value, picks))
    picked = pick_pieces(wanted, after(pieces, far_out, far_down, queries, picks))
    far_gate = peer(after(w_gate[0], picked), 2)
    far_up = peer(after(w_up[0], picked), 2)
    earlier = to_all(picked.reshape(dp_count, steps * piece, SHARE))
    earlier = earlier.reshape(dp_count, steps, piece, SHARE)

    outs = [w_out, peer(after(w_out, picked), 1), far_out, peer(far_out, 1)]

    grad_rows = jnp.dot(picks, after(out_grad, picked), preferred_element_type=jnp.bfloat16)
    grad_arrived = to_experts(after(grad_rows, earlier, begun[1], far_gate, far_up).reshape(EXPERTS, QUARTER, WIDTH))
    attended, attended_t, lse = attend(reach, begun, earlier)
    far = peer(attended, 2)
    residual, moe_cat, gates, moe_rows = residual_step(
        [attended, peer(attended, 1), far, peer(far, 1)],
        outs,
        hidden_in,
        gain_moe,
        router_t,
        ranks,
        picks,
    )
    own = [after(w[0], moe_rows) for w in (w_down, w_gate, w_up)]
    far = [after(w, moe_rows) for w in (far_down, far_gate, far_up)]
    downs, gates_all, ups = [[w, peer(w, 1), v, peer(v, 1)] for w, v in zip(own, far)]
    grouped = to_experts(moe_rows.reshape(EXPERTS, QUARTER, -1)).reshape(SLOTS, -1)
    mix = mix_weights(begin, ranks, moe_cat)
    grouped_grad = grad_arrived.reshape(SLOTS, WIDTH)
    row_grad, hidden_units, unit_grad = expert_step(
        lane, grouped, grouped_grad, downs, gates_all, ups
    )
    row_home = to_experts(row_grad.reshape(dp_count, QUARTER, -1)).reshape(SLOTS, -1)
    rows_out = output_rows(hidden_units, downs)
    rows_home = to_experts(after(rows_out, row_home).reshape(dp_count, QUARTER, -1)).reshape(SLOTS, -1)

    unit_keep, unit_send = unit_grads(lane, grouped, grouped_grad, hidden_units, unit_grad)
    unit_near = unit_keep.astype(jnp.float32) + peer(unit_send, 1).astype(jnp.float32)
    unit_low = unit_near[1].astype(jnp.bfloat16)
    cut = PACKED // 2
    unit_far_a = peer(unit_low[:cut], 2)
    keep, send = sum_home(rank, after(mix, unit_far_a, rows_out), row_home)
    near = keep + peer(send, 1).astype(jnp.float32)
    mine = swap_sum(near, peer(near.astype(jnp.bfloat16), 2))
    theirs = peer(mine, 1)
    branch_grad, logit_grad, residual_grad, attended_grad, attended_grad_t, moe_gain = norm_back_step(
        rank, mine, theirs, gates, residual, gain_moe, router_t, out_grad, w_out
    )

    query_pre_grad, own_grads, later_grads = attend_back(
        reach,
        queries,
        begun[0],
        key_value,
        earlier,
        attended_grad,
        attended_grad_t,
        attended_t,
        lse,
        cosine,
        sine,
    )
    unit_far_b = peer(after(unit_low[cut:], later_grads), 2)
    unit_far_b = peer(after(unit_low[cut : cut + cut // 2], branch_grad), 2)
    later_pieces = to_all(after(later_grads, rows_home, unit_far_b).reshape(dp_count, steps * piece, SHARE))
    summed = sum_pieces(
        later, live, later_pieces.reshape(dp_count * steps, piece, SHARE), dp_count
    )
    kv_home = to_all(summed).reshape(BLOCK, SHARE)
    made = dense_grads(
        branch_grad, attended, normed, query_pre_grad, logit_grad, moe_cat, moe_gain
    )

    unit_far_c = peer(after(unit_low[cut + cut // 2 :], kv_home, made), 2)

    every, keep, send, inner = last_grads(
        rank,
        own_grads,
        kv_home,
        query_pre_grad,
        normed,
        hidden_in,
        w_query,
        w_key,
        w_value,
        cosine,
        sine,
        made,
        gain_attn,
    )
    near_norm = keep + peer(send, 1).astype(jnp.float32)
    far_norm = peer(near_norm[BLOCK:].astype(jnp.bfloat16), 2)
    inners = [inner] + [peer(inner, flip) for flip in (1, 2, 3)]
    every = after(every, unit_far_c)
    arrived = to_all(every.reshape(dp_count, WIDTH // dp_count, -1))
    keep, send = sum_home(rank, mix, after(rows_home, every))
    near_mix = keep + peer(send, 1).astype(jnp.float32)
    far_mix = peer(near_mix[BLOCK:].astype(jnp.bfloat16), 2)
    grad_w_gate, grad_w_up, grad_w_down = unit_finish(
        unit_near, unit_far_a, after(unit_far_b, every), unit_far_c
    )
    dense = jnp.sum(arrived.astype(jnp.float32), axis=0)
    at = 3 * SHARE
    attn_gain = dense[:, at + EXPERTS + 8]
    attn_gain = attn_gain + peer(attn_gain, 1) + peer(attn_gain, 2) + peer(attn_gain, 3)
    residual_cols = lax.dynamic_slice_in_dim(residual, column_start, SHARE, 1)
    mixture = near_mix[:BLOCK] + after(far_mix, attn_gain).astype(jnp.float32)
    out_hidden = (residual_cols + mixture).astype(jnp.bfloat16)

    grad_hidden = input_finish(
        rank, near_norm, after(far_norm, dense), inners, hidden_in, gain_attn, residual_grad
    )
    return (
        out_hidden,
        grad_hidden,
        dense[:, SHARE : 2 * SHARE],
        dense[:, 2 * SHARE : 2 * SHARE + LANES],
        dense[:, 2 * SHARE + LANES : at],
        dense[:, :SHARE].T,
        attn_gain,
        dense[:, at + EXPERTS],
        dense[:, at : at + EXPERTS],
        grad_w_gate,
        grad_w_up,
        grad_w_down,
    )


def solution(mesh):
    in_specs = (
        P("dp", None),
        P(),
        P(),
        P("dp", None),
        P(),
        P(None, "mp"),
        P(None, "mp"),
        P(None, "mp"),
        P("mp", None),
        P(),
        P(),
        P("dp", None, "mp"),
        P("dp", None, "mp"),
        P("dp", "mp", None),
        P("dp", None),
    )
    out_specs = (
        P("dp", "mp"),
        P("dp", "mp"),
        P("dp", "mp"),
        P("dp", "mp"),
        P("dp", "mp"),
        P("mp", "dp"),
        P("dp"),
        P("dp"),
        P("dp", None),
        P("dp", None, "mp"),
        P("dp", None, "mp"),
        P("dp", "mp", None),
    )
    return jax.shard_map(
        per_device, mesh=mesh, in_specs=in_specs, out_specs=out_specs, check_vma=False
    )
```

```python
import jax
import jax.numpy as jnp
import numpy as np
from jax import lax
from jax.experimental import pallas as pl
from jax.experimental.pallas import tpu as pltpu
from jax.sharding import PartitionSpec as P

HEAD_DIM = 64
EXPERTS = 32
BLOCK = 512
MAXLEN = 2048
CAP = 160
WIDTH = 1024
SHARE = 256
QUARTER = 40
SLOTS = 1280
LANES = 128
PACKED = 384

epsilon = 1e-06
residual_mult = 0.22
score_mult = 0.015625
rope_base = 10000.0
masked_score = -1e30

NN = (((1,), (0,)), ((), ()))
NT = (((1,), (1,)), ((), ()))
TN = (((0,), (0,)), ((), ()))


def mm(a, b, dims=NN):
    return lax.dot_general(a, b, dims, preferred_element_type=jnp.float32)


def to_all(x):
    return lax.all_to_all(x, "dp", 0, 0, tiled=True)


def crossed_groups(dp_count, cores):
    groups = []
    for chip in range(2):
        for core in range(2):
            turn = 1 if core in cores else 0
            groups.append([i * 4 + (chip ^ (i & turn)) * 2 + core for i in range(dp_count)])
    return groups


def to_experts(x, cores=(0, 1)):
    return lax.all_to_all(
        x, ("dp", "mp"), 0, 0, axis_index_groups=crossed_groups(x.shape[0], cores), tiled=True
    )


def peer(x, flip):
    return lax.ppermute(x, "mp", [(i, i ^ flip) for i in range(4)])


def after(x, *others):
    return lax.optimization_barrier((x, *others))[0]


def vmem():
    return pl.BlockSpec(memory_space=pltpu.VMEM)


def smem():
    return pl.BlockSpec(memory_space=pltpu.SMEM)


def tiles(rows, width, row0=0):
    return pl.BlockSpec((rows, width), lambda i: (i + row0, 0))


def fixed(rows, width):
    return pl.BlockSpec((rows, width), lambda i: (0, 0))


def once(*shape):
    return pl.BlockSpec(shape, lambda i: (0,) * len(shape), pipeline_mode=pl.Buffered(1))


def run(kernel, name, steps, in_specs, out_specs, out_shape, args, estimate, scratch=(), free=(), limit=32):
    in_specs = [once(*a.shape) if s is None else s for s, a in zip(in_specs, args)]
    out_specs = [once(*o.shape) if s is None else s for s, o in zip(out_specs, out_shape)]
    args = [
        a
        if s.memory_space is not None or i in free
        else pltpu.with_memory_space_constraint(a, pltpu.HBM)
        for i, (s, a) in enumerate(zip(in_specs, args))
    ]
    out_shape = [
        o if s.memory_space == pltpu.SMEM else pltpu.HBM(o.shape, o.dtype)
        for s, o in zip(out_specs, out_shape)
    ]
    return pl.pallas_call(
        kernel,
        name=name,
        grid=(steps,),
        in_specs=in_specs,
        out_specs=out_specs,
        out_shape=out_shape,
        scratch_shapes=list(scratch),
        compiler_params=pltpu.CompilerParams(vmem_limit_bytes=limit << 20),
        cost_estimate=estimate,
    )(*args)


def out(shape, dtype):
    return jax.ShapeDtypeStruct(shape, dtype)


def cost(flops, moved, exps=0):
    return pl.CostEstimate(flops=flops, bytes_accessed=moved, transcendentals=exps)


def rope_constants():
    frequency = rope_base ** (-(np.arange(HEAD_DIM // 2, dtype=np.float64) * 2.0) / HEAD_DIM)
    wide = np.tile(frequency, 4)[None, :]
    made = []
    for count, apart in ((BLOCK // 16, 16), (16, 1), (8, BLOCK)):
        angles = np.arange(count, dtype=np.float64)[:, None] * apart * wide
        made += [np.cos(angles), np.sin(angles)]
    return [jnp.asarray(a.astype(np.float32)) for a in made]


def half_front(rows):
    lane = lax.broadcasted_iota(jnp.int32, (rows, LANES), 1)
    return (lane % HEAD_DIM) < HEAD_DIM // 2


def turned(chunk, cosine, signed_sine, back=False):
    partner = jnp.where(
        half_front(chunk.shape[0]), pltpu.roll(chunk, 96, 1), pltpu.roll(chunk, 32, 1)
    )
    if back:
        return chunk * cosine - partner * signed_sine
    return chunk * cosine + partner * signed_sine


def block_tables_in(lengths_ref, order_ref, rank_ref, offset_ref, inverse_ref, reach_ref, wanted_ref, later_ref, live_ref):
    count = order_ref.shape[0]
    steps = MAXLEN // BLOCK - 1

    def sequence(s, begin):
        def one(j, at):
            offset_ref[jnp.minimum(at, count - 1)] = j
            return at + 1

        return lax.fori_loop(0, lengths_ref[s], one, begin)

    lax.fori_loop(0, lengths_ref.shape[0], sequence, jnp.int32(0))

    def invert(d, carry):
        inverse_ref[order_ref[d]] = d
        return carry

    lax.fori_loop(0, count, invert, jnp.int32(0))
    reach_ref[0] = offset_ref[order_ref[rank_ref[0]]]

    def look(d, carry):
        packed = order_ref[d]
        for s in range(1, steps + 1):
            wanted_ref[d * steps + s - 1] = inverse_ref[jnp.maximum(packed - s, 0)]
            next_at = jnp.minimum(packed + s, count - 1)
            later_ref[d * steps + s - 1] = inverse_ref[next_at] * steps + s - 1
            is_live = jnp.logical_and(packed + s < count, offset_ref[next_at] >= s)
            live_ref[d * steps + s - 1] = jnp.where(is_live, 1, 0)
        return carry

    lax.fori_loop(0, count, look, jnp.int32(0))


def project_kernel(
    lengths_ref, order_ref, rank_ref, x_ref, gain_ref, wk_ref, wv_ref,
    cos16_ref, sin16_ref, cos1_ref, sin1_ref, cos0_ref, sin0_ref,
    normed_ref, kv_ref, cosine_ref, sine_ref, reach_ref, wanted_ref, later_ref, live_ref,
    offset_ref, inverse_ref,
):
    @pl.when(pl.program_id(0) == 0)
    def _():
        block_tables_in(
            lengths_ref, order_ref, rank_ref, offset_ref, inverse_ref, reach_ref, wanted_ref, later_ref, live_ref
        )

    x = x_ref[...].astype(jnp.float32)
    scale = lax.rsqrt(jnp.mean(x * x, axis=1, keepdims=True) + epsilon)
    normed = (x * scale * gain_ref[...]).astype(jnp.bfloat16)
    normed_ref[...] = normed
    at = reach_ref[0]
    cos0, sin0 = cos0_ref[pl.ds(at, 1), :], sin0_ref[pl.ds(at, 1), :]
    cos16 = cos16_ref[...] * cos0 - sin16_ref[...] * sin0
    sin16 = sin16_ref[...] * cos0 + cos16_ref[...] * sin0
    cos1, sin1 = cos1_ref[...][None], sin1_ref[...][None]
    cosine = (cos16[:, None, :] * cos1 - sin16[:, None, :] * sin1).reshape(x.shape[0], LANES)
    sine = (sin16[:, None, :] * cos1 + cos16[:, None, :] * sin1).reshape(x.shape[0], LANES)
    sine = jnp.where(half_front(x.shape[0]), -sine, sine)
    cosine_ref[...] = cosine
    sine_ref[...] = sine
    kv_ref[:, :LANES] = turned(mm(normed, wk_ref[...]), cosine, sine).astype(jnp.bfloat16)
    kv_ref[:, LANES:] = mm(normed, wv_ref[...]).astype(jnp.bfloat16)


def query_kernel(normed_ref, wq_ref, cosine_ref, sine_ref, q_ref):
    queries = mm(normed_ref[...], wq_ref[...])
    for i in range(0, SHARE, LANES):
        q_ref[:, i : i + LANES] = turned(
            queries[:, i : i + LANES], cosine_ref[...], sine_ref[...]
        ).astype(jnp.bfloat16)


def project_queries(normed, w_query, cosine, sine):
    tile = 256
    return run(
        query_kernel,
        "project_queries",
        BLOCK // tile,
        [tiles(tile, WIDTH), None, tiles(tile, LANES), tiles(tile, LANES)],
        [tiles(tile, SHARE)],
        [out((BLOCK, SHARE), jnp.bfloat16)],
        (normed, w_query, cosine, sine),
        cost(270_000_000, 2_500_000),
    )[0]


def project(lengths, order, rank, x, gain, w_key, w_value):
    tile = 256
    count = order.shape[0]
    steps = MAXLEN // BLOCK - 1
    bf16, f32 = jnp.bfloat16, jnp.float32
    return run(
        project_kernel,
        "project",
        BLOCK // tile,
        [smem()] * 3
        + [tiles(tile, WIDTH), None, None, None]
        + [tiles(tile // 16, LANES)] * 2
        + [None] * 4,
        [tiles(tile, WIDTH), tiles(tile, SHARE)] + [tiles(tile, LANES)] * 2 + [smem()] * 4,
        [out((BLOCK, WIDTH), bf16), out((BLOCK, SHARE), bf16)]
        + [out((BLOCK, LANES), f32)] * 2
        + [out((1,), jnp.int32)]
        + [out((count * steps,), jnp.int32)] * 3,
        (lengths, order, rank, x, gain, w_key, w_value, *rope_constants()),
        cost(540_000_000, 4_000_000, 512),
        [pltpu.SMEM((count,), jnp.int32), pltpu.SMEM((count,), jnp.int32)],
    )


def pick_kernel(wanted_ref, pieces_ref, picked_ref):
    def one(i, carry):
        picked_ref[i] = pieces_ref[wanted_ref[i]]
        return carry

    lax.fori_loop(0, picked_ref.shape[0], one, jnp.int32(0), unroll=4)


def pick_pieces(wanted, pieces):
    shape = out((wanted.shape[0], *pieces.shape[1:]), pieces.dtype)
    return run(
        pick_kernel, "pick_pieces", 1, [smem(), None], [None], [shape], (wanted, pieces), cost(0, 1_100_000), free=(1,)
    )[0]


def sum_kernel(later_ref, live_ref, pieces_ref, sum_ref):
    steps = MAXLEN // BLOCK - 1

    def one(d, carry):
        total = jnp.zeros(sum_ref.shape[1:], jnp.float32)
        for s in range(steps):
            part = pieces_ref[later_ref[d * steps + s]].astype(jnp.float32)
            total = total + jnp.where(live_ref[d * steps + s] == 1, part, 0.0)
        sum_ref[d] = total.astype(sum_ref.dtype)
        return carry

    lax.fori_loop(0, sum_ref.shape[0], one, jnp.int32(0), unroll=2)


def sum_pieces(later, live, pieces, count):
    shape = out((count, *pieces.shape[1:]), pieces.dtype)
    return run(
        sum_kernel,
        "sum_pieces",
        1,
        [smem(), smem(), None],
        [None],
        [shape],
        (later, live, pieces),
        cost(0, 1_100_000),
        free=(2,),
    )[0]


def route_kernel(begin_ref, bases_ref, routes_ref, picks_ref, sends_ref, ranks_ref):
    tokens = routes_ref.shape[1]
    expert_at = lax.broadcasted_iota(jnp.int32, (LANES, tokens), 0)
    hits = jnp.zeros((LANES, tokens), jnp.float32)
    for k in range(routes_ref.shape[0]):
        hits = hits + jnp.where(routes_ref[k : k + 1, :] == expert_at, 1.0, 0.0)
    row_at = lax.broadcasted_iota(jnp.int32, (tokens, tokens), 0)
    column_at = lax.broadcasted_iota(jnp.int32, (tokens, tokens), 1)
    before = jnp.where(row_at < column_at, 1.0, 0.0).astype(jnp.bfloat16)
    ranks = jnp.where(hits > 0.5, mm(hits.astype(jnp.bfloat16), before), -1.0)
    ranks_ref[...] = ranks
    slot_at = lax.broadcasted_iota(jnp.int32, (QUARTER, tokens), 0)
    own_at = (slot_at + begin_ref[0]).astype(jnp.float32)
    sent_at = [(slot_at + bases_ref[i]).astype(jnp.float32) for i in range(2)]
    for e in range(EXPERTS):
        here = slice(e * QUARTER, (e + 1) * QUARTER)
        rank_here = ranks[e : e + 1, :]
        picks_ref[here, :] = jnp.where(rank_here == own_at, 1.0, 0.0).astype(jnp.bfloat16)
        sends_ref[here, :] = jnp.where(rank_here == sent_at[e % 2], 1.0, 0.0).astype(jnp.bfloat16)


def route(begin, bases, routes_t):
    return run(
        route_kernel,
        "route",
        1,
        [smem(), smem(), None],
        [None, None, None],
        [
            out((SLOTS, BLOCK), jnp.bfloat16),
            out((SLOTS, BLOCK), jnp.bfloat16),
            out((LANES, BLOCK), jnp.float32),
        ],
        (begin, bases, routes_t),
        cost(100_000_000, 3_000_000),
        free=(2,),
    )


def padded_columns(rows_t, out_ref):
    zero = jnp.zeros((HEAD_DIM, rows_t.shape[1]), out_ref.dtype)
    for h in range(4):
        mine = rows_t[h * HEAD_DIM : (h + 1) * HEAD_DIM].astype(out_ref.dtype)
        at = (h // 2) * HEAD_DIM
        out_ref[h, pl.ds(at, HEAD_DIM), :] = mine
        out_ref[h, pl.ds(HEAD_DIM - at, HEAD_DIM), :] = zero


def padded_rows(rows, out_ref):
    n = rows.shape[0]
    lane = lax.broadcasted_iota(jnp.int32, (n, 128), 1)
    for h in range(4):
        pair = rows[:, (h // 2) * 128 : (h // 2) * 128 + 128].astype(jnp.float32)
        if h % 2 != h // 2:
            pair = pltpu.roll(pair, HEAD_DIM, 1)
        own = (lane < HEAD_DIM) if h // 2 == 0 else (lane >= HEAD_DIM)
        out_ref[pl.ds(h * n, n), :] = jnp.where(own, pair, 0.0).astype(out_ref.dtype)


def attend_block(key_rows, value_rows, first, qpad_ref, max_ref, sum_ref, out_t_ref):
    half = BLOCK // 2
    for h in range(4):
        group = (h // 2) * HEAD_DIM
        for t in range(2):
            cols = slice(t * half, (t + 1) * half)
            rows = half if first and t == 0 else BLOCK
            scores = mm(key_rows[:rows], qpad_ref[h, :, cols])
            if first:
                key_at = lax.broadcasted_iota(jnp.int32, scores.shape, 0)
                query_at = lax.broadcasted_iota(jnp.int32, scores.shape, 1) + t * half
                scores = jnp.where(key_at > query_at, masked_score, scores)
            new_max = jnp.max(scores, axis=0, keepdims=True)
            if not first:
                old_max = max_ref[h : h + 1, cols]
                new_max = jnp.maximum(new_max, old_max)
                shrink = jnp.exp(old_max - new_max)
            weights = jnp.exp(scores - new_max)
            total = jnp.sum(weights, axis=0, keepdims=True)
            part = mm(value_rows[:rows], weights.astype(jnp.bfloat16), TN)[group : group + HEAD_DIM]
            mine = pl.ds(h * HEAD_DIM, HEAD_DIM)
            if not first:
                total = total + sum_ref[h : h + 1, cols] * shrink
                part = part + out_t_ref[mine, cols] * shrink
            max_ref[h : h + 1, cols] = new_max
            sum_ref[h : h + 1, cols] = total
            out_t_ref[mine, cols] = part


def attend_own_kernel(q_ref, own_ref, qpad_ref, max_ref, sum_ref, out_t_ref):
    padded_columns(jnp.transpose(q_ref[...].astype(jnp.float32) * score_mult), qpad_ref)
    max_ref[...] = jnp.zeros_like(max_ref)
    sum_ref[...] = jnp.ones_like(sum_ref)
    attend_block(own_ref[:, :LANES], own_ref[:, LANES:], True, qpad_ref, max_ref, sum_ref, out_t_ref)


def attend_own(queries, own_kv):
    return pl.pallas_call(
        attend_own_kernel,
        name="attend_own",
        in_specs=[vmem()] * 2,
        out_specs=[vmem()] * 4,
        out_shape=[
            out((4, LANES, BLOCK), jnp.bfloat16),
            out((8, BLOCK), jnp.float32),
            out((8, BLOCK), jnp.float32),
            out((SHARE, BLOCK), jnp.float32),
        ],
        compiler_params=pltpu.CompilerParams(vmem_limit_bytes=36 << 20),
        cost_estimate=cost(1_000_000_000, 2_000_000, 600_000),
    )(queries, own_kv)


def attend_kernel(
    reach_ref, qpad_ref, max0_ref, sum0_ref, out0_ref, prev_ref, att_ref, out_t_ref, lse_ref, max_ref, sum_ref
):
    max_ref[...] = max0_ref[...]
    sum_ref[...] = sum0_ref[...]
    out_t_ref[...] = out0_ref[...]

    @pl.loop(1, reach_ref[0] + 1)
    def _(step):
        rows = prev_ref[:, pl.ds(step - 1, 1)].reshape(BLOCK, SHARE)
        attend_block(rows[:, :LANES], rows[:, LANES:], False, qpad_ref, max_ref, sum_ref, out_t_ref)

    lse_ref[...] = max_ref[...] + jnp.log(sum_ref[...])
    for h in range(4):
        mine = pl.ds(h * HEAD_DIM, HEAD_DIM)
        out_t_ref[mine, :] = out_t_ref[mine, :] / sum_ref[h : h + 1, :]
    att_ref[...] = jnp.transpose(out_t_ref[...]).astype(jnp.bfloat16)


def attend(reach, begun, earlier):
    return run(
        attend_kernel,
        "attend",
        1,
        [smem()] + [vmem()] * 5,
        [None] * 3,
        [
            out((BLOCK, SHARE), jnp.bfloat16),
            out((SHARE, BLOCK), jnp.float32),
            out((8, BLOCK), jnp.float32),
        ],
        (reach, *begun, earlier),
        cost(4_000_000_000, 3_000_000, 3_000_000),
        [pltpu.VMEM((8, BLOCK), jnp.float32), pltpu.VMEM((8, BLOCK), jnp.float32)],
        limit=36,
    )


def attend_back_kernel(
    reach_ref, q_ref, qpad_ref, own_ref, prev_ref, grad_ref, grad_t_ref, out_t_ref, lse_ref, cos_ref, sin_ref,
    qgrad_ref, own_grad_ref, prev_grad_ref,
    gpad_ref, qrows_ref, grows_ref, ds_ref, p_ref, delta_ref, dq_ref,
):
    half = BLOCK // 2
    q_scaled = q_ref[...].astype(jnp.float32) * score_mult
    padded_rows(q_scaled, qrows_ref)
    padded_columns(grad_t_ref[...], gpad_ref)
    padded_rows(grad_ref[...], grows_ref)
    both = grad_t_ref[...].astype(jnp.float32) * out_t_ref[...]
    for h in range(4):
        delta_ref[h : h + 1, :] = jnp.sum(
            both[h * HEAD_DIM : (h + 1) * HEAD_DIM], axis=0, keepdims=True
        )


    def block(key_rows, value_rows, first):
        for h in range(4):
            for t in range(2):
                cols = slice(t * half, (t + 1) * half)
                wide = slice(h * BLOCK + t * half, h * BLOCK + (t + 1) * half)
                rows = half if first and t == 0 else BLOCK
                scores = mm(key_rows[:rows], qpad_ref[h, :, cols])
                weights = jnp.exp(scores - lse_ref[h : h + 1, cols])
                if first:
                    key_at = lax.broadcasted_iota(jnp.int32, scores.shape, 0)
                    query_at = lax.broadcasted_iota(jnp.int32, scores.shape, 1) + t * half
                    weights = jnp.where(key_at > query_at, 0.0, weights)
                weight_grad = mm(value_rows[:rows], gpad_ref[h, :, cols])
                score_grad = weights * (weight_grad - delta_ref[h : h + 1, cols])
                p_ref[:rows, wide] = weights.astype(jnp.bfloat16)
                ds_ref[:rows, wide] = score_grad.astype(jnp.bfloat16)
                if rows < BLOCK:
                    p_ref[rows:, wide] = jnp.zeros((BLOCK - rows, half), jnp.bfloat16)
                    ds_ref[rows:, wide] = jnp.zeros((BLOCK - rows, half), jnp.bfloat16)
        key_grad = mm(ds_ref[...], qrows_ref[...])
        value_grad = mm(p_ref[...], grows_ref[...])
        for h in range(4):
            group = (h // 2) * HEAD_DIM
            mine = pl.ds(h * HEAD_DIM, HEAD_DIM)
            part = mm(key_rows, ds_ref[:, h * BLOCK : (h + 1) * BLOCK], TN)[group : group + HEAD_DIM]
            dq_ref[mine, :] = part if first else dq_ref[mine, :] + part
        return key_grad, value_grad

    key_grad, value_grad = block(own_ref[:, :LANES], own_ref[:, LANES:], True)
    own_grad_ref[:, :LANES] = key_grad
    own_grad_ref[:, LANES:] = value_grad

    @pl.loop(1, reach_ref[0] + 1)
    def _(step):
        rows = prev_ref[:, pl.ds(step - 1, 1)].reshape(BLOCK, SHARE)
        key_grad, value_grad = block(rows[:, :LANES], rows[:, LANES:], False)
        parts = prev_grad_ref.shape[0]
        shape = (parts, 1, BLOCK // parts, LANES)
        prev_grad_ref[:, pl.ds(step - 1, 1), :, :LANES] = key_grad.astype(jnp.bfloat16).reshape(shape)
        prev_grad_ref[:, pl.ds(step - 1, 1), :, LANES:] = value_grad.astype(jnp.bfloat16).reshape(shape)

    query_grad = jnp.transpose(dq_ref[...]) * score_mult
    for i in range(0, SHARE, LANES):
        qgrad_ref[:, i : i + LANES] = turned(
            query_grad[:, i : i + LANES], cos_ref[...], sin_ref[...], back=True
        ).astype(jnp.bfloat16)


def attend_back(reach, queries, padded, own_kv, earlier, grad, grad_t, out_t, lse, cosine, signed_sine):
    return run(
        attend_back_kernel,
        "attend_back",
        1,
        [smem()] + [vmem()] * 10,
        [None] * 3,
        [
            out((BLOCK, SHARE), jnp.bfloat16),
            out((BLOCK, SHARE), jnp.float32),
            out(earlier.shape, jnp.bfloat16),
        ],
        (reach, queries, padded, own_kv, earlier, grad, grad_t, out_t, lse, cosine, signed_sine),
        cost(12_000_000_000, 5_000_000, 3_000_000),
        [
            pltpu.VMEM((4, LANES, BLOCK), jnp.bfloat16),
            pltpu.VMEM((4 * BLOCK, LANES), jnp.bfloat16),
            pltpu.VMEM((4 * BLOCK, LANES), jnp.bfloat16),
            pltpu.VMEM((BLOCK, 4 * BLOCK), jnp.bfloat16),
            pltpu.VMEM((BLOCK, 4 * BLOCK), jnp.bfloat16),
            pltpu.VMEM((8, BLOCK), jnp.float32),
            pltpu.VMEM((SHARE, BLOCK), jnp.float32),
        ],
        limit=36,
    )


def residual_kernel(
    a0, a1, a2, a3, w0, w1, w2, w3, x_ref, gain_ref, router_ref, ranks_ref, picks_ref,
    residual_ref, moe_ref, gates_ref, rows_ref, held_ref,
):
    step = pl.program_id(0)
    tile = x_ref.shape[0]

    @pl.when(step < BLOCK // tile)
    def _():
        branch = mm(a0[...], w0[...])
        for a, w in ((a1, w1), (a2, w2), (a3, w3)):
            branch = branch + mm(a[...], w[...])
        residual = x_ref[...].astype(jnp.float32) + residual_mult * branch
        residual_ref[...] = residual
        scale = lax.rsqrt(jnp.mean(residual * residual, axis=1, keepdims=True) + epsilon)
        moe_in = (residual * scale * gain_ref[...]).astype(jnp.bfloat16)
        moe_ref[:, :WIDTH] = moe_in
        logits = mm(router_ref[...], moe_in, NT)
        chosen = ranks_ref[...] >= 0.0
        kept = jnp.where(chosen, logits, masked_score)
        top = jnp.max(kept, axis=0, keepdims=True)
        raised = jnp.where(chosen, jnp.exp(kept - top), 0.0)
        gates = raised / jnp.sum(raised, axis=0, keepdims=True)
        gates_ref[...] = gates
        low = (residual_mult * jnp.transpose(gates)).astype(jnp.bfloat16)
        moe_ref[:, WIDTH:] = low
        held_ref[pl.ds(step * tile, tile), :WIDTH] = moe_in
        held_ref[pl.ds(step * tile, tile), WIDTH:] = low

    @pl.when(step >= BLOCK // tile)
    def _():
        rows_ref[...] = mm(picks_ref[...], held_ref[...]).astype(jnp.bfloat16)


def residual_step(attended, w_out, x, gain, router_t, ranks, picks):
    tile = 256
    first = BLOCK // tile
    slot_tile = SLOTS // 2

    def early(rows, width):
        return pl.BlockSpec((rows, width), lambda i: (jnp.minimum(i, first - 1), 0))

    def late(rows, width):
        return pl.BlockSpec((rows, width), lambda i: (jnp.maximum(i - first, 0), 0))

    by_columns = pl.BlockSpec((LANES, tile), lambda i: (0, jnp.minimum(i, first - 1)))
    return run(
        residual_kernel,
        "residual_step",
        first + 2,
        [early(tile, SHARE)] * 4
        + [None] * 4
        + [early(tile, WIDTH), None, None, by_columns, late(slot_tile, BLOCK)],
        [early(tile, WIDTH), early(tile, WIDTH + LANES), by_columns, late(slot_tile, WIDTH + LANES)],
        [
            out((BLOCK, WIDTH), jnp.float32),
            out((BLOCK, WIDTH + LANES), jnp.bfloat16),
            out((LANES, BLOCK), jnp.float32),
            out((SLOTS, WIDTH + LANES), jnp.bfloat16),
        ],
        (*attended, *w_out, x, gain, router_t, ranks, picks),
        cost(2_700_000_000, 12_000_000, 70_000),
        [pltpu.VMEM((BLOCK, WIDTH + LANES), jnp.bfloat16)],
        free=(1, 2, 3, 5, 6, 7, 10),
    )


def mix_kernel(begin_ref, ranks_ref, moe_ref, mix_ref):
    ranks = jnp.transpose(ranks_ref[...]).astype(jnp.bfloat16)
    gates = moe_ref[:, WIDTH:]
    width = 640
    for at in range(0, SLOTS, width):
        expert_at = lax.broadcasted_iota(jnp.int32, (LANES, width), 0)
        first = expert_at * QUARTER - at
        slot_at = lax.broadcasted_iota(jnp.int32, (LANES, width), 1)
        inside = jnp.logical_and(slot_at >= first, slot_at < first + QUARTER)
        spread = jnp.where(inside, 1.0, 0.0).astype(jnp.bfloat16)
        within = jnp.sum(jnp.where(inside, slot_at - first, 0), axis=0, keepdims=True) + begin_ref[0]
        hit = mm(ranks, spread) == within.astype(jnp.float32)
        mix_ref[:, at : at + width] = jnp.where(hit, mm(gates, spread), 0.0).astype(jnp.bfloat16)


def mix_weights(begin, ranks, moe_cat):
    return run(
        mix_kernel,
        "mix_weights",
        1,
        [smem(), None, None],
        [None],
        [out((BLOCK, SLOTS), jnp.bfloat16)],
        (begin, ranks, moe_cat),
        cost(350_000_000, 3_000_000),
    )[0]


def expert_kernel(lane_ref, x_ref, grad_ref, *refs):
    downs, gate_refs, up_refs = refs[:4], refs[4:8], refs[8:12]
    row_ref, hidden_ref, units_ref = refs[12:]
    rows = row_ref.shape[0]
    here = pl.ds(pl.program_id(0) * rows, rows)
    lane = lax.broadcasted_iota(jnp.int32, (rows, LANES), 1) == lane_ref[0]
    gate = jnp.sum(
        jnp.where(lane, x_ref[here, WIDTH:].astype(jnp.float32), 0.0), axis=1, keepdims=True
    )
    x = x_ref[here, :WIDTH]
    gates, ups, sigmoids = [], [], []
    for j in range(4):
        pre = mm(x, jnp.concatenate([gate_refs[j][...], up_refs[j][...]], axis=1))
        gate_pre, up_pre = pre[:, :LANES], pre[:, LANES:]
        gates.append(gate_pre)
        ups.append(up_pre)
        sigmoids.append(1.0 / (1.0 + jnp.exp(-gate_pre)))
    down = jnp.concatenate([p[...] for p in downs], axis=0)
    hidden_grad = mm(grad_ref[...], down, NT)
    gate_grad = jnp.zeros((rows, LANES), jnp.float32)
    row = None
    for j in range(4):
        part = hidden_grad[:, j * LANES : (j + 1) * LANES]
        silu = gates[j] * sigmoids[j]
        hidden = (silu * ups[j]).astype(jnp.bfloat16)
        hidden_ref[:, j * LANES : (j + 1) * LANES] = hidden
        gate_grad = gate_grad + hidden.astype(jnp.float32) * part
        gate_pre_grad = part * ups[j] * sigmoids[j] * (1.0 + gates[j] * (1.0 - sigmoids[j]))
        up_pre_grad = part * silu
        units_ref[:, j * SHARE : j * SHARE + LANES] = (gate_pre_grad * gate).astype(jnp.bfloat16)
        units_ref[:, j * SHARE + LANES : (j + 1) * SHARE] = (up_pre_grad * gate).astype(jnp.bfloat16)
        both = jnp.concatenate([gate_pre_grad, up_pre_grad], axis=1).astype(jnp.bfloat16)
        term = mm(both, jnp.concatenate([gate_refs[j][...], up_refs[j][...]], axis=1), NT)
        row = term if row is None else row + term
    row_ref[:, :WIDTH] = row.astype(jnp.bfloat16)
    gate_grad = jnp.sum(gate_grad, axis=1, keepdims=True)
    row_ref[:, WIDTH:] = jnp.where(lane, gate_grad, 0.0).astype(jnp.bfloat16)


def output_kernel(hidden_ref, d0, d1, d2, d3, out_ref):
    down = jnp.concatenate([p[...] for p in (d0, d1, d2, d3)], axis=0)
    out_ref[...] = mm(hidden_ref[...], down).astype(jnp.bfloat16)


def output_rows(hidden, downs):
    tile = 320
    return run(
        output_kernel,
        "output_rows",
        SLOTS // tile,
        [tiles(tile, 512)] + [None] * 4,
        [tiles(tile, WIDTH)],
        [out((SLOTS, WIDTH), jnp.bfloat16)],
        (hidden, *downs),
        cost(1_300_000_000, 5_000_000),
    )[0]


def expert_step(lane, x, grad, downs, gates, ups):
    tile = 320
    return run(
        expert_kernel,
        "expert_step",
        SLOTS // tile,
        [smem(), vmem(), tiles(tile, WIDTH)] + [None] * 12,
        [tiles(tile, WIDTH + LANES), tiles(tile, 512), tiles(tile, WIDTH)],
        [
            out((SLOTS, WIDTH + LANES), jnp.bfloat16),
            out((SLOTS, 512), jnp.bfloat16),
            out((SLOTS, WIDTH), jnp.bfloat16),
        ],
        (lane, x, grad, *downs, *gates, *ups),
        cost(6_700_000_000, 15_000_000, 700_000),
        limit=40,
    )


def unit_grads_kernel(lane_ref, x_ref, grad_ref, hidden_ref, units_ref, keep_ref, send_ref, turned_ref, gate_ref):
    step = pl.program_id(0)

    @pl.when(step == 0)
    def _():
        for k in range(4):
            columns = slice(k * SHARE, (k + 1) * SHARE)
            turned_ref[columns, :] = jnp.transpose(x_ref[:, columns])
        lane = lax.broadcasted_iota(jnp.int32, (SLOTS, LANES), 1) == lane_ref[0]
        gate = jnp.where(lane, x_ref[:, WIDTH:].astype(jnp.float32), 0.0)
        gate_ref[...] = jnp.broadcast_to(jnp.sum(gate, axis=1, keepdims=True), (SLOTS, LANES))

    def write(to_ref):
        scaled = (hidden_ref[...].astype(jnp.float32) * gate_ref[...]).astype(jnp.bfloat16)
        to_ref[0, :LANES, :] = mm(scaled, grad_ref[...], TN).astype(jnp.bfloat16)
        for k in range(4):
            columns = slice(k * SHARE, (k + 1) * SHARE)
            to_ref[0, LANES:, columns] = mm(turned_ref[columns, :], units_ref[...]).astype(jnp.bfloat16)

    @pl.when(step < 2)
    def _():
        write(keep_ref)

    @pl.when(step >= 2)
    def _():
        write(send_ref)


def unit_grads(lane, x, grad, hidden, units):
    rows = SHARE + LANES

    def share_of(i):
        return jnp.where(i < 2, 2 * i, 2 * i - 3)

    return run(
        unit_grads_kernel,
        "unit_grads",
        4,
        [
            smem(),
            vmem(),
            None,
            pl.BlockSpec((SLOTS, LANES), lambda i: (0, share_of(i))),
            pl.BlockSpec((SLOTS, SHARE), lambda i: (0, share_of(i))),
        ],
        [
            pl.BlockSpec((1, rows, WIDTH), lambda i: (jnp.minimum(i, 1), 0, 0)),
            pl.BlockSpec((1, rows, WIDTH), lambda i: (jnp.maximum(i - 2, 0), 0, 0)),
        ],
        [out((2, rows, WIDTH), jnp.bfloat16), out((2, rows, WIDTH), jnp.bfloat16)],
        (lane, x, grad, hidden, units),
        cost(4_000_000_000, 12_000_000),
        [pltpu.VMEM((WIDTH, SLOTS), jnp.bfloat16), pltpu.VMEM((SLOTS, LANES), jnp.float32)],
        limit=36,
    )


def unit_finish_kernel(mine_ref, first_ref, second_ref, third_ref, gate_ref, up_ref, down_ref):
    got = jnp.concatenate([first_ref[...], second_ref[...], third_ref[...]], axis=0)
    total = mine_ref[0] + got.astype(jnp.float32)
    down_ref[0] = total[:LANES, :]
    for k in range(4):
        rows = slice(k * SHARE, (k + 1) * SHARE)
        gate_ref[0, rows, :] = total[LANES:, k * SHARE : k * SHARE + LANES]
        up_ref[0, rows, :] = total[LANES:, k * SHARE + LANES : (k + 1) * SHARE]


def unit_finish(mine, first, second, third):
    return run(
        unit_finish_kernel,
        "unit_finish",
        1,
        [once(1, PACKED, WIDTH), None, None, None],
        [None] * 3,
        [
            out((1, WIDTH, LANES), jnp.float32),
            out((1, WIDTH, LANES), jnp.float32),
            out((1, LANES, WIDTH), jnp.float32),
        ],
        (mine, first, second, third),
        cost(1_000_000, 3_000_000),
        free=(0, 1, 2, 3),
    )


def home_kernel(rank_ref, mix_ref, rows_ref, keep_ref, send_ref):
    rank = rank_ref[0]
    extra = rows_ref.shape[1] > WIDTH
    for j in range(4):
        at = pl.multiple_of(jnp.bitwise_xor(rank, j) * SHARE, SHARE)
        total = mm(mix_ref[...], rows_ref[:, pl.ds(at, SHARE)])
        to_ref = send_ref if j % 2 else keep_ref
        to_ref[(j // 2) * BLOCK : (j // 2 + 1) * BLOCK, :] = total.astype(to_ref.dtype)
    if extra:
        gate_grads = jnp.transpose(mm(mix_ref[...], rows_ref[:, WIDTH:]))[:EXPERTS]
        for to_ref in (keep_ref, send_ref):
            for i in range(2):
                at = 2 * BLOCK + i * EXPERTS
                to_ref[at : at + EXPERTS, :] = gate_grads[:, i * SHARE : (i + 1) * SHARE].astype(
                    to_ref.dtype
                )


def sum_home(rank, mix, rows):
    height = 2 * BLOCK + (2 * EXPERTS if rows.shape[1] > WIDTH else 0)
    return run(
        home_kernel,
        "sum_home",
        1,
        [smem(), None, vmem()],
        [None] * 2,
        [out((height, SHARE), jnp.float32), out((height, SHARE), jnp.bfloat16)],
        (rank, mix, rows),
        cost(1_500_000_000, 6_000_000),
        limit=36,
    )


def swap_kernel(mine_ref, got_ref, total_ref):
    mine, got = mine_ref, got_ref
    half = BLOCK
    total_ref[:half] = (mine[:half] + got[half : 2 * half].astype(jnp.float32)).astype(total_ref.dtype)
    total_ref[half : 2 * half] = (
        mine[half : 2 * half] + got[:half].astype(jnp.float32)
    ).astype(total_ref.dtype)
    total_ref[2 * half :] = (mine[2 * half :] + got[2 * half :].astype(jnp.float32)).astype(
        total_ref.dtype
    )


def swap_sum(mine, got):
    return run(
        swap_kernel,
        "swap_sum",
        1,
        [None] * 2,
        [None],
        [out(mine.shape, jnp.bfloat16)],
        (mine, got),
        cost(1_000_000, 2_500_000),
        free=(0, 1),
    )[0]


def norm_back_kernel(
    rank_ref, g0, g2, g1, g3, z_ref, gates_ref, residual_ref, gain_ref, router_ref, grad_ref, w_ref,
    low_ref, logit_ref, own_ref, att_ref, att_t_ref, gain_grad_ref, u_ref,
):
    rank = rank_ref[0]
    for flip, part in enumerate((g0, g1, g2, g3)):
        at = pl.multiple_of(jnp.bitwise_xor(rank, flip) * SHARE, SHARE)
        u_ref[:, pl.ds(at, SHARE)] = part[...].astype(jnp.float32)
    weighted_grads = z_ref[...].astype(jnp.float32)
    gates = gates_ref[:EXPERTS, :]
    inner = jnp.sum(weighted_grads, axis=0, keepdims=True)
    logit_grad = (weighted_grads - gates * inner).astype(jnp.bfloat16)
    logit_ref[...] = logit_grad
    u = u_ref[...] + mm(logit_grad, router_ref[:EXPERTS, :], TN)
    v = residual_ref[...]
    scale = lax.rsqrt(jnp.mean(v * v, axis=1, keepdims=True) + epsilon)
    weighted = u * gain_ref[...]
    mean = jnp.mean(weighted * v, axis=1, keepdims=True)
    total = grad_ref[...].astype(jnp.float32) + scale * weighted - v * (scale * scale * scale * mean)

    @pl.when(pl.program_id(0) == 0)
    def _():
        gain_grad_ref[...] = jnp.zeros_like(gain_grad_ref)

    gain_grad_ref[0:1, :] += jnp.sum(u * v * scale, axis=0, keepdims=True)
    low = (residual_mult * total).astype(jnp.bfloat16)
    low_ref[...] = low
    u_ref[...] = total
    own_ref[...] = u_ref[:, pl.ds(pl.multiple_of(rank * SHARE, SHARE), SHARE)]
    att_ref[...] = mm(low, w_ref[...], NT).astype(jnp.bfloat16)
    att_t_ref[...] = mm(w_ref[...], low, NT).astype(jnp.bfloat16)


def norm_back_step(rank, mine, theirs, gates, residual, gain, router_t, out_grad, w_out):
    tile = 256
    by_columns = pl.BlockSpec((EXPERTS, tile), lambda i: (0, i))
    return run(
        norm_back_kernel,
        "norm_back_step",
        BLOCK // tile,
        [smem()]
        + [tiles(tile, SHARE), tiles(tile, SHARE, BLOCK // tile)] * 2
        + [
            tiles(EXPERTS, SHARE, 2 * BLOCK // EXPERTS),
            pl.BlockSpec((LANES, tile), lambda i: (0, i)),
            tiles(tile, WIDTH),
            None,
            None,
            tiles(tile, WIDTH),
            None,
        ],
        [
            tiles(tile, WIDTH),
            by_columns,
            tiles(tile, SHARE),
            tiles(tile, SHARE),
            pl.BlockSpec((SHARE, tile), lambda i: (0, i)),
            fixed(8, WIDTH),
        ],
        [
            out((BLOCK, WIDTH), jnp.bfloat16),
            out((EXPERTS, BLOCK), jnp.bfloat16),
            out((BLOCK, SHARE), jnp.float32),
            out((BLOCK, SHARE), jnp.bfloat16),
            out((SHARE, BLOCK), jnp.bfloat16),
            out((8, WIDTH), jnp.float32),
        ],
        (rank, mine, mine, theirs, theirs, mine, gates, residual, gain, router_t, out_grad, w_out),
        cost(700_000_000, 9_000_000, 512),
        [pltpu.VMEM((tile, WIDTH), jnp.float32)],
        free=(3, 4, 9),
    )


def dense_grads_kernel(low_ref, attended_ref, normed_ref, qgrad_ref, logit_ref, moe_ref, gain_ref, made_ref):
    made_ref[:, :SHARE] = mm(low_ref[...], attended_ref[...], TN).astype(jnp.bfloat16)
    made_ref[:, SHARE : 2 * SHARE] = mm(normed_ref[...], qgrad_ref[...], TN).astype(jnp.bfloat16)
    router = mm(logit_ref[...], moe_ref[:, :WIDTH])
    stacked = jnp.concatenate(
        [router, gain_ref[...], jnp.zeros((LANES - EXPERTS - 8, WIDTH), jnp.float32)], axis=0
    )
    made_ref[:, 2 * SHARE :] = jnp.transpose(stacked).astype(jnp.bfloat16)


def dense_grads(low, attended, normed, qgrad, logit, moe_cat, gain_grad):
    return run(
        dense_grads_kernel,
        "dense_grads",
        1,
        [None] * 7,
        [None],
        [out((WIDTH, 2 * SHARE + LANES), jnp.bfloat16)],
        (low, attended, normed, qgrad, logit, moe_cat, gain_grad),
        cost(600_000_000, 6_000_000),
    )[0]


def last_grads_kernel(
    rank_ref, own_ref, home_ref, qgrad_ref, normed_ref, x_ref, wq_ref, wk_ref, wv_ref, cos_ref, sin_ref, made_ref,
    gain_ref, all_ref, keep_ref, send_ref, inner_ref, part_ref,
):
    rank = rank_ref[0]
    kv = own_ref[...] + home_ref[...].astype(jnp.float32)
    key_grad = turned(kv[:, :LANES], cos_ref[...], sin_ref[...], back=True).astype(jnp.bfloat16)
    value_grad = kv[:, LANES:].astype(jnp.bfloat16)
    both = jnp.concatenate([key_grad, value_grad], axis=1)
    all_ref[:, : 2 * SHARE] = made_ref[:, : 2 * SHARE]
    all_ref[:, 2 * SHARE : 3 * SHARE] = mm(normed_ref[...], both, TN).astype(jnp.bfloat16)
    gain = jnp.zeros((1, WIDTH), jnp.float32)
    tile = 128
    for i in range(0, BLOCK, tile):
        rows = slice(i, i + tile)
        part = mm(qgrad_ref[rows, :], wq_ref[...], NT)
        part = part + mm(key_grad[rows], wk_ref[...], NT) + mm(value_grad[rows], wv_ref[...], NT)
        x = x_ref[rows, :].astype(jnp.float32)
        scale = lax.rsqrt(jnp.mean(x * x, axis=1, keepdims=True) + epsilon)
        along = part * x
        gain = gain + jnp.sum(along * scale, axis=0, keepdims=True)
        inner = jnp.sum(along * gain_ref[...], axis=1, keepdims=True)
        inner_ref[:, rows] = jnp.transpose(jnp.broadcast_to(inner, (tile, LANES)))[:8]
        part_ref[rows, :] = part
    for j in range(4):
        at = pl.multiple_of(jnp.bitwise_xor(rank, j) * SHARE, SHARE)
        to_ref = send_ref if j % 2 else keep_ref
        to_ref[(j // 2) * BLOCK : (j // 2 + 1) * BLOCK, :] = part_ref[:, pl.ds(at, SHARE)].astype(to_ref.dtype)
    lane = lax.broadcasted_iota(jnp.int32, (WIDTH, LANES), 1)
    column = jnp.transpose(jnp.broadcast_to(gain, (LANES, WIDTH)))
    rest = jnp.where(lane == EXPERTS + 8, column, made_ref[:, 2 * SHARE :].astype(jnp.float32))
    all_ref[:, 3 * SHARE :] = rest.astype(jnp.bfloat16)


def last_grads(rank, own, home, qgrad, normed, x, w_query, w_key, w_value, cosine, sine, made, gain):
    return run(
        last_grads_kernel,
        "last_grads",
        1,
        [smem()] + [None] * 12,
        [None] * 4,
        [
            out((WIDTH, 3 * SHARE + LANES), jnp.bfloat16),
            out((2 * BLOCK, SHARE), jnp.float32),
            out((2 * BLOCK, SHARE), jnp.bfloat16),
            out((8, BLOCK), jnp.float32),
        ],
        (rank, own, home, qgrad, normed, x, w_query, w_key, w_value, cosine, sine, made, gain),
        cost(1_000_000_000, 8_000_000, 512),
        [pltpu.VMEM((BLOCK, WIDTH), jnp.float32)],
        free=(2,),
    )


def input_finish_kernel(
    rank_ref, near_ref, far_ref, i0, i1, i2, i3, x_ref, gain_ref, residual_ref, made_ref
):
    mine = pl.ds(pl.multiple_of(rank_ref[0] * SHARE, SHARE), SHARE)
    x = x_ref[...].astype(jnp.float32)
    scale = lax.rsqrt(jnp.mean(x * x, axis=1, keepdims=True) + epsilon)
    inner = (i0[...] + i1[...] + i2[...] + i3[...]) * (1.0 / WIDTH)
    inner = jnp.transpose(jnp.broadcast_to(inner[:1], (LANES, BLOCK)))[:, :1]
    weighted = (near_ref[...] + far_ref[...].astype(jnp.float32)) * gain_ref[:, mine]
    x_own = x_ref[:, mine].astype(jnp.float32)
    made_ref[...] = residual_ref[...] + scale * weighted - x_own * (scale * scale * scale * inner)


def input_finish(rank, near, far, inners, x, gain, residual):
    return run(
        input_finish_kernel,
        "input_finish",
        1,
        [smem(), once(BLOCK, SHARE), None] + [None] * 7,
        [None],
        [out((BLOCK, SHARE), jnp.float32)],
        (rank, near, far, *inners, x, gain, residual),
        cost(3_000_000, 3_000_000, 512),
        free=(1, 2, 3, 4, 5, 6),
    )[0]


def per_device(
    hidden_in,
    lengths,
    block_order,
    routes,
    norm_gain_attn,
    w_query,
    w_key,
    w_value,
    w_out,
    norm_gain_moe,
    w_router,
    w_gate,
    w_up,
    w_down,
    out_grad,
):
    dp_count = block_order.shape[0]
    mp_rank = lax.axis_index("mp").astype(jnp.int32)
    column_start = mp_rank * SHARE
    piece = BLOCK // dp_count
    steps = MAXLEN // BLOCK - 1
    rank = mp_rank.reshape(1)
    lane = lax.axis_index("dp").astype(jnp.int32).reshape(1)
    begin = rank * QUARTER
    other = jnp.bitwise_xor(rank, 2 * (1 - jnp.bitwise_and(rank, 1)))
    parity = jnp.bitwise_and(lane, 1)
    bases = jnp.where(jnp.arange(2, dtype=jnp.int32) == parity, rank, other) * QUARTER
    gain_attn = norm_gain_attn[None, :]
    gain_moe = norm_gain_moe[None, :]
    router_t = jnp.pad(w_router.T, ((0, LANES - EXPERTS), (0, 0)))

    far_out = peer(w_out, 2)
    cores = ([(0, 2), (2, 0)], [(1, 3), (3, 1)])
    experts = (w_down[0], w_gate[0], w_up[0])
    far_early = [lax.ppermute(w, "mp", cores[0]) for w in experts]

    normed, key_value, cosine, sine, reach, wanted, later, live = project(
        lengths, block_order, lane, hidden_in, gain_attn, w_key, w_value
    )
    queries = project_queries(normed, w_query, cosine, sine)
    pieces = to_all(key_value.reshape(dp_count, piece, SHARE))
    picks, sends, ranks = route(begin, bases, after(routes.T, key_value))
    begun = attend_own(queries, after(key_value, picks))
    picked = pick_pieces(wanted, after(pieces, far_out, *far_early, queries, picks))
    earlier = to_all(picked.reshape(dp_count, steps * piece, SHARE))
    earlier = earlier.reshape(dp_count, steps, piece, SHARE)

    outs = [w_out, peer(after(w_out, picked), 1), far_out, peer(far_out, 1)]

    grad_rows = jnp.dot(picks, after(out_grad, picked), preferred_element_type=jnp.bfloat16)
    grad_arrived = to_experts(after(grad_rows, earlier, begun[1]).reshape(EXPERTS, QUARTER, WIDTH))
    attended, attended_t, lse = attend(reach, begun, earlier)
    far = peer(attended, 2)
    residual, moe_cat, gates, moe_rows = residual_step(
        [attended, peer(attended, 1), far, peer(far, 1)],
        outs,
        hidden_in,
        gain_moe,
        router_t,
        ranks,
        sends,
    )
    late = [lax.ppermute(after(w, moe_rows), "mp", cores[1]) for w in experts]
    far = [a + b for a, b in zip(far_early, late)]
    own = [after(w, moe_rows) for w in experts]
    downs, gates_all, ups = [[w, peer(w, 1), v, peer(v, 1)] for w, v in zip(own, far)]
    grouped = to_experts(moe_rows.reshape(EXPERTS, QUARTER, -1), (1,)).reshape(SLOTS, -1)
    mix = mix_weights(begin, ranks, moe_cat)
    grouped_grad = grad_arrived.reshape(SLOTS, WIDTH)
    row_grad, hidden_units, unit_grad = expert_step(
        lane, grouped, grouped_grad, downs, gates_all, ups
    )
    row_home = to_experts(row_grad.reshape(dp_count, QUARTER, -1)).reshape(SLOTS, -1)
    rows_out = output_rows(hidden_units, downs)
    rows_home = to_experts(after(rows_out, row_home).reshape(dp_count, QUARTER, -1)).reshape(SLOTS, -1)

    unit_keep, unit_send = unit_grads(lane, grouped, grouped_grad, hidden_units, unit_grad)
    unit_near = unit_keep.astype(jnp.float32) + peer(unit_send, 1).astype(jnp.float32)
    unit_low = unit_near[1].astype(jnp.bfloat16)
    cut = PACKED // 2
    unit_far_a = peer(unit_low[:cut], 2)
    keep, send = sum_home(rank, after(mix, unit_far_a, rows_out), row_home)
    near = keep + peer(send, 1).astype(jnp.float32)
    mine = swap_sum(near, peer(near.astype(jnp.bfloat16), 2))
    theirs = peer(mine, 1)
    branch_grad, logit_grad, residual_grad, attended_grad, attended_grad_t, moe_gain = norm_back_step(
        rank, mine, theirs, gates, residual, gain_moe, router_t, out_grad, w_out
    )

    query_pre_grad, own_grads, later_grads = attend_back(
        reach,
        queries,
        begun[0],
        key_value,
        earlier,
        attended_grad,
        attended_grad_t,
        attended_t,
        lse,
        cosine,
        sine,
    )
    unit_far_b = peer(after(unit_low[cut:], later_grads), 2)
    unit_far_b = peer(after(unit_low[cut : cut + cut // 2], branch_grad), 2)
    later_pieces = to_all(after(later_grads, rows_home, unit_far_b).reshape(dp_count, steps * piece, SHARE))
    summed = sum_pieces(
        later, live, later_pieces.reshape(dp_count * steps, piece, SHARE), dp_count
    )
    kv_home = to_all(summed).reshape(BLOCK, SHARE)
    made = dense_grads(
        branch_grad, attended, normed, query_pre_grad, logit_grad, moe_cat, moe_gain
    )

    unit_far_c = peer(after(unit_low[cut + cut // 2 :], kv_home, made), 2)

    every, keep, send, inner = last_grads(
        rank,
        own_grads,
        kv_home,
        query_pre_grad,
        normed,
        hidden_in,
        w_query,
        w_key,
        w_value,
        cosine,
        sine,
        made,
        gain_attn,
    )
    near_norm = keep + peer(send, 1).astype(jnp.float32)
    far_norm = peer(near_norm[BLOCK:].astype(jnp.bfloat16), 2)
    inners = [inner] + [peer(inner, flip) for flip in (1, 2, 3)]
    every = after(every, unit_far_c)
    arrived = to_all(every.reshape(dp_count, WIDTH // dp_count, -1))
    keep, send = sum_home(rank, mix, after(rows_home, every))
    near_mix = keep + peer(send, 1).astype(jnp.float32)
    far_mix = peer(near_mix[BLOCK:].astype(jnp.bfloat16), 2)
    grad_w_gate, grad_w_up, grad_w_down = unit_finish(
        unit_near, unit_far_a, after(unit_far_b, every), unit_far_c
    )
    dense = jnp.sum(arrived.astype(jnp.float32), axis=0)
    at = 3 * SHARE
    attn_gain = dense[:, at + EXPERTS + 8]
    attn_gain = attn_gain + peer(attn_gain, 1) + peer(attn_gain, 2) + peer(attn_gain, 3)
    residual_cols = lax.dynamic_slice_in_dim(residual, column_start, SHARE, 1)
    mixture = near_mix[:BLOCK] + after(far_mix, attn_gain).astype(jnp.float32)
    out_hidden = (residual_cols + mixture).astype(jnp.bfloat16)

    grad_hidden = input_finish(
        rank, near_norm, after(far_norm, dense), inners, hidden_in, gain_attn, residual_grad
    )
    return (
        out_hidden,
        grad_hidden,
        dense[:, SHARE : 2 * SHARE],
        dense[:, 2 * SHARE : 2 * SHARE + LANES],
        dense[:, 2 * SHARE + LANES : at],
        dense[:, :SHARE].T,
        attn_gain,
        dense[:, at + EXPERTS],
        dense[:, at : at + EXPERTS],
        grad_w_gate,
        grad_w_up,
        grad_w_down,
    )


def solution(mesh):
    in_specs = (
        P("dp", None),
        P(),
        P(),
        P("dp", None),
        P(),
        P(None, "mp"),
        P(None, "mp"),
        P(None, "mp"),
        P("mp", None),
        P(),
        P(),
        P("dp", None, "mp"),
        P("dp", None, "mp"),
        P("dp", "mp", None),
        P("dp", None),
    )
    out_specs = (
        P("dp", "mp"),
        P("dp", "mp"),
        P("dp", "mp"),
        P("dp", "mp"),
        P("dp", "mp"),
        P("mp", "dp"),
        P("dp"),
        P("dp"),
        P("dp", None),
        P("dp", None, "mp"),
        P("dp", None, "mp"),
        P("dp", "mp", None),
    )
    return jax.shard_map(
        per_device, mesh=mesh, in_specs=in_specs, out_specs=out_specs, check_vma=False
    )
```

```python
import jax
import jax.numpy as jnp
import numpy as np
from jax import lax
from jax.experimental import pallas as pl
from jax.experimental.pallas import tpu as pltpu
from jax.sharding import PartitionSpec as P

HEAD_DIM = 64
EXPERTS = 32
BLOCK = 512
MAXLEN = 2048
CAP = 160
WIDTH = 1024
SHARE = 256
QUARTER = 40
SLOTS = 1280
LANES = 128
PACKED = 384

epsilon = 1e-06
residual_mult = 0.22
score_mult = 0.015625
rope_base = 10000.0
masked_score = -1e30

NN = (((1,), (0,)), ((), ()))
NT = (((1,), (1,)), ((), ()))
TN = (((0,), (0,)), ((), ()))


def mm(a, b, dims=NN):
    return lax.dot_general(a, b, dims, preferred_element_type=jnp.float32)


def to_all(x):
    return lax.all_to_all(x, "dp", 0, 0, tiled=True)


def crossed_groups(dp_count, cores):
    groups = []
    for chip in range(2):
        for core in range(2):
            turn = 1 if core in cores else 0
            groups.append([i * 4 + (chip ^ (i & turn)) * 2 + core for i in range(dp_count)])
    return groups


def to_experts(x, cores=(0, 1)):
    return lax.all_to_all(
        x, ("dp", "mp"), 0, 0, axis_index_groups=crossed_groups(x.shape[0], cores), tiled=True
    )


def peer(x, flip):
    return lax.ppermute(x, "mp", [(i, i ^ flip) for i in range(4)])


def after(x, *others):
    return lax.optimization_barrier((x, *others))[0]


def vmem():
    return pl.BlockSpec(memory_space=pltpu.VMEM)


def smem():
    return pl.BlockSpec(memory_space=pltpu.SMEM)


def tiles(rows, width, row0=0):
    return pl.BlockSpec((rows, width), lambda i: (i + row0, 0))


def fixed(rows, width):
    return pl.BlockSpec((rows, width), lambda i: (0, 0))


def once(*shape):
    return pl.BlockSpec(shape, lambda i: (0,) * len(shape), pipeline_mode=pl.Buffered(1))


def run(kernel, name, steps, in_specs, out_specs, out_shape, args, estimate, scratch=(), free=(), limit=32):
    in_specs = [once(*a.shape) if s is None else s for s, a in zip(in_specs, args)]
    out_specs = [once(*o.shape) if s is None else s for s, o in zip(out_specs, out_shape)]
    args = [
        a
        if s.memory_space is not None or i in free
        else pltpu.with_memory_space_constraint(a, pltpu.HBM)
        for i, (s, a) in enumerate(zip(in_specs, args))
    ]
    out_shape = [
        o if s.memory_space == pltpu.SMEM else pltpu.HBM(o.shape, o.dtype)
        for s, o in zip(out_specs, out_shape)
    ]
    return pl.pallas_call(
        kernel,
        name=name,
        grid=(steps,),
        in_specs=in_specs,
        out_specs=out_specs,
        out_shape=out_shape,
        scratch_shapes=list(scratch),
        compiler_params=pltpu.CompilerParams(vmem_limit_bytes=limit << 20),
        cost_estimate=estimate,
    )(*args)


def out(shape, dtype):
    return jax.ShapeDtypeStruct(shape, dtype)


def cost(flops, moved, exps=0):
    return pl.CostEstimate(flops=flops, bytes_accessed=moved, transcendentals=exps)


def rope_constants():
    frequency = rope_base ** (-(np.arange(HEAD_DIM // 2, dtype=np.float64) * 2.0) / HEAD_DIM)
    wide = np.tile(frequency, 4)[None, :]
    made = []
    for count, apart in ((BLOCK // 16, 16), (16, 1), (8, BLOCK)):
        angles = np.arange(count, dtype=np.float64)[:, None] * apart * wide
        made += [np.cos(angles), np.sin(angles)]
    return [jnp.asarray(a.astype(np.float32)) for a in made]


def half_front(rows):
    lane = lax.broadcasted_iota(jnp.int32, (rows, LANES), 1)
    return (lane % HEAD_DIM) < HEAD_DIM // 2


def turned(chunk, cosine, signed_sine, back=False):
    partner = jnp.where(
        half_front(chunk.shape[0]), pltpu.roll(chunk, 96, 1), pltpu.roll(chunk, 32, 1)
    )
    if back:
        return chunk * cosine - partner * signed_sine
    return chunk * cosine + partner * signed_sine


def block_tables_in(lengths_ref, order_ref, rank_ref, offset_ref, inverse_ref, reach_ref, wanted_ref, later_ref, live_ref):
    count = order_ref.shape[0]
    steps = MAXLEN // BLOCK - 1

    def sequence(s, begin):
        def one(j, at):
            offset_ref[jnp.minimum(at, count - 1)] = j
            return at + 1

        return lax.fori_loop(0, lengths_ref[s], one, begin)

    lax.fori_loop(0, lengths_ref.shape[0], sequence, jnp.int32(0))

    def invert(d, carry):
        inverse_ref[order_ref[d]] = d
        return carry

    lax.fori_loop(0, count, invert, jnp.int32(0))
    reach_ref[0] = offset_ref[order_ref[rank_ref[0]]]

    def look(d, carry):
        packed = order_ref[d]
        for s in range(1, steps + 1):
            wanted_ref[d * steps + s - 1] = inverse_ref[jnp.maximum(packed - s, 0)]
            next_at = jnp.minimum(packed + s, count - 1)
            later_ref[d * steps + s - 1] = inverse_ref[next_at] * steps + s - 1
            is_live = jnp.logical_and(packed + s < count, offset_ref[next_at] >= s)
            live_ref[d * steps + s - 1] = jnp.where(is_live, 1, 0)
        return carry

    lax.fori_loop(0, count, look, jnp.int32(0))


def project_kernel(
    lengths_ref, order_ref, rank_ref, x_ref, gain_ref, wk_ref, wv_ref,
    cos16_ref, sin16_ref, cos1_ref, sin1_ref, cos0_ref, sin0_ref,
    normed_ref, kv_ref, cosine_ref, sine_ref, reach_ref, wanted_ref, later_ref, live_ref,
    offset_ref, inverse_ref,
):
    @pl.when(pl.program_id(0) == 0)
    def _():
        block_tables_in(
            lengths_ref, order_ref, rank_ref, offset_ref, inverse_ref, reach_ref, wanted_ref, later_ref, live_ref
        )

    x = x_ref[...].astype(jnp.float32)
    scale = lax.rsqrt(jnp.mean(x * x, axis=1, keepdims=True) + epsilon)
    normed = (x * scale * gain_ref[...]).astype(jnp.bfloat16)
    normed_ref[...] = normed
    at = reach_ref[0]
    cos0, sin0 = cos0_ref[pl.ds(at, 1), :], sin0_ref[pl.ds(at, 1), :]
    cos16 = cos16_ref[...] * cos0 - sin16_ref[...] * sin0
    sin16 = sin16_ref[...] * cos0 + cos16_ref[...] * sin0
    cos1, sin1 = cos1_ref[...][None], sin1_ref[...][None]
    cosine = (cos16[:, None, :] * cos1 - sin16[:, None, :] * sin1).reshape(x.shape[0], LANES)
    sine = (sin16[:, None, :] * cos1 + cos16[:, None, :] * sin1).reshape(x.shape[0], LANES)
    sine = jnp.where(half_front(x.shape[0]), -sine, sine)
    cosine_ref[...] = cosine
    sine_ref[...] = sine
    kv_ref[:, :LANES] = turned(mm(normed, wk_ref[...]), cosine, sine).astype(jnp.bfloat16)
    kv_ref[:, LANES:] = mm(normed, wv_ref[...]).astype(jnp.bfloat16)


def query_kernel(normed_ref, wq_ref, cosine_ref, sine_ref, q_ref):
    queries = mm(normed_ref[...], wq_ref[...])
    for i in range(0, SHARE, LANES):
        q_ref[:, i : i + LANES] = turned(
            queries[:, i : i + LANES], cosine_ref[...], sine_ref[...]
        ).astype(jnp.bfloat16)


def project_queries(normed, w_query, cosine, sine):
    tile = 256
    return run(
        query_kernel,
        "project_queries",
        BLOCK // tile,
        [tiles(tile, WIDTH), None, tiles(tile, LANES), tiles(tile, LANES)],
        [tiles(tile, SHARE)],
        [out((BLOCK, SHARE), jnp.bfloat16)],
        (normed, w_query, cosine, sine),
        cost(270_000_000, 2_500_000),
    )[0]


def project(lengths, order, rank, x, gain, w_key, w_value):
    tile = 256
    count = order.shape[0]
    steps = MAXLEN // BLOCK - 1
    bf16, f32 = jnp.bfloat16, jnp.float32
    return run(
        project_kernel,
        "project",
        BLOCK // tile,
        [smem()] * 3
        + [tiles(tile, WIDTH), None, None, None]
        + [tiles(tile // 16, LANES)] * 2
        + [None] * 4,
        [tiles(tile, WIDTH), tiles(tile, SHARE)] + [tiles(tile, LANES)] * 2 + [smem()] * 4,
        [out((BLOCK, WIDTH), bf16), out((BLOCK, SHARE), bf16)]
        + [out((BLOCK, LANES), f32)] * 2
        + [out((1,), jnp.int32)]
        + [out((count * steps,), jnp.int32)] * 3,
        (lengths, order, rank, x, gain, w_key, w_value, *rope_constants()),
        cost(540_000_000, 4_000_000, 512),
        [pltpu.SMEM((count,), jnp.int32), pltpu.SMEM((count,), jnp.int32)],
    )


def pick_kernel(wanted_ref, pieces_ref, picked_ref):
    def one(i, carry):
        picked_ref[i] = pieces_ref[wanted_ref[i]]
        return carry

    lax.fori_loop(0, picked_ref.shape[0], one, jnp.int32(0), unroll=4)


def pick_pieces(wanted, pieces):
    shape = out((wanted.shape[0], *pieces.shape[1:]), pieces.dtype)
    return run(
        pick_kernel, "pick_pieces", 1, [smem(), None], [None], [shape], (wanted, pieces), cost(0, 1_100_000), free=(1,)
    )[0]


def sum_kernel(later_ref, live_ref, pieces_ref, sum_ref):
    steps = MAXLEN // BLOCK - 1

    def one(d, carry):
        total = jnp.zeros(sum_ref.shape[1:], jnp.float32)
        for s in range(steps):
            part = pieces_ref[later_ref[d * steps + s]].astype(jnp.float32)
            total = total + jnp.where(live_ref[d * steps + s] == 1, part, 0.0)
        sum_ref[d] = total.astype(sum_ref.dtype)
        return carry

    lax.fori_loop(0, sum_ref.shape[0], one, jnp.int32(0), unroll=2)


def sum_pieces(later, live, pieces, count):
    shape = out((count, *pieces.shape[1:]), pieces.dtype)
    return run(
        sum_kernel,
        "sum_pieces",
        1,
        [smem(), smem(), None],
        [None],
        [shape],
        (later, live, pieces),
        cost(0, 1_100_000),
        free=(2,),
    )[0]


def route_kernel(begin_ref, bases_ref, routes_ref, picks_ref, sends_ref, ranks_ref):
    tokens = routes_ref.shape[1]
    expert_at = lax.broadcasted_iota(jnp.int32, (LANES, tokens), 0)
    hits = jnp.zeros((LANES, tokens), jnp.float32)
    for k in range(routes_ref.shape[0]):
        hits = hits + jnp.where(routes_ref[k : k + 1, :] == expert_at, 1.0, 0.0)
    row_at = lax.broadcasted_iota(jnp.int32, (tokens, tokens), 0)
    column_at = lax.broadcasted_iota(jnp.int32, (tokens, tokens), 1)
    before = jnp.where(row_at < column_at, 1.0, 0.0).astype(jnp.bfloat16)
    ranks = jnp.where(hits > 0.5, mm(hits.astype(jnp.bfloat16), before), -1.0)
    ranks_ref[...] = ranks
    slot_at = lax.broadcasted_iota(jnp.int32, (QUARTER, tokens), 0)
    own_at = (slot_at + begin_ref[0]).astype(jnp.float32)
    sent_at = [(slot_at + bases_ref[i]).astype(jnp.float32) for i in range(2)]
    for e in range(EXPERTS):
        here = slice(e * QUARTER, (e + 1) * QUARTER)
        rank_here = ranks[e : e + 1, :]
        picks_ref[here, :] = jnp.where(rank_here == own_at, 1.0, 0.0).astype(jnp.bfloat16)
        sends_ref[here, :] = jnp.where(rank_here == sent_at[e % 2], 1.0, 0.0).astype(jnp.bfloat16)


def route(begin, bases, routes_t):
    return run(
        route_kernel,
        "route",
        1,
        [smem(), smem(), None],
        [None, None, None],
        [
            out((SLOTS, BLOCK), jnp.bfloat16),
            out((SLOTS, BLOCK), jnp.bfloat16),
            out((LANES, BLOCK), jnp.float32),
        ],
        (begin, bases, routes_t),
        cost(100_000_000, 3_000_000),
        free=(2,),
    )


def padded_columns(rows_t, out_ref):
    zero = jnp.zeros((HEAD_DIM, rows_t.shape[1]), out_ref.dtype)
    for h in range(4):
        mine = rows_t[h * HEAD_DIM : (h + 1) * HEAD_DIM].astype(out_ref.dtype)
        at = (h // 2) * HEAD_DIM
        out_ref[h, pl.ds(at, HEAD_DIM), :] = mine
        out_ref[h, pl.ds(HEAD_DIM - at, HEAD_DIM), :] = zero


def padded_rows(rows, out_ref):
    n = rows.shape[0]
    lane = lax.broadcasted_iota(jnp.int32, (n, 128), 1)
    for h in range(4):
        pair = rows[:, (h // 2) * 128 : (h // 2) * 128 + 128].astype(jnp.float32)
        if h % 2 != h // 2:
            pair = pltpu.roll(pair, HEAD_DIM, 1)
        own = (lane < HEAD_DIM) if h // 2 == 0 else (lane >= HEAD_DIM)
        out_ref[pl.ds(h * n, n), :] = jnp.where(own, pair, 0.0).astype(out_ref.dtype)


def attend_block(key_rows, value_rows, first, qpad_ref, max_ref, sum_ref, out_t_ref):
    half = BLOCK // 2
    for h in range(4):
        group = (h // 2) * HEAD_DIM
        for t in range(2):
            cols = slice(t * half, (t + 1) * half)
            rows = half if first and t == 0 else BLOCK
            scores = mm(key_rows[:rows], qpad_ref[h, :, cols])
            if first:
                key_at = lax.broadcasted_iota(jnp.int32, scores.shape, 0)
                query_at = lax.broadcasted_iota(jnp.int32, scores.shape, 1) + t * half
                scores = jnp.where(key_at > query_at, masked_score, scores)
            new_max = jnp.max(scores, axis=0, keepdims=True)
            if not first:
                old_max = max_ref[h : h + 1, cols]
                new_max = jnp.maximum(new_max, old_max)
                shrink = jnp.exp(old_max - new_max)
            weights = jnp.exp(scores - new_max)
            total = jnp.sum(weights, axis=0, keepdims=True)
            part = mm(value_rows[:rows], weights.astype(jnp.bfloat16), TN)[group : group + HEAD_DIM]
            mine = pl.ds(h * HEAD_DIM, HEAD_DIM)
            if not first:
                total = total + sum_ref[h : h + 1, cols] * shrink
                part = part + out_t_ref[mine, cols] * shrink
            max_ref[h : h + 1, cols] = new_max
            sum_ref[h : h + 1, cols] = total
            out_t_ref[mine, cols] = part


def attend_own_kernel(q_ref, own_ref, qpad_ref, max_ref, sum_ref, out_t_ref):
    padded_columns(jnp.transpose(q_ref[...].astype(jnp.float32) * score_mult), qpad_ref)
    max_ref[...] = jnp.zeros_like(max_ref)
    sum_ref[...] = jnp.ones_like(sum_ref)
    attend_block(own_ref[:, :LANES], own_ref[:, LANES:], True, qpad_ref, max_ref, sum_ref, out_t_ref)


def attend_own(queries, own_kv):
    return pl.pallas_call(
        attend_own_kernel,
        name="attend_own",
        in_specs=[vmem()] * 2,
        out_specs=[vmem()] * 4,
        out_shape=[
            out((4, LANES, BLOCK), jnp.bfloat16),
            out((8, BLOCK), jnp.float32),
            out((8, BLOCK), jnp.float32),
            out((SHARE, BLOCK), jnp.float32),
        ],
        compiler_params=pltpu.CompilerParams(vmem_limit_bytes=36 << 20),
        cost_estimate=cost(1_000_000_000, 2_000_000, 600_000),
    )(queries, own_kv)


def attend_kernel(
    reach_ref, qpad_ref, max0_ref, sum0_ref, out0_ref, prev_ref, att_ref, out_t_ref, lse_ref, max_ref, sum_ref
):
    max_ref[...] = max0_ref[...]
    sum_ref[...] = sum0_ref[...]
    out_t_ref[...] = out0_ref[...]

    @pl.loop(1, reach_ref[0] + 1)
    def _(step):
        rows = prev_ref[:, pl.ds(step - 1, 1)].reshape(BLOCK, SHARE)
        attend_block(rows[:, :LANES], rows[:, LANES:], False, qpad_ref, max_ref, sum_ref, out_t_ref)

    lse_ref[...] = max_ref[...] + jnp.log(sum_ref[...])
    for h in range(4):
        mine = pl.ds(h * HEAD_DIM, HEAD_DIM)
        out_t_ref[mine, :] = out_t_ref[mine, :] / sum_ref[h : h + 1, :]
    att_ref[...] = jnp.transpose(out_t_ref[...]).astype(jnp.bfloat16)


def attend(reach, begun, earlier):
    return run(
        attend_kernel,
        "attend",
        1,
        [smem()] + [vmem()] * 5,
        [None] * 3,
        [
            out((BLOCK, SHARE), jnp.bfloat16),
            out((SHARE, BLOCK), jnp.float32),
            out((8, BLOCK), jnp.float32),
        ],
        (reach, *begun, earlier),
        cost(4_000_000_000, 3_000_000, 3_000_000),
        [pltpu.VMEM((8, BLOCK), jnp.float32), pltpu.VMEM((8, BLOCK), jnp.float32)],
        limit=36,
    )


def attend_back_kernel(
    reach_ref, q_ref, qpad_ref, own_ref, prev_ref, grad_ref, grad_t_ref, out_t_ref, lse_ref, cos_ref, sin_ref,
    qgrad_ref, own_grad_ref, prev_grad_ref,
    gpad_ref, qrows_ref, grows_ref, ds_ref, p_ref, delta_ref, dq_ref,
):
    half = BLOCK // 2
    q_scaled = q_ref[...].astype(jnp.float32) * score_mult
    padded_rows(q_scaled, qrows_ref)
    padded_columns(grad_t_ref[...], gpad_ref)
    padded_rows(grad_ref[...], grows_ref)
    both = grad_t_ref[...].astype(jnp.float32) * out_t_ref[...]
    for h in range(4):
        delta_ref[h : h + 1, :] = jnp.sum(
            both[h * HEAD_DIM : (h + 1) * HEAD_DIM], axis=0, keepdims=True
        )


    def block(key_rows, value_rows, first):
        for h in range(4):
            for t in range(2):
                cols = slice(t * half, (t + 1) * half)
                wide = slice(h * BLOCK + t * half, h * BLOCK + (t + 1) * half)
                rows = half if first and t == 0 else BLOCK
                scores = mm(key_rows[:rows], qpad_ref[h, :, cols])
                weights = jnp.exp(scores - lse_ref[h : h + 1, cols])
                if first:
                    key_at = lax.broadcasted_iota(jnp.int32, scores.shape, 0)
                    query_at = lax.broadcasted_iota(jnp.int32, scores.shape, 1) + t * half
                    weights = jnp.where(key_at > query_at, 0.0, weights)
                weight_grad = mm(value_rows[:rows], gpad_ref[h, :, cols])
                score_grad = weights * (weight_grad - delta_ref[h : h + 1, cols])
                p_ref[:rows, wide] = weights.astype(jnp.bfloat16)
                ds_ref[:rows, wide] = score_grad.astype(jnp.bfloat16)
                if rows < BLOCK:
                    p_ref[rows:, wide] = jnp.zeros((BLOCK - rows, half), jnp.bfloat16)
                    ds_ref[rows:, wide] = jnp.zeros((BLOCK - rows, half), jnp.bfloat16)
        key_grad = mm(ds_ref[...], qrows_ref[...])
        value_grad = mm(p_ref[...], grows_ref[...])
        for h in range(4):
            group = (h // 2) * HEAD_DIM
            mine = pl.ds(h * HEAD_DIM, HEAD_DIM)
            part = mm(key_rows, ds_ref[:, h * BLOCK : (h + 1) * BLOCK], TN)[group : group + HEAD_DIM]
            dq_ref[mine, :] = part if first else dq_ref[mine, :] + part
        return key_grad, value_grad

    key_grad, value_grad = block(own_ref[:, :LANES], own_ref[:, LANES:], True)
    own_grad_ref[:, :LANES] = key_grad
    own_grad_ref[:, LANES:] = value_grad

    @pl.loop(1, reach_ref[0] + 1)
    def _(step):
        rows = prev_ref[:, pl.ds(step - 1, 1)].reshape(BLOCK, SHARE)
        key_grad, value_grad = block(rows[:, :LANES], rows[:, LANES:], False)
        parts = prev_grad_ref.shape[0]
        shape = (parts, 1, BLOCK // parts, LANES)
        prev_grad_ref[:, pl.ds(step - 1, 1), :, :LANES] = key_grad.astype(jnp.bfloat16).reshape(shape)
        prev_grad_ref[:, pl.ds(step - 1, 1), :, LANES:] = value_grad.astype(jnp.bfloat16).reshape(shape)

    query_grad = jnp.transpose(dq_ref[...]) * score_mult
    for i in range(0, SHARE, LANES):
        qgrad_ref[:, i : i + LANES] = turned(
            query_grad[:, i : i + LANES], cos_ref[...], sin_ref[...], back=True
        ).astype(jnp.bfloat16)


def attend_back(reach, queries, padded, own_kv, earlier, grad, grad_t, out_t, lse, cosine, signed_sine):
    return run(
        attend_back_kernel,
        "attend_back",
        1,
        [smem()] + [vmem()] * 10,
        [None] * 3,
        [
            out((BLOCK, SHARE), jnp.bfloat16),
            out((BLOCK, SHARE), jnp.float32),
            out(earlier.shape, jnp.bfloat16),
        ],
        (reach, queries, padded, own_kv, earlier, grad, grad_t, out_t, lse, cosine, signed_sine),
        cost(12_000_000_000, 5_000_000, 3_000_000),
        [
            pltpu.VMEM((4, LANES, BLOCK), jnp.bfloat16),
            pltpu.VMEM((4 * BLOCK, LANES), jnp.bfloat16),
            pltpu.VMEM((4 * BLOCK, LANES), jnp.bfloat16),
            pltpu.VMEM((BLOCK, 4 * BLOCK), jnp.bfloat16),
            pltpu.VMEM((BLOCK, 4 * BLOCK), jnp.bfloat16),
            pltpu.VMEM((8, BLOCK), jnp.float32),
            pltpu.VMEM((SHARE, BLOCK), jnp.float32),
        ],
        limit=36,
    )


def residual_kernel(
    a0, a1, a2, a3, w0, w1, w2, w3, x_ref, gain_ref, router_ref, ranks_ref, picks_ref,
    residual_ref, moe_ref, gates_ref, rows_ref, held_ref,
):
    step = pl.program_id(0)
    tile = x_ref.shape[0]

    @pl.when(step < BLOCK // tile)
    def _():
        branch = mm(a0[...], w0[...])
        for a, w in ((a1, w1), (a2, w2), (a3, w3)):
            branch = branch + mm(a[...], w[...])
        residual = x_ref[...].astype(jnp.float32) + residual_mult * branch
        residual_ref[...] = residual
        scale = lax.rsqrt(jnp.mean(residual * residual, axis=1, keepdims=True) + epsilon)
        moe_in = (residual * scale * gain_ref[...]).astype(jnp.bfloat16)
        moe_ref[:, :WIDTH] = moe_in
        logits = mm(router_ref[...], moe_in, NT)
        chosen = ranks_ref[...] >= 0.0
        kept = jnp.where(chosen, logits, masked_score)
        top = jnp.max(kept, axis=0, keepdims=True)
        raised = jnp.where(chosen, jnp.exp(kept - top), 0.0)
        gates = raised / jnp.sum(raised, axis=0, keepdims=True)
        gates_ref[...] = gates
        low = (residual_mult * jnp.transpose(gates)).astype(jnp.bfloat16)
        moe_ref[:, WIDTH:] = low
        held_ref[pl.ds(step * tile, tile), :WIDTH] = moe_in
        held_ref[pl.ds(step * tile, tile), WIDTH:] = low

    @pl.when(step >= BLOCK // tile)
    def _():
        rows_ref[...] = mm(picks_ref[...], held_ref[...]).astype(jnp.bfloat16)


def residual_step(attended, w_out, x, gain, router_t, ranks, picks):
    tile = 256
    first = BLOCK // tile
    slot_tile = SLOTS // 2

    def early(rows, width):
        return pl.BlockSpec((rows, width), lambda i: (jnp.minimum(i, first - 1), 0))

    def late(rows, width):
        return pl.BlockSpec((rows, width), lambda i: (jnp.maximum(i - first, 0), 0))

    by_columns = pl.BlockSpec((LANES, tile), lambda i: (0, jnp.minimum(i, first - 1)))
    return run(
        residual_kernel,
        "residual_step",
        first + 2,
        [early(tile, SHARE)] * 4
        + [None] * 4
        + [early(tile, WIDTH), None, None, by_columns, late(slot_tile, BLOCK)],
        [early(tile, WIDTH), early(tile, WIDTH + LANES), by_columns, late(slot_tile, WIDTH + LANES)],
        [
            out((BLOCK, WIDTH), jnp.float32),
            out((BLOCK, WIDTH + LANES), jnp.bfloat16),
            out((LANES, BLOCK), jnp.float32),
            out((SLOTS, WIDTH + LANES), jnp.bfloat16),
        ],
        (*attended, *w_out, x, gain, router_t, ranks, picks),
        cost(2_700_000_000, 12_000_000, 70_000),
        [pltpu.VMEM((BLOCK, WIDTH + LANES), jnp.bfloat16)],
        free=(1, 2, 3, 5, 6, 7, 10),
    )


def mix_kernel(begin_ref, ranks_ref, moe_ref, mix_ref):
    ranks = jnp.transpose(ranks_ref[...]).astype(jnp.bfloat16)
    gates = moe_ref[:, WIDTH:]
    width = 640
    for at in range(0, SLOTS, width):
        expert_at = lax.broadcasted_iota(jnp.int32, (LANES, width), 0)
        first = expert_at * QUARTER - at
        slot_at = lax.broadcasted_iota(jnp.int32, (LANES, width), 1)
        inside = jnp.logical_and(slot_at >= first, slot_at < first + QUARTER)
        spread = jnp.where(inside, 1.0, 0.0).astype(jnp.bfloat16)
        within = jnp.sum(jnp.where(inside, slot_at - first, 0), axis=0, keepdims=True) + begin_ref[0]
        hit = mm(ranks, spread) == within.astype(jnp.float32)
        mix_ref[:, at : at + width] = jnp.where(hit, mm(gates, spread), 0.0).astype(jnp.bfloat16)


def mix_weights(begin, ranks, moe_cat):
    return run(
        mix_kernel,
        "mix_weights",
        1,
        [smem(), None, None],
        [None],
        [out((BLOCK, SLOTS), jnp.bfloat16)],
        (begin, ranks, moe_cat),
        cost(350_000_000, 3_000_000),
    )[0]


def expert_kernel(lane_ref, x_ref, grad_ref, *refs):
    downs, gate_refs, up_refs = refs[:4], refs[4:8], refs[8:12]
    row_ref, hidden_ref, units_ref = refs[12:]
    rows = row_ref.shape[0]
    here = pl.ds(pl.program_id(0) * rows, rows)
    lane = lax.broadcasted_iota(jnp.int32, (rows, LANES), 1) == lane_ref[0]
    gate = jnp.sum(
        jnp.where(lane, x_ref[here, WIDTH:].astype(jnp.float32), 0.0), axis=1, keepdims=True
    )
    x = x_ref[here, :WIDTH]
    gates, ups, sigmoids = [], [], []
    for j in range(4):
        pre = mm(x, jnp.concatenate([gate_refs[j][...], up_refs[j][...]], axis=1))
        gate_pre, up_pre = pre[:, :LANES], pre[:, LANES:]
        gates.append(gate_pre)
        ups.append(up_pre)
        sigmoids.append(1.0 / (1.0 + jnp.exp(-gate_pre)))
    down = jnp.concatenate([p[...] for p in downs], axis=0)
    hidden_grad = mm(grad_ref[...], down, NT)
    gate_grad = jnp.zeros((rows, LANES), jnp.float32)
    row = None
    for j in range(4):
        part = hidden_grad[:, j * LANES : (j + 1) * LANES]
        silu = gates[j] * sigmoids[j]
        hidden = (silu * ups[j]).astype(jnp.bfloat16)
        hidden_ref[:, j * LANES : (j + 1) * LANES] = hidden
        gate_grad = gate_grad + hidden.astype(jnp.float32) * part
        gate_pre_grad = part * ups[j] * sigmoids[j] * (1.0 + gates[j] * (1.0 - sigmoids[j]))
        up_pre_grad = part * silu
        units_ref[:, j * SHARE : j * SHARE + LANES] = (gate_pre_grad * gate).astype(jnp.bfloat16)
        units_ref[:, j * SHARE + LANES : (j + 1) * SHARE] = (up_pre_grad * gate).astype(jnp.bfloat16)
        both = jnp.concatenate([gate_pre_grad, up_pre_grad], axis=1).astype(jnp.bfloat16)
        term = mm(both, jnp.concatenate([gate_refs[j][...], up_refs[j][...]], axis=1), NT)
        row = term if row is None else row + term
    row_ref[:, :WIDTH] = row.astype(jnp.bfloat16)
    gate_grad = jnp.sum(gate_grad, axis=1, keepdims=True)
    row_ref[:, WIDTH:] = jnp.where(lane, gate_grad, 0.0).astype(jnp.bfloat16)


def output_kernel(hidden_ref, d0, d1, d2, d3, out_ref):
    down = jnp.concatenate([p[...] for p in (d0, d1, d2, d3)], axis=0)
    out_ref[...] = mm(hidden_ref[...], down).astype(jnp.bfloat16)


def output_rows(hidden, downs):
    tile = 320
    return run(
        output_kernel,
        "output_rows",
        SLOTS // tile,
        [tiles(tile, 512)] + [None] * 4,
        [tiles(tile, WIDTH)],
        [out((SLOTS, WIDTH), jnp.bfloat16)],
        (hidden, *downs),
        cost(1_300_000_000, 5_000_000),
    )[0]


def expert_step(lane, x, grad, downs, gates, ups):
    tile = 320
    return run(
        expert_kernel,
        "expert_step",
        SLOTS // tile,
        [smem(), vmem(), tiles(tile, WIDTH)] + [None] * 12,
        [tiles(tile, WIDTH + LANES), tiles(tile, 512), tiles(tile, WIDTH)],
        [
            out((SLOTS, WIDTH + LANES), jnp.bfloat16),
            out((SLOTS, 512), jnp.bfloat16),
            out((SLOTS, WIDTH), jnp.bfloat16),
        ],
        (lane, x, grad, *downs, *gates, *ups),
        cost(6_700_000_000, 15_000_000, 700_000),
        limit=40,
    )


def unit_grads_kernel(lane_ref, x_ref, grad_ref, hidden_ref, units_ref, keep_ref, send_ref, turned_ref, gate_ref):
    step = pl.program_id(0)

    @pl.when(step == 0)
    def _():
        for k in range(4):
            columns = slice(k * SHARE, (k + 1) * SHARE)
            turned_ref[columns, :] = jnp.transpose(x_ref[:, columns])
        lane = lax.broadcasted_iota(jnp.int32, (SLOTS, LANES), 1) == lane_ref[0]
        gate = jnp.where(lane, x_ref[:, WIDTH:].astype(jnp.float32), 0.0)
        gate_ref[...] = jnp.broadcast_to(jnp.sum(gate, axis=1, keepdims=True), (SLOTS, LANES))

    def write(to_ref):
        scaled = (hidden_ref[...].astype(jnp.float32) * gate_ref[...]).astype(jnp.bfloat16)
        to_ref[0, :LANES, :] = mm(scaled, grad_ref[...], TN).astype(jnp.bfloat16)
        for k in range(4):
            columns = slice(k * SHARE, (k + 1) * SHARE)
            to_ref[0, LANES:, columns] = mm(turned_ref[columns, :], units_ref[...]).astype(jnp.bfloat16)

    @pl.when(step < 2)
    def _():
        write(keep_ref)

    @pl.when(step >= 2)
    def _():
        write(send_ref)


def unit_grads(lane, x, grad, hidden, units):
    rows = SHARE + LANES

    def share_of(i):
        return jnp.where(i < 2, 2 * i, 2 * i - 3)

    return run(
        unit_grads_kernel,
        "unit_grads",
        4,
        [
            smem(),
            vmem(),
            None,
            pl.BlockSpec((SLOTS, LANES), lambda i: (0, share_of(i))),
            pl.BlockSpec((SLOTS, SHARE), lambda i: (0, share_of(i))),
        ],
        [
            pl.BlockSpec((1, rows, WIDTH), lambda i: (jnp.minimum(i, 1), 0, 0)),
            pl.BlockSpec((1, rows, WIDTH), lambda i: (jnp.maximum(i - 2, 0), 0, 0)),
        ],
        [out((2, rows, WIDTH), jnp.bfloat16), out((2, rows, WIDTH), jnp.bfloat16)],
        (lane, x, grad, hidden, units),
        cost(4_000_000_000, 12_000_000),
        [pltpu.VMEM((WIDTH, SLOTS), jnp.bfloat16), pltpu.VMEM((SLOTS, LANES), jnp.float32)],
        limit=36,
    )


def unit_finish_kernel(mine_ref, first_ref, second_ref, third_ref, gate_ref, up_ref, down_ref):
    got = jnp.concatenate([first_ref[...], second_ref[...], third_ref[...]], axis=0)
    total = mine_ref[0] + got.astype(jnp.float32)
    down_ref[0] = total[:LANES, :]
    for k in range(4):
        rows = slice(k * SHARE, (k + 1) * SHARE)
        gate_ref[0, rows, :] = total[LANES:, k * SHARE : k * SHARE + LANES]
        up_ref[0, rows, :] = total[LANES:, k * SHARE + LANES : (k + 1) * SHARE]


def unit_finish(mine, first, second, third):
    return run(
        unit_finish_kernel,
        "unit_finish",
        1,
        [once(1, PACKED, WIDTH), None, None, None],
        [None] * 3,
        [
            out((1, WIDTH, LANES), jnp.float32),
            out((1, WIDTH, LANES), jnp.float32),
            out((1, LANES, WIDTH), jnp.float32),
        ],
        (mine, first, second, third),
        cost(1_000_000, 3_000_000),
        free=(0, 1, 2, 3),
    )


def home_kernel(rank_ref, mix_ref, rows_ref, keep_ref, send_ref):
    rank = rank_ref[0]
    extra = rows_ref.shape[1] > WIDTH
    for j in range(4):
        at = pl.multiple_of(jnp.bitwise_xor(rank, j) * SHARE, SHARE)
        total = mm(mix_ref[...], rows_ref[:, pl.ds(at, SHARE)])
        to_ref = send_ref if j % 2 else keep_ref
        to_ref[(j // 2) * BLOCK : (j // 2 + 1) * BLOCK, :] = total.astype(to_ref.dtype)
    if extra:
        gate_grads = jnp.transpose(mm(mix_ref[...], rows_ref[:, WIDTH:]))[:EXPERTS]
        for to_ref in (keep_ref, send_ref):
            for i in range(2):
                at = 2 * BLOCK + i * EXPERTS
                to_ref[at : at + EXPERTS, :] = gate_grads[:, i * SHARE : (i + 1) * SHARE].astype(
                    to_ref.dtype
                )


def sum_home(rank, mix, rows):
    height = 2 * BLOCK + (2 * EXPERTS if rows.shape[1] > WIDTH else 0)
    return run(
        home_kernel,
        "sum_home",
        1,
        [smem(), None, vmem()],
        [None] * 2,
        [out((height, SHARE), jnp.float32), out((height, SHARE), jnp.bfloat16)],
        (rank, mix, rows),
        cost(1_500_000_000, 6_000_000),
        limit=36,
    )


def swap_kernel(mine_ref, got_ref, total_ref):
    mine, got = mine_ref, got_ref
    half = BLOCK
    total_ref[:half] = (mine[:half] + got[half : 2 * half].astype(jnp.float32)).astype(total_ref.dtype)
    total_ref[half : 2 * half] = (
        mine[half : 2 * half] + got[:half].astype(jnp.float32)
    ).astype(total_ref.dtype)
    total_ref[2 * half :] = (mine[2 * half :] + got[2 * half :].astype(jnp.float32)).astype(
        total_ref.dtype
    )


def swap_sum(mine, got):
    return run(
        swap_kernel,
        "swap_sum",
        1,
        [None] * 2,
        [None],
        [out(mine.shape, jnp.bfloat16)],
        (mine, got),
        cost(1_000_000, 2_500_000),
        free=(0, 1),
    )[0]


def norm_back_kernel(
    rank_ref, g0, g2, g1, g3, z_ref, gates_ref, residual_ref, gain_ref, router_ref, grad_ref, w_ref,
    low_ref, logit_ref, own_ref, att_ref, att_t_ref, gain_grad_ref, u_ref,
):
    rank = rank_ref[0]
    for flip, part in enumerate((g0, g1, g2, g3)):
        at = pl.multiple_of(jnp.bitwise_xor(rank, flip) * SHARE, SHARE)
        u_ref[:, pl.ds(at, SHARE)] = part[...].astype(jnp.float32)
    weighted_grads = z_ref[...].astype(jnp.float32)
    gates = gates_ref[:EXPERTS, :]
    inner = jnp.sum(weighted_grads, axis=0, keepdims=True)
    logit_grad = (weighted_grads - gates * inner).astype(jnp.bfloat16)
    logit_ref[...] = logit_grad
    u = u_ref[...] + mm(logit_grad, router_ref[:EXPERTS, :], TN)
    v = residual_ref[...]
    scale = lax.rsqrt(jnp.mean(v * v, axis=1, keepdims=True) + epsilon)
    weighted = u * gain_ref[...]
    mean = jnp.mean(weighted * v, axis=1, keepdims=True)
    total = grad_ref[...].astype(jnp.float32) + scale * weighted - v * (scale * scale * scale * mean)

    @pl.when(pl.program_id(0) == 0)
    def _():
        gain_grad_ref[...] = jnp.zeros_like(gain_grad_ref)

    gain_grad_ref[0:1, :] += jnp.sum(u * v * scale, axis=0, keepdims=True)
    low = (residual_mult * total).astype(jnp.bfloat16)
    low_ref[...] = low
    u_ref[...] = total
    own_ref[...] = u_ref[:, pl.ds(pl.multiple_of(rank * SHARE, SHARE), SHARE)]
    att_ref[...] = mm(low, w_ref[...], NT).astype(jnp.bfloat16)
    att_t_ref[...] = mm(w_ref[...], low, NT).astype(jnp.bfloat16)


def norm_back_step(rank, mine, theirs, gates, residual, gain, router_t, out_grad, w_out):
    tile = 256
    by_columns = pl.BlockSpec((EXPERTS, tile), lambda i: (0, i))
    return run(
        norm_back_kernel,
        "norm_back_step",
        BLOCK // tile,
        [smem()]
        + [tiles(tile, SHARE), tiles(tile, SHARE, BLOCK // tile)] * 2
        + [
            tiles(EXPERTS, SHARE, 2 * BLOCK // EXPERTS),
            pl.BlockSpec((LANES, tile), lambda i: (0, i)),
            tiles(tile, WIDTH),
            None,
            None,
            tiles(tile, WIDTH),
            None,
        ],
        [
            tiles(tile, WIDTH),
            by_columns,
            tiles(tile, SHARE),
            tiles(tile, SHARE),
            pl.BlockSpec((SHARE, tile), lambda i: (0, i)),
            fixed(8, WIDTH),
        ],
        [
            out((BLOCK, WIDTH), jnp.bfloat16),
            out((EXPERTS, BLOCK), jnp.bfloat16),
            out((BLOCK, SHARE), jnp.float32),
            out((BLOCK, SHARE), jnp.bfloat16),
            out((SHARE, BLOCK), jnp.bfloat16),
            out((8, WIDTH), jnp.float32),
        ],
        (rank, mine, mine, theirs, theirs, mine, gates, residual, gain, router_t, out_grad, w_out),
        cost(700_000_000, 9_000_000, 512),
        [pltpu.VMEM((tile, WIDTH), jnp.float32)],
        free=(3, 4, 9),
    )


def dense_grads_kernel(low_ref, attended_ref, normed_ref, qgrad_ref, logit_ref, moe_ref, gain_ref, made_ref):
    made_ref[:, :SHARE] = mm(low_ref[...], attended_ref[...], TN).astype(jnp.bfloat16)
    made_ref[:, SHARE : 2 * SHARE] = mm(normed_ref[...], qgrad_ref[...], TN).astype(jnp.bfloat16)
    router = mm(logit_ref[...], moe_ref[:, :WIDTH])
    stacked = jnp.concatenate(
        [router, gain_ref[...], jnp.zeros((LANES - EXPERTS - 8, WIDTH), jnp.float32)], axis=0
    )
    made_ref[:, 2 * SHARE :] = jnp.transpose(stacked).astype(jnp.bfloat16)


def dense_grads(low, attended, normed, qgrad, logit, moe_cat, gain_grad):
    return run(
        dense_grads_kernel,
        "dense_grads",
        1,
        [None] * 7,
        [None],
        [out((WIDTH, 2 * SHARE + LANES), jnp.bfloat16)],
        (low, attended, normed, qgrad, logit, moe_cat, gain_grad),
        cost(600_000_000, 6_000_000),
    )[0]


def last_grads_kernel(
    rank_ref, own_ref, home_ref, qgrad_ref, normed_ref, x_ref, wq_ref, wk_ref, wv_ref, cos_ref, sin_ref, made_ref,
    gain_ref, all_ref, keep_ref, send_ref, inner_ref, part_ref,
):
    rank = rank_ref[0]
    kv = own_ref[...] + home_ref[...].astype(jnp.float32)
    key_grad = turned(kv[:, :LANES], cos_ref[...], sin_ref[...], back=True).astype(jnp.bfloat16)
    value_grad = kv[:, LANES:].astype(jnp.bfloat16)
    both = jnp.concatenate([key_grad, value_grad], axis=1)
    all_ref[:, : 2 * SHARE] = made_ref[:, : 2 * SHARE]
    all_ref[:, 2 * SHARE : 3 * SHARE] = mm(normed_ref[...], both, TN).astype(jnp.bfloat16)
    gain = jnp.zeros((1, WIDTH), jnp.float32)
    tile = 128
    for i in range(0, BLOCK, tile):
        rows = slice(i, i + tile)
        part = mm(qgrad_ref[rows, :], wq_ref[...], NT)
        part = part + mm(key_grad[rows], wk_ref[...], NT) + mm(value_grad[rows], wv_ref[...], NT)
        x = x_ref[rows, :].astype(jnp.float32)
        scale = lax.rsqrt(jnp.mean(x * x, axis=1, keepdims=True) + epsilon)
        along = part * x
        gain = gain + jnp.sum(along * scale, axis=0, keepdims=True)
        inner = jnp.sum(along * gain_ref[...], axis=1, keepdims=True)
        inner_ref[:, rows] = jnp.transpose(jnp.broadcast_to(inner, (tile, LANES)))[:8]
        part_ref[rows, :] = part
    for j in range(4):
        at = pl.multiple_of(jnp.bitwise_xor(rank, j) * SHARE, SHARE)
        to_ref = send_ref if j % 2 else keep_ref
        to_ref[(j // 2) * BLOCK : (j // 2 + 1) * BLOCK, :] = part_ref[:, pl.ds(at, SHARE)].astype(to_ref.dtype)
    lane = lax.broadcasted_iota(jnp.int32, (WIDTH, LANES), 1)
    column = jnp.transpose(jnp.broadcast_to(gain, (LANES, WIDTH)))
    rest = jnp.where(lane == EXPERTS + 8, column, made_ref[:, 2 * SHARE :].astype(jnp.float32))
    all_ref[:, 3 * SHARE :] = rest.astype(jnp.bfloat16)


def last_grads(rank, own, home, qgrad, normed, x, w_query, w_key, w_value, cosine, sine, made, gain):
    return run(
        last_grads_kernel,
        "last_grads",
        1,
        [smem()] + [None] * 12,
        [None] * 4,
        [
            out((WIDTH, 3 * SHARE + LANES), jnp.bfloat16),
            out((2 * BLOCK, SHARE), jnp.float32),
            out((2 * BLOCK, SHARE), jnp.bfloat16),
            out((8, BLOCK), jnp.float32),
        ],
        (rank, own, home, qgrad, normed, x, w_query, w_key, w_value, cosine, sine, made, gain),
        cost(1_000_000_000, 8_000_000, 512),
        [pltpu.VMEM((BLOCK, WIDTH), jnp.float32)],
        free=(2,),
    )


def input_finish_kernel(
    rank_ref, near_ref, far_ref, i0, i1, i2, i3, x_ref, gain_ref, residual_ref, made_ref
):
    mine = pl.ds(pl.multiple_of(rank_ref[0] * SHARE, SHARE), SHARE)
    x = x_ref[...].astype(jnp.float32)
    scale = lax.rsqrt(jnp.mean(x * x, axis=1, keepdims=True) + epsilon)
    inner = (i0[...] + i1[...] + i2[...] + i3[...]) * (1.0 / WIDTH)
    inner = jnp.transpose(jnp.broadcast_to(inner[:1], (LANES, BLOCK)))[:, :1]
    weighted = (near_ref[...] + far_ref[...].astype(jnp.float32)) * gain_ref[:, mine]
    x_own = x_ref[:, mine].astype(jnp.float32)
    made_ref[...] = residual_ref[...] + scale * weighted - x_own * (scale * scale * scale * inner)


def input_finish(rank, near, far, inners, x, gain, residual):
    return run(
        input_finish_kernel,
        "input_finish",
        1,
        [smem(), once(BLOCK, SHARE), None] + [None] * 7,
        [None],
        [out((BLOCK, SHARE), jnp.float32)],
        (rank, near, far, *inners, x, gain, residual),
        cost(3_000_000, 3_000_000, 512),
        free=(1, 2, 3, 4, 5, 6),
    )[0]


def per_device(
    hidden_in,
    lengths,
    block_order,
    routes,
    norm_gain_attn,
    w_query,
    w_key,
    w_value,
    w_out,
    norm_gain_moe,
    w_router,
    w_gate,
    w_up,
    w_down,
    out_grad,
):
    dp_count = block_order.shape[0]
    mp_rank = lax.axis_index("mp").astype(jnp.int32)
    column_start = mp_rank * SHARE
    piece = BLOCK // dp_count
    steps = MAXLEN // BLOCK - 1
    rank = mp_rank.reshape(1)
    lane = lax.axis_index("dp").astype(jnp.int32).reshape(1)
    begin = rank * QUARTER
    other = jnp.bitwise_xor(rank, 2 * (1 - jnp.bitwise_and(rank, 1)))
    parity = jnp.bitwise_and(lane, 1)
    bases = jnp.where(jnp.arange(2, dtype=jnp.int32) == parity, rank, other) * QUARTER
    gain_attn = norm_gain_attn[None, :]
    gain_moe = norm_gain_moe[None, :]
    router_t = jnp.pad(w_router.T, ((0, LANES - EXPERTS), (0, 0)))

    far_out = peer(w_out, 2)
    cores = ([(0, 2), (2, 0)], [(1, 3), (3, 1)])
    experts = (w_down[0], w_gate[0], w_up[0])
    far_early = [lax.ppermute(w, "mp", cores[0]) for w in experts]

    normed, key_value, cosine, sine, reach, wanted, later, live = project(
        lengths, block_order, lane, hidden_in, gain_attn, w_key, w_value
    )
    queries = project_queries(normed, w_query, cosine, sine)
    pieces = to_all(key_value.reshape(dp_count, piece, SHARE))
    picks, sends, ranks = route(begin, bases, after(routes.T, key_value))
    begun = attend_own(queries, after(key_value, picks))
    picked = pick_pieces(wanted, after(pieces, far_out, *far_early, queries, picks))
    earlier = to_all(picked.reshape(dp_count, steps * piece, SHARE))
    earlier = earlier.reshape(dp_count, steps, piece, SHARE)

    outs = [w_out, peer(after(w_out, picked), 1), far_out, peer(far_out, 1)]

    grad_rows = jnp.dot(picks, after(out_grad, picked), preferred_element_type=jnp.bfloat16)
    grad_arrived = to_experts(after(grad_rows, earlier, begun[1]).reshape(EXPERTS, QUARTER, WIDTH))
    attended, attended_t, lse = attend(reach, begun, earlier)
    far = peer(attended, 2)
    residual, moe_cat, gates, moe_rows = residual_step(
        [attended, peer(attended, 1), far, peer(far, 1)],
        outs,
        hidden_in,
        gain_moe,
        router_t,
        ranks,
        sends,
    )
    late = [lax.ppermute(after(w, moe_rows), "mp", cores[1]) for w in experts]
    far = [a + b for a, b in zip(far_early, late)]
    own = [after(w, moe_rows) for w in experts]
    downs, gates_all, ups = [[w, peer(w, 1), v, peer(v, 1)] for w, v in zip(own, far)]
    grouped = to_experts(moe_rows.reshape(EXPERTS, QUARTER, -1), (1,)).reshape(SLOTS, -1)
    mix = mix_weights(begin, ranks, moe_cat)
    grouped_grad = grad_arrived.reshape(SLOTS, WIDTH)
    row_grad, hidden_units, unit_grad = expert_step(
        lane, grouped, grouped_grad, downs, gates_all, ups
    )
    row_home = to_experts(row_grad.reshape(dp_count, QUARTER, -1)).reshape(SLOTS, -1)
    rows_out = output_rows(hidden_units, downs)
    rows_home = to_experts(after(rows_out, row_home).reshape(dp_count, QUARTER, -1)).reshape(SLOTS, -1)

    unit_keep, unit_send = unit_grads(lane, grouped, grouped_grad, hidden_units, unit_grad)
    unit_near = unit_keep.astype(jnp.float32) + peer(unit_send, 1).astype(jnp.float32)
    unit_low = unit_near[1].astype(jnp.bfloat16)
    cut = PACKED // 2
    unit_far_a = peer(unit_low[:cut], 2)
    keep, send = sum_home(rank, after(mix, unit_far_a, rows_out), row_home)
    near = keep + peer(send, 1).astype(jnp.float32)
    mine = swap_sum(near, peer(near.astype(jnp.bfloat16), 2))
    theirs = peer(mine, 1)
    branch_grad, logit_grad, residual_grad, attended_grad, attended_grad_t, moe_gain = norm_back_step(
        rank, mine, theirs, gates, residual, gain_moe, router_t, out_grad, w_out
    )

    query_pre_grad, own_grads, later_grads = attend_back(
        reach,
        queries,
        begun[0],
        key_value,
        earlier,
        attended_grad,
        attended_grad_t,
        attended_t,
        lse,
        cosine,
        sine,
    )
    unit_far_b = peer(after(unit_low[cut:], later_grads), 2)
    unit_far_b = peer(after(unit_low[cut : cut + cut // 2], branch_grad), 2)
    later_pieces = to_all(after(later_grads, rows_home, unit_far_b).reshape(dp_count, steps * piece, SHARE))
    summed = sum_pieces(
        later, live, later_pieces.reshape(dp_count * steps, piece, SHARE), dp_count
    )
    kv_home = to_all(summed).reshape(BLOCK, SHARE)
    made = dense_grads(
        branch_grad, attended, normed, query_pre_grad, logit_grad, moe_cat, moe_gain
    )

    unit_far_c = peer(after(unit_low[cut + cut // 2 :], kv_home, made), 2)

    every, keep, send, inner = last_grads(
        rank,
        own_grads,
        kv_home,
        query_pre_grad,
        normed,
        hidden_in,
        w_query,
        w_key,
        w_value,
        cosine,
        sine,
        made,
        gain_attn,
    )
    near_norm = keep + peer(send, 1).astype(jnp.float32)
    far_norm = peer(near_norm[BLOCK:].astype(jnp.bfloat16), 2)
    inners = [inner] + [peer(inner, flip) for flip in (1, 2, 3)]
    every = after(every, unit_far_c)
    arrived = to_all(every.reshape(dp_count, WIDTH // dp_count, -1))
    keep, send = sum_home(rank, mix, after(rows_home, every))
    near_mix = keep + peer(send, 1).astype(jnp.float32)
    far_mix = peer(near_mix[BLOCK:].astype(jnp.bfloat16), 2)
    grad_w_gate, grad_w_up, grad_w_down = unit_finish(
        unit_near, unit_far_a, after(unit_far_b, every), unit_far_c
    )
    grad_hidden = input_finish(
        rank, near_norm, far_norm, inners, hidden_in, gain_attn, residual_grad
    )
    residual_cols = lax.dynamic_slice_in_dim(residual, column_start, SHARE, 1)
    mixture = near_mix[:BLOCK] + far_mix.astype(jnp.float32)
    out_hidden = (residual_cols + mixture).astype(jnp.bfloat16)

    dense = jnp.sum(after(arrived, grad_hidden, out_hidden).astype(jnp.float32), axis=0)
    at = 3 * SHARE
    attn_gain = dense[:, at + EXPERTS + 8]
    attn_gain = attn_gain + peer(attn_gain, 1) + peer(attn_gain, 2) + peer(attn_gain, 3)
    return (
        out_hidden,
        grad_hidden,
        dense[:, SHARE : 2 * SHARE],
        dense[:, 2 * SHARE : 2 * SHARE + LANES],
        dense[:, 2 * SHARE + LANES : at],
        dense[:, :SHARE].T,
        attn_gain,
        dense[:, at + EXPERTS],
        dense[:, at : at + EXPERTS],
        grad_w_gate,
        grad_w_up,
        grad_w_down,
    )


def solution(mesh):
    in_specs = (
        P("dp", None),
        P(),
        P(),
        P("dp", None),
        P(),
        P(None, "mp"),
        P(None, "mp"),
        P(None, "mp"),
        P("mp", None),
        P(),
        P(),
        P("dp", None, "mp"),
        P("dp", None, "mp"),
        P("dp", "mp", None),
        P("dp", None),
    )
    out_specs = (
        P("dp", "mp"),
        P("dp", "mp"),
        P("dp", "mp"),
        P("dp", "mp"),
        P("dp", "mp"),
        P("mp", "dp"),
        P("dp"),
        P("dp"),
        P("dp", None),
        P("dp", None, "mp"),
        P("dp", None, "mp"),
        P("dp", "mp", None),
    )
    return jax.shard_map(
        per_device, mesh=mesh, in_specs=in_specs, out_specs=out_specs, check_vma=False
    )
```

```python
import jax
import jax.numpy as jnp
import numpy as np
from jax import lax
from jax.experimental import pallas as pl
from jax.experimental.pallas import tpu as pltpu
from jax.sharding import PartitionSpec as P

HEAD_DIM = 64
EXPERTS = 32
BLOCK = 512
MAXLEN = 2048
CAP = 160
WIDTH = 1024
SHARE = 256
QUARTER = 40
SLOTS = 1280
LANES = 128
PACKED = 384

epsilon = 1e-06
residual_mult = 0.22
score_mult = 0.015625
rope_base = 10000.0
masked_score = -1e30

NN = (((1,), (0,)), ((), ()))
NT = (((1,), (1,)), ((), ()))
TN = (((0,), (0,)), ((), ()))


def mm(a, b, dims=NN):
    return lax.dot_general(a, b, dims, preferred_element_type=jnp.float32)


def to_all(x):
    return lax.all_to_all(x, "dp", 0, 0, tiled=True)


def crossed_groups(dp_count=32):
    groups = []
    for chip in range(2):
        for core in range(2):
            groups.append([i * 4 + (chip ^ (i & 1)) * 2 + core for i in range(dp_count)])
    return groups


def to_experts(x):
    return lax.all_to_all(
        x, ("dp", "mp"), 0, 0, axis_index_groups=crossed_groups(x.shape[0]), tiled=True
    )


def peer(x, flip):
    return lax.ppermute(x, "mp", [(i, i ^ flip) for i in range(4)])


def after(x, *others):
    return lax.optimization_barrier((x, *others))[0]


def vmem():
    return pl.BlockSpec(memory_space=pltpu.VMEM)


def smem():
    return pl.BlockSpec(memory_space=pltpu.SMEM)


def tiles(rows, width, row0=0):
    return pl.BlockSpec((rows, width), lambda i: (i + row0, 0))


def fixed(rows, width):
    return pl.BlockSpec((rows, width), lambda i: (0, 0))


def once(*shape):
    return pl.BlockSpec(shape, lambda i: (0,) * len(shape), pipeline_mode=pl.Buffered(1))


def run(kernel, name, steps, in_specs, out_specs, out_shape, args, estimate, scratch=(), free=(), limit=32):
    in_specs = [once(*a.shape) if s is None else s for s, a in zip(in_specs, args)]
    out_specs = [once(*o.shape) if s is None else s for s, o in zip(out_specs, out_shape)]
    args = [
        a
        if s.memory_space is not None or i in free
        else pltpu.with_memory_space_constraint(a, pltpu.HBM)
        for i, (s, a) in enumerate(zip(in_specs, args))
    ]
    out_shape = [
        o if s.memory_space == pltpu.SMEM else pltpu.HBM(o.shape, o.dtype)
        for s, o in zip(out_specs, out_shape)
    ]
    return pl.pallas_call(
        kernel,
        name=name,
        grid=(steps,),
        in_specs=in_specs,
        out_specs=out_specs,
        out_shape=out_shape,
        scratch_shapes=list(scratch),
        compiler_params=pltpu.CompilerParams(vmem_limit_bytes=limit << 20),
        cost_estimate=estimate,
    )(*args)


def out(shape, dtype):
    return jax.ShapeDtypeStruct(shape, dtype)


def cost(flops, moved, exps=0):
    return pl.CostEstimate(flops=flops, bytes_accessed=moved, transcendentals=exps)


def rope_constants():
    frequency = rope_base ** (-(np.arange(HEAD_DIM // 2, dtype=np.float64) * 2.0) / HEAD_DIM)
    wide = np.tile(frequency, 4)[None, :]
    made = []
    for count, apart in ((BLOCK // 16, 16), (16, 1), (8, BLOCK)):
        angles = np.arange(count, dtype=np.float64)[:, None] * apart * wide
        made += [np.cos(angles), np.sin(angles)]
    return [jnp.asarray(a.astype(np.float32)) for a in made]


def half_front(rows):
    lane = lax.broadcasted_iota(jnp.int32, (rows, LANES), 1)
    return (lane % HEAD_DIM) < HEAD_DIM // 2


def turned(chunk, cosine, signed_sine, back=False):
    partner = jnp.where(
        half_front(chunk.shape[0]), pltpu.roll(chunk, 96, 1), pltpu.roll(chunk, 32, 1)
    )
    if back:
        return chunk * cosine - partner * signed_sine
    return chunk * cosine + partner * signed_sine


def block_tables_in(lengths_ref, order_ref, rank_ref, offset_ref, inverse_ref, reach_ref, wanted_ref, later_ref, live_ref):
    count = order_ref.shape[0]
    steps = MAXLEN // BLOCK - 1

    def sequence(s, begin):
        def one(j, at):
            offset_ref[jnp.minimum(at, count - 1)] = j
            return at + 1

        return lax.fori_loop(0, lengths_ref[s], one, begin)

    lax.fori_loop(0, lengths_ref.shape[0], sequence, jnp.int32(0))

    def invert(d, carry):
        inverse_ref[order_ref[d]] = d
        return carry

    lax.fori_loop(0, count, invert, jnp.int32(0))
    reach_ref[0] = offset_ref[order_ref[rank_ref[0]]]

    def look(d, carry):
        packed = order_ref[d]
        for s in range(1, steps + 1):
            wanted_ref[d * steps + s - 1] = inverse_ref[jnp.maximum(packed - s, 0)]
            next_at = jnp.minimum(packed + s, count - 1)
            later_ref[d * steps + s - 1] = inverse_ref[next_at] * steps + s - 1
            is_live = jnp.logical_and(packed + s < count, offset_ref[next_at] >= s)
            live_ref[d * steps + s - 1] = jnp.where(is_live, 1, 0)
        return carry

    lax.fori_loop(0, count, look, jnp.int32(0))


def project_kernel(
    lengths_ref, order_ref, rank_ref, x_ref, gain_ref, wk_ref, wv_ref,
    cos16_ref, sin16_ref, cos1_ref, sin1_ref, cos0_ref, sin0_ref,
    normed_ref, kv_ref, cosine_ref, sine_ref, reach_ref, wanted_ref, later_ref, live_ref,
    offset_ref, inverse_ref,
):
    @pl.when(pl.program_id(0) == 0)
    def _():
        block_tables_in(
            lengths_ref, order_ref, rank_ref, offset_ref, inverse_ref, reach_ref, wanted_ref, later_ref, live_ref
        )

    x = x_ref[...].astype(jnp.float32)
    scale = lax.rsqrt(jnp.mean(x * x, axis=1, keepdims=True) + epsilon)
    normed = (x * scale * gain_ref[...]).astype(jnp.bfloat16)
    normed_ref[...] = normed
    at = reach_ref[0]
    cos0, sin0 = cos0_ref[pl.ds(at, 1), :], sin0_ref[pl.ds(at, 1), :]
    cos16 = cos16_ref[...] * cos0 - sin16_ref[...] * sin0
    sin16 = sin16_ref[...] * cos0 + cos16_ref[...] * sin0
    cos1, sin1 = cos1_ref[...][None], sin1_ref[...][None]
    cosine = (cos16[:, None, :] * cos1 - sin16[:, None, :] * sin1).reshape(x.shape[0], LANES)
    sine = (sin16[:, None, :] * cos1 + cos16[:, None, :] * sin1).reshape(x.shape[0], LANES)
    sine = jnp.where(half_front(x.shape[0]), -sine, sine)
    cosine_ref[...] = cosine
    sine_ref[...] = sine
    kv_ref[:, :LANES] = turned(mm(normed, wk_ref[...]), cosine, sine).astype(jnp.bfloat16)
    kv_ref[:, LANES:] = mm(normed, wv_ref[...]).astype(jnp.bfloat16)


def query_kernel(normed_ref, wq_ref, cosine_ref, sine_ref, q_ref):
    queries = mm(normed_ref[...], wq_ref[...])
    for i in range(0, SHARE, LANES):
        q_ref[:, i : i + LANES] = turned(
            queries[:, i : i + LANES], cosine_ref[...], sine_ref[...]
        ).astype(jnp.bfloat16)


def project_queries(normed, w_query, cosine, sine):
    tile = 256
    return run(
        query_kernel,
        "project_queries",
        BLOCK // tile,
        [tiles(tile, WIDTH), None, tiles(tile, LANES), tiles(tile, LANES)],
        [tiles(tile, SHARE)],
        [out((BLOCK, SHARE), jnp.bfloat16)],
        (normed, w_query, cosine, sine),
        cost(270_000_000, 2_500_000),
    )[0]


def project(lengths, order, rank, x, gain, w_key, w_value):
    tile = 256
    count = order.shape[0]
    steps = MAXLEN // BLOCK - 1
    bf16, f32 = jnp.bfloat16, jnp.float32
    return run(
        project_kernel,
        "project",
        BLOCK // tile,
        [smem()] * 3
        + [tiles(tile, WIDTH), None, None, None]
        + [tiles(tile // 16, LANES)] * 2
        + [None] * 4,
        [tiles(tile, WIDTH), tiles(tile, SHARE)] + [tiles(tile, LANES)] * 2 + [smem()] * 4,
        [out((BLOCK, WIDTH), bf16), out((BLOCK, SHARE), bf16)]
        + [out((BLOCK, LANES), f32)] * 2
        + [out((1,), jnp.int32)]
        + [out((count * steps,), jnp.int32)] * 3,
        (lengths, order, rank, x, gain, w_key, w_value, *rope_constants()),
        cost(540_000_000, 4_000_000, 512),
        [pltpu.SMEM((count,), jnp.int32), pltpu.SMEM((count,), jnp.int32)],
    )


def pick_kernel(wanted_ref, pieces_ref, picked_ref):
    def one(i, carry):
        picked_ref[i] = pieces_ref[wanted_ref[i]]
        return carry

    lax.fori_loop(0, picked_ref.shape[0], one, jnp.int32(0), unroll=4)


def pick_pieces(wanted, pieces):
    shape = out((wanted.shape[0], *pieces.shape[1:]), pieces.dtype)
    return run(
        pick_kernel, "pick_pieces", 1, [smem(), None], [None], [shape], (wanted, pieces), cost(0, 1_100_000), free=(1,)
    )[0]


def sum_kernel(later_ref, live_ref, pieces_ref, sum_ref):
    steps = MAXLEN // BLOCK - 1

    def one(d, carry):
        total = jnp.zeros(sum_ref.shape[1:], jnp.float32)
        for s in range(steps):
            part = pieces_ref[later_ref[d * steps + s]].astype(jnp.float32)
            total = total + jnp.where(live_ref[d * steps + s] == 1, part, 0.0)
        sum_ref[d] = total.astype(sum_ref.dtype)
        return carry

    lax.fori_loop(0, sum_ref.shape[0], one, jnp.int32(0), unroll=2)


def sum_pieces(later, live, pieces, count):
    shape = out((count, *pieces.shape[1:]), pieces.dtype)
    return run(
        sum_kernel,
        "sum_pieces",
        1,
        [smem(), smem(), None],
        [None],
        [shape],
        (later, live, pieces),
        cost(0, 1_100_000),
        free=(2,),
    )[0]


def route_kernel(begin_ref, routes_ref, picks_ref, ranks_ref):
    tokens = routes_ref.shape[1]
    expert_at = lax.broadcasted_iota(jnp.int32, (LANES, tokens), 0)
    hits = jnp.zeros((LANES, tokens), jnp.float32)
    for k in range(routes_ref.shape[0]):
        hits = hits + jnp.where(routes_ref[k : k + 1, :] == expert_at, 1.0, 0.0)
    row_at = lax.broadcasted_iota(jnp.int32, (tokens, tokens), 0)
    column_at = lax.broadcasted_iota(jnp.int32, (tokens, tokens), 1)
    before = jnp.where(row_at < column_at, 1.0, 0.0).astype(jnp.bfloat16)
    ranks = jnp.where(hits > 0.5, mm(hits.astype(jnp.bfloat16), before), -1.0)
    ranks_ref[...] = ranks
    slot_at = lax.broadcasted_iota(jnp.int32, (QUARTER, tokens), 0) + begin_ref[0]
    slot_at = slot_at.astype(jnp.float32)
    for e in range(EXPERTS):
        picks_ref[e * QUARTER : (e + 1) * QUARTER, :] = jnp.where(
            ranks[e : e + 1, :] == slot_at, 1.0, 0.0
        ).astype(jnp.bfloat16)


def route(begin, routes_t):
    return run(
        route_kernel,
        "route",
        1,
        [smem(), None],
        [None, None],
        [out((SLOTS, BLOCK), jnp.bfloat16), out((LANES, BLOCK), jnp.float32)],
        (begin, routes_t),
        cost(100_000_000, 1_600_000),
        free=(1,),
    )


def padded_columns(rows_t, out_ref):
    zero = jnp.zeros((HEAD_DIM, rows_t.shape[1]), out_ref.dtype)
    for h in range(4):
        mine = rows_t[h * HEAD_DIM : (h + 1) * HEAD_DIM].astype(out_ref.dtype)
        at = (h // 2) * HEAD_DIM
        out_ref[h, pl.ds(at, HEAD_DIM), :] = mine
        out_ref[h, pl.ds(HEAD_DIM - at, HEAD_DIM), :] = zero


def padded_rows(rows, out_ref):
    n = rows.shape[0]
    lane = lax.broadcasted_iota(jnp.int32, (n, 128), 1)
    for h in range(4):
        pair = rows[:, (h // 2) * 128 : (h // 2) * 128 + 128].astype(jnp.float32)
        if h % 2 != h // 2:
            pair = pltpu.roll(pair, HEAD_DIM, 1)
        own = (lane < HEAD_DIM) if h // 2 == 0 else (lane >= HEAD_DIM)
        out_ref[pl.ds(h * n, n), :] = jnp.where(own, pair, 0.0).astype(out_ref.dtype)


def attend_block(key_rows, value_rows, first, qpad_ref, max_ref, sum_ref, out_t_ref):
    half = BLOCK // 2
    for h in range(4):
        group = (h // 2) * HEAD_DIM
        for t in range(2):
            cols = slice(t * half, (t + 1) * half)
            rows = half if first and t == 0 else BLOCK
            scores = mm(key_rows[:rows], qpad_ref[h, :, cols])
            if first:
                key_at = lax.broadcasted_iota(jnp.int32, scores.shape, 0)
                query_at = lax.broadcasted_iota(jnp.int32, scores.shape, 1) + t * half
                scores = jnp.where(key_at > query_at, masked_score, scores)
            new_max = jnp.max(scores, axis=0, keepdims=True)
            if not first:
                old_max = max_ref[h : h + 1, cols]
                new_max = jnp.maximum(new_max, old_max)
                shrink = jnp.exp(old_max - new_max)
            weights = jnp.exp(scores - new_max)
            total = jnp.sum(weights, axis=0, keepdims=True)
            part = mm(value_rows[:rows], weights.astype(jnp.bfloat16), TN)[group : group + HEAD_DIM]
            mine = pl.ds(h * HEAD_DIM, HEAD_DIM)
            if not first:
                total = total + sum_ref[h : h + 1, cols] * shrink
                part = part + out_t_ref[mine, cols] * shrink
            max_ref[h : h + 1, cols] = new_max
            sum_ref[h : h + 1, cols] = total
            out_t_ref[mine, cols] = part


def attend_own_kernel(q_ref, own_ref, qpad_ref, max_ref, sum_ref, out_t_ref):
    padded_columns(jnp.transpose(q_ref[...].astype(jnp.float32) * score_mult), qpad_ref)
    max_ref[...] = jnp.zeros_like(max_ref)
    sum_ref[...] = jnp.ones_like(sum_ref)
    attend_block(own_ref[:, :LANES], own_ref[:, LANES:], True, qpad_ref, max_ref, sum_ref, out_t_ref)


def attend_own(queries, own_kv):
    return pl.pallas_call(
        attend_own_kernel,
        name="attend_own",
        in_specs=[vmem()] * 2,
        out_specs=[vmem()] * 4,
        out_shape=[
            out((4, LANES, BLOCK), jnp.bfloat16),
            out((8, BLOCK), jnp.float32),
            out((8, BLOCK), jnp.float32),
            out((SHARE, BLOCK), jnp.float32),
        ],
        compiler_params=pltpu.CompilerParams(vmem_limit_bytes=36 << 20),
        cost_estimate=cost(1_000_000_000, 2_000_000, 600_000),
    )(queries, own_kv)


def attend_kernel(
    reach_ref, qpad_ref, max0_ref, sum0_ref, out0_ref, prev_ref, att_ref, out_t_ref, lse_ref, max_ref, sum_ref
):
    max_ref[...] = max0_ref[...]
    sum_ref[...] = sum0_ref[...]
    out_t_ref[...] = out0_ref[...]

    @pl.loop(1, reach_ref[0] + 1)
    def _(step):
        rows = prev_ref[:, pl.ds(step - 1, 1)].reshape(BLOCK, SHARE)
        attend_block(rows[:, :LANES], rows[:, LANES:], False, qpad_ref, max_ref, sum_ref, out_t_ref)

    lse_ref[...] = max_ref[...] + jnp.log(sum_ref[...])
    for h in range(4):
        mine = pl.ds(h * HEAD_DIM, HEAD_DIM)
        out_t_ref[mine, :] = out_t_ref[mine, :] / sum_ref[h : h + 1, :]
    att_ref[...] = jnp.transpose(out_t_ref[...]).astype(jnp.bfloat16)


def attend(reach, begun, earlier):
    return run(
        attend_kernel,
        "attend",
        1,
        [smem()] + [vmem()] * 5,
        [None] * 3,
        [
            out((BLOCK, SHARE), jnp.bfloat16),
            out((SHARE, BLOCK), jnp.float32),
            out((8, BLOCK), jnp.float32),
        ],
        (reach, *begun, earlier),
        cost(4_000_000_000, 3_000_000, 3_000_000),
        [pltpu.VMEM((8, BLOCK), jnp.float32), pltpu.VMEM((8, BLOCK), jnp.float32)],
        limit=36,
    )


def attend_back_kernel(
    reach_ref, q_ref, qpad_ref, own_ref, prev_ref, grad_ref, grad_t_ref, out_t_ref, lse_ref, cos_ref, sin_ref,
    qgrad_ref, own_grad_ref, prev_grad_ref,
    gpad_ref, qrows_ref, grows_ref, ds_ref, p_ref, delta_ref, dq_ref,
):
    half = BLOCK // 2
    q_scaled = q_ref[...].astype(jnp.float32) * score_mult
    padded_rows(q_scaled, qrows_ref)
    padded_columns(grad_t_ref[...], gpad_ref)
    padded_rows(grad_ref[...], grows_ref)
    both = grad_t_ref[...].astype(jnp.float32) * out_t_ref[...]
    for h in range(4):
        delta_ref[h : h + 1, :] = jnp.sum(
            both[h * HEAD_DIM : (h + 1) * HEAD_DIM], axis=0, keepdims=True
        )


    def block(key_rows, value_rows, first):
        for h in range(4):
            for t in range(2):
                cols = slice(t * half, (t + 1) * half)
                wide = slice(h * BLOCK + t * half, h * BLOCK + (t + 1) * half)
                rows = half if first and t == 0 else BLOCK
                scores = mm(key_rows[:rows], qpad_ref[h, :, cols])
                weights = jnp.exp(scores - lse_ref[h : h + 1, cols])
                if first:
                    key_at = lax.broadcasted_iota(jnp.int32, scores.shape, 0)
                    query_at = lax.broadcasted_iota(jnp.int32, scores.shape, 1) + t * half
                    weights = jnp.where(key_at > query_at, 0.0, weights)
                weight_grad = mm(value_rows[:rows], gpad_ref[h, :, cols])
                score_grad = weights * (weight_grad - delta_ref[h : h + 1, cols])
                p_ref[:rows, wide] = weights.astype(jnp.bfloat16)
                ds_ref[:rows, wide] = score_grad.astype(jnp.bfloat16)
                if rows < BLOCK:
                    p_ref[rows:, wide] = jnp.zeros((BLOCK - rows, half), jnp.bfloat16)
                    ds_ref[rows:, wide] = jnp.zeros((BLOCK - rows, half), jnp.bfloat16)
        key_grad = mm(ds_ref[...], qrows_ref[...])
        value_grad = mm(p_ref[...], grows_ref[...])
        for h in range(4):
            group = (h // 2) * HEAD_DIM
            mine = pl.ds(h * HEAD_DIM, HEAD_DIM)
            part = mm(key_rows, ds_ref[:, h * BLOCK : (h + 1) * BLOCK], TN)[group : group + HEAD_DIM]
            dq_ref[mine, :] = part if first else dq_ref[mine, :] + part
        return key_grad, value_grad

    key_grad, value_grad = block(own_ref[:, :LANES], own_ref[:, LANES:], True)
    own_grad_ref[:, :LANES] = key_grad
    own_grad_ref[:, LANES:] = value_grad

    @pl.loop(1, reach_ref[0] + 1)
    def _(step):
        rows = prev_ref[:, pl.ds(step - 1, 1)].reshape(BLOCK, SHARE)
        key_grad, value_grad = block(rows[:, :LANES], rows[:, LANES:], False)
        parts = prev_grad_ref.shape[0]
        shape = (parts, 1, BLOCK // parts, LANES)
        prev_grad_ref[:, pl.ds(step - 1, 1), :, :LANES] = key_grad.astype(jnp.bfloat16).reshape(shape)
        prev_grad_ref[:, pl.ds(step - 1, 1), :, LANES:] = value_grad.astype(jnp.bfloat16).reshape(shape)

    query_grad = jnp.transpose(dq_ref[...]) * score_mult
    for i in range(0, SHARE, LANES):
        qgrad_ref[:, i : i + LANES] = turned(
            query_grad[:, i : i + LANES], cos_ref[...], sin_ref[...], back=True
        ).astype(jnp.bfloat16)


def attend_back(reach, queries, padded, own_kv, earlier, grad, grad_t, out_t, lse, cosine, signed_sine):
    return run(
        attend_back_kernel,
        "attend_back",
        1,
        [smem()] + [vmem()] * 10,
        [None] * 3,
        [
            out((BLOCK, SHARE), jnp.bfloat16),
            out((BLOCK, SHARE), jnp.float32),
            out(earlier.shape, jnp.bfloat16),
        ],
        (reach, queries, padded, own_kv, earlier, grad, grad_t, out_t, lse, cosine, signed_sine),
        cost(12_000_000_000, 5_000_000, 3_000_000),
        [
            pltpu.VMEM((4, LANES, BLOCK), jnp.bfloat16),
            pltpu.VMEM((4 * BLOCK, LANES), jnp.bfloat16),
            pltpu.VMEM((4 * BLOCK, LANES), jnp.bfloat16),
            pltpu.VMEM((BLOCK, 4 * BLOCK), jnp.bfloat16),
            pltpu.VMEM((BLOCK, 4 * BLOCK), jnp.bfloat16),
            pltpu.VMEM((8, BLOCK), jnp.float32),
            pltpu.VMEM((SHARE, BLOCK), jnp.float32),
        ],
        limit=36,
    )


def residual_kernel(
    a0, a1, a2, a3, w0, w1, w2, w3, x_ref, gain_ref, router_ref, ranks_ref, picks_ref,
    residual_ref, moe_ref, gates_ref, rows_ref, held_ref,
):
    step = pl.program_id(0)
    tile = x_ref.shape[0]

    @pl.when(step < BLOCK // tile)
    def _():
        branch = mm(a0[...], w0[...])
        for a, w in ((a1, w1), (a2, w2), (a3, w3)):
            branch = branch + mm(a[...], w[...])
        residual = x_ref[...].astype(jnp.float32) + residual_mult * branch
        residual_ref[...] = residual
        scale = lax.rsqrt(jnp.mean(residual * residual, axis=1, keepdims=True) + epsilon)
        moe_in = (residual * scale * gain_ref[...]).astype(jnp.bfloat16)
        moe_ref[:, :WIDTH] = moe_in
        logits = mm(router_ref[...], moe_in, NT)
        chosen = ranks_ref[...] >= 0.0
        kept = jnp.where(chosen, logits, masked_score)
        top = jnp.max(kept, axis=0, keepdims=True)
        raised = jnp.where(chosen, jnp.exp(kept - top), 0.0)
        gates = raised / jnp.sum(raised, axis=0, keepdims=True)
        gates_ref[...] = gates
        low = (residual_mult * jnp.transpose(gates)).astype(jnp.bfloat16)
        moe_ref[:, WIDTH:] = low
        held_ref[pl.ds(step * tile, tile), :WIDTH] = moe_in
        held_ref[pl.ds(step * tile, tile), WIDTH:] = low

    @pl.when(step >= BLOCK // tile)
    def _():
        rows_ref[...] = mm(picks_ref[...], held_ref[...]).astype(jnp.bfloat16)


def residual_step(attended, w_out, x, gain, router_t, ranks, picks):
    tile = 256
    first = BLOCK // tile
    slot_tile = SLOTS // 2

    def early(rows, width):
        return pl.BlockSpec((rows, width), lambda i: (jnp.minimum(i, first - 1), 0))

    def late(rows, width):
        return pl.BlockSpec((rows, width), lambda i: (jnp.maximum(i - first, 0), 0))

    by_columns = pl.BlockSpec((LANES, tile), lambda i: (0, jnp.minimum(i, first - 1)))
    return run(
        residual_kernel,
        "residual_step",
        first + 2,
        [early(tile, SHARE)] * 4
        + [None] * 4
        + [early(tile, WIDTH), None, None, by_columns, late(slot_tile, BLOCK)],
        [early(tile, WIDTH), early(tile, WIDTH + LANES), by_columns, late(slot_tile, WIDTH + LANES)],
        [
            out((BLOCK, WIDTH), jnp.float32),
            out((BLOCK, WIDTH + LANES), jnp.bfloat16),
            out((LANES, BLOCK), jnp.float32),
            out((SLOTS, WIDTH + LANES), jnp.bfloat16),
        ],
        (*attended, *w_out, x, gain, router_t, ranks, picks),
        cost(2_700_000_000, 12_000_000, 70_000),
        [pltpu.VMEM((BLOCK, WIDTH + LANES), jnp.bfloat16)],
        free=(1, 2, 3, 5, 6, 7, 10),
    )


def mix_kernel(begin_ref, ranks_ref, moe_ref, mix_ref):
    ranks = jnp.transpose(ranks_ref[...]).astype(jnp.bfloat16)
    gates = moe_ref[:, WIDTH:]
    width = 640
    for at in range(0, SLOTS, width):
        expert_at = lax.broadcasted_iota(jnp.int32, (LANES, width), 0)
        first = expert_at * QUARTER - at
        slot_at = lax.broadcasted_iota(jnp.int32, (LANES, width), 1)
        inside = jnp.logical_and(slot_at >= first, slot_at < first + QUARTER)
        spread = jnp.where(inside, 1.0, 0.0).astype(jnp.bfloat16)
        within = jnp.sum(jnp.where(inside, slot_at - first, 0), axis=0, keepdims=True) + begin_ref[0]
        hit = mm(ranks, spread) == within.astype(jnp.float32)
        mix_ref[:, at : at + width] = jnp.where(hit, mm(gates, spread), 0.0).astype(jnp.bfloat16)


def mix_weights(begin, ranks, moe_cat):
    return run(
        mix_kernel,
        "mix_weights",
        1,
        [smem(), None, None],
        [None],
        [out((BLOCK, SLOTS), jnp.bfloat16)],
        (begin, ranks, moe_cat),
        cost(350_000_000, 3_000_000),
    )[0]


def expert_kernel(lane_ref, x_ref, grad_ref, *refs):
    downs, gate_refs, up_refs = refs[:4], refs[4:8], refs[8:12]
    row_ref, hidden_ref, units_ref = refs[12:]
    rows = row_ref.shape[0]
    here = pl.ds(pl.program_id(0) * rows, rows)
    lane = lax.broadcasted_iota(jnp.int32, (rows, LANES), 1) == lane_ref[0]
    gate = jnp.sum(
        jnp.where(lane, x_ref[here, WIDTH:].astype(jnp.float32), 0.0), axis=1, keepdims=True
    )
    x = x_ref[here, :WIDTH]
    gates, ups, sigmoids = [], [], []
    for j in range(4):
        pre = mm(x, jnp.concatenate([gate_refs[j][...], up_refs[j][...]], axis=1))
        gate_pre, up_pre = pre[:, :LANES], pre[:, LANES:]
        gates.append(gate_pre)
        ups.append(up_pre)
        sigmoids.append(1.0 / (1.0 + jnp.exp(-gate_pre)))
    down = jnp.concatenate([p[...] for p in downs], axis=0)
    hidden_grad = mm(grad_ref[...], down, NT)
    gate_grad = jnp.zeros((rows, LANES), jnp.float32)
    row = None
    for j in range(4):
        part = hidden_grad[:, j * LANES : (j + 1) * LANES]
        silu = gates[j] * sigmoids[j]
        hidden = (silu * ups[j]).astype(jnp.bfloat16)
        hidden_ref[:, j * LANES : (j + 1) * LANES] = hidden
        gate_grad = gate_grad + hidden.astype(jnp.float32) * part
        gate_pre_grad = part * ups[j] * sigmoids[j] * (1.0 + gates[j] * (1.0 - sigmoids[j]))
        up_pre_grad = part * silu
        units_ref[:, j * SHARE : j * SHARE + LANES] = (gate_pre_grad * gate).astype(jnp.bfloat16)
        units_ref[:, j * SHARE + LANES : (j + 1) * SHARE] = (up_pre_grad * gate).astype(jnp.bfloat16)
        both = jnp.concatenate([gate_pre_grad, up_pre_grad], axis=1).astype(jnp.bfloat16)
        term = mm(both, jnp.concatenate([gate_refs[j][...], up_refs[j][...]], axis=1), NT)
        row = term if row is None else row + term
    row_ref[:, :WIDTH] = row.astype(jnp.bfloat16)
    gate_grad = jnp.sum(gate_grad, axis=1, keepdims=True)
    row_ref[:, WIDTH:] = jnp.where(lane, gate_grad, 0.0).astype(jnp.bfloat16)


def output_kernel(hidden_ref, d0, d1, d2, d3, out_ref):
    down = jnp.concatenate([p[...] for p in (d0, d1, d2, d3)], axis=0)
    out_ref[...] = mm(hidden_ref[...], down).astype(jnp.bfloat16)


def output_rows(hidden, downs):
    tile = 320
    return run(
        output_kernel,
        "output_rows",
        SLOTS // tile,
        [tiles(tile, 512)] + [None] * 4,
        [tiles(tile, WIDTH)],
        [out((SLOTS, WIDTH), jnp.bfloat16)],
        (hidden, *downs),
        cost(1_300_000_000, 5_000_000),
    )[0]


def expert_step(lane, x, grad, downs, gates, ups):
    tile = 320
    return run(
        expert_kernel,
        "expert_step",
        SLOTS // tile,
        [smem(), vmem(), tiles(tile, WIDTH)] + [None] * 12,
        [tiles(tile, WIDTH + LANES), tiles(tile, 512), tiles(tile, WIDTH)],
        [
            out((SLOTS, WIDTH + LANES), jnp.bfloat16),
            out((SLOTS, 512), jnp.bfloat16),
            out((SLOTS, WIDTH), jnp.bfloat16),
        ],
        (lane, x, grad, *downs, *gates, *ups),
        cost(6_700_000_000, 15_000_000, 700_000),
        limit=40,
    )


def unit_grads_kernel(lane_ref, x_ref, grad_ref, hidden_ref, units_ref, keep_ref, send_ref, turned_ref, gate_ref):
    step = pl.program_id(0)

    @pl.when(step == 0)
    def _():
        for k in range(4):
            columns = slice(k * SHARE, (k + 1) * SHARE)
            turned_ref[columns, :] = jnp.transpose(x_ref[:, columns])
        lane = lax.broadcasted_iota(jnp.int32, (SLOTS, LANES), 1) == lane_ref[0]
        gate = jnp.where(lane, x_ref[:, WIDTH:].astype(jnp.float32), 0.0)
        gate_ref[...] = jnp.broadcast_to(jnp.sum(gate, axis=1, keepdims=True), (SLOTS, LANES))

    def write(to_ref):
        scaled = (hidden_ref[...].astype(jnp.float32) * gate_ref[...]).astype(jnp.bfloat16)
        to_ref[0, :LANES, :] = mm(scaled, grad_ref[...], TN).astype(jnp.bfloat16)
        for k in range(4):
            columns = slice(k * SHARE, (k + 1) * SHARE)
            to_ref[0, LANES:, columns] = mm(turned_ref[columns, :], units_ref[...]).astype(jnp.bfloat16)

    @pl.when(step < 2)
    def _():
        write(keep_ref)

    @pl.when(step >= 2)
    def _():
        write(send_ref)


def unit_grads(lane, x, grad, hidden, units):
    rows = SHARE + LANES

    def share_of(i):
        return jnp.where(i < 2, 2 * i, 2 * i - 3)

    return run(
        unit_grads_kernel,
        "unit_grads",
        4,
        [
            smem(),
            vmem(),
            None,
            pl.BlockSpec((SLOTS, LANES), lambda i: (0, share_of(i))),
            pl.BlockSpec((SLOTS, SHARE), lambda i: (0, share_of(i))),
        ],
        [
            pl.BlockSpec((1, rows, WIDTH), lambda i: (jnp.minimum(i, 1), 0, 0)),
            pl.BlockSpec((1, rows, WIDTH), lambda i: (jnp.maximum(i - 2, 0), 0, 0)),
        ],
        [out((2, rows, WIDTH), jnp.bfloat16), out((2, rows, WIDTH), jnp.bfloat16)],
        (lane, x, grad, hidden, units),
        cost(4_000_000_000, 12_000_000),
        [pltpu.VMEM((WIDTH, SLOTS), jnp.bfloat16), pltpu.VMEM((SLOTS, LANES), jnp.float32)],
        limit=36,
    )


def unit_finish_kernel(mine_ref, first_ref, second_ref, third_ref, gate_ref, up_ref, down_ref):
    got = jnp.concatenate([first_ref[...], second_ref[...], third_ref[...]], axis=0)
    total = mine_ref[0] + got.astype(jnp.float32)
    down_ref[0] = total[:LANES, :]
    for k in range(4):
        rows = slice(k * SHARE, (k + 1) * SHARE)
        gate_ref[0, rows, :] = total[LANES:, k * SHARE : k * SHARE + LANES]
        up_ref[0, rows, :] = total[LANES:, k * SHARE + LANES : (k + 1) * SHARE]


def unit_finish(mine, first, second, third):
    return run(
        unit_finish_kernel,
        "unit_finish",
        1,
        [once(1, PACKED, WIDTH), None, None, None],
        [None] * 3,
        [
            out((1, WIDTH, LANES), jnp.float32),
            out((1, WIDTH, LANES), jnp.float32),
            out((1, LANES, WIDTH), jnp.float32),
        ],
        (mine, first, second, third),
        cost(1_000_000, 3_000_000),
        free=(0, 1, 2, 3),
    )


def home_kernel(rank_ref, mix_ref, rows_ref, keep_ref, send_ref):
    rank = rank_ref[0]
    extra = rows_ref.shape[1] > WIDTH
    for j in range(4):
        at = pl.multiple_of(jnp.bitwise_xor(rank, j) * SHARE, SHARE)
        total = mm(mix_ref[...], rows_ref[:, pl.ds(at, SHARE)])
        to_ref = send_ref if j % 2 else keep_ref
        to_ref[(j // 2) * BLOCK : (j // 2 + 1) * BLOCK, :] = total.astype(to_ref.dtype)
    if extra:
        gate_grads = jnp.transpose(mm(mix_ref[...], rows_ref[:, WIDTH:]))[:EXPERTS]
        for to_ref in (keep_ref, send_ref):
            for i in range(2):
                at = 2 * BLOCK + i * EXPERTS
                to_ref[at : at + EXPERTS, :] = gate_grads[:, i * SHARE : (i + 1) * SHARE].astype(
                    to_ref.dtype
                )


def sum_home(rank, mix, rows):
    height = 2 * BLOCK + (2 * EXPERTS if rows.shape[1] > WIDTH else 0)
    return run(
        home_kernel,
        "sum_home",
        1,
        [smem(), None, vmem()],
        [None] * 2,
        [out((height, SHARE), jnp.float32), out((height, SHARE), jnp.bfloat16)],
        (rank, mix, rows),
        cost(1_500_000_000, 6_000_000),
        limit=36,
    )


def swap_kernel(mine_ref, got_ref, total_ref):
    mine, got = mine_ref, got_ref
    half = BLOCK
    total_ref[:half] = (mine[:half] + got[half : 2 * half].astype(jnp.float32)).astype(total_ref.dtype)
    total_ref[half : 2 * half] = (
        mine[half : 2 * half] + got[:half].astype(jnp.float32)
    ).astype(total_ref.dtype)
    total_ref[2 * half :] = (mine[2 * half :] + got[2 * half :].astype(jnp.float32)).astype(
        total_ref.dtype
    )


def swap_sum(mine, got):
    return run(
        swap_kernel,
        "swap_sum",
        1,
        [None] * 2,
        [None],
        [out(mine.shape, jnp.bfloat16)],
        (mine, got),
        cost(1_000_000, 2_500_000),
        free=(0, 1),
    )[0]


def norm_back_kernel(
    rank_ref, g0, g2, g1, g3, z_ref, gates_ref, residual_ref, gain_ref, router_ref, grad_ref, w_ref,
    low_ref, logit_ref, own_ref, att_ref, att_t_ref, gain_grad_ref, u_ref,
):
    rank = rank_ref[0]
    for flip, part in enumerate((g0, g1, g2, g3)):
        at = pl.multiple_of(jnp.bitwise_xor(rank, flip) * SHARE, SHARE)
        u_ref[:, pl.ds(at, SHARE)] = part[...].astype(jnp.float32)
    weighted_grads = z_ref[...].astype(jnp.float32)
    gates = gates_ref[:EXPERTS, :]
    inner = jnp.sum(weighted_grads, axis=0, keepdims=True)
    logit_grad = (weighted_grads - gates * inner).astype(jnp.bfloat16)
    logit_ref[...] = logit_grad
    u = u_ref[...] + mm(logit_grad, router_ref[:EXPERTS, :], TN)
    v = residual_ref[...]
    scale = lax.rsqrt(jnp.mean(v * v, axis=1, keepdims=True) + epsilon)
    weighted = u * gain_ref[...]
    mean = jnp.mean(weighted * v, axis=1, keepdims=True)
    total = grad_ref[...].astype(jnp.float32) + scale * weighted - v * (scale * scale * scale * mean)

    @pl.when(pl.program_id(0) == 0)
    def _():
        gain_grad_ref[...] = jnp.zeros_like(gain_grad_ref)

    gain_grad_ref[0:1, :] += jnp.sum(u * v * scale, axis=0, keepdims=True)
    low = (residual_mult * total).astype(jnp.bfloat16)
    low_ref[...] = low
    u_ref[...] = total
    own_ref[...] = u_ref[:, pl.ds(pl.multiple_of(rank * SHARE, SHARE), SHARE)]
    att_ref[...] = mm(low, w_ref[...], NT).astype(jnp.bfloat16)
    att_t_ref[...] = mm(w_ref[...], low, NT).astype(jnp.bfloat16)


def norm_back_step(rank, mine, theirs, gates, residual, gain, router_t, out_grad, w_out):
    tile = 256
    by_columns = pl.BlockSpec((EXPERTS, tile), lambda i: (0, i))
    return run(
        norm_back_kernel,
        "norm_back_step",
        BLOCK // tile,
        [smem()]
        + [tiles(tile, SHARE), tiles(tile, SHARE, BLOCK // tile)] * 2
        + [
            tiles(EXPERTS, SHARE, 2 * BLOCK // EXPERTS),
            pl.BlockSpec((LANES, tile), lambda i: (0, i)),
            tiles(tile, WIDTH),
            None,
            None,
            tiles(tile, WIDTH),
            None,
        ],
        [
            tiles(tile, WIDTH),
            by_columns,
            tiles(tile, SHARE),
            tiles(tile, SHARE),
            pl.BlockSpec((SHARE, tile), lambda i: (0, i)),
            fixed(8, WIDTH),
        ],
        [
            out((BLOCK, WIDTH), jnp.bfloat16),
            out((EXPERTS, BLOCK), jnp.bfloat16),
            out((BLOCK, SHARE), jnp.float32),
            out((BLOCK, SHARE), jnp.bfloat16),
            out((SHARE, BLOCK), jnp.bfloat16),
            out((8, WIDTH), jnp.float32),
        ],
        (rank, mine, mine, theirs, theirs, mine, gates, residual, gain, router_t, out_grad, w_out),
        cost(700_000_000, 9_000_000, 512),
        [pltpu.VMEM((tile, WIDTH), jnp.float32)],
        free=(3, 4, 9),
    )


def dense_grads_kernel(low_ref, attended_ref, normed_ref, qgrad_ref, logit_ref, moe_ref, gain_ref, made_ref):
    made_ref[:, :SHARE] = mm(low_ref[...], attended_ref[...], TN).astype(jnp.bfloat16)
    made_ref[:, SHARE : 2 * SHARE] = mm(normed_ref[...], qgrad_ref[...], TN).astype(jnp.bfloat16)
    router = mm(logit_ref[...], moe_ref[:, :WIDTH])
    stacked = jnp.concatenate(
        [router, gain_ref[...], jnp.zeros((LANES - EXPERTS - 8, WIDTH), jnp.float32)], axis=0
    )
    made_ref[:, 2 * SHARE :] = jnp.transpose(stacked).astype(jnp.bfloat16)


def dense_grads(low, attended, normed, qgrad, logit, moe_cat, gain_grad):
    return run(
        dense_grads_kernel,
        "dense_grads",
        1,
        [None] * 7,
        [None],
        [out((WIDTH, 2 * SHARE + LANES), jnp.bfloat16)],
        (low, attended, normed, qgrad, logit, moe_cat, gain_grad),
        cost(600_000_000, 6_000_000),
    )[0]


def last_grads_kernel(
    rank_ref, own_ref, home_ref, qgrad_ref, normed_ref, x_ref, wq_ref, wk_ref, wv_ref, cos_ref, sin_ref, made_ref,
    gain_ref, all_ref, keep_ref, send_ref, inner_ref, part_ref,
):
    rank = rank_ref[0]
    kv = own_ref[...] + home_ref[...].astype(jnp.float32)
    key_grad = turned(kv[:, :LANES], cos_ref[...], sin_ref[...], back=True).astype(jnp.bfloat16)
    value_grad = kv[:, LANES:].astype(jnp.bfloat16)
    both = jnp.concatenate([key_grad, value_grad], axis=1)
    all_ref[:, : 2 * SHARE] = made_ref[:, : 2 * SHARE]
    all_ref[:, 2 * SHARE : 3 * SHARE] = mm(normed_ref[...], both, TN).astype(jnp.bfloat16)
    gain = jnp.zeros((1, WIDTH), jnp.float32)
    tile = 128
    for i in range(0, BLOCK, tile):
        rows = slice(i, i + tile)
        part = mm(qgrad_ref[rows, :], wq_ref[...], NT)
        part = part + mm(key_grad[rows], wk_ref[...], NT) + mm(value_grad[rows], wv_ref[...], NT)
        x = x_ref[rows, :].astype(jnp.float32)
        scale = lax.rsqrt(jnp.mean(x * x, axis=1, keepdims=True) + epsilon)
        along = part * x
        gain = gain + jnp.sum(along * scale, axis=0, keepdims=True)
        inner = jnp.sum(along * gain_ref[...], axis=1, keepdims=True)
        inner_ref[:, rows] = jnp.transpose(jnp.broadcast_to(inner, (tile, LANES)))[:8]
        part_ref[rows, :] = part
    for j in range(4):
        at = pl.multiple_of(jnp.bitwise_xor(rank, j) * SHARE, SHARE)
        to_ref = send_ref if j % 2 else keep_ref
        to_ref[(j // 2) * BLOCK : (j // 2 + 1) * BLOCK, :] = part_ref[:, pl.ds(at, SHARE)].astype(to_ref.dtype)
    lane = lax.broadcasted_iota(jnp.int32, (WIDTH, LANES), 1)
    column = jnp.transpose(jnp.broadcast_to(gain, (LANES, WIDTH)))
    rest = jnp.where(lane == EXPERTS + 8, column, made_ref[:, 2 * SHARE :].astype(jnp.float32))
    all_ref[:, 3 * SHARE :] = rest.astype(jnp.bfloat16)


def last_grads(rank, own, home, qgrad, normed, x, w_query, w_key, w_value, cosine, sine, made, gain):
    return run(
        last_grads_kernel,
        "last_grads",
        1,
        [smem()] + [None] * 12,
        [None] * 4,
        [
            out((WIDTH, 3 * SHARE + LANES), jnp.bfloat16),
            out((2 * BLOCK, SHARE), jnp.float32),
            out((2 * BLOCK, SHARE), jnp.bfloat16),
            out((8, BLOCK), jnp.float32),
        ],
        (rank, own, home, qgrad, normed, x, w_query, w_key, w_value, cosine, sine, made, gain),
        cost(1_000_000_000, 8_000_000, 512),
        [pltpu.VMEM((BLOCK, WIDTH), jnp.float32)],
        free=(2,),
    )


def input_finish_kernel(
    rank_ref, near_ref, far_ref, i0, i1, i2, i3, x_ref, gain_ref, residual_ref, made_ref
):
    mine = pl.ds(pl.multiple_of(rank_ref[0] * SHARE, SHARE), SHARE)
    x = x_ref[...].astype(jnp.float32)
    scale = lax.rsqrt(jnp.mean(x * x, axis=1, keepdims=True) + epsilon)
    inner = (i0[...] + i1[...] + i2[...] + i3[...]) * (1.0 / WIDTH)
    inner = jnp.transpose(jnp.broadcast_to(inner[:1], (LANES, BLOCK)))[:, :1]
    weighted = (near_ref[...] + far_ref[...].astype(jnp.float32)) * gain_ref[:, mine]
    x_own = x_ref[:, mine].astype(jnp.float32)
    made_ref[...] = residual_ref[...] + scale * weighted - x_own * (scale * scale * scale * inner)


def input_finish(rank, near, far, inners, x, gain, residual):
    return run(
        input_finish_kernel,
        "input_finish",
        1,
        [smem(), once(BLOCK, SHARE), None] + [None] * 7,
        [None],
        [out((BLOCK, SHARE), jnp.float32)],
        (rank, near, far, *inners, x, gain, residual),
        cost(3_000_000, 3_000_000, 512),
        free=(1, 2, 3, 4, 5, 6),
    )[0]


def per_device(
    hidden_in,
    lengths,
    block_order,
    routes,
    norm_gain_attn,
    w_query,
    w_key,
    w_value,
    w_out,
    norm_gain_moe,
    w_router,
    w_gate,
    w_up,
    w_down,
    out_grad,
):
    dp_count = block_order.shape[0]
    mp_rank = lax.axis_index("mp").astype(jnp.int32)
    column_start = mp_rank * SHARE
    piece = BLOCK // dp_count
    steps = MAXLEN // BLOCK - 1
    rank = mp_rank.reshape(1)
    lane = lax.axis_index("dp").astype(jnp.int32).reshape(1)
    begin = rank * QUARTER
    gain_attn = norm_gain_attn[None, :]
    gain_moe = norm_gain_moe[None, :]
    router_t = jnp.pad(w_router.T, ((0, LANES - EXPERTS), (0, 0)))

    far_out = peer(w_out, 2)
    cores = ([(0, 2), (2, 0)], [(1, 3), (3, 1)])
    experts = (w_down[0], w_gate[0], w_up[0])
    far_early = [lax.ppermute(w, "mp", cores[0]) for w in experts]

    normed, key_value, cosine, sine, reach, wanted, later, live = project(
        lengths, block_order, lane, hidden_in, gain_attn, w_key, w_value
    )
    queries = project_queries(normed, w_query, cosine, sine)
    pieces = to_all(key_value.reshape(dp_count, piece, SHARE))
    picks, ranks = route(begin, after(routes.T, key_value))
    begun = attend_own(queries, after(key_value, picks))
    picked = pick_pieces(wanted, after(pieces, far_out, *far_early, queries, picks))
    earlier = to_all(picked.reshape(dp_count, steps * piece, SHARE))
    earlier = earlier.reshape(dp_count, steps, piece, SHARE)

    outs = [w_out, peer(after(w_out, picked), 1), far_out, peer(far_out, 1)]

    grad_rows = jnp.dot(picks, after(out_grad, picked), preferred_element_type=jnp.bfloat16)
    grad_arrived = to_experts(after(grad_rows, earlier, begun[1]).reshape(EXPERTS, QUARTER, WIDTH))
    attended, attended_t, lse = attend(reach, begun, earlier)
    far = peer(attended, 2)
    residual, moe_cat, gates, moe_rows = residual_step(
        [attended, peer(attended, 1), far, peer(far, 1)],
        outs,
        hidden_in,
        gain_moe,
        router_t,
        ranks,
        picks,
    )
    late = [lax.ppermute(after(w, moe_rows), "mp", cores[1]) for w in experts]
    far = [a + b for a, b in zip(far_early, late)]
    own = [after(w, moe_rows) for w in experts]
    downs, gates_all, ups = [[w, peer(w, 1), v, peer(v, 1)] for w, v in zip(own, far)]
    grouped = to_experts(moe_rows.reshape(EXPERTS, QUARTER, -1)).reshape(SLOTS, -1)
    mix = mix_weights(begin, ranks, moe_cat)
    grouped_grad = grad_arrived.reshape(SLOTS, WIDTH)
    row_grad, hidden_units, unit_grad = expert_step(
        lane, grouped, grouped_grad, downs, gates_all, ups
    )
    row_home = to_experts(row_grad.reshape(dp_count, QUARTER, -1)).reshape(SLOTS, -1)
    rows_out = output_rows(hidden_units, downs)
    rows_home = to_experts(after(rows_out, row_home).reshape(dp_count, QUARTER, -1)).reshape(SLOTS, -1)

    unit_keep, unit_send = unit_grads(lane, grouped, grouped_grad, hidden_units, unit_grad)
    unit_near = unit_keep.astype(jnp.float32) + peer(unit_send, 1).astype(jnp.float32)
    unit_low = unit_near[1].astype(jnp.bfloat16)
    cut = PACKED // 2
    unit_far_a = peer(unit_low[:cut], 2)
    keep, send = sum_home(rank, after(mix, unit_far_a, rows_out), row_home)
    near = keep + peer(send, 1).astype(jnp.float32)
    mine = swap_sum(near, peer(near.astype(jnp.bfloat16), 2))
    theirs = peer(mine, 1)
    branch_grad, logit_grad, residual_grad, attended_grad, attended_grad_t, moe_gain = norm_back_step(
        rank, mine, theirs, gates, residual, gain_moe, router_t, out_grad, w_out
    )

    query_pre_grad, own_grads, later_grads = attend_back(
        reach,
        queries,
        begun[0],
        key_value,
        earlier,
        attended_grad,
        attended_grad_t,
        attended_t,
        lse,
        cosine,
        sine,
    )
    unit_far_b = peer(after(unit_low[cut:], later_grads), 2)
    unit_far_b = peer(after(unit_low[cut : cut + cut // 2], branch_grad), 2)
    later_pieces = to_all(after(later_grads, rows_home, unit_far_b).reshape(dp_count, steps * piece, SHARE))
    summed = sum_pieces(
        later, live, later_pieces.reshape(dp_count * steps, piece, SHARE), dp_count
    )
    kv_home = to_all(summed).reshape(BLOCK, SHARE)
    made = dense_grads(
        branch_grad, attended, normed, query_pre_grad, logit_grad, moe_cat, moe_gain
    )

    unit_far_c = peer(after(unit_low[cut + cut // 2 :], kv_home, made), 2)

    every, keep, send, inner = last_grads(
        rank,
        own_grads,
        kv_home,
        query_pre_grad,
        normed,
        hidden_in,
        w_query,
        w_key,
        w_value,
        cosine,
        sine,
        made,
        gain_attn,
    )
    near_norm = keep + peer(send, 1).astype(jnp.float32)
    far_norm = peer(near_norm[BLOCK:].astype(jnp.bfloat16), 2)
    inners = [inner] + [peer(inner, flip) for flip in (1, 2, 3)]
    every = after(every, unit_far_c)
    arrived = to_all(every.reshape(dp_count, WIDTH // dp_count, -1))
    keep, send = sum_home(rank, mix, after(rows_home, every))
    near_mix = keep + peer(send, 1).astype(jnp.float32)
    far_mix = peer(near_mix[BLOCK:].astype(jnp.bfloat16), 2)
    grad_w_gate, grad_w_up, grad_w_down = unit_finish(
        unit_near, unit_far_a, after(unit_far_b, every), unit_far_c
    )
    dense = jnp.sum(arrived.astype(jnp.float32), axis=0)
    at = 3 * SHARE
    attn_gain = dense[:, at + EXPERTS + 8]
    attn_gain = attn_gain + peer(attn_gain, 1) + peer(attn_gain, 2) + peer(attn_gain, 3)
    residual_cols = lax.dynamic_slice_in_dim(residual, column_start, SHARE, 1)
    mixture = near_mix[:BLOCK] + after(far_mix, attn_gain).astype(jnp.float32)
    out_hidden = (residual_cols + mixture).astype(jnp.bfloat16)

    grad_hidden = input_finish(
        rank, near_norm, after(far_norm, dense), inners, hidden_in, gain_attn, residual_grad
    )
    return (
        out_hidden,
        grad_hidden,
        dense[:, SHARE : 2 * SHARE],
        dense[:, 2 * SHARE : 2 * SHARE + LANES],
        dense[:, 2 * SHARE + LANES : at],
        dense[:, :SHARE].T,
        attn_gain,
        dense[:, at + EXPERTS],
        dense[:, at : at + EXPERTS],
        grad_w_gate,
        grad_w_up,
        grad_w_down,
    )


def solution(mesh):
    in_specs = (
        P("dp", None),
        P(),
        P(),
        P("dp", None),
        P(),
        P(None, "mp"),
        P(None, "mp"),
        P(None, "mp"),
        P("mp", None),
        P(),
        P(),
        P("dp", None, "mp"),
        P("dp", None, "mp"),
        P("dp", "mp", None),
        P("dp", None),
    )
    out_specs = (
        P("dp", "mp"),
        P("dp", "mp"),
        P("dp", "mp"),
        P("dp", "mp"),
        P("dp", "mp"),
        P("mp", "dp"),
        P("dp"),
        P("dp"),
        P("dp", None),
        P("dp", None, "mp"),
        P("dp", None, "mp"),
        P("dp", "mp", None),
    )
    return jax.shard_map(
        per_device, mesh=mesh, in_specs=in_specs, out_specs=out_specs, check_vma=False
    )
```
